32 devices in a mesh: row: 2 (over core), nar: 4 (over y, x), wid: 4 (over z).
Axes of the slice: x: 2, y: 2, z: 4, core: 2. Of those that a mesh axis runs over, the one named last changes fastest.
Arguments:
- hidden_in: bfloat16 [2, 2048, 2048], P('row', ('nar', 'wid')), may hold values from -6 to 6
- doc_lengths: int32 [2, 8], P('row'), may hold values from 1 to 1024, 2048 in all within a row
- w_query: bfloat16 [2048, 2048], P('nar', 'wid'), may hold values from -0.125 to 0.125
- w_key: bfloat16 [2048, 512], P('nar'), may hold values from -0.125 to 0.125
- w_value: bfloat16 [2048, 512], P('nar'), may hold values from -0.125 to 0.125
- w_output: bfloat16 [2048, 2048], P('wid', 'nar'), may hold values from -1 to 1
- w_gate: bfloat16 [2048, 8192], P('nar', 'wid'), may hold values from -0.125 to 0.125
- w_up: bfloat16 [2048, 8192], P('nar', 'wid'), may hold values from -0.125 to 0.125
- w_down: bfloat16 [8192, 2048], P('wid', 'nar'), may hold values from -0.0625 to 0.0625
- gain_attn: float32 [2048], replicated, may hold values from 0.5 to 1.5
- gain_ffn: float32 [2048], replicated, may hold values from 0.5 to 1.5
- grad_out: bfloat16 [2, 2048, 2048], P('row', ('nar', 'wid')), may hold values from -9 to 9
Outputs:
- hidden_out: bfloat16 [2, 2048, 2048], P('row', ('nar', 'wid'))
- grad_in: bfloat16 [2, 2048, 2048], P('row', ('nar', 'wid'))
- grad_query: float32 [2048, 2048], P(('row', 'nar'), 'wid')
- grad_key: float32 [2048, 512], P(('row', 'nar'))
- grad_value: float32 [2048, 512], P(('row', 'nar'))
- grad_output: float32 [2048, 2048], P('wid', ('row', 'nar'))
- grad_gate: float32 [2048, 8192], P(('row', 'nar'), 'wid')
- grad_up: float32 [2048, 8192], P(('row', 'nar'), 'wid')
- grad_down: float32 [8192, 2048], P('wid', ('row', 'nar'))
- grad_gain_attn: float32 [2048], P(('row', 'nar'))
- grad_gain_ffn: float32 [2048], P(('row', 'nar'))
The draws below stay inside these ranges and needn't reach their ends.
Inputs may be any that keep to these rules, and one draw needn't show every extreme that they name: `doc_lengths`: each row's 8 lengths add up to 2048, and the longest is exactly 1024.
All inputs are finite; a program needn't handle non-finite values.
Results may differ from the reference program's by a relative error of at most 0.024.
Values may be sent and summed in bfloat16 or wider, within the bound.
A program may use at most 192 MiB of HBM per device.

```python
import math
import jax
import jax.numpy as jnp
import numpy as np
from jax import lax

D = 2048
H = 32
KV = 8
HD = 64
FF = 8192
DOCS = 8
ROWS = 2
LEN = 2048
MOST = 1024
N_WID = 4


def draw_grad_out(key, part):
    position_ramp = jnp.arange(LEN, dtype=jnp.float32) / max(LEN - 1, 1)
    base_draw = jnp.clip(jax.random.normal(key, (ROWS, LEN, D), jnp.float32), -5.0, 5.0)
    scaled = base_draw * (0.6 + 1.2 * position_ramp)[None, :, None]
    return scaled.astype(jnp.bfloat16)


def level_of(rng, dims, pieces, least, high):
    level = 1.0
    for position, shards_of in pieces:
        draws = jax.random.uniform(jax.random.fold_in(jax.random.fold_in(rng, 6), position), (shards_of,), jnp.float32, least / len(pieces), high / len(pieces))
        level = level * jnp.repeat(jnp.exp(draws), dims[position] // shards_of).reshape((-1,) + (1,) * (len(dims) - 1 - position))
    return level


def split_up(count, total, bound, slope):
    loads = [(1 << 20) // math.isqrt(standing ** slope) + 1 for standing in range(2, count + 1)]
    spare, holding = total - bound - (count - 1), [1] * (count - 1)
    while spare > 0:
        candidates = [i for i in range(count - 1) if holding[i] < bound]
        mass, left = sum([loads[i] for i in candidates]), spare
        for i in candidates:
            extra = min(bound - holding[i], max(1, left * loads[i] // mass), spare)
            holding[i] = holding[i] + extra
            spare = spare - extra
    return np.array([bound] + holding)


def uneven(key, amount, total, bound, slope):
    if amount == 2:
        one = jax.random.randint(key, (), max(1, total - bound), min(bound, total - 1) + 1)
        return jnp.stack([one, total - one])
    sizes = jnp.asarray(split_up(amount, total, bound, slope), jnp.int32)
    couples = (amount - 1) // 2
    donor, receiver = sizes[1:1 + 2 * couples:2], sizes[2:2 + 2 * couples:2]
    room = jnp.minimum(donor - 1, bound - receiver)
    passed = jax.random.randint(jax.random.fold_in(key, 1), (couples,), 0, 1 << 20) % (room + 1)
    sizes = sizes.at[1:1 + 2 * couples:2].set(donor - passed).at[2:2 + 2 * couples:2].set(receiver + passed)
    return sizes[jax.random.permutation(jax.random.fold_in(key, 2), amount)]


def gaussian(rng, shape, spread, limit, shards=(), kind=jnp.bfloat16):
    entries = jax.random.normal(rng, shape, jnp.float32) * spread
    if len(shards) > 0:
        entries = level_of(rng, shape, shards, -0.22, 0.18) * entries
    return jnp.clip(entries, min=-limit, max=limit).astype(kind)


def setup_inputs(seed: int = 0) -> dict:
    key_of = jax.random.split(jax.random.key(seed), 13)
    return {
        "hidden_in": gaussian(key_of[0], (ROWS, LEN, D), 1.0, 6.0, ((0, 2), (1, 16))),
        "doc_lengths": jax.vmap(lambda own: uneven(own, DOCS, LEN, MOST, 2))(jax.random.split(key_of[1], ROWS)).reshape((ROWS, DOCS)).astype(jnp.int32),
        "w_query": gaussian(key_of[2], (D, H * HD), D ** -0.5, 0.125, ((0, 4), (1, 4))),
        "w_key": gaussian(key_of[3], (D, KV * HD), D ** -0.5, 0.125, ((0, 4),)),
        "w_value": gaussian(key_of[4], (D, KV * HD), D ** -0.5, 0.125, ((0, 4),)),
        "w_output": gaussian(key_of[5], (H * HD, D), (H * HD // 64) ** -0.5, 1.0, ((0, 4), (1, 4))),
        "w_gate": gaussian(key_of[6], (D, FF), D ** -0.5, 0.125, ((0, 4), (1, 4))),
        "w_up": gaussian(key_of[7], (D, FF), D ** -0.5, 0.125, ((0, 4), (1, 4))),
        "w_down": gaussian(key_of[8], (FF, D), FF ** -0.5, 0.0625, ((0, 4), (1, 4))),
        "gain_attn": jnp.clip(1.0 + 0.1 * jax.random.normal(key_of[9], (D,), jnp.float32), 0.5, 1.5),
        "gain_ffn": jnp.clip(1.0 + 0.1 * jax.random.normal(key_of[10], (D,), jnp.float32), 0.5, 1.5),
        "grad_out": draw_grad_out(jax.random.fold_in(key_of[12], 71), 0),
    }


norm_eps = 1e-05
masked_score = -1e+30
highest = lax.Precision.HIGHEST

@jax.custom_vjp
def low(v):
    return lax.optimization_barrier(v.astype(jnp.bfloat16)).astype(jnp.float32)

@jax.custom_vjp
def low_back(v):
    return v

def low_keep(v):
    return (low(v), None)

def low_pass(kept, grad):
    return (grad,)

def back_keep(v):
    return (v, None)

def back_low(kept, grad):
    return (low(grad),)
low.defvjp(low_keep, low_pass)
low_back.defvjp(back_keep, back_low)

def inverse_freq():
    listed = []
    for pair_index in range(HD // 2):
        base_freq = 500000.0 ** (-2.0 * pair_index / HD)
        wavelength = 2.0 * math.pi / base_freq
        smoothing = (8192.0 / wavelength - 1.0) / 3.0
        blended = (1.0 - smoothing) * base_freq / 32.0 + smoothing * base_freq
        if wavelength < 2048.0:
            listed.append(base_freq)
        elif wavelength > 8192.0:
            listed.append(base_freq / 32.0)
        else:
            listed.append(blended)
    return jnp.asarray(listed, dtype=jnp.float32)

def rotate(values, cosine_table, sine_table):
    half_dim = HD // 2
    first_half = values[..., :half_dim]
    second_half = values[..., half_dim:]
    return jnp.concatenate([first_half * cosine_table - second_half * sine_table, second_half * cosine_table + first_half * sine_table], axis=-1)

def doc_layout(lengths_row, token_ids):
    ends_at = jnp.cumsum(lengths_row, dtype=jnp.int32).astype(jnp.int32)
    starts_at = (ends_at - lengths_row).astype(jnp.int32)
    inside = (token_ids[:, None] >= starts_at[None, :]) & (token_ids[:, None] < ends_at[None, :])
    doc_start = lax.optimization_barrier(jnp.sum(jnp.where(inside, starts_at[None, :], 0), axis=1, dtype=jnp.int32)).astype(jnp.int32)
    return (doc_start, (token_ids - doc_start).astype(jnp.int32))

def copy_heads():
    query_heads = H // N_WID
    group_size = H // KV
    kv_local = max(query_heads // group_size, 1)
    per_copy = query_heads // kv_local
    copy_head = jnp.asarray([copy_id // kv_local * query_heads // group_size + copy_id % kv_local for copy_id in range(N_WID * kv_local)], dtype=jnp.int32)
    head_copy = jnp.asarray([head_id // query_heads * kv_local + head_id % query_heads // per_copy for head_id in range(H)], dtype=jnp.int32)
    return (copy_head, head_copy)

def row_forward(hidden_row, lengths_row, query_weight, key_weight, value_weight, output_weight, gate_weight, up_weight, down_weight, gain_attn, gain_ffn):
    row_length = hidden_row.shape[0]
    copy_head, head_copy = copy_heads()
    copies = copy_head.shape[0]
    token_ids = jnp.arange(row_length, dtype=jnp.int32)
    doc_start, places = doc_layout(lengths_row, token_ids)
    angles = places.astype(jnp.float32)[:, None] * inverse_freq()[None, :]
    cosine_table = jnp.cos(angles)[:, None, :]
    sine_table = jnp.sin(angles)[:, None, :]
    root_attn = lax.rsqrt(lax.optimization_barrier(jnp.mean(hidden_row * hidden_row, axis=-1, keepdims=True)) + norm_eps)
    normed_attn = low(hidden_row * root_attn * gain_attn)
    key_copies = key_weight.reshape(D, KV, HD)[:, copy_head, :].reshape(D, copies * HD)
    value_copies = value_weight.reshape(D, KV, HD)[:, copy_head, :].reshape(D, copies * HD)
    query_pre = low_back(jnp.dot(normed_attn, query_weight, precision=highest))
    key_pre = low_back(jnp.dot(normed_attn, key_copies, precision=highest))
    value_rows = low(low_back(jnp.dot(normed_attn, value_copies, precision=highest)))
    query_rot = low(rotate(query_pre.reshape(row_length, H, HD), cosine_table, sine_table))
    key_rot = low(rotate(key_pre.reshape(row_length, copies, HD), cosine_table, sine_table))
    key_heads = key_rot[:, head_copy, :]
    value_heads = value_rows.reshape(row_length, copies, HD)[:, head_copy, :]
    block_size = min(512, row_length)
    block_count = row_length // block_size
    attn_scale = HD ** (-0.5)

    def attend_block(block_index):
        row_first = block_index * block_size
        query_part = lax.dynamic_slice_in_dim(query_rot, row_first, block_size, 0)
        query_ids = lax.dynamic_slice_in_dim(token_ids, row_first, block_size, 0)
        query_starts = lax.dynamic_slice_in_dim(doc_start, row_first, block_size, 0)
        scores = low_back(jnp.einsum('qhd,khd->hqk', query_part, key_heads, precision=highest) * attn_scale)
        allowed = (token_ids[None, :] <= query_ids[:, None]) & (token_ids[None, :] >= query_starts[:, None])
        scores = jnp.where(allowed[None, :, :], scores, masked_score)
        row_max = lax.optimization_barrier(jnp.max(scores, axis=-1, keepdims=True))
        exp_scores = jnp.exp(scores - row_max)
        probability = low(exp_scores / lax.optimization_barrier(jnp.sum(exp_scores, axis=-1, keepdims=True)))
        return jnp.einsum('hqk,khd->qhd', probability, value_heads, precision=highest)
    attended = lax.map(jax.checkpoint(attend_block), jnp.arange(block_count, dtype=jnp.int32))
    attended = low(low_back(attended.reshape(row_length, H * HD)))
    branch_attn = low_back(jnp.dot(attended, output_weight, precision=highest))
    middle = hidden_row + branch_attn
    root_ffn = lax.rsqrt(lax.optimization_barrier(jnp.mean(middle * middle, axis=-1, keepdims=True)) + norm_eps)
    normed_ffn = low(middle * root_ffn * gain_ffn)
    gate_proj = low_back(jnp.dot(normed_ffn, gate_weight, precision=highest))
    up_proj = low_back(jnp.dot(normed_ffn, up_weight, precision=highest))
    activated = low(jax.nn.silu(gate_proj) * up_proj)
    branch_ffn = low_back(jnp.dot(activated, down_weight, precision=highest))
    return middle + branch_ffn

def reference(hidden_in, doc_lengths, w_query, w_key, w_value, w_output, w_gate, w_up, w_down, gain_attn, gain_ffn, grad_out):

    def forward(hidden_all, query_weight, key_weight, value_weight, output_weight, gate_weight, up_weight, down_weight, gain_first, gain_second):
        outputs = [row_forward(hidden_all[row_index], doc_lengths[row_index], query_weight, key_weight, value_weight, output_weight, gate_weight, up_weight, down_weight, gain_first, gain_second) for row_index in range(hidden_all.shape[0])]
        return jnp.stack(outputs)
    inputs_f = (hidden_in.astype(jnp.float32), w_query.astype(jnp.float32), w_key.astype(jnp.float32), w_value.astype(jnp.float32), w_output.astype(jnp.float32), w_gate.astype(jnp.float32), w_up.astype(jnp.float32), w_down.astype(jnp.float32), gain_attn.astype(jnp.float32), gain_ffn.astype(jnp.float32))
    result, pullback = jax.vjp(forward, *inputs_f)
    gradients = pullback(grad_out.astype(jnp.float32))
    return (result.astype(jnp.bfloat16), gradients[0].astype(jnp.bfloat16), gradients[1], gradients[2], gradients[3], gradients[4], gradients[5], gradients[6], gradients[7], gradients[8], gradients[9])
```

```python
import math

import jax
import jax.numpy as jnp
from jax import lax
from jax.experimental import pallas as pl
from jax.experimental.pallas import tpu as pltpu
from jax.sharding import PartitionSpec as P

H = 32
KV = 8
HD = 64


norm_eps = 1e-05
masked_score = -1e30


def inverse_freq():
    listed = []
    for pair_index in range(HD // 2):
        base_freq = 500000.0 ** (-2.0 * pair_index / HD)
        wavelength = 2.0 * math.pi / base_freq
        smoothing = (8192.0 / wavelength - 1.0) / 3.0
        blended = (1.0 - smoothing) * base_freq / 32.0 + smoothing * base_freq
        if wavelength < 2048.0:
            listed.append(base_freq)
        elif wavelength > 8192.0:
            listed.append(base_freq / 32.0)
        else:
            listed.append(blended)
    return jnp.asarray(listed, dtype=jnp.float32)


def rotate(values, cosine_table, sine_table):
    half_dim = HD // 2
    first_half = values[..., :half_dim]
    second_half = values[..., half_dim:]
    return jnp.concatenate(
        [
            first_half * cosine_table - second_half * sine_table,
            second_half * cosine_table + first_half * sine_table,
        ],
        axis=-1,
    )


def rotate_back(grads_in, cosine_table, sine_table):
    half_dim = HD // 2
    first_half = grads_in[..., :half_dim]
    second_half = grads_in[..., half_dim:]
    return jnp.concatenate(
        [
            first_half * cosine_table + second_half * sine_table,
            second_half * cosine_table - first_half * sine_table,
        ],
        axis=-1,
    )


def doc_layout(lengths_row, token_ids):
    ends_at = jnp.cumsum(lengths_row, dtype=jnp.int32)
    starts_at = ends_at - lengths_row
    inside = (token_ids[:, None] >= starts_at[None, :]) & (token_ids[:, None] < ends_at[None, :])
    doc_start = jnp.sum(jnp.where(inside, starts_at[None, :], 0), axis=1, dtype=jnp.int32)
    return (doc_start, token_ids - doc_start)


def norm_forward(values, gain_vector):
    root_inv = lax.rsqrt(jnp.mean(values * values, axis=-1, keepdims=True) + norm_eps)
    return (root_inv, (values * root_inv * gain_vector).astype(jnp.bfloat16))


def norm_backward(values, root_inv, gain_vector, grad_normed):
    weighted = grad_normed * gain_vector
    inner_sum = jnp.mean(weighted * values, axis=-1, keepdims=True)
    grad_values = root_inv * weighted - values * (root_inv * root_inv * root_inv) * inner_sum
    gain_term = jnp.sum(grad_normed * values * root_inv, axis=0)
    return (grad_values, gain_term)


def contract_last(left_side, right_side):
    return lax.dot_general(
        left_side, right_side, (((1,), (1,)), ((), ())), preferred_element_type=jnp.float32
    )


def contract_first(left_side, right_side):
    return lax.dot_general(
        left_side, right_side, (((0,), (0,)), ((), ())), preferred_element_type=jnp.float32
    )


def local(
    hidden_in,
    doc_lengths,
    w_query,
    w_key,
    w_value,
    w_output,
    w_gate,
    w_up,
    w_down,
    gain_attn,
    gain_ffn,
    grad_out,
):
    wid_count = lax.axis_size("wid")
    nar_count = lax.axis_size("nar")
    wid_index = lax.axis_index("wid")
    nar_index = lax.axis_index("nar")
    local_tokens = hidden_in.shape[1]
    block_tokens = local_tokens * wid_count
    seq_length = block_tokens * nar_count
    query_heads = w_query.shape[1] // HD
    group_size = H // KV
    kv_local = max(query_heads // group_size, 1)
    heads_per_kv = query_heads // kv_local
    kv_first = wid_index * query_heads // group_size
    query_block = min(512, block_tokens)
    block_count = block_tokens // query_block
    item_count = block_count * query_heads
    attn_scale = HD ** (-0.5)
    query_full, key_full, value_full, output_full, gate_full, up_full, down_full = (
        lax.all_gather(w_query, "nar", axis=0, tiled=True),
        lax.all_gather(w_key, "nar", axis=0, tiled=True),
        lax.all_gather(w_value, "nar", axis=0, tiled=True),
        lax.all_gather(w_output, "nar", axis=1, tiled=True),
        lax.all_gather(w_gate, "nar", axis=0, tiled=True),
        lax.all_gather(w_up, "nar", axis=0, tiled=True),
        lax.all_gather(w_down, "nar", axis=1, tiled=True),
    )
    key_local = lax.dynamic_slice_in_dim(key_full, kv_first * HD, kv_local * HD, 1)
    value_local = lax.dynamic_slice_in_dim(value_full, kv_first * HD, kv_local * HD, 1)
    token_ids = nar_index * block_tokens + jnp.arange(block_tokens, dtype=jnp.int32)
    doc_start, places = doc_layout(doc_lengths[0], token_ids)
    angles = places.astype(jnp.float32)[:, None] * inverse_freq()[None, :]
    cosine_table = jnp.cos(angles)[:, None, :]
    sine_table = jnp.sin(angles)[:, None, :]
    key_ids = jnp.arange(seq_length, dtype=jnp.int32)
    residual = hidden_in[0].astype(jnp.float32)
    root_attn, normed_attn = norm_forward(residual, gain_attn)
    normed_rows = lax.all_gather(normed_attn, "wid", axis=0, tiled=True)
    query_pre = jnp.dot(normed_rows, query_full, preferred_element_type=jnp.float32)
    key_pre = jnp.dot(normed_rows, key_local, preferred_element_type=jnp.float32)
    value_rows = jnp.dot(normed_rows, value_local, preferred_element_type=jnp.float32).astype(
        jnp.bfloat16
    )
    query_rot = (
        rotate(query_pre.reshape(block_tokens, query_heads, HD), cosine_table, sine_table)
        .astype(jnp.bfloat16)
        .reshape(block_tokens, query_heads * HD)
    )
    key_rot = (
        rotate(key_pre.reshape(block_tokens, kv_local, HD), cosine_table, sine_table)
        .astype(jnp.bfloat16)
        .reshape(block_tokens, kv_local * HD)
    )
    key_seq, value_seq = (
        lax.all_gather(key_rot, "nar", axis=0, tiled=True),
        lax.all_gather(value_rows, "nar", axis=0, tiled=True),
    )

    def item_inputs(item_index):
        block_index = item_index // query_heads
        head_index = item_index % query_heads
        kv_index = head_index // heads_per_kv
        row_first = block_index * query_block
        query_part = lax.dynamic_slice(query_rot, (row_first, head_index * HD), (query_block, HD))
        key_head = lax.dynamic_slice_in_dim(key_seq, kv_index * HD, HD, 1)
        value_head = lax.dynamic_slice_in_dim(value_seq, kv_index * HD, HD, 1)
        query_ids = lax.dynamic_slice_in_dim(token_ids, row_first, query_block, 0)
        query_starts = lax.dynamic_slice_in_dim(doc_start, row_first, query_block, 0)
        allowed = (key_ids[None, :] <= query_ids[:, None]) & (
            key_ids[None, :] >= query_starts[:, None]
        )
        scores = contract_last(query_part, key_head) * attn_scale
        return (
            row_first,
            head_index,
            kv_index,
            query_part,
            key_head,
            value_head,
            jnp.where(allowed, scores, masked_score),
        )

    def attend(item_index):
        row_first, head_index, kv_index, query_part, key_head, value_head, scores = item_inputs(
            item_index
        )
        row_max = jnp.max(scores, axis=1, keepdims=True)
        exp_scores = jnp.exp(scores - row_max)
        row_total = jnp.sum(exp_scores, axis=1, keepdims=True)
        probability = (exp_scores / row_total).astype(jnp.bfloat16)
        attended = jnp.dot(probability, value_head, preferred_element_type=jnp.float32)
        return (attended, (row_max + jnp.log(row_total))[:, 0])

    attended_items, logsum_items = lax.map(attend, jnp.arange(item_count, dtype=jnp.int32))
    attended_rows = (
        attended_items.reshape(block_count, query_heads, query_block, HD)
        .transpose(0, 2, 1, 3)
        .reshape(block_tokens, query_heads * HD)
        .astype(jnp.bfloat16)
    )
    rows_here = attended_rows
    branch_attn = lax.psum_scatter(
        jnp.dot(rows_here, output_full, preferred_element_type=jnp.float32),
        "wid",
        scatter_dimension=0,
        tiled=True,
    )
    middle = residual + branch_attn
    root_ffn, normed_ffn = norm_forward(middle, gain_ffn)
    ffn_rows = lax.all_gather(normed_ffn, "wid", axis=0, tiled=True)
    gate_proj = jnp.dot(ffn_rows, gate_full, preferred_element_type=jnp.float32)
    up_proj = jnp.dot(ffn_rows, up_full, preferred_element_type=jnp.float32)
    gate_sigmoid = jax.nn.sigmoid(gate_proj)
    gate_silu = gate_proj * gate_sigmoid
    activated = (gate_silu * up_proj).astype(jnp.bfloat16)
    rows_here = activated
    branch_ffn = lax.psum_scatter(
        jnp.dot(rows_here, down_full, preferred_element_type=jnp.float32).astype(jnp.bfloat16),
        "wid",
        scatter_dimension=0,
        tiled=True,
    ).astype(jnp.float32)
    hidden_out = (middle + branch_ffn).astype(jnp.bfloat16)[None]
    grad_top = grad_out[0]
    grad_rows = lax.all_gather(grad_top, "wid", axis=0, tiled=True)
    grad_activated = contract_last(grad_rows, down_full)
    down_weight_grad = contract_first(activated, grad_rows)
    silu_slope = gate_sigmoid * (1.0 + gate_proj * (1.0 - gate_sigmoid))
    grad_gate_b = (grad_activated * up_proj * silu_slope).astype(jnp.bfloat16)
    grad_up_b = (grad_activated * gate_silu).astype(jnp.bfloat16)
    gate_weight_grad = contract_first(ffn_rows, grad_gate_b)
    up_weight_grad = contract_first(ffn_rows, grad_up_b)
    grad_normed_ffn = lax.psum_scatter(
        contract_last(grad_gate_b, gate_full) + contract_last(grad_up_b, up_full),
        "wid",
        scatter_dimension=0,
        tiled=True,
    )
    grad_middle, gain_ffn_term = norm_backward(middle, root_ffn, gain_ffn, grad_normed_ffn)
    grad_middle = grad_middle + grad_top.astype(jnp.float32)
    grad_branch = grad_middle.astype(jnp.bfloat16)
    branch_rows = lax.all_gather(grad_branch, "wid", axis=0, tiled=True)
    grad_attended = contract_last(branch_rows, output_full).astype(jnp.bfloat16)
    output_weight_grad = contract_first(attended_rows, branch_rows)

    def attend_back(carried, item_index):
        key_grad, value_grad = carried
        row_first, head_index, kv_index, query_part, key_head, value_head, scores = item_inputs(
            item_index
        )
        logsum = lax.dynamic_index_in_dim(logsum_items, item_index, 0, keepdims=False)
        probability = jnp.exp(scores - logsum[:, None])
        grad_part = lax.dynamic_slice(
            grad_attended, (row_first, head_index * HD), (query_block, HD)
        )
        grad_prob = contract_last(grad_part, value_head)
        inner_sum = jnp.sum(probability * grad_prob, axis=1, keepdims=True)
        grad_scores = (probability * (grad_prob - inner_sum)).astype(jnp.bfloat16)
        query_grad = jnp.dot(grad_scores, key_head, preferred_element_type=jnp.float32) * attn_scale
        key_part = contract_first(grad_scores, query_part) * attn_scale
        value_part = contract_first(probability.astype(jnp.bfloat16), grad_part)
        key_old = lax.dynamic_slice_in_dim(key_grad, kv_index * HD, HD, 1)
        key_grad = lax.dynamic_update_slice_in_dim(key_grad, key_old + key_part, kv_index * HD, 1)
        value_old = lax.dynamic_slice_in_dim(value_grad, kv_index * HD, HD, 1)
        value_grad = lax.dynamic_update_slice_in_dim(
            value_grad, value_old + value_part, kv_index * HD, 1
        )
        return ((key_grad, value_grad), query_grad)

    zero_grads = jnp.zeros((seq_length, kv_local * HD), jnp.float32)
    (key_grad_seq, value_grad_seq), query_grad_items = lax.scan(
        attend_back, (zero_grads, zero_grads), jnp.arange(item_count, dtype=jnp.int32)
    )
    key_grad_block, value_grad_block = (
        lax.psum_scatter(
            key_grad_seq.astype(jnp.bfloat16), "nar", scatter_dimension=0, tiled=True
        ).astype(jnp.float32),
        lax.psum_scatter(
            value_grad_seq.astype(jnp.bfloat16), "nar", scatter_dimension=0, tiled=True
        ).astype(jnp.float32),
    )
    query_grad_rows = (
        query_grad_items.reshape(block_count, query_heads, query_block, HD)
        .transpose(0, 2, 1, 3)
        .reshape(block_tokens, query_heads, HD)
    )
    query_grad_b = (
        rotate_back(query_grad_rows, cosine_table, sine_table)
        .astype(jnp.bfloat16)
        .reshape(block_tokens, query_heads * HD)
    )
    key_grad_b = (
        rotate_back(key_grad_block.reshape(block_tokens, kv_local, HD), cosine_table, sine_table)
        .astype(jnp.bfloat16)
        .reshape(block_tokens, kv_local * HD)
    )
    value_grad_b = value_grad_block.astype(jnp.bfloat16)
    query_weight_grad = contract_first(normed_rows, query_grad_b)
    key_weight_grad = contract_first(normed_rows, key_grad_b)
    value_weight_grad = contract_first(normed_rows, value_grad_b)
    grad_normed_attn = lax.psum_scatter(
        (
            contract_last(query_grad_b, query_full)
            + contract_last(key_grad_b, key_local)
            + contract_last(value_grad_b, value_local)
        ).astype(jnp.bfloat16),
        "wid",
        scatter_dimension=0,
        tiled=True,
    ).astype(jnp.float32)
    grad_residual, gain_attn_term = norm_backward(residual, root_attn, gain_attn, grad_normed_attn)
    grad_in = (grad_residual + grad_middle).astype(jnp.bfloat16)[None]
    summed = (
        lax.psum_scatter(
            query_weight_grad.astype(jnp.bfloat16), ("row", "nar"), scatter_dimension=0, tiled=True
        ).astype(jnp.float32),
        lax.psum_scatter(
            key_weight_grad.astype(jnp.bfloat16), ("row", "nar"), scatter_dimension=0, tiled=True
        ).astype(jnp.float32),
        lax.psum_scatter(
            value_weight_grad.astype(jnp.bfloat16), ("row", "nar"), scatter_dimension=0, tiled=True
        ).astype(jnp.float32),
        lax.psum_scatter(
            output_weight_grad.astype(jnp.bfloat16), ("row", "nar"), scatter_dimension=1, tiled=True
        ).astype(jnp.float32),
        lax.psum_scatter(
            gate_weight_grad.astype(jnp.bfloat16), ("row", "nar"), scatter_dimension=0, tiled=True
        ).astype(jnp.float32),
        lax.psum_scatter(
            up_weight_grad.astype(jnp.bfloat16), ("row", "nar"), scatter_dimension=0, tiled=True
        ).astype(jnp.float32),
        lax.psum_scatter(
            down_weight_grad.astype(jnp.bfloat16), ("row", "nar"), scatter_dimension=1, tiled=True
        ).astype(jnp.float32),
        lax.psum_scatter(
            gain_attn_term.astype(jnp.bfloat16), ("row", "nar"), scatter_dimension=0, tiled=True
        ).astype(jnp.float32),
        lax.psum_scatter(
            gain_ffn_term.astype(jnp.bfloat16), ("row", "nar"), scatter_dimension=0, tiled=True
        ).astype(jnp.float32),
    )
    (
        grad_query,
        key_sum,
        value_sum,
        grad_output,
        grad_gate,
        grad_up,
        grad_down,
        gain_attn_sum,
        gain_ffn_sum,
    ) = summed
    key_all, value_all, gain_attn_all, gain_ffn_all = (
        lax.all_gather(key_sum.astype(jnp.bfloat16), "wid", axis=1, tiled=True).astype(
            key_sum.dtype
        ),
        lax.all_gather(value_sum.astype(jnp.bfloat16), "wid", axis=1, tiled=True).astype(
            value_sum.dtype
        ),
        lax.all_gather(gain_attn_sum.astype(jnp.bfloat16), "wid", axis=0, tiled=True).astype(
            gain_attn_sum.dtype
        ),
        lax.all_gather(gain_ffn_sum.astype(jnp.bfloat16), "wid", axis=0, tiled=True).astype(
            gain_ffn_sum.dtype
        ),
    )
    shard_rows = key_sum.shape[0]
    repeats = wid_count * kv_local // KV
    grad_key = key_all.reshape(shard_rows, KV, repeats, HD).sum(axis=2).reshape(shard_rows, KV * HD)
    grad_value = (
        value_all.reshape(shard_rows, KV, repeats, HD).sum(axis=2).reshape(shard_rows, KV * HD)
    )
    grad_gain_attn = gain_attn_all.reshape(wid_count, shard_rows).sum(axis=0)
    grad_gain_ffn = gain_ffn_all.reshape(wid_count, shard_rows).sum(axis=0)
    return (
        hidden_out,
        grad_in,
        grad_query,
        grad_key,
        grad_value,
        grad_output,
        grad_gate,
        grad_up,
        grad_down,
        grad_gain_attn,
        grad_gain_ffn,
    )


MESH = pl.DeviceIdType.MESH
bf16 = jnp.bfloat16
f32 = jnp.float32
VMEM_LIMIT = 60 * 2**20


def spot():
    return lax.axis_index("row"), lax.axis_index("nar"), lax.axis_index("wid")


def greet(partners):
    barrier = pltpu.get_barrier_semaphore()
    total = 0
    for there, device in partners:
        @pl.when(there)
        def _():
            pl.semaphore_signal(barrier, inc=1, device_id=device, device_id_type=MESH)

        total = total + there.astype(jnp.int32)
    pl.semaphore_wait(barrier, total)


def line_partners(r, n, w, wid_count):
    return [
        (w < wid_count - 1, (r, n, jnp.minimum(w + 1, wid_count - 1))),
        (w > 0, (r, n, jnp.maximum(w - 1, 0))),
        (w >= 0, (1 - r, n, w)),
    ]


def each_rows(count, step, body):
    def run(i, carry):
        body(pl.ds(pl.multiple_of(i * step, step), step))
        return carry

    lax.fori_loop(0, count // step, run, 0)


class Gather:
    def __init__(self, buf, sems, me, wid_count):
        self.buf, (self.up_s, self.dn_s, self.pt_s, self.got) = buf, sems
        self.r, self.n, self.w = me
        self.last = wid_count - 1
        self.up = (self.r, self.n, jnp.minimum(self.w + 1, self.last))
        self.dn = (self.r, self.n, jnp.maximum(self.w - 1, 0))
        self.pt = (1 - self.r, self.n, self.w)

    def copy(self, j, sem, device, row=None):
        row = self.r if row is None else row
        return pltpu.make_async_remote_copy(
            self.buf.at[row, j],
            self.buf.at[row, j],
            sem.at[j],
            self.got.at[row, j],
            device_id=device,
            device_id_type=MESH,
        )

    def pass_on(self, j, go_up, go_dn):
        if go_up:
            @pl.when(self.w < self.last)
            def _():
                self.copy(j, self.up_s, self.up).start()

        if go_dn:
            @pl.when(self.w > 0)
            def _():
                self.copy(j, self.dn_s, self.dn).start()

        self.copy(j, self.pt_s, self.pt).start()

    def own(self):
        self.pass_on(self.w, True, True)

    def arrive(self, row, j):
        self.copy(j, self.pt_s, self.pt, row).wait_recv()

    def step(self, k):
        below, above = self.w - k, self.w + k

        @pl.when(below >= 0)
        def _():
            self.arrive(self.r, below)
            self.pass_on(below, True, False)

        @pl.when(above <= self.last)
        def _():
            self.arrive(self.r, above)
            self.pass_on(above, False, True)

    def rest(self):
        for j in range(self.last + 1):
            self.arrive(1 - self.r, j)

    def sent(self):
        for j in range(self.last + 1):
            @pl.when((j <= self.w) & (self.w < self.last))
            def _():
                self.copy(j, self.up_s, self.up).wait_send()

            @pl.when((j >= self.w) & (self.w > 0))
            def _():
                self.copy(j, self.dn_s, self.dn).wait_send()

            self.copy(j, self.pt_s, self.pt).wait_send()


def gather_scratch(shard, width):
    return [pltpu.VMEM((2, 4, shard, width), bf16)] + gather_sems()


def gather_sems():
    return [pltpu.SemaphoreType.DMA((4,))] * 3 + [pltpu.SemaphoreType.DMA((2, 4))]


class Scatter:
    def __init__(self, mine, theirs, bufs, sems, me, wid_count):
        self.mine, self.theirs = mine, theirs
        self.from_pt, self.from_up, self.from_dn = bufs
        self.pt_s, self.pt_g, self.up_s, self.up_g, self.dn_s, self.dn_g = sems
        self.r, self.n, self.w = me
        self.last = wid_count - 1
        self.up = (self.r, self.n, jnp.minimum(self.w + 1, self.last))
        self.dn = (self.r, self.n, jnp.maximum(self.w - 1, 0))
        self.pt = (1 - self.r, self.n, self.w)

    def order(self, i):
        low, high = (3, 0, 2, 1)[i], (0, 3, 1, 2)[i]
        return jnp.where(self.w < 2, low, high)

    def pair(self, s):
        return pltpu.make_async_remote_copy(
            self.theirs.at[s], self.from_pt.at[s], self.pt_s.at[s], self.pt_g.at[s],
            device_id=self.pt, device_id_type=MESH,
        )

    def climb(self, s):
        return pltpu.make_async_remote_copy(
            self.mine.at[s], self.from_dn.at[s], self.up_s.at[s], self.up_g.at[s],
            device_id=self.up, device_id_type=MESH,
        )

    def fall(self, s):
        return pltpu.make_async_remote_copy(
            self.mine.at[s], self.from_up.at[s], self.dn_s.at[s], self.dn_g.at[s],
            device_id=self.dn, device_id_type=MESH,
        )

    def add(self, s, others):
        def body(rows):
            total = self.mine[s, rows, :].astype(f32)
            for other in others:
                total = total + other[s, rows, :].astype(f32)
            self.mine[s, rows, :] = total.astype(bf16)

        each_rows(self.mine.shape[1], 16, body)

    def step(self, s):
        self.pair(s).wait_recv()

        @pl.when((s > self.w) & (self.w > 0))
        def _():
            self.climb(s).wait_recv()
            self.add(s, (self.from_pt, self.from_dn))

        @pl.when((s < self.w) & (self.w < self.last))
        def _():
            self.fall(s).wait_recv()
            self.add(s, (self.from_pt, self.from_up))

        @pl.when(((s > self.w) & (self.w == 0)) | ((s < self.w) & (self.w == self.last)))
        def _():
            self.add(s, (self.from_pt,))

        @pl.when(s > self.w)
        def _():
            self.climb(s).start()

        @pl.when(s < self.w)
        def _():
            self.fall(s).start()

    def total(self, out):
        w = self.w

        def first(rows):
            out[rows, :] = self.mine[w, rows, :].astype(f32) + self.from_pt[w, rows, :].astype(f32)

        each_rows(out.shape[0], 16, first)

        @pl.when(w > 0)
        def _():
            self.climb(w).wait_recv()

            def more(rows):
                out[rows, :] += self.from_dn[w, rows, :].astype(f32)

            each_rows(out.shape[0], 16, more)

        @pl.when(w < self.last)
        def _():
            self.fall(w).wait_recv()

            def more(rows):
                out[rows, :] += self.from_up[w, rows, :].astype(f32)

            each_rows(out.shape[0], 16, more)

    def sent(self):
        for s in range(self.last + 1):
            self.pair(s).wait_send()

            @pl.when(s > self.w)
            def _():
                self.climb(s).wait_send()

            @pl.when(s < self.w)
            def _():
                self.fall(s).wait_send()


def scatter_bufs(shard, width):
    return [pltpu.VMEM((4, shard, width), bf16)] * 3


def scatter_sems():
    return [pltpu.SemaphoreType.DMA((4,))] * 6


def vmem():
    return pl.BlockSpec(memory_space=pltpu.VMEM)


def hbm():
    return pl.BlockSpec(memory_space=pl.ANY)


def comm_call(kernel, name, cid, out_shape, in_specs, out_specs, scratch, args, flops=0, sent=0):
    return pl.pallas_call(
        kernel,
        out_shape=out_shape,
        in_specs=in_specs,
        out_specs=out_specs,
        scratch_shapes=scratch,
        compiler_params=pltpu.CompilerParams(
            collective_id=cid, has_side_effects=True, vmem_limit_bytes=VMEM_LIMIT
        ),
        cost_estimate=pl.CostEstimate(flops=flops, bytes_accessed=sent, transcendentals=0),
        name=name,
    )(*args)


def norm_rows(x, gain):
    root = lax.rsqrt(jnp.mean(x * x, axis=-1, keepdims=True) + norm_eps)
    return x * root * gain


def turn(x, cosine, sine):
    lane = lax.broadcasted_iota(jnp.int32, x.shape, 1)
    swapped = jnp.where(lane % 64 < 32, pltpu.roll(x, 96, 1), pltpu.roll(x, 32, 1))
    return x * cosine + swapped * sine


def enter_kernel(hidden, gain, tab, rows_out, tabs_out, buf, up_s, dn_s, pt_s, got, tabs, tab_s, tab_g, out_s):
    me = spot()
    r, n, w = me
    greet(line_partners(r, n, w, 4))
    gather = Gather(buf, (up_s, dn_s, pt_s, got), me, 4)
    tab_copy = pltpu.make_async_remote_copy(
        tab, tabs.at[r], tab_s, tab_g, device_id=(1 - r, n, w), device_id_type=MESH
    )

    def body(rows):
        buf[r, w, rows, :] = norm_rows(hidden[rows, :].astype(f32), gain[...]).astype(bf16)

    each_rows(hidden.shape[0], 16, body)
    gather.own()
    tab_copy.start()

    def keep(rows):
        tabs[r, rows, :] = tab[rows, :]

    each_rows(tab.shape[0], 16, keep)
    for k in (1, 2, 3):
        gather.step(k)
    gather.rest()
    out = pltpu.make_async_copy(buf, rows_out, out_s.at[0])
    out.start()
    tab_copy.wait_recv()
    out_tab = pltpu.make_async_copy(tabs, tabs_out, out_s.at[1])
    out_tab.start()
    gather.sent()
    tab_copy.wait_send()
    out.wait()
    out_tab.wait()


def enter(hidden, gain, tab):
    shard, width = hidden.shape
    return comm_call(
        enter_kernel, "enter", 1,
        (
            jax.ShapeDtypeStruct((2, 4, shard, width), bf16),
            jax.ShapeDtypeStruct((2,) + tab.shape, f32),
        ),
        [vmem()] * 3, [hbm()] * 2,
        gather_scratch(shard, width)
        + [
            pltpu.VMEM((2,) + tab.shape, f32),
            pltpu.SemaphoreType.DMA(()),
            pltpu.SemaphoreType.DMA(()),
            pltpu.SemaphoreType.DMA((2,)),
        ],
        (hidden, gain, tab), flops=10**10, sent=10**8,
    )


def nar_device(r, n, w, by):
    return (r, jnp.clip(n + by, 0, 3), w)


def project_kernel(x, p1, tabs, q_out, kv_out, kv, s_s, s_g, out_s):
    r, n, w = spot()
    greet(
        [
            (n >= 1, nar_device(r, n, w, -1)),
            (n >= 2, nar_device(r, n, w, -2)),
            (n <= 2, nar_device(r, n, w, 1)),
            (n <= 1, nar_device(r, n, w, 2)),
        ]
    )

    def copy(row, slot, by):
        return pltpu.make_async_remote_copy(
            kv.at[row, 2], kv.at[row, slot], s_s.at[row, slot], s_g.at[row, slot],
            device_id=nar_device(r, n, w, by), device_id_type=MESH,
        )

    lane = lax.broadcasted_iota(jnp.int32, (256, 128), 1)
    weight = p1[:, :, 0:384].reshape(2048, 384)
    for row in range(2):
        def tile(i, carry):
            rows = pl.ds(pl.multiple_of(i * 256, 256), 256)
            cosine, sine = tabs[row, rows, 0:128], tabs[row, rows, 128:256]
            pre = jnp.dot(x[row, rows, :], weight, preferred_element_type=f32)
            q_out[row, rows, 0:128] = turn(pre[:, 0:128], cosine, sine).astype(bf16)
            q_out[row, rows, 128:256] = turn(pre[:, 128:256], cosine, sine).astype(bf16)
            both = pre[:, 256:384]
            kv[row, 2, rows, :] = jnp.where(lane < 64, turn(both, cosine, sine), both).astype(bf16)
            return carry

        lax.fori_loop(0, 2, tile, 0)

        @pl.when(n <= 2)
        def _():
            copy(row, 1, 1).start()

        @pl.when(n <= 1)
        def _():
            copy(row, 0, 2).start()

        for slot, least in ((1, 1), (0, 2)):
            @pl.when(n < least)
            def _():
                kv[row, slot] = jnp.zeros((512, 128), bf16)

    for row in range(2):
        for slot, least, by in ((1, 1, 1), (0, 2, 2)):
            @pl.when(n >= least)
            def _():
                copy(row, slot, by).wait_recv()

    out = pltpu.make_async_copy(kv, kv_out, out_s)
    out.start()
    for row in range(2):
        @pl.when(n <= 2)
        def _():
            copy(row, 1, 1).wait_send()

        @pl.when(n <= 1)
        def _():
            copy(row, 0, 2).wait_send()

    out.wait()


def project(x, p1, tabs):
    return comm_call(
        project_kernel, "project", 2,
        (
            jax.ShapeDtypeStruct((2, 512, 256), bf16),
            jax.ShapeDtypeStruct((2, 3, 512, 128), bf16),
        ),
        [vmem()] * 3, [vmem(), hbm()],
        [
            pltpu.VMEM((2, 3, 512, 128), bf16),
            pltpu.SemaphoreType.DMA((2, 3)),
            pltpu.SemaphoreType.DMA((2, 3)),
            pltpu.SemaphoreType.DMA(()),
        ],
        (x, p1, tabs), flops=10**10, sent=10**7,
    )


KEYS = 256
QUERIES = 128


def stack_low(x):
    lane = lax.broadcasted_iota(jnp.int32, (QUERIES, 128), 1)
    zero = jnp.zeros((QUERIES, 128), x.dtype)
    parts = []
    for pair in range(2):
        block = x[:, pair * 128 : pair * 128 + 128]
        parts.append(jnp.where(lane < 64, block, zero))
        parts.append(jnp.where(lane < 64, pltpu.roll(block, 64, 1), zero))
    return jnp.concatenate(parts, axis=0)


def stack_high(x):
    lane = lax.broadcasted_iota(jnp.int32, (QUERIES, 128), 1)
    zero = jnp.zeros((QUERIES, 128), x.dtype)
    parts = []
    for pair in range(2):
        block = x[:, pair * 128 : pair * 128 + 128]
        parts.append(jnp.where(lane >= 64, pltpu.roll(block, 64, 1), zero))
        parts.append(jnp.where(lane >= 64, block, zero))
    return jnp.concatenate(parts, axis=0)


def unstack(x, low):
    lane = lax.broadcasted_iota(jnp.int32, (QUERIES, 128), 1)
    out = []
    for pair in range(2):
        even = x[2 * pair * QUERIES : (2 * pair + 1) * QUERIES]
        odd = x[(2 * pair + 1) * QUERIES : (2 * pair + 2) * QUERIES]
        if low:
            out.append(jnp.where(lane < 64, even, pltpu.roll(odd, 64, 1)))
        else:
            out.append(jnp.where(lane < 64, pltpu.roll(even, 64, 1), odd))
    return jnp.concatenate(out, axis=1)


def allowed_tile(starts, tile, first_query):
    key = lax.broadcasted_iota(jnp.int32, (QUERIES, KEYS), 1) + tile * KEYS
    query = lax.broadcasted_iota(jnp.int32, (QUERIES, KEYS), 0) + first_query
    start = jnp.concatenate([starts] * (KEYS // 128), axis=1)
    ok = (key <= query) & (key.astype(f32) >= start)
    return jnp.concatenate([ok] * 4, axis=0)


def key_tiles(low, row, block):
    first_query = 1024 + block * QUERIES
    return low[row * 4 + block] // KEYS, first_query // KEYS + 1, first_query


def attend_kernel(low, q, kv, starts, out, lse):
    row, block = pl.program_id(0), pl.program_id(1)
    first, end, first_query = key_tiles(low, row, block)
    query = stack_low(q[0].astype(f32)).astype(bf16)

    def body(tile, carry):
        top, total, acc = carry
        both = kv[0, pl.ds(pl.multiple_of(tile * KEYS, KEYS), KEYS), :]
        scores = contract_last(query, both) * 0.125
        ok = allowed_tile(starts[0], tile, first_query)
        scores = jnp.where(ok, scores, masked_score)
        new_top = jnp.maximum(top, jnp.max(scores, axis=1, keepdims=True))
        shrink = jnp.exp(top - new_top)
        part = jnp.exp(scores - new_top)
        total = total * shrink + jnp.sum(part, axis=1, keepdims=True)
        acc = acc * shrink + jnp.dot(part.astype(bf16), both, preferred_element_type=f32)
        return new_top, total, acc

    top, total, acc = lax.fori_loop(
        first, end, body,
        (
            jnp.full((4 * QUERIES, 1), masked_score, f32),
            jnp.zeros((4 * QUERIES, 1), f32),
            jnp.zeros((4 * QUERIES, 128), f32),
        ),
    )
    out[0] = unstack(acc / total, False).astype(bf16)
    lse[0, 0] = jnp.broadcast_to(top + jnp.log(total), (4 * QUERIES, 128))


def attend_specs():
    return [
        pl.BlockSpec((1, QUERIES, 256), lambda i, j, low: (i, j, 0)),
        pl.BlockSpec((1, 1536, 128), lambda i, j, low: (i, 0, 0)),
        pl.BlockSpec((1, QUERIES, 128), lambda i, j, low: (i, j, 2)),
    ]


def attend(low, q, kv, tabs):
    return pl.pallas_call(
        attend_kernel,
        out_shape=(
            jax.ShapeDtypeStruct((2, 512, 256), bf16),
            jax.ShapeDtypeStruct((2, 4, 4 * QUERIES, 128), f32),
        ),
        grid_spec=pltpu.PrefetchScalarGridSpec(
            num_scalar_prefetch=1, grid=(2, 4),
            in_specs=attend_specs(),
            out_specs=[
                pl.BlockSpec((1, QUERIES, 256), lambda i, j, low: (i, j, 0)),
                pl.BlockSpec((1, 1, 4 * QUERIES, 128), lambda i, j, low: (i, j, 0, 0)),
            ],
        ),
        compiler_params=pltpu.CompilerParams(vmem_limit_bytes=VMEM_LIMIT),
        cost_estimate=pl.CostEstimate(flops=2 * 10**10, bytes_accessed=10**7, transcendentals=10**7),
        name="attend",
    )(low, q, kv, tabs)


def attend_back_kernel(low, q, kv, starts, turns, att, grad, lse, dq_out, dkv_out, dkv):
    row, block = pl.program_id(0), pl.program_id(1)
    first, end, first_query = key_tiles(low, row, block)

    @pl.when(block == 0)
    def _():
        dkv[...] = jnp.zeros_like(dkv)

    query = stack_low(q[0].astype(f32)).astype(bf16)
    grads = stack_high(grad[0].astype(f32))
    inner = jnp.sum(grads * stack_high(att[0].astype(f32)), axis=1, keepdims=True)
    grads = grads.astype(bf16)
    logsum = jnp.concatenate([lse[0, 0]] * (KEYS // 128), axis=1)

    def body(tile, dq):
        rows = pl.ds(pl.multiple_of(tile * KEYS, KEYS), KEYS)
        both = kv[0, rows, :]
        ok = allowed_tile(starts[0], tile, first_query)
        scores = contract_last(query, both) * 0.125
        prob = jnp.where(ok, jnp.exp(scores - logsum), 0.0)
        grad_prob = contract_last(grads, both)
        grad_scores = (prob * (grad_prob - inner)).astype(bf16)
        dkv[rows, :] += contract_first(grad_scores, query) * 0.125 + contract_first(
            prob.astype(bf16), grads
        )
        return dq + jnp.dot(grad_scores, both, preferred_element_type=f32)

    dq = lax.fori_loop(first, end, body, jnp.zeros((4 * QUERIES, 128), f32))
    flat = unstack(dq, True) * 0.125
    cosine, sine = turns[0, :, 0:128], -turns[0, :, 128:256]
    dq_out[0, :, 0:128] = turn(flat[:, 0:128], cosine, sine).astype(bf16)
    dq_out[0, :, 128:256] = turn(flat[:, 128:256], cosine, sine).astype(bf16)

    @pl.when(block == 3)
    def _():
        dkv_out[0] = dkv[...]


def attend_back(low, q, kv, tabs, att, grad, lse):
    tile = pl.BlockSpec((1, QUERIES, 256), lambda i, j, low: (i, j, 0))
    return pl.pallas_call(
        attend_back_kernel,
        out_shape=(
            jax.ShapeDtypeStruct((2, 512, 256), bf16),
            jax.ShapeDtypeStruct((2, 1536, 128), f32),
        ),
        grid_spec=pltpu.PrefetchScalarGridSpec(
            num_scalar_prefetch=1, grid=(2, 4),
            in_specs=attend_specs()
            + [tile, tile, tile, pl.BlockSpec((1, 1, 4 * QUERIES, 128), lambda i, j, low: (i, j, 0, 0))],
            out_specs=[tile, pl.BlockSpec((1, 1536, 128), lambda i, j, low: (i, 0, 0))],
            scratch_shapes=[pltpu.VMEM((1536, 128), f32)],
        ),
        compiler_params=pltpu.CompilerParams(vmem_limit_bytes=VMEM_LIMIT),
        cost_estimate=pl.CostEstimate(flops=4 * 10**10, bytes_accessed=10**7, transcendentals=10**7),
        name="attend_back",
    )(low, q, kv, tabs, tabs, att, grad, lse)


def out_block(p1, nn, half):
    return p1[nn, half * 256 : half * 256 + 256, 384:640]


def middle_kernel(
    att, p1, hidden, gain, grad_top, mid_out, ffn_out, grad_out,
    theirs, mine, from_pt, from_up, from_dn, s0, s1, s2, s3, s4, s5,
    gbuf, g0, g1, g2, g3, fbuf, h0, h1, h2, h3, out_s,
):
    me = spot()
    r, n, w = me
    greet(line_partners(r, n, w, 4))
    scatter = Scatter(
        mine, theirs, (from_pt, from_up, from_dn), (s0, s1, s2, s3, s4, s5), me, 4
    )
    tops = Gather(gbuf, (g0, g1, g2, g3), me, 4)
    ffn = Gather(fbuf, (h0, h1, h2, h3), me, 4)

    def keep(rows):
        gbuf[r, w, rows, :] = grad_top[rows, :]

    each_rows(grad_top.shape[0], 16, keep)
    for i in range(4):
        s = scatter.order(i)
        rows = pl.ds(pl.multiple_of(s * 128, 128), 128)
        left = jnp.concatenate([att[1 - r, rows, :], att[r, rows, :]], axis=0)
        for nn in range(4):
            for half in range(2):
                part = jnp.dot(left, out_block(p1, nn, half), preferred_element_type=f32).astype(bf16)
                columns = slice(nn * 512 + half * 256, nn * 512 + half * 256 + 256)
                theirs[s, :, columns] = part[0:128]
                mine[s, :, columns] = part[128:256]
        scatter.pair(s).start()
    for i in range(4):
        scatter.step(scatter.order(i))
        if i == 0:
            tops.own()
        else:
            tops.step(i)
    scatter.total(mid_out)

    def body(rows):
        middle = mid_out[rows, :] + hidden[rows, :].astype(f32)
        mid_out[rows, :] = middle
        fbuf[r, w, rows, :] = norm_rows(middle, gain[...]).astype(bf16)

    each_rows(hidden.shape[0], 16, body)
    ffn.own()
    tops.rest()
    out_g = pltpu.make_async_copy(gbuf, grad_out, out_s.at[0])
    out_g.start()
    for k in (1, 2, 3):
        ffn.step(k)
    ffn.rest()
    out_f = pltpu.make_async_copy(fbuf, ffn_out, out_s.at[1])
    out_f.start()
    scatter.sent()
    tops.sent()
    ffn.sent()
    out_g.wait()
    out_f.wait()


def middle_stage(att, p1, hidden, gain, grad_top):
    shard, width = hidden.shape
    rows = jax.ShapeDtypeStruct((2, 4, shard, width), bf16)
    return comm_call(
        middle_kernel, "middle", 3,
        (jax.ShapeDtypeStruct((shard, width), f32), rows, rows),
        [vmem()] * 5, [vmem(), hbm(), hbm()],
        [pltpu.VMEM((4, shard, width), bf16)] * 2
        + scatter_bufs(shard, width) + scatter_sems()
        + gather_scratch(shard, width) + gather_scratch(shard, width)
        + [pltpu.SemaphoreType.DMA((2,))],
        (att, p1, hidden, gain, grad_top), flops=10**10, sent=2 * 10**8,
    )


def ffn_kernel(
    x, tops, p2, gain, part_out, sum_out, gain_out, grads_out,
    theirs, mine, from_pt, from_up, from_dn, s0, s1, s2, s3, s4, s5,
    act, dgu, stage, wide, out_s, give_s, give_g, keep_s,
):
    me = spot()
    r, n, w = me
    greet(line_partners(r, n, w, 4))
    scatter = Scatter(
        mine, theirs, (from_pt, from_up, from_dn), (s0, s1, s2, s3, s4, s5), me, 4
    )
    gain_out[...] = jnp.zeros_like(gain_out)

    def put(s, slot, row_slot, row):
        return pltpu.make_async_copy(
            stage.at[slot, row_slot], part_out.at[row, s], out_s.at[slot, row_slot]
        )

    for i in range(4):
        s = scatter.order(i)
        slot = i % 2
        rows_t = pl.ds(pl.multiple_of((1 - r) * 512 + s * 128, 128), 128)
        rows_m = pl.ds(pl.multiple_of(r * 512 + s * 128, 128), 128)
        if i >= 2:
            put(s, slot, 0, 1 - r).wait()
            put(s, slot, 1, r).wait()

        def hidden_tile(ft, carry):
            columns = pl.ds(pl.multiple_of(ft * 256, 256), 256)
            left = jnp.concatenate([x[rows_t, :], x[rows_m, :]], axis=0)
            gate = jnp.dot(left, p2[:, 0, :, columns].reshape(2048, 256), preferred_element_type=f32)
            up = jnp.dot(left, p2[:, 1, :, columns].reshape(2048, 256), preferred_element_type=f32)
            sig = 1.0 / (1.0 + jnp.exp(-gate))
            silu = gate * sig
            active = (silu * up).astype(bf16)
            act[rows_t, columns] = active[0:128]
            act[rows_m, columns] = active[128:256]
            f_rows = pl.ds(pl.multiple_of((ft % 2) * 256, 256), 256)
            f_cols = pl.ds(pl.multiple_of((ft // 2) * 512, 512), 512)
            right = jnp.concatenate([p2[nn, 2, f_rows, f_cols] for nn in range(4)], axis=1)
            top = jnp.concatenate([tops[rows_t, :], tops[rows_m, :]], axis=0)
            dact = contract_last(top, right)
            dgate = (dact * up * (sig * (1.0 + gate * (1.0 - sig)))).astype(bf16)
            dup = (dact * silu).astype(bf16)
            dgu[rows_t, columns] = dgate[0:128]
            dgu[rows_m, columns] = dgate[128:256]
            later = pl.ds(pl.multiple_of(1024 + ft * 256, 256), 256)
            dgu[rows_t, later] = dup[0:128]
            dgu[rows_m, later] = dup[128:256]
            return carry

        lax.fori_loop(0, 4, hidden_tile, 0)

        def model_tile(dt, carry):
            nn, half = dt // 2, dt % 2
            columns = pl.ds(pl.multiple_of(dt * 256, 256), 256)
            inner = pl.ds(pl.multiple_of(half * 256, 256), 256)
            other = pl.ds(pl.multiple_of(512 + half * 256, 256), 256)
            left = jnp.concatenate([dgu[rows_t, :], dgu[rows_m, :]], axis=0)
            right = jnp.concatenate([p2[nn, 0, inner, :], p2[nn, 1, inner, :]], axis=1)
            part = contract_last(left, right)
            seen = jnp.concatenate([x[rows_t, columns], x[rows_m, columns]], axis=0)
            terms = part * seen.astype(f32)
            gain_out[:, columns] += jnp.sum(terms.reshape(32, 8, 256), axis=0)
            part = part.astype(bf16)
            theirs[s, :, columns] = part[0:128]
            mine[s, :, columns] = part[128:256]
            left = jnp.concatenate([act[rows_t, :], act[rows_m, :]], axis=0)
            right = jnp.concatenate([p2[nn, 2, :, inner], p2[nn, 2, :, other]], axis=0)
            part = jnp.dot(left, right, preferred_element_type=f32).astype(bf16)
            stage[slot, 0, :, columns] = part[0:128]
            stage[slot, 1, :, columns] = part[128:256]
            return carry

        lax.fori_loop(0, 8, model_tile, 0)
        scatter.pair(s).start()
        put(s, slot, 0, 1 - r).start()
        put(s, slot, 1, r).start()

    def scale(rows):
        gain_out[rows, :] = gain_out[rows, :] / gain[...]

    each_rows(8, 8, scale)

    def give(which, half):
        return pltpu.make_async_remote_copy(
            wide.at[which % 2, half],
            grads_out.at[:, which, :, pl.ds(pl.multiple_of(r * 1024, 1024), 1024)],
            give_s.at[which], give_g.at[which],
            device_id=(1 - r, n, w), device_id_type=MESH,
        )

    def keep(which):
        return pltpu.make_async_copy(
            wide.at[which % 2, 1],
            grads_out.at[:, which, :, pl.ds(pl.multiple_of(r * 1024, 1024), 1024)],
            keep_s.at[which],
        )

    for which in range(3):
        scatter.step(scatter.order(which))
        if which == 2:
            give(0, 0).wait_send()
            keep(0).wait()
        for half in range(2):
            d_first = (jnp.where(half == 0, 1 - r, r)) * 1024

            def weight_tile(i, carry):
                d_rows = pl.ds(pl.multiple_of(d_first + i * 256, 256), 256)
                source = x if which < 2 else tops
                left = source[:, d_rows]
                if which < 2:
                    right = dgu[:, which * 1024 : which * 1024 + 1024]
                else:
                    right = act[...]
                wide[which % 2, half, i] = contract_first(left, right).astype(bf16)
                return carry

            lax.fori_loop(0, 4, weight_tile, 0)
            if half == 0:
                give(which, 0).start()
            else:
                keep(which).start()
    scatter.step(scatter.order(3))
    scatter.total(sum_out)
    scatter.sent()
    for which in range(3):
        give(which, 0).wait_recv()
        if which > 0:
            give(which, 0).wait_send()
            keep(which).wait()
    for slot in range(2):
        put(0, slot, 0, 1 - r).wait()
        put(0, slot, 1, r).wait()


def ffn_stage(x, tops, p2, gain):
    shard, width = 128, 2048
    return comm_call(
        ffn_kernel, "ffn", 4,
        (
            jax.ShapeDtypeStruct((2, 4, shard, width), bf16),
            jax.ShapeDtypeStruct((shard, width), f32),
            jax.ShapeDtypeStruct((8, width), f32),
            jax.ShapeDtypeStruct((4, 3, 256, width), bf16),
        ),
        [vmem()] * 4, [hbm(), vmem(), vmem(), hbm()],
        [pltpu.VMEM((4, shard, width), bf16)] * 2
        + scatter_bufs(shard, width) + scatter_sems()
        + [
            pltpu.VMEM((1024, 1024), bf16),
            pltpu.VMEM((1024, 2048), bf16),
            pltpu.VMEM((2, 2, shard, width), bf16),
            pltpu.VMEM((2, 2, 4, 256, 1024), bf16),
            pltpu.SemaphoreType.DMA((2, 2)),
            pltpu.SemaphoreType.DMA((3,)),
            pltpu.SemaphoreType.DMA((3,)),
            pltpu.SemaphoreType.DMA((3,)),
        ],
        (x, tops, p2, gain), flops=4 * 10**10, sent=10**8,
    )


def norm_back(values, gain, grad):
    root = lax.rsqrt(jnp.mean(values * values, axis=-1, keepdims=True) + norm_eps)
    weighted = grad * gain
    inner = jnp.mean(weighted * values, axis=-1, keepdims=True)
    return root * weighted - values * (root * root * root) * inner


def branch_kernel(
    total, mid, grad_top, gain, parts, p1, att, hid_out, gmid_out, datt_out, go_out,
    mine, from_pt, from_up, from_dn, s0, s1, s2, s3, s4, s5,
    buf, g0, g1, g2, g3, acc, wide, give_s, give_g, keep_s,
):
    me = spot()
    r, n, w = me
    greet(line_partners(r, n, w, 4))
    scatter = Scatter(
        mine, parts.at[1 - r], (from_pt, from_up, from_dn), (s0, s1, s2, s3, s4, s5), me, 4
    )
    gather = Gather(buf, (g0, g1, g2, g3), me, 4)

    def body(rows):
        grad = norm_back(mid[rows, :], gain[...], total[rows, :]) + grad_top[rows, :].astype(f32)
        gmid_out[rows, :] = grad
        buf[r, w, rows, :] = grad.astype(bf16)

    each_rows(mid.shape[0], 16, body)
    gather.own()
    for i in range(4):
        scatter.pair(scatter.order(i)).start()

    for s in range(4):
        def fill(rows):
            mine[s, rows, :] = parts[r, s, rows, :]

        each_rows(128, 16, fill)
    for i in range(4):
        scatter.step(scatter.order(i))
        if i < 3:
            gather.step(i + 1)
    gather.rest()
    for row in range(2):
        for pair in range(2):
            left = jnp.concatenate([buf[row, 2 * pair], buf[row, 2 * pair + 1]], axis=0)
            right = jnp.concatenate(
                [out_block(p1, nn, half) for nn in range(4) for half in range(2)], axis=1
            )
            datt_out[row, pair * 256 : pair * 256 + 256, :] = contract_last(left, right).astype(bf16)

    give = pltpu.make_async_remote_copy(
        wide.at[0], go_out.at[:, pl.ds(pl.multiple_of(r * 256, 256), 256)], give_s, give_g,
        device_id=(1 - r, n, w), device_id_type=MESH,
    )
    keep = pltpu.make_async_copy(
        wide.at[1], go_out.at[:, pl.ds(pl.multiple_of(r * 256, 256), 256)], keep_s
    )
    for half in range(2):
        d_first = (jnp.where(half == 0, 1 - r, r)) * 1024

        def weight_tile(i, carry):
            columns = pl.ds(pl.multiple_of(d_first + i * 256, 256), 256)
            left = buf[:, :, :, columns].reshape(1024, 256)
            wide[half, pl.ds(pl.multiple_of(i * 256, 256), 256), :] = contract_first(
                left, att[...]
            ).astype(bf16)
            return carry

        lax.fori_loop(0, 4, weight_tile, 0)
        if half == 0:
            give.start()
        else:
            keep.start()
    scatter.total(acc)

    def last(rows):
        hid_out[rows, :] = (acc[rows, :] + mid[rows, :]).astype(bf16)

    each_rows(mid.shape[0], 16, last)
    scatter.sent()
    gather.sent()
    give.wait()
    keep.wait()


def branch_stage(total, mid, grad_top, gain, parts, p1, att):
    shard, width = mid.shape
    return comm_call(
        branch_kernel, "branch", 5,
        (
            jax.ShapeDtypeStruct((shard, width), bf16),
            jax.ShapeDtypeStruct((shard, width), f32),
            jax.ShapeDtypeStruct((2, 512, 256), bf16),
            jax.ShapeDtypeStruct((1024, 512), bf16),
        ),
        [vmem()] * 7, [vmem(), vmem(), vmem(), hbm()],
        [pltpu.VMEM((4, shard, width), bf16)]
        + scatter_bufs(shard, width) + scatter_sems()
        + gather_scratch(shard, width)
        + [
            pltpu.VMEM((shard, width), f32),
            pltpu.VMEM((2, 1024, 256), bf16),
            pltpu.SemaphoreType.DMA(()),
            pltpu.SemaphoreType.DMA(()),
            pltpu.SemaphoreType.DMA(()),
        ],
        (total, mid, grad_top, gain, parts, p1, att), flops=10**10, sent=10**8,
    )


def unproject_kernel(
    dq, dkv, x, p1, tabs, gain, part_out, gain_out, gq_out, gkv_out,
    send, recv, both, wide_q, wide_kv, s_s, s_g, q_s, q_g, kv_s, kv_g, keep_s,
):
    r, n, w = spot()
    greet(
        [
            (n >= 1, nar_device(r, n, w, -1)),
            (n >= 2, nar_device(r, n, w, -2)),
            (n <= 2, nar_device(r, n, w, 1)),
            (n <= 1, nar_device(r, n, w, 2)),
            (n >= 0, (1 - r, n, w)),
        ]
    )

    def copy(row, slot, by):
        return pltpu.make_async_remote_copy(
            send.at[row, slot], recv.at[row, slot], s_s.at[row, slot], s_g.at[row, slot],
            device_id=nar_device(r, n, w, by), device_id_type=MESH,
        )

    for row in range(2):
        for slot, by in ((1, -1), (0, -2)):
            @pl.when(n >= -by)
            def _():
                send[row, slot] = dkv[row, slot].astype(bf16)
                copy(row, slot, by).start()

    partner = (1 - r, n, w)
    give_q = pltpu.make_async_remote_copy(
        wide_q.at[0], gq_out.at[:, pl.ds(pl.multiple_of(r * 256, 256), 256)], q_s, q_g,
        device_id=partner, device_id_type=MESH,
    )
    keep_q = pltpu.make_async_copy(
        wide_q.at[1], gq_out.at[:, pl.ds(pl.multiple_of(r * 256, 256), 256)], keep_s.at[0]
    )
    give_kv = pltpu.make_async_remote_copy(
        wide_kv.at[0], gkv_out.at[:, pl.ds(pl.multiple_of(r * 128, 128), 128)], kv_s, kv_g,
        device_id=partner, device_id_type=MESH,
    )
    keep_kv = pltpu.make_async_copy(
        wide_kv.at[1], gkv_out.at[:, pl.ds(pl.multiple_of(r * 128, 128), 128)], keep_s.at[1]
    )

    for row in range(2):
        both[row * 512 : row * 512 + 512, 0:256] = dq[row]

    def weight(half, columns, wide):
        d_first = (jnp.where(half == 0, 1 - r, r)) * 1024

        def tile(i, carry):
            d_cols = pl.ds(pl.multiple_of(d_first + i * 256, 256), 256)
            wide[half, pl.ds(pl.multiple_of(i * 256, 256), 256), :] = contract_first(
                x[:, d_cols], both[:, columns]
            ).astype(bf16)
            return carry

        lax.fori_loop(0, 4, tile, 0)

    weight(0, slice(0, 256), wide_q)
    give_q.start()
    weight(1, slice(0, 256), wide_q)
    keep_q.start()
    lane = lax.broadcasted_iota(jnp.int32, (128, 128), 1)
    for row in range(2):
        for slot, by in ((1, -1), (0, -2)):
            @pl.when(n <= 3 + by)
            def _():
                copy(row, slot, by).wait_recv()

        def tile(i, carry):
            rows = pl.ds(pl.multiple_of(i * 128, 128), 128)
            total = dkv[row, 2, rows, :]
            zero = jnp.zeros_like(total)
            total = total + jnp.where(n <= 2, recv[row, 1, rows, :].astype(f32), zero)
            total = total + jnp.where(n <= 1, recv[row, 0, rows, :].astype(f32), zero)
            turned = turn(total, tabs[row, rows, 0:128], -tabs[row, rows, 128:256])
            both[pl.ds(pl.multiple_of(row * 512 + i * 128, 128), 128), 256:384] = jnp.where(
                lane < 64, turned, total
            ).astype(bf16)
            return carry

        lax.fori_loop(0, 4, tile, 0)
    weight(0, slice(256, 384), wide_kv)
    give_kv.start()
    weight(1, slice(256, 384), wide_kv)
    keep_kv.start()
    gain_out[...] = jnp.zeros_like(gain_out)

    def model_tile(dt, carry):
        nn, half = dt // 2, dt % 2
        columns = pl.ds(pl.multiple_of(dt * 256, 256), 256)
        inner = pl.ds(pl.multiple_of(half * 256, 256), 256)
        right = p1[nn, inner, 0:384]
        for row in range(2):
            for block in range(2):
                first = row * 512 + block * 256
                part = contract_last(both[first : first + 256, :], right)
                terms = part * x[first : first + 256, columns].astype(f32)
                gain_out[:, columns] += jnp.sum(terms.reshape(32, 8, 256), axis=0)
                part_out[row, 2 * block, :, columns] = part[0:128].astype(bf16)
                part_out[row, 2 * block + 1, :, columns] = part[128:256].astype(bf16)
        return carry

    lax.fori_loop(0, 8, model_tile, 0)
    gain_out[...] = gain_out[...] / gain[...]
    for row in range(2):
        for slot, by in ((1, -1), (0, -2)):
            @pl.when(n >= -by)
            def _():
                copy(row, slot, by).wait_send()

    give_q.wait()
    keep_q.wait()
    give_kv.wait()
    keep_kv.wait()


def unproject(dq, dkv, x, p1, tabs, gain):
    return comm_call(
        unproject_kernel, "unproject", 6,
        (
            jax.ShapeDtypeStruct((2, 4, 128, 2048), bf16),
            jax.ShapeDtypeStruct((8, 2048), f32),
            jax.ShapeDtypeStruct((1024, 512), bf16),
            jax.ShapeDtypeStruct((1024, 256), bf16),
        ),
        [vmem()] * 6, [vmem(), vmem(), hbm(), hbm()],
        [
            pltpu.VMEM((2, 2, 512, 128), bf16),
            pltpu.VMEM((2, 2, 512, 128), bf16),
            pltpu.VMEM((1024, 384), bf16),
            pltpu.VMEM((2, 1024, 256), bf16),
            pltpu.VMEM((2, 1024, 128), bf16),
            pltpu.SemaphoreType.DMA((2, 2)),
            pltpu.SemaphoreType.DMA((2, 2)),
            pltpu.SemaphoreType.DMA(()),
            pltpu.SemaphoreType.DMA(()),
            pltpu.SemaphoreType.DMA(()),
            pltpu.SemaphoreType.DMA(()),
            pltpu.SemaphoreType.DMA((2,)),
        ],
        (dq, dkv, x, p1, tabs, gain), flops=10**10, sent=10**7,
    )


def leave_kernel(
    parts, hidden, gain, gmid, gains, grad_out, ga_out,
    mine, from_pt, from_up, from_dn, s0, s1, s2, s3, s4, s5,
    acc, over_wid, summed, over_rest, w_s, w_g, t_s, t_g,
):
    me = spot()
    r, n, w = me
    partners = [(w != j, (r, n, jnp.int32(j))) for j in range(4)]
    partners += [
        ((r != a) | (n != b), (jnp.int32(a), jnp.int32(b), w)) for a in range(2) for b in range(4)
    ]
    greet(partners)
    scatter = Scatter(
        mine, parts.at[1 - r], (from_pt, from_up, from_dn), (s0, s1, s2, s3, s4, s5), me, 4
    )
    for i in range(4):
        scatter.pair(scatter.order(i)).start()

    def wid_copy(j, slot):
        return pltpu.make_async_remote_copy(
            gains, over_wid.at[slot], w_s.at[j], w_g.at[slot],
            device_id=(r, n, jnp.int32(j)), device_id_type=MESH,
        )

    def rest_copy(a, b, slot):
        return pltpu.make_async_remote_copy(
            summed, over_rest.at[slot], t_s.at[a * 4 + b], t_g.at[slot],
            device_id=(jnp.int32(a), jnp.int32(b), w), device_id_type=MESH,
        )

    for j in range(4):
        @pl.when(w != j)
        def _():
            wid_copy(j, w).start()

    for s in range(4):
        def fill(rows):
            mine[s, rows, :] = parts[r, s, rows, :]

        each_rows(128, 16, fill)
    scatter.step(scatter.order(0))
    summed[...] = gains[...]
    for j in range(4):
        @pl.when(w != j)
        def _():
            wid_copy(j, j).wait_recv()
            summed[...] += over_wid[j]

    for a in range(2):
        for b in range(4):
            @pl.when((r != a) | (n != b))
            def _():
                rest_copy(a, b, r * 4 + n).start()

    for i in (1, 2, 3):
        scatter.step(scatter.order(i))
    mine_block = r * 4 + n
    ga_out[0:1] = summed[pl.ds(mine_block, 1), :]
    ga_out[1:2] = summed[pl.ds(mine_block + 8, 1), :]
    for a in range(2):
        for b in range(4):
            @pl.when((r != a) | (n != b))
            def _():
                slot = a * 4 + b
                rest_copy(a, b, slot).wait_recv()
                ga_out[0:1] += over_rest[slot, pl.ds(mine_block, 1), :]
                ga_out[1:2] += over_rest[slot, pl.ds(mine_block + 8, 1), :]

    scatter.total(acc)

    def last(rows):
        grad = norm_back(hidden[rows, :].astype(f32), gain[...], acc[rows, :])
        grad_out[rows, :] = (grad + gmid[rows, :]).astype(bf16)

    each_rows(hidden.shape[0], 16, last)
    scatter.sent()
    for j in range(4):
        @pl.when(w != j)
        def _():
            wid_copy(j, w).wait_send()

    for a in range(2):
        for b in range(4):
            @pl.when((r != a) | (n != b))
            def _():
                rest_copy(a, b, r * 4 + n).wait_send()


def leave(parts, hidden, gain, gmid, gains):
    shard, width = hidden.shape
    return comm_call(
        leave_kernel, "leave", 7,
        (jax.ShapeDtypeStruct((shard, width), bf16), jax.ShapeDtypeStruct((8, 256), f32)),
        [vmem()] * 5, [vmem()] * 2,
        [pltpu.VMEM((4, shard, width), bf16)]
        + scatter_bufs(shard, width) + scatter_sems()
        + [
            pltpu.VMEM((shard, width), f32),
            pltpu.VMEM((4, 16, 256), f32),
            pltpu.VMEM((16, 256), f32),
            pltpu.VMEM((8, 16, 256), f32),
            pltpu.SemaphoreType.DMA((4,)),
            pltpu.SemaphoreType.DMA((4,)),
            pltpu.SemaphoreType.DMA((8,)),
            pltpu.SemaphoreType.DMA((8,)),
        ],
        (parts, hidden, gain, gmid, gains), flops=10**10, sent=10**8,
    )


def local_fast(
    hidden_in, doc_lengths, w_query, w_key, w_value, w_output, w_gate, w_up, w_down,
    gain_attn, gain_ffn, grad_out,
):
    r, n, w = spot()
    hidden, grad_top = hidden_in[0], grad_out[0]
    gain_a, gain_f = gain_attn[None], gain_ffn[None]
    def half(weight, axis):
        size = weight.shape[axis] // 2
        return lax.dynamic_slice_in_dim(weight, r * size, size, axis)

    head = (w * 2 + r) * HD
    kv_pack = jnp.concatenate(
        [lax.dynamic_slice_in_dim(w_key, head, HD, 1), lax.dynamic_slice_in_dim(w_value, head, HD, 1)],
        axis=1,
    )
    out_half = half(w_output, 0)
    p1_shard = jnp.concatenate(
        [half(w_query, 1), kv_pack, jnp.concatenate([out_half[:, :256], out_half[:, 256:]], axis=0)],
        axis=1,
    )
    down_half = half(w_down, 0)
    p2_shard = jnp.stack(
        [
            half(w_gate, 1),
            half(w_up, 1),
            jnp.concatenate([down_half[:512], down_half[512:]], axis=1),
        ]
    )
    p1 = lax.all_gather(p1_shard, "nar", axis=0)
    p2 = lax.all_gather(p2_shard, "nar", axis=0)

    token_ids = n * 512 + jnp.arange(512, dtype=jnp.int32)
    doc_start, places = doc_layout(doc_lengths[0], token_ids)
    angles = places.astype(f32)[:, None] * inverse_freq()[None, :]
    cosine, sine = jnp.cos(angles), jnp.sin(angles)
    start_here = (doc_start - (n - 2) * 512).astype(f32)
    tab = jnp.concatenate(
        [cosine] * 4 + [-sine, sine] * 2 + [jnp.broadcast_to(start_here[:, None], (512, 128))],
        axis=1,
    )

    rows, tabs = enter(hidden, gain_a, tab)
    rows3, rows2 = rows.reshape(2, 512, 2048), rows.reshape(1024, 2048)
    q, kv = project(rows3, p1, tabs)
    low = tabs[:, ::QUERIES, 256].astype(jnp.int32).reshape(8)
    kv_flat = kv.reshape(2, 1536, 128)
    att, lse = attend(low, q, kv_flat, tabs)
    mid, ffn_rows, top_rows = middle_stage(att, p1, hidden, gain_f, grad_top)
    parts, total, gain_f_part, grads = ffn_stage(
        ffn_rows.reshape(1024, 2048), top_rows.reshape(1024, 2048), p2, gain_f
    )
    summed = lax.psum_scatter(
        grads.reshape(4 * 768, 2048), "nar", scatter_dimension=0, tiled=True
    ).reshape(3, 256, 2048)
    hidden_out, gmid, datt, grad_o = branch_stage(
        total, mid, grad_top, gain_f, parts, p1, att.reshape(1024, 256)
    )
    dq, dkv = attend_back(low, q, kv_flat, tabs, att, datt, lse)
    dparts, gain_a_part, grad_q, grad_kv = unproject(
        dq, dkv.reshape(2, 3, 512, 128), rows2, p1, tabs, gain_a
    )
    small = lax.psum_scatter(
        jnp.concatenate([grad_q, grad_o, grad_kv], axis=1), "nar", scatter_dimension=0, tiled=True
    )
    gains = jnp.concatenate(
        [gain_f_part.sum(axis=0).reshape(8, 256), gain_a_part.sum(axis=0).reshape(8, 256)], axis=0
    )
    grad_in, gain_sums = leave(dparts, hidden, gain_a, gmid, gains)
    kv_all = lax.all_gather(small[:, 1024:1280], "wid", axis=1, tiled=True)
    kv_all = kv_all.astype(f32).reshape(256, KV, 2, HD)
    return (
        hidden_out[None],
        grad_in[None],
        small[:, 0:512].astype(f32),
        kv_all[:, :, 0].reshape(256, KV * HD),
        kv_all[:, :, 1].reshape(256, KV * HD),
        small[:, 512:1024].T.astype(f32),
        summed[0].astype(f32),
        summed[1].astype(f32),
        summed[2].T.astype(f32),
        gain_sums[1],
        gain_sums[0],
    )


def solution(mesh):
    in_specs = (
        P("row", ("nar", "wid"), None),
        P("row", None),
        P("nar", "wid"),
        P("nar", None),
        P("nar", None),
        P("wid", "nar"),
        P("nar", "wid"),
        P("nar", "wid"),
        P("wid", "nar"),
        P(),
        P(),
        P("row", ("nar", "wid"), None),
    )
    out_specs = (
        P("row", ("nar", "wid"), None),
        P("row", ("nar", "wid"), None),
        P(("row", "nar"), "wid"),
        P(("row", "nar"), None),
        P(("row", "nar"), None),
        P("wid", ("row", "nar")),
        P(("row", "nar"), "wid"),
        P(("row", "nar"), "wid"),
        P("wid", ("row", "nar")),
        P(("row", "nar")),
        P(("row", "nar")),
    )
    sizes = dict(mesh.shape)
    fits = sizes == {"row": 2, "nar": 4, "wid": 4}

    def body(*args):
        small = args[0].shape == (1, 128, 2048)
        return (local_fast if fits and small else local)(*args)

    return jax.shard_map(body, mesh=mesh, in_specs=in_specs, out_specs=out_specs, check_vma=False)
```

```python
import math

import jax
import jax.numpy as jnp
from jax import lax
from jax.experimental import pallas as pl
from jax.experimental.pallas import tpu as pltpu
from jax.sharding import PartitionSpec as P

H = 32
KV = 8
HD = 64


norm_eps = 1e-05
masked_score = -1e30


def inverse_freq():
    listed = []
    for pair_index in range(HD // 2):
        base_freq = 500000.0 ** (-2.0 * pair_index / HD)
        wavelength = 2.0 * math.pi / base_freq
        smoothing = (8192.0 / wavelength - 1.0) / 3.0
        blended = (1.0 - smoothing) * base_freq / 32.0 + smoothing * base_freq
        if wavelength < 2048.0:
            listed.append(base_freq)
        elif wavelength > 8192.0:
            listed.append(base_freq / 32.0)
        else:
            listed.append(blended)
    return jnp.asarray(listed, dtype=jnp.float32)


def rotate(values, cosine_table, sine_table):
    half_dim = HD // 2
    first_half = values[..., :half_dim]
    second_half = values[..., half_dim:]
    return jnp.concatenate(
        [
            first_half * cosine_table - second_half * sine_table,
            second_half * cosine_table + first_half * sine_table,
        ],
        axis=-1,
    )


def rotate_back(grads_in, cosine_table, sine_table):
    half_dim = HD // 2
    first_half = grads_in[..., :half_dim]
    second_half = grads_in[..., half_dim:]
    return jnp.concatenate(
        [
            first_half * cosine_table + second_half * sine_table,
            second_half * cosine_table - first_half * sine_table,
        ],
        axis=-1,
    )


def doc_layout(lengths_row, token_ids):
    ends_at = jnp.cumsum(lengths_row, dtype=jnp.int32)
    starts_at = ends_at - lengths_row
    inside = (token_ids[:, None] >= starts_at[None, :]) & (token_ids[:, None] < ends_at[None, :])
    doc_start = jnp.sum(jnp.where(inside, starts_at[None, :], 0), axis=1, dtype=jnp.int32)
    return (doc_start, token_ids - doc_start)


def norm_forward(values, gain_vector):
    root_inv = lax.rsqrt(jnp.mean(values * values, axis=-1, keepdims=True) + norm_eps)
    return (root_inv, (values * root_inv * gain_vector).astype(jnp.bfloat16))


def norm_backward(values, root_inv, gain_vector, grad_normed):
    weighted = grad_normed * gain_vector
    inner_sum = jnp.mean(weighted * values, axis=-1, keepdims=True)
    grad_values = root_inv * weighted - values * (root_inv * root_inv * root_inv) * inner_sum
    gain_term = jnp.sum(grad_normed * values * root_inv, axis=0)
    return (grad_values, gain_term)


def contract_last(left_side, right_side):
    return lax.dot_general(
        left_side, right_side, (((1,), (1,)), ((), ())), preferred_element_type=jnp.float32
    )


def contract_first(left_side, right_side):
    return lax.dot_general(
        left_side, right_side, (((0,), (0,)), ((), ())), preferred_element_type=jnp.float32
    )


def local(
    hidden_in,
    doc_lengths,
    w_query,
    w_key,
    w_value,
    w_output,
    w_gate,
    w_up,
    w_down,
    gain_attn,
    gain_ffn,
    grad_out,
):
    wid_count = lax.axis_size("wid")
    nar_count = lax.axis_size("nar")
    wid_index = lax.axis_index("wid")
    nar_index = lax.axis_index("nar")
    local_tokens = hidden_in.shape[1]
    block_tokens = local_tokens * wid_count
    seq_length = block_tokens * nar_count
    query_heads = w_query.shape[1] // HD
    group_size = H // KV
    kv_local = max(query_heads // group_size, 1)
    heads_per_kv = query_heads // kv_local
    kv_first = wid_index * query_heads // group_size
    query_block = min(512, block_tokens)
    block_count = block_tokens // query_block
    item_count = block_count * query_heads
    attn_scale = HD ** (-0.5)
    query_full, key_full, value_full, output_full, gate_full, up_full, down_full = (
        lax.all_gather(w_query, "nar", axis=0, tiled=True),
        lax.all_gather(w_key, "nar", axis=0, tiled=True),
        lax.all_gather(w_value, "nar", axis=0, tiled=True),
        lax.all_gather(w_output, "nar", axis=1, tiled=True),
        lax.all_gather(w_gate, "nar", axis=0, tiled=True),
        lax.all_gather(w_up, "nar", axis=0, tiled=True),
        lax.all_gather(w_down, "nar", axis=1, tiled=True),
    )
    key_local = lax.dynamic_slice_in_dim(key_full, kv_first * HD, kv_local * HD, 1)
    value_local = lax.dynamic_slice_in_dim(value_full, kv_first * HD, kv_local * HD, 1)
    token_ids = nar_index * block_tokens + jnp.arange(block_tokens, dtype=jnp.int32)
    doc_start, places = doc_layout(doc_lengths[0], token_ids)
    angles = places.astype(jnp.float32)[:, None] * inverse_freq()[None, :]
    cosine_table = jnp.cos(angles)[:, None, :]
    sine_table = jnp.sin(angles)[:, None, :]
    key_ids = jnp.arange(seq_length, dtype=jnp.int32)
    residual = hidden_in[0].astype(jnp.float32)
    root_attn, normed_attn = norm_forward(residual, gain_attn)
    normed_rows = lax.all_gather(normed_attn, "wid", axis=0, tiled=True)
    query_pre = jnp.dot(normed_rows, query_full, preferred_element_type=jnp.float32)
    key_pre = jnp.dot(normed_rows, key_local, preferred_element_type=jnp.float32)
    value_rows = jnp.dot(normed_rows, value_local, preferred_element_type=jnp.float32).astype(
        jnp.bfloat16
    )
    query_rot = (
        rotate(query_pre.reshape(block_tokens, query_heads, HD), cosine_table, sine_table)
        .astype(jnp.bfloat16)
        .reshape(block_tokens, query_heads * HD)
    )
    key_rot = (
        rotate(key_pre.reshape(block_tokens, kv_local, HD), cosine_table, sine_table)
        .astype(jnp.bfloat16)
        .reshape(block_tokens, kv_local * HD)
    )
    key_seq, value_seq = (
        lax.all_gather(key_rot, "nar", axis=0, tiled=True),
        lax.all_gather(value_rows, "nar", axis=0, tiled=True),
    )

    def item_inputs(item_index):
        block_index = item_index // query_heads
        head_index = item_index % query_heads
        kv_index = head_index // heads_per_kv
        row_first = block_index * query_block
        query_part = lax.dynamic_slice(query_rot, (row_first, head_index * HD), (query_block, HD))
        key_head = lax.dynamic_slice_in_dim(key_seq, kv_index * HD, HD, 1)
        value_head = lax.dynamic_slice_in_dim(value_seq, kv_index * HD, HD, 1)
        query_ids = lax.dynamic_slice_in_dim(token_ids, row_first, query_block, 0)
        query_starts = lax.dynamic_slice_in_dim(doc_start, row_first, query_block, 0)
        allowed = (key_ids[None, :] <= query_ids[:, None]) & (
            key_ids[None, :] >= query_starts[:, None]
        )
        scores = contract_last(query_part, key_head) * attn_scale
        return (
            row_first,
            head_index,
            kv_index,
            query_part,
            key_head,
            value_head,
            jnp.where(allowed, scores, masked_score),
        )

    def attend(item_index):
        row_first, head_index, kv_index, query_part, key_head, value_head, scores = item_inputs(
            item_index
        )
        row_max = jnp.max(scores, axis=1, keepdims=True)
        exp_scores = jnp.exp(scores - row_max)
        row_total = jnp.sum(exp_scores, axis=1, keepdims=True)
        probability = (exp_scores / row_total).astype(jnp.bfloat16)
        attended = jnp.dot(probability, value_head, preferred_element_type=jnp.float32)
        return (attended, (row_max + jnp.log(row_total))[:, 0])

    attended_items, logsum_items = lax.map(attend, jnp.arange(item_count, dtype=jnp.int32))
    attended_rows = (
        attended_items.reshape(block_count, query_heads, query_block, HD)
        .transpose(0, 2, 1, 3)
        .reshape(block_tokens, query_heads * HD)
        .astype(jnp.bfloat16)
    )
    rows_here = attended_rows
    branch_attn = lax.psum_scatter(
        jnp.dot(rows_here, output_full, preferred_element_type=jnp.float32),
        "wid",
        scatter_dimension=0,
        tiled=True,
    )
    middle = residual + branch_attn
    root_ffn, normed_ffn = norm_forward(middle, gain_ffn)
    ffn_rows = lax.all_gather(normed_ffn, "wid", axis=0, tiled=True)
    gate_proj = jnp.dot(ffn_rows, gate_full, preferred_element_type=jnp.float32)
    up_proj = jnp.dot(ffn_rows, up_full, preferred_element_type=jnp.float32)
    gate_sigmoid = jax.nn.sigmoid(gate_proj)
    gate_silu = gate_proj * gate_sigmoid
    activated = (gate_silu * up_proj).astype(jnp.bfloat16)
    rows_here = activated
    branch_ffn = lax.psum_scatter(
        jnp.dot(rows_here, down_full, preferred_element_type=jnp.float32).astype(jnp.bfloat16),
        "wid",
        scatter_dimension=0,
        tiled=True,
    ).astype(jnp.float32)
    hidden_out = (middle + branch_ffn).astype(jnp.bfloat16)[None]
    grad_top = grad_out[0]
    grad_rows = lax.all_gather(grad_top, "wid", axis=0, tiled=True)
    grad_activated = contract_last(grad_rows, down_full)
    down_weight_grad = contract_first(activated, grad_rows)
    silu_slope = gate_sigmoid * (1.0 + gate_proj * (1.0 - gate_sigmoid))
    grad_gate_b = (grad_activated * up_proj * silu_slope).astype(jnp.bfloat16)
    grad_up_b = (grad_activated * gate_silu).astype(jnp.bfloat16)
    gate_weight_grad = contract_first(ffn_rows, grad_gate_b)
    up_weight_grad = contract_first(ffn_rows, grad_up_b)
    grad_normed_ffn = lax.psum_scatter(
        contract_last(grad_gate_b, gate_full) + contract_last(grad_up_b, up_full),
        "wid",
        scatter_dimension=0,
        tiled=True,
    )
    grad_middle, gain_ffn_term = norm_backward(middle, root_ffn, gain_ffn, grad_normed_ffn)
    grad_middle = grad_middle + grad_top.astype(jnp.float32)
    grad_branch = grad_middle.astype(jnp.bfloat16)
    branch_rows = lax.all_gather(grad_branch, "wid", axis=0, tiled=True)
    grad_attended = contract_last(branch_rows, output_full).astype(jnp.bfloat16)
    output_weight_grad = contract_first(attended_rows, branch_rows)

    def attend_back(carried, item_index):
        key_grad, value_grad = carried
        row_first, head_index, kv_index, query_part, key_head, value_head, scores = item_inputs(
            item_index
        )
        logsum = lax.dynamic_index_in_dim(logsum_items, item_index, 0, keepdims=False)
        probability = jnp.exp(scores - logsum[:, None])
        grad_part = lax.dynamic_slice(
            grad_attended, (row_first, head_index * HD), (query_block, HD)
        )
        grad_prob = contract_last(grad_part, value_head)
        inner_sum = jnp.sum(probability * grad_prob, axis=1, keepdims=True)
        grad_scores = (probability * (grad_prob - inner_sum)).astype(jnp.bfloat16)
        query_grad = jnp.dot(grad_scores, key_head, preferred_element_type=jnp.float32) * attn_scale
        key_part = contract_first(grad_scores, query_part) * attn_scale
        value_part = contract_first(probability.astype(jnp.bfloat16), grad_part)
        key_old = lax.dynamic_slice_in_dim(key_grad, kv_index * HD, HD, 1)
        key_grad = lax.dynamic_update_slice_in_dim(key_grad, key_old + key_part, kv_index * HD, 1)
        value_old = lax.dynamic_slice_in_dim(value_grad, kv_index * HD, HD, 1)
        value_grad = lax.dynamic_update_slice_in_dim(
            value_grad, value_old + value_part, kv_index * HD, 1
        )
        return ((key_grad, value_grad), query_grad)

    zero_grads = jnp.zeros((seq_length, kv_local * HD), jnp.float32)
    (key_grad_seq, value_grad_seq), query_grad_items = lax.scan(
        attend_back, (zero_grads, zero_grads), jnp.arange(item_count, dtype=jnp.int32)
    )
    key_grad_block, value_grad_block = (
        lax.psum_scatter(
            key_grad_seq.astype(jnp.bfloat16), "nar", scatter_dimension=0, tiled=True
        ).astype(jnp.float32),
        lax.psum_scatter(
            value_grad_seq.astype(jnp.bfloat16), "nar", scatter_dimension=0, tiled=True
        ).astype(jnp.float32),
    )
    query_grad_rows = (
        query_grad_items.reshape(block_count, query_heads, query_block, HD)
        .transpose(0, 2, 1, 3)
        .reshape(block_tokens, query_heads, HD)
    )
    query_grad_b = (
        rotate_back(query_grad_rows, cosine_table, sine_table)
        .astype(jnp.bfloat16)
        .reshape(block_tokens, query_heads * HD)
    )
    key_grad_b = (
        rotate_back(key_grad_block.reshape(block_tokens, kv_local, HD), cosine_table, sine_table)
        .astype(jnp.bfloat16)
        .reshape(block_tokens, kv_local * HD)
    )
    value_grad_b = value_grad_block.astype(jnp.bfloat16)
    query_weight_grad = contract_first(normed_rows, query_grad_b)
    key_weight_grad = contract_first(normed_rows, key_grad_b)
    value_weight_grad = contract_first(normed_rows, value_grad_b)
    grad_normed_attn = lax.psum_scatter(
        (
            contract_last(query_grad_b, query_full)
            + contract_last(key_grad_b, key_local)
            + contract_last(value_grad_b, value_local)
        ).astype(jnp.bfloat16),
        "wid",
        scatter_dimension=0,
        tiled=True,
    ).astype(jnp.float32)
    grad_residual, gain_attn_term = norm_backward(residual, root_attn, gain_attn, grad_normed_attn)
    grad_in = (grad_residual + grad_middle).astype(jnp.bfloat16)[None]
    summed = (
        lax.psum_scatter(
            query_weight_grad.astype(jnp.bfloat16), ("row", "nar"), scatter_dimension=0, tiled=True
        ).astype(jnp.float32),
        lax.psum_scatter(
            key_weight_grad.astype(jnp.bfloat16), ("row", "nar"), scatter_dimension=0, tiled=True
        ).astype(jnp.float32),
        lax.psum_scatter(
            value_weight_grad.astype(jnp.bfloat16), ("row", "nar"), scatter_dimension=0, tiled=True
        ).astype(jnp.float32),
        lax.psum_scatter(
            output_weight_grad.astype(jnp.bfloat16), ("row", "nar"), scatter_dimension=1, tiled=True
        ).astype(jnp.float32),
        lax.psum_scatter(
            gate_weight_grad.astype(jnp.bfloat16), ("row", "nar"), scatter_dimension=0, tiled=True
        ).astype(jnp.float32),
        lax.psum_scatter(
            up_weight_grad.astype(jnp.bfloat16), ("row", "nar"), scatter_dimension=0, tiled=True
        ).astype(jnp.float32),
        lax.psum_scatter(
            down_weight_grad.astype(jnp.bfloat16), ("row", "nar"), scatter_dimension=1, tiled=True
        ).astype(jnp.float32),
        lax.psum_scatter(
            gain_attn_term.astype(jnp.bfloat16), ("row", "nar"), scatter_dimension=0, tiled=True
        ).astype(jnp.float32),
        lax.psum_scatter(
            gain_ffn_term.astype(jnp.bfloat16), ("row", "nar"), scatter_dimension=0, tiled=True
        ).astype(jnp.float32),
    )
    (
        grad_query,
        key_sum,
        value_sum,
        grad_output,
        grad_gate,
        grad_up,
        grad_down,
        gain_attn_sum,
        gain_ffn_sum,
    ) = summed
    key_all, value_all, gain_attn_all, gain_ffn_all = (
        lax.all_gather(key_sum.astype(jnp.bfloat16), "wid", axis=1, tiled=True).astype(
            key_sum.dtype
        ),
        lax.all_gather(value_sum.astype(jnp.bfloat16), "wid", axis=1, tiled=True).astype(
            value_sum.dtype
        ),
        lax.all_gather(gain_attn_sum.astype(jnp.bfloat16), "wid", axis=0, tiled=True).astype(
            gain_attn_sum.dtype
        ),
        lax.all_gather(gain_ffn_sum.astype(jnp.bfloat16), "wid", axis=0, tiled=True).astype(
            gain_ffn_sum.dtype
        ),
    )
    shard_rows = key_sum.shape[0]
    repeats = wid_count * kv_local // KV
    grad_key = key_all.reshape(shard_rows, KV, repeats, HD).sum(axis=2).reshape(shard_rows, KV * HD)
    grad_value = (
        value_all.reshape(shard_rows, KV, repeats, HD).sum(axis=2).reshape(shard_rows, KV * HD)
    )
    grad_gain_attn = gain_attn_all.reshape(wid_count, shard_rows).sum(axis=0)
    grad_gain_ffn = gain_ffn_all.reshape(wid_count, shard_rows).sum(axis=0)
    return (
        hidden_out,
        grad_in,
        grad_query,
        grad_key,
        grad_value,
        grad_output,
        grad_gate,
        grad_up,
        grad_down,
        grad_gain_attn,
        grad_gain_ffn,
    )


MESH = pl.DeviceIdType.MESH
bf16 = jnp.bfloat16
f32 = jnp.float32
VMEM_LIMIT = 60 * 2**20


def spot():
    return lax.axis_index("row"), lax.axis_index("nar"), lax.axis_index("wid")


def greet(partners):
    barrier = pltpu.get_barrier_semaphore()
    total = 0
    for there, device in partners:
        @pl.when(there)
        def _():
            pl.semaphore_signal(barrier, inc=1, device_id=device, device_id_type=MESH)

        total = total + there.astype(jnp.int32)
    pl.semaphore_wait(barrier, total)


def line_partners(r, n, w, wid_count):
    return [
        (w < wid_count - 1, (r, n, jnp.minimum(w + 1, wid_count - 1))),
        (w > 0, (r, n, jnp.maximum(w - 1, 0))),
        (w >= 0, (1 - r, n, w)),
    ]


def each_rows(count, step, body):
    def run(i, carry):
        body(pl.ds(pl.multiple_of(i * step, step), step))
        return carry

    lax.fori_loop(0, count // step, run, 0)


class Gather:
    def __init__(self, buf, sems, me, wid_count):
        self.buf, (self.up_s, self.dn_s, self.pt_s, self.got) = buf, sems
        self.r, self.n, self.w = me
        self.last = wid_count - 1
        self.up = (self.r, self.n, jnp.minimum(self.w + 1, self.last))
        self.dn = (self.r, self.n, jnp.maximum(self.w - 1, 0))
        self.pt = (1 - self.r, self.n, self.w)

    def copy(self, j, sem, device, row=None):
        row = self.r if row is None else row
        return pltpu.make_async_remote_copy(
            self.buf.at[row, j],
            self.buf.at[row, j],
            sem.at[j],
            self.got.at[row, j],
            device_id=device,
            device_id_type=MESH,
        )

    def pass_on(self, j, go_up, go_dn):
        if go_up:
            @pl.when(self.w < self.last)
            def _():
                self.copy(j, self.up_s, self.up).start()

        if go_dn:
            @pl.when(self.w > 0)
            def _():
                self.copy(j, self.dn_s, self.dn).start()

        self.copy(j, self.pt_s, self.pt).start()

    def own(self):
        self.pass_on(self.w, True, True)

    def arrive(self, row, j):
        self.copy(j, self.pt_s, self.pt, row).wait_recv()

    def step(self, k):
        below, above = self.w - k, self.w + k

        @pl.when(below >= 0)
        def _():
            self.arrive(self.r, below)
            self.pass_on(below, True, False)

        @pl.when(above <= self.last)
        def _():
            self.arrive(self.r, above)
            self.pass_on(above, False, True)

    def rest(self):
        for j in range(self.last + 1):
            self.arrive(1 - self.r, j)

    def sent(self):
        for j in range(self.last + 1):
            @pl.when((j <= self.w) & (self.w < self.last))
            def _():
                self.copy(j, self.up_s, self.up).wait_send()

            @pl.when((j >= self.w) & (self.w > 0))
            def _():
                self.copy(j, self.dn_s, self.dn).wait_send()

            self.copy(j, self.pt_s, self.pt).wait_send()


def gather_scratch(shard, width):
    return [pltpu.VMEM((2, 4, shard, width), bf16)] + gather_sems()


def gather_sems():
    return [pltpu.SemaphoreType.DMA((4,))] * 3 + [pltpu.SemaphoreType.DMA((2, 4))]


class Scatter:
    def __init__(self, mine, theirs, bufs, sems, me, wid_count):
        self.mine, self.theirs = mine, theirs
        self.from_pt, self.from_up, self.from_dn = bufs
        self.pt_s, self.pt_g, self.up_s, self.up_g, self.dn_s, self.dn_g = sems
        self.r, self.n, self.w = me
        self.last = wid_count - 1
        self.up = (self.r, self.n, jnp.minimum(self.w + 1, self.last))
        self.dn = (self.r, self.n, jnp.maximum(self.w - 1, 0))
        self.pt = (1 - self.r, self.n, self.w)

    def order(self, i):
        low, high = (3, 0, 2, 1)[i], (0, 3, 1, 2)[i]
        return jnp.where(self.w < 2, low, high)

    def pair(self, s):
        return pltpu.make_async_remote_copy(
            self.theirs.at[s], self.from_pt.at[s], self.pt_s.at[s], self.pt_g.at[s],
            device_id=self.pt, device_id_type=MESH,
        )

    def climb(self, s):
        return pltpu.make_async_remote_copy(
            self.mine.at[s], self.from_dn.at[s], self.up_s.at[s], self.up_g.at[s],
            device_id=self.up, device_id_type=MESH,
        )

    def fall(self, s):
        return pltpu.make_async_remote_copy(
            self.mine.at[s], self.from_up.at[s], self.dn_s.at[s], self.dn_g.at[s],
            device_id=self.dn, device_id_type=MESH,
        )

    def add(self, s, others):
        def body(rows):
            total = self.mine[s, rows, :].astype(f32)
            for other in others:
                total = total + other[s, rows, :].astype(f32)
            self.mine[s, rows, :] = total.astype(bf16)

        each_rows(self.mine.shape[1], 16, body)

    def step(self, s):
        self.pair(s).wait_recv()

        @pl.when((s > self.w) & (self.w > 0))
        def _():
            self.climb(s).wait_recv()
            self.add(s, (self.from_pt, self.from_dn))

        @pl.when((s < self.w) & (self.w < self.last))
        def _():
            self.fall(s).wait_recv()
            self.add(s, (self.from_pt, self.from_up))

        @pl.when(((s > self.w) & (self.w == 0)) | ((s < self.w) & (self.w == self.last)))
        def _():
            self.add(s, (self.from_pt,))

        @pl.when(s > self.w)
        def _():
            self.climb(s).start()

        @pl.when(s < self.w)
        def _():
            self.fall(s).start()

    def total(self, out):
        w = self.w

        def first(rows):
            out[rows, :] = self.mine[w, rows, :].astype(f32) + self.from_pt[w, rows, :].astype(f32)

        each_rows(out.shape[0], 16, first)

        @pl.when(w > 0)
        def _():
            self.climb(w).wait_recv()

            def more(rows):
                out[rows, :] += self.from_dn[w, rows, :].astype(f32)

            each_rows(out.shape[0], 16, more)

        @pl.when(w < self.last)
        def _():
            self.fall(w).wait_recv()

            def more(rows):
                out[rows, :] += self.from_up[w, rows, :].astype(f32)

            each_rows(out.shape[0], 16, more)

    def sent(self):
        for s in range(self.last + 1):
            self.pair(s).wait_send()

            @pl.when(s > self.w)
            def _():
                self.climb(s).wait_send()

            @pl.when(s < self.w)
            def _():
                self.fall(s).wait_send()


def scatter_bufs(shard, width):
    return [pltpu.VMEM((4, shard, width), bf16)] * 3


def scatter_sems():
    return [pltpu.SemaphoreType.DMA((4,))] * 6


def vmem():
    return pl.BlockSpec(memory_space=pltpu.VMEM)


def hbm():
    return pl.BlockSpec(memory_space=pl.ANY)


def comm_call(kernel, name, cid, out_shape, in_specs, out_specs, scratch, args, flops=0, sent=0):
    return pl.pallas_call(
        kernel,
        out_shape=out_shape,
        in_specs=in_specs,
        out_specs=out_specs,
        scratch_shapes=scratch,
        compiler_params=pltpu.CompilerParams(
            collective_id=cid, has_side_effects=True, vmem_limit_bytes=VMEM_LIMIT
        ),
        cost_estimate=pl.CostEstimate(flops=flops, bytes_accessed=sent, transcendentals=0),
        name=name,
    )(*args)


def norm_rows(x, gain):
    root = lax.rsqrt(jnp.mean(x * x, axis=-1, keepdims=True) + norm_eps)
    return x * root * gain


def turn(x, cosine, sine):
    lane = lax.broadcasted_iota(jnp.int32, x.shape, 1)
    swapped = jnp.where(lane % 64 < 32, pltpu.roll(x, 96, 1), pltpu.roll(x, 32, 1))
    return x * cosine + swapped * sine


def enter_kernel(hidden, gain, tab, rows_out, tabs_out, buf, up_s, dn_s, pt_s, got, tabs, tab_s, tab_g, out_s):
    me = spot()
    r, n, w = me
    greet(line_partners(r, n, w, 4))
    gather = Gather(buf, (up_s, dn_s, pt_s, got), me, 4)
    tab_copy = pltpu.make_async_remote_copy(
        tab, tabs.at[r], tab_s, tab_g, device_id=(1 - r, n, w), device_id_type=MESH
    )

    def body(rows):
        buf[r, w, rows, :] = norm_rows(hidden[rows, :].astype(f32), gain[...]).astype(bf16)

    each_rows(hidden.shape[0], 16, body)
    gather.own()
    tab_copy.start()

    def keep(rows):
        tabs[r, rows, :] = tab[rows, :]

    each_rows(tab.shape[0], 16, keep)
    for k in (1, 2, 3):
        gather.step(k)
    gather.rest()
    out = pltpu.make_async_copy(buf, rows_out, out_s.at[0])
    out.start()
    tab_copy.wait_recv()
    out_tab = pltpu.make_async_copy(tabs, tabs_out, out_s.at[1])
    out_tab.start()
    gather.sent()
    tab_copy.wait_send()
    out.wait()
    out_tab.wait()


def enter(hidden, gain, tab):
    shard, width = hidden.shape
    return comm_call(
        enter_kernel, "enter", 1,
        (
            jax.ShapeDtypeStruct((2, 4, shard, width), bf16),
            jax.ShapeDtypeStruct((2,) + tab.shape, f32),
        ),
        [vmem()] * 3, [hbm()] * 2,
        gather_scratch(shard, width)
        + [
            pltpu.VMEM((2,) + tab.shape, f32),
            pltpu.SemaphoreType.DMA(()),
            pltpu.SemaphoreType.DMA(()),
            pltpu.SemaphoreType.DMA((2,)),
        ],
        (hidden, gain, tab), flops=10**10, sent=10**8,
    )


def nar_device(r, n, w, by):
    return (r, jnp.clip(n + by, 0, 3), w)


def load_pieces(pieces, target, sems, n):
    own, by_x, by_y, far_a, far_b = pieces
    rows = own.shape[0] // 2
    copies = [
        pltpu.make_async_copy(own, target.at[n], sems.at[0]),
        pltpu.make_async_copy(by_x, target.at[n ^ 1], sems.at[1]),
        pltpu.make_async_copy(by_y, target.at[n ^ 2], sems.at[2]),
        pltpu.make_async_copy(far_a, target.at[n ^ 3, pl.ds(0, rows)], sems.at[3]),
        pltpu.make_async_copy(far_b, target.at[n ^ 3, pl.ds(rows, rows)], sems.at[4]),
    ]
    for copy in copies:
        copy.start()
    return copies


def project_kernel(
    x, a0, a1, a2, a3, a4, tabs, q_out, kv_out, p1_out, kv, s_s, s_g, out_s, p1, in_s, p1_s
):
    r, n, w = spot()
    loads = load_pieces((a0, a1, a2, a3, a4), p1, in_s, n)
    greet(
        [
            (n >= 1, nar_device(r, n, w, -1)),
            (n >= 2, nar_device(r, n, w, -2)),
            (n <= 2, nar_device(r, n, w, 1)),
            (n <= 1, nar_device(r, n, w, 2)),
        ]
    )

    def copy(row, slot, by):
        return pltpu.make_async_remote_copy(
            kv.at[row, 2], kv.at[row, slot], s_s.at[row, slot], s_g.at[row, slot],
            device_id=nar_device(r, n, w, by), device_id_type=MESH,
        )

    for load in loads:
        load.wait()
    p1_copy = pltpu.make_async_copy(p1, p1_out, p1_s)
    p1_copy.start()
    lane = lax.broadcasted_iota(jnp.int32, (256, 128), 1)
    weight = p1[:, :, 0:384].reshape(2048, 384)
    for row in range(2):
        def tile(i, carry):
            rows = pl.ds(pl.multiple_of(i * 256, 256), 256)
            cosine, sine = tabs[row, rows, 0:128], tabs[row, rows, 128:256]
            pre = jnp.dot(x[row, rows, :], weight, preferred_element_type=f32)
            q_out[row, rows, 0:128] = turn(pre[:, 0:128], cosine, sine).astype(bf16)
            q_out[row, rows, 128:256] = turn(pre[:, 128:256], cosine, sine).astype(bf16)
            both = pre[:, 256:384]
            kv[row, 2, rows, :] = jnp.where(lane < 64, turn(both, cosine, sine), both).astype(bf16)
            return carry

        lax.fori_loop(0, 2, tile, 0)

        @pl.when(n <= 2)
        def _():
            copy(row, 1, 1).start()

        @pl.when(n <= 1)
        def _():
            copy(row, 0, 2).start()

        for slot, least in ((1, 1), (0, 2)):
            @pl.when(n < least)
            def _():
                kv[row, slot] = jnp.zeros((512, 128), bf16)

    for row in range(2):
        for slot, least, by in ((1, 1, 1), (0, 2, 2)):
            @pl.when(n >= least)
            def _():
                copy(row, slot, by).wait_recv()

    out = pltpu.make_async_copy(kv, kv_out, out_s)
    out.start()
    for row in range(2):
        @pl.when(n <= 2)
        def _():
            copy(row, 1, 1).wait_send()

        @pl.when(n <= 1)
        def _():
            copy(row, 0, 2).wait_send()

    out.wait()
    p1_copy.wait()


def project(x, pieces, tabs):
    return comm_call(
        project_kernel, "project", 2,
        (
            jax.ShapeDtypeStruct((2, 512, 256), bf16),
            jax.ShapeDtypeStruct((2, 3, 512, 128), bf16),
            jax.ShapeDtypeStruct((4, 512, 640), bf16),
        ),
        [vmem()] + [hbm()] * 5 + [vmem()], [vmem(), hbm(), hbm()],
        [
            pltpu.VMEM((2, 3, 512, 128), bf16),
            pltpu.SemaphoreType.DMA((2, 3)),
            pltpu.SemaphoreType.DMA((2, 3)),
            pltpu.SemaphoreType.DMA(()),
            pltpu.VMEM((4, 512, 640), bf16),
            pltpu.SemaphoreType.DMA((5,)),
            pltpu.SemaphoreType.DMA(()),
        ],
        (x, *pieces, tabs), flops=10**10, sent=10**7,
    )


KEYS = 256
QUERIES = 128


def stack_low(x):
    lane = lax.broadcasted_iota(jnp.int32, (QUERIES, 128), 1)
    zero = jnp.zeros((QUERIES, 128), x.dtype)
    parts = []
    for pair in range(2):
        block = x[:, pair * 128 : pair * 128 + 128]
        parts.append(jnp.where(lane < 64, block, zero))
        parts.append(jnp.where(lane < 64, pltpu.roll(block, 64, 1), zero))
    return jnp.concatenate(parts, axis=0)


def stack_high(x):
    lane = lax.broadcasted_iota(jnp.int32, (QUERIES, 128), 1)
    zero = jnp.zeros((QUERIES, 128), x.dtype)
    parts = []
    for pair in range(2):
        block = x[:, pair * 128 : pair * 128 + 128]
        parts.append(jnp.where(lane >= 64, pltpu.roll(block, 64, 1), zero))
        parts.append(jnp.where(lane >= 64, block, zero))
    return jnp.concatenate(parts, axis=0)


def unstack(x, low):
    lane = lax.broadcasted_iota(jnp.int32, (QUERIES, 128), 1)
    out = []
    for pair in range(2):
        even = x[2 * pair * QUERIES : (2 * pair + 1) * QUERIES]
        odd = x[(2 * pair + 1) * QUERIES : (2 * pair + 2) * QUERIES]
        if low:
            out.append(jnp.where(lane < 64, even, pltpu.roll(odd, 64, 1)))
        else:
            out.append(jnp.where(lane < 64, pltpu.roll(even, 64, 1), odd))
    return jnp.concatenate(out, axis=1)


def allowed_tile(starts, tile, first_query):
    key = lax.broadcasted_iota(jnp.int32, (QUERIES, KEYS), 1) + tile * KEYS
    query = lax.broadcasted_iota(jnp.int32, (QUERIES, KEYS), 0) + first_query
    start = jnp.concatenate([starts] * (KEYS // 128), axis=1)
    ok = (key <= query) & (key.astype(f32) >= start)
    return jnp.concatenate([ok] * 4, axis=0)


def key_tiles(low, row, block):
    first_query = 1024 + block * QUERIES
    return low[row * 4 + block] // KEYS, first_query // KEYS + 1, first_query


def attend_kernel(low, q, kv, starts, out, lse):
    row, block = pl.program_id(0), pl.program_id(1)
    first, end, first_query = key_tiles(low, row, block)
    query = stack_low(q[0].astype(f32)).astype(bf16)

    def body(tile, carry):
        top, total, acc = carry
        both = kv[0, pl.ds(pl.multiple_of(tile * KEYS, KEYS), KEYS), :]
        scores = contract_last(query, both) * 0.125
        ok = allowed_tile(starts[0], tile, first_query)
        scores = jnp.where(ok, scores, masked_score)
        new_top = jnp.maximum(top, jnp.max(scores, axis=1, keepdims=True))
        shrink = jnp.exp(top - new_top)
        part = jnp.exp(scores - new_top)
        total = total * shrink + jnp.sum(part, axis=1, keepdims=True)
        acc = acc * shrink + jnp.dot(part.astype(bf16), both, preferred_element_type=f32)
        return new_top, total, acc

    top, total, acc = lax.fori_loop(
        first, end, body,
        (
            jnp.full((4 * QUERIES, 1), masked_score, f32),
            jnp.zeros((4 * QUERIES, 1), f32),
            jnp.zeros((4 * QUERIES, 128), f32),
        ),
    )
    out[0] = unstack(acc / total, False).astype(bf16)
    lse[0, 0] = jnp.broadcast_to(top + jnp.log(total), (4 * QUERIES, 128))


def attend_specs():
    return [
        pl.BlockSpec((1, QUERIES, 256), lambda i, j, low: (i, j, 0)),
        pl.BlockSpec((1, 1536, 128), lambda i, j, low: (i, 0, 0)),
        pl.BlockSpec((1, QUERIES, 128), lambda i, j, low: (i, j, 2)),
    ]


def attend(low, q, kv, tabs):
    return pl.pallas_call(
        attend_kernel,
        out_shape=(
            jax.ShapeDtypeStruct((2, 512, 256), bf16),
            jax.ShapeDtypeStruct((2, 4, 4 * QUERIES, 128), f32),
        ),
        grid_spec=pltpu.PrefetchScalarGridSpec(
            num_scalar_prefetch=1, grid=(2, 4),
            in_specs=attend_specs(),
            out_specs=[
                pl.BlockSpec((1, QUERIES, 256), lambda i, j, low: (i, j, 0)),
                pl.BlockSpec((1, 1, 4 * QUERIES, 128), lambda i, j, low: (i, j, 0, 0)),
            ],
        ),
        compiler_params=pltpu.CompilerParams(vmem_limit_bytes=VMEM_LIMIT),
        cost_estimate=pl.CostEstimate(flops=2 * 10**10, bytes_accessed=10**7, transcendentals=10**7),
        name="attend",
    )(low, q, kv, tabs)


def attend_back_kernel(low, q, kv, starts, turns, att, grad, lse, dq_out, dkv_out, dkv):
    row, block = pl.program_id(0), pl.program_id(1)
    first, end, first_query = key_tiles(low, row, block)

    @pl.when(block == 0)
    def _():
        dkv[...] = jnp.zeros_like(dkv)

    query = stack_low(q[0].astype(f32)).astype(bf16)
    grads = stack_high(grad[0].astype(f32))
    inner = jnp.sum(grads * stack_high(att[0].astype(f32)), axis=1, keepdims=True)
    grads = grads.astype(bf16)
    logsum = jnp.concatenate([lse[0, 0]] * (KEYS // 128), axis=1)

    def body(tile, dq):
        rows = pl.ds(pl.multiple_of(tile * KEYS, KEYS), KEYS)
        both = kv[0, rows, :]
        ok = allowed_tile(starts[0], tile, first_query)
        scores = contract_last(query, both) * 0.125
        prob = jnp.where(ok, jnp.exp(scores - logsum), 0.0)
        grad_prob = contract_last(grads, both)
        grad_scores = (prob * (grad_prob - inner)).astype(bf16)
        dkv[rows, :] += contract_first(grad_scores, query) * 0.125 + contract_first(
            prob.astype(bf16), grads
        )
        return dq + jnp.dot(grad_scores, both, preferred_element_type=f32)

    dq = lax.fori_loop(first, end, body, jnp.zeros((4 * QUERIES, 128), f32))
    flat = unstack(dq, True) * 0.125
    cosine, sine = turns[0, :, 0:128], -turns[0, :, 128:256]
    dq_out[0, :, 0:128] = turn(flat[:, 0:128], cosine, sine).astype(bf16)
    dq_out[0, :, 128:256] = turn(flat[:, 128:256], cosine, sine).astype(bf16)

    @pl.when(block == 3)
    def _():
        dkv_out[0] = dkv[...]


def attend_back(low, q, kv, tabs, att, grad, lse):
    tile = pl.BlockSpec((1, QUERIES, 256), lambda i, j, low: (i, j, 0))
    return pl.pallas_call(
        attend_back_kernel,
        out_shape=(
            jax.ShapeDtypeStruct((2, 512, 256), bf16),
            jax.ShapeDtypeStruct((2, 1536, 128), f32),
        ),
        grid_spec=pltpu.PrefetchScalarGridSpec(
            num_scalar_prefetch=1, grid=(2, 4),
            in_specs=attend_specs()
            + [tile, tile, tile, pl.BlockSpec((1, 1, 4 * QUERIES, 128), lambda i, j, low: (i, j, 0, 0))],
            out_specs=[tile, pl.BlockSpec((1, 1536, 128), lambda i, j, low: (i, 0, 0))],
            scratch_shapes=[pltpu.VMEM((1536, 128), f32)],
        ),
        compiler_params=pltpu.CompilerParams(vmem_limit_bytes=VMEM_LIMIT),
        cost_estimate=pl.CostEstimate(flops=4 * 10**10, bytes_accessed=10**7, transcendentals=10**7),
        name="attend_back",
    )(low, q, kv, tabs, tabs, att, grad, lse)


def out_block(p1, nn, half):
    return p1[nn, half * 256 : half * 256 + 256, 384:640]


def middle_kernel(
    att, p1, hidden, gain, grad_top, mid_out, ffn_out, grad_out,
    theirs, mine, from_pt, from_up, from_dn, s0, s1, s2, s3, s4, s5,
    gbuf, g0, g1, g2, g3, fbuf, h0, h1, h2, h3, out_s,
):
    me = spot()
    r, n, w = me
    greet(line_partners(r, n, w, 4))
    scatter = Scatter(
        mine, theirs, (from_pt, from_up, from_dn), (s0, s1, s2, s3, s4, s5), me, 4
    )
    tops = Gather(gbuf, (g0, g1, g2, g3), me, 4)
    ffn = Gather(fbuf, (h0, h1, h2, h3), me, 4)

    def keep(rows):
        gbuf[r, w, rows, :] = grad_top[rows, :]

    each_rows(grad_top.shape[0], 16, keep)
    for i in range(4):
        s = scatter.order(i)
        rows = pl.ds(pl.multiple_of(s * 128, 128), 128)
        left = jnp.concatenate([att[1 - r, rows, :], att[r, rows, :]], axis=0)
        for nn in range(4):
            for half in range(2):
                part = jnp.dot(left, out_block(p1, nn, half), preferred_element_type=f32).astype(bf16)
                columns = slice(nn * 512 + half * 256, nn * 512 + half * 256 + 256)
                theirs[s, :, columns] = part[0:128]
                mine[s, :, columns] = part[128:256]
        scatter.pair(s).start()
    for i in range(4):
        scatter.step(scatter.order(i))
        if i == 0:
            tops.own()
        else:
            tops.step(i)
    scatter.total(mid_out)

    def body(rows):
        middle = mid_out[rows, :] + hidden[rows, :].astype(f32)
        mid_out[rows, :] = middle
        fbuf[r, w, rows, :] = norm_rows(middle, gain[...]).astype(bf16)

    each_rows(hidden.shape[0], 16, body)
    ffn.own()
    tops.rest()
    out_g = pltpu.make_async_copy(gbuf, grad_out, out_s.at[0])
    out_g.start()
    for k in (1, 2, 3):
        ffn.step(k)
    ffn.rest()
    out_f = pltpu.make_async_copy(fbuf, ffn_out, out_s.at[1])
    out_f.start()
    scatter.sent()
    tops.sent()
    ffn.sent()
    out_g.wait()
    out_f.wait()


def middle_stage(att, p1, hidden, gain, grad_top):
    shard, width = hidden.shape
    rows = jax.ShapeDtypeStruct((2, 4, shard, width), bf16)
    return comm_call(
        middle_kernel, "middle", 3,
        (jax.ShapeDtypeStruct((shard, width), f32), rows, rows),
        [vmem()] * 5, [vmem(), hbm(), hbm()],
        [pltpu.VMEM((4, shard, width), bf16)] * 2
        + scatter_bufs(shard, width) + scatter_sems()
        + gather_scratch(shard, width) + gather_scratch(shard, width)
        + [pltpu.SemaphoreType.DMA((2,))],
        (att, p1, hidden, gain, grad_top), flops=10**10, sent=2 * 10**8,
    )


class Spread:
    def __init__(self, outs, sems, me):
        self.a_send, self.a_keep, self.b_send, self.b_keep = outs
        self.r, self.n, self.w = me
        self.give_s, self.give_g, self.keep_s = sems

    def copies(self, wide, row, place, give):
        for k in range(4):
            block = wide.at[self.n ^ k]
            for part in range(2):
                source = block.at[pl.ds(part * 128, 128)]
                if part == 0:
                    target = (self.a_send if k & 1 else self.a_keep).at[k >> 1]
                else:
                    target = (self.b_send if k >= 2 else self.b_keep).at[k & 1]
                target = place(target)
                at = k * 2 + part
                if give:
                    yield pltpu.make_async_remote_copy(
                        source, target, self.give_s.at[row, at], self.give_g.at[row, at],
                        device_id=(1 - self.r, self.n, self.w), device_id_type=MESH,
                    )
                else:
                    yield pltpu.make_async_copy(source, target, self.keep_s.at[row, at])

    def start(self, *args):
        for copy in self.copies(*args):
            copy.start()

    def wait_send(self, *args):
        for copy in self.copies(*args):
            copy.wait_send()

    def wait_recv(self, *args):
        for copy in self.copies(*args):
            copy.wait_recv()

    def wait(self, *args):
        for copy in self.copies(*args):
            copy.wait()


def spread_sems(count):
    return [pltpu.SemaphoreType.DMA((count, 8))] * 3


def ffn_kernel(
    x, tops, *refs
):
    pieces, refs = refs[:15], refs[15:]
    (
        gain, part_out, sum_out, gain_out, o0, o1, o2, o3,
        theirs, mine, from_pt, from_up, from_dn, s0, s1, s2, s3, s4, s5,
        act, dgu, stage, wide, out_s, give_s, give_g, keep_s, p2, in_s,
    ) = refs
    me = spot()
    r, n, w = me
    loads = []
    for j in range(3):
        loads += load_pieces(pieces[5 * j : 5 * j + 5], p2.at[j], in_s.at[j], n)
    greet(line_partners(r, n, w, 4))
    scatter = Scatter(
        mine, theirs, (from_pt, from_up, from_dn), (s0, s1, s2, s3, s4, s5), me, 4
    )
    gain_out[...] = jnp.zeros_like(gain_out)
    for load in loads:
        load.wait()

    def put(s, slot, row_slot, row):
        return pltpu.make_async_copy(
            stage.at[slot, row_slot], part_out.at[row, s], out_s.at[slot, row_slot]
        )

    for i in range(4):
        s = scatter.order(i)
        slot = i % 2
        rows_t = pl.ds(pl.multiple_of((1 - r) * 512 + s * 128, 128), 128)
        rows_m = pl.ds(pl.multiple_of(r * 512 + s * 128, 128), 128)
        if i >= 2:
            put(s, slot, 0, 1 - r).wait()
            put(s, slot, 1, r).wait()

        def hidden_tile(ft, carry):
            columns = pl.ds(pl.multiple_of(ft * 256, 256), 256)
            left = jnp.concatenate([x[rows_t, :], x[rows_m, :]], axis=0)
            gate = jnp.dot(left, p2[0, :, :, columns].reshape(2048, 256), preferred_element_type=f32)
            up = jnp.dot(left, p2[1, :, :, columns].reshape(2048, 256), preferred_element_type=f32)
            sig = 1.0 / (1.0 + jnp.exp(-gate))
            silu = gate * sig
            active = (silu * up).astype(bf16)
            act[rows_t, columns] = active[0:128]
            act[rows_m, columns] = active[128:256]
            f_rows = pl.ds(pl.multiple_of((ft % 2) * 256, 256), 256)
            f_cols = pl.ds(pl.multiple_of((ft // 2) * 512, 512), 512)
            right = jnp.concatenate([p2[2, nn, f_rows, f_cols] for nn in range(4)], axis=1)
            top = jnp.concatenate([tops[rows_t, :], tops[rows_m, :]], axis=0)
            dact = contract_last(top, right)
            dgate = (dact * up * (sig * (1.0 + gate * (1.0 - sig)))).astype(bf16)
            dup = (dact * silu).astype(bf16)
            dgu[rows_t, columns] = dgate[0:128]
            dgu[rows_m, columns] = dgate[128:256]
            later = pl.ds(pl.multiple_of(1024 + ft * 256, 256), 256)
            dgu[rows_t, later] = dup[0:128]
            dgu[rows_m, later] = dup[128:256]
            return carry

        lax.fori_loop(0, 4, hidden_tile, 0)

        def model_tile(dt, carry):
            nn, half = dt // 2, dt % 2
            columns = pl.ds(pl.multiple_of(dt * 256, 256), 256)
            inner = pl.ds(pl.multiple_of(half * 256, 256), 256)
            other = pl.ds(pl.multiple_of(512 + half * 256, 256), 256)
            left = jnp.concatenate([dgu[rows_t, :], dgu[rows_m, :]], axis=0)
            right = jnp.concatenate([p2[0, nn, inner, :], p2[1, nn, inner, :]], axis=1)
            part = contract_last(left, right)
            seen = jnp.concatenate([x[rows_t, columns], x[rows_m, columns]], axis=0)
            terms = part * seen.astype(f32)
            gain_out[:, columns] += jnp.sum(terms.reshape(32, 8, 256), axis=0)
            part = part.astype(bf16)
            theirs[s, :, columns] = part[0:128]
            mine[s, :, columns] = part[128:256]
            left = jnp.concatenate([act[rows_t, :], act[rows_m, :]], axis=0)
            right = jnp.concatenate([p2[2, nn, :, inner], p2[2, nn, :, other]], axis=0)
            part = jnp.dot(left, right, preferred_element_type=f32).astype(bf16)
            stage[slot, 0, :, columns] = part[0:128]
            stage[slot, 1, :, columns] = part[128:256]
            return carry

        lax.fori_loop(0, 8, model_tile, 0)
        scatter.pair(s).start()
        put(s, slot, 0, 1 - r).start()
        put(s, slot, 1, r).start()

    def scale(rows):
        gain_out[rows, :] = gain_out[rows, :] / gain[...]

    each_rows(8, 8, scale)

    spread = Spread((o0, o1, o2, o3), (give_s, give_g, keep_s), me)
    columns_here = pl.ds(pl.multiple_of(r * 1024, 1024), 1024)

    def moved(which, half):
        def place(target):
            return target.at[which, :, columns_here]

        return wide.at[which % 2, half], which, place, half == 0

    for which in range(3):
        scatter.step(scatter.order(which))
        if which == 2:
            spread.wait_send(*moved(0, 0))
            spread.wait(*moved(0, 1))
        for half in range(2):
            d_first = (jnp.where(half == 0, 1 - r, r)) * 1024

            def weight_tile(i, carry):
                d_rows = pl.ds(pl.multiple_of(d_first + i * 256, 256), 256)
                source = x if which < 2 else tops
                left = source[:, d_rows]
                if which < 2:
                    right = dgu[:, which * 1024 : which * 1024 + 1024]
                else:
                    right = act[...]
                wide[which % 2, half, i] = contract_first(left, right).astype(bf16)
                return carry

            lax.fori_loop(0, 4, weight_tile, 0)
            spread.start(*moved(which, half))
    scatter.step(scatter.order(3))
    scatter.total(sum_out)
    scatter.sent()
    for which in range(3):
        spread.wait_recv(*moved(which, 0))
        if which > 0:
            spread.wait_send(*moved(which, 0))
            spread.wait(*moved(which, 1))
    for slot in range(2):
        put(0, slot, 0, 1 - r).wait()
        put(0, slot, 1, r).wait()


def spread_shapes(*dims):
    return (jax.ShapeDtypeStruct((2,) + dims, bf16),) * 4


def ffn_stage(x, tops, pieces, gain):
    shard, width = 128, 2048
    return comm_call(
        ffn_kernel, "ffn", 4,
        (
            jax.ShapeDtypeStruct((2, 4, shard, width), bf16),
            jax.ShapeDtypeStruct((shard, width), f32),
            jax.ShapeDtypeStruct((8, width), f32),
        )
        + spread_shapes(3, 128, width),
        [vmem()] * 2 + [hbm()] * 15 + [vmem()], [hbm(), vmem(), vmem()] + [hbm()] * 4,
        [pltpu.VMEM((4, shard, width), bf16)] * 2
        + scatter_bufs(shard, width) + scatter_sems()
        + [
            pltpu.VMEM((1024, 1024), bf16),
            pltpu.VMEM((1024, 2048), bf16),
            pltpu.VMEM((2, 2, shard, width), bf16),
            pltpu.VMEM((2, 2, 4, 256, 1024), bf16),
            pltpu.SemaphoreType.DMA((2, 2)),
        ]
        + spread_sems(3)
        + [pltpu.VMEM((3, 4, 512, 1024), bf16), pltpu.SemaphoreType.DMA((3, 5))],
        (x, tops, *pieces, gain), flops=4 * 10**10, sent=10**8,
    )


def norm_back(values, gain, grad):
    root = lax.rsqrt(jnp.mean(values * values, axis=-1, keepdims=True) + norm_eps)
    weighted = grad * gain
    inner = jnp.mean(weighted * values, axis=-1, keepdims=True)
    return root * weighted - values * (root * root * root) * inner


def branch_kernel(
    total, mid, grad_top, gain, parts, p1, att, hid_out, gmid_out, datt_out, o0, o1, o2, o3,
    mine, from_pt, from_up, from_dn, s0, s1, s2, s3, s4, s5,
    buf, g0, g1, g2, g3, acc, wide, give_s, give_g, keep_s,
):
    me = spot()
    r, n, w = me
    greet(line_partners(r, n, w, 4))
    scatter = Scatter(
        mine, parts.at[1 - r], (from_pt, from_up, from_dn), (s0, s1, s2, s3, s4, s5), me, 4
    )
    gather = Gather(buf, (g0, g1, g2, g3), me, 4)

    def body(rows):
        grad = norm_back(mid[rows, :], gain[...], total[rows, :]) + grad_top[rows, :].astype(f32)
        gmid_out[rows, :] = grad
        buf[r, w, rows, :] = grad.astype(bf16)

    each_rows(mid.shape[0], 16, body)
    gather.own()
    for i in range(4):
        scatter.pair(scatter.order(i)).start()

    for s in range(4):
        def fill(rows):
            mine[s, rows, :] = parts[r, s, rows, :]

        each_rows(128, 16, fill)
    for i in range(4):
        scatter.step(scatter.order(i))
        if i < 3:
            gather.step(i + 1)
    gather.rest()
    for row in range(2):
        for pair in range(2):
            left = jnp.concatenate([buf[row, 2 * pair], buf[row, 2 * pair + 1]], axis=0)
            right = jnp.concatenate(
                [out_block(p1, nn, half) for nn in range(4) for half in range(2)], axis=1
            )
            datt_out[row, pair * 256 : pair * 256 + 256, :] = contract_last(left, right).astype(bf16)

    spread = Spread((o0, o1, o2, o3), (give_s, give_g, keep_s), me)

    def moved(half):
        def place(target):
            return target.at[:, pl.ds(pl.multiple_of(r * 256, 256), 256)]

        return wide.at[half], 0, place, half == 0

    for half in range(2):
        d_first = (jnp.where(half == 0, 1 - r, r)) * 1024

        def weight_tile(i, carry):
            columns = pl.ds(pl.multiple_of(d_first + i * 256, 256), 256)
            left = buf[:, :, :, columns].reshape(1024, 256)
            wide[half, i] = contract_first(left, att[...]).astype(bf16)
            return carry

        lax.fori_loop(0, 4, weight_tile, 0)
        spread.start(*moved(half))
    scatter.total(acc)

    def last(rows):
        hid_out[rows, :] = (acc[rows, :] + mid[rows, :]).astype(bf16)

    each_rows(mid.shape[0], 16, last)
    scatter.sent()
    gather.sent()
    spread.wait(*moved(0))
    spread.wait(*moved(1))


def branch_stage(total, mid, grad_top, gain, parts, p1, att):
    shard, width = mid.shape
    return comm_call(
        branch_kernel, "branch", 5,
        (
            jax.ShapeDtypeStruct((shard, width), bf16),
            jax.ShapeDtypeStruct((shard, width), f32),
            jax.ShapeDtypeStruct((2, 512, 256), bf16),
        )
        + spread_shapes(128, 512),
        [vmem()] * 7, [vmem(), vmem(), vmem()] + [hbm()] * 4,
        [pltpu.VMEM((4, shard, width), bf16)]
        + scatter_bufs(shard, width) + scatter_sems()
        + gather_scratch(shard, width)
        + [
            pltpu.VMEM((shard, width), f32),
            pltpu.VMEM((2, 4, 256, 256), bf16),
        ]
        + spread_sems(1),
        (total, mid, grad_top, gain, parts, p1, att), flops=10**10, sent=10**8,
    )


def unproject_kernel(
    dq, dkv, x, p1, tabs, gain, part_out, gain_out, o0, o1, o2, o3,
    send, recv, both, wide_q, wide_kv, s_s, s_g, give_s, give_g, keep_s,
):
    r, n, w = spot()
    greet(
        [
            (n >= 1, nar_device(r, n, w, -1)),
            (n >= 2, nar_device(r, n, w, -2)),
            (n <= 2, nar_device(r, n, w, 1)),
            (n <= 1, nar_device(r, n, w, 2)),
            (n >= 0, (1 - r, n, w)),
        ]
    )

    def copy(row, slot, by):
        return pltpu.make_async_remote_copy(
            send.at[row, slot], recv.at[row, slot], s_s.at[row, slot], s_g.at[row, slot],
            device_id=nar_device(r, n, w, by), device_id_type=MESH,
        )

    for row in range(2):
        for slot, by in ((1, -1), (0, -2)):
            @pl.when(n >= -by)
            def _():
                send[row, slot] = dkv[row, slot].astype(bf16)
                copy(row, slot, by).start()

    spread = Spread((o0, o1, o2, o3), (give_s, give_g, keep_s), (r, n, w))

    def moved_q(half):
        def place(target):
            return target.at[:, pl.ds(pl.multiple_of(r * 256, 256), 256)]

        return wide_q.at[half], 0, place, half == 0

    def moved_kv(half):
        def place(target):
            return target.at[:, pl.ds(pl.multiple_of(512 + r * 128, 128), 128)]

        return wide_kv.at[half], 1, place, half == 0

    for row in range(2):
        both[row * 512 : row * 512 + 512, 0:256] = dq[row]

    def weight(half, columns, wide):
        d_first = (jnp.where(half == 0, 1 - r, r)) * 1024

        def tile(i, carry):
            d_cols = pl.ds(pl.multiple_of(d_first + i * 256, 256), 256)
            wide[half, i] = contract_first(x[:, d_cols], both[:, columns]).astype(bf16)
            return carry

        lax.fori_loop(0, 4, tile, 0)

    for half in range(2):
        weight(half, slice(0, 256), wide_q)
        spread.start(*moved_q(half))
    lane = lax.broadcasted_iota(jnp.int32, (128, 128), 1)
    for row in range(2):
        for slot, by in ((1, -1), (0, -2)):
            @pl.when(n <= 3 + by)
            def _():
                copy(row, slot, by).wait_recv()

        def tile(i, carry):
            rows = pl.ds(pl.multiple_of(i * 128, 128), 128)
            total = dkv[row, 2, rows, :]
            zero = jnp.zeros_like(total)
            total = total + jnp.where(n <= 2, recv[row, 1, rows, :].astype(f32), zero)
            total = total + jnp.where(n <= 1, recv[row, 0, rows, :].astype(f32), zero)
            turned = turn(total, tabs[row, rows, 0:128], -tabs[row, rows, 128:256])
            both[pl.ds(pl.multiple_of(row * 512 + i * 128, 128), 128), 256:384] = jnp.where(
                lane < 64, turned, total
            ).astype(bf16)
            return carry

        lax.fori_loop(0, 4, tile, 0)
    for half in range(2):
        weight(half, slice(256, 384), wide_kv)
        spread.start(*moved_kv(half))
    gain_out[...] = jnp.zeros_like(gain_out)

    def model_tile(dt, carry):
        nn, half = dt // 2, dt % 2
        columns = pl.ds(pl.multiple_of(dt * 256, 256), 256)
        inner = pl.ds(pl.multiple_of(half * 256, 256), 256)
        right = p1[nn, inner, 0:384]
        for row in range(2):
            for block in range(2):
                first = row * 512 + block * 256
                part = contract_last(both[first : first + 256, :], right)
                terms = part * x[first : first + 256, columns].astype(f32)
                gain_out[:, columns] += jnp.sum(terms.reshape(32, 8, 256), axis=0)
                part_out[row, 2 * block, :, columns] = part[0:128].astype(bf16)
                part_out[row, 2 * block + 1, :, columns] = part[128:256].astype(bf16)
        return carry

    lax.fori_loop(0, 8, model_tile, 0)
    gain_out[...] = gain_out[...] / gain[...]
    for row in range(2):
        for slot, by in ((1, -1), (0, -2)):
            @pl.when(n >= -by)
            def _():
                copy(row, slot, by).wait_send()

    for half in range(2):
        spread.wait(*moved_q(half))
        spread.wait(*moved_kv(half))


def unproject(dq, dkv, x, p1, tabs, gain):
    return comm_call(
        unproject_kernel, "unproject", 6,
        (
            jax.ShapeDtypeStruct((2, 4, 128, 2048), bf16),
            jax.ShapeDtypeStruct((8, 2048), f32),
        )
        + spread_shapes(128, 768),
        [vmem()] * 6, [vmem(), vmem()] + [hbm()] * 4,
        [
            pltpu.VMEM((2, 2, 512, 128), bf16),
            pltpu.VMEM((2, 2, 512, 128), bf16),
            pltpu.VMEM((1024, 384), bf16),
            pltpu.VMEM((2, 4, 256, 256), bf16),
            pltpu.VMEM((2, 4, 256, 128), bf16),
            pltpu.SemaphoreType.DMA((2, 2)),
            pltpu.SemaphoreType.DMA((2, 2)),
        ]
        + spread_sems(2),
        (dq, dkv, x, p1, tabs, gain), flops=10**10, sent=10**7,
    )


def leave_kernel(
    parts, hidden, gain, gmid, gains, grad_out, ga_out,
    mine, from_pt, from_up, from_dn, s0, s1, s2, s3, s4, s5,
    acc, over_wid, summed, over_rest, w_s, w_g, t_s, t_g,
):
    me = spot()
    r, n, w = me
    partners = [(w != j, (r, n, jnp.int32(j))) for j in range(4)]
    partners += [
        ((r != a) | (n != b), (jnp.int32(a), jnp.int32(b), w)) for a in range(2) for b in range(4)
    ]
    greet(partners)
    scatter = Scatter(
        mine, parts.at[1 - r], (from_pt, from_up, from_dn), (s0, s1, s2, s3, s4, s5), me, 4
    )
    for i in range(4):
        scatter.pair(scatter.order(i)).start()

    def wid_copy(j, slot):
        return pltpu.make_async_remote_copy(
            gains, over_wid.at[slot], w_s.at[j], w_g.at[slot],
            device_id=(r, n, jnp.int32(j)), device_id_type=MESH,
        )

    def rest_copy(a, b, slot):
        return pltpu.make_async_remote_copy(
            summed, over_rest.at[slot], t_s.at[a * 4 + b], t_g.at[slot],
            device_id=(jnp.int32(a), jnp.int32(b), w), device_id_type=MESH,
        )

    for j in range(4):
        @pl.when(w != j)
        def _():
            wid_copy(j, w).start()

    for s in range(4):
        def fill(rows):
            mine[s, rows, :] = parts[r, s, rows, :]

        each_rows(128, 16, fill)
    scatter.step(scatter.order(0))
    summed[...] = gains[...]
    for j in range(4):
        @pl.when(w != j)
        def _():
            wid_copy(j, j).wait_recv()
            summed[...] += over_wid[j]

    for a in range(2):
        for b in range(4):
            @pl.when((r != a) | (n != b))
            def _():
                rest_copy(a, b, r * 4 + n).start()

    for i in (1, 2, 3):
        scatter.step(scatter.order(i))
    mine_block = r * 4 + n
    ga_out[0:1] = summed[pl.ds(mine_block, 1), :]
    ga_out[1:2] = summed[pl.ds(mine_block + 8, 1), :]
    for a in range(2):
        for b in range(4):
            @pl.when((r != a) | (n != b))
            def _():
                slot = a * 4 + b
                rest_copy(a, b, slot).wait_recv()
                ga_out[0:1] += over_rest[slot, pl.ds(mine_block, 1), :]
                ga_out[1:2] += over_rest[slot, pl.ds(mine_block + 8, 1), :]

    scatter.total(acc)

    def last(rows):
        grad = norm_back(hidden[rows, :].astype(f32), gain[...], acc[rows, :])
        grad_out[rows, :] = (grad + gmid[rows, :]).astype(bf16)

    each_rows(hidden.shape[0], 16, last)
    scatter.sent()
    for j in range(4):
        @pl.when(w != j)
        def _():
            wid_copy(j, w).wait_send()

    for a in range(2):
        for b in range(4):
            @pl.when((r != a) | (n != b))
            def _():
                rest_copy(a, b, r * 4 + n).wait_send()


def leave(parts, hidden, gain, gmid, gains):
    shard, width = hidden.shape
    return comm_call(
        leave_kernel, "leave", 7,
        (jax.ShapeDtypeStruct((shard, width), bf16), jax.ShapeDtypeStruct((8, 256), f32)),
        [vmem()] * 5, [vmem()] * 2,
        [pltpu.VMEM((4, shard, width), bf16)]
        + scatter_bufs(shard, width) + scatter_sems()
        + [
            pltpu.VMEM((shard, width), f32),
            pltpu.VMEM((4, 16, 256), f32),
            pltpu.VMEM((16, 256), f32),
            pltpu.VMEM((8, 16, 256), f32),
            pltpu.SemaphoreType.DMA((4,)),
            pltpu.SemaphoreType.DMA((4,)),
            pltpu.SemaphoreType.DMA((8,)),
            pltpu.SemaphoreType.DMA((8,)),
        ],
        (parts, hidden, gain, gmid, gains), flops=10**10, sent=10**8,
    )


def swap_nar(x, bit):
    return lax.ppermute(x, "nar", [(i, i ^ bit) for i in range(4)])


def nar_gather(shard):
    rows = shard.shape[0] // 2
    by_x, by_y = swap_nar(shard, 1), swap_nar(shard, 2)
    return shard, by_x, by_y, swap_nar(by_x[:rows], 2), swap_nar(by_y[rows:], 1)


def nar_scatter(a_send, a_keep, b_send, b_keep):
    def halves(send, keep, first, then):
        total = (keep.astype(f32) + swap_nar(send, first).astype(f32))
        over = swap_nar(total[1].astype(bf16), then)
        return total[0] + over.astype(f32)

    return jnp.concatenate(
        [halves(a_send, a_keep, 1, 2), halves(b_send, b_keep, 2, 1)], axis=-2
    )


def local_fast(
    hidden_in, doc_lengths, w_query, w_key, w_value, w_output, w_gate, w_up, w_down,
    gain_attn, gain_ffn, grad_out,
):
    r, n, w = spot()
    hidden, grad_top = hidden_in[0], grad_out[0]
    gain_a, gain_f = gain_attn[None], gain_ffn[None]
    def half(weight, axis):
        size = weight.shape[axis] // 2
        return lax.dynamic_slice_in_dim(weight, r * size, size, axis)

    head = (w * 2 + r) * HD
    kv_pack = jnp.concatenate(
        [lax.dynamic_slice_in_dim(w_key, head, HD, 1), lax.dynamic_slice_in_dim(w_value, head, HD, 1)],
        axis=1,
    )
    out_half = half(w_output, 0)
    p1_shard = jnp.concatenate(
        [half(w_query, 1), kv_pack, jnp.concatenate([out_half[:, :256], out_half[:, 256:]], axis=0)],
        axis=1,
    )
    down_half = half(w_down, 0)
    p1_pieces = nar_gather(p1_shard)
    gate_pieces = nar_gather(half(w_gate, 1))
    up_pieces = nar_gather(half(w_up, 1))
    down_pieces = nar_gather(jnp.concatenate([down_half[:512], down_half[512:]], axis=1))

    token_ids = n * 512 + jnp.arange(512, dtype=jnp.int32)
    doc_start, places = doc_layout(doc_lengths[0], token_ids)
    angles = places.astype(f32)[:, None] * inverse_freq()[None, :]
    cosine, sine = jnp.cos(angles), jnp.sin(angles)
    start_here = (doc_start - (n - 2) * 512).astype(f32)
    tab = jnp.concatenate(
        [cosine] * 4 + [-sine, sine] * 2 + [jnp.broadcast_to(start_here[:, None], (512, 128))],
        axis=1,
    )

    rows, tabs = enter(hidden, gain_a, tab)
    rows3, rows2 = rows.reshape(2, 512, 2048), rows.reshape(1024, 2048)
    q, kv, p1 = project(rows3, p1_pieces, tabs)
    low = tabs[:, ::QUERIES, 256].astype(jnp.int32).reshape(8)
    kv_flat = kv.reshape(2, 1536, 128)
    att, lse = attend(low, q, kv_flat, tabs)
    mid, ffn_rows, top_rows = middle_stage(att, p1, hidden, gain_f, grad_top)
    parts, total, gain_f_part, *grads = ffn_stage(
        ffn_rows.reshape(1024, 2048), top_rows.reshape(1024, 2048),
        gate_pieces + up_pieces + down_pieces, gain_f,
    )
    summed = nar_scatter(*grads)
    hidden_out, gmid, datt, *grad_o = branch_stage(
        total, mid, grad_top, gain_f, parts, p1, att.reshape(1024, 256)
    )
    summed_o = nar_scatter(*grad_o)
    dq, dkv = attend_back(low, q, kv_flat, tabs, att, datt, lse)
    dparts, gain_a_part, *grad_qkv = unproject(
        dq, dkv.reshape(2, 3, 512, 128), rows2, p1, tabs, gain_a
    )
    summed_qkv = nar_scatter(*grad_qkv)
    gains = jnp.concatenate(
        [gain_f_part.sum(axis=0).reshape(8, 256), gain_a_part.sum(axis=0).reshape(8, 256)], axis=0
    )
    grad_in, gain_sums = leave(dparts, hidden, gain_a, gmid, gains)
    kv_all = lax.all_gather(summed_qkv[:, 512:768].astype(bf16), "wid", axis=1, tiled=True)
    kv_all = kv_all.astype(f32).reshape(256, KV, 2, HD)
    return (
        hidden_out[None],
        grad_in[None],
        summed_qkv[:, 0:512],
        kv_all[:, :, 0].reshape(256, KV * HD),
        kv_all[:, :, 1].reshape(256, KV * HD),
        summed_o.T,
        summed[0],
        summed[1],
        summed[2].T,
        gain_sums[1],
        gain_sums[0],
    )


def solution(mesh):
    in_specs = (
        P("row", ("nar", "wid"), None),
        P("row", None),
        P("nar", "wid"),
        P("nar", None),
        P("nar", None),
        P("wid", "nar"),
        P("nar", "wid"),
        P("nar", "wid"),
        P("wid", "nar"),
        P(),
        P(),
        P("row", ("nar", "wid"), None),
    )
    out_specs = (
        P("row", ("nar", "wid"), None),
        P("row", ("nar", "wid"), None),
        P(("row", "nar"), "wid"),
        P(("row", "nar"), None),
        P(("row", "nar"), None),
        P("wid", ("row", "nar")),
        P(("row", "nar"), "wid"),
        P(("row", "nar"), "wid"),
        P("wid", ("row", "nar")),
        P(("row", "nar")),
        P(("row", "nar")),
    )
    sizes = dict(mesh.shape)
    fits = sizes == {"row": 2, "nar": 4, "wid": 4}

    def body(*args):
        small = args[0].shape == (1, 128, 2048)
        return (local_fast if fits and small else local)(*args)

    return jax.shard_map(body, mesh=mesh, in_specs=in_specs, out_specs=out_specs, check_vma=False)
```

```python
import math

import jax
import jax.numpy as jnp
from jax import lax
from jax.experimental import pallas as pl
from jax.experimental.pallas import tpu as pltpu
from jax.sharding import PartitionSpec as P

H = 32
KV = 8
HD = 64


norm_eps = 1e-05
masked_score = -1e30


def inverse_freq():
    listed = []
    for pair_index in range(HD // 2):
        base_freq = 500000.0 ** (-2.0 * pair_index / HD)
        wavelength = 2.0 * math.pi / base_freq
        smoothing = (8192.0 / wavelength - 1.0) / 3.0
        blended = (1.0 - smoothing) * base_freq / 32.0 + smoothing * base_freq
        if wavelength < 2048.0:
            listed.append(base_freq)
        elif wavelength > 8192.0:
            listed.append(base_freq / 32.0)
        else:
            listed.append(blended)
    return jnp.asarray(listed, dtype=jnp.float32)


def rotate(values, cosine_table, sine_table):
    half_dim = HD // 2
    first_half = values[..., :half_dim]
    second_half = values[..., half_dim:]
    return jnp.concatenate(
        [
            first_half * cosine_table - second_half * sine_table,
            second_half * cosine_table + first_half * sine_table,
        ],
        axis=-1,
    )


def rotate_back(grads_in, cosine_table, sine_table):
    half_dim = HD // 2
    first_half = grads_in[..., :half_dim]
    second_half = grads_in[..., half_dim:]
    return jnp.concatenate(
        [
            first_half * cosine_table + second_half * sine_table,
            second_half * cosine_table - first_half * sine_table,
        ],
        axis=-1,
    )


def doc_layout(lengths_row, token_ids):
    ends_at = jnp.cumsum(lengths_row, dtype=jnp.int32)
    starts_at = ends_at - lengths_row
    inside = (token_ids[:, None] >= starts_at[None, :]) & (token_ids[:, None] < ends_at[None, :])
    doc_start = jnp.sum(jnp.where(inside, starts_at[None, :], 0), axis=1, dtype=jnp.int32)
    return (doc_start, token_ids - doc_start)


def norm_forward(values, gain_vector):
    root_inv = lax.rsqrt(jnp.mean(values * values, axis=-1, keepdims=True) + norm_eps)
    return (root_inv, (values * root_inv * gain_vector).astype(jnp.bfloat16))


def norm_backward(values, root_inv, gain_vector, grad_normed):
    weighted = grad_normed * gain_vector
    inner_sum = jnp.mean(weighted * values, axis=-1, keepdims=True)
    grad_values = root_inv * weighted - values * (root_inv * root_inv * root_inv) * inner_sum
    gain_term = jnp.sum(grad_normed * values * root_inv, axis=0)
    return (grad_values, gain_term)


def contract_last(left_side, right_side):
    return lax.dot_general(
        left_side, right_side, (((1,), (1,)), ((), ())), preferred_element_type=jnp.float32
    )


def contract_first(left_side, right_side):
    return lax.dot_general(
        left_side, right_side, (((0,), (0,)), ((), ())), preferred_element_type=jnp.float32
    )


def local(
    hidden_in,
    doc_lengths,
    w_query,
    w_key,
    w_value,
    w_output,
    w_gate,
    w_up,
    w_down,
    gain_attn,
    gain_ffn,
    grad_out,
):
    wid_count = lax.axis_size("wid")
    nar_count = lax.axis_size("nar")
    wid_index = lax.axis_index("wid")
    nar_index = lax.axis_index("nar")
    local_tokens = hidden_in.shape[1]
    block_tokens = local_tokens * wid_count
    seq_length = block_tokens * nar_count
    query_heads = w_query.shape[1] // HD
    group_size = H // KV
    kv_local = max(query_heads // group_size, 1)
    heads_per_kv = query_heads // kv_local
    kv_first = wid_index * query_heads // group_size
    query_block = min(512, block_tokens)
    block_count = block_tokens // query_block
    item_count = block_count * query_heads
    attn_scale = HD ** (-0.5)
    query_full, key_full, value_full, output_full, gate_full, up_full, down_full = (
        lax.all_gather(w_query, "nar", axis=0, tiled=True),
        lax.all_gather(w_key, "nar", axis=0, tiled=True),
        lax.all_gather(w_value, "nar", axis=0, tiled=True),
        lax.all_gather(w_output, "nar", axis=1, tiled=True),
        lax.all_gather(w_gate, "nar", axis=0, tiled=True),
        lax.all_gather(w_up, "nar", axis=0, tiled=True),
        lax.all_gather(w_down, "nar", axis=1, tiled=True),
    )
    key_local = lax.dynamic_slice_in_dim(key_full, kv_first * HD, kv_local * HD, 1)
    value_local = lax.dynamic_slice_in_dim(value_full, kv_first * HD, kv_local * HD, 1)
    token_ids = nar_index * block_tokens + jnp.arange(block_tokens, dtype=jnp.int32)
    doc_start, places = doc_layout(doc_lengths[0], token_ids)
    angles = places.astype(jnp.float32)[:, None] * inverse_freq()[None, :]
    cosine_table = jnp.cos(angles)[:, None, :]
    sine_table = jnp.sin(angles)[:, None, :]
    key_ids = jnp.arange(seq_length, dtype=jnp.int32)
    residual = hidden_in[0].astype(jnp.float32)
    root_attn, normed_attn = norm_forward(residual, gain_attn)
    normed_rows = lax.all_gather(normed_attn, "wid", axis=0, tiled=True)
    query_pre = jnp.dot(normed_rows, query_full, preferred_element_type=jnp.float32)
    key_pre = jnp.dot(normed_rows, key_local, preferred_element_type=jnp.float32)
    value_rows = jnp.dot(normed_rows, value_local, preferred_element_type=jnp.float32).astype(
        jnp.bfloat16
    )
    query_rot = (
        rotate(query_pre.reshape(block_tokens, query_heads, HD), cosine_table, sine_table)
        .astype(jnp.bfloat16)
        .reshape(block_tokens, query_heads * HD)
    )
    key_rot = (
        rotate(key_pre.reshape(block_tokens, kv_local, HD), cosine_table, sine_table)
        .astype(jnp.bfloat16)
        .reshape(block_tokens, kv_local * HD)
    )
    key_seq, value_seq = (
        lax.all_gather(key_rot, "nar", axis=0, tiled=True),
        lax.all_gather(value_rows, "nar", axis=0, tiled=True),
    )

    def item_inputs(item_index):
        block_index = item_index // query_heads
        head_index = item_index % query_heads
        kv_index = head_index // heads_per_kv
        row_first = block_index * query_block
        query_part = lax.dynamic_slice(query_rot, (row_first, head_index * HD), (query_block, HD))
        key_head = lax.dynamic_slice_in_dim(key_seq, kv_index * HD, HD, 1)
        value_head = lax.dynamic_slice_in_dim(value_seq, kv_index * HD, HD, 1)
        query_ids = lax.dynamic_slice_in_dim(token_ids, row_first, query_block, 0)
        query_starts = lax.dynamic_slice_in_dim(doc_start, row_first, query_block, 0)
        allowed = (key_ids[None, :] <= query_ids[:, None]) & (
            key_ids[None, :] >= query_starts[:, None]
        )
        scores = contract_last(query_part, key_head) * attn_scale
        return (
            row_first,
            head_index,
            kv_index,
            query_part,
            key_head,
            value_head,
            jnp.where(allowed, scores, masked_score),
        )

    def attend(item_index):
        row_first, head_index, kv_index, query_part, key_head, value_head, scores = item_inputs(
            item_index
        )
        row_max = jnp.max(scores, axis=1, keepdims=True)
        exp_scores = jnp.exp(scores - row_max)
        row_total = jnp.sum(exp_scores, axis=1, keepdims=True)
        probability = (exp_scores / row_total).astype(jnp.bfloat16)
        attended = jnp.dot(probability, value_head, preferred_element_type=jnp.float32)
        return (attended, (row_max + jnp.log(row_total))[:, 0])

    attended_items, logsum_items = lax.map(attend, jnp.arange(item_count, dtype=jnp.int32))
    attended_rows = (
        attended_items.reshape(block_count, query_heads, query_block, HD)
        .transpose(0, 2, 1, 3)
        .reshape(block_tokens, query_heads * HD)
        .astype(jnp.bfloat16)
    )
    rows_here = attended_rows
    branch_attn = lax.psum_scatter(
        jnp.dot(rows_here, output_full, preferred_element_type=jnp.float32),
        "wid",
        scatter_dimension=0,
        tiled=True,
    )
    middle = residual + branch_attn
    root_ffn, normed_ffn = norm_forward(middle, gain_ffn)
    ffn_rows = lax.all_gather(normed_ffn, "wid", axis=0, tiled=True)
    gate_proj = jnp.dot(ffn_rows, gate_full, preferred_element_type=jnp.float32)
    up_proj = jnp.dot(ffn_rows, up_full, preferred_element_type=jnp.float32)
    gate_sigmoid = jax.nn.sigmoid(gate_proj)
    gate_silu = gate_proj * gate_sigmoid
    activated = (gate_silu * up_proj).astype(jnp.bfloat16)
    rows_here = activated
    branch_ffn = lax.psum_scatter(
        jnp.dot(rows_here, down_full, preferred_element_type=jnp.float32).astype(jnp.bfloat16),
        "wid",
        scatter_dimension=0,
        tiled=True,
    ).astype(jnp.float32)
    hidden_out = (middle + branch_ffn).astype(jnp.bfloat16)[None]
    grad_top = grad_out[0]
    grad_rows = lax.all_gather(grad_top, "wid", axis=0, tiled=True)
    grad_activated = contract_last(grad_rows, down_full)
    down_weight_grad = contract_first(activated, grad_rows)
    silu_slope = gate_sigmoid * (1.0 + gate_proj * (1.0 - gate_sigmoid))
    grad_gate_b = (grad_activated * up_proj * silu_slope).astype(jnp.bfloat16)
    grad_up_b = (grad_activated * gate_silu).astype(jnp.bfloat16)
    gate_weight_grad = contract_first(ffn_rows, grad_gate_b)
    up_weight_grad = contract_first(ffn_rows, grad_up_b)
    grad_normed_ffn = lax.psum_scatter(
        contract_last(grad_gate_b, gate_full) + contract_last(grad_up_b, up_full),
        "wid",
        scatter_dimension=0,
        tiled=True,
    )
    grad_middle, gain_ffn_term = norm_backward(middle, root_ffn, gain_ffn, grad_normed_ffn)
    grad_middle = grad_middle + grad_top.astype(jnp.float32)
    grad_branch = grad_middle.astype(jnp.bfloat16)
    branch_rows = lax.all_gather(grad_branch, "wid", axis=0, tiled=True)
    grad_attended = contract_last(branch_rows, output_full).astype(jnp.bfloat16)
    output_weight_grad = contract_first(attended_rows, branch_rows)

    def attend_back(carried, item_index):
        key_grad, value_grad = carried
        row_first, head_index, kv_index, query_part, key_head, value_head, scores = item_inputs(
            item_index
        )
        logsum = lax.dynamic_index_in_dim(logsum_items, item_index, 0, keepdims=False)
        probability = jnp.exp(scores - logsum[:, None])
        grad_part = lax.dynamic_slice(
            grad_attended, (row_first, head_index * HD), (query_block, HD)
        )
        grad_prob = contract_last(grad_part, value_head)
        inner_sum = jnp.sum(probability * grad_prob, axis=1, keepdims=True)
        grad_scores = (probability * (grad_prob - inner_sum)).astype(jnp.bfloat16)
        query_grad = jnp.dot(grad_scores, key_head, preferred_element_type=jnp.float32) * attn_scale
        key_part = contract_first(grad_scores, query_part) * attn_scale
        value_part = contract_first(probability.astype(jnp.bfloat16), grad_part)
        key_old = lax.dynamic_slice_in_dim(key_grad, kv_index * HD, HD, 1)
        key_grad = lax.dynamic_update_slice_in_dim(key_grad, key_old + key_part, kv_index * HD, 1)
        value_old = lax.dynamic_slice_in_dim(value_grad, kv_index * HD, HD, 1)
        value_grad = lax.dynamic_update_slice_in_dim(
            value_grad, value_old + value_part, kv_index * HD, 1
        )
        return ((key_grad, value_grad), query_grad)

    zero_grads = jnp.zeros((seq_length, kv_local * HD), jnp.float32)
    (key_grad_seq, value_grad_seq), query_grad_items = lax.scan(
        attend_back, (zero_grads, zero_grads), jnp.arange(item_count, dtype=jnp.int32)
    )
    key_grad_block, value_grad_block = (
        lax.psum_scatter(
            key_grad_seq.astype(jnp.bfloat16), "nar", scatter_dimension=0, tiled=True
        ).astype(jnp.float32),
        lax.psum_scatter(
            value_grad_seq.astype(jnp.bfloat16), "nar", scatter_dimension=0, tiled=True
        ).astype(jnp.float32),
    )
    query_grad_rows = (
        query_grad_items.reshape(block_count, query_heads, query_block, HD)
        .transpose(0, 2, 1, 3)
        .reshape(block_tokens, query_heads, HD)
    )
    query_grad_b = (
        rotate_back(query_grad_rows, cosine_table, sine_table)
        .astype(jnp.bfloat16)
        .reshape(block_tokens, query_heads * HD)
    )
    key_grad_b = (
        rotate_back(key_grad_block.reshape(block_tokens, kv_local, HD), cosine_table, sine_table)
        .astype(jnp.bfloat16)
        .reshape(block_tokens, kv_local * HD)
    )
    value_grad_b = value_grad_block.astype(jnp.bfloat16)
    query_weight_grad = contract_first(normed_rows, query_grad_b)
    key_weight_grad = contract_first(normed_rows, key_grad_b)
    value_weight_grad = contract_first(normed_rows, value_grad_b)
    grad_normed_attn = lax.psum_scatter(
        (
            contract_last(query_grad_b, query_full)
            + contract_last(key_grad_b, key_local)
            + contract_last(value_grad_b, value_local)
        ).astype(jnp.bfloat16),
        "wid",
        scatter_dimension=0,
        tiled=True,
    ).astype(jnp.float32)
    grad_residual, gain_attn_term = norm_backward(residual, root_attn, gain_attn, grad_normed_attn)
    grad_in = (grad_residual + grad_middle).astype(jnp.bfloat16)[None]
    summed = (
        lax.psum_scatter(
            query_weight_grad.astype(jnp.bfloat16), ("row", "nar"), scatter_dimension=0, tiled=True
        ).astype(jnp.float32),
        lax.psum_scatter(
            key_weight_grad.astype(jnp.bfloat16), ("row", "nar"), scatter_dimension=0, tiled=True
        ).astype(jnp.float32),
        lax.psum_scatter(
            value_weight_grad.astype(jnp.bfloat16), ("row", "nar"), scatter_dimension=0, tiled=True
        ).astype(jnp.float32),
        lax.psum_scatter(
            output_weight_grad.astype(jnp.bfloat16), ("row", "nar"), scatter_dimension=1, tiled=True
        ).astype(jnp.float32),
        lax.psum_scatter(
            gate_weight_grad.astype(jnp.bfloat16), ("row", "nar"), scatter_dimension=0, tiled=True
        ).astype(jnp.float32),
        lax.psum_scatter(
            up_weight_grad.astype(jnp.bfloat16), ("row", "nar"), scatter_dimension=0, tiled=True
        ).astype(jnp.float32),
        lax.psum_scatter(
            down_weight_grad.astype(jnp.bfloat16), ("row", "nar"), scatter_dimension=1, tiled=True
        ).astype(jnp.float32),
        lax.psum_scatter(
            gain_attn_term.astype(jnp.bfloat16), ("row", "nar"), scatter_dimension=0, tiled=True
        ).astype(jnp.float32),
        lax.psum_scatter(
            gain_ffn_term.astype(jnp.bfloat16), ("row", "nar"), scatter_dimension=0, tiled=True
        ).astype(jnp.float32),
    )
    (
        grad_query,
        key_sum,
        value_sum,
        grad_output,
        grad_gate,
        grad_up,
        grad_down,
        gain_attn_sum,
        gain_ffn_sum,
    ) = summed
    key_all, value_all, gain_attn_all, gain_ffn_all = (
        lax.all_gather(key_sum.astype(jnp.bfloat16), "wid", axis=1, tiled=True).astype(
            key_sum.dtype
        ),
        lax.all_gather(value_sum.astype(jnp.bfloat16), "wid", axis=1, tiled=True).astype(
            value_sum.dtype
        ),
        lax.all_gather(gain_attn_sum.astype(jnp.bfloat16), "wid", axis=0, tiled=True).astype(
            gain_attn_sum.dtype
        ),
        lax.all_gather(gain_ffn_sum.astype(jnp.bfloat16), "wid", axis=0, tiled=True).astype(
            gain_ffn_sum.dtype
        ),
    )
    shard_rows = key_sum.shape[0]
    repeats = wid_count * kv_local // KV
    grad_key = key_all.reshape(shard_rows, KV, repeats, HD).sum(axis=2).reshape(shard_rows, KV * HD)
    grad_value = (
        value_all.reshape(shard_rows, KV, repeats, HD).sum(axis=2).reshape(shard_rows, KV * HD)
    )
    grad_gain_attn = gain_attn_all.reshape(wid_count, shard_rows).sum(axis=0)
    grad_gain_ffn = gain_ffn_all.reshape(wid_count, shard_rows).sum(axis=0)
    return (
        hidden_out,
        grad_in,
        grad_query,
        grad_key,
        grad_value,
        grad_output,
        grad_gate,
        grad_up,
        grad_down,
        grad_gain_attn,
        grad_gain_ffn,
    )


MESH = pl.DeviceIdType.MESH
bf16 = jnp.bfloat16
f32 = jnp.float32
VMEM_LIMIT = 60 * 2**20


def spot():
    return lax.axis_index("row"), lax.axis_index("nar"), lax.axis_index("wid")


def greet(partners):
    barrier = pltpu.get_barrier_semaphore()
    total = 0
    for there, device in partners:
        @pl.when(there)
        def _():
            pl.semaphore_signal(barrier, inc=1, device_id=device, device_id_type=MESH)

        total = total + there.astype(jnp.int32)
    pl.semaphore_wait(barrier, total)


def line_partners(r, n, w, wid_count):
    return [
        (w < wid_count - 1, (r, n, jnp.minimum(w + 1, wid_count - 1))),
        (w > 0, (r, n, jnp.maximum(w - 1, 0))),
        (w >= 0, (1 - r, n, w)),
    ]


def each_rows(count, step, body):
    def run(i, carry):
        body(pl.ds(pl.multiple_of(i * step, step), step))
        return carry

    lax.fori_loop(0, count // step, run, 0)


def square_partners(r, n, w):
    return [(n >= 0, over_x(r, n, w)), (n >= 0, over_y(r, n, w))]


def over_x(r, n, w):
    return (r, n + 1 - 2 * (n % 2), w)


def over_y(r, n, w):
    return (r, (n + 2) % 4, w)


def push(source, target, s_s, s_g, device):
    return pltpu.make_async_remote_copy(
        source, target, s_s, s_g, device_id=device, device_id_type=MESH
    )


class Gather:
    def __init__(self, buf, sems, me, wid_count):
        self.buf, (self.up_s, self.dn_s, self.pt_s, self.got) = buf, sems
        self.r, self.n, self.w = me
        self.last = wid_count - 1
        self.up = (self.r, self.n, jnp.minimum(self.w + 1, self.last))
        self.dn = (self.r, self.n, jnp.maximum(self.w - 1, 0))
        self.pt = (1 - self.r, self.n, self.w)

    def copy(self, j, sem, device, row=None):
        row = self.r if row is None else row
        return pltpu.make_async_remote_copy(
            self.buf.at[row, j],
            self.buf.at[row, j],
            sem.at[j],
            self.got.at[row, j],
            device_id=device,
            device_id_type=MESH,
        )

    def pass_on(self, j, go_up, go_dn):
        if go_up:
            @pl.when(self.w < self.last)
            def _():
                self.copy(j, self.up_s, self.up).start()

        if go_dn:
            @pl.when(self.w > 0)
            def _():
                self.copy(j, self.dn_s, self.dn).start()

        self.copy(j, self.pt_s, self.pt).start()

    def own(self):
        self.pass_on(self.w, True, True)

    def arrive(self, row, j):
        self.copy(j, self.pt_s, self.pt, row).wait_recv()

    def step(self, k):
        below, above = self.w - k, self.w + k

        @pl.when(below >= 0)
        def _():
            self.arrive(self.r, below)
            self.pass_on(below, True, False)

        @pl.when(above <= self.last)
        def _():
            self.arrive(self.r, above)
            self.pass_on(above, False, True)

    def rest(self):
        for j in range(self.last + 1):
            self.arrive(1 - self.r, j)

    def sent(self):
        for j in range(self.last + 1):
            @pl.when((j <= self.w) & (self.w < self.last))
            def _():
                self.copy(j, self.up_s, self.up).wait_send()

            @pl.when((j >= self.w) & (self.w > 0))
            def _():
                self.copy(j, self.dn_s, self.dn).wait_send()

            self.copy(j, self.pt_s, self.pt).wait_send()


def gather_scratch(shard, width):
    return [pltpu.VMEM((2, 4, shard, width), bf16)] + gather_sems()


def gather_sems():
    return [pltpu.SemaphoreType.DMA((4,))] * 3 + [pltpu.SemaphoreType.DMA((2, 4))]


class Scatter:
    def __init__(self, mine, theirs, bufs, sems, me, wid_count):
        self.mine, self.theirs = mine, theirs
        self.from_pt, self.from_up, self.from_dn = bufs
        self.pt_s, self.pt_g, self.up_s, self.up_g, self.dn_s, self.dn_g = sems
        self.r, self.n, self.w = me
        self.last = wid_count - 1
        self.up = (self.r, self.n, jnp.minimum(self.w + 1, self.last))
        self.dn = (self.r, self.n, jnp.maximum(self.w - 1, 0))
        self.pt = (1 - self.r, self.n, self.w)

    def order(self, i):
        low, high = (3, 0, 2, 1)[i], (0, 3, 1, 2)[i]
        return jnp.where(self.w < 2, low, high)

    def pair(self, s):
        return pltpu.make_async_remote_copy(
            self.theirs.at[s], self.from_pt.at[s], self.pt_s.at[s], self.pt_g.at[s],
            device_id=self.pt, device_id_type=MESH,
        )

    def climb(self, s):
        return pltpu.make_async_remote_copy(
            self.mine.at[s], self.from_dn.at[s], self.up_s.at[s], self.up_g.at[s],
            device_id=self.up, device_id_type=MESH,
        )

    def fall(self, s):
        return pltpu.make_async_remote_copy(
            self.mine.at[s], self.from_up.at[s], self.dn_s.at[s], self.dn_g.at[s],
            device_id=self.dn, device_id_type=MESH,
        )

    def add(self, s, others):
        def body(rows):
            total = self.mine[s, rows, :].astype(f32)
            for other in others:
                total = total + other[s, rows, :].astype(f32)
            self.mine[s, rows, :] = total.astype(bf16)

        each_rows(self.mine.shape[1], 16, body)

    def step(self, s):
        self.pair(s).wait_recv()

        @pl.when((s > self.w) & (self.w > 0))
        def _():
            self.climb(s).wait_recv()
            self.add(s, (self.from_pt, self.from_dn))

        @pl.when((s < self.w) & (self.w < self.last))
        def _():
            self.fall(s).wait_recv()
            self.add(s, (self.from_pt, self.from_up))

        @pl.when(((s > self.w) & (self.w == 0)) | ((s < self.w) & (self.w == self.last)))
        def _():
            self.add(s, (self.from_pt,))

        @pl.when(s > self.w)
        def _():
            self.climb(s).start()

        @pl.when(s < self.w)
        def _():
            self.fall(s).start()

    def advance(self, edge_steps, inner_steps):
        for ends, steps in ((True, edge_steps), (False, inner_steps)):
            at_end = (self.w == 0) | (self.w == self.last)

            @pl.when(at_end if ends else jnp.logical_not(at_end))
            def _():
                for i in steps:
                    self.step(self.order(i))

    def total(self, out):
        w = self.w

        def first(rows):
            out[rows, :] = self.mine[w, rows, :].astype(f32) + self.from_pt[w, rows, :].astype(f32)

        each_rows(out.shape[0], 16, first)

        @pl.when(w > 0)
        def _():
            self.climb(w).wait_recv()

            def more(rows):
                out[rows, :] += self.from_dn[w, rows, :].astype(f32)

            each_rows(out.shape[0], 16, more)

        @pl.when(w < self.last)
        def _():
            self.fall(w).wait_recv()

            def more(rows):
                out[rows, :] += self.from_up[w, rows, :].astype(f32)

            each_rows(out.shape[0], 16, more)

    def sent(self):
        for s in range(self.last + 1):
            self.pair(s).wait_send()

            @pl.when(s > self.w)
            def _():
                self.climb(s).wait_send()

            @pl.when(s < self.w)
            def _():
                self.fall(s).wait_send()


def scatter_bufs(shard, width):
    return [pltpu.VMEM((4, shard, width), bf16)] * 3


def scatter_sems():
    return [pltpu.SemaphoreType.DMA((4,))] * 6


def vmem():
    return pl.BlockSpec(memory_space=pltpu.VMEM)


def hbm():
    return pl.BlockSpec(memory_space=pl.ANY)


def comm_call(kernel, name, cid, out_shape, in_specs, out_specs, scratch, args, flops=0, sent=0):
    return pl.pallas_call(
        kernel,
        out_shape=out_shape,
        in_specs=in_specs,
        out_specs=out_specs,
        scratch_shapes=scratch,
        compiler_params=pltpu.CompilerParams(
            collective_id=cid, has_side_effects=True, vmem_limit_bytes=VMEM_LIMIT
        ),
        cost_estimate=pl.CostEstimate(flops=flops, bytes_accessed=sent, transcendentals=0),
        name=name,
    )(*args)


def norm_rows(x, gain):
    root = lax.rsqrt(jnp.mean(x * x, axis=-1, keepdims=True) + norm_eps)
    return x * root * gain


def turn(x, cosine, sine):
    lane = lax.broadcasted_iota(jnp.int32, x.shape, 1)
    swapped = jnp.where(lane % 64 < 32, pltpu.roll(x, 96, 1), pltpu.roll(x, 32, 1))
    return x * cosine + swapped * sine


def enter_kernel(hidden, gain, tab, rows_out, tabs_out, buf, up_s, dn_s, pt_s, got, tabs, tab_s, tab_g, out_s):
    me = spot()
    r, n, w = me
    greet(line_partners(r, n, w, 4))
    gather = Gather(buf, (up_s, dn_s, pt_s, got), me, 4)
    tab_copy = pltpu.make_async_remote_copy(
        tab, tabs.at[r], tab_s, tab_g, device_id=(1 - r, n, w), device_id_type=MESH
    )

    def body(rows):
        buf[r, w, rows, :] = norm_rows(hidden[rows, :].astype(f32), gain[...]).astype(bf16)

    each_rows(hidden.shape[0], 16, body)
    gather.own()
    tab_copy.start()

    def keep(rows):
        tabs[r, rows, :] = tab[rows, :]

    each_rows(tab.shape[0], 16, keep)
    for k in (1, 2, 3):
        gather.step(k)
    gather.rest()
    out = pltpu.make_async_copy(buf, rows_out, out_s.at[0])
    out.start()
    tab_copy.wait_recv()
    out_tab = pltpu.make_async_copy(tabs, tabs_out, out_s.at[1])
    out_tab.start()
    gather.sent()
    tab_copy.wait_send()
    out.wait()
    out_tab.wait()


def enter(hidden, gain, tab):
    shard, width = hidden.shape
    return comm_call(
        enter_kernel, "enter", 1,
        (
            jax.ShapeDtypeStruct((2, 4, shard, width), bf16),
            jax.ShapeDtypeStruct((2,) + tab.shape, f32),
        ),
        [vmem()] * 3, [hbm()] * 2,
        gather_scratch(shard, width)
        + [
            pltpu.VMEM((2,) + tab.shape, f32),
            pltpu.SemaphoreType.DMA(()),
            pltpu.SemaphoreType.DMA(()),
            pltpu.SemaphoreType.DMA((2,)),
        ],
        (hidden, gain, tab), flops=10**10, sent=10**8,
    )


def nar_device(r, n, w, by):
    return (r, jnp.clip(n + by, 0, 3), w)


def project_kernel(x, p1, tabs, q_out, kv_out, kv, s_s, s_g, out_s):
    r, n, w = spot()
    greet(
        [
            (n >= 1, nar_device(r, n, w, -1)),
            (n >= 2, nar_device(r, n, w, -2)),
            (n <= 2, nar_device(r, n, w, 1)),
            (n <= 1, nar_device(r, n, w, 2)),
        ]
    )

    def copy(row, slot, by):
        return pltpu.make_async_remote_copy(
            kv.at[row, 2], kv.at[row, slot], s_s.at[row, slot], s_g.at[row, slot],
            device_id=nar_device(r, n, w, by), device_id_type=MESH,
        )

    lane = lax.broadcasted_iota(jnp.int32, (256, 128), 1)
    weight = p1[:, :, 0:384].reshape(2048, 384)
    for row in range(2):
        def tile(i, carry):
            rows = pl.ds(pl.multiple_of(i * 256, 256), 256)
            cosine, sine = tabs[row, rows, 0:128], tabs[row, rows, 128:256]
            pre = jnp.dot(x[row, rows, :], weight, preferred_element_type=f32)
            q_out[row, rows, 0:128] = turn(pre[:, 0:128], cosine, sine).astype(bf16)
            q_out[row, rows, 128:256] = turn(pre[:, 128:256], cosine, sine).astype(bf16)
            both = pre[:, 256:384]
            kv[row, 2, rows, :] = jnp.where(lane < 64, turn(both, cosine, sine), both).astype(bf16)
            return carry

        lax.fori_loop(0, 2, tile, 0)

        @pl.when(n <= 2)
        def _():
            copy(row, 1, 1).start()

        @pl.when(n <= 1)
        def _():
            copy(row, 0, 2).start()

        for slot, least in ((1, 1), (0, 2)):
            @pl.when(n < least)
            def _():
                kv[row, slot] = jnp.zeros((512, 128), bf16)

    for row in range(2):
        for slot, least, by in ((1, 1, 1), (0, 2, 2)):
            @pl.when(n >= least)
            def _():
                copy(row, slot, by).wait_recv()

    out = pltpu.make_async_copy(kv, kv_out, out_s)
    out.start()
    for row in range(2):
        @pl.when(n <= 2)
        def _():
            copy(row, 1, 1).wait_send()

        @pl.when(n <= 1)
        def _():
            copy(row, 0, 2).wait_send()

    out.wait()


def project(x, p1, tabs):
    return comm_call(
        project_kernel, "project", 2,
        (
            jax.ShapeDtypeStruct((2, 512, 256), bf16),
            jax.ShapeDtypeStruct((2, 3, 512, 128), bf16),
        ),
        [vmem()] * 3, [vmem(), hbm()],
        [
            pltpu.VMEM((2, 3, 512, 128), bf16),
            pltpu.SemaphoreType.DMA((2, 3)),
            pltpu.SemaphoreType.DMA((2, 3)),
            pltpu.SemaphoreType.DMA(()),
        ],
        (x, p1, tabs), flops=10**10, sent=10**7,
    )


KEYS = 256
QUERIES = 128


def stack_low(x):
    lane = lax.broadcasted_iota(jnp.int32, (QUERIES, 128), 1)
    zero = jnp.zeros((QUERIES, 128), x.dtype)
    parts = []
    for pair in range(2):
        block = x[:, pair * 128 : pair * 128 + 128]
        parts.append(jnp.where(lane < 64, block, zero))
        parts.append(jnp.where(lane < 64, pltpu.roll(block, 64, 1), zero))
    return jnp.concatenate(parts, axis=0)


def stack_high(x):
    lane = lax.broadcasted_iota(jnp.int32, (QUERIES, 128), 1)
    zero = jnp.zeros((QUERIES, 128), x.dtype)
    parts = []
    for pair in range(2):
        block = x[:, pair * 128 : pair * 128 + 128]
        parts.append(jnp.where(lane >= 64, pltpu.roll(block, 64, 1), zero))
        parts.append(jnp.where(lane >= 64, block, zero))
    return jnp.concatenate(parts, axis=0)


def unstack(x, low):
    lane = lax.broadcasted_iota(jnp.int32, (QUERIES, 128), 1)
    out = []
    for pair in range(2):
        even = x[2 * pair * QUERIES : (2 * pair + 1) * QUERIES]
        odd = x[(2 * pair + 1) * QUERIES : (2 * pair + 2) * QUERIES]
        if low:
            out.append(jnp.where(lane < 64, even, pltpu.roll(odd, 64, 1)))
        else:
            out.append(jnp.where(lane < 64, pltpu.roll(even, 64, 1), odd))
    return jnp.concatenate(out, axis=1)


def allowed_tile(starts, tile, first_query):
    key = lax.broadcasted_iota(jnp.int32, (QUERIES, KEYS), 1) + tile * KEYS
    query = lax.broadcasted_iota(jnp.int32, (QUERIES, KEYS), 0) + first_query
    start = jnp.concatenate([starts] * (KEYS // 128), axis=1)
    ok = (key <= query) & (key.astype(f32) >= start)
    return jnp.concatenate([ok] * 4, axis=0)


def key_tiles(low, row, block):
    first_query = 1024 + block * QUERIES
    return low[row * 4 + block] // KEYS, first_query // KEYS + 1, first_query


def attend_kernel(low, q, kv, starts, out, lse):
    row, block = pl.program_id(0), pl.program_id(1)
    first, end, first_query = key_tiles(low, row, block)
    query = stack_low(q[0].astype(f32)).astype(bf16)

    def body(tile, carry):
        top, total, acc = carry
        both = kv[0, pl.ds(pl.multiple_of(tile * KEYS, KEYS), KEYS), :]
        scores = contract_last(query, both) * 0.125
        ok = allowed_tile(starts[0], tile, first_query)
        scores = jnp.where(ok, scores, masked_score)
        new_top = jnp.maximum(top, jnp.max(scores, axis=1, keepdims=True))
        shrink = jnp.exp(top - new_top)
        part = jnp.exp(scores - new_top)
        total = total * shrink + jnp.sum(part, axis=1, keepdims=True)
        acc = acc * shrink + jnp.dot(part.astype(bf16), both, preferred_element_type=f32)
        return new_top, total, acc

    top, total, acc = lax.fori_loop(
        first, end, body,
        (
            jnp.full((4 * QUERIES, 1), masked_score, f32),
            jnp.zeros((4 * QUERIES, 1), f32),
            jnp.zeros((4 * QUERIES, 128), f32),
        ),
    )
    out[0] = unstack(acc / total, False).astype(bf16)
    lse[0, 0] = jnp.broadcast_to(top + jnp.log(total), (4 * QUERIES, 128))


def attend_specs():
    return [
        pl.BlockSpec((1, QUERIES, 256), lambda i, j, low: (i, j, 0)),
        pl.BlockSpec((1, 1536, 128), lambda i, j, low: (i, 0, 0)),
        pl.BlockSpec((1, QUERIES, 128), lambda i, j, low: (i, j, 2)),
    ]


def attend(low, q, kv, tabs):
    return pl.pallas_call(
        attend_kernel,
        out_shape=(
            jax.ShapeDtypeStruct((2, 512, 256), bf16),
            jax.ShapeDtypeStruct((2, 4, 4 * QUERIES, 128), f32),
        ),
        grid_spec=pltpu.PrefetchScalarGridSpec(
            num_scalar_prefetch=1, grid=(2, 4),
            in_specs=attend_specs(),
            out_specs=[
                pl.BlockSpec((1, QUERIES, 256), lambda i, j, low: (i, j, 0)),
                pl.BlockSpec((1, 1, 4 * QUERIES, 128), lambda i, j, low: (i, j, 0, 0)),
            ],
        ),
        compiler_params=pltpu.CompilerParams(vmem_limit_bytes=VMEM_LIMIT),
        cost_estimate=pl.CostEstimate(flops=2 * 10**10, bytes_accessed=10**7, transcendentals=10**7),
        name="attend",
    )(low, q, kv, tabs)


def attend_back_kernel(low, q, kv, starts, turns, att, grad, lse, dq_out, dkv_out, dkv):
    row, block = pl.program_id(0), pl.program_id(1)
    first, end, first_query = key_tiles(low, row, block)

    @pl.when(block == 0)
    def _():
        dkv[...] = jnp.zeros_like(dkv)

    query = stack_low(q[0].astype(f32)).astype(bf16)
    grads = stack_high(grad[0].astype(f32))
    inner = jnp.sum(grads * stack_high(att[0].astype(f32)), axis=1, keepdims=True)
    grads = grads.astype(bf16)
    logsum = jnp.concatenate([lse[0, 0]] * (KEYS // 128), axis=1)

    def body(tile, dq):
        rows = pl.ds(pl.multiple_of(tile * KEYS, KEYS), KEYS)
        both = kv[0, rows, :]
        ok = allowed_tile(starts[0], tile, first_query)
        scores = contract_last(query, both) * 0.125
        prob = jnp.where(ok, jnp.exp(scores - logsum), 0.0)
        grad_prob = contract_last(grads, both)
        grad_scores = (prob * (grad_prob - inner)).astype(bf16)
        dkv[rows, :] += contract_first(grad_scores, query) * 0.125 + contract_first(
            prob.astype(bf16), grads
        )
        return dq + jnp.dot(grad_scores, both, preferred_element_type=f32)

    dq = lax.fori_loop(first, end, body, jnp.zeros((4 * QUERIES, 128), f32))
    flat = unstack(dq, True) * 0.125
    cosine, sine = turns[0, :, 0:128], -turns[0, :, 128:256]
    dq_out[0, :, 0:128] = turn(flat[:, 0:128], cosine, sine).astype(bf16)
    dq_out[0, :, 128:256] = turn(flat[:, 128:256], cosine, sine).astype(bf16)

    @pl.when(block == 3)
    def _():
        dkv_out[0] = dkv[...]


def attend_back(low, q, kv, tabs, att, grad, lse):
    tile = pl.BlockSpec((1, QUERIES, 256), lambda i, j, low: (i, j, 0))
    return pl.pallas_call(
        attend_back_kernel,
        out_shape=(
            jax.ShapeDtypeStruct((2, 512, 256), bf16),
            jax.ShapeDtypeStruct((2, 1536, 128), f32),
        ),
        grid_spec=pltpu.PrefetchScalarGridSpec(
            num_scalar_prefetch=1, grid=(2, 4),
            in_specs=attend_specs()
            + [tile, tile, tile, pl.BlockSpec((1, 1, 4 * QUERIES, 128), lambda i, j, low: (i, j, 0, 0))],
            out_specs=[tile, pl.BlockSpec((1, 1536, 128), lambda i, j, low: (i, 0, 0))],
            scratch_shapes=[pltpu.VMEM((1536, 128), f32)],
        ),
        compiler_params=pltpu.CompilerParams(vmem_limit_bytes=VMEM_LIMIT),
        cost_estimate=pl.CostEstimate(flops=4 * 10**10, bytes_accessed=10**7, transcendentals=10**7),
        name="attend_back",
    )(low, q, kv, tabs, tabs, att, grad, lse)


def out_block(p1, nn, half):
    return p1[nn, half * 256 : half * 256 + 256, 384:640]


def middle_kernel(
    att, p1, hidden, gain, grad_top, mid_out, ffn_out, grad_out,
    theirs, mine, from_pt, from_up, from_dn, s0, s1, s2, s3, s4, s5,
    gbuf, g0, g1, g2, g3, fbuf, h0, h1, h2, h3, out_s,
):
    me = spot()
    r, n, w = me
    greet(line_partners(r, n, w, 4))
    scatter = Scatter(
        mine, theirs, (from_pt, from_up, from_dn), (s0, s1, s2, s3, s4, s5), me, 4
    )
    tops = Gather(gbuf, (g0, g1, g2, g3), me, 4)
    ffn = Gather(fbuf, (h0, h1, h2, h3), me, 4)

    def keep(rows):
        gbuf[r, w, rows, :] = grad_top[rows, :]

    each_rows(grad_top.shape[0], 16, keep)
    for i in range(4):
        s = scatter.order(i)
        rows = pl.ds(pl.multiple_of(s * 128, 128), 128)
        left = jnp.concatenate([att[1 - r, rows, :], att[r, rows, :]], axis=0)
        for nn in range(4):
            for half in range(2):
                part = jnp.dot(left, out_block(p1, nn, half), preferred_element_type=f32).astype(bf16)
                columns = slice(nn * 512 + half * 256, nn * 512 + half * 256 + 256)
                theirs[s, :, columns] = part[0:128]
                mine[s, :, columns] = part[128:256]
        scatter.pair(s).start()
    for i in range(4):
        scatter.step(scatter.order(i))
        if i == 0:
            tops.own()
        else:
            tops.step(i)
    scatter.total(mid_out)

    def body(rows):
        middle = mid_out[rows, :] + hidden[rows, :].astype(f32)
        mid_out[rows, :] = middle
        fbuf[r, w, rows, :] = norm_rows(middle, gain[...]).astype(bf16)

    each_rows(hidden.shape[0], 16, body)
    ffn.own()
    tops.rest()
    out_g = pltpu.make_async_copy(gbuf, grad_out, out_s.at[0])
    out_g.start()
    for k in (1, 2, 3):
        ffn.step(k)
    ffn.rest()
    out_f = pltpu.make_async_copy(fbuf, ffn_out, out_s.at[1])
    out_f.start()
    scatter.sent()
    tops.sent()
    ffn.sent()
    out_g.wait()
    out_f.wait()


def middle_stage(att, p1, hidden, gain, grad_top):
    shard, width = hidden.shape
    rows = jax.ShapeDtypeStruct((2, 4, shard, width), bf16)
    return comm_call(
        middle_kernel, "middle", 3,
        (jax.ShapeDtypeStruct((shard, width), f32), rows, rows),
        [vmem()] * 5, [vmem(), hbm(), hbm()],
        [pltpu.VMEM((4, shard, width), bf16)] * 2
        + scatter_bufs(shard, width) + scatter_sems()
        + gather_scratch(shard, width) + gather_scratch(shard, width)
        + [pltpu.SemaphoreType.DMA((2,))],
        (att, p1, hidden, gain, grad_top), flops=10**10, sent=2 * 10**8,
    )


class Spread:
    def __init__(self, outs, sems, me):
        self.a_send, self.a_keep, self.b_send, self.b_keep = outs
        self.r, self.n, self.w = me
        self.give_s, self.give_g, self.keep_s = sems

    def copies(self, wide, row, place, give):
        for k in range(4):
            block = wide.at[self.n ^ k]
            for part in range(2):
                source = block.at[pl.ds(part * 128, 128)]
                if part == 0:
                    target = (self.a_send if k & 1 else self.a_keep).at[k >> 1]
                else:
                    target = (self.b_send if k >= 2 else self.b_keep).at[k & 1]
                target = place(target)
                at = k * 2 + part
                if give:
                    yield pltpu.make_async_remote_copy(
                        source, target, self.give_s.at[row, at], self.give_g.at[row, at],
                        device_id=(1 - self.r, self.n, self.w), device_id_type=MESH,
                    )
                else:
                    yield pltpu.make_async_copy(source, target, self.keep_s.at[row, at])

    def start(self, *args):
        for copy in self.copies(*args):
            copy.start()

    def wait_send(self, *args):
        for copy in self.copies(*args):
            copy.wait_send()

    def wait_recv(self, *args):
        for copy in self.copies(*args):
            copy.wait_recv()

    def wait(self, *args):
        for copy in self.copies(*args):
            copy.wait()


def spread_sems(count):
    return [pltpu.SemaphoreType.DMA((count, 8))] * 3


def ffn_kernel(
    x, tops, p2_all, gain, part_out, sum_out, gain_out, o0, o1, o2, o3, ra_out, rb_out,
    theirs, mine, from_pt, from_up, from_dn, s0, s1, s2, s3, s4, s5,
    act, dgu, stage, wide, out_s, give_s, give_g, keep_s, p2, in_s, n_s, n_g,
):
    me = spot()
    r, n, w = me
    loads = [pltpu.make_async_copy(p2_all.at[:, j], p2.at[j], in_s.at[j]) for j in range(3)]
    for load in loads:
        load.start()
    greet(line_partners(r, n, w, 4) + square_partners(r, n, w))
    scatter = Scatter(
        mine, theirs, (from_pt, from_up, from_dn), (s0, s1, s2, s3, s4, s5), me, 4
    )
    gain_out[...] = jnp.zeros_like(gain_out)
    for load in loads:
        load.wait()

    def put(s, slot, row_slot, row):
        return pltpu.make_async_copy(
            stage.at[slot, row_slot], part_out.at[row, s], out_s.at[slot, row_slot]
        )

    def hidden_tile(i, carry):
        ft, row = i // 2, i % 2
        rows = pl.ds(pl.multiple_of(row * 512, 512), 512)
        columns = pl.ds(pl.multiple_of(ft * 256, 256), 256)
        left = x[rows, :]
        gate = jnp.dot(left, p2[0, :, :, columns].reshape(2048, 256), preferred_element_type=f32)
        up = jnp.dot(left, p2[1, :, :, columns].reshape(2048, 256), preferred_element_type=f32)
        f_rows = pl.ds(pl.multiple_of((ft % 2) * 256, 256), 256)
        f_cols = pl.ds(pl.multiple_of((ft // 2) * 512, 512), 512)
        right = jnp.concatenate([p2[2, nn, f_rows, f_cols] for nn in range(4)], axis=1)
        dact = contract_last(tops[rows, :], right)
        sig = 1.0 / (1.0 + jnp.exp(-gate))
        silu = gate * sig
        act[rows, columns] = (silu * up).astype(bf16)
        dgu[rows, columns] = (dact * up * (sig * (1.0 + gate * (1.0 - sig)))).astype(bf16)
        later = pl.ds(pl.multiple_of(1024 + ft * 256, 256), 256)
        dgu[rows, later] = (dact * silu).astype(bf16)
        return carry

    lax.fori_loop(0, 8, hidden_tile, 0)

    spread = Spread((o0, o1, o2, o3), (give_s, give_g, keep_s), me)
    columns_here = pl.ds(pl.multiple_of(r * 1024, 1024), 1024)
    slots = {2: 0, 0: 1, 1: 0}

    def moved(which, half):
        def place(target):
            return target.at[which, :, columns_here]

        return wide.at[slots[which], half], which, place, half == 0

    def weights(which):
        for half in range(2):
            d_first = (jnp.where(half == 0, 1 - r, r)) * 1024

            def weight_tile(i, carry):
                d_rows = pl.ds(pl.multiple_of(d_first + i * 256, 256), 256)
                source = x if which < 2 else tops
                left = source[:, d_rows]
                if which < 2:
                    right = dgu[:, which * 1024 : which * 1024 + 1024]
                else:
                    right = act[...]
                wide[slots[which], half, i] = contract_first(left, right).astype(bf16)
                return carry

            lax.fori_loop(0, 4, weight_tile, 0)
            spread.start(*moved(which, half))

    hops = [
        push(o0.at[:, 2], ra_out, n_s.at[0], n_g.at[0], over_x(r, n, w)),
        push(o2.at[:, 2], rb_out, n_s.at[1], n_g.at[1], over_y(r, n, w)),
    ]
    weights(2)
    for i in range(4):
        s = scatter.order(i)
        slot = i % 2
        rows_t = pl.ds(pl.multiple_of((1 - r) * 512 + s * 128, 128), 128)
        rows_m = pl.ds(pl.multiple_of(r * 512 + s * 128, 128), 128)
        if i >= 2:
            put(s, slot, 0, 1 - r).wait()
            put(s, slot, 1, r).wait()

        def model_tile(dt, carry):
            nn, half = dt // 2, dt % 2
            columns = pl.ds(pl.multiple_of(dt * 256, 256), 256)
            inner = pl.ds(pl.multiple_of(half * 256, 256), 256)
            other = pl.ds(pl.multiple_of(512 + half * 256, 256), 256)
            left = jnp.concatenate([dgu[rows_t, :], dgu[rows_m, :]], axis=0)
            right = jnp.concatenate([p2[0, nn, inner, :], p2[1, nn, inner, :]], axis=1)
            part = contract_last(left, right)
            seen = jnp.concatenate([x[rows_t, columns], x[rows_m, columns]], axis=0)
            terms = part * seen.astype(f32)
            gain_out[:, columns] += jnp.sum(terms.reshape(32, 8, 256), axis=0)
            part = part.astype(bf16)
            theirs[s, :, columns] = part[0:128]
            mine[s, :, columns] = part[128:256]
            left = jnp.concatenate([act[rows_t, :], act[rows_m, :]], axis=0)
            right = jnp.concatenate([p2[2, nn, :, inner], p2[2, nn, :, other]], axis=0)
            part = jnp.dot(left, right, preferred_element_type=f32).astype(bf16)
            stage[slot, 0, :, columns] = part[0:128]
            stage[slot, 1, :, columns] = part[128:256]
            return carry

        lax.fori_loop(0, 8, model_tile, 0)
        scatter.pair(s).start()
        put(s, slot, 0, 1 - r).start()
        put(s, slot, 1, r).start()
        if i == 0:
            spread.wait_recv(*moved(2, 0))
            spread.wait(*moved(2, 1))
            for hop in hops:
                hop.start()
        else:
            scatter.advance((i - 1,), (i - 2,) if i > 1 else ())

    def scale(rows):
        gain_out[rows, :] = gain_out[rows, :] / gain[...]

    each_rows(8, 8, scale)
    scatter.advance((3,), ())
    weights(0)
    scatter.advance((), (2,))
    spread.wait_send(*moved(2, 0))
    weights(1)
    scatter.advance((), (3,))
    scatter.total(sum_out)
    scatter.sent()
    for which in (0, 1):
        spread.wait_recv(*moved(which, 0))
        spread.wait_send(*moved(which, 0))
        spread.wait(*moved(which, 1))
    for slot in range(2):
        put(0, slot, 0, 1 - r).wait()
        put(0, slot, 1, r).wait()
    for hop in hops:
        hop.wait()


def spread_shapes(*dims):
    return (jax.ShapeDtypeStruct((2,) + dims, bf16),) * 4


def ffn_stage(x, tops, p2, gain):
    shard, width = 128, 2048
    return comm_call(
        ffn_kernel, "ffn", 4,
        (
            jax.ShapeDtypeStruct((2, 4, shard, width), bf16),
            jax.ShapeDtypeStruct((shard, width), f32),
            jax.ShapeDtypeStruct((8, width), f32),
        )
        + spread_shapes(3, 128, width)
        + (jax.ShapeDtypeStruct((2, 128, width), bf16),) * 2,
        [vmem()] * 2 + [hbm()] + [vmem()], [hbm(), vmem(), vmem()] + [hbm()] * 6,
        [pltpu.VMEM((4, shard, width), bf16)] * 2
        + scatter_bufs(shard, width) + scatter_sems()
        + [
            pltpu.VMEM((1024, 1024), bf16),
            pltpu.VMEM((1024, 2048), bf16),
            pltpu.VMEM((2, 2, shard, width), bf16),
            pltpu.VMEM((2, 2, 4, 256, 1024), bf16),
            pltpu.SemaphoreType.DMA((2, 2)),
        ]
        + spread_sems(3)
        + [pltpu.VMEM((3, 4, 512, 1024), bf16), pltpu.SemaphoreType.DMA((3,))]
        + [pltpu.SemaphoreType.DMA((2,))] * 2,
        (x, tops, p2, gain), flops=4 * 10**10, sent=10**8,
    )


def norm_back(values, gain, grad):
    root = lax.rsqrt(jnp.mean(values * values, axis=-1, keepdims=True) + norm_eps)
    weighted = grad * gain
    inner = jnp.mean(weighted * values, axis=-1, keepdims=True)
    return root * weighted - values * (root * root * root) * inner


def branch_kernel(
    total, mid, grad_top, gain, p1, att, a_in, b_in, gmid_out, datt_out, o0, o1, o2, o3, ra_out, rb_out,
    buf, g0, g1, g2, g3, wide, give_s, give_g, keep_s, n_s, n_g,
):
    me = spot()
    r, n, w = me
    greet(line_partners(r, n, w, 4) + square_partners(r, n, w))
    gather = Gather(buf, (g0, g1, g2, g3), me, 4)
    hops = [
        push(a_in.at[:, 0:2], ra_out, n_s.at[0], n_g.at[0], over_x(r, n, w)),
        push(b_in.at[:, 0:2], rb_out, n_s.at[1], n_g.at[1], over_y(r, n, w)),
    ]
    for hop in hops:
        hop.start()

    def body(rows):
        grad = norm_back(mid[rows, :], gain[...], total[rows, :]) + grad_top[rows, :].astype(f32)
        gmid_out[rows, :] = grad
        buf[r, w, rows, :] = grad.astype(bf16)

    each_rows(mid.shape[0], 16, body)
    gather.own()
    for k in (1, 2, 3):
        gather.step(k)
    gather.rest()
    for row in range(2):
        for pair in range(2):
            left = jnp.concatenate([buf[row, 2 * pair], buf[row, 2 * pair + 1]], axis=0)
            right = jnp.concatenate(
                [out_block(p1, nn, half) for nn in range(4) for half in range(2)], axis=1
            )
            datt_out[row, pair * 256 : pair * 256 + 256, :] = contract_last(left, right).astype(bf16)

    spread = Spread((o0, o1, o2, o3), (give_s, give_g, keep_s), me)

    def moved(half):
        def place(target):
            return target.at[:, pl.ds(pl.multiple_of(r * 256, 256), 256)]

        return wide.at[half], 0, place, half == 0

    for half in range(2):
        d_first = (jnp.where(half == 0, 1 - r, r)) * 1024

        def weight_tile(i, carry):
            columns = pl.ds(pl.multiple_of(d_first + i * 256, 256), 256)
            left = buf[:, :, :, columns].reshape(1024, 256)
            wide[half, i] = contract_first(left, att[...]).astype(bf16)
            return carry

        lax.fori_loop(0, 4, weight_tile, 0)
        spread.start(*moved(half))
    gather.sent()
    spread.wait(*moved(0))
    spread.wait(*moved(1))
    for hop in hops:
        hop.wait()


def branch_stage(total, mid, grad_top, gain, p1, att, a_in, b_in):
    shard, width = mid.shape
    return comm_call(
        branch_kernel, "branch", 5,
        (
            jax.ShapeDtypeStruct((shard, width), f32),
            jax.ShapeDtypeStruct((2, 512, 256), bf16),
        )
        + spread_shapes(128, 512)
        + (jax.ShapeDtypeStruct((2, 2, 128, width), bf16),) * 2,
        [vmem()] * 6 + [hbm()] * 2, [vmem(), vmem()] + [hbm()] * 6,
        gather_scratch(shard, width)
        + [pltpu.VMEM((2, 4, 256, 256), bf16)]
        + spread_sems(1)
        + [pltpu.SemaphoreType.DMA((2,))] * 2,
        (total, mid, grad_top, gain, p1, att, a_in, b_in), flops=10**10, sent=10**8,
    )


def unproject_kernel(
    dq, dkv, x, p1, tabs, gain, parts, mid, a_keep, b_keep, ra_gu, rb_gu, ra_d, rb_d, oa_in, ob_in,
    part_out, gain_out, o0, o1, o2, o3, hid_out, ra_out, rb_out, roa_out, rob_out,
    send, recv, both, wide_q, wide_kv, s_s, s_g, give_s, give_g, keep_s,
    mine, from_pt, from_up, from_dn, s0, s1, s2, s3, s4, s5,
    kept, came, acc, in_s, n_s, n_g, m_s,
):
    me = spot()
    r, n, w = me
    loads = []
    for j, (keep, gate_up, down) in enumerate(((a_keep, ra_gu, ra_d), (b_keep, rb_gu, rb_d))):
        loads += [
            pltpu.make_async_copy(keep.at[1], kept.at[j], in_s.at[j, 0]),
            pltpu.make_async_copy(gate_up.at[1], came.at[j, 0:2], in_s.at[j, 1]),
            pltpu.make_async_copy(down.at[1], came.at[j, 2], in_s.at[j, 2]),
        ]
    loads.append(pltpu.make_async_copy(parts.at[r], mine, m_s))
    for load in loads:
        load.start()
    greet(
        line_partners(r, n, w, 4)
        + [
            (n >= 1, nar_device(r, n, w, -1)),
            (n >= 2, nar_device(r, n, w, -2)),
            (n <= 2, nar_device(r, n, w, 1)),
            (n <= 1, nar_device(r, n, w, 2)),
        ]
        + square_partners(r, n, w)
    )
    scatter = Scatter(
        mine, parts.at[1 - r], (from_pt, from_up, from_dn), (s0, s1, s2, s3, s4, s5), me, 4
    )
    hops = [
        push(kept.at[0], ra_out, n_s.at[0], n_g.at[0], over_y(r, n, w)),
        push(kept.at[1], rb_out, n_s.at[1], n_g.at[1], over_x(r, n, w)),
        push(oa_in, roa_out, n_s.at[2], n_g.at[2], over_x(r, n, w)),
        push(ob_in, rob_out, n_s.at[3], n_g.at[3], over_y(r, n, w)),
    ]

    def copy(row, slot, by):
        return pltpu.make_async_remote_copy(
            send.at[row, slot], recv.at[row, slot], s_s.at[row, slot], s_g.at[row, slot],
            device_id=nar_device(r, n, w, by), device_id_type=MESH,
        )

    for row in range(2):
        for slot, by in ((1, -1), (0, -2)):
            @pl.when(n >= -by)
            def _():
                send[row, slot] = dkv[row, slot].astype(bf16)
                copy(row, slot, by).start()

    for i in range(4):
        scatter.pair(scatter.order(i)).start()
    for load in loads:
        load.wait()
    for j in range(2):
        for which in range(3):
            def join(rows):
                total = kept[j, which, rows, :].astype(f32) + came[j, which, rows, :].astype(f32)
                kept[j, which, rows, :] = total.astype(bf16)

            each_rows(128, 16, join)
        hops[j].start()
    hops[2].start()
    hops[3].start()
    scatter.advance((0, 1, 2, 3), ())

    spread = Spread((o0, o1, o2, o3), (give_s, give_g, keep_s), (r, n, w))

    def moved_q(half):
        def place(target):
            return target.at[:, pl.ds(pl.multiple_of(r * 256, 256), 256)]

        return wide_q.at[half], 0, place, half == 0

    def moved_kv(half):
        def place(target):
            return target.at[:, pl.ds(pl.multiple_of(512 + r * 128, 128), 128)]

        return wide_kv.at[half], 1, place, half == 0

    for row in range(2):
        both[row * 512 : row * 512 + 512, 0:256] = dq[row]

    def weight(half, columns, wide):
        d_first = (jnp.where(half == 0, 1 - r, r)) * 1024

        def tile(i, carry):
            d_cols = pl.ds(pl.multiple_of(d_first + i * 256, 256), 256)
            wide[half, i] = contract_first(x[:, d_cols], both[:, columns]).astype(bf16)
            return carry

        lax.fori_loop(0, 4, tile, 0)

    for half in range(2):
        weight(half, slice(0, 256), wide_q)
        spread.start(*moved_q(half))
    scatter.advance((), (0,))
    lane = lax.broadcasted_iota(jnp.int32, (128, 128), 1)
    for row in range(2):
        for slot, by in ((1, -1), (0, -2)):
            @pl.when(n <= 3 + by)
            def _():
                copy(row, slot, by).wait_recv()

        def tile(i, carry):
            rows = pl.ds(pl.multiple_of(i * 128, 128), 128)
            total = dkv[row, 2, rows, :]
            zero = jnp.zeros_like(total)
            total = total + jnp.where(n <= 2, recv[row, 1, rows, :].astype(f32), zero)
            total = total + jnp.where(n <= 1, recv[row, 0, rows, :].astype(f32), zero)
            turned = turn(total, tabs[row, rows, 0:128], -tabs[row, rows, 128:256])
            both[pl.ds(pl.multiple_of(row * 512 + i * 128, 128), 128), 256:384] = jnp.where(
                lane < 64, turned, total
            ).astype(bf16)
            return carry

        lax.fori_loop(0, 4, tile, 0)
    for half in range(2):
        weight(half, slice(256, 384), wide_kv)
        spread.start(*moved_kv(half))
    scatter.advance((), (1,))
    gain_out[...] = jnp.zeros_like(gain_out)

    def model_tile(dt, carry):
        nn, half = dt // 2, dt % 2
        columns = pl.ds(pl.multiple_of(dt * 256, 256), 256)
        inner = pl.ds(pl.multiple_of(half * 256, 256), 256)
        right = p1[nn, inner, 0:384]
        for row in range(2):
            for block in range(2):
                first = row * 512 + block * 256
                part = contract_last(both[first : first + 256, :], right)
                terms = part * x[first : first + 256, columns].astype(f32)
                gain_out[:, columns] += jnp.sum(terms.reshape(32, 8, 256), axis=0)
                part_out[row, 2 * block, :, columns] = part[0:128].astype(bf16)
                part_out[row, 2 * block + 1, :, columns] = part[128:256].astype(bf16)
        return carry

    lax.fori_loop(0, 8, model_tile, 0)
    gain_out[...] = gain_out[...] / gain[...]
    scatter.advance((), (2, 3))
    scatter.total(acc)

    def last(rows):
        hid_out[rows, :] = (acc[rows, :] + mid[rows, :]).astype(bf16)

    each_rows(128, 16, last)
    scatter.sent()
    for row in range(2):
        for slot, by in ((1, -1), (0, -2)):
            @pl.when(n >= -by)
            def _():
                copy(row, slot, by).wait_send()

    for half in range(2):
        spread.wait(*moved_q(half))
        spread.wait(*moved_kv(half))
    for hop in hops:
        hop.wait()


def unproject(*args):
    return comm_call(
        unproject_kernel, "unproject", 6,
        (
            jax.ShapeDtypeStruct((2, 4, 128, 2048), bf16),
            jax.ShapeDtypeStruct((8, 2048), f32),
        )
        + spread_shapes(128, 768)
        + (jax.ShapeDtypeStruct((128, 2048), bf16),)
        + (jax.ShapeDtypeStruct((3, 128, 2048), bf16),) * 2
        + (jax.ShapeDtypeStruct((2, 128, 512), bf16),) * 2,
        [vmem()] * 6 + [hbm(), vmem()] + [hbm()] * 8,
        [vmem(), vmem()] + [hbm()] * 4 + [vmem()] + [hbm()] * 4,
        [
            pltpu.VMEM((2, 2, 512, 128), bf16),
            pltpu.VMEM((2, 2, 512, 128), bf16),
            pltpu.VMEM((1024, 384), bf16),
            pltpu.VMEM((2, 4, 256, 256), bf16),
            pltpu.VMEM((2, 4, 256, 128), bf16),
            pltpu.SemaphoreType.DMA((2, 2)),
            pltpu.SemaphoreType.DMA((2, 2)),
        ]
        + spread_sems(2)
        + [pltpu.VMEM((4, 128, 2048), bf16)]
        + scatter_bufs(128, 2048) + scatter_sems()
        + [
            pltpu.VMEM((2, 3, 128, 2048), bf16),
            pltpu.VMEM((2, 3, 128, 2048), bf16),
            pltpu.VMEM((128, 2048), f32),
            pltpu.SemaphoreType.DMA((2, 3)),
            pltpu.SemaphoreType.DMA((4,)),
            pltpu.SemaphoreType.DMA((4,)),
            pltpu.SemaphoreType.DMA(()),
        ],
        args, flops=10**10, sent=10**7,
    )


def leave_kernel(
    parts, hidden, gain, gmid, gains, qa_send, qa_keep, qb_send, qb_keep, oa_keep, ob_keep, oa_in, ob_in,
    grad_out, ga_out, query_out, key_out, value_out, output_out,
    mine, from_pt, from_up, from_dn, s0, s1, s2, s3, s4, s5,
    acc, over_wid, summed, over_rest, w_s, w_g, t_s, t_g,
    first_q, next_q, then_q, next_o, then_o, kv, n_s, n_g, k_s, k_g,
):
    me = spot()
    r, n, w = me
    partners = [(w != j, (r, n, jnp.int32(j))) for j in range(4)]
    partners += [
        ((r != a) | (n != b), (jnp.int32(a), jnp.int32(b), w)) for a in range(2) for b in range(4)
    ]
    greet(partners)
    x_side, y_side = over_x(r, n, w), over_y(r, n, w)
    q_hops = [
        push(qa_send, first_q.at[0], n_s.at[0], n_g.at[0], x_side),
        push(qb_send, first_q.at[1], n_s.at[1], n_g.at[1], y_side),
    ]
    q_later = [
        push(next_q.at[0], then_q.at[0], n_s.at[2], n_g.at[2], y_side),
        push(next_q.at[1], then_q.at[1], n_s.at[3], n_g.at[3], x_side),
    ]
    o_hops = [
        push(next_o.at[0], then_o.at[0], n_s.at[4], n_g.at[4], y_side),
        push(next_o.at[1], then_o.at[1], n_s.at[5], n_g.at[5], x_side),
    ]
    for hop in q_hops:
        hop.start()
    scatter = Scatter(
        mine, parts.at[1 - r], (from_pt, from_up, from_dn), (s0, s1, s2, s3, s4, s5), me, 4
    )
    for i in range(4):
        scatter.pair(scatter.order(i)).start()

    def wid_copy(j, slot):
        return pltpu.make_async_remote_copy(
            gains, over_wid.at[slot], w_s.at[j], w_g.at[slot],
            device_id=(r, n, jnp.int32(j)), device_id_type=MESH,
        )

    def rest_copy(a, b, slot):
        return pltpu.make_async_remote_copy(
            summed, over_rest.at[slot], t_s.at[a * 4 + b], t_g.at[slot],
            device_id=(jnp.int32(a), jnp.int32(b), w), device_id_type=MESH,
        )

    for j in range(4):
        @pl.when(w != j)
        def _():
            wid_copy(j, w).start()

    for s in range(4):
        def fill(rows):
            mine[s, rows, :] = parts[r, s, rows, :]

        each_rows(128, 16, fill)
    scatter.advance((0, 1, 2, 3), ())
    for j, (keep, came) in enumerate(((oa_keep, oa_in), (ob_keep, ob_in))):
        next_o[j] = (keep[1].astype(f32) + came[1].astype(f32)).astype(bf16)
        o_hops[j].start()
    summed[...] = gains[...]
    for j in range(4):
        @pl.when(w != j)
        def _():
            wid_copy(j, j).wait_recv()
            summed[...] += over_wid[j]

    for a in range(2):
        for b in range(4):
            @pl.when((r != a) | (n != b))
            def _():
                rest_copy(a, b, r * 4 + n).start()

    for j, keep in enumerate((qa_keep, qb_keep)):
        q_hops[j].wait_recv()
        next_q[j] = (keep[1].astype(f32) + first_q[j, 1].astype(f32)).astype(bf16)
        q_later[j].start()
    scatter.advance((), (0, 1))
    for j, keep in enumerate((qa_keep, qb_keep)):
        q_later[j].wait_recv()
        total = keep[0].astype(f32) + first_q[j, 0].astype(f32) + then_q[j].astype(f32)
        query_out[j * 128 : j * 128 + 128, :] = total[:, 0:512]
        kv[w, j * 128 : j * 128 + 128, :] = total[:, 512:768].astype(bf16)

    def kv_copy(j, slot):
        return pltpu.make_async_remote_copy(
            kv.at[w], kv.at[w], k_s.at[j], k_g.at[slot],
            device_id=(r, n, jnp.int32(j)), device_id_type=MESH,
        )

    def kv_wait(j):
        return pltpu.make_async_remote_copy(
            kv.at[j], kv.at[j], k_s.at[j], k_g.at[j],
            device_id=(r, n, jnp.int32(j)), device_id_type=MESH,
        )

    for j in range(4):
        @pl.when(w != j)
        def _():
            kv_copy(j, w).start()

    scatter.advance((), (2, 3))
    for j, (keep, came) in enumerate(((oa_keep, oa_in), (ob_keep, ob_in))):
        o_hops[j].wait_recv()
        output_out[j * 128 : j * 128 + 128, :] = (
            keep[0].astype(f32) + came[0].astype(f32) + then_o[j].astype(f32)
        )
    mine_block = r * 4 + n
    ga_out[0:1] = summed[pl.ds(mine_block, 1), :]
    ga_out[1:2] = summed[pl.ds(mine_block + 8, 1), :]
    for a in range(2):
        for b in range(4):
            @pl.when((r != a) | (n != b))
            def _():
                slot = a * 4 + b
                rest_copy(a, b, slot).wait_recv()
                ga_out[0:1] += over_rest[slot, pl.ds(mine_block, 1), :]
                ga_out[1:2] += over_rest[slot, pl.ds(mine_block + 8, 1), :]

    scatter.total(acc)

    def last(rows):
        grad = norm_back(hidden[rows, :].astype(f32), gain[...], acc[rows, :])
        grad_out[rows, :] = (grad + gmid[rows, :]).astype(bf16)

    each_rows(hidden.shape[0], 16, last)
    lane = lax.broadcasted_iota(jnp.int32, (256, 128), 1)
    for j in range(4):
        @pl.when(w != j)
        def _():
            kv_wait(j).wait_recv()

        even, odd = kv[j, :, 0:128].astype(f32), kv[j, :, 128:256].astype(f32)
        here = slice(j * 128, j * 128 + 128)
        key_out[:, here] = jnp.where(lane < 64, even, pltpu.roll(odd, 64, 1))
        value_out[:, here] = jnp.where(lane < 64, pltpu.roll(even, 64, 1), odd)
    scatter.sent()
    for hop in q_hops + q_later + o_hops:
        hop.wait_send()
    for j in range(4):
        @pl.when(w != j)
        def _():
            kv_copy(j, w).wait_send()

    for j in range(4):
        @pl.when(w != j)
        def _():
            wid_copy(j, w).wait_send()

    for a in range(2):
        for b in range(4):
            @pl.when((r != a) | (n != b))
            def _():
                rest_copy(a, b, r * 4 + n).wait_send()


def leave(*args):
    shard, width = 128, 2048
    grad = jax.ShapeDtypeStruct((256, 512), f32)
    return comm_call(
        leave_kernel, "leave", 7,
        (jax.ShapeDtypeStruct((shard, width), bf16), jax.ShapeDtypeStruct((8, 256), f32))
        + (grad,) * 4,
        [vmem()] * 13, [vmem()] * 6,
        [pltpu.VMEM((4, shard, width), bf16)]
        + scatter_bufs(shard, width) + scatter_sems()
        + [
            pltpu.VMEM((shard, width), f32),
            pltpu.VMEM((4, 16, 256), f32),
            pltpu.VMEM((16, 256), f32),
            pltpu.VMEM((8, 16, 256), f32),
            pltpu.SemaphoreType.DMA((4,)),
            pltpu.SemaphoreType.DMA((4,)),
            pltpu.SemaphoreType.DMA((8,)),
            pltpu.SemaphoreType.DMA((8,)),
            pltpu.VMEM((2, 2, 128, 768), bf16),
            pltpu.VMEM((2, 128, 768), bf16),
            pltpu.VMEM((2, 128, 768), bf16),
            pltpu.VMEM((2, 128, 512), bf16),
            pltpu.VMEM((2, 128, 512), bf16),
            pltpu.VMEM((4, 256, 256), bf16),
            pltpu.SemaphoreType.DMA((6,)),
            pltpu.SemaphoreType.DMA((6,)),
            pltpu.SemaphoreType.DMA((4,)),
            pltpu.SemaphoreType.DMA((4,)),
        ],
        args, flops=10**10, sent=10**8,
    )


def local_fast(
    hidden_in, doc_lengths, w_query, w_key, w_value, w_output, w_gate, w_up, w_down,
    gain_attn, gain_ffn, grad_out,
):
    r, n, w = spot()
    hidden, grad_top = hidden_in[0], grad_out[0]
    gain_a, gain_f = gain_attn[None], gain_ffn[None]
    def half(weight, axis):
        size = weight.shape[axis] // 2
        return lax.dynamic_slice_in_dim(weight, r * size, size, axis)

    head = (w * 2 + r) * HD
    kv_pack = jnp.concatenate(
        [lax.dynamic_slice_in_dim(w_key, head, HD, 1), lax.dynamic_slice_in_dim(w_value, head, HD, 1)],
        axis=1,
    )
    out_half = half(w_output, 0)
    p1_shard = jnp.concatenate(
        [half(w_query, 1), kv_pack, jnp.concatenate([out_half[:, :256], out_half[:, 256:]], axis=0)],
        axis=1,
    )
    down_half = half(w_down, 0)
    p2_shard = jnp.stack(
        [
            half(w_gate, 1),
            half(w_up, 1),
            jnp.concatenate([down_half[:512], down_half[512:]], axis=1),
        ]
    )
    p1 = lax.all_gather(p1_shard, "nar", axis=0)
    p2 = lax.all_gather(p2_shard, "nar", axis=0)

    token_ids = n * 512 + jnp.arange(512, dtype=jnp.int32)
    doc_start, places = doc_layout(doc_lengths[0], token_ids)
    angles = places.astype(f32)[:, None] * inverse_freq()[None, :]
    cosine, sine = jnp.cos(angles), jnp.sin(angles)
    start_here = (doc_start - (n - 2) * 512).astype(f32)
    tab = jnp.concatenate(
        [cosine] * 4 + [-sine, sine] * 2 + [jnp.broadcast_to(start_here[:, None], (512, 128))],
        axis=1,
    )

    rows, tabs = enter(hidden, gain_a, tab)
    rows3, rows2 = rows.reshape(2, 512, 2048), rows.reshape(1024, 2048)
    q, kv = project(rows3, p1, tabs)
    low = tabs[:, ::QUERIES, 256].astype(jnp.int32).reshape(8)
    kv_flat = kv.reshape(2, 1536, 128)
    att, lse = attend(low, q, kv_flat, tabs)
    mid, ffn_rows, top_rows = middle_stage(att, p1, hidden, gain_f, grad_top)
    parts, total, gain_f_part, a_send, a_keep, b_send, b_keep, ra_d, rb_d = ffn_stage(
        ffn_rows.reshape(1024, 2048), top_rows.reshape(1024, 2048), p2, gain_f
    )
    gmid, datt, oa_send, oa_keep, ob_send, ob_keep, ra_gu, rb_gu = branch_stage(
        total, mid, grad_top, gain_f, p1, att.reshape(1024, 256), a_send, b_send
    )
    dq, dkv = attend_back(low, q, kv_flat, tabs, att, datt, lse)
    (
        dparts, gain_a_part, qa_send, qa_keep, qb_send, qb_keep,
        hidden_out, ra_last, rb_last, oa_came, ob_came,
    ) = unproject(
        dq, dkv.reshape(2, 3, 512, 128), rows2, p1, tabs, gain_a, parts, mid,
        a_keep, b_keep, ra_gu, rb_gu, ra_d, rb_d, oa_send, ob_send,
    )
    gains = jnp.concatenate(
        [gain_f_part.sum(axis=0).reshape(8, 256), gain_a_part.sum(axis=0).reshape(8, 256)], axis=0
    )
    grad_in, gain_sums, grad_query, grad_key, grad_value, output_sum = leave(
        dparts, hidden, gain_a, gmid, gains,
        qa_send, qa_keep, qb_send, qb_keep, oa_keep, ob_keep, oa_came, ob_came,
    )

    def joined(which):
        def half_rows(keep, came, last):
            return keep[0, which].astype(f32) + came.astype(f32) + last[which].astype(f32)

        a_came, b_came = (ra_d[0], rb_d[0]) if which == 2 else (ra_gu[0, which], rb_gu[0, which])
        return jnp.concatenate(
            [half_rows(a_keep, a_came, ra_last), half_rows(b_keep, b_came, rb_last)], axis=0
        )

    return (
        hidden_out[None],
        grad_in[None],
        grad_query,
        grad_key,
        grad_value,
        output_sum.T,
        joined(0),
        joined(1),
        joined(2).T,
        gain_sums[1],
        gain_sums[0],
    )


def solution(mesh):
    in_specs = (
        P("row", ("nar", "wid"), None),
        P("row", None),
        P("nar", "wid"),
        P("nar", None),
        P("nar", None),
        P("wid", "nar"),
        P("nar", "wid"),
        P("nar", "wid"),
        P("wid", "nar"),
        P(),
        P(),
        P("row", ("nar", "wid"), None),
    )
    out_specs = (
        P("row", ("nar", "wid"), None),
        P("row", ("nar", "wid"), None),
        P(("row", "nar"), "wid"),
        P(("row", "nar"), None),
        P(("row", "nar"), None),
        P("wid", ("row", "nar")),
        P(("row", "nar"), "wid"),
        P(("row", "nar"), "wid"),
        P("wid", ("row", "nar")),
        P(("row", "nar")),
        P(("row", "nar")),
    )
    sizes = dict(mesh.shape)
    fits = sizes == {"row": 2, "nar": 4, "wid": 4}

    def body(*args):
        small = args[0].shape == (1, 128, 2048)
        return (local_fast if fits and small else local)(*args)

    return jax.shard_map(body, mesh=mesh, in_specs=in_specs, out_specs=out_specs, check_vma=False)
```

```python
import math

import jax
import jax.numpy as jnp
from jax import lax
from jax.experimental import pallas as pl
from jax.experimental.pallas import tpu as pltpu
from jax.sharding import PartitionSpec as P

H = 32
KV = 8
HD = 64


norm_eps = 1e-05
masked_score = -1e30


def inverse_freq():
    listed = []
    for pair_index in range(HD // 2):
        base_freq = 500000.0 ** (-2.0 * pair_index / HD)
        wavelength = 2.0 * math.pi / base_freq
        smoothing = (8192.0 / wavelength - 1.0) / 3.0
        blended = (1.0 - smoothing) * base_freq / 32.0 + smoothing * base_freq
        if wavelength < 2048.0:
            listed.append(base_freq)
        elif wavelength > 8192.0:
            listed.append(base_freq / 32.0)
        else:
            listed.append(blended)
    return jnp.asarray(listed, dtype=jnp.float32)


def rotate(values, cosine_table, sine_table):
    half_dim = HD // 2
    first_half = values[..., :half_dim]
    second_half = values[..., half_dim:]
    return jnp.concatenate(
        [
            first_half * cosine_table - second_half * sine_table,
            second_half * cosine_table + first_half * sine_table,
        ],
        axis=-1,
    )


def rotate_back(grads_in, cosine_table, sine_table):
    half_dim = HD // 2
    first_half = grads_in[..., :half_dim]
    second_half = grads_in[..., half_dim:]
    return jnp.concatenate(
        [
            first_half * cosine_table + second_half * sine_table,
            second_half * cosine_table - first_half * sine_table,
        ],
        axis=-1,
    )


def doc_layout(lengths_row, token_ids):
    ends_at = jnp.cumsum(lengths_row, dtype=jnp.int32)
    starts_at = ends_at - lengths_row
    inside = (token_ids[:, None] >= starts_at[None, :]) & (token_ids[:, None] < ends_at[None, :])
    doc_start = jnp.sum(jnp.where(inside, starts_at[None, :], 0), axis=1, dtype=jnp.int32)
    return (doc_start, token_ids - doc_start)


def norm_forward(values, gain_vector):
    root_inv = lax.rsqrt(jnp.mean(values * values, axis=-1, keepdims=True) + norm_eps)
    return (root_inv, (values * root_inv * gain_vector).astype(jnp.bfloat16))


def norm_backward(values, root_inv, gain_vector, grad_normed):
    weighted = grad_normed * gain_vector
    inner_sum = jnp.mean(weighted * values, axis=-1, keepdims=True)
    grad_values = root_inv * weighted - values * (root_inv * root_inv * root_inv) * inner_sum
    gain_term = jnp.sum(grad_normed * values * root_inv, axis=0)
    return (grad_values, gain_term)


def contract_last(left_side, right_side):
    return lax.dot_general(
        left_side, right_side, (((1,), (1,)), ((), ())), preferred_element_type=jnp.float32
    )


def contract_first(left_side, right_side):
    return lax.dot_general(
        left_side, right_side, (((0,), (0,)), ((), ())), preferred_element_type=jnp.float32
    )


def local(
    hidden_in,
    doc_lengths,
    w_query,
    w_key,
    w_value,
    w_output,
    w_gate,
    w_up,
    w_down,
    gain_attn,
    gain_ffn,
    grad_out,
):
    wid_count = lax.axis_size("wid")
    nar_count = lax.axis_size("nar")
    wid_index = lax.axis_index("wid")
    nar_index = lax.axis_index("nar")
    local_tokens = hidden_in.shape[1]
    block_tokens = local_tokens * wid_count
    seq_length = block_tokens * nar_count
    query_heads = w_query.shape[1] // HD
    group_size = H // KV
    kv_local = max(query_heads // group_size, 1)
    heads_per_kv = query_heads // kv_local
    kv_first = wid_index * query_heads // group_size
    query_block = min(512, block_tokens)
    block_count = block_tokens // query_block
    item_count = block_count * query_heads
    attn_scale = HD ** (-0.5)
    query_full, key_full, value_full, output_full, gate_full, up_full, down_full = (
        lax.all_gather(w_query, "nar", axis=0, tiled=True),
        lax.all_gather(w_key, "nar", axis=0, tiled=True),
        lax.all_gather(w_value, "nar", axis=0, tiled=True),
        lax.all_gather(w_output, "nar", axis=1, tiled=True),
        lax.all_gather(w_gate, "nar", axis=0, tiled=True),
        lax.all_gather(w_up, "nar", axis=0, tiled=True),
        lax.all_gather(w_down, "nar", axis=1, tiled=True),
    )
    key_local = lax.dynamic_slice_in_dim(key_full, kv_first * HD, kv_local * HD, 1)
    value_local = lax.dynamic_slice_in_dim(value_full, kv_first * HD, kv_local * HD, 1)
    token_ids = nar_index * block_tokens + jnp.arange(block_tokens, dtype=jnp.int32)
    doc_start, places = doc_layout(doc_lengths[0], token_ids)
    angles = places.astype(jnp.float32)[:, None] * inverse_freq()[None, :]
    cosine_table = jnp.cos(angles)[:, None, :]
    sine_table = jnp.sin(angles)[:, None, :]
    key_ids = jnp.arange(seq_length, dtype=jnp.int32)
    residual = hidden_in[0].astype(jnp.float32)
    root_attn, normed_attn = norm_forward(residual, gain_attn)
    normed_rows = lax.all_gather(normed_attn, "wid", axis=0, tiled=True)
    query_pre = jnp.dot(normed_rows, query_full, preferred_element_type=jnp.float32)
    key_pre = jnp.dot(normed_rows, key_local, preferred_element_type=jnp.float32)
    value_rows = jnp.dot(normed_rows, value_local, preferred_element_type=jnp.float32).astype(
        jnp.bfloat16
    )
    query_rot = (
        rotate(query_pre.reshape(block_tokens, query_heads, HD), cosine_table, sine_table)
        .astype(jnp.bfloat16)
        .reshape(block_tokens, query_heads * HD)
    )
    key_rot = (
        rotate(key_pre.reshape(block_tokens, kv_local, HD), cosine_table, sine_table)
        .astype(jnp.bfloat16)
        .reshape(block_tokens, kv_local * HD)
    )
    key_seq, value_seq = (
        lax.all_gather(key_rot, "nar", axis=0, tiled=True),
        lax.all_gather(value_rows, "nar", axis=0, tiled=True),
    )

    def item_inputs(item_index):
        block_index = item_index // query_heads
        head_index = item_index % query_heads
        kv_index = head_index // heads_per_kv
        row_first = block_index * query_block
        query_part = lax.dynamic_slice(query_rot, (row_first, head_index * HD), (query_block, HD))
        key_head = lax.dynamic_slice_in_dim(key_seq, kv_index * HD, HD, 1)
        value_head = lax.dynamic_slice_in_dim(value_seq, kv_index * HD, HD, 1)
        query_ids = lax.dynamic_slice_in_dim(token_ids, row_first, query_block, 0)
        query_starts = lax.dynamic_slice_in_dim(doc_start, row_first, query_block, 0)
        allowed = (key_ids[None, :] <= query_ids[:, None]) & (
            key_ids[None, :] >= query_starts[:, None]
        )
        scores = contract_last(query_part, key_head) * attn_scale
        return (
            row_first,
            head_index,
            kv_index,
            query_part,
            key_head,
            value_head,
            jnp.where(allowed, scores, masked_score),
        )

    def attend(item_index):
        row_first, head_index, kv_index, query_part, key_head, value_head, scores = item_inputs(
            item_index
        )
        row_max = jnp.max(scores, axis=1, keepdims=True)
        exp_scores = jnp.exp(scores - row_max)
        row_total = jnp.sum(exp_scores, axis=1, keepdims=True)
        probability = (exp_scores / row_total).astype(jnp.bfloat16)
        attended = jnp.dot(probability, value_head, preferred_element_type=jnp.float32)
        return (attended, (row_max + jnp.log(row_total))[:, 0])

    attended_items, logsum_items = lax.map(attend, jnp.arange(item_count, dtype=jnp.int32))
    attended_rows = (
        attended_items.reshape(block_count, query_heads, query_block, HD)
        .transpose(0, 2, 1, 3)
        .reshape(block_tokens, query_heads * HD)
        .astype(jnp.bfloat16)
    )
    rows_here = attended_rows
    branch_attn = lax.psum_scatter(
        jnp.dot(rows_here, output_full, preferred_element_type=jnp.float32),
        "wid",
        scatter_dimension=0,
        tiled=True,
    )
    middle = residual + branch_attn
    root_ffn, normed_ffn = norm_forward(middle, gain_ffn)
    ffn_rows = lax.all_gather(normed_ffn, "wid", axis=0, tiled=True)
    gate_proj = jnp.dot(ffn_rows, gate_full, preferred_element_type=jnp.float32)
    up_proj = jnp.dot(ffn_rows, up_full, preferred_element_type=jnp.float32)
    gate_sigmoid = jax.nn.sigmoid(gate_proj)
    gate_silu = gate_proj * gate_sigmoid
    activated = (gate_silu * up_proj).astype(jnp.bfloat16)
    rows_here = activated
    branch_ffn = lax.psum_scatter(
        jnp.dot(rows_here, down_full, preferred_element_type=jnp.float32).astype(jnp.bfloat16),
        "wid",
        scatter_dimension=0,
        tiled=True,
    ).astype(jnp.float32)
    hidden_out = (middle + branch_ffn).astype(jnp.bfloat16)[None]
    grad_top = grad_out[0]
    grad_rows = lax.all_gather(grad_top, "wid", axis=0, tiled=True)
    grad_activated = contract_last(grad_rows, down_full)
    down_weight_grad = contract_first(activated, grad_rows)
    silu_slope = gate_sigmoid * (1.0 + gate_proj * (1.0 - gate_sigmoid))
    grad_gate_b = (grad_activated * up_proj * silu_slope).astype(jnp.bfloat16)
    grad_up_b = (grad_activated * gate_silu).astype(jnp.bfloat16)
    gate_weight_grad = contract_first(ffn_rows, grad_gate_b)
    up_weight_grad = contract_first(ffn_rows, grad_up_b)
    grad_normed_ffn = lax.psum_scatter(
        contract_last(grad_gate_b, gate_full) + contract_last(grad_up_b, up_full),
        "wid",
        scatter_dimension=0,
        tiled=True,
    )
    grad_middle, gain_ffn_term = norm_backward(middle, root_ffn, gain_ffn, grad_normed_ffn)
    grad_middle = grad_middle + grad_top.astype(jnp.float32)
    grad_branch = grad_middle.astype(jnp.bfloat16)
    branch_rows = lax.all_gather(grad_branch, "wid", axis=0, tiled=True)
    grad_attended = contract_last(branch_rows, output_full).astype(jnp.bfloat16)
    output_weight_grad = contract_first(attended_rows, branch_rows)

    def attend_back(carried, item_index):
        key_grad, value_grad = carried
        row_first, head_index, kv_index, query_part, key_head, value_head, scores = item_inputs(
            item_index
        )
        logsum = lax.dynamic_index_in_dim(logsum_items, item_index, 0, keepdims=False)
        probability = jnp.exp(scores - logsum[:, None])
        grad_part = lax.dynamic_slice(
            grad_attended, (row_first, head_index * HD), (query_block, HD)
        )
        grad_prob = contract_last(grad_part, value_head)
        inner_sum = jnp.sum(probability * grad_prob, axis=1, keepdims=True)
        grad_scores = (probability * (grad_prob - inner_sum)).astype(jnp.bfloat16)
        query_grad = jnp.dot(grad_scores, key_head, preferred_element_type=jnp.float32) * attn_scale
        key_part = contract_first(grad_scores, query_part) * attn_scale
        value_part = contract_first(probability.astype(jnp.bfloat16), grad_part)
        key_old = lax.dynamic_slice_in_dim(key_grad, kv_index * HD, HD, 1)
        key_grad = lax.dynamic_update_slice_in_dim(key_grad, key_old + key_part, kv_index * HD, 1)
        value_old = lax.dynamic_slice_in_dim(value_grad, kv_index * HD, HD, 1)
        value_grad = lax.dynamic_update_slice_in_dim(
            value_grad, value_old + value_part, kv_index * HD, 1
        )
        return ((key_grad, value_grad), query_grad)

    zero_grads = jnp.zeros((seq_length, kv_local * HD), jnp.float32)
    (key_grad_seq, value_grad_seq), query_grad_items = lax.scan(
        attend_back, (zero_grads, zero_grads), jnp.arange(item_count, dtype=jnp.int32)
    )
    key_grad_block, value_grad_block = (
        lax.psum_scatter(
            key_grad_seq.astype(jnp.bfloat16), "nar", scatter_dimension=0, tiled=True
        ).astype(jnp.float32),
        lax.psum_scatter(
            value_grad_seq.astype(jnp.bfloat16), "nar", scatter_dimension=0, tiled=True
        ).astype(jnp.float32),
    )
    query_grad_rows = (
        query_grad_items.reshape(block_count, query_heads, query_block, HD)
        .transpose(0, 2, 1, 3)
        .reshape(block_tokens, query_heads, HD)
    )
    query_grad_b = (
        rotate_back(query_grad_rows, cosine_table, sine_table)
        .astype(jnp.bfloat16)
        .reshape(block_tokens, query_heads * HD)
    )
    key_grad_b = (
        rotate_back(key_grad_block.reshape(block_tokens, kv_local, HD), cosine_table, sine_table)
        .astype(jnp.bfloat16)
        .reshape(block_tokens, kv_local * HD)
    )
    value_grad_b = value_grad_block.astype(jnp.bfloat16)
    query_weight_grad = contract_first(normed_rows, query_grad_b)
    key_weight_grad = contract_first(normed_rows, key_grad_b)
    value_weight_grad = contract_first(normed_rows, value_grad_b)
    grad_normed_attn = lax.psum_scatter(
        (
            contract_last(query_grad_b, query_full)
            + contract_last(key_grad_b, key_local)
            + contract_last(value_grad_b, value_local)
        ).astype(jnp.bfloat16),
        "wid",
        scatter_dimension=0,
        tiled=True,
    ).astype(jnp.float32)
    grad_residual, gain_attn_term = norm_backward(residual, root_attn, gain_attn, grad_normed_attn)
    grad_in = (grad_residual + grad_middle).astype(jnp.bfloat16)[None]
    summed = (
        lax.psum_scatter(
            query_weight_grad.astype(jnp.bfloat16), ("row", "nar"), scatter_dimension=0, tiled=True
        ).astype(jnp.float32),
        lax.psum_scatter(
            key_weight_grad.astype(jnp.bfloat16), ("row", "nar"), scatter_dimension=0, tiled=True
        ).astype(jnp.float32),
        lax.psum_scatter(
            value_weight_grad.astype(jnp.bfloat16), ("row", "nar"), scatter_dimension=0, tiled=True
        ).astype(jnp.float32),
        lax.psum_scatter(
            output_weight_grad.astype(jnp.bfloat16), ("row", "nar"), scatter_dimension=1, tiled=True
        ).astype(jnp.float32),
        lax.psum_scatter(
            gate_weight_grad.astype(jnp.bfloat16), ("row", "nar"), scatter_dimension=0, tiled=True
        ).astype(jnp.float32),
        lax.psum_scatter(
            up_weight_grad.astype(jnp.bfloat16), ("row", "nar"), scatter_dimension=0, tiled=True
        ).astype(jnp.float32),
        lax.psum_scatter(
            down_weight_grad.astype(jnp.bfloat16), ("row", "nar"), scatter_dimension=1, tiled=True
        ).astype(jnp.float32),
        lax.psum_scatter(
            gain_attn_term.astype(jnp.bfloat16), ("row", "nar"), scatter_dimension=0, tiled=True
        ).astype(jnp.float32),
        lax.psum_scatter(
            gain_ffn_term.astype(jnp.bfloat16), ("row", "nar"), scatter_dimension=0, tiled=True
        ).astype(jnp.float32),
    )
    (
        grad_query,
        key_sum,
        value_sum,
        grad_output,
        grad_gate,
        grad_up,
        grad_down,
        gain_attn_sum,
        gain_ffn_sum,
    ) = summed
    key_all, value_all, gain_attn_all, gain_ffn_all = (
        lax.all_gather(key_sum.astype(jnp.bfloat16), "wid", axis=1, tiled=True).astype(
            key_sum.dtype
        ),
        lax.all_gather(value_sum.astype(jnp.bfloat16), "wid", axis=1, tiled=True).astype(
            value_sum.dtype
        ),
        lax.all_gather(gain_attn_sum.astype(jnp.bfloat16), "wid", axis=0, tiled=True).astype(
            gain_attn_sum.dtype
        ),
        lax.all_gather(gain_ffn_sum.astype(jnp.bfloat16), "wid", axis=0, tiled=True).astype(
            gain_ffn_sum.dtype
        ),
    )
    shard_rows = key_sum.shape[0]
    repeats = wid_count * kv_local // KV
    grad_key = key_all.reshape(shard_rows, KV, repeats, HD).sum(axis=2).reshape(shard_rows, KV * HD)
    grad_value = (
        value_all.reshape(shard_rows, KV, repeats, HD).sum(axis=2).reshape(shard_rows, KV * HD)
    )
    grad_gain_attn = gain_attn_all.reshape(wid_count, shard_rows).sum(axis=0)
    grad_gain_ffn = gain_ffn_all.reshape(wid_count, shard_rows).sum(axis=0)
    return (
        hidden_out,
        grad_in,
        grad_query,
        grad_key,
        grad_value,
        grad_output,
        grad_gate,
        grad_up,
        grad_down,
        grad_gain_attn,
        grad_gain_ffn,
    )


MESH = pl.DeviceIdType.MESH
bf16 = jnp.bfloat16
f32 = jnp.float32
VMEM_LIMIT = 60 * 2**20


def spot():
    return lax.axis_index("row"), lax.axis_index("nar"), lax.axis_index("wid")


def greet(partners):
    barrier = pltpu.get_barrier_semaphore()
    total = 0
    for there, device in partners:
        @pl.when(there)
        def _():
            pl.semaphore_signal(barrier, inc=1, device_id=device, device_id_type=MESH)

        total = total + there.astype(jnp.int32)
    pl.semaphore_wait(barrier, total)


def line_partners(r, n, w, wid_count):
    return [
        (w < wid_count - 1, (r, n, jnp.minimum(w + 1, wid_count - 1))),
        (w > 0, (r, n, jnp.maximum(w - 1, 0))),
        (w >= 0, (1 - r, n, w)),
    ]


def each_rows(count, step, body):
    def run(i, carry):
        body(pl.ds(pl.multiple_of(i * step, step), step))
        return carry

    lax.fori_loop(0, count // step, run, 0)


def square_partners(r, n, w):
    return [(n >= 0, over_x(r, n, w)), (n >= 0, over_y(r, n, w))]


def over_x(r, n, w):
    return (r, n + 1 - 2 * (n % 2), w)


def over_y(r, n, w):
    return (r, (n + 2) % 4, w)


def push(source, target, s_s, s_g, device):
    return pltpu.make_async_remote_copy(
        source, target, s_s, s_g, device_id=device, device_id_type=MESH
    )


class Gather:
    def __init__(self, buf, sems, me, wid_count, rows=slice(None)):
        self.rows = rows
        self.buf, (self.up_s, self.dn_s, self.pt_s, self.got) = buf, sems
        self.r, self.n, self.w = me
        self.last = wid_count - 1
        self.up = (self.r, self.n, jnp.minimum(self.w + 1, self.last))
        self.dn = (self.r, self.n, jnp.maximum(self.w - 1, 0))
        self.pt = (1 - self.r, self.n, self.w)

    def copy(self, j, sem, device, row=None):
        row = self.r if row is None else row
        return pltpu.make_async_remote_copy(
            self.buf.at[row, j, self.rows],
            self.buf.at[row, j, self.rows],
            sem.at[j],
            self.got.at[row, j],
            device_id=device,
            device_id_type=MESH,
        )

    def pass_on(self, j, go_up, go_dn):
        if go_up:
            @pl.when(self.w < self.last)
            def _():
                self.copy(j, self.up_s, self.up).start()

        if go_dn:
            @pl.when(self.w > 0)
            def _():
                self.copy(j, self.dn_s, self.dn).start()

        self.copy(j, self.pt_s, self.pt).start()

    def own(self):
        self.pass_on(self.w, True, True)

    def arrive(self, row, j):
        self.copy(j, self.pt_s, self.pt, row).wait_recv()

    def step(self, k):
        below, above = self.w - k, self.w + k

        @pl.when(below >= 0)
        def _():
            self.arrive(self.r, below)
            self.pass_on(below, True, False)

        @pl.when(above <= self.last)
        def _():
            self.arrive(self.r, above)
            self.pass_on(above, False, True)

    def rest(self):
        for j in range(self.last + 1):
            self.arrive(1 - self.r, j)

    def sent(self):
        for j in range(self.last + 1):
            @pl.when((j <= self.w) & (self.w < self.last))
            def _():
                self.copy(j, self.up_s, self.up).wait_send()

            @pl.when((j >= self.w) & (self.w > 0))
            def _():
                self.copy(j, self.dn_s, self.dn).wait_send()

            self.copy(j, self.pt_s, self.pt).wait_send()


def gather_scratch(shard, width):
    return [pltpu.VMEM((2, 4, shard, width), bf16)] + gather_sems()


def gather_sems():
    return [pltpu.SemaphoreType.DMA((4,))] * 3 + [pltpu.SemaphoreType.DMA((2, 4))]


class Scatter:
    def __init__(self, mine, theirs, bufs, sems, me, wid_count):
        self.mine, self.theirs = mine, theirs
        self.from_pt, self.from_up, self.from_dn = bufs
        self.pt_s, self.pt_g, self.up_s, self.up_g, self.dn_s, self.dn_g = sems
        self.r, self.n, self.w = me
        self.last = wid_count - 1
        self.up = (self.r, self.n, jnp.minimum(self.w + 1, self.last))
        self.dn = (self.r, self.n, jnp.maximum(self.w - 1, 0))
        self.pt = (1 - self.r, self.n, self.w)

    def order(self, i):
        low, high = (3, 0, 2, 1)[i], (0, 3, 1, 2)[i]
        return jnp.where(self.w < 2, low, high)

    def pair(self, s):
        return pltpu.make_async_remote_copy(
            self.theirs.at[s], self.from_pt.at[s], self.pt_s.at[s], self.pt_g.at[s],
            device_id=self.pt, device_id_type=MESH,
        )

    def climb(self, s):
        return pltpu.make_async_remote_copy(
            self.mine.at[s], self.from_dn.at[s], self.up_s.at[s], self.up_g.at[s],
            device_id=self.up, device_id_type=MESH,
        )

    def fall(self, s):
        return pltpu.make_async_remote_copy(
            self.mine.at[s], self.from_up.at[s], self.dn_s.at[s], self.dn_g.at[s],
            device_id=self.dn, device_id_type=MESH,
        )

    def add(self, s, others):
        def body(rows):
            total = self.mine[s, rows, :].astype(f32)
            for other in others:
                total = total + other[s, rows, :].astype(f32)
            self.mine[s, rows, :] = total.astype(bf16)

        each_rows(self.mine.shape[1], 16, body)

    def step(self, s):
        self.pair(s).wait_recv()

        @pl.when((s > self.w) & (self.w > 0))
        def _():
            self.climb(s).wait_recv()
            self.add(s, (self.from_pt, self.from_dn))

        @pl.when((s < self.w) & (self.w < self.last))
        def _():
            self.fall(s).wait_recv()
            self.add(s, (self.from_pt, self.from_up))

        @pl.when(((s > self.w) & (self.w == 0)) | ((s < self.w) & (self.w == self.last)))
        def _():
            self.add(s, (self.from_pt,))

        @pl.when(s > self.w)
        def _():
            self.climb(s).start()

        @pl.when(s < self.w)
        def _():
            self.fall(s).start()

    def advance(self, edge_steps, inner_steps):
        for ends, steps in ((True, edge_steps), (False, inner_steps)):
            at_end = (self.w == 0) | (self.w == self.last)

            @pl.when(at_end if ends else jnp.logical_not(at_end))
            def _():
                for i in steps:
                    self.step(self.order(i))

    def total(self, out):
        w = self.w

        def first(rows):
            out[rows, :] = self.mine[w, rows, :].astype(f32) + self.from_pt[w, rows, :].astype(f32)

        each_rows(out.shape[0], 16, first)

        @pl.when(w > 0)
        def _():
            self.climb(w).wait_recv()

            def more(rows):
                out[rows, :] += self.from_dn[w, rows, :].astype(f32)

            each_rows(out.shape[0], 16, more)

        @pl.when(w < self.last)
        def _():
            self.fall(w).wait_recv()

            def more(rows):
                out[rows, :] += self.from_up[w, rows, :].astype(f32)

            each_rows(out.shape[0], 16, more)

    def sent(self):
        for s in range(self.last + 1):
            self.pair(s).wait_send()

            @pl.when(s > self.w)
            def _():
                self.climb(s).wait_send()

            @pl.when(s < self.w)
            def _():
                self.fall(s).wait_send()


def scatter_bufs(shard, width):
    return [pltpu.VMEM((4, shard, width), bf16)] * 3


def scatter_sems():
    return [pltpu.SemaphoreType.DMA((4,))] * 6


def vmem():
    return pl.BlockSpec(memory_space=pltpu.VMEM)


def hbm():
    return pl.BlockSpec(memory_space=pl.ANY)


def comm_call(kernel, name, cid, out_shape, in_specs, out_specs, scratch, args, flops=0, sent=0):
    return pl.pallas_call(
        kernel,
        out_shape=out_shape,
        in_specs=in_specs,
        out_specs=out_specs,
        scratch_shapes=scratch,
        compiler_params=pltpu.CompilerParams(
            collective_id=cid, has_side_effects=True, vmem_limit_bytes=VMEM_LIMIT
        ),
        cost_estimate=pl.CostEstimate(flops=flops, bytes_accessed=sent, transcendentals=0),
        name=name,
    )(*args)


def norm_rows(x, gain):
    root = lax.rsqrt(jnp.mean(x * x, axis=-1, keepdims=True) + norm_eps)
    return x * root * gain


def turn(x, cosine, sine):
    lane = lax.broadcasted_iota(jnp.int32, x.shape, 1)
    swapped = jnp.where(lane % 64 < 32, pltpu.roll(x, 96, 1), pltpu.roll(x, 32, 1))
    return x * cosine + swapped * sine


def enter_kernel(hidden, gain, tab, rows_out, tabs_out, buf, up_s, dn_s, pt_s, got, tabs, tab_s, tab_g, out_s):
    me = spot()
    r, n, w = me
    greet(line_partners(r, n, w, 4))
    gather = Gather(buf, (up_s, dn_s, pt_s, got), me, 4)
    tab_copy = pltpu.make_async_remote_copy(
        tab, tabs.at[r], tab_s, tab_g, device_id=(1 - r, n, w), device_id_type=MESH
    )

    def body(rows):
        buf[r, w, rows, :] = norm_rows(hidden[rows, :].astype(f32), gain[...]).astype(bf16)

    each_rows(hidden.shape[0], 16, body)
    gather.own()
    tab_copy.start()

    def keep(rows):
        tabs[r, rows, :] = tab[rows, :]

    each_rows(tab.shape[0], 16, keep)
    for k in (1, 2, 3):
        gather.step(k)
    gather.rest()
    out = pltpu.make_async_copy(buf, rows_out, out_s.at[0])
    out.start()
    tab_copy.wait_recv()
    out_tab = pltpu.make_async_copy(tabs, tabs_out, out_s.at[1])
    out_tab.start()
    gather.sent()
    tab_copy.wait_send()
    out.wait()
    out_tab.wait()


def enter(hidden, gain, tab):
    shard, width = hidden.shape
    return comm_call(
        enter_kernel, "enter", 1,
        (
            jax.ShapeDtypeStruct((2, 4, shard, width), bf16),
            jax.ShapeDtypeStruct((2,) + tab.shape, f32),
        ),
        [vmem()] * 3, [hbm()] * 2,
        gather_scratch(shard, width)
        + [
            pltpu.VMEM((2,) + tab.shape, f32),
            pltpu.SemaphoreType.DMA(()),
            pltpu.SemaphoreType.DMA(()),
            pltpu.SemaphoreType.DMA((2,)),
        ],
        (hidden, gain, tab), flops=10**10, sent=10**8,
    )


def nar_device(r, n, w, by):
    return (r, jnp.clip(n + by, 0, 3), w)


def project_kernel(
    x, p1, tabs, grad_top, q_out, kv_out, tops_out, kv, s_s, s_g, out_s, buf, g0, g1, g2, g3, tops_s
):
    r, n, w = spot()
    greet(
        line_partners(r, n, w, 4)
        + [
            (n >= 1, nar_device(r, n, w, -1)),
            (n >= 2, nar_device(r, n, w, -2)),
            (n <= 2, nar_device(r, n, w, 1)),
            (n <= 1, nar_device(r, n, w, 2)),
        ]
    )
    gather = Gather(buf, (g0, g1, g2, g3), (r, n, w), 4)

    def keep(rows):
        buf[r, w, rows, :] = grad_top[rows, :]

    each_rows(64, 16, keep)
    gather.own()

    def copy(row, slot, by):
        return pltpu.make_async_remote_copy(
            kv.at[row, 2], kv.at[row, slot], s_s.at[row, slot], s_g.at[row, slot],
            device_id=nar_device(r, n, w, by), device_id_type=MESH,
        )

    lane = lax.broadcasted_iota(jnp.int32, (256, 128), 1)
    weight = p1[:, :, 0:384].reshape(2048, 384)
    for row in range(2):
        def tile(i, carry):
            rows = pl.ds(pl.multiple_of(i * 256, 256), 256)
            cosine, sine = tabs[row, rows, 0:128], tabs[row, rows, 128:256]
            pre = jnp.dot(x[row, rows, :], weight, preferred_element_type=f32)
            q_out[row, rows, 0:128] = turn(pre[:, 0:128], cosine, sine).astype(bf16)
            q_out[row, rows, 128:256] = turn(pre[:, 128:256], cosine, sine).astype(bf16)
            both = pre[:, 256:384]
            kv[row, 2, rows, :] = jnp.where(lane < 64, turn(both, cosine, sine), both).astype(bf16)
            return carry

        lax.fori_loop(0, 2, tile, 0)

        @pl.when(n <= 2)
        def _():
            copy(row, 1, 1).start()

        @pl.when(n <= 1)
        def _():
            copy(row, 0, 2).start()

        for slot, least in ((1, 1), (0, 2)):
            @pl.when(n < least)
            def _():
                kv[row, slot] = jnp.zeros((512, 128), bf16)

    for k in (1, 2, 3):
        gather.step(k)
    gather.rest()
    tops_copy = pltpu.make_async_copy(buf, tops_out, tops_s)
    tops_copy.start()
    for row in range(2):
        for slot, least, by in ((1, 1, 1), (0, 2, 2)):
            @pl.when(n >= least)
            def _():
                copy(row, slot, by).wait_recv()

    out = pltpu.make_async_copy(kv, kv_out, out_s)
    out.start()
    for row in range(2):
        @pl.when(n <= 2)
        def _():
            copy(row, 1, 1).wait_send()

        @pl.when(n <= 1)
        def _():
            copy(row, 0, 2).wait_send()

    gather.sent()
    out.wait()
    tops_copy.wait()


def project(x, p1, tabs, grad_top):
    return comm_call(
        project_kernel, "project", 2,
        (
            jax.ShapeDtypeStruct((2, 512, 256), bf16),
            jax.ShapeDtypeStruct((2, 3, 512, 128), bf16),
            jax.ShapeDtypeStruct((2, 4, 64, 2048), bf16),
        ),
        [vmem()] * 4, [vmem(), hbm(), hbm()],
        [
            pltpu.VMEM((2, 3, 512, 128), bf16),
            pltpu.SemaphoreType.DMA((2, 3)),
            pltpu.SemaphoreType.DMA((2, 3)),
            pltpu.SemaphoreType.DMA(()),
        ]
        + gather_scratch(64, 2048)
        + [pltpu.SemaphoreType.DMA(())],
        (x, p1, tabs, grad_top), flops=10**10, sent=10**7,
    )


KEYS = 256
QUERIES = 128


def stack_low(x):
    lane = lax.broadcasted_iota(jnp.int32, (QUERIES, 128), 1)
    zero = jnp.zeros((QUERIES, 128), x.dtype)
    parts = []
    for pair in range(2):
        block = x[:, pair * 128 : pair * 128 + 128]
        parts.append(jnp.where(lane < 64, block, zero))
        parts.append(jnp.where(lane < 64, pltpu.roll(block, 64, 1), zero))
    return jnp.concatenate(parts, axis=0)


def stack_high(x):
    lane = lax.broadcasted_iota(jnp.int32, (QUERIES, 128), 1)
    zero = jnp.zeros((QUERIES, 128), x.dtype)
    parts = []
    for pair in range(2):
        block = x[:, pair * 128 : pair * 128 + 128]
        parts.append(jnp.where(lane >= 64, pltpu.roll(block, 64, 1), zero))
        parts.append(jnp.where(lane >= 64, block, zero))
    return jnp.concatenate(parts, axis=0)


def unstack(x, low):
    lane = lax.broadcasted_iota(jnp.int32, (QUERIES, 128), 1)
    out = []
    for pair in range(2):
        even = x[2 * pair * QUERIES : (2 * pair + 1) * QUERIES]
        odd = x[(2 * pair + 1) * QUERIES : (2 * pair + 2) * QUERIES]
        if low:
            out.append(jnp.where(lane < 64, even, pltpu.roll(odd, 64, 1)))
        else:
            out.append(jnp.where(lane < 64, pltpu.roll(even, 64, 1), odd))
    return jnp.concatenate(out, axis=1)


def allowed_tile(starts, tile, first_query):
    key = lax.broadcasted_iota(jnp.int32, (QUERIES, KEYS), 1) + tile * KEYS
    query = lax.broadcasted_iota(jnp.int32, (QUERIES, KEYS), 0) + first_query
    start = jnp.concatenate([starts] * (KEYS // 128), axis=1)
    ok = (key <= query) & (key.astype(f32) >= start)
    return jnp.concatenate([ok] * 4, axis=0)


def key_tiles(low, row, block):
    first_query = 1024 + block * QUERIES
    return low[row * 4 + block] // KEYS, first_query // KEYS + 1, first_query


def attend_kernel(low, q, kv, starts, out, lse):
    row, block = pl.program_id(0), pl.program_id(1)
    first, end, first_query = key_tiles(low, row, block)
    query = stack_low(q[0].astype(f32)).astype(bf16)

    def body(tile, carry):
        top, total, acc = carry
        both = kv[0, pl.ds(pl.multiple_of(tile * KEYS, KEYS), KEYS), :]
        scores = contract_last(query, both) * 0.125
        ok = allowed_tile(starts[0], tile, first_query)
        scores = jnp.where(ok, scores, masked_score)
        new_top = jnp.maximum(top, jnp.max(scores, axis=1, keepdims=True))
        shrink = jnp.exp(top - new_top)
        part = jnp.exp(scores - new_top)
        total = total * shrink + jnp.sum(part, axis=1, keepdims=True)
        acc = acc * shrink + jnp.dot(part.astype(bf16), both, preferred_element_type=f32)
        return new_top, total, acc

    top, total, acc = lax.fori_loop(
        first, end, body,
        (
            jnp.full((4 * QUERIES, 1), masked_score, f32),
            jnp.zeros((4 * QUERIES, 1), f32),
            jnp.zeros((4 * QUERIES, 128), f32),
        ),
    )
    out[0] = unstack(acc / total, False).astype(bf16)
    lse[0, 0] = jnp.broadcast_to(top + jnp.log(total), (4 * QUERIES, 128))


def attend_specs():
    return [
        pl.BlockSpec((1, QUERIES, 256), lambda i, j, low: (i, j, 0)),
        pl.BlockSpec((1, 1536, 128), lambda i, j, low: (i, 0, 0)),
        pl.BlockSpec((1, QUERIES, 128), lambda i, j, low: (i, j, 2)),
    ]


def attend(low, q, kv, tabs):
    return pl.pallas_call(
        attend_kernel,
        out_shape=(
            jax.ShapeDtypeStruct((2, 512, 256), bf16),
            jax.ShapeDtypeStruct((2, 4, 4 * QUERIES, 128), f32),
        ),
        grid_spec=pltpu.PrefetchScalarGridSpec(
            num_scalar_prefetch=1, grid=(2, 4),
            in_specs=attend_specs(),
            out_specs=[
                pl.BlockSpec((1, QUERIES, 256), lambda i, j, low: (i, j, 0)),
                pl.BlockSpec((1, 1, 4 * QUERIES, 128), lambda i, j, low: (i, j, 0, 0)),
            ],
        ),
        compiler_params=pltpu.CompilerParams(vmem_limit_bytes=VMEM_LIMIT),
        cost_estimate=pl.CostEstimate(flops=2 * 10**10, bytes_accessed=10**7, transcendentals=10**7),
        name="attend",
    )(low, q, kv, tabs)


def attend_back_kernel(low, q, kv, starts, turns, att, grad, lse, dq_out, dkv_out, dkv):
    row, block = pl.program_id(0), pl.program_id(1)
    first, end, first_query = key_tiles(low, row, block)

    @pl.when(block == 0)
    def _():
        dkv[...] = jnp.zeros_like(dkv)

    query = stack_low(q[0].astype(f32)).astype(bf16)
    grads = stack_high(grad[0].astype(f32))
    inner = jnp.sum(grads * stack_high(att[0].astype(f32)), axis=1, keepdims=True)
    grads = grads.astype(bf16)
    logsum = jnp.concatenate([lse[0, 0]] * (KEYS // 128), axis=1)

    def body(tile, dq):
        rows = pl.ds(pl.multiple_of(tile * KEYS, KEYS), KEYS)
        both = kv[0, rows, :]
        ok = allowed_tile(starts[0], tile, first_query)
        scores = contract_last(query, both) * 0.125
        prob = jnp.where(ok, jnp.exp(scores - logsum), 0.0)
        grad_prob = contract_last(grads, both)
        grad_scores = (prob * (grad_prob - inner)).astype(bf16)
        dkv[rows, :] += contract_first(grad_scores, query) * 0.125 + contract_first(
            prob.astype(bf16), grads
        )
        return dq + jnp.dot(grad_scores, both, preferred_element_type=f32)

    dq = lax.fori_loop(first, end, body, jnp.zeros((4 * QUERIES, 128), f32))
    flat = unstack(dq, True) * 0.125
    cosine, sine = turns[0, :, 0:128], -turns[0, :, 128:256]
    dq_out[0, :, 0:128] = turn(flat[:, 0:128], cosine, sine).astype(bf16)
    dq_out[0, :, 128:256] = turn(flat[:, 128:256], cosine, sine).astype(bf16)

    @pl.when(block == 3)
    def _():
        dkv_out[0] = dkv[...]


def attend_back(low, q, kv, tabs, att, grad, lse):
    tile = pl.BlockSpec((1, QUERIES, 256), lambda i, j, low: (i, j, 0))
    return pl.pallas_call(
        attend_back_kernel,
        out_shape=(
            jax.ShapeDtypeStruct((2, 512, 256), bf16),
            jax.ShapeDtypeStruct((2, 1536, 128), f32),
        ),
        grid_spec=pltpu.PrefetchScalarGridSpec(
            num_scalar_prefetch=1, grid=(2, 4),
            in_specs=attend_specs()
            + [tile, tile, tile, pl.BlockSpec((1, 1, 4 * QUERIES, 128), lambda i, j, low: (i, j, 0, 0))],
            out_specs=[tile, pl.BlockSpec((1, 1536, 128), lambda i, j, low: (i, 0, 0))],
            scratch_shapes=[pltpu.VMEM((1536, 128), f32)],
        ),
        compiler_params=pltpu.CompilerParams(vmem_limit_bytes=VMEM_LIMIT),
        cost_estimate=pl.CostEstimate(flops=4 * 10**10, bytes_accessed=10**7, transcendentals=10**7),
        name="attend_back",
    )(low, q, kv, tabs, tabs, att, grad, lse)


def out_block(p1, nn, half):
    return p1[nn, half * 256 : half * 256 + 256, 384:640]


def middle_kernel(
    att, p1, hidden, gain, mid_out, ffn_out,
    theirs, mine, from_pt, from_up, from_dn, s0, s1, s2, s3, s4, s5, fbuf, h0, h1, h2, h3, out_s,
):
    me = spot()
    r, n, w = me
    greet(line_partners(r, n, w, 4))
    scatter = Scatter(
        mine, theirs, (from_pt, from_up, from_dn), (s0, s1, s2, s3, s4, s5), me, 4
    )
    ffn = Gather(fbuf, (h0, h1, h2, h3), me, 4)
    for i in range(4):
        s = scatter.order(i)
        rows = pl.ds(pl.multiple_of(s * 128, 128), 128)
        left = jnp.concatenate([att[1 - r, rows, :], att[r, rows, :]], axis=0)
        for nn in range(4):
            for half in range(2):
                part = jnp.dot(left, out_block(p1, nn, half), preferred_element_type=f32).astype(bf16)
                columns = slice(nn * 512 + half * 256, nn * 512 + half * 256 + 256)
                theirs[s, :, columns] = part[0:128]
                mine[s, :, columns] = part[128:256]
        scatter.pair(s).start()
    for i in range(4):
        scatter.step(scatter.order(i))
    scatter.total(mid_out)

    def body(rows):
        middle = mid_out[rows, :] + hidden[rows, :].astype(f32)
        mid_out[rows, :] = middle
        fbuf[r, w, rows, :] = norm_rows(middle, gain[...]).astype(bf16)

    each_rows(hidden.shape[0], 16, body)
    ffn.own()
    for k in (1, 2, 3):
        ffn.step(k)
    ffn.rest()
    out_f = pltpu.make_async_copy(fbuf, ffn_out, out_s)
    out_f.start()
    scatter.sent()
    ffn.sent()
    out_f.wait()


def middle_stage(att, p1, hidden, gain):
    shard, width = hidden.shape
    rows = jax.ShapeDtypeStruct((2, 4, shard, width), bf16)
    return comm_call(
        middle_kernel, "middle", 3,
        (jax.ShapeDtypeStruct((shard, width), f32), rows),
        [vmem()] * 4, [vmem(), hbm()],
        [pltpu.VMEM((4, shard, width), bf16)] * 2
        + scatter_bufs(shard, width) + scatter_sems()
        + gather_scratch(shard, width)
        + [pltpu.SemaphoreType.DMA(())],
        (att, p1, hidden, gain), flops=10**10, sent=2 * 10**8,
    )


class Spread:
    def __init__(self, outs, sems, me):
        self.a_send, self.a_keep, self.b_send, self.b_keep = outs
        self.r, self.n, self.w = me
        self.give_s, self.give_g, self.keep_s = sems

    def copies(self, wide, row, place, give):
        for k in range(4):
            block = wide.at[self.n ^ k]
            for part in range(2):
                source = block.at[pl.ds(part * 128, 128)]
                if part == 0:
                    target = (self.a_send if k & 1 else self.a_keep).at[k >> 1]
                else:
                    target = (self.b_send if k >= 2 else self.b_keep).at[k & 1]
                target = place(target)
                at = k * 2 + part
                if give:
                    yield pltpu.make_async_remote_copy(
                        source, target, self.give_s.at[row, at], self.give_g.at[row, at],
                        device_id=(1 - self.r, self.n, self.w), device_id_type=MESH,
                    )
                else:
                    yield pltpu.make_async_copy(source, target, self.keep_s.at[row, at])

    def start(self, *args):
        for copy in self.copies(*args):
            copy.start()

    def wait_send(self, *args):
        for copy in self.copies(*args):
            copy.wait_send()

    def wait_recv(self, *args):
        for copy in self.copies(*args):
            copy.wait_recv()

    def wait(self, *args):
        for copy in self.copies(*args):
            copy.wait()


def spread_sems(count):
    return [pltpu.SemaphoreType.DMA((count, 8))] * 3


def ffn_kernel(
    x, tops_in, grad_top, p2_all, gain,
    part_out, sum_out, gain_out, o0, o1, o2, o3, ra_out, rb_out,
    theirs, mine, from_pt, from_up, from_dn, s0, s1, s2, s3, s4, s5,
    act, dgu, wide, out_s, give_s, give_g, keep_s, p2, in_s, n_s, n_g,
    tops4, h0, h1, h2, h3, tops_s,
):
    me = spot()
    r, n, w = me
    loads = [pltpu.make_async_copy(p2_all.at[:, j], p2.at[j], in_s.at[j]) for j in range(3)]
    loads.append(pltpu.make_async_copy(tops_in, tops4.at[:, :, 0:64], tops_s))
    for load in loads:
        load.start()
    greet(line_partners(r, n, w, 4) + square_partners(r, n, w))
    scatter = Scatter(
        mine, theirs, (from_pt, from_up, from_dn), (s0, s1, s2, s3, s4, s5), me, 4
    )
    late = pl.ds(64, 64)
    gather = Gather(tops4, (h0, h1, h2, h3), me, 4, late)

    def keep(rows):
        tops4[r, w, pl.ds(64 + rows.start, 16), :] = grad_top[pl.ds(64 + rows.start, 16), :]

    each_rows(64, 16, keep)
    gather.own()
    gain_out[...] = jnp.zeros_like(gain_out)
    loads[0].wait()
    loads[1].wait()

    def hidden_tile(i, carry):
        ft, row = i // 2, i % 2
        rows = pl.ds(pl.multiple_of(row * 512, 512), 512)
        columns = pl.ds(pl.multiple_of(ft * 256, 256), 256)
        left = x[rows, :]
        gate = jnp.dot(left, p2[0, :, :, columns].reshape(2048, 256), preferred_element_type=f32)
        up = jnp.dot(left, p2[1, :, :, columns].reshape(2048, 256), preferred_element_type=f32)
        sig = 1.0 / (1.0 + jnp.exp(-gate))
        silu = gate * sig
        act[rows, columns] = (silu * up).astype(bf16)
        dgu[rows, columns] = (up * (sig * (1.0 + gate * (1.0 - sig)))).astype(bf16)
        later = pl.ds(pl.multiple_of(1024 + ft * 256, 256), 256)
        dgu[rows, later] = silu.astype(bf16)
        return carry

    lax.fori_loop(0, 4, hidden_tile, 0)
    gather.step(1)
    lax.fori_loop(4, 8, hidden_tile, 0)
    gather.step(2)
    loads[2].wait()

    def down_tile(dt, carry):
        nn, half = dt // 2, dt % 2
        columns = pl.ds(pl.multiple_of(dt * 256, 256), 256)
        inner = pl.ds(pl.multiple_of(half * 256, 256), 256)
        other = pl.ds(pl.multiple_of(512 + half * 256, 256), 256)
        right = jnp.concatenate([p2[2, nn, :, inner], p2[2, nn, :, other]], axis=0)
        for row, stage in ((0, theirs), (1, mine)):
            part = jnp.dot(act[row * 512 : row * 512 + 512, :], right, preferred_element_type=f32)
            stage[:, :, columns] = part.astype(bf16).reshape(4, 128, 256)
        return carry

    lax.fori_loop(0, 8, down_tile, 0)
    puts = [
        pltpu.make_async_copy(theirs, part_out.at[0], out_s.at[0]),
        pltpu.make_async_copy(mine, part_out.at[1], out_s.at[1]),
    ]
    for put in puts:
        put.start()
    gather.step(3)
    gather.rest()
    loads[3].wait()

    def top_rows(row):
        return tops4[row].reshape(512, 2048)

    def back_tile(ft, carry):
        columns = pl.ds(pl.multiple_of(ft * 256, 256), 256)
        f_rows = pl.ds(pl.multiple_of((ft % 2) * 256, 256), 256)
        f_cols = pl.ds(pl.multiple_of((ft // 2) * 512, 512), 512)
        later = pl.ds(pl.multiple_of(1024 + ft * 256, 256), 256)
        right = jnp.concatenate([p2[2, nn, f_rows, f_cols] for nn in range(4)], axis=1)
        for row in range(2):
            rows = slice(row * 512, row * 512 + 512)
            dact = contract_last(top_rows(row), right)
            dgu[rows, columns] = (dact * dgu[rows, columns].astype(f32)).astype(bf16)
            dgu[rows, later] = (dact * dgu[rows, later].astype(f32)).astype(bf16)
        return carry

    lax.fori_loop(0, 4, back_tile, 0)
    for put in puts:
        put.wait()

    spread = Spread((o0, o1, o2, o3), (give_s, give_g, keep_s), me)
    columns_here = pl.ds(pl.multiple_of(r * 1024, 1024), 1024)
    slots = {2: 0, 0: 1, 1: 0}

    def moved(which, half):
        def place(target):
            return target.at[which, :, columns_here]

        return wide.at[slots[which], half], which, place, half == 0

    def weights(which, between=None):
        for half in range(2):
            d_first = (jnp.where(half == 0, 1 - r, r)) * 1024

            def weight_tile(i, carry):
                d_cols = pl.ds(pl.multiple_of(d_first + i * 256, 256), 256)
                if which < 2:
                    left = x[:, d_cols]
                    right = dgu[:, which * 1024 : which * 1024 + 1024]
                else:
                    left = tops4[:, :, :, d_cols].reshape(1024, 256)
                    right = act[...]
                wide[slots[which], half, i] = contract_first(left, right).astype(bf16)
                return carry

            lax.fori_loop(0, 4, weight_tile, 0)
            spread.start(*moved(which, half))
            if half == 0 and between is not None:
                between()

    def hop(which, at):
        return (
            push(o0.at[:, which], ra_out.at[at], n_s.at[0, at], n_g.at[0, at], over_x(r, n, w)),
            push(o2.at[:, which], rb_out.at[at], n_s.at[1, at], n_g.at[1, at], over_y(r, n, w)),
        )

    hops = hop(2, 0) + hop(0, 1)
    weights(2)
    for i in range(4):
        s = scatter.order(i)
        rows_t = pl.ds(pl.multiple_of((1 - r) * 512 + s * 128, 128), 128)
        rows_m = pl.ds(pl.multiple_of(r * 512 + s * 128, 128), 128)

        def model_tile(dt, carry):
            nn, half = dt // 2, dt % 2
            columns = pl.ds(pl.multiple_of(dt * 256, 256), 256)
            inner = pl.ds(pl.multiple_of(half * 256, 256), 256)
            left = jnp.concatenate([dgu[rows_t, :], dgu[rows_m, :]], axis=0)
            right = jnp.concatenate([p2[0, nn, inner, :], p2[1, nn, inner, :]], axis=1)
            part = contract_last(left, right)
            seen = jnp.concatenate([x[rows_t, columns], x[rows_m, columns]], axis=0)
            terms = part * seen.astype(f32)
            gain_out[:, columns] += jnp.sum(terms.reshape(32, 8, 256), axis=0)
            part = part.astype(bf16)
            theirs[s, :, columns] = part[0:128]
            mine[s, :, columns] = part[128:256]
            return carry

        lax.fori_loop(0, 8, model_tile, 0)
        scatter.pair(s).start()
        if i < 2:
            which = (2, 0)[i]
            spread.wait_recv(*moved(which, 0))
            spread.wait(*moved(which, 1))
            hops[2 * i].start()
            hops[2 * i + 1].start()
        if i == 0:
            weights(0)
            scatter.advance((0,), ())
        elif i > 1:
            scatter.advance((i - 1,), (i - 2,))

    def scale(rows):
        gain_out[rows, :] = gain_out[rows, :] / gain[...]

    each_rows(8, 8, scale)
    spread.wait_send(*moved(2, 0))
    weights(1, lambda: scatter.advance((3,), (2,)))
    scatter.advance((), (3,))
    scatter.total(sum_out)
    scatter.sent()
    gather.sent()
    spread.wait_send(*moved(0, 0))
    spread.wait_recv(*moved(1, 0))
    spread.wait_send(*moved(1, 0))
    spread.wait(*moved(1, 1))
    for hop in hops:
        hop.wait()


def spread_shapes(*dims):
    return (jax.ShapeDtypeStruct((2,) + dims, bf16),) * 4


def ffn_stage(*args):
    shard, width = 128, 2048
    return comm_call(
        ffn_kernel, "ffn", 4,
        (
            jax.ShapeDtypeStruct((2, 4, shard, width), bf16),
            jax.ShapeDtypeStruct((shard, width), f32),
            jax.ShapeDtypeStruct((8, width), f32),
        )
        + spread_shapes(3, 128, width)
        + (jax.ShapeDtypeStruct((2, 2, 128, width), bf16),) * 2,
        [vmem(), hbm(), vmem(), hbm(), vmem()], [hbm(), vmem(), vmem()] + [hbm()] * 6,
        [pltpu.VMEM((4, shard, width), bf16)] * 2
        + scatter_bufs(shard, width) + scatter_sems()
        + [
            pltpu.VMEM((1024, 1024), bf16),
            pltpu.VMEM((1024, 2048), bf16),
            pltpu.VMEM((2, 2, 4, 256, 1024), bf16),
            pltpu.SemaphoreType.DMA((2,)),
        ]
        + spread_sems(3)
        + [pltpu.VMEM((3, 4, 512, 1024), bf16), pltpu.SemaphoreType.DMA((3,))]
        + [pltpu.SemaphoreType.DMA((2, 2))] * 2
        + gather_scratch(shard, width)
        + [pltpu.SemaphoreType.DMA(())],
        args, flops=4 * 10**10, sent=10**8,
    )


def norm_back(values, gain, grad):
    root = lax.rsqrt(jnp.mean(values * values, axis=-1, keepdims=True) + norm_eps)
    weighted = grad * gain
    inner = jnp.mean(weighted * values, axis=-1, keepdims=True)
    return root * weighted - values * (root * root * root) * inner


def branch_kernel(
    total, mid, grad_top, gain, p1, att, a_in, b_in, a_keep, b_keep, a_came, b_came,
    gmid_out, datt_out, o0, o1, o2, o3, ra_out, rb_out, la_out, lb_out,
    buf, g0, g1, g2, g3, wide, give_s, give_g, keep_s, n_s, n_g, kept, came, in_s,
):
    me = spot()
    r, n, w = me
    greet(line_partners(r, n, w, 4) + square_partners(r, n, w))
    gather = Gather(buf, (g0, g1, g2, g3), me, 4)
    hops = [
        push(a_in.at[:, 1], ra_out, n_s.at[0], n_g.at[0], over_x(r, n, w)),
        push(b_in.at[:, 1], rb_out, n_s.at[1], n_g.at[1], over_y(r, n, w)),
        push(kept.at[0], la_out, n_s.at[2], n_g.at[2], over_y(r, n, w)),
        push(kept.at[1], lb_out, n_s.at[3], n_g.at[3], over_x(r, n, w)),
    ]
    loads = []
    for j, (keep, first) in enumerate(((a_keep, a_came), (b_keep, b_came))):
        loads += [
            pltpu.make_async_copy(keep.at[1, 2], kept.at[j], in_s.at[j, 0]),
            pltpu.make_async_copy(first.at[0, 1], came.at[j], in_s.at[j, 1]),
        ]
    for load in loads:
        load.start()
    hops[0].start()
    hops[1].start()

    def body(rows):
        grad = norm_back(mid[rows, :], gain[...], total[rows, :]) + grad_top[rows, :].astype(f32)
        gmid_out[rows, :] = grad
        buf[r, w, rows, :] = grad.astype(bf16)

    each_rows(mid.shape[0], 16, body)
    gather.own()
    for load in loads:
        load.wait()
    for j in range(2):
        def join(rows):
            kept[j, rows, :] = (kept[j, rows, :].astype(f32) + came[j, rows, :].astype(f32)).astype(bf16)

        each_rows(128, 16, join)
        hops[2 + j].start()
    for k in (1, 2, 3):
        gather.step(k)
    gather.rest()
    for row in range(2):
        for pair in range(2):
            left = jnp.concatenate([buf[row, 2 * pair], buf[row, 2 * pair + 1]], axis=0)
            right = jnp.concatenate(
                [out_block(p1, nn, half) for nn in range(4) for half in range(2)], axis=1
            )
            datt_out[row, pair * 256 : pair * 256 + 256, :] = contract_last(left, right).astype(bf16)

    spread = Spread((o0, o1, o2, o3), (give_s, give_g, keep_s), me)

    def moved(half):
        def place(target):
            return target.at[:, pl.ds(pl.multiple_of(r * 256, 256), 256)]

        return wide.at[half], 0, place, half == 0

    for half in range(2):
        d_first = (jnp.where(half == 0, 1 - r, r)) * 1024

        def weight_tile(i, carry):
            columns = pl.ds(pl.multiple_of(d_first + i * 256, 256), 256)
            left = buf[:, :, :, columns].reshape(1024, 256)
            wide[half, i] = contract_first(left, att[...]).astype(bf16)
            return carry

        lax.fori_loop(0, 4, weight_tile, 0)
        spread.start(*moved(half))
    gather.sent()
    spread.wait(*moved(0))
    spread.wait(*moved(1))
    for hop in hops:
        hop.wait()


def branch_stage(*args):
    shard, width = 128, 2048
    return comm_call(
        branch_kernel, "branch", 5,
        (
            jax.ShapeDtypeStruct((shard, width), f32),
            jax.ShapeDtypeStruct((2, 512, 256), bf16),
        )
        + spread_shapes(128, 512)
        + (jax.ShapeDtypeStruct((2, 128, width), bf16),) * 2
        + (jax.ShapeDtypeStruct((128, width), bf16),) * 2,
        [vmem()] * 6 + [hbm()] * 6, [vmem(), vmem()] + [hbm()] * 8,
        gather_scratch(shard, width)
        + [pltpu.VMEM((2, 4, 256, 256), bf16)]
        + spread_sems(1)
        + [pltpu.SemaphoreType.DMA((4,))] * 2
        + [pltpu.VMEM((2, 128, width), bf16)] * 2
        + [pltpu.SemaphoreType.DMA((2, 2))],
        args, flops=10**10, sent=10**8,
    )


def unproject_kernel(
    dq, dkv, x, p1, tabs, gain, parts, mid, a_keep, b_keep, a_gate, b_gate, a_up, b_up, oa_in, ob_in,
    part_out, gain_out, o0, o1, o2, o3, hid_out, ra_out, rb_out, roa_out, rob_out,
    send, recv, both, wide_q, wide_kv, s_s, s_g, give_s, give_g, keep_s,
    mine, from_pt, from_up, from_dn, s0, s1, s2, s3, s4, s5,
    kept, came, acc, in_s, n_s, n_g, m_s,
):
    me = spot()
    r, n, w = me
    loads = []
    for j, (keep, gate, up) in enumerate(((a_keep, a_gate, a_up), (b_keep, b_gate, b_up))):
        loads += [
            pltpu.make_async_copy(keep.at[1, 0:2], kept.at[j], in_s.at[j, 0]),
            pltpu.make_async_copy(gate.at[1, 1], came.at[j, 0], in_s.at[j, 1]),
            pltpu.make_async_copy(up.at[1], came.at[j, 1], in_s.at[j, 2]),
        ]
    loads.append(pltpu.make_async_copy(parts.at[r], mine, m_s))
    for load in loads:
        load.start()
    greet(
        line_partners(r, n, w, 4)
        + [
            (n >= 1, nar_device(r, n, w, -1)),
            (n >= 2, nar_device(r, n, w, -2)),
            (n <= 2, nar_device(r, n, w, 1)),
            (n <= 1, nar_device(r, n, w, 2)),
        ]
        + square_partners(r, n, w)
    )
    scatter = Scatter(
        mine, parts.at[1 - r], (from_pt, from_up, from_dn), (s0, s1, s2, s3, s4, s5), me, 4
    )
    hops = [
        push(kept.at[0], ra_out, n_s.at[0], n_g.at[0], over_y(r, n, w)),
        push(kept.at[1], rb_out, n_s.at[1], n_g.at[1], over_x(r, n, w)),
        push(oa_in, roa_out, n_s.at[2], n_g.at[2], over_x(r, n, w)),
        push(ob_in, rob_out, n_s.at[3], n_g.at[3], over_y(r, n, w)),
    ]

    def copy(row, slot, by):
        return pltpu.make_async_remote_copy(
            send.at[row, slot], recv.at[row, slot], s_s.at[row, slot], s_g.at[row, slot],
            device_id=nar_device(r, n, w, by), device_id_type=MESH,
        )

    for row in range(2):
        for slot, by in ((1, -1), (0, -2)):
            @pl.when(n >= -by)
            def _():
                send[row, slot] = dkv[row, slot].astype(bf16)
                copy(row, slot, by).start()

    for i in range(4):
        scatter.pair(scatter.order(i)).start()
    for load in loads:
        load.wait()
    for j in range(2):
        for which in range(2):
            def join(rows):
                total = kept[j, which, rows, :].astype(f32) + came[j, which, rows, :].astype(f32)
                kept[j, which, rows, :] = total.astype(bf16)

            each_rows(128, 16, join)
        hops[j].start()
    hops[2].start()
    hops[3].start()
    scatter.advance((0, 1, 2, 3), ())

    spread = Spread((o0, o1, o2, o3), (give_s, give_g, keep_s), (r, n, w))

    def moved_q(half):
        def place(target):
            return target.at[:, pl.ds(pl.multiple_of(r * 256, 256), 256)]

        return wide_q.at[half], 0, place, half == 0

    def moved_kv(half):
        def place(target):
            return target.at[:, pl.ds(pl.multiple_of(512 + r * 128, 128), 128)]

        return wide_kv.at[half], 1, place, half == 0

    for row in range(2):
        both[row * 512 : row * 512 + 512, 0:256] = dq[row]

    def weight(half, columns, wide):
        d_first = (jnp.where(half == 0, 1 - r, r)) * 1024

        def tile(i, carry):
            d_cols = pl.ds(pl.multiple_of(d_first + i * 256, 256), 256)
            wide[half, i] = contract_first(x[:, d_cols], both[:, columns]).astype(bf16)
            return carry

        lax.fori_loop(0, 4, tile, 0)

    for half in range(2):
        weight(half, slice(0, 256), wide_q)
        spread.start(*moved_q(half))
    scatter.advance((), (0,))
    lane = lax.broadcasted_iota(jnp.int32, (128, 128), 1)
    for row in range(2):
        for slot, by in ((1, -1), (0, -2)):
            @pl.when(n <= 3 + by)
            def _():
                copy(row, slot, by).wait_recv()

        def tile(i, carry):
            rows = pl.ds(pl.multiple_of(i * 128, 128), 128)
            total = dkv[row, 2, rows, :]
            zero = jnp.zeros_like(total)
            total = total + jnp.where(n <= 2, recv[row, 1, rows, :].astype(f32), zero)
            total = total + jnp.where(n <= 1, recv[row, 0, rows, :].astype(f32), zero)
            turned = turn(total, tabs[row, rows, 0:128], -tabs[row, rows, 128:256])
            both[pl.ds(pl.multiple_of(row * 512 + i * 128, 128), 128), 256:384] = jnp.where(
                lane < 64, turned, total
            ).astype(bf16)
            return carry

        lax.fori_loop(0, 4, tile, 0)
    for half in range(2):
        weight(half, slice(256, 384), wide_kv)
        spread.start(*moved_kv(half))
    scatter.advance((), (1,))
    gain_out[...] = jnp.zeros_like(gain_out)

    def model_tile(dt, carry):
        nn, half = dt // 2, dt % 2
        columns = pl.ds(pl.multiple_of(dt * 256, 256), 256)
        inner = pl.ds(pl.multiple_of(half * 256, 256), 256)
        right = p1[nn, inner, 0:384]
        for row in range(2):
            for block in range(2):
                first = row * 512 + block * 256
                part = contract_last(both[first : first + 256, :], right)
                terms = part * x[first : first + 256, columns].astype(f32)
                gain_out[:, columns] += jnp.sum(terms.reshape(32, 8, 256), axis=0)
                part_out[row, 2 * block, :, columns] = part[0:128].astype(bf16)
                part_out[row, 2 * block + 1, :, columns] = part[128:256].astype(bf16)
        return carry

    lax.fori_loop(0, 8, model_tile, 0)
    gain_out[...] = gain_out[...] / gain[...]
    scatter.advance((), (2, 3))
    scatter.total(acc)

    def last(rows):
        hid_out[rows, :] = (acc[rows, :] + mid[rows, :]).astype(bf16)

    each_rows(128, 16, last)
    scatter.sent()
    for row in range(2):
        for slot, by in ((1, -1), (0, -2)):
            @pl.when(n >= -by)
            def _():
                copy(row, slot, by).wait_send()

    for half in range(2):
        spread.wait(*moved_q(half))
        spread.wait(*moved_kv(half))
    for hop in hops:
        hop.wait()


def unproject(*args):
    return comm_call(
        unproject_kernel, "unproject", 6,
        (
            jax.ShapeDtypeStruct((2, 4, 128, 2048), bf16),
            jax.ShapeDtypeStruct((8, 2048), f32),
        )
        + spread_shapes(128, 768)
        + (jax.ShapeDtypeStruct((128, 2048), bf16),)
        + (jax.ShapeDtypeStruct((2, 128, 2048), bf16),) * 2
        + (jax.ShapeDtypeStruct((2, 128, 512), bf16),) * 2,
        [vmem()] * 6 + [hbm(), vmem()] + [hbm()] * 8,
        [vmem(), vmem()] + [hbm()] * 4 + [vmem()] + [hbm()] * 4,
        [
            pltpu.VMEM((2, 2, 512, 128), bf16),
            pltpu.VMEM((2, 2, 512, 128), bf16),
            pltpu.VMEM((1024, 384), bf16),
            pltpu.VMEM((2, 4, 256, 256), bf16),
            pltpu.VMEM((2, 4, 256, 128), bf16),
            pltpu.SemaphoreType.DMA((2, 2)),
            pltpu.SemaphoreType.DMA((2, 2)),
        ]
        + spread_sems(2)
        + [pltpu.VMEM((4, 128, 2048), bf16)]
        + scatter_bufs(128, 2048) + scatter_sems()
        + [
            pltpu.VMEM((2, 2, 128, 2048), bf16),
            pltpu.VMEM((2, 2, 128, 2048), bf16),
            pltpu.VMEM((128, 2048), f32),
            pltpu.SemaphoreType.DMA((2, 3)),
            pltpu.SemaphoreType.DMA((4,)),
            pltpu.SemaphoreType.DMA((4,)),
            pltpu.SemaphoreType.DMA(()),
        ],
        args, flops=10**10, sent=10**7,
    )


def leave_kernel(
    parts, hidden, gain, gmid, gains, qa_send, qa_keep, qb_send, qb_keep, oa_keep, ob_keep, oa_in, ob_in,
    grad_out, ga_out, query_out, key_out, value_out, output_out,
    mine, from_pt, from_up, from_dn, s0, s1, s2, s3, s4, s5,
    acc, over_wid, summed, over_rest, w_s, w_g, t_s, t_g,
    first_q, next_q, then_q, next_o, then_o, kv, n_s, n_g, k_s, k_g,
):
    me = spot()
    r, n, w = me
    partners = [(w != j, (r, n, jnp.int32(j))) for j in range(4)]
    partners += [
        ((r != a) | (n != b), (jnp.int32(a), jnp.int32(b), w)) for a in range(2) for b in range(4)
    ]
    greet(partners)
    x_side, y_side = over_x(r, n, w), over_y(r, n, w)
    q_hops = [
        push(qa_send, first_q.at[0], n_s.at[0], n_g.at[0], x_side),
        push(qb_send, first_q.at[1], n_s.at[1], n_g.at[1], y_side),
    ]
    q_later = [
        push(next_q.at[0], then_q.at[0], n_s.at[2], n_g.at[2], y_side),
        push(next_q.at[1], then_q.at[1], n_s.at[3], n_g.at[3], x_side),
    ]
    o_hops = [
        push(next_o.at[0], then_o.at[0], n_s.at[4], n_g.at[4], y_side),
        push(next_o.at[1], then_o.at[1], n_s.at[5], n_g.at[5], x_side),
    ]
    for hop in q_hops:
        hop.start()
    scatter = Scatter(
        mine, parts.at[1 - r], (from_pt, from_up, from_dn), (s0, s1, s2, s3, s4, s5), me, 4
    )
    for i in range(4):
        scatter.pair(scatter.order(i)).start()

    def wid_copy(j, slot):
        return pltpu.make_async_remote_copy(
            gains, over_wid.at[slot], w_s.at[j], w_g.at[slot],
            device_id=(r, n, jnp.int32(j)), device_id_type=MESH,
        )

    def rest_copy(a, b, slot):
        return pltpu.make_async_remote_copy(
            summed, over_rest.at[slot], t_s.at[a * 4 + b], t_g.at[slot],
            device_id=(jnp.int32(a), jnp.int32(b), w), device_id_type=MESH,
        )

    for j in range(4):
        @pl.when(w != j)
        def _():
            wid_copy(j, w).start()

    for s in range(4):
        def fill(rows):
            mine[s, rows, :] = parts[r, s, rows, :]

        each_rows(128, 16, fill)
    scatter.advance((0, 1, 2, 3), ())
    for j, (keep, came) in enumerate(((oa_keep, oa_in), (ob_keep, ob_in))):
        next_o[j] = (keep[1].astype(f32) + came[1].astype(f32)).astype(bf16)
        o_hops[j].start()
    summed[...] = gains[...]
    for j in range(4):
        @pl.when(w != j)
        def _():
            wid_copy(j, j).wait_recv()
            summed[...] += over_wid[j]

    for a in range(2):
        for b in range(4):
            @pl.when((r != a) | (n != b))
            def _():
                rest_copy(a, b, r * 4 + n).start()

    for j, keep in enumerate((qa_keep, qb_keep)):
        q_hops[j].wait_recv()
        next_q[j] = (keep[1].astype(f32) + first_q[j, 1].astype(f32)).astype(bf16)
        q_later[j].start()
    scatter.advance((), (0, 1))
    for j, keep in enumerate((qa_keep, qb_keep)):
        q_later[j].wait_recv()
        total = keep[0].astype(f32) + first_q[j, 0].astype(f32) + then_q[j].astype(f32)
        query_out[j * 128 : j * 128 + 128, :] = total[:, 0:512]
        kv[w, j * 128 : j * 128 + 128, :] = total[:, 512:768].astype(bf16)

    def kv_copy(j, slot):
        return pltpu.make_async_remote_copy(
            kv.at[w], kv.at[w], k_s.at[j], k_g.at[slot],
            device_id=(r, n, jnp.int32(j)), device_id_type=MESH,
        )

    def kv_wait(j):
        return pltpu.make_async_remote_copy(
            kv.at[j], kv.at[j], k_s.at[j], k_g.at[j],
            device_id=(r, n, jnp.int32(j)), device_id_type=MESH,
        )

    for j in range(4):
        @pl.when(w != j)
        def _():
            kv_copy(j, w).start()

    scatter.advance((), (2, 3))
    for j, (keep, came) in enumerate(((oa_keep, oa_in), (ob_keep, ob_in))):
        o_hops[j].wait_recv()
        output_out[j * 128 : j * 128 + 128, :] = (
            keep[0].astype(f32) + came[0].astype(f32) + then_o[j].astype(f32)
        )
    mine_block = r * 4 + n
    ga_out[0:1] = summed[pl.ds(mine_block, 1), :]
    ga_out[1:2] = summed[pl.ds(mine_block + 8, 1), :]
    for a in range(2):
        for b in range(4):
            @pl.when((r != a) | (n != b))
            def _():
                slot = a * 4 + b
                rest_copy(a, b, slot).wait_recv()
                ga_out[0:1] += over_rest[slot, pl.ds(mine_block, 1), :]
                ga_out[1:2] += over_rest[slot, pl.ds(mine_block + 8, 1), :]

    scatter.total(acc)

    def last(rows):
        grad = norm_back(hidden[rows, :].astype(f32), gain[...], acc[rows, :])
        grad_out[rows, :] = (grad + gmid[rows, :]).astype(bf16)

    each_rows(hidden.shape[0], 16, last)
    lane = lax.broadcasted_iota(jnp.int32, (256, 128), 1)
    for j in range(4):
        @pl.when(w != j)
        def _():
            kv_wait(j).wait_recv()

        even, odd = kv[j, :, 0:128].astype(f32), kv[j, :, 128:256].astype(f32)
        here = slice(j * 128, j * 128 + 128)
        key_out[:, here] = jnp.where(lane < 64, even, pltpu.roll(odd, 64, 1))
        value_out[:, here] = jnp.where(lane < 64, pltpu.roll(even, 64, 1), odd)
    scatter.sent()
    for hop in q_hops + q_later + o_hops:
        hop.wait_send()
    for j in range(4):
        @pl.when(w != j)
        def _():
            kv_copy(j, w).wait_send()

    for j in range(4):
        @pl.when(w != j)
        def _():
            wid_copy(j, w).wait_send()

    for a in range(2):
        for b in range(4):
            @pl.when((r != a) | (n != b))
            def _():
                rest_copy(a, b, r * 4 + n).wait_send()


def leave(*args):
    shard, width = 128, 2048
    grad = jax.ShapeDtypeStruct((256, 512), f32)
    return comm_call(
        leave_kernel, "leave", 7,
        (jax.ShapeDtypeStruct((shard, width), bf16), jax.ShapeDtypeStruct((8, 256), f32))
        + (grad,) * 4,
        [vmem()] * 13, [vmem()] * 6,
        [pltpu.VMEM((4, shard, width), bf16)]
        + scatter_bufs(shard, width) + scatter_sems()
        + [
            pltpu.VMEM((shard, width), f32),
            pltpu.VMEM((4, 16, 256), f32),
            pltpu.VMEM((16, 256), f32),
            pltpu.VMEM((8, 16, 256), f32),
            pltpu.SemaphoreType.DMA((4,)),
            pltpu.SemaphoreType.DMA((4,)),
            pltpu.SemaphoreType.DMA((8,)),
            pltpu.SemaphoreType.DMA((8,)),
            pltpu.VMEM((2, 2, 128, 768), bf16),
            pltpu.VMEM((2, 128, 768), bf16),
            pltpu.VMEM((2, 128, 768), bf16),
            pltpu.VMEM((2, 128, 512), bf16),
            pltpu.VMEM((2, 128, 512), bf16),
            pltpu.VMEM((4, 256, 256), bf16),
            pltpu.SemaphoreType.DMA((6,)),
            pltpu.SemaphoreType.DMA((6,)),
            pltpu.SemaphoreType.DMA((4,)),
            pltpu.SemaphoreType.DMA((4,)),
        ],
        args, flops=10**10, sent=10**8,
    )


def local_fast(
    hidden_in, doc_lengths, w_query, w_key, w_value, w_output, w_gate, w_up, w_down,
    gain_attn, gain_ffn, grad_out,
):
    r, n, w = spot()
    hidden, grad_top = hidden_in[0], grad_out[0]
    gain_a, gain_f = gain_attn[None], gain_ffn[None]
    def half(weight, axis):
        size = weight.shape[axis] // 2
        return lax.dynamic_slice_in_dim(weight, r * size, size, axis)

    head = (w * 2 + r) * HD
    kv_pack = jnp.concatenate(
        [lax.dynamic_slice_in_dim(w_key, head, HD, 1), lax.dynamic_slice_in_dim(w_value, head, HD, 1)],
        axis=1,
    )
    out_half = half(w_output, 0)
    p1_shard = jnp.concatenate(
        [half(w_query, 1), kv_pack, jnp.concatenate([out_half[:, :256], out_half[:, 256:]], axis=0)],
        axis=1,
    )
    down_half = half(w_down, 0)
    p2_shard = jnp.stack(
        [
            half(w_gate, 1),
            half(w_up, 1),
            jnp.concatenate([down_half[:512], down_half[512:]], axis=1),
        ]
    )
    p1 = lax.all_gather(p1_shard, "nar", axis=0)
    p2 = lax.all_gather(p2_shard, "nar", axis=0)

    token_ids = n * 512 + jnp.arange(512, dtype=jnp.int32)
    doc_start, places = doc_layout(doc_lengths[0], token_ids)
    angles = places.astype(f32)[:, None] * inverse_freq()[None, :]
    cosine, sine = jnp.cos(angles), jnp.sin(angles)
    start_here = (doc_start - (n - 2) * 512).astype(f32)
    tab = jnp.concatenate(
        [cosine] * 4 + [-sine, sine] * 2 + [jnp.broadcast_to(start_here[:, None], (512, 128))],
        axis=1,
    )

    rows, tabs = enter(hidden, gain_a, tab)
    rows3, rows2 = rows.reshape(2, 512, 2048), rows.reshape(1024, 2048)
    q, kv, tops = project(rows3, p1, tabs, grad_top)
    low = tabs[:, ::QUERIES, 256].astype(jnp.int32).reshape(8)
    kv_flat = kv.reshape(2, 1536, 128)
    att, lse = attend(low, q, kv_flat, tabs)
    mid, ffn_rows = middle_stage(att, p1, hidden, gain_f)
    parts, total, gain_f_part, a_send, a_keep, b_send, b_keep, ra_dg, rb_dg = ffn_stage(
        ffn_rows.reshape(1024, 2048), tops, grad_top, p2, gain_f
    )
    gmid, datt, oa_send, oa_keep, ob_send, ob_keep, ra_u, rb_u, la_d, lb_d = branch_stage(
        total, mid, grad_top, gain_f, p1, att.reshape(1024, 256),
        a_send, b_send, a_keep, b_keep, ra_dg, rb_dg,
    )
    dq, dkv = attend_back(low, q, kv_flat, tabs, att, datt, lse)
    (
        dparts, gain_a_part, qa_send, qa_keep, qb_send, qb_keep,
        hidden_out, ra_last, rb_last, oa_came, ob_came,
    ) = unproject(
        dq, dkv.reshape(2, 3, 512, 128), rows2, p1, tabs, gain_a, parts, mid,
        a_keep, b_keep, ra_dg, rb_dg, ra_u, rb_u, oa_send, ob_send,
    )
    gains = jnp.concatenate(
        [gain_f_part.sum(axis=0).reshape(8, 256), gain_a_part.sum(axis=0).reshape(8, 256)], axis=0
    )
    grad_in, gain_sums, grad_query, grad_key, grad_value, output_sum = leave(
        dparts, hidden, gain_a, gmid, gains,
        qa_send, qa_keep, qb_send, qb_keep, oa_keep, ob_keep, oa_came, ob_came,
    )

    def joined(which):
        def half_rows(keep, came, last):
            return keep[0, which].astype(f32) + came.astype(f32) + last.astype(f32)

        a_came, b_came, a_last, b_last = (
            (ra_dg[1, 0], rb_dg[1, 0], ra_last[0], rb_last[0]),
            (ra_u[0], rb_u[0], ra_last[1], rb_last[1]),
            (ra_dg[0, 0], rb_dg[0, 0], la_d, lb_d),
        )[which]
        return jnp.concatenate(
            [half_rows(a_keep, a_came, a_last), half_rows(b_keep, b_came, b_last)], axis=0
        )

    return (
        hidden_out[None],
        grad_in[None],
        grad_query,
        grad_key,
        grad_value,
        output_sum.T,
        joined(0),
        joined(1),
        joined(2).T,
        gain_sums[1],
        gain_sums[0],
    )


def solution(mesh):
    in_specs = (
        P("row", ("nar", "wid"), None),
        P("row", None),
        P("nar", "wid"),
        P("nar", None),
        P("nar", None),
        P("wid", "nar"),
        P("nar", "wid"),
        P("nar", "wid"),
        P("wid", "nar"),
        P(),
        P(),
        P("row", ("nar", "wid"), None),
    )
    out_specs = (
        P("row", ("nar", "wid"), None),
        P("row", ("nar", "wid"), None),
        P(("row", "nar"), "wid"),
        P(("row", "nar"), None),
        P(("row", "nar"), None),
        P("wid", ("row", "nar")),
        P(("row", "nar"), "wid"),
        P(("row", "nar"), "wid"),
        P("wid", ("row", "nar")),
        P(("row", "nar")),
        P(("row", "nar")),
    )
    sizes = dict(mesh.shape)
    fits = sizes == {"row": 2, "nar": 4, "wid": 4}

    def body(*args):
        small = args[0].shape == (1, 128, 2048)
        return (local_fast if fits and small else local)(*args)

    return jax.shard_map(body, mesh=mesh, in_specs=in_specs, out_specs=out_specs, check_vma=False)
```

```python
import math

import jax
import jax.numpy as jnp
from jax import lax
from jax.experimental import pallas as pl
from jax.experimental.pallas import tpu as pltpu
from jax.sharding import PartitionSpec as P

H = 32
KV = 8
HD = 64


norm_eps = 1e-05
masked_score = -1e30


def inverse_freq():
    listed = []
    for pair_index in range(HD // 2):
        base_freq = 500000.0 ** (-2.0 * pair_index / HD)
        wavelength = 2.0 * math.pi / base_freq
        smoothing = (8192.0 / wavelength - 1.0) / 3.0
        blended = (1.0 - smoothing) * base_freq / 32.0 + smoothing * base_freq
        if wavelength < 2048.0:
            listed.append(base_freq)
        elif wavelength > 8192.0:
            listed.append(base_freq / 32.0)
        else:
            listed.append(blended)
    return jnp.asarray(listed, dtype=jnp.float32)


def rotate(values, cosine_table, sine_table):
    half_dim = HD // 2
    first_half = values[..., :half_dim]
    second_half = values[..., half_dim:]
    return jnp.concatenate(
        [
            first_half * cosine_table - second_half * sine_table,
            second_half * cosine_table + first_half * sine_table,
        ],
        axis=-1,
    )


def rotate_back(grads_in, cosine_table, sine_table):
    half_dim = HD // 2
    first_half = grads_in[..., :half_dim]
    second_half = grads_in[..., half_dim:]
    return jnp.concatenate(
        [
            first_half * cosine_table + second_half * sine_table,
            second_half * cosine_table - first_half * sine_table,
        ],
        axis=-1,
    )


def doc_layout(lengths_row, token_ids):
    ends_at = jnp.cumsum(lengths_row, dtype=jnp.int32)
    starts_at = ends_at - lengths_row
    inside = (token_ids[:, None] >= starts_at[None, :]) & (token_ids[:, None] < ends_at[None, :])
    doc_start = jnp.sum(jnp.where(inside, starts_at[None, :], 0), axis=1, dtype=jnp.int32)
    return (doc_start, token_ids - doc_start)


def norm_forward(values, gain_vector):
    root_inv = lax.rsqrt(jnp.mean(values * values, axis=-1, keepdims=True) + norm_eps)
    return (root_inv, (values * root_inv * gain_vector).astype(jnp.bfloat16))


def norm_backward(values, root_inv, gain_vector, grad_normed):
    weighted = grad_normed * gain_vector
    inner_sum = jnp.mean(weighted * values, axis=-1, keepdims=True)
    grad_values = root_inv * weighted - values * (root_inv * root_inv * root_inv) * inner_sum
    gain_term = jnp.sum(grad_normed * values * root_inv, axis=0)
    return (grad_values, gain_term)


def contract_last(left_side, right_side):
    return lax.dot_general(
        left_side, right_side, (((1,), (1,)), ((), ())), preferred_element_type=jnp.float32
    )


def contract_first(left_side, right_side):
    return lax.dot_general(
        left_side, right_side, (((0,), (0,)), ((), ())), preferred_element_type=jnp.float32
    )


def local(
    hidden_in,
    doc_lengths,
    w_query,
    w_key,
    w_value,
    w_output,
    w_gate,
    w_up,
    w_down,
    gain_attn,
    gain_ffn,
    grad_out,
):
    wid_count = lax.axis_size("wid")
    nar_count = lax.axis_size("nar")
    wid_index = lax.axis_index("wid")
    nar_index = lax.axis_index("nar")
    local_tokens = hidden_in.shape[1]
    block_tokens = local_tokens * wid_count
    seq_length = block_tokens * nar_count
    query_heads = w_query.shape[1] // HD
    group_size = H // KV
    kv_local = max(query_heads // group_size, 1)
    heads_per_kv = query_heads // kv_local
    kv_first = wid_index * query_heads // group_size
    query_block = min(512, block_tokens)
    block_count = block_tokens // query_block
    item_count = block_count * query_heads
    attn_scale = HD ** (-0.5)
    query_full, key_full, value_full, output_full, gate_full, up_full, down_full = (
        lax.all_gather(w_query, "nar", axis=0, tiled=True),
        lax.all_gather(w_key, "nar", axis=0, tiled=True),
        lax.all_gather(w_value, "nar", axis=0, tiled=True),
        lax.all_gather(w_output, "nar", axis=1, tiled=True),
        lax.all_gather(w_gate, "nar", axis=0, tiled=True),
        lax.all_gather(w_up, "nar", axis=0, tiled=True),
        lax.all_gather(w_down, "nar", axis=1, tiled=True),
    )
    key_local = lax.dynamic_slice_in_dim(key_full, kv_first * HD, kv_local * HD, 1)
    value_local = lax.dynamic_slice_in_dim(value_full, kv_first * HD, kv_local * HD, 1)
    token_ids = nar_index * block_tokens + jnp.arange(block_tokens, dtype=jnp.int32)
    doc_start, places = doc_layout(doc_lengths[0], token_ids)
    angles = places.astype(jnp.float32)[:, None] * inverse_freq()[None, :]
    cosine_table = jnp.cos(angles)[:, None, :]
    sine_table = jnp.sin(angles)[:, None, :]
    key_ids = jnp.arange(seq_length, dtype=jnp.int32)
    residual = hidden_in[0].astype(jnp.float32)
    root_attn, normed_attn = norm_forward(residual, gain_attn)
    normed_rows = lax.all_gather(normed_attn, "wid", axis=0, tiled=True)
    query_pre = jnp.dot(normed_rows, query_full, preferred_element_type=jnp.float32)
    key_pre = jnp.dot(normed_rows, key_local, preferred_element_type=jnp.float32)
    value_rows = jnp.dot(normed_rows, value_local, preferred_element_type=jnp.float32).astype(
        jnp.bfloat16
    )
    query_rot = (
        rotate(query_pre.reshape(block_tokens, query_heads, HD), cosine_table, sine_table)
        .astype(jnp.bfloat16)
        .reshape(block_tokens, query_heads * HD)
    )
    key_rot = (
        rotate(key_pre.reshape(block_tokens, kv_local, HD), cosine_table, sine_table)
        .astype(jnp.bfloat16)
        .reshape(block_tokens, kv_local * HD)
    )
    key_seq, value_seq = (
        lax.all_gather(key_rot, "nar", axis=0, tiled=True),
        lax.all_gather(value_rows, "nar", axis=0, tiled=True),
    )

    def item_inputs(item_index):
        block_index = item_index // query_heads
        head_index = item_index % query_heads
        kv_index = head_index // heads_per_kv
        row_first = block_index * query_block
        query_part = lax.dynamic_slice(query_rot, (row_first, head_index * HD), (query_block, HD))
        key_head = lax.dynamic_slice_in_dim(key_seq, kv_index * HD, HD, 1)
        value_head = lax.dynamic_slice_in_dim(value_seq, kv_index * HD, HD, 1)
        query_ids = lax.dynamic_slice_in_dim(token_ids, row_first, query_block, 0)
        query_starts = lax.dynamic_slice_in_dim(doc_start, row_first, query_block, 0)
        allowed = (key_ids[None, :] <= query_ids[:, None]) & (
            key_ids[None, :] >= query_starts[:, None]
        )
        scores = contract_last(query_part, key_head) * attn_scale
        return (
            row_first,
            head_index,
            kv_index,
            query_part,
            key_head,
            value_head,
            jnp.where(allowed, scores, masked_score),
        )

    def attend(item_index):
        row_first, head_index, kv_index, query_part, key_head, value_head, scores = item_inputs(
            item_index
        )
        row_max = jnp.max(scores, axis=1, keepdims=True)
        exp_scores = jnp.exp(scores - row_max)
        row_total = jnp.sum(exp_scores, axis=1, keepdims=True)
        probability = (exp_scores / row_total).astype(jnp.bfloat16)
        attended = jnp.dot(probability, value_head, preferred_element_type=jnp.float32)
        return (attended, (row_max + jnp.log(row_total))[:, 0])

    attended_items, logsum_items = lax.map(attend, jnp.arange(item_count, dtype=jnp.int32))
    attended_rows = (
        attended_items.reshape(block_count, query_heads, query_block, HD)
        .transpose(0, 2, 1, 3)
        .reshape(block_tokens, query_heads * HD)
        .astype(jnp.bfloat16)
    )
    rows_here = attended_rows
    branch_attn = lax.psum_scatter(
        jnp.dot(rows_here, output_full, preferred_element_type=jnp.float32),
        "wid",
        scatter_dimension=0,
        tiled=True,
    )
    middle = residual + branch_attn
    root_ffn, normed_ffn = norm_forward(middle, gain_ffn)
    ffn_rows = lax.all_gather(normed_ffn, "wid", axis=0, tiled=True)
    gate_proj = jnp.dot(ffn_rows, gate_full, preferred_element_type=jnp.float32)
    up_proj = jnp.dot(ffn_rows, up_full, preferred_element_type=jnp.float32)
    gate_sigmoid = jax.nn.sigmoid(gate_proj)
    gate_silu = gate_proj * gate_sigmoid
    activated = (gate_silu * up_proj).astype(jnp.bfloat16)
    rows_here = activated
    branch_ffn = lax.psum_scatter(
        jnp.dot(rows_here, down_full, preferred_element_type=jnp.float32).astype(jnp.bfloat16),
        "wid",
        scatter_dimension=0,
        tiled=True,
    ).astype(jnp.float32)
    hidden_out = (middle + branch_ffn).astype(jnp.bfloat16)[None]
    grad_top = grad_out[0]
    grad_rows = lax.all_gather(grad_top, "wid", axis=0, tiled=True)
    grad_activated = contract_last(grad_rows, down_full)
    down_weight_grad = contract_first(activated, grad_rows)
    silu_slope = gate_sigmoid * (1.0 + gate_proj * (1.0 - gate_sigmoid))
    grad_gate_b = (grad_activated * up_proj * silu_slope).astype(jnp.bfloat16)
    grad_up_b = (grad_activated * gate_silu).astype(jnp.bfloat16)
    gate_weight_grad = contract_first(ffn_rows, grad_gate_b)
    up_weight_grad = contract_first(ffn_rows, grad_up_b)
    grad_normed_ffn = lax.psum_scatter(
        contract_last(grad_gate_b, gate_full) + contract_last(grad_up_b, up_full),
        "wid",
        scatter_dimension=0,
        tiled=True,
    )
    grad_middle, gain_ffn_term = norm_backward(middle, root_ffn, gain_ffn, grad_normed_ffn)
    grad_middle = grad_middle + grad_top.astype(jnp.float32)
    grad_branch = grad_middle.astype(jnp.bfloat16)
    branch_rows = lax.all_gather(grad_branch, "wid", axis=0, tiled=True)
    grad_attended = contract_last(branch_rows, output_full).astype(jnp.bfloat16)
    output_weight_grad = contract_first(attended_rows, branch_rows)

    def attend_back(carried, item_index):
        key_grad, value_grad = carried
        row_first, head_index, kv_index, query_part, key_head, value_head, scores = item_inputs(
            item_index
        )
        logsum = lax.dynamic_index_in_dim(logsum_items, item_index, 0, keepdims=False)
        probability = jnp.exp(scores - logsum[:, None])
        grad_part = lax.dynamic_slice(
            grad_attended, (row_first, head_index * HD), (query_block, HD)
        )
        grad_prob = contract_last(grad_part, value_head)
        inner_sum = jnp.sum(probability * grad_prob, axis=1, keepdims=True)
        grad_scores = (probability * (grad_prob - inner_sum)).astype(jnp.bfloat16)
        query_grad = jnp.dot(grad_scores, key_head, preferred_element_type=jnp.float32) * attn_scale
        key_part = contract_first(grad_scores, query_part) * attn_scale
        value_part = contract_first(probability.astype(jnp.bfloat16), grad_part)
        key_old = lax.dynamic_slice_in_dim(key_grad, kv_index * HD, HD, 1)
        key_grad = lax.dynamic_update_slice_in_dim(key_grad, key_old + key_part, kv_index * HD, 1)
        value_old = lax.dynamic_slice_in_dim(value_grad, kv_index * HD, HD, 1)
        value_grad = lax.dynamic_update_slice_in_dim(
            value_grad, value_old + value_part, kv_index * HD, 1
        )
        return ((key_grad, value_grad), query_grad)

    zero_grads = jnp.zeros((seq_length, kv_local * HD), jnp.float32)
    (key_grad_seq, value_grad_seq), query_grad_items = lax.scan(
        attend_back, (zero_grads, zero_grads), jnp.arange(item_count, dtype=jnp.int32)
    )
    key_grad_block, value_grad_block = (
        lax.psum_scatter(
            key_grad_seq.astype(jnp.bfloat16), "nar", scatter_dimension=0, tiled=True
        ).astype(jnp.float32),
        lax.psum_scatter(
            value_grad_seq.astype(jnp.bfloat16), "nar", scatter_dimension=0, tiled=True
        ).astype(jnp.float32),
    )
    query_grad_rows = (
        query_grad_items.reshape(block_count, query_heads, query_block, HD)
        .transpose(0, 2, 1, 3)
        .reshape(block_tokens, query_heads, HD)
    )
    query_grad_b = (
        rotate_back(query_grad_rows, cosine_table, sine_table)
        .astype(jnp.bfloat16)
        .reshape(block_tokens, query_heads * HD)
    )
    key_grad_b = (
        rotate_back(key_grad_block.reshape(block_tokens, kv_local, HD), cosine_table, sine_table)
        .astype(jnp.bfloat16)
        .reshape(block_tokens, kv_local * HD)
    )
    value_grad_b = value_grad_block.astype(jnp.bfloat16)
    query_weight_grad = contract_first(normed_rows, query_grad_b)
    key_weight_grad = contract_first(normed_rows, key_grad_b)
    value_weight_grad = contract_first(normed_rows, value_grad_b)
    grad_normed_attn = lax.psum_scatter(
        (
            contract_last(query_grad_b, query_full)
            + contract_last(key_grad_b, key_local)
            + contract_last(value_grad_b, value_local)
        ).astype(jnp.bfloat16),
        "wid",
        scatter_dimension=0,
        tiled=True,
    ).astype(jnp.float32)
    grad_residual, gain_attn_term = norm_backward(residual, root_attn, gain_attn, grad_normed_attn)
    grad_in = (grad_residual + grad_middle).astype(jnp.bfloat16)[None]
    summed = (
        lax.psum_scatter(
            query_weight_grad.astype(jnp.bfloat16), ("row", "nar"), scatter_dimension=0, tiled=True
        ).astype(jnp.float32),
        lax.psum_scatter(
            key_weight_grad.astype(jnp.bfloat16), ("row", "nar"), scatter_dimension=0, tiled=True
        ).astype(jnp.float32),
        lax.psum_scatter(
            value_weight_grad.astype(jnp.bfloat16), ("row", "nar"), scatter_dimension=0, tiled=True
        ).astype(jnp.float32),
        lax.psum_scatter(
            output_weight_grad.astype(jnp.bfloat16), ("row", "nar"), scatter_dimension=1, tiled=True
        ).astype(jnp.float32),
        lax.psum_scatter(
            gate_weight_grad.astype(jnp.bfloat16), ("row", "nar"), scatter_dimension=0, tiled=True
        ).astype(jnp.float32),
        lax.psum_scatter(
            up_weight_grad.astype(jnp.bfloat16), ("row", "nar"), scatter_dimension=0, tiled=True
        ).astype(jnp.float32),
        lax.psum_scatter(
            down_weight_grad.astype(jnp.bfloat16), ("row", "nar"), scatter_dimension=1, tiled=True
        ).astype(jnp.float32),
        lax.psum_scatter(
            gain_attn_term.astype(jnp.bfloat16), ("row", "nar"), scatter_dimension=0, tiled=True
        ).astype(jnp.float32),
        lax.psum_scatter(
            gain_ffn_term.astype(jnp.bfloat16), ("row", "nar"), scatter_dimension=0, tiled=True
        ).astype(jnp.float32),
    )
    (
        grad_query,
        key_sum,
        value_sum,
        grad_output,
        grad_gate,
        grad_up,
        grad_down,
        gain_attn_sum,
        gain_ffn_sum,
    ) = summed
    key_all, value_all, gain_attn_all, gain_ffn_all = (
        lax.all_gather(key_sum.astype(jnp.bfloat16), "wid", axis=1, tiled=True).astype(
            key_sum.dtype
        ),
        lax.all_gather(value_sum.astype(jnp.bfloat16), "wid", axis=1, tiled=True).astype(
            value_sum.dtype
        ),
        lax.all_gather(gain_attn_sum.astype(jnp.bfloat16), "wid", axis=0, tiled=True).astype(
            gain_attn_sum.dtype
        ),
        lax.all_gather(gain_ffn_sum.astype(jnp.bfloat16), "wid", axis=0, tiled=True).astype(
            gain_ffn_sum.dtype
        ),
    )
    shard_rows = key_sum.shape[0]
    repeats = wid_count * kv_local // KV
    grad_key = key_all.reshape(shard_rows, KV, repeats, HD).sum(axis=2).reshape(shard_rows, KV * HD)
    grad_value = (
        value_all.reshape(shard_rows, KV, repeats, HD).sum(axis=2).reshape(shard_rows, KV * HD)
    )
    grad_gain_attn = gain_attn_all.reshape(wid_count, shard_rows).sum(axis=0)
    grad_gain_ffn = gain_ffn_all.reshape(wid_count, shard_rows).sum(axis=0)
    return (
        hidden_out,
        grad_in,
        grad_query,
        grad_key,
        grad_value,
        grad_output,
        grad_gate,
        grad_up,
        grad_down,
        grad_gain_attn,
        grad_gain_ffn,
    )


MESH = pl.DeviceIdType.MESH
bf16 = jnp.bfloat16
f32 = jnp.float32
VMEM_LIMIT = 60 * 2**20


def spot():
    return lax.axis_index("row"), lax.axis_index("nar"), lax.axis_index("wid")


def greet(partners):
    barrier = pltpu.get_barrier_semaphore()
    total = 0
    for there, device in partners:
        @pl.when(there)
        def _():
            pl.semaphore_signal(barrier, inc=1, device_id=device, device_id_type=MESH)

        total = total + there.astype(jnp.int32)
    pl.semaphore_wait(barrier, total)


def line_partners(r, n, w, wid_count):
    return [
        (w < wid_count - 1, (r, n, jnp.minimum(w + 1, wid_count - 1))),
        (w > 0, (r, n, jnp.maximum(w - 1, 0))),
        (w >= 0, (1 - r, n, w)),
    ]


def each_rows(count, step, body):
    def run(i, carry):
        body(pl.ds(pl.multiple_of(i * step, step), step))
        return carry

    lax.fori_loop(0, count // step, run, 0)


def square_partners(r, n, w):
    return [(n >= 0, over_x(r, n, w)), (n >= 0, over_y(r, n, w))]


def over_x(r, n, w):
    return (r, n + 1 - 2 * (n % 2), w)


def over_y(r, n, w):
    return (r, (n + 2) % 4, w)


def push(source, target, s_s, s_g, device):
    return pltpu.make_async_remote_copy(
        source, target, s_s, s_g, device_id=device, device_id_type=MESH
    )


class Gather:
    def __init__(self, buf, sems, me, wid_count, rows=slice(None)):
        self.rows = rows
        self.buf, (self.up_s, self.dn_s, self.pt_s, self.got) = buf, sems
        self.r, self.n, self.w = me
        self.last = wid_count - 1
        self.up = (self.r, self.n, jnp.minimum(self.w + 1, self.last))
        self.dn = (self.r, self.n, jnp.maximum(self.w - 1, 0))
        self.pt = (1 - self.r, self.n, self.w)

    def copy(self, j, sem, device, row=None):
        row = self.r if row is None else row
        return pltpu.make_async_remote_copy(
            self.buf.at[row, j, self.rows],
            self.buf.at[row, j, self.rows],
            sem.at[j],
            self.got.at[row, j],
            device_id=device,
            device_id_type=MESH,
        )

    def pass_on(self, j, go_up, go_dn):
        if go_up:
            @pl.when(self.w < self.last)
            def _():
                self.copy(j, self.up_s, self.up).start()

        if go_dn:
            @pl.when(self.w > 0)
            def _():
                self.copy(j, self.dn_s, self.dn).start()

        self.copy(j, self.pt_s, self.pt).start()

    def own(self):
        self.pass_on(self.w, True, True)

    def arrive(self, row, j):
        self.copy(j, self.pt_s, self.pt, row).wait_recv()

    def step(self, k):
        below, above = self.w - k, self.w + k

        @pl.when(below >= 0)
        def _():
            self.arrive(self.r, below)
            self.pass_on(below, True, False)

        @pl.when(above <= self.last)
        def _():
            self.arrive(self.r, above)
            self.pass_on(above, False, True)

    def rest(self):
        for j in range(self.last + 1):
            self.arrive(1 - self.r, j)

    def sent(self):
        for j in range(self.last + 1):
            @pl.when((j <= self.w) & (self.w < self.last))
            def _():
                self.copy(j, self.up_s, self.up).wait_send()

            @pl.when((j >= self.w) & (self.w > 0))
            def _():
                self.copy(j, self.dn_s, self.dn).wait_send()

            self.copy(j, self.pt_s, self.pt).wait_send()


def gather_scratch(shard, width):
    return [pltpu.VMEM((2, 4, shard, width), bf16)] + gather_sems()


def gather_sems():
    return [pltpu.SemaphoreType.DMA((4,))] * 3 + [pltpu.SemaphoreType.DMA((2, 4))]


class Scatter:
    def __init__(self, mine, theirs, bufs, sems, me, wid_count):
        self.mine, self.theirs = mine, theirs
        self.from_pt, self.from_up, self.from_dn = bufs
        self.pt_s, self.pt_g, self.up_s, self.up_g, self.dn_s, self.dn_g = sems
        self.r, self.n, self.w = me
        self.last = wid_count - 1
        self.up = (self.r, self.n, jnp.minimum(self.w + 1, self.last))
        self.dn = (self.r, self.n, jnp.maximum(self.w - 1, 0))
        self.pt = (1 - self.r, self.n, self.w)

    def order(self, i):
        low, high = (3, 0, 2, 1)[i], (0, 3, 1, 2)[i]
        return jnp.where(self.w < 2, low, high)

    def pair(self, s):
        return pltpu.make_async_remote_copy(
            self.theirs.at[s], self.from_pt.at[s], self.pt_s.at[s], self.pt_g.at[s],
            device_id=self.pt, device_id_type=MESH,
        )

    def climb(self, s):
        return pltpu.make_async_remote_copy(
            self.mine.at[s], self.from_dn.at[s], self.up_s.at[s], self.up_g.at[s],
            device_id=self.up, device_id_type=MESH,
        )

    def fall(self, s):
        return pltpu.make_async_remote_copy(
            self.mine.at[s], self.from_up.at[s], self.dn_s.at[s], self.dn_g.at[s],
            device_id=self.dn, device_id_type=MESH,
        )

    def add(self, s, others):
        def body(rows):
            total = self.mine[s, rows, :].astype(f32)
            for other in others:
                total = total + other[s, rows, :].astype(f32)
            self.mine[s, rows, :] = total.astype(bf16)

        each_rows(self.mine.shape[1], 16, body)

    def step(self, s):
        self.pair(s).wait_recv()

        @pl.when((s > self.w) & (self.w > 0))
        def _():
            self.climb(s).wait_recv()
            self.add(s, (self.from_pt, self.from_dn))

        @pl.when((s < self.w) & (self.w < self.last))
        def _():
            self.fall(s).wait_recv()
            self.add(s, (self.from_pt, self.from_up))

        @pl.when(((s > self.w) & (self.w == 0)) | ((s < self.w) & (self.w == self.last)))
        def _():
            self.add(s, (self.from_pt,))

        @pl.when(s > self.w)
        def _():
            self.climb(s).start()

        @pl.when(s < self.w)
        def _():
            self.fall(s).start()

    def advance(self, edge_steps, inner_steps):
        for ends, steps in ((True, edge_steps), (False, inner_steps)):
            at_end = (self.w == 0) | (self.w == self.last)

            @pl.when(at_end if ends else jnp.logical_not(at_end))
            def _():
                for i in steps:
                    self.step(self.order(i))

    def total(self, out):
        w = self.w

        def first(rows):
            out[rows, :] = self.mine[w, rows, :].astype(f32) + self.from_pt[w, rows, :].astype(f32)

        each_rows(out.shape[0], 16, first)

        @pl.when(w > 0)
        def _():
            self.climb(w).wait_recv()

            def more(rows):
                out[rows, :] += self.from_dn[w, rows, :].astype(f32)

            each_rows(out.shape[0], 16, more)

        @pl.when(w < self.last)
        def _():
            self.fall(w).wait_recv()

            def more(rows):
                out[rows, :] += self.from_up[w, rows, :].astype(f32)

            each_rows(out.shape[0], 16, more)

    def sent(self):
        for s in range(self.last + 1):
            self.pair(s).wait_send()

            @pl.when(s > self.w)
            def _():
                self.climb(s).wait_send()

            @pl.when(s < self.w)
            def _():
                self.fall(s).wait_send()


def scatter_bufs(shard, width):
    return [pltpu.VMEM((4, shard, width), bf16)] * 3


def scatter_sems():
    return [pltpu.SemaphoreType.DMA((4,))] * 6


def vmem():
    return pl.BlockSpec(memory_space=pltpu.VMEM)


def hbm():
    return pl.BlockSpec(memory_space=pl.ANY)


def comm_call(kernel, name, cid, out_shape, in_specs, out_specs, scratch, args, flops=0, sent=0):
    return pl.pallas_call(
        kernel,
        out_shape=out_shape,
        in_specs=in_specs,
        out_specs=out_specs,
        scratch_shapes=scratch,
        compiler_params=pltpu.CompilerParams(
            collective_id=cid, has_side_effects=True, vmem_limit_bytes=VMEM_LIMIT
        ),
        cost_estimate=pl.CostEstimate(flops=flops, bytes_accessed=sent, transcendentals=0),
        name=name,
    )(*args)


def norm_rows(x, gain):
    root = lax.rsqrt(jnp.mean(x * x, axis=-1, keepdims=True) + norm_eps)
    return x * root * gain


def turn(x, cosine, sine):
    lane = lax.broadcasted_iota(jnp.int32, x.shape, 1)
    swapped = jnp.where(lane % 64 < 32, pltpu.roll(x, 96, 1), pltpu.roll(x, 32, 1))
    return x * cosine + swapped * sine


def enter_kernel(hidden, gain, tab, rows_out, tabs_out, buf, up_s, dn_s, pt_s, got, tabs, tab_s, tab_g, out_s):
    me = spot()
    r, n, w = me
    greet(line_partners(r, n, w, 4))
    gather = Gather(buf, (up_s, dn_s, pt_s, got), me, 4)
    tab_copy = pltpu.make_async_remote_copy(
        tab, tabs.at[r], tab_s, tab_g, device_id=(1 - r, n, w), device_id_type=MESH
    )

    def body(rows):
        buf[r, w, rows, :] = norm_rows(hidden[rows, :].astype(f32), gain[...]).astype(bf16)

    each_rows(hidden.shape[0], 16, body)
    gather.own()
    tab_copy.start()

    def keep(rows):
        tabs[r, rows, :] = tab[rows, :]

    each_rows(tab.shape[0], 16, keep)
    for k in (1, 2, 3):
        gather.step(k)
    gather.rest()
    out = pltpu.make_async_copy(buf, rows_out, out_s.at[0])
    out.start()
    tab_copy.wait_recv()
    out_tab = pltpu.make_async_copy(tabs, tabs_out, out_s.at[1])
    out_tab.start()
    gather.sent()
    tab_copy.wait_send()
    out.wait()
    out_tab.wait()


def enter(hidden, gain, tab):
    shard, width = hidden.shape
    return comm_call(
        enter_kernel, "enter", 1,
        (
            jax.ShapeDtypeStruct((2, 4, shard, width), bf16),
            jax.ShapeDtypeStruct((2,) + tab.shape, f32),
        ),
        [vmem()] * 3, [hbm()] * 2,
        gather_scratch(shard, width)
        + [
            pltpu.VMEM((2,) + tab.shape, f32),
            pltpu.SemaphoreType.DMA(()),
            pltpu.SemaphoreType.DMA(()),
            pltpu.SemaphoreType.DMA((2,)),
        ],
        (hidden, gain, tab), flops=10**10, sent=10**8,
    )


def nar_device(r, n, w, by):
    return (r, jnp.clip(n + by, 0, 3), w)


def project_kernel(
    x, p1, tabs, grad_top, q_out, kv_out, tops_out, kv, s_s, s_g, out_s, buf, g0, g1, g2, g3, tops_s
):
    r, n, w = spot()
    greet(
        line_partners(r, n, w, 4)
        + [
            (n >= 1, nar_device(r, n, w, -1)),
            (n >= 2, nar_device(r, n, w, -2)),
            (n <= 2, nar_device(r, n, w, 1)),
            (n <= 1, nar_device(r, n, w, 2)),
        ]
    )
    gather = Gather(buf, (g0, g1, g2, g3), (r, n, w), 4)

    def keep(rows):
        buf[r, w, rows, :] = grad_top[rows, :]

    each_rows(64, 16, keep)
    gather.own()

    def copy(row, slot, by):
        return pltpu.make_async_remote_copy(
            kv.at[row, 2], kv.at[row, slot], s_s.at[row, slot], s_g.at[row, slot],
            device_id=nar_device(r, n, w, by), device_id_type=MESH,
        )

    lane = lax.broadcasted_iota(jnp.int32, (256, 128), 1)
    weight = p1[:, :, 0:384].reshape(2048, 384)
    for row in range(2):
        def tile(i, carry):
            rows = pl.ds(pl.multiple_of(i * 256, 256), 256)
            cosine, sine = tabs[row, rows, 0:128], tabs[row, rows, 128:256]
            pre = jnp.dot(x[row, rows, :], weight, preferred_element_type=f32)
            q_out[row, rows, 0:128] = turn(pre[:, 0:128], cosine, sine).astype(bf16)
            q_out[row, rows, 128:256] = turn(pre[:, 128:256], cosine, sine).astype(bf16)
            both = pre[:, 256:384]
            kv[row, 2, rows, :] = jnp.where(lane < 64, turn(both, cosine, sine), both).astype(bf16)
            return carry

        lax.fori_loop(0, 2, tile, 0)

        @pl.when(n <= 2)
        def _():
            copy(row, 1, 1).start()

        @pl.when(n <= 1)
        def _():
            copy(row, 0, 2).start()

        for slot, least in ((1, 1), (0, 2)):
            @pl.when(n < least)
            def _():
                kv[row, slot] = jnp.zeros((512, 128), bf16)

    for k in (1, 2, 3):
        gather.step(k)
    gather.rest()
    tops_copy = pltpu.make_async_copy(buf, tops_out, tops_s)
    tops_copy.start()
    for row in range(2):
        for slot, least, by in ((1, 1, 1), (0, 2, 2)):
            @pl.when(n >= least)
            def _():
                copy(row, slot, by).wait_recv()

    out = pltpu.make_async_copy(kv, kv_out, out_s)
    out.start()
    for row in range(2):
        @pl.when(n <= 2)
        def _():
            copy(row, 1, 1).wait_send()

        @pl.when(n <= 1)
        def _():
            copy(row, 0, 2).wait_send()

    gather.sent()
    out.wait()
    tops_copy.wait()


def project(x, p1, tabs, grad_top):
    return comm_call(
        project_kernel, "project", 2,
        (
            jax.ShapeDtypeStruct((2, 512, 256), bf16),
            jax.ShapeDtypeStruct((2, 3, 512, 128), bf16),
            jax.ShapeDtypeStruct((2, 4, 64, 2048), bf16),
        ),
        [vmem()] * 4, [vmem(), hbm(), hbm()],
        [
            pltpu.VMEM((2, 3, 512, 128), bf16),
            pltpu.SemaphoreType.DMA((2, 3)),
            pltpu.SemaphoreType.DMA((2, 3)),
            pltpu.SemaphoreType.DMA(()),
        ]
        + gather_scratch(64, 2048)
        + [pltpu.SemaphoreType.DMA(())],
        (x, p1, tabs, grad_top), flops=10**10, sent=10**7,
    )


KEYS = 256
QUERIES = 128


def stack_low(x):
    lane = lax.broadcasted_iota(jnp.int32, (QUERIES, 128), 1)
    zero = jnp.zeros((QUERIES, 128), x.dtype)
    parts = []
    for pair in range(2):
        block = x[:, pair * 128 : pair * 128 + 128]
        parts.append(jnp.where(lane < 64, block, zero))
        parts.append(jnp.where(lane < 64, pltpu.roll(block, 64, 1), zero))
    return jnp.concatenate(parts, axis=0)


def stack_high(x):
    lane = lax.broadcasted_iota(jnp.int32, (QUERIES, 128), 1)
    zero = jnp.zeros((QUERIES, 128), x.dtype)
    parts = []
    for pair in range(2):
        block = x[:, pair * 128 : pair * 128 + 128]
        parts.append(jnp.where(lane >= 64, pltpu.roll(block, 64, 1), zero))
        parts.append(jnp.where(lane >= 64, block, zero))
    return jnp.concatenate(parts, axis=0)


def unstack(x, low):
    lane = lax.broadcasted_iota(jnp.int32, (QUERIES, 128), 1)
    out = []
    for pair in range(2):
        even = x[2 * pair * QUERIES : (2 * pair + 1) * QUERIES]
        odd = x[(2 * pair + 1) * QUERIES : (2 * pair + 2) * QUERIES]
        if low:
            out.append(jnp.where(lane < 64, even, pltpu.roll(odd, 64, 1)))
        else:
            out.append(jnp.where(lane < 64, pltpu.roll(even, 64, 1), odd))
    return jnp.concatenate(out, axis=1)


def allowed_tile(starts, tile, first_query):
    key = lax.broadcasted_iota(jnp.int32, (QUERIES, KEYS), 1) + tile * KEYS
    query = lax.broadcasted_iota(jnp.int32, (QUERIES, KEYS), 0) + first_query
    start = jnp.concatenate([starts] * (KEYS // 128), axis=1)
    ok = (key <= query) & (key.astype(f32) >= start)
    return jnp.concatenate([ok] * 4, axis=0)


def key_tiles(low, row, block):
    first_query = 1024 + block * QUERIES
    return low[row * 4 + block] // KEYS, first_query // KEYS + 1, first_query


def attend_kernel(low, q, kv, starts, out, lse):
    row, block = pl.program_id(0), pl.program_id(1)
    first, end, first_query = key_tiles(low, row, block)
    query = stack_low(q[0].astype(f32)).astype(bf16)

    def body(tile, carry):
        top, total, acc = carry
        both = kv[0, pl.ds(pl.multiple_of(tile * KEYS, KEYS), KEYS), :]
        scores = contract_last(query, both) * 0.125
        ok = allowed_tile(starts[0], tile, first_query)
        scores = jnp.where(ok, scores, masked_score)
        new_top = jnp.maximum(top, jnp.max(scores, axis=1, keepdims=True))
        shrink = jnp.exp(top - new_top)
        part = jnp.exp(scores - new_top)
        total = total * shrink + jnp.sum(part, axis=1, keepdims=True)
        acc = acc * shrink + jnp.dot(part.astype(bf16), both, preferred_element_type=f32)
        return new_top, total, acc

    top, total, acc = lax.fori_loop(
        first, end, body,
        (
            jnp.full((4 * QUERIES, 1), masked_score, f32),
            jnp.zeros((4 * QUERIES, 1), f32),
            jnp.zeros((4 * QUERIES, 128), f32),
        ),
    )
    out[0] = unstack(acc / total, False).astype(bf16)
    lse[0, 0] = jnp.broadcast_to(top + jnp.log(total), (4 * QUERIES, 128))


def attend_specs():
    return [
        pl.BlockSpec((1, QUERIES, 256), lambda i, j, low: (i, j, 0)),
        pl.BlockSpec((1, 1536, 128), lambda i, j, low: (i, 0, 0)),
        pl.BlockSpec((1, QUERIES, 128), lambda i, j, low: (i, j, 2)),
    ]


def attend(low, q, kv, tabs):
    return pl.pallas_call(
        attend_kernel,
        out_shape=(
            jax.ShapeDtypeStruct((2, 512, 256), bf16),
            jax.ShapeDtypeStruct((2, 4, 4 * QUERIES, 128), f32),
        ),
        grid_spec=pltpu.PrefetchScalarGridSpec(
            num_scalar_prefetch=1, grid=(2, 4),
            in_specs=attend_specs(),
            out_specs=[
                pl.BlockSpec((1, QUERIES, 256), lambda i, j, low: (i, j, 0)),
                pl.BlockSpec((1, 1, 4 * QUERIES, 128), lambda i, j, low: (i, j, 0, 0)),
            ],
        ),
        compiler_params=pltpu.CompilerParams(vmem_limit_bytes=VMEM_LIMIT),
        cost_estimate=pl.CostEstimate(flops=2 * 10**10, bytes_accessed=10**7, transcendentals=10**7),
        name="attend",
    )(low, q, kv, tabs)


def out_block(p1, nn, half):
    return p1[nn, half * 256 : half * 256 + 256, 384:640]


def middle_kernel(
    att, p1, hidden, gain, mid_out, ffn_out,
    theirs, mine, from_pt, from_up, from_dn, s0, s1, s2, s3, s4, s5, fbuf, h0, h1, h2, h3, out_s,
):
    me = spot()
    r, n, w = me
    greet(line_partners(r, n, w, 4))
    scatter = Scatter(
        mine, theirs, (from_pt, from_up, from_dn), (s0, s1, s2, s3, s4, s5), me, 4
    )
    ffn = Gather(fbuf, (h0, h1, h2, h3), me, 4)
    for i in range(4):
        s = scatter.order(i)
        rows = pl.ds(pl.multiple_of(s * 128, 128), 128)
        left = jnp.concatenate([att[1 - r, rows, :], att[r, rows, :]], axis=0)
        for nn in range(4):
            for half in range(2):
                part = jnp.dot(left, out_block(p1, nn, half), preferred_element_type=f32).astype(bf16)
                columns = slice(nn * 512 + half * 256, nn * 512 + half * 256 + 256)
                theirs[s, :, columns] = part[0:128]
                mine[s, :, columns] = part[128:256]
        scatter.pair(s).start()
    for i in range(4):
        scatter.step(scatter.order(i))
    scatter.total(mid_out)

    def body(rows):
        middle = mid_out[rows, :] + hidden[rows, :].astype(f32)
        mid_out[rows, :] = middle
        fbuf[r, w, rows, :] = norm_rows(middle, gain[...]).astype(bf16)

    each_rows(hidden.shape[0], 16, body)
    ffn.own()
    for k in (1, 2, 3):
        ffn.step(k)
    ffn.rest()
    out_f = pltpu.make_async_copy(fbuf, ffn_out, out_s)
    out_f.start()
    scatter.sent()
    ffn.sent()
    out_f.wait()


def middle_stage(att, p1, hidden, gain):
    shard, width = hidden.shape
    rows = jax.ShapeDtypeStruct((2, 4, shard, width), bf16)
    return comm_call(
        middle_kernel, "middle", 3,
        (jax.ShapeDtypeStruct((shard, width), f32), rows),
        [vmem()] * 4, [vmem(), hbm()],
        [pltpu.VMEM((4, shard, width), bf16)] * 2
        + scatter_bufs(shard, width) + scatter_sems()
        + gather_scratch(shard, width)
        + [pltpu.SemaphoreType.DMA(())],
        (att, p1, hidden, gain), flops=10**10, sent=2 * 10**8,
    )


class Spread:
    def __init__(self, outs, sems, me):
        self.a_send, self.a_keep, self.b_send, self.b_keep = outs
        self.r, self.n, self.w = me
        self.give_s, self.give_g, self.keep_s = sems

    def copies(self, wide, row, place, give):
        for k in range(4):
            block = wide.at[self.n ^ k]
            for part in range(2):
                source = block.at[pl.ds(part * 128, 128)]
                if part == 0:
                    target = (self.a_send if k & 1 else self.a_keep).at[k >> 1]
                else:
                    target = (self.b_send if k >= 2 else self.b_keep).at[k & 1]
                target = place(target)
                at = k * 2 + part
                if give:
                    yield pltpu.make_async_remote_copy(
                        source, target, self.give_s.at[row, at], self.give_g.at[row, at],
                        device_id=(1 - self.r, self.n, self.w), device_id_type=MESH,
                    )
                else:
                    yield pltpu.make_async_copy(source, target, self.keep_s.at[row, at])

    def start(self, *args):
        for copy in self.copies(*args):
            copy.start()

    def wait_send(self, *args):
        for copy in self.copies(*args):
            copy.wait_send()

    def wait_recv(self, *args):
        for copy in self.copies(*args):
            copy.wait_recv()

    def wait(self, *args):
        for copy in self.copies(*args):
            copy.wait()


def spread_sems(count):
    return [pltpu.SemaphoreType.DMA((count, 8))] * 3


def ffn_kernel(
    x, tops_in, grad_top, p2_all, gain,
    part_out, sum_out, gain_out, o0, o1, o2, o3, ra_out, rb_out,
    theirs, mine, from_pt, from_up, from_dn, s0, s1, s2, s3, s4, s5,
    act, dgu, wide, out_s, give_s, give_g, keep_s, p2, in_s, n_s, n_g,
    tops4, h0, h1, h2, h3, tops_s,
):
    me = spot()
    r, n, w = me
    loads = [pltpu.make_async_copy(p2_all.at[:, j], p2.at[j], in_s.at[j]) for j in range(3)]
    loads.append(pltpu.make_async_copy(tops_in, tops4.at[:, :, 0:64], tops_s))
    for load in loads:
        load.start()
    greet(line_partners(r, n, w, 4) + square_partners(r, n, w))
    scatter = Scatter(
        mine, theirs, (from_pt, from_up, from_dn), (s0, s1, s2, s3, s4, s5), me, 4
    )
    late = pl.ds(64, 64)
    gather = Gather(tops4, (h0, h1, h2, h3), me, 4, late)

    def keep(rows):
        tops4[r, w, pl.ds(64 + rows.start, 16), :] = grad_top[pl.ds(64 + rows.start, 16), :]

    each_rows(64, 16, keep)
    gather.own()
    gain_out[...] = jnp.zeros_like(gain_out)
    loads[0].wait()
    loads[1].wait()

    def hidden_tile(i, carry):
        ft, row = i // 2, i % 2
        rows = pl.ds(pl.multiple_of(row * 512, 512), 512)
        columns = pl.ds(pl.multiple_of(ft * 256, 256), 256)
        left = x[rows, :]
        gate = jnp.dot(left, p2[0, :, :, columns].reshape(2048, 256), preferred_element_type=f32)
        up = jnp.dot(left, p2[1, :, :, columns].reshape(2048, 256), preferred_element_type=f32)
        sig = 1.0 / (1.0 + jnp.exp(-gate))
        silu = gate * sig
        act[rows, columns] = (silu * up).astype(bf16)
        dgu[rows, columns] = (up * (sig * (1.0 + gate * (1.0 - sig)))).astype(bf16)
        later = pl.ds(pl.multiple_of(1024 + ft * 256, 256), 256)
        dgu[rows, later] = silu.astype(bf16)
        return carry

    lax.fori_loop(0, 4, hidden_tile, 0)
    gather.step(1)
    lax.fori_loop(4, 8, hidden_tile, 0)
    gather.step(2)
    loads[2].wait()

    def down_tile(dt, carry):
        nn, half = dt // 2, dt % 2
        columns = pl.ds(pl.multiple_of(dt * 256, 256), 256)
        inner = pl.ds(pl.multiple_of(half * 256, 256), 256)
        other = pl.ds(pl.multiple_of(512 + half * 256, 256), 256)
        right = jnp.concatenate([p2[2, nn, :, inner], p2[2, nn, :, other]], axis=0)
        for row, stage in ((0, theirs), (1, mine)):
            part = jnp.dot(act[row * 512 : row * 512 + 512, :], right, preferred_element_type=f32)
            stage[:, :, columns] = part.astype(bf16).reshape(4, 128, 256)
        return carry

    lax.fori_loop(0, 8, down_tile, 0)
    puts = [
        pltpu.make_async_copy(theirs, part_out.at[0], out_s.at[0]),
        pltpu.make_async_copy(mine, part_out.at[1], out_s.at[1]),
    ]
    for put in puts:
        put.start()
    gather.step(3)
    gather.rest()
    loads[3].wait()

    def top_rows(row):
        return tops4[row].reshape(512, 2048)

    def back_tile(ft, carry):
        columns = pl.ds(pl.multiple_of(ft * 256, 256), 256)
        f_rows = pl.ds(pl.multiple_of((ft % 2) * 256, 256), 256)
        f_cols = pl.ds(pl.multiple_of((ft // 2) * 512, 512), 512)
        later = pl.ds(pl.multiple_of(1024 + ft * 256, 256), 256)
        right = jnp.concatenate([p2[2, nn, f_rows, f_cols] for nn in range(4)], axis=1)
        for row in range(2):
            rows = slice(row * 512, row * 512 + 512)
            dact = contract_last(top_rows(row), right)
            dgu[rows, columns] = (dact * dgu[rows, columns].astype(f32)).astype(bf16)
            dgu[rows, later] = (dact * dgu[rows, later].astype(f32)).astype(bf16)
        return carry

    lax.fori_loop(0, 4, back_tile, 0)
    for put in puts:
        put.wait()

    spread = Spread((o0, o1, o2, o3), (give_s, give_g, keep_s), me)
    columns_here = pl.ds(pl.multiple_of(r * 1024, 1024), 1024)
    slots = {2: 0, 0: 1, 1: 0}

    def moved(which, half):
        def place(target):
            return target.at[which, :, columns_here]

        return wide.at[slots[which], half], which, place, half == 0

    def weights(which, between=None):
        for half in range(2):
            d_first = (jnp.where(half == 0, 1 - r, r)) * 1024

            def weight_tile(i, carry):
                d_cols = pl.ds(pl.multiple_of(d_first + i * 256, 256), 256)
                if which < 2:
                    left = x[:, d_cols]
                    right = dgu[:, which * 1024 : which * 1024 + 1024]
                else:
                    left = tops4[:, :, :, d_cols].reshape(1024, 256)
                    right = act[...]
                wide[slots[which], half, i] = contract_first(left, right).astype(bf16)
                return carry

            lax.fori_loop(0, 4, weight_tile, 0)
            spread.start(*moved(which, half))
            if half == 0 and between is not None:
                between()

    def hop(which, at):
        return (
            push(o0.at[:, which], ra_out.at[at], n_s.at[0, at], n_g.at[0, at], over_x(r, n, w)),
            push(o2.at[:, which], rb_out.at[at], n_s.at[1, at], n_g.at[1, at], over_y(r, n, w)),
        )

    hops = hop(2, 0) + hop(0, 1)
    weights(2)
    for i in range(4):
        s = scatter.order(i)
        rows_t = pl.ds(pl.multiple_of((1 - r) * 512 + s * 128, 128), 128)
        rows_m = pl.ds(pl.multiple_of(r * 512 + s * 128, 128), 128)

        def model_tile(dt, carry):
            nn, half = dt // 2, dt % 2
            columns = pl.ds(pl.multiple_of(dt * 256, 256), 256)
            inner = pl.ds(pl.multiple_of(half * 256, 256), 256)
            left = jnp.concatenate([dgu[rows_t, :], dgu[rows_m, :]], axis=0)
            right = jnp.concatenate([p2[0, nn, inner, :], p2[1, nn, inner, :]], axis=1)
            part = contract_last(left, right)
            seen = jnp.concatenate([x[rows_t, columns], x[rows_m, columns]], axis=0)
            terms = part * seen.astype(f32)
            gain_out[:, columns] += jnp.sum(terms.reshape(32, 8, 256), axis=0)
            part = part.astype(bf16)
            theirs[s, :, columns] = part[0:128]
            mine[s, :, columns] = part[128:256]
            return carry

        lax.fori_loop(0, 8, model_tile, 0)
        scatter.pair(s).start()
        if i < 2:
            which = (2, 0)[i]
            spread.wait_recv(*moved(which, 0))
            spread.wait(*moved(which, 1))
            hops[2 * i].start()
            hops[2 * i + 1].start()
        if i == 0:
            weights(0)
            scatter.advance((0,), ())
        elif i > 1:
            scatter.advance((i - 1,), (i - 2,))

    def scale(rows):
        gain_out[rows, :] = gain_out[rows, :] / gain[...]

    each_rows(8, 8, scale)
    spread.wait_send(*moved(2, 0))
    weights(1, lambda: scatter.advance((3,), (2,)))
    scatter.advance((), (3,))
    scatter.total(sum_out)
    scatter.sent()
    gather.sent()
    spread.wait_send(*moved(0, 0))
    spread.wait_recv(*moved(1, 0))
    spread.wait_send(*moved(1, 0))
    spread.wait(*moved(1, 1))
    for hop in hops:
        hop.wait()


def spread_shapes(*dims):
    return (jax.ShapeDtypeStruct((2,) + dims, bf16),) * 4


def ffn_stage(*args):
    shard, width = 128, 2048
    return comm_call(
        ffn_kernel, "ffn", 4,
        (
            jax.ShapeDtypeStruct((2, 4, shard, width), bf16),
            jax.ShapeDtypeStruct((shard, width), f32),
            jax.ShapeDtypeStruct((8, width), f32),
        )
        + spread_shapes(3, 128, width)
        + (jax.ShapeDtypeStruct((2, 2, 128, width), bf16),) * 2,
        [vmem(), hbm(), vmem(), hbm(), vmem()], [hbm(), vmem(), vmem()] + [hbm()] * 6,
        [pltpu.VMEM((4, shard, width), bf16)] * 2
        + scatter_bufs(shard, width) + scatter_sems()
        + [
            pltpu.VMEM((1024, 1024), bf16),
            pltpu.VMEM((1024, 2048), bf16),
            pltpu.VMEM((2, 2, 4, 256, 1024), bf16),
            pltpu.SemaphoreType.DMA((2,)),
        ]
        + spread_sems(3)
        + [pltpu.VMEM((3, 4, 512, 1024), bf16), pltpu.SemaphoreType.DMA((3,))]
        + [pltpu.SemaphoreType.DMA((2, 2))] * 2
        + gather_scratch(shard, width)
        + [pltpu.SemaphoreType.DMA(())],
        args, flops=4 * 10**10, sent=10**8,
    )


def norm_back(values, gain, grad):
    root = lax.rsqrt(jnp.mean(values * values, axis=-1, keepdims=True) + norm_eps)
    weighted = grad * gain
    inner = jnp.mean(weighted * values, axis=-1, keepdims=True)
    return root * weighted - values * (root * root * root) * inner


def branch_kernel(
    total, mid, grad_top, gain, p1, att, a_in, b_in, a_keep, b_keep, a_came, b_came,
    gmid_out, datt_out, o0, o1, o2, o3, ra_out, rb_out, la_out, lb_out,
    buf, g0, g1, g2, g3, wide, give_s, give_g, keep_s, n_s, n_g, kept, came, in_s,
):
    me = spot()
    r, n, w = me
    greet(line_partners(r, n, w, 4) + square_partners(r, n, w))
    gather = Gather(buf, (g0, g1, g2, g3), me, 4)
    hops = [
        push(a_in.at[:, 1], ra_out, n_s.at[0], n_g.at[0], over_x(r, n, w)),
        push(b_in.at[:, 1], rb_out, n_s.at[1], n_g.at[1], over_y(r, n, w)),
        push(kept.at[0], la_out, n_s.at[2], n_g.at[2], over_y(r, n, w)),
        push(kept.at[1], lb_out, n_s.at[3], n_g.at[3], over_x(r, n, w)),
    ]
    loads = []
    for j, (keep, first) in enumerate(((a_keep, a_came), (b_keep, b_came))):
        loads += [
            pltpu.make_async_copy(keep.at[1, 2], kept.at[j], in_s.at[j, 0]),
            pltpu.make_async_copy(first.at[0, 1], came.at[j], in_s.at[j, 1]),
        ]
    for load in loads:
        load.start()
    hops[0].start()
    hops[1].start()

    def body(rows):
        grad = norm_back(mid[rows, :], gain[...], total[rows, :]) + grad_top[rows, :].astype(f32)
        gmid_out[rows, :] = grad
        buf[r, w, rows, :] = grad.astype(bf16)

    each_rows(mid.shape[0], 16, body)
    gather.own()
    for load in loads:
        load.wait()
    for j in range(2):
        def join(rows):
            kept[j, rows, :] = (kept[j, rows, :].astype(f32) + came[j, rows, :].astype(f32)).astype(bf16)

        each_rows(128, 16, join)
        hops[2 + j].start()
    for k in (1, 2, 3):
        gather.step(k)
    gather.rest()
    for row in range(2):
        for pair in range(2):
            left = jnp.concatenate([buf[row, 2 * pair], buf[row, 2 * pair + 1]], axis=0)
            right = jnp.concatenate(
                [out_block(p1, nn, half) for nn in range(4) for half in range(2)], axis=1
            )
            datt_out[row, pair * 256 : pair * 256 + 256, :] = contract_last(left, right).astype(bf16)

    spread = Spread((o0, o1, o2, o3), (give_s, give_g, keep_s), me)

    def moved(half):
        def place(target):
            return target.at[:, pl.ds(pl.multiple_of(r * 256, 256), 256)]

        return wide.at[half], 0, place, half == 0

    for half in range(2):
        d_first = (jnp.where(half == 0, 1 - r, r)) * 1024

        def weight_tile(i, carry):
            columns = pl.ds(pl.multiple_of(d_first + i * 256, 256), 256)
            left = buf[:, :, :, columns].reshape(1024, 256)
            wide[half, i] = contract_first(left, att[...]).astype(bf16)
            return carry

        lax.fori_loop(0, 4, weight_tile, 0)
        spread.start(*moved(half))
    gather.sent()
    spread.wait(*moved(0))
    spread.wait(*moved(1))
    for hop in hops:
        hop.wait()


def branch_stage(*args):
    shard, width = 128, 2048
    return comm_call(
        branch_kernel, "branch", 5,
        (
            jax.ShapeDtypeStruct((shard, width), f32),
            jax.ShapeDtypeStruct((2, 512, 256), bf16),
        )
        + spread_shapes(128, 512)
        + (jax.ShapeDtypeStruct((2, 128, width), bf16),) * 2
        + (jax.ShapeDtypeStruct((128, width), bf16),) * 2,
        [vmem()] * 6 + [hbm()] * 6, [vmem(), vmem()] + [hbm()] * 8,
        gather_scratch(shard, width)
        + [pltpu.VMEM((2, 4, 256, 256), bf16)]
        + spread_sems(1)
        + [pltpu.SemaphoreType.DMA((4,))] * 2
        + [pltpu.VMEM((2, 128, width), bf16)] * 2
        + [pltpu.SemaphoreType.DMA((2, 2))],
        args, flops=10**10, sent=10**8,
    )


def unproject_kernel(
    q, kv, att, grad, lse, x, p1, tabs, gain, parts, mid, a_keep, b_keep, a_gate, b_gate, a_up, b_up, oa_in, ob_in,
    part_out, gain_out, o0, o1, o2, o3, hid_out, ra_out, rb_out, roa_out, rob_out,
    send, recv, both, wide_q, wide_kv, s_s, s_g, give_s, give_g, keep_s,
    mine, from_pt, from_up, from_dn, s0, s1, s2, s3, s4, s5,
    kept, came, acc, in_s, n_s, n_g, m_s, dkv,
):
    me = spot()
    r, n, w = me
    loads = []
    for j, (keep, gate, up) in enumerate(((a_keep, a_gate, a_up), (b_keep, b_gate, b_up))):
        loads += [
            pltpu.make_async_copy(keep.at[1, 0:2], kept.at[j], in_s.at[j, 0]),
            pltpu.make_async_copy(gate.at[1, 1], came.at[j, 0], in_s.at[j, 1]),
            pltpu.make_async_copy(up.at[1], came.at[j, 1], in_s.at[j, 2]),
        ]
    loads.append(pltpu.make_async_copy(parts.at[r], mine, m_s))
    for load in loads:
        load.start()
    greet(
        line_partners(r, n, w, 4)
        + [
            (n >= 1, nar_device(r, n, w, -1)),
            (n >= 2, nar_device(r, n, w, -2)),
            (n <= 2, nar_device(r, n, w, 1)),
            (n <= 1, nar_device(r, n, w, 2)),
        ]
        + square_partners(r, n, w)
    )
    scatter = Scatter(
        mine, parts.at[1 - r], (from_pt, from_up, from_dn), (s0, s1, s2, s3, s4, s5), me, 4
    )
    hops = [
        push(kept.at[0], ra_out, n_s.at[0], n_g.at[0], over_y(r, n, w)),
        push(kept.at[1], rb_out, n_s.at[1], n_g.at[1], over_x(r, n, w)),
        push(oa_in, roa_out, n_s.at[2], n_g.at[2], over_x(r, n, w)),
        push(ob_in, rob_out, n_s.at[3], n_g.at[3], over_y(r, n, w)),
    ]

    def copy(row, slot, by):
        return pltpu.make_async_remote_copy(
            send.at[row, slot], recv.at[row, slot], s_s.at[row, slot], s_g.at[row, slot],
            device_id=nar_device(r, n, w, by), device_id_type=MESH,
        )

    for i in range(4):
        scatter.pair(scatter.order(i)).start()
    for load in loads:
        load.wait()
    for j in range(2):
        for which in range(2):
            def join(rows):
                total = kept[j, which, rows, :].astype(f32) + came[j, which, rows, :].astype(f32)
                kept[j, which, rows, :] = total.astype(bf16)

            each_rows(128, 16, join)
        hops[j].start()
    hops[2].start()
    hops[3].start()
    scatter.advance((0, 1, 2, 3), ())

    def attention(i, carry):
        row, block = i // 4, i % 4
        first_query = 1024 + block * QUERIES
        here = pl.ds(pl.multiple_of(block * QUERIES, QUERIES), QUERIES)

        @pl.when(block == 0)
        def _():
            dkv[row] = jnp.zeros((1536, 128), f32)

        query = stack_low(q[row, here, :].astype(f32)).astype(bf16)
        grads = stack_high(grad[row, here, :].astype(f32))
        inner = jnp.sum(grads * stack_high(att[row, here, :].astype(f32)), axis=1, keepdims=True)
        grads = grads.astype(bf16)
        logsum = jnp.concatenate([lse[row, block]] * (KEYS // 128), axis=1)
        starts = tabs[row, here, 256:384]

        def key_tile(step, dq):
            tile = block // 2 + step
            rows = pl.ds(pl.multiple_of(tile * KEYS, KEYS), KEYS)
            pair = kv[row, rows, :]
            ok = allowed_tile(starts, tile, first_query)
            scores = contract_last(query, pair) * 0.125
            prob = jnp.where(ok, jnp.exp(scores - logsum), 0.0)
            grad_prob = contract_last(grads, pair)
            grad_scores = (prob * (grad_prob - inner)).astype(bf16)
            dkv[row, rows, :] += contract_first(grad_scores, query) * 0.125 + contract_first(
                prob.astype(bf16), grads
            )
            return dq + jnp.dot(grad_scores, pair, preferred_element_type=f32)

        dq = lax.fori_loop(0, 5, key_tile, jnp.zeros((4 * QUERIES, 128), f32))
        flat = unstack(dq, True) * 0.125
        cosine, sine = tabs[row, here, 0:128], -tabs[row, here, 128:256]
        there = pl.ds(pl.multiple_of(i * QUERIES, QUERIES), QUERIES)
        both[there, 0:128] = turn(flat[:, 0:128], cosine, sine).astype(bf16)
        both[there, 128:256] = turn(flat[:, 128:256], cosine, sine).astype(bf16)

        @pl.when(block == 3)
        def _():
            for slot, by in ((1, -1), (0, -2)):
                @pl.when(n >= -by)
                def _():
                    send[row, slot] = dkv[row, slot * 512 : slot * 512 + 512, :].astype(bf16)
                    copy(row, slot, by).start()

        @pl.when(i == 3)
        def _():
            scatter.advance((), (0,))

        return carry

    lax.fori_loop(0, 8, attention, 0)
    scatter.advance((), (1,))

    spread = Spread((o0, o1, o2, o3), (give_s, give_g, keep_s), (r, n, w))

    def moved_q(half):
        def place(target):
            return target.at[:, pl.ds(pl.multiple_of(r * 256, 256), 256)]

        return wide_q.at[half], 0, place, half == 0

    def moved_kv(half):
        def place(target):
            return target.at[:, pl.ds(pl.multiple_of(512 + r * 128, 128), 128)]

        return wide_kv.at[half], 1, place, half == 0

    def weight(half, columns, wide):
        d_first = (jnp.where(half == 0, 1 - r, r)) * 1024

        def tile(i, carry):
            d_cols = pl.ds(pl.multiple_of(d_first + i * 256, 256), 256)
            wide[half, i] = contract_first(x[:, d_cols], both[:, columns]).astype(bf16)
            return carry

        lax.fori_loop(0, 4, tile, 0)

    for half in range(2):
        weight(half, slice(0, 256), wide_q)
        spread.start(*moved_q(half))
    lane = lax.broadcasted_iota(jnp.int32, (128, 128), 1)
    for row in range(2):
        for slot, by in ((1, -1), (0, -2)):
            @pl.when(n <= 3 + by)
            def _():
                copy(row, slot, by).wait_recv()

        def tile(i, carry):
            rows = pl.ds(pl.multiple_of(i * 128, 128), 128)
            total = dkv[row, pl.ds(pl.multiple_of(1024 + i * 128, 128), 128), :]
            zero = jnp.zeros_like(total)
            total = total + jnp.where(n <= 2, recv[row, 1, rows, :].astype(f32), zero)
            total = total + jnp.where(n <= 1, recv[row, 0, rows, :].astype(f32), zero)
            turned = turn(total, tabs[row, rows, 0:128], -tabs[row, rows, 128:256])
            both[pl.ds(pl.multiple_of(row * 512 + i * 128, 128), 128), 256:384] = jnp.where(
                lane < 64, turned, total
            ).astype(bf16)
            return carry

        lax.fori_loop(0, 4, tile, 0)
    for half in range(2):
        weight(half, slice(256, 384), wide_kv)
        spread.start(*moved_kv(half))
    scatter.advance((), (2,))
    gain_out[...] = jnp.zeros_like(gain_out)

    def model_tile(dt, carry):
        nn, half = dt // 2, dt % 2
        columns = pl.ds(pl.multiple_of(dt * 256, 256), 256)
        inner = pl.ds(pl.multiple_of(half * 256, 256), 256)
        right = p1[nn, inner, 0:384]
        for row in range(2):
            for block in range(2):
                first = row * 512 + block * 256
                part = contract_last(both[first : first + 256, :], right)
                terms = part * x[first : first + 256, columns].astype(f32)
                gain_out[:, columns] += jnp.sum(terms.reshape(32, 8, 256), axis=0)
                part_out[row, 2 * block, :, columns] = part[0:128].astype(bf16)
                part_out[row, 2 * block + 1, :, columns] = part[128:256].astype(bf16)
        return carry

    lax.fori_loop(0, 8, model_tile, 0)
    gain_out[...] = gain_out[...] / gain[...]
    scatter.advance((), (3,))
    scatter.total(acc)

    def last(rows):
        hid_out[rows, :] = (acc[rows, :] + mid[rows, :]).astype(bf16)

    each_rows(128, 16, last)
    scatter.sent()
    for row in range(2):
        for slot, by in ((1, -1), (0, -2)):
            @pl.when(n >= -by)
            def _():
                copy(row, slot, by).wait_send()

    for half in range(2):
        spread.wait(*moved_q(half))
        spread.wait(*moved_kv(half))
    for hop in hops:
        hop.wait()


def unproject(*args):
    return comm_call(
        unproject_kernel, "unproject", 6,
        (
            jax.ShapeDtypeStruct((2, 4, 128, 2048), bf16),
            jax.ShapeDtypeStruct((8, 2048), f32),
        )
        + spread_shapes(128, 768)
        + (jax.ShapeDtypeStruct((128, 2048), bf16),)
        + (jax.ShapeDtypeStruct((2, 128, 2048), bf16),) * 2
        + (jax.ShapeDtypeStruct((2, 128, 512), bf16),) * 2,
        [vmem()] * 9 + [hbm(), vmem()] + [hbm()] * 8,
        [vmem(), vmem()] + [hbm()] * 4 + [vmem()] + [hbm()] * 4,
        [
            pltpu.VMEM((2, 2, 512, 128), bf16),
            pltpu.VMEM((2, 2, 512, 128), bf16),
            pltpu.VMEM((1024, 384), bf16),
            pltpu.VMEM((2, 4, 256, 256), bf16),
            pltpu.VMEM((2, 4, 256, 128), bf16),
            pltpu.SemaphoreType.DMA((2, 2)),
            pltpu.SemaphoreType.DMA((2, 2)),
        ]
        + spread_sems(2)
        + [pltpu.VMEM((4, 128, 2048), bf16)]
        + scatter_bufs(128, 2048) + scatter_sems()
        + [
            pltpu.VMEM((2, 2, 128, 2048), bf16),
            pltpu.VMEM((2, 2, 128, 2048), bf16),
            pltpu.VMEM((128, 2048), f32),
            pltpu.SemaphoreType.DMA((2, 3)),
            pltpu.SemaphoreType.DMA((4,)),
            pltpu.SemaphoreType.DMA((4,)),
            pltpu.SemaphoreType.DMA(()),
            pltpu.VMEM((2, 1536, 128), f32),
        ],
        args, flops=10**10, sent=10**7,
    )


def leave_kernel(
    parts, hidden, gain, gmid, gains, qa_send, qa_keep, qb_send, qb_keep, oa_keep, ob_keep, oa_in, ob_in,
    grad_out, ga_out, query_out, key_out, value_out, output_out,
    mine, from_pt, from_up, from_dn, s0, s1, s2, s3, s4, s5,
    acc, over_wid, summed, over_rest, w_s, w_g, t_s, t_g,
    first_q, next_q, then_q, next_o, then_o, kv, n_s, n_g, k_s, k_g,
):
    me = spot()
    r, n, w = me
    partners = [(w != j, (r, n, jnp.int32(j))) for j in range(4)]
    partners += [
        ((r != a) | (n != b), (jnp.int32(a), jnp.int32(b), w)) for a in range(2) for b in range(4)
    ]
    greet(partners)
    x_side, y_side = over_x(r, n, w), over_y(r, n, w)
    q_hops = [
        push(qa_send, first_q.at[0], n_s.at[0], n_g.at[0], x_side),
        push(qb_send, first_q.at[1], n_s.at[1], n_g.at[1], y_side),
    ]
    q_later = [
        push(next_q.at[0], then_q.at[0], n_s.at[2], n_g.at[2], y_side),
        push(next_q.at[1], then_q.at[1], n_s.at[3], n_g.at[3], x_side),
    ]
    o_hops = [
        push(next_o.at[0], then_o.at[0], n_s.at[4], n_g.at[4], y_side),
        push(next_o.at[1], then_o.at[1], n_s.at[5], n_g.at[5], x_side),
    ]
    for hop in q_hops:
        hop.start()
    scatter = Scatter(
        mine, parts.at[1 - r], (from_pt, from_up, from_dn), (s0, s1, s2, s3, s4, s5), me, 4
    )
    for i in range(4):
        scatter.pair(scatter.order(i)).start()

    def wid_copy(j, slot):
        return pltpu.make_async_remote_copy(
            gains, over_wid.at[slot], w_s.at[j], w_g.at[slot],
            device_id=(r, n, jnp.int32(j)), device_id_type=MESH,
        )

    def rest_copy(a, b, slot):
        return pltpu.make_async_remote_copy(
            summed, over_rest.at[slot], t_s.at[a * 4 + b], t_g.at[slot],
            device_id=(jnp.int32(a), jnp.int32(b), w), device_id_type=MESH,
        )

    for j in range(4):
        @pl.when(w != j)
        def _():
            wid_copy(j, w).start()

    for s in range(4):
        def fill(rows):
            mine[s, rows, :] = parts[r, s, rows, :]

        each_rows(128, 16, fill)
    scatter.advance((0, 1, 2, 3), ())
    for j, (keep, came) in enumerate(((oa_keep, oa_in), (ob_keep, ob_in))):
        next_o[j] = (keep[1].astype(f32) + came[1].astype(f32)).astype(bf16)
        o_hops[j].start()
    summed[...] = gains[...]
    for j in range(4):
        @pl.when(w != j)
        def _():
            wid_copy(j, j).wait_recv()
            summed[...] += over_wid[j]

    for a in range(2):
        for b in range(4):
            @pl.when((r != a) | (n != b))
            def _():
                rest_copy(a, b, r * 4 + n).start()

    for j, keep in enumerate((qa_keep, qb_keep)):
        q_hops[j].wait_recv()
        next_q[j] = (keep[1].astype(f32) + first_q[j, 1].astype(f32)).astype(bf16)
        q_later[j].start()
    scatter.advance((), (0, 1))
    for j, keep in enumerate((qa_keep, qb_keep)):
        q_later[j].wait_recv()
        total = keep[0].astype(f32) + first_q[j, 0].astype(f32) + then_q[j].astype(f32)
        query_out[j * 128 : j * 128 + 128, :] = total[:, 0:512]
        kv[w, j * 128 : j * 128 + 128, :] = total[:, 512:768].astype(bf16)

    def kv_copy(j, slot):
        return pltpu.make_async_remote_copy(
            kv.at[w], kv.at[w], k_s.at[j], k_g.at[slot],
            device_id=(r, n, jnp.int32(j)), device_id_type=MESH,
        )

    def kv_wait(j):
        return pltpu.make_async_remote_copy(
            kv.at[j], kv.at[j], k_s.at[j], k_g.at[j],
            device_id=(r, n, jnp.int32(j)), device_id_type=MESH,
        )

    for j in range(4):
        @pl.when(w != j)
        def _():
            kv_copy(j, w).start()

    scatter.advance((), (2, 3))
    for j, (keep, came) in enumerate(((oa_keep, oa_in), (ob_keep, ob_in))):
        o_hops[j].wait_recv()
        output_out[j * 128 : j * 128 + 128, :] = (
            keep[0].astype(f32) + came[0].astype(f32) + then_o[j].astype(f32)
        )
    mine_block = r * 4 + n
    ga_out[0:1] = summed[pl.ds(mine_block, 1), :]
    ga_out[1:2] = summed[pl.ds(mine_block + 8, 1), :]
    for a in range(2):
        for b in range(4):
            @pl.when((r != a) | (n != b))
            def _():
                slot = a * 4 + b
                rest_copy(a, b, slot).wait_recv()
                ga_out[0:1] += over_rest[slot, pl.ds(mine_block, 1), :]
                ga_out[1:2] += over_rest[slot, pl.ds(mine_block + 8, 1), :]

    scatter.total(acc)

    def last(rows):
        grad = norm_back(hidden[rows, :].astype(f32), gain[...], acc[rows, :])
        grad_out[rows, :] = (grad + gmid[rows, :]).astype(bf16)

    each_rows(hidden.shape[0], 16, last)
    lane = lax.broadcasted_iota(jnp.int32, (256, 128), 1)
    for j in range(4):
        @pl.when(w != j)
        def _():
            kv_wait(j).wait_recv()

        even, odd = kv[j, :, 0:128].astype(f32), kv[j, :, 128:256].astype(f32)
        here = slice(j * 128, j * 128 + 128)
        key_out[:, here] = jnp.where(lane < 64, even, pltpu.roll(odd, 64, 1))
        value_out[:, here] = jnp.where(lane < 64, pltpu.roll(even, 64, 1), odd)
    scatter.sent()
    for hop in q_hops + q_later + o_hops:
        hop.wait_send()
    for j in range(4):
        @pl.when(w != j)
        def _():
            kv_copy(j, w).wait_send()

    for j in range(4):
        @pl.when(w != j)
        def _():
            wid_copy(j, w).wait_send()

    for a in range(2):
        for b in range(4):
            @pl.when((r != a) | (n != b))
            def _():
                rest_copy(a, b, r * 4 + n).wait_send()


def leave(*args):
    shard, width = 128, 2048
    grad = jax.ShapeDtypeStruct((256, 512), f32)
    return comm_call(
        leave_kernel, "leave", 7,
        (jax.ShapeDtypeStruct((shard, width), bf16), jax.ShapeDtypeStruct((8, 256), f32))
        + (grad,) * 4,
        [vmem()] * 13, [vmem()] * 6,
        [pltpu.VMEM((4, shard, width), bf16)]
        + scatter_bufs(shard, width) + scatter_sems()
        + [
            pltpu.VMEM((shard, width), f32),
            pltpu.VMEM((4, 16, 256), f32),
            pltpu.VMEM((16, 256), f32),
            pltpu.VMEM((8, 16, 256), f32),
            pltpu.SemaphoreType.DMA((4,)),
            pltpu.SemaphoreType.DMA((4,)),
            pltpu.SemaphoreType.DMA((8,)),
            pltpu.SemaphoreType.DMA((8,)),
            pltpu.VMEM((2, 2, 128, 768), bf16),
            pltpu.VMEM((2, 128, 768), bf16),
            pltpu.VMEM((2, 128, 768), bf16),
            pltpu.VMEM((2, 128, 512), bf16),
            pltpu.VMEM((2, 128, 512), bf16),
            pltpu.VMEM((4, 256, 256), bf16),
            pltpu.SemaphoreType.DMA((6,)),
            pltpu.SemaphoreType.DMA((6,)),
            pltpu.SemaphoreType.DMA((4,)),
            pltpu.SemaphoreType.DMA((4,)),
        ],
        args, flops=10**10, sent=10**8,
    )


def local_fast(
    hidden_in, doc_lengths, w_query, w_key, w_value, w_output, w_gate, w_up, w_down,
    gain_attn, gain_ffn, grad_out,
):
    r, n, w = spot()
    hidden, grad_top = hidden_in[0], grad_out[0]
    gain_a, gain_f = gain_attn[None], gain_ffn[None]
    def half(weight, axis):
        size = weight.shape[axis] // 2
        return lax.dynamic_slice_in_dim(weight, r * size, size, axis)

    head = (w * 2 + r) * HD
    kv_pack = jnp.concatenate(
        [lax.dynamic_slice_in_dim(w_key, head, HD, 1), lax.dynamic_slice_in_dim(w_value, head, HD, 1)],
        axis=1,
    )
    out_half = half(w_output, 0)
    p1_shard = jnp.concatenate(
        [half(w_query, 1), kv_pack, jnp.concatenate([out_half[:, :256], out_half[:, 256:]], axis=0)],
        axis=1,
    )
    down_half = half(w_down, 0)
    p2_shard = jnp.stack(
        [
            half(w_gate, 1),
            half(w_up, 1),
            jnp.concatenate([down_half[:512], down_half[512:]], axis=1),
        ]
    )
    p1 = lax.all_gather(p1_shard, "nar", axis=0)
    p2 = lax.all_gather(p2_shard, "nar", axis=0)

    token_ids = n * 512 + jnp.arange(512, dtype=jnp.int32)
    doc_start, places = doc_layout(doc_lengths[0], token_ids)
    angles = places.astype(f32)[:, None] * inverse_freq()[None, :]
    cosine, sine = jnp.cos(angles), jnp.sin(angles)
    start_here = (doc_start - (n - 2) * 512).astype(f32)
    tab = jnp.concatenate(
        [cosine] * 4 + [-sine, sine] * 2 + [jnp.broadcast_to(start_here[:, None], (512, 128))],
        axis=1,
    )

    rows, tabs = enter(hidden, gain_a, tab)
    rows3, rows2 = rows.reshape(2, 512, 2048), rows.reshape(1024, 2048)
    q, kv, tops = project(rows3, p1, tabs, grad_top)
    low = tabs[:, ::QUERIES, 256].astype(jnp.int32).reshape(8)
    kv_flat = kv.reshape(2, 1536, 128)
    att, lse = attend(low, q, kv_flat, tabs)
    mid, ffn_rows = middle_stage(att, p1, hidden, gain_f)
    parts, total, gain_f_part, a_send, a_keep, b_send, b_keep, ra_dg, rb_dg = ffn_stage(
        ffn_rows.reshape(1024, 2048), tops, grad_top, p2, gain_f
    )
    gmid, datt, oa_send, oa_keep, ob_send, ob_keep, ra_u, rb_u, la_d, lb_d = branch_stage(
        total, mid, grad_top, gain_f, p1, att.reshape(1024, 256),
        a_send, b_send, a_keep, b_keep, ra_dg, rb_dg,
    )
    (
        dparts, gain_a_part, qa_send, qa_keep, qb_send, qb_keep,
        hidden_out, ra_last, rb_last, oa_came, ob_came,
    ) = unproject(
        q, kv_flat, att, datt, lse, rows2, p1, tabs, gain_a, parts, mid,
        a_keep, b_keep, ra_dg, rb_dg, ra_u, rb_u, oa_send, ob_send,
    )
    gains = jnp.concatenate(
        [gain_f_part.sum(axis=0).reshape(8, 256), gain_a_part.sum(axis=0).reshape(8, 256)], axis=0
    )
    grad_in, gain_sums, grad_query, grad_key, grad_value, output_sum = leave(
        dparts, hidden, gain_a, gmid, gains,
        qa_send, qa_keep, qb_send, qb_keep, oa_keep, ob_keep, oa_came, ob_came,
    )

    def joined(which):
        def half_rows(keep, came, last):
            return keep[0, which].astype(f32) + came.astype(f32) + last.astype(f32)

        a_came, b_came, a_last, b_last = (
            (ra_dg[1, 0], rb_dg[1, 0], ra_last[0], rb_last[0]),
            (ra_u[0], rb_u[0], ra_last[1], rb_last[1]),
            (ra_dg[0, 0], rb_dg[0, 0], la_d, lb_d),
        )[which]
        return jnp.concatenate(
            [half_rows(a_keep, a_came, a_last), half_rows(b_keep, b_came, b_last)], axis=0
        )

    return (
        hidden_out[None],
        grad_in[None],
        grad_query,
        grad_key,
        grad_value,
        output_sum.T,
        joined(0),
        joined(1),
        joined(2).T,
        gain_sums[1],
        gain_sums[0],
    )


def solution(mesh):
    in_specs = (
        P("row", ("nar", "wid"), None),
        P("row", None),
        P("nar", "wid"),
        P("nar", None),
        P("nar", None),
        P("wid", "nar"),
        P("nar", "wid"),
        P("nar", "wid"),
        P("wid", "nar"),
        P(),
        P(),
        P("row", ("nar", "wid"), None),
    )
    out_specs = (
        P("row", ("nar", "wid"), None),
        P("row", ("nar", "wid"), None),
        P(("row", "nar"), "wid"),
        P(("row", "nar"), None),
        P(("row", "nar"), None),
        P("wid", ("row", "nar")),
        P(("row", "nar"), "wid"),
        P(("row", "nar"), "wid"),
        P("wid", ("row", "nar")),
        P(("row", "nar")),
        P(("row", "nar")),
    )
    sizes = dict(mesh.shape)
    fits = sizes == {"row": 2, "nar": 4, "wid": 4}

    def body(*args):
        small = args[0].shape == (1, 128, 2048)
        return (local_fast if fits and small else local)(*args)

    return jax.shard_map(body, mesh=mesh, in_specs=in_specs, out_specs=out_specs, check_vma=False)
```

```python
import math

import jax
import jax.numpy as jnp
from jax import lax
from jax.experimental import pallas as pl
from jax.experimental.pallas import tpu as pltpu
from jax.sharding import PartitionSpec as P

H = 32
KV = 8
HD = 64


norm_eps = 1e-05
masked_score = -1e30


def inverse_freq():
    listed = []
    for pair_index in range(HD // 2):
        base_freq = 500000.0 ** (-2.0 * pair_index / HD)
        wavelength = 2.0 * math.pi / base_freq
        smoothing = (8192.0 / wavelength - 1.0) / 3.0
        blended = (1.0 - smoothing) * base_freq / 32.0 + smoothing * base_freq
        if wavelength < 2048.0:
            listed.append(base_freq)
        elif wavelength > 8192.0:
            listed.append(base_freq / 32.0)
        else:
            listed.append(blended)
    return jnp.asarray(listed, dtype=jnp.float32)


def rotate(values, cosine_table, sine_table):
    half_dim = HD // 2
    first_half = values[..., :half_dim]
    second_half = values[..., half_dim:]
    return jnp.concatenate(
        [
            first_half * cosine_table - second_half * sine_table,
            second_half * cosine_table + first_half * sine_table,
        ],
        axis=-1,
    )


def rotate_back(grads_in, cosine_table, sine_table):
    half_dim = HD // 2
    first_half = grads_in[..., :half_dim]
    second_half = grads_in[..., half_dim:]
    return jnp.concatenate(
        [
            first_half * cosine_table + second_half * sine_table,
            second_half * cosine_table - first_half * sine_table,
        ],
        axis=-1,
    )


def doc_layout(lengths_row, token_ids):
    ends_at = jnp.cumsum(lengths_row, dtype=jnp.int32)
    starts_at = ends_at - lengths_row
    inside = (token_ids[:, None] >= starts_at[None, :]) & (token_ids[:, None] < ends_at[None, :])
    doc_start = jnp.sum(jnp.where(inside, starts_at[None, :], 0), axis=1, dtype=jnp.int32)
    return (doc_start, token_ids - doc_start)


def norm_forward(values, gain_vector):
    root_inv = lax.rsqrt(jnp.mean(values * values, axis=-1, keepdims=True) + norm_eps)
    return (root_inv, (values * root_inv * gain_vector).astype(jnp.bfloat16))


def norm_backward(values, root_inv, gain_vector, grad_normed):
    weighted = grad_normed * gain_vector
    inner_sum = jnp.mean(weighted * values, axis=-1, keepdims=True)
    grad_values = root_inv * weighted - values * (root_inv * root_inv * root_inv) * inner_sum
    gain_term = jnp.sum(grad_normed * values * root_inv, axis=0)
    return (grad_values, gain_term)


def contract_last(left_side, right_side):
    return lax.dot_general(
        left_side, right_side, (((1,), (1,)), ((), ())), preferred_element_type=jnp.float32
    )


def contract_first(left_side, right_side):
    return lax.dot_general(
        left_side, right_side, (((0,), (0,)), ((), ())), preferred_element_type=jnp.float32
    )


def local(
    hidden_in,
    doc_lengths,
    w_query,
    w_key,
    w_value,
    w_output,
    w_gate,
    w_up,
    w_down,
    gain_attn,
    gain_ffn,
    grad_out,
):
    wid_count = lax.axis_size("wid")
    nar_count = lax.axis_size("nar")
    wid_index = lax.axis_index("wid")
    nar_index = lax.axis_index("nar")
    local_tokens = hidden_in.shape[1]
    block_tokens = local_tokens * wid_count
    seq_length = block_tokens * nar_count
    query_heads = w_query.shape[1] // HD
    group_size = H // KV
    kv_local = max(query_heads // group_size, 1)
    heads_per_kv = query_heads // kv_local
    kv_first = wid_index * query_heads // group_size
    query_block = min(512, block_tokens)
    block_count = block_tokens // query_block
    item_count = block_count * query_heads
    attn_scale = HD ** (-0.5)
    query_full, key_full, value_full, output_full, gate_full, up_full, down_full = (
        lax.all_gather(w_query, "nar", axis=0, tiled=True),
        lax.all_gather(w_key, "nar", axis=0, tiled=True),
        lax.all_gather(w_value, "nar", axis=0, tiled=True),
        lax.all_gather(w_output, "nar", axis=1, tiled=True),
        lax.all_gather(w_gate, "nar", axis=0, tiled=True),
        lax.all_gather(w_up, "nar", axis=0, tiled=True),
        lax.all_gather(w_down, "nar", axis=1, tiled=True),
    )
    key_local = lax.dynamic_slice_in_dim(key_full, kv_first * HD, kv_local * HD, 1)
    value_local = lax.dynamic_slice_in_dim(value_full, kv_first * HD, kv_local * HD, 1)
    token_ids = nar_index * block_tokens + jnp.arange(block_tokens, dtype=jnp.int32)
    doc_start, places = doc_layout(doc_lengths[0], token_ids)
    angles = places.astype(jnp.float32)[:, None] * inverse_freq()[None, :]
    cosine_table = jnp.cos(angles)[:, None, :]
    sine_table = jnp.sin(angles)[:, None, :]
    key_ids = jnp.arange(seq_length, dtype=jnp.int32)
    residual = hidden_in[0].astype(jnp.float32)
    root_attn, normed_attn = norm_forward(residual, gain_attn)
    normed_rows = lax.all_gather(normed_attn, "wid", axis=0, tiled=True)
    query_pre = jnp.dot(normed_rows, query_full, preferred_element_type=jnp.float32)
    key_pre = jnp.dot(normed_rows, key_local, preferred_element_type=jnp.float32)
    value_rows = jnp.dot(normed_rows, value_local, preferred_element_type=jnp.float32).astype(
        jnp.bfloat16
    )
    query_rot = (
        rotate(query_pre.reshape(block_tokens, query_heads, HD), cosine_table, sine_table)
        .astype(jnp.bfloat16)
        .reshape(block_tokens, query_heads * HD)
    )
    key_rot = (
        rotate(key_pre.reshape(block_tokens, kv_local, HD), cosine_table, sine_table)
        .astype(jnp.bfloat16)
        .reshape(block_tokens, kv_local * HD)
    )
    key_seq, value_seq = (
        lax.all_gather(key_rot, "nar", axis=0, tiled=True),
        lax.all_gather(value_rows, "nar", axis=0, tiled=True),
    )

    def item_inputs(item_index):
        block_index = item_index // query_heads
        head_index = item_index % query_heads
        kv_index = head_index // heads_per_kv
        row_first = block_index * query_block
        query_part = lax.dynamic_slice(query_rot, (row_first, head_index * HD), (query_block, HD))
        key_head = lax.dynamic_slice_in_dim(key_seq, kv_index * HD, HD, 1)
        value_head = lax.dynamic_slice_in_dim(value_seq, kv_index * HD, HD, 1)
        query_ids = lax.dynamic_slice_in_dim(token_ids, row_first, query_block, 0)
        query_starts = lax.dynamic_slice_in_dim(doc_start, row_first, query_block, 0)
        allowed = (key_ids[None, :] <= query_ids[:, None]) & (
            key_ids[None, :] >= query_starts[:, None]
        )
        scores = contract_last(query_part, key_head) * attn_scale
        return (
            row_first,
            head_index,
            kv_index,
            query_part,
            key_head,
            value_head,
            jnp.where(allowed, scores, masked_score),
        )

    def attend(item_index):
        row_first, head_index, kv_index, query_part, key_head, value_head, scores = item_inputs(
            item_index
        )
        row_max = jnp.max(scores, axis=1, keepdims=True)
        exp_scores = jnp.exp(scores - row_max)
        row_total = jnp.sum(exp_scores, axis=1, keepdims=True)
        probability = (exp_scores / row_total).astype(jnp.bfloat16)
        attended = jnp.dot(probability, value_head, preferred_element_type=jnp.float32)
        return (attended, (row_max + jnp.log(row_total))[:, 0])

    attended_items, logsum_items = lax.map(attend, jnp.arange(item_count, dtype=jnp.int32))
    attended_rows = (
        attended_items.reshape(block_count, query_heads, query_block, HD)
        .transpose(0, 2, 1, 3)
        .reshape(block_tokens, query_heads * HD)
        .astype(jnp.bfloat16)
    )
    rows_here = attended_rows
    branch_attn = lax.psum_scatter(
        jnp.dot(rows_here, output_full, preferred_element_type=jnp.float32),
        "wid",
        scatter_dimension=0,
        tiled=True,
    )
    middle = residual + branch_attn
    root_ffn, normed_ffn = norm_forward(middle, gain_ffn)
    ffn_rows = lax.all_gather(normed_ffn, "wid", axis=0, tiled=True)
    gate_proj = jnp.dot(ffn_rows, gate_full, preferred_element_type=jnp.float32)
    up_proj = jnp.dot(ffn_rows, up_full, preferred_element_type=jnp.float32)
    gate_sigmoid = jax.nn.sigmoid(gate_proj)
    gate_silu = gate_proj * gate_sigmoid
    activated = (gate_silu * up_proj).astype(jnp.bfloat16)
    rows_here = activated
    branch_ffn = lax.psum_scatter(
        jnp.dot(rows_here, down_full, preferred_element_type=jnp.float32).astype(jnp.bfloat16),
        "wid",
        scatter_dimension=0,
        tiled=True,
    ).astype(jnp.float32)
    hidden_out = (middle + branch_ffn).astype(jnp.bfloat16)[None]
    grad_top = grad_out[0]
    grad_rows = lax.all_gather(grad_top, "wid", axis=0, tiled=True)
    grad_activated = contract_last(grad_rows, down_full)
    down_weight_grad = contract_first(activated, grad_rows)
    silu_slope = gate_sigmoid * (1.0 + gate_proj * (1.0 - gate_sigmoid))
    grad_gate_b = (grad_activated * up_proj * silu_slope).astype(jnp.bfloat16)
    grad_up_b = (grad_activated * gate_silu).astype(jnp.bfloat16)
    gate_weight_grad = contract_first(ffn_rows, grad_gate_b)
    up_weight_grad = contract_first(ffn_rows, grad_up_b)
    grad_normed_ffn = lax.psum_scatter(
        contract_last(grad_gate_b, gate_full) + contract_last(grad_up_b, up_full),
        "wid",
        scatter_dimension=0,
        tiled=True,
    )
    grad_middle, gain_ffn_term = norm_backward(middle, root_ffn, gain_ffn, grad_normed_ffn)
    grad_middle = grad_middle + grad_top.astype(jnp.float32)
    grad_branch = grad_middle.astype(jnp.bfloat16)
    branch_rows = lax.all_gather(grad_branch, "wid", axis=0, tiled=True)
    grad_attended = contract_last(branch_rows, output_full).astype(jnp.bfloat16)
    output_weight_grad = contract_first(attended_rows, branch_rows)

    def attend_back(carried, item_index):
        key_grad, value_grad = carried
        row_first, head_index, kv_index, query_part, key_head, value_head, scores = item_inputs(
            item_index
        )
        logsum = lax.dynamic_index_in_dim(logsum_items, item_index, 0, keepdims=False)
        probability = jnp.exp(scores - logsum[:, None])
        grad_part = lax.dynamic_slice(
            grad_attended, (row_first, head_index * HD), (query_block, HD)
        )
        grad_prob = contract_last(grad_part, value_head)
        inner_sum = jnp.sum(probability * grad_prob, axis=1, keepdims=True)
        grad_scores = (probability * (grad_prob - inner_sum)).astype(jnp.bfloat16)
        query_grad = jnp.dot(grad_scores, key_head, preferred_element_type=jnp.float32) * attn_scale
        key_part = contract_first(grad_scores, query_part) * attn_scale
        value_part = contract_first(probability.astype(jnp.bfloat16), grad_part)
        key_old = lax.dynamic_slice_in_dim(key_grad, kv_index * HD, HD, 1)
        key_grad = lax.dynamic_update_slice_in_dim(key_grad, key_old + key_part, kv_index * HD, 1)
        value_old = lax.dynamic_slice_in_dim(value_grad, kv_index * HD, HD, 1)
        value_grad = lax.dynamic_update_slice_in_dim(
            value_grad, value_old + value_part, kv_index * HD, 1
        )
        return ((key_grad, value_grad), query_grad)

    zero_grads = jnp.zeros((seq_length, kv_local * HD), jnp.float32)
    (key_grad_seq, value_grad_seq), query_grad_items = lax.scan(
        attend_back, (zero_grads, zero_grads), jnp.arange(item_count, dtype=jnp.int32)
    )
    key_grad_block, value_grad_block = (
        lax.psum_scatter(
            key_grad_seq.astype(jnp.bfloat16), "nar", scatter_dimension=0, tiled=True
        ).astype(jnp.float32),
        lax.psum_scatter(
            value_grad_seq.astype(jnp.bfloat16), "nar", scatter_dimension=0, tiled=True
        ).astype(jnp.float32),
    )
    query_grad_rows = (
        query_grad_items.reshape(block_count, query_heads, query_block, HD)
        .transpose(0, 2, 1, 3)
        .reshape(block_tokens, query_heads, HD)
    )
    query_grad_b = (
        rotate_back(query_grad_rows, cosine_table, sine_table)
        .astype(jnp.bfloat16)
        .reshape(block_tokens, query_heads * HD)
    )
    key_grad_b = (
        rotate_back(key_grad_block.reshape(block_tokens, kv_local, HD), cosine_table, sine_table)
        .astype(jnp.bfloat16)
        .reshape(block_tokens, kv_local * HD)
    )
    value_grad_b = value_grad_block.astype(jnp.bfloat16)
    query_weight_grad = contract_first(normed_rows, query_grad_b)
    key_weight_grad = contract_first(normed_rows, key_grad_b)
    value_weight_grad = contract_first(normed_rows, value_grad_b)
    grad_normed_attn = lax.psum_scatter(
        (
            contract_last(query_grad_b, query_full)
            + contract_last(key_grad_b, key_local)
            + contract_last(value_grad_b, value_local)
        ).astype(jnp.bfloat16),
        "wid",
        scatter_dimension=0,
        tiled=True,
    ).astype(jnp.float32)
    grad_residual, gain_attn_term = norm_backward(residual, root_attn, gain_attn, grad_normed_attn)
    grad_in = (grad_residual + grad_middle).astype(jnp.bfloat16)[None]
    summed = (
        lax.psum_scatter(
            query_weight_grad.astype(jnp.bfloat16), ("row", "nar"), scatter_dimension=0, tiled=True
        ).astype(jnp.float32),
        lax.psum_scatter(
            key_weight_grad.astype(jnp.bfloat16), ("row", "nar"), scatter_dimension=0, tiled=True
        ).astype(jnp.float32),
        lax.psum_scatter(
            value_weight_grad.astype(jnp.bfloat16), ("row", "nar"), scatter_dimension=0, tiled=True
        ).astype(jnp.float32),
        lax.psum_scatter(
            output_weight_grad.astype(jnp.bfloat16), ("row", "nar"), scatter_dimension=1, tiled=True
        ).astype(jnp.float32),
        lax.psum_scatter(
            gate_weight_grad.astype(jnp.bfloat16), ("row", "nar"), scatter_dimension=0, tiled=True
        ).astype(jnp.float32),
        lax.psum_scatter(
            up_weight_grad.astype(jnp.bfloat16), ("row", "nar"), scatter_dimension=0, tiled=True
        ).astype(jnp.float32),
        lax.psum_scatter(
            down_weight_grad.astype(jnp.bfloat16), ("row", "nar"), scatter_dimension=1, tiled=True
        ).astype(jnp.float32),
        lax.psum_scatter(
            gain_attn_term.astype(jnp.bfloat16), ("row", "nar"), scatter_dimension=0, tiled=True
        ).astype(jnp.float32),
        lax.psum_scatter(
            gain_ffn_term.astype(jnp.bfloat16), ("row", "nar"), scatter_dimension=0, tiled=True
        ).astype(jnp.float32),
    )
    (
        grad_query,
        key_sum,
        value_sum,
        grad_output,
        grad_gate,
        grad_up,
        grad_down,
        gain_attn_sum,
        gain_ffn_sum,
    ) = summed
    key_all, value_all, gain_attn_all, gain_ffn_all = (
        lax.all_gather(key_sum.astype(jnp.bfloat16), "wid", axis=1, tiled=True).astype(
            key_sum.dtype
        ),
        lax.all_gather(value_sum.astype(jnp.bfloat16), "wid", axis=1, tiled=True).astype(
            value_sum.dtype
        ),
        lax.all_gather(gain_attn_sum.astype(jnp.bfloat16), "wid", axis=0, tiled=True).astype(
            gain_attn_sum.dtype
        ),
        lax.all_gather(gain_ffn_sum.astype(jnp.bfloat16), "wid", axis=0, tiled=True).astype(
            gain_ffn_sum.dtype
        ),
    )
    shard_rows = key_sum.shape[0]
    repeats = wid_count * kv_local // KV
    grad_key = key_all.reshape(shard_rows, KV, repeats, HD).sum(axis=2).reshape(shard_rows, KV * HD)
    grad_value = (
        value_all.reshape(shard_rows, KV, repeats, HD).sum(axis=2).reshape(shard_rows, KV * HD)
    )
    grad_gain_attn = gain_attn_all.reshape(wid_count, shard_rows).sum(axis=0)
    grad_gain_ffn = gain_ffn_all.reshape(wid_count, shard_rows).sum(axis=0)
    return (
        hidden_out,
        grad_in,
        grad_query,
        grad_key,
        grad_value,
        grad_output,
        grad_gate,
        grad_up,
        grad_down,
        grad_gain_attn,
        grad_gain_ffn,
    )


MESH = pl.DeviceIdType.MESH
bf16 = jnp.bfloat16
f32 = jnp.float32
VMEM_LIMIT = 60 * 2**20


def spot():
    return lax.axis_index("row"), lax.axis_index("nar"), lax.axis_index("wid")


def greet(partners):
    barrier = pltpu.get_barrier_semaphore()
    total = 0
    for there, device in partners:
        @pl.when(there)
        def _():
            pl.semaphore_signal(barrier, inc=1, device_id=device, device_id_type=MESH)

        total = total + there.astype(jnp.int32)
    pl.semaphore_wait(barrier, total)


def line_partners(r, n, w, wid_count):
    return [
        (w < wid_count - 1, (r, n, jnp.minimum(w + 1, wid_count - 1))),
        (w > 0, (r, n, jnp.maximum(w - 1, 0))),
        (w >= 0, (1 - r, n, w)),
    ]


def each_rows(count, step, body):
    def run(i, carry):
        body(pl.ds(pl.multiple_of(i * step, step), step))
        return carry

    lax.fori_loop(0, count // step, run, 0)


def square_partners(r, n, w):
    return [(n >= 0, over_x(r, n, w)), (n >= 0, over_y(r, n, w))]


def over_x(r, n, w):
    return (r, n + 1 - 2 * (n % 2), w)


def over_y(r, n, w):
    return (r, (n + 2) % 4, w)


def push(source, target, s_s, s_g, device):
    return pltpu.make_async_remote_copy(
        source, target, s_s, s_g, device_id=device, device_id_type=MESH
    )


class Gather:
    def __init__(self, buf, sems, me, wid_count, rows=slice(None)):
        self.rows = rows
        self.buf, (self.up_s, self.dn_s, self.pt_s, self.got) = buf, sems
        self.r, self.n, self.w = me
        self.last = wid_count - 1
        self.up = (self.r, self.n, jnp.minimum(self.w + 1, self.last))
        self.dn = (self.r, self.n, jnp.maximum(self.w - 1, 0))
        self.pt = (1 - self.r, self.n, self.w)

    def copy(self, j, sem, device, row=None):
        row = self.r if row is None else row
        return pltpu.make_async_remote_copy(
            self.buf.at[row, j, self.rows],
            self.buf.at[row, j, self.rows],
            sem.at[j],
            self.got.at[row, j],
            device_id=device,
            device_id_type=MESH,
        )

    def pass_on(self, j, go_up, go_dn):
        if go_up:
            @pl.when(self.w < self.last)
            def _():
                self.copy(j, self.up_s, self.up).start()

        if go_dn:
            @pl.when(self.w > 0)
            def _():
                self.copy(j, self.dn_s, self.dn).start()

        self.copy(j, self.pt_s, self.pt).start()

    def own(self):
        self.pass_on(self.w, True, True)

    def arrive(self, row, j):
        self.copy(j, self.pt_s, self.pt, row).wait_recv()

    def step(self, k):
        below, above = self.w - k, self.w + k

        @pl.when(below >= 0)
        def _():
            self.arrive(self.r, below)
            self.pass_on(below, True, False)

        @pl.when(above <= self.last)
        def _():
            self.arrive(self.r, above)
            self.pass_on(above, False, True)

    def advance(self, edge_steps, inner_steps):
        at_end = (self.w == 0) | (self.w == self.last)
        for ends, steps in ((True, edge_steps), (False, inner_steps)):
            if steps:
                @pl.when(at_end if ends else jnp.logical_not(at_end))
                def _():
                    for k in steps:
                        self.step(k)

    def rest(self):
        for j in range(self.last + 1):
            self.arrive(1 - self.r, j)

    def sent(self):
        for j in range(self.last + 1):
            @pl.when((j <= self.w) & (self.w < self.last))
            def _():
                self.copy(j, self.up_s, self.up).wait_send()

            @pl.when((j >= self.w) & (self.w > 0))
            def _():
                self.copy(j, self.dn_s, self.dn).wait_send()

            self.copy(j, self.pt_s, self.pt).wait_send()


def gather_scratch(shard, width):
    return [pltpu.VMEM((2, 4, shard, width), bf16)] + gather_sems()


def gather_sems():
    return [pltpu.SemaphoreType.DMA((4,))] * 3 + [pltpu.SemaphoreType.DMA((2, 4))]


class Scatter:
    def __init__(self, mine, theirs, bufs, sems, me, wid_count, first=0, count=None):
        self.mine, self.theirs = mine, theirs
        self.from_pt, self.from_up, self.from_dn = bufs
        self.pt_s, self.pt_g, self.up_s, self.up_g, self.dn_s, self.dn_g = sems
        self.r, self.n, self.w = me
        self.first, self.count = first, mine.shape[1] if count is None else count
        self.rows = pl.ds(first, self.count)
        self.last = wid_count - 1
        self.up = (self.r, self.n, jnp.minimum(self.w + 1, self.last))
        self.dn = (self.r, self.n, jnp.maximum(self.w - 1, 0))
        self.pt = (1 - self.r, self.n, self.w)

    def order(self, i):
        low = jnp.where(i == 0, 3, jnp.where(i == 1, 0, jnp.where(i == 2, 2, 1)))
        return jnp.where(self.w < 2, low, 3 - low)

    def send(self, source, target, sent, got, s, device):
        return pltpu.make_async_remote_copy(
            source.at[s, self.rows], target.at[s, self.rows], sent.at[s], got.at[s],
            device_id=device, device_id_type=MESH,
        )

    def pair(self, s):
        return self.send(self.theirs, self.from_pt, self.pt_s, self.pt_g, s, self.pt)

    def climb(self, s):
        return self.send(self.mine, self.from_dn, self.up_s, self.up_g, s, self.up)

    def fall(self, s):
        return self.send(self.mine, self.from_up, self.dn_s, self.dn_g, s, self.dn)

    def each(self, body):
        def run(i, carry):
            body(pl.ds(pl.multiple_of(self.first + i * 16, 16), 16))
            return carry

        lax.fori_loop(0, self.count // 16, run, 0)

    def add(self, s, others):
        def body(rows):
            total = self.mine[s, rows, :].astype(f32)
            for other in others:
                total = total + other[s, rows, :].astype(f32)
            self.mine[s, rows, :] = total.astype(bf16)

        self.each(body)

    def step(self, s):
        self.pair(s).wait_recv()

        @pl.when((s > self.w) & (self.w > 0))
        def _():
            self.climb(s).wait_recv()
            self.add(s, (self.from_pt, self.from_dn))

        @pl.when((s < self.w) & (self.w < self.last))
        def _():
            self.fall(s).wait_recv()
            self.add(s, (self.from_pt, self.from_up))

        @pl.when(((s > self.w) & (self.w == 0)) | ((s < self.w) & (self.w == self.last)))
        def _():
            self.add(s, (self.from_pt,))

        @pl.when(s > self.w)
        def _():
            self.climb(s).start()

        @pl.when(s < self.w)
        def _():
            self.fall(s).start()

    def advance(self, edge_steps, inner_steps):
        for ends, steps in ((True, edge_steps), (False, inner_steps)):
            at_end = (self.w == 0) | (self.w == self.last)

            def body(i, carry):
                self.step(self.order(i))
                return carry

            if steps:
                @pl.when(at_end if ends else jnp.logical_not(at_end))
                def _():
                    lax.fori_loop(steps[0], steps[-1] + 1, body, 0)

    def total(self, out):
        w = self.w

        def first(rows):
            out[rows, :] = self.mine[w, rows, :].astype(f32) + self.from_pt[w, rows, :].astype(f32)

        self.each(first)

        @pl.when(w > 0)
        def _():
            self.climb(w).wait_recv()

            def more(rows):
                out[rows, :] += self.from_dn[w, rows, :].astype(f32)

            self.each(more)

        @pl.when(w < self.last)
        def _():
            self.fall(w).wait_recv()

            def more(rows):
                out[rows, :] += self.from_up[w, rows, :].astype(f32)

            self.each(more)

    def sent(self):
        for s in range(self.last + 1):
            self.pair(s).wait_send()

            @pl.when(s > self.w)
            def _():
                self.climb(s).wait_send()

            @pl.when(s < self.w)
            def _():
                self.fall(s).wait_send()


def scatter_bufs(shard, width):
    return [pltpu.VMEM((4, shard, width), bf16)] * 3


def scatter_sems():
    return [pltpu.SemaphoreType.DMA((4,))] * 6


def vmem():
    return pl.BlockSpec(memory_space=pltpu.VMEM)


def hbm():
    return pl.BlockSpec(memory_space=pl.ANY)


def comm_call(kernel, name, cid, out_shape, in_specs, out_specs, scratch, args, flops=0, sent=0):
    return pl.pallas_call(
        kernel,
        out_shape=out_shape,
        in_specs=in_specs,
        out_specs=out_specs,
        scratch_shapes=scratch,
        compiler_params=pltpu.CompilerParams(
            collective_id=cid, has_side_effects=True, vmem_limit_bytes=VMEM_LIMIT
        ),
        cost_estimate=pl.CostEstimate(flops=flops, bytes_accessed=sent, transcendentals=0),
        name=name,
    )(*args)


def norm_rows(x, gain):
    root = lax.rsqrt(jnp.mean(x * x, axis=-1, keepdims=True) + norm_eps)
    return x * root * gain


def turn(x, cosine, sine):
    lane = lax.broadcasted_iota(jnp.int32, x.shape, 1)
    swapped = jnp.where(lane % 64 < 32, pltpu.roll(x, 96, 1), pltpu.roll(x, 32, 1))
    return x * cosine + swapped * sine


def enter_kernel(hidden, gain, tab, rows_out, tabs_out, buf, up_s, dn_s, pt_s, got, tabs, tab_s, tab_g, out_s):
    me = spot()
    r, n, w = me
    greet(line_partners(r, n, w, 4))
    gather = Gather(buf, (up_s, dn_s, pt_s, got), me, 4)
    tab_copy = pltpu.make_async_remote_copy(
        tab, tabs.at[r], tab_s, tab_g, device_id=(1 - r, n, w), device_id_type=MESH
    )

    def body(rows):
        buf[r, w, rows, :] = norm_rows(hidden[rows, :].astype(f32), gain[...]).astype(bf16)

    each_rows(hidden.shape[0], 16, body)
    gather.own()
    tab_copy.start()

    def keep(rows):
        tabs[r, rows, :] = tab[rows, :]

    each_rows(tab.shape[0], 16, keep)
    for k in (1, 2, 3):
        gather.step(k)
    gather.rest()
    out = pltpu.make_async_copy(buf, rows_out, out_s.at[0])
    out.start()
    tab_copy.wait_recv()
    out_tab = pltpu.make_async_copy(tabs, tabs_out, out_s.at[1])
    out_tab.start()
    gather.sent()
    tab_copy.wait_send()
    out.wait()
    out_tab.wait()


def enter(hidden, gain, tab):
    shard, width = hidden.shape
    return comm_call(
        enter_kernel, "enter", 1,
        (
            jax.ShapeDtypeStruct((2, 4, shard, width), bf16),
            jax.ShapeDtypeStruct((2,) + tab.shape, f32),
        ),
        [vmem()] * 3, [hbm()] * 2,
        gather_scratch(shard, width)
        + [
            pltpu.VMEM((2,) + tab.shape, f32),
            pltpu.SemaphoreType.DMA(()),
            pltpu.SemaphoreType.DMA(()),
            pltpu.SemaphoreType.DMA((2,)),
        ],
        (hidden, gain, tab), flops=10**10, sent=10**8,
    )


def nar_device(r, n, w, by):
    return (r, jnp.clip(n + by, 0, 3), w)


def project_kernel(
    x, p1, tabs, grad_top, q_out, kv_out, tops_out, kv, s_s, s_g, out_s, buf, g0, g1, g2, g3, tops_s
):
    r, n, w = spot()
    greet(
        line_partners(r, n, w, 4)
        + [
            (n >= 1, nar_device(r, n, w, -1)),
            (n >= 2, nar_device(r, n, w, -2)),
            (n <= 2, nar_device(r, n, w, 1)),
            (n <= 1, nar_device(r, n, w, 2)),
        ]
    )
    gather = Gather(buf, (g0, g1, g2, g3), (r, n, w), 4)

    def keep(rows):
        buf[r, w, rows, :] = grad_top[rows, :]

    each_rows(64, 16, keep)
    gather.own()

    def copy(row, slot, by):
        return pltpu.make_async_remote_copy(
            kv.at[row, 2], kv.at[row, slot], s_s.at[row, slot], s_g.at[row, slot],
            device_id=nar_device(r, n, w, by), device_id_type=MESH,
        )

    lane = lax.broadcasted_iota(jnp.int32, (256, 128), 1)
    weight = p1[:, :, 0:384].reshape(2048, 384)
    for row in range(2):
        def tile(i, carry):
            rows = pl.ds(pl.multiple_of(i * 256, 256), 256)
            cosine, sine = tabs[row, rows, 0:128], tabs[row, rows, 128:256]
            pre = jnp.dot(x[row, rows, :], weight, preferred_element_type=f32)
            q_out[row, rows, 0:128] = turn(pre[:, 0:128], cosine, sine).astype(bf16)
            q_out[row, rows, 128:256] = turn(pre[:, 128:256], cosine, sine).astype(bf16)
            both = pre[:, 256:384]
            kv[row, 2, rows, :] = jnp.where(lane < 64, turn(both, cosine, sine), both).astype(bf16)
            return carry

        lax.fori_loop(0, 2, tile, 0)

        @pl.when(n <= 2)
        def _():
            copy(row, 1, 1).start()

        @pl.when(n <= 1)
        def _():
            copy(row, 0, 2).start()

        for slot, least in ((1, 1), (0, 2)):
            @pl.when(n < least)
            def _():
                kv[row, slot] = jnp.zeros((512, 128), bf16)

    for k in (1, 2, 3):
        gather.step(k)
    gather.rest()
    tops_copy = pltpu.make_async_copy(buf, tops_out, tops_s)
    tops_copy.start()
    for row in range(2):
        for slot, least, by in ((1, 1, 1), (0, 2, 2)):
            @pl.when(n >= least)
            def _():
                copy(row, slot, by).wait_recv()

    out = pltpu.make_async_copy(kv, kv_out, out_s)
    out.start()
    for row in range(2):
        @pl.when(n <= 2)
        def _():
            copy(row, 1, 1).wait_send()

        @pl.when(n <= 1)
        def _():
            copy(row, 0, 2).wait_send()

    gather.sent()
    out.wait()
    tops_copy.wait()


def project(x, p1, tabs, grad_top):
    return comm_call(
        project_kernel, "project", 2,
        (
            jax.ShapeDtypeStruct((2, 512, 256), bf16),
            jax.ShapeDtypeStruct((2, 3, 512, 128), bf16),
            jax.ShapeDtypeStruct((2, 4, 64, 2048), bf16),
        ),
        [vmem()] * 4, [vmem(), hbm(), hbm()],
        [
            pltpu.VMEM((2, 3, 512, 128), bf16),
            pltpu.SemaphoreType.DMA((2, 3)),
            pltpu.SemaphoreType.DMA((2, 3)),
            pltpu.SemaphoreType.DMA(()),
        ]
        + gather_scratch(64, 2048)
        + [pltpu.SemaphoreType.DMA(())],
        (x, p1, tabs, grad_top), flops=10**10, sent=10**7,
    )


KEYS = 256
QUERIES = 128


def stack_low(x):
    lane = lax.broadcasted_iota(jnp.int32, (QUERIES, 128), 1)
    zero = jnp.zeros((QUERIES, 128), x.dtype)
    parts = []
    for pair in range(2):
        block = x[:, pair * 128 : pair * 128 + 128]
        parts.append(jnp.where(lane < 64, block, zero))
        parts.append(jnp.where(lane < 64, pltpu.roll(block, 64, 1), zero))
    return jnp.concatenate(parts, axis=0)


def stack_high(x):
    lane = lax.broadcasted_iota(jnp.int32, (QUERIES, 128), 1)
    zero = jnp.zeros((QUERIES, 128), x.dtype)
    parts = []
    for pair in range(2):
        block = x[:, pair * 128 : pair * 128 + 128]
        parts.append(jnp.where(lane >= 64, pltpu.roll(block, 64, 1), zero))
        parts.append(jnp.where(lane >= 64, block, zero))
    return jnp.concatenate(parts, axis=0)


def unstack(x, low):
    lane = lax.broadcasted_iota(jnp.int32, (QUERIES, 128), 1)
    out = []
    for pair in range(2):
        even = x[2 * pair * QUERIES : (2 * pair + 1) * QUERIES]
        odd = x[(2 * pair + 1) * QUERIES : (2 * pair + 2) * QUERIES]
        if low:
            out.append(jnp.where(lane < 64, even, pltpu.roll(odd, 64, 1)))
        else:
            out.append(jnp.where(lane < 64, pltpu.roll(even, 64, 1), odd))
    return jnp.concatenate(out, axis=1)


def allowed_tile(starts, tile, first_query):
    key = lax.broadcasted_iota(jnp.int32, (QUERIES, KEYS), 1) + tile * KEYS
    query = lax.broadcasted_iota(jnp.int32, (QUERIES, KEYS), 0) + first_query
    start = jnp.concatenate([starts] * (KEYS // 128), axis=1)
    ok = (key <= query) & (key.astype(f32) >= start)
    return jnp.concatenate([ok] * 4, axis=0)


def key_tiles(low, row, block):
    first_query = 1024 + block * QUERIES
    return low[row * 4 + block] // KEYS, first_query // KEYS + 1, first_query


def attend_kernel(low, q, kv, starts, out, lse):
    row, block = pl.program_id(0), pl.program_id(1)
    first, end, first_query = key_tiles(low, row, block)
    query = stack_low(q[0].astype(f32)).astype(bf16)

    def body(tile, carry):
        top, total, acc = carry
        both = kv[0, pl.ds(pl.multiple_of(tile * KEYS, KEYS), KEYS), :]
        scores = contract_last(query, both) * 0.125
        ok = allowed_tile(starts[0], tile, first_query)
        scores = jnp.where(ok, scores, masked_score)
        new_top = jnp.maximum(top, jnp.max(scores, axis=1, keepdims=True))
        shrink = jnp.exp(top - new_top)
        part = jnp.exp(scores - new_top)
        total = total * shrink + jnp.sum(part, axis=1, keepdims=True)
        acc = acc * shrink + jnp.dot(part.astype(bf16), both, preferred_element_type=f32)
        return new_top, total, acc

    top, total, acc = lax.fori_loop(
        first, end, body,
        (
            jnp.full((4 * QUERIES, 1), masked_score, f32),
            jnp.zeros((4 * QUERIES, 1), f32),
            jnp.zeros((4 * QUERIES, 128), f32),
        ),
    )
    out[0] = unstack(acc / total, False).astype(bf16)
    lse[0, 0] = jnp.broadcast_to(top + jnp.log(total), (4 * QUERIES, 128))


def attend_specs():
    return [
        pl.BlockSpec((1, QUERIES, 256), lambda i, j, low: (i, j, 0)),
        pl.BlockSpec((1, 1536, 128), lambda i, j, low: (i, 0, 0)),
        pl.BlockSpec((1, QUERIES, 128), lambda i, j, low: (i, j, 2)),
    ]


def attend(low, q, kv, tabs):
    return pl.pallas_call(
        attend_kernel,
        out_shape=(
            jax.ShapeDtypeStruct((2, 512, 256), bf16),
            jax.ShapeDtypeStruct((2, 4, 4 * QUERIES, 128), f32),
        ),
        grid_spec=pltpu.PrefetchScalarGridSpec(
            num_scalar_prefetch=1, grid=(2, 4),
            in_specs=attend_specs(),
            out_specs=[
                pl.BlockSpec((1, QUERIES, 256), lambda i, j, low: (i, j, 0)),
                pl.BlockSpec((1, 1, 4 * QUERIES, 128), lambda i, j, low: (i, j, 0, 0)),
            ],
        ),
        compiler_params=pltpu.CompilerParams(vmem_limit_bytes=VMEM_LIMIT),
        cost_estimate=pl.CostEstimate(flops=2 * 10**10, bytes_accessed=10**7, transcendentals=10**7),
        name="attend",
    )(low, q, kv, tabs)


def out_block(p1, nn, half):
    return p1[nn, half * 256 : half * 256 + 256, 384:640]


def middle_kernel(
    att, p1, hidden, gain, mid_out, ffn_out, theirs, mine, from_pt, from_up, from_dn, *refs
):
    s_sems, g_sems, refs = refs[:12], refs[13:21], (refs[12], refs[21])
    fbuf, out_s = refs
    me = spot()
    r, n, w = me
    greet(line_partners(r, n, w, 4))
    sums = [
        Scatter(
            mine, theirs, (from_pt, from_up, from_dn), s_sems[6 * c : 6 * c + 6], me, 4, 64 * c, 64
        )
        for c in range(2)
    ]
    gathers = [Gather(fbuf, g_sems[4 * c : 4 * c + 4], me, 4, pl.ds(64 * c, 64)) for c in range(2)]

    def shard(i, carry):
        s = sums[0].order(i)
        rows = pl.ds(pl.multiple_of(s * 128, 128), 128)
        left = jnp.concatenate([att[1 - r, rows, :], att[r, rows, :]], axis=0)
        for nn in range(4):
            for half in range(2):
                part = jnp.dot(left, out_block(p1, nn, half), preferred_element_type=f32).astype(bf16)
                columns = slice(nn * 512 + half * 256, nn * 512 + half * 256 + 256)
                theirs[s, :, columns] = part[0:128]
                mine[s, :, columns] = part[128:256]
        sums[0].pair(s).start()
        sums[1].pair(s).start()
        return carry

    lax.fori_loop(0, 4, shard, 0)

    def finish(c):
        sums[c].total(mid_out)

        def body(rows):
            middle = mid_out[rows, :] + hidden[rows, :].astype(f32)
            mid_out[rows, :] = middle
            fbuf[r, w, rows, :] = norm_rows(middle, gain[...]).astype(bf16)

        sums[c].each(body)
        gathers[c].own()

    sums[0].advance((0, 1, 2, 3), (0, 1, 2, 3))
    sums[1].advance((0, 1, 2, 3), ())
    finish(0)
    sums[1].advance((), (0, 1))
    gathers[0].advance((), (1,))
    sums[1].advance((), (2, 3))
    finish(1)
    gathers[0].advance((1, 2), (2,))
    gathers[0].step(3)
    for k in (1, 2, 3):
        gathers[1].step(k)
    gathers[0].rest()
    gathers[1].rest()
    out_f = pltpu.make_async_copy(fbuf, ffn_out, out_s)
    out_f.start()
    for c in range(2):
        sums[c].sent()
        gathers[c].sent()
    out_f.wait()


def middle_stage(att, p1, hidden, gain):
    shard, width = hidden.shape
    rows = jax.ShapeDtypeStruct((2, 4, shard, width), bf16)
    return comm_call(
        middle_kernel, "middle", 3,
        (jax.ShapeDtypeStruct((shard, width), f32), rows),
        [vmem()] * 4, [vmem(), hbm()],
        [pltpu.VMEM((4, shard, width), bf16)] * 2
        + scatter_bufs(shard, width) + scatter_sems() * 2
        + gather_scratch(shard, width) + gather_sems()
        + [pltpu.SemaphoreType.DMA(())],
        (att, p1, hidden, gain), flops=10**10, sent=2 * 10**8,
    )


class Spread:
    def __init__(self, outs, sems, me):
        self.a_send, self.a_keep, self.b_send, self.b_keep = outs
        self.r, self.n, self.w = me
        self.give_s, self.give_g, self.keep_s = sems

    def copies(self, wide, row, place, give):
        for k in range(4):
            block = wide.at[self.n ^ k]
            for part in range(2):
                source = block.at[pl.ds(part * 128, 128)]
                if part == 0:
                    target = (self.a_send if k & 1 else self.a_keep).at[k >> 1]
                else:
                    target = (self.b_send if k >= 2 else self.b_keep).at[k & 1]
                target = place(target)
                at = k * 2 + part
                if give:
                    yield pltpu.make_async_remote_copy(
                        source, target, self.give_s.at[row, at], self.give_g.at[row, at],
                        device_id=(1 - self.r, self.n, self.w), device_id_type=MESH,
                    )
                else:
                    yield pltpu.make_async_copy(source, target, self.keep_s.at[row, at])

    def start(self, *args):
        for copy in self.copies(*args):
            copy.start()

    def wait_send(self, *args):
        for copy in self.copies(*args):
            copy.wait_send()

    def wait_recv(self, *args):
        for copy in self.copies(*args):
            copy.wait_recv()

    def wait(self, *args):
        for copy in self.copies(*args):
            copy.wait()


def spread_sems(count):
    return [pltpu.SemaphoreType.DMA((count, 8))] * 3


def ffn_kernel(
    x, tops_in, grad_top, p2_all, gain,
    part_out, sum_out, gain_out, o0, o1, o2, o3, ra_out, rb_out,
    theirs, mine, from_pt, from_up, from_dn, s0, s1, s2, s3, s4, s5,
    act, dgu, wide, out_s, give_s, give_g, keep_s, p2, in_s, n_s, n_g,
    tops4, h0, h1, h2, h3, tops_s,
):
    me = spot()
    r, n, w = me
    loads = [pltpu.make_async_copy(p2_all.at[:, j], p2.at[j], in_s.at[j]) for j in range(3)]
    loads.append(pltpu.make_async_copy(tops_in, tops4.at[:, :, 0:64], tops_s))
    for load in loads:
        load.start()
    greet(line_partners(r, n, w, 4) + square_partners(r, n, w))
    scatter = Scatter(
        mine, theirs, (from_pt, from_up, from_dn), (s0, s1, s2, s3, s4, s5), me, 4
    )
    late = pl.ds(64, 64)
    gather = Gather(tops4, (h0, h1, h2, h3), me, 4, late)

    def keep(rows):
        tops4[r, w, pl.ds(64 + rows.start, 16), :] = grad_top[pl.ds(64 + rows.start, 16), :]

    each_rows(64, 16, keep)
    gather.own()
    gain_out[...] = jnp.zeros_like(gain_out)
    loads[0].wait()
    loads[1].wait()

    def hidden_tile(i, carry):
        ft, row = i // 2, i % 2
        rows = pl.ds(pl.multiple_of(row * 512, 512), 512)
        columns = pl.ds(pl.multiple_of(ft * 256, 256), 256)
        left = x[rows, :]
        gate = jnp.dot(left, p2[0, :, :, columns].reshape(2048, 256), preferred_element_type=f32)
        up = jnp.dot(left, p2[1, :, :, columns].reshape(2048, 256), preferred_element_type=f32)
        sig = 1.0 / (1.0 + jnp.exp(-gate))
        silu = gate * sig
        act[rows, columns] = (silu * up).astype(bf16)
        dgu[rows, columns] = (up * (sig * (1.0 + gate * (1.0 - sig)))).astype(bf16)
        later = pl.ds(pl.multiple_of(1024 + ft * 256, 256), 256)
        dgu[rows, later] = silu.astype(bf16)
        return carry

    lax.fori_loop(0, 4, hidden_tile, 0)
    gather.step(1)
    lax.fori_loop(4, 8, hidden_tile, 0)
    gather.step(2)
    loads[2].wait()

    def down_tile(dt, carry):
        nn, half = dt // 2, dt % 2
        columns = pl.ds(pl.multiple_of(dt * 256, 256), 256)
        inner = pl.ds(pl.multiple_of(half * 256, 256), 256)
        other = pl.ds(pl.multiple_of(512 + half * 256, 256), 256)
        right = jnp.concatenate([p2[2, nn, :, inner], p2[2, nn, :, other]], axis=0)
        for row, stage in ((0, theirs), (1, mine)):
            part = jnp.dot(act[row * 512 : row * 512 + 512, :], right, preferred_element_type=f32)
            stage[:, :, columns] = part.astype(bf16).reshape(4, 128, 256)
        return carry

    lax.fori_loop(0, 8, down_tile, 0)
    puts = [
        pltpu.make_async_copy(theirs, part_out.at[0], out_s.at[0]),
        pltpu.make_async_copy(mine, part_out.at[1], out_s.at[1]),
    ]
    for put in puts:
        put.start()
    gather.step(3)
    gather.rest()
    loads[3].wait()

    def top_rows(row):
        return tops4[row].reshape(512, 2048)

    def back_tile(ft, carry):
        columns = pl.ds(pl.multiple_of(ft * 256, 256), 256)
        f_rows = pl.ds(pl.multiple_of((ft % 2) * 256, 256), 256)
        f_cols = pl.ds(pl.multiple_of((ft // 2) * 512, 512), 512)
        later = pl.ds(pl.multiple_of(1024 + ft * 256, 256), 256)
        right = jnp.concatenate([p2[2, nn, f_rows, f_cols] for nn in range(4)], axis=1)
        for row in range(2):
            rows = slice(row * 512, row * 512 + 512)
            dact = contract_last(top_rows(row), right)
            dgu[rows, columns] = (dact * dgu[rows, columns].astype(f32)).astype(bf16)
            dgu[rows, later] = (dact * dgu[rows, later].astype(f32)).astype(bf16)
        return carry

    lax.fori_loop(0, 4, back_tile, 0)
    for put in puts:
        put.wait()

    spread = Spread((o0, o1, o2, o3), (give_s, give_g, keep_s), me)
    columns_here = pl.ds(pl.multiple_of(r * 1024, 1024), 1024)
    slots = {2: 0, 0: 1, 1: 0}

    def moved(which, half):
        def place(target):
            return target.at[which, :, columns_here]

        return wide.at[slots[which], half], which, place, half == 0

    def weights(which, between=None):
        for half in range(2):
            d_first = (jnp.where(half == 0, 1 - r, r)) * 1024

            def weight_tile(i, carry):
                d_cols = pl.ds(pl.multiple_of(d_first + i * 256, 256), 256)
                if which < 2:
                    left = x[:, d_cols]
                    right = dgu[:, which * 1024 : which * 1024 + 1024]
                else:
                    left = tops4[:, :, :, d_cols].reshape(1024, 256)
                    right = act[...]
                wide[slots[which], half, i] = contract_first(left, right).astype(bf16)
                return carry

            lax.fori_loop(0, 4, weight_tile, 0)
            spread.start(*moved(which, half))
            if half == 0 and between is not None:
                between()

    def hop(which, at):
        return (
            push(o0.at[:, which], ra_out.at[at], n_s.at[0, at], n_g.at[0, at], over_x(r, n, w)),
            push(o2.at[:, which], rb_out.at[at], n_s.at[1, at], n_g.at[1, at], over_y(r, n, w)),
        )

    hops = hop(2, 0) + hop(0, 1)
    weights(2)
    for i in range(4):
        s = scatter.order(i)
        rows_t = pl.ds(pl.multiple_of((1 - r) * 512 + s * 128, 128), 128)
        rows_m = pl.ds(pl.multiple_of(r * 512 + s * 128, 128), 128)

        def model_tile(dt, carry):
            nn, half = dt // 2, dt % 2
            columns = pl.ds(pl.multiple_of(dt * 256, 256), 256)
            inner = pl.ds(pl.multiple_of(half * 256, 256), 256)
            left = jnp.concatenate([dgu[rows_t, :], dgu[rows_m, :]], axis=0)
            right = jnp.concatenate([p2[0, nn, inner, :], p2[1, nn, inner, :]], axis=1)
            part = contract_last(left, right)
            seen = jnp.concatenate([x[rows_t, columns], x[rows_m, columns]], axis=0)
            terms = part * seen.astype(f32)
            gain_out[:, columns] += jnp.sum(terms.reshape(32, 8, 256), axis=0)
            part = part.astype(bf16)
            theirs[s, :, columns] = part[0:128]
            mine[s, :, columns] = part[128:256]
            return carry

        lax.fori_loop(0, 8, model_tile, 0)
        scatter.pair(s).start()
        if i < 2:
            which = (2, 0)[i]
            spread.wait_recv(*moved(which, 0))
            spread.wait(*moved(which, 1))
            hops[2 * i].start()
            hops[2 * i + 1].start()
        if i == 0:
            weights(0)
            scatter.advance((0,), ())
        elif i > 1:
            scatter.advance((i - 1,), (i - 2,))

    def scale(rows):
        gain_out[rows, :] = gain_out[rows, :] / gain[...]

    each_rows(8, 8, scale)
    spread.wait_send(*moved(2, 0))
    weights(1, lambda: scatter.advance((3,), (2,)))
    scatter.advance((), (3,))
    scatter.total(sum_out)
    scatter.sent()
    gather.sent()
    spread.wait_send(*moved(0, 0))
    spread.wait_recv(*moved(1, 0))
    spread.wait_send(*moved(1, 0))
    spread.wait(*moved(1, 1))
    for hop in hops:
        hop.wait()


def spread_shapes(*dims):
    return (jax.ShapeDtypeStruct((2,) + dims, bf16),) * 4


def ffn_stage(*args):
    shard, width = 128, 2048
    return comm_call(
        ffn_kernel, "ffn", 4,
        (
            jax.ShapeDtypeStruct((2, 4, shard, width), bf16),
            jax.ShapeDtypeStruct((shard, width), f32),
            jax.ShapeDtypeStruct((8, width), f32),
        )
        + spread_shapes(3, 128, width)
        + (jax.ShapeDtypeStruct((2, 2, 128, width), bf16),) * 2,
        [vmem(), hbm(), vmem(), hbm(), vmem()], [hbm(), vmem(), vmem()] + [hbm()] * 6,
        [pltpu.VMEM((4, shard, width), bf16)] * 2
        + scatter_bufs(shard, width) + scatter_sems()
        + [
            pltpu.VMEM((1024, 1024), bf16),
            pltpu.VMEM((1024, 2048), bf16),
            pltpu.VMEM((2, 2, 4, 256, 1024), bf16),
            pltpu.SemaphoreType.DMA((2,)),
        ]
        + spread_sems(3)
        + [pltpu.VMEM((3, 4, 512, 1024), bf16), pltpu.SemaphoreType.DMA((3,))]
        + [pltpu.SemaphoreType.DMA((2, 2))] * 2
        + gather_scratch(shard, width)
        + [pltpu.SemaphoreType.DMA(())],
        args, flops=4 * 10**10, sent=10**8,
    )


def norm_back(values, gain, grad):
    root = lax.rsqrt(jnp.mean(values * values, axis=-1, keepdims=True) + norm_eps)
    weighted = grad * gain
    inner = jnp.mean(weighted * values, axis=-1, keepdims=True)
    return root * weighted - values * (root * root * root) * inner


def branch_kernel(
    total, mid, grad_top, gain, p1, att, a_in, b_in, a_keep, b_keep, a_came, b_came,
    gmid_out, datt_out, o0, o1, o2, o3, ra_out, rb_out, la_out, lb_out,
    buf, g0, g1, g2, g3, wide, give_s, give_g, keep_s, n_s, n_g, kept, came, in_s,
):
    me = spot()
    r, n, w = me
    greet(line_partners(r, n, w, 4) + square_partners(r, n, w))
    gather = Gather(buf, (g0, g1, g2, g3), me, 4)
    hops = [
        push(a_in.at[:, 1], ra_out, n_s.at[0], n_g.at[0], over_x(r, n, w)),
        push(b_in.at[:, 1], rb_out, n_s.at[1], n_g.at[1], over_y(r, n, w)),
        push(kept.at[0], la_out, n_s.at[2], n_g.at[2], over_y(r, n, w)),
        push(kept.at[1], lb_out, n_s.at[3], n_g.at[3], over_x(r, n, w)),
    ]
    loads = []
    for j, (keep, first) in enumerate(((a_keep, a_came), (b_keep, b_came))):
        loads += [
            pltpu.make_async_copy(keep.at[1, 2], kept.at[j], in_s.at[j, 0]),
            pltpu.make_async_copy(first.at[0, 1], came.at[j], in_s.at[j, 1]),
        ]
    for load in loads:
        load.start()
    hops[0].start()
    hops[1].start()

    def body(rows):
        grad = norm_back(mid[rows, :], gain[...], total[rows, :]) + grad_top[rows, :].astype(f32)
        gmid_out[rows, :] = grad
        buf[r, w, rows, :] = grad.astype(bf16)

    each_rows(mid.shape[0], 16, body)
    gather.own()
    for load in loads:
        load.wait()
    for j in range(2):
        def join(rows):
            kept[j, rows, :] = (kept[j, rows, :].astype(f32) + came[j, rows, :].astype(f32)).astype(bf16)

        each_rows(128, 16, join)
        hops[2 + j].start()
    for k in (1, 2, 3):
        gather.step(k)
    gather.rest()
    for row in range(2):
        for pair in range(2):
            left = jnp.concatenate([buf[row, 2 * pair], buf[row, 2 * pair + 1]], axis=0)
            right = jnp.concatenate(
                [out_block(p1, nn, half) for nn in range(4) for half in range(2)], axis=1
            )
            datt_out[row, pair * 256 : pair * 256 + 256, :] = contract_last(left, right).astype(bf16)

    spread = Spread((o0, o1, o2, o3), (give_s, give_g, keep_s), me)

    def moved(half):
        def place(target):
            return target.at[:, pl.ds(pl.multiple_of(r * 256, 256), 256)]

        return wide.at[half], 0, place, half == 0

    for half in range(2):
        d_first = (jnp.where(half == 0, 1 - r, r)) * 1024

        def weight_tile(i, carry):
            columns = pl.ds(pl.multiple_of(d_first + i * 256, 256), 256)
            left = buf[:, :, :, columns].reshape(1024, 256)
            wide[half, i] = contract_first(left, att[...]).astype(bf16)
            return carry

        lax.fori_loop(0, 4, weight_tile, 0)
        spread.start(*moved(half))
    gather.sent()
    spread.wait(*moved(0))
    spread.wait(*moved(1))
    for hop in hops:
        hop.wait()


def branch_stage(*args):
    shard, width = 128, 2048
    return comm_call(
        branch_kernel, "branch", 5,
        (
            jax.ShapeDtypeStruct((shard, width), f32),
            jax.ShapeDtypeStruct((2, 512, 256), bf16),
        )
        + spread_shapes(128, 512)
        + (jax.ShapeDtypeStruct((2, 128, width), bf16),) * 2
        + (jax.ShapeDtypeStruct((128, width), bf16),) * 2,
        [vmem()] * 6 + [hbm()] * 6, [vmem(), vmem()] + [hbm()] * 8,
        gather_scratch(shard, width)
        + [pltpu.VMEM((2, 4, 256, 256), bf16)]
        + spread_sems(1)
        + [pltpu.SemaphoreType.DMA((4,))] * 2
        + [pltpu.VMEM((2, 128, width), bf16)] * 2
        + [pltpu.SemaphoreType.DMA((2, 2))],
        args, flops=10**10, sent=10**8,
    )


def unproject_kernel(
    q, kv, att, grad, lse, x, p1, tabs, gain, parts, mid, a_keep, b_keep, a_gate, b_gate, a_up, b_up, oa_in, ob_in,
    part_out, gain_out, o0, o1, o2, o3, hid_out, ra_out, rb_out, roa_out, rob_out,
    send, recv, both, wide_q, wide_kv, s_s, s_g, give_s, give_g, keep_s,
    mine, from_pt, from_up, from_dn, s0, s1, s2, s3, s4, s5,
    kept, came, acc, in_s, n_s, n_g, m_s, dkv,
):
    me = spot()
    r, n, w = me
    loads = []
    for j, (keep, gate, up) in enumerate(((a_keep, a_gate, a_up), (b_keep, b_gate, b_up))):
        loads += [
            pltpu.make_async_copy(keep.at[1, 0:2], kept.at[j], in_s.at[j, 0]),
            pltpu.make_async_copy(gate.at[1, 1], came.at[j, 0], in_s.at[j, 1]),
            pltpu.make_async_copy(up.at[1], came.at[j, 1], in_s.at[j, 2]),
        ]
    loads.append(pltpu.make_async_copy(parts.at[r], mine, m_s))
    for load in loads:
        load.start()
    greet(
        line_partners(r, n, w, 4)
        + [
            (n >= 1, nar_device(r, n, w, -1)),
            (n >= 2, nar_device(r, n, w, -2)),
            (n <= 2, nar_device(r, n, w, 1)),
            (n <= 1, nar_device(r, n, w, 2)),
        ]
        + square_partners(r, n, w)
    )
    scatter = Scatter(
        mine, parts.at[1 - r], (from_pt, from_up, from_dn), (s0, s1, s2, s3, s4, s5), me, 4
    )
    hops = [
        push(kept.at[0], ra_out, n_s.at[0], n_g.at[0], over_y(r, n, w)),
        push(kept.at[1], rb_out, n_s.at[1], n_g.at[1], over_x(r, n, w)),
        push(oa_in, roa_out, n_s.at[2], n_g.at[2], over_x(r, n, w)),
        push(ob_in, rob_out, n_s.at[3], n_g.at[3], over_y(r, n, w)),
    ]

    def copy(row, slot, by):
        return pltpu.make_async_remote_copy(
            send.at[row, slot], recv.at[row, slot], s_s.at[row, slot], s_g.at[row, slot],
            device_id=nar_device(r, n, w, by), device_id_type=MESH,
        )

    for i in range(4):
        scatter.pair(scatter.order(i)).start()
    for load in loads:
        load.wait()
    for j in range(2):
        for which in range(2):
            def join(rows):
                total = kept[j, which, rows, :].astype(f32) + came[j, which, rows, :].astype(f32)
                kept[j, which, rows, :] = total.astype(bf16)

            each_rows(128, 16, join)
        hops[j].start()
    hops[2].start()
    hops[3].start()
    scatter.advance((0, 1, 2, 3), ())

    def attention(i, carry):
        row, block = i // 4, i % 4
        first_query = 1024 + block * QUERIES
        here = pl.ds(pl.multiple_of(block * QUERIES, QUERIES), QUERIES)

        @pl.when(block == 0)
        def _():
            dkv[row] = jnp.zeros((1536, 128), f32)

        query = stack_low(q[row, here, :].astype(f32)).astype(bf16)
        grads = stack_high(grad[row, here, :].astype(f32))
        inner = jnp.sum(grads * stack_high(att[row, here, :].astype(f32)), axis=1, keepdims=True)
        grads = grads.astype(bf16)
        logsum = jnp.concatenate([lse[row, block]] * (KEYS // 128), axis=1)
        starts = tabs[row, here, 256:384]

        def key_tile(step, dq):
            tile = block // 2 + step
            rows = pl.ds(pl.multiple_of(tile * KEYS, KEYS), KEYS)
            pair = kv[row, rows, :]
            ok = allowed_tile(starts, tile, first_query)
            scores = contract_last(query, pair) * 0.125
            prob = jnp.where(ok, jnp.exp(scores - logsum), 0.0)
            grad_prob = contract_last(grads, pair)
            grad_scores = (prob * (grad_prob - inner)).astype(bf16)
            dkv[row, rows, :] += contract_first(grad_scores, query) * 0.125 + contract_first(
                prob.astype(bf16), grads
            )
            return dq + jnp.dot(grad_scores, pair, preferred_element_type=f32)

        dq = lax.fori_loop(0, 5, key_tile, jnp.zeros((4 * QUERIES, 128), f32))
        flat = unstack(dq, True) * 0.125
        cosine, sine = tabs[row, here, 0:128], -tabs[row, here, 128:256]
        there = pl.ds(pl.multiple_of(i * QUERIES, QUERIES), QUERIES)
        both[there, 0:128] = turn(flat[:, 0:128], cosine, sine).astype(bf16)
        both[there, 128:256] = turn(flat[:, 128:256], cosine, sine).astype(bf16)

        @pl.when(block == 3)
        def _():
            for slot, by in ((1, -1), (0, -2)):
                @pl.when(n >= -by)
                def _():
                    send[row, slot] = dkv[row, slot * 512 : slot * 512 + 512, :].astype(bf16)
                    copy(row, slot, by).start()

        @pl.when(i == 3)
        def _():
            scatter.advance((), (0,))

        return carry

    lax.fori_loop(0, 8, attention, 0)
    scatter.advance((), (1,))

    spread = Spread((o0, o1, o2, o3), (give_s, give_g, keep_s), (r, n, w))

    def moved_q(half):
        def place(target):
            return target.at[:, pl.ds(pl.multiple_of(r * 256, 256), 256)]

        return wide_q.at[half], 0, place, half == 0

    def moved_kv(half):
        def place(target):
            return target.at[:, pl.ds(pl.multiple_of(512 + r * 128, 128), 128)]

        return wide_kv.at[half], 1, place, half == 0

    def weight(half, columns, wide):
        d_first = (jnp.where(half == 0, 1 - r, r)) * 1024

        def tile(i, carry):
            d_cols = pl.ds(pl.multiple_of(d_first + i * 256, 256), 256)
            wide[half, i] = contract_first(x[:, d_cols], both[:, columns]).astype(bf16)
            return carry

        lax.fori_loop(0, 4, tile, 0)

    for half in range(2):
        weight(half, slice(0, 256), wide_q)
        spread.start(*moved_q(half))
    lane = lax.broadcasted_iota(jnp.int32, (128, 128), 1)
    for row in range(2):
        for slot, by in ((1, -1), (0, -2)):
            @pl.when(n <= 3 + by)
            def _():
                copy(row, slot, by).wait_recv()

        def tile(i, carry):
            rows = pl.ds(pl.multiple_of(i * 128, 128), 128)
            total = dkv[row, pl.ds(pl.multiple_of(1024 + i * 128, 128), 128), :]
            zero = jnp.zeros_like(total)
            total = total + jnp.where(n <= 2, recv[row, 1, rows, :].astype(f32), zero)
            total = total + jnp.where(n <= 1, recv[row, 0, rows, :].astype(f32), zero)
            turned = turn(total, tabs[row, rows, 0:128], -tabs[row, rows, 128:256])
            both[pl.ds(pl.multiple_of(row * 512 + i * 128, 128), 128), 256:384] = jnp.where(
                lane < 64, turned, total
            ).astype(bf16)
            return carry

        lax.fori_loop(0, 4, tile, 0)
    for half in range(2):
        weight(half, slice(256, 384), wide_kv)
        spread.start(*moved_kv(half))
    scatter.advance((), (2,))
    gain_out[...] = jnp.zeros_like(gain_out)

    def model_tile(dt, carry):
        nn, half = dt // 2, dt % 2
        columns = pl.ds(pl.multiple_of(dt * 256, 256), 256)
        inner = pl.ds(pl.multiple_of(half * 256, 256), 256)
        right = p1[nn, inner, 0:384]
        for row in range(2):
            for block in range(2):
                first = row * 512 + block * 256
                part = contract_last(both[first : first + 256, :], right)
                terms = part * x[first : first + 256, columns].astype(f32)
                gain_out[:, columns] += jnp.sum(terms.reshape(32, 8, 256), axis=0)
                part_out[row, 2 * block, :, columns] = part[0:128].astype(bf16)
                part_out[row, 2 * block + 1, :, columns] = part[128:256].astype(bf16)
        return carry

    lax.fori_loop(0, 8, model_tile, 0)
    gain_out[...] = gain_out[...] / gain[...]
    scatter.advance((), (3,))
    scatter.total(acc)

    def last(rows):
        hid_out[rows, :] = (acc[rows, :] + mid[rows, :]).astype(bf16)

    each_rows(128, 16, last)
    scatter.sent()
    for row in range(2):
        for slot, by in ((1, -1), (0, -2)):
            @pl.when(n >= -by)
            def _():
                copy(row, slot, by).wait_send()

    for half in range(2):
        spread.wait(*moved_q(half))
        spread.wait(*moved_kv(half))
    for hop in hops:
        hop.wait()


def unproject(*args):
    return comm_call(
        unproject_kernel, "unproject", 6,
        (
            jax.ShapeDtypeStruct((2, 4, 128, 2048), bf16),
            jax.ShapeDtypeStruct((8, 2048), f32),
        )
        + spread_shapes(128, 768)
        + (jax.ShapeDtypeStruct((128, 2048), bf16),)
        + (jax.ShapeDtypeStruct((2, 128, 2048), bf16),) * 2
        + (jax.ShapeDtypeStruct((2, 128, 512), bf16),) * 2,
        [vmem()] * 9 + [hbm(), vmem()] + [hbm()] * 8,
        [vmem(), vmem()] + [hbm()] * 4 + [vmem()] + [hbm()] * 4,
        [
            pltpu.VMEM((2, 2, 512, 128), bf16),
            pltpu.VMEM((2, 2, 512, 128), bf16),
            pltpu.VMEM((1024, 384), bf16),
            pltpu.VMEM((2, 4, 256, 256), bf16),
            pltpu.VMEM((2, 4, 256, 128), bf16),
            pltpu.SemaphoreType.DMA((2, 2)),
            pltpu.SemaphoreType.DMA((2, 2)),
        ]
        + spread_sems(2)
        + [pltpu.VMEM((4, 128, 2048), bf16)]
        + scatter_bufs(128, 2048) + scatter_sems()
        + [
            pltpu.VMEM((2, 2, 128, 2048), bf16),
            pltpu.VMEM((2, 2, 128, 2048), bf16),
            pltpu.VMEM((128, 2048), f32),
            pltpu.SemaphoreType.DMA((2, 3)),
            pltpu.SemaphoreType.DMA((4,)),
            pltpu.SemaphoreType.DMA((4,)),
            pltpu.SemaphoreType.DMA(()),
            pltpu.VMEM((2, 1536, 128), f32),
        ],
        args, flops=10**10, sent=10**7,
    )


def leave_kernel(
    parts, hidden, gain, gmid, gains, qa_send, qa_keep, qb_send, qb_keep, oa_keep, ob_keep, oa_in, ob_in,
    grad_out, ga_out, query_out, key_out, value_out, output_out,
    mine, from_pt, from_up, from_dn, s0, s1, s2, s3, s4, s5,
    acc, over_wid, summed, over_rest, w_s, w_g, t_s, t_g,
    first_q, next_q, then_q, next_o, then_o, kv, n_s, n_g, k_s, k_g,
):
    me = spot()
    r, n, w = me
    partners = [(w != j, (r, n, jnp.int32(j))) for j in range(4)]
    partners += [
        ((r != a) | (n != b), (jnp.int32(a), jnp.int32(b), w)) for a in range(2) for b in range(4)
    ]
    greet(partners)
    x_side, y_side = over_x(r, n, w), over_y(r, n, w)
    q_hops = [
        push(qa_send, first_q.at[0], n_s.at[0], n_g.at[0], x_side),
        push(qb_send, first_q.at[1], n_s.at[1], n_g.at[1], y_side),
    ]
    q_later = [
        push(next_q.at[0], then_q.at[0], n_s.at[2], n_g.at[2], y_side),
        push(next_q.at[1], then_q.at[1], n_s.at[3], n_g.at[3], x_side),
    ]
    o_hops = [
        push(next_o.at[0], then_o.at[0], n_s.at[4], n_g.at[4], y_side),
        push(next_o.at[1], then_o.at[1], n_s.at[5], n_g.at[5], x_side),
    ]
    for hop in q_hops:
        hop.start()
    scatter = Scatter(
        mine, parts.at[1 - r], (from_pt, from_up, from_dn), (s0, s1, s2, s3, s4, s5), me, 4
    )
    for i in range(4):
        scatter.pair(scatter.order(i)).start()

    def wid_copy(j, slot):
        return pltpu.make_async_remote_copy(
            gains, over_wid.at[slot], w_s.at[j], w_g.at[slot],
            device_id=(r, n, jnp.int32(j)), device_id_type=MESH,
        )

    def rest_copy(a, b, slot):
        return pltpu.make_async_remote_copy(
            summed, over_rest.at[slot], t_s.at[a * 4 + b], t_g.at[slot],
            device_id=(jnp.int32(a), jnp.int32(b), w), device_id_type=MESH,
        )

    for j in range(4):
        @pl.when(w != j)
        def _():
            wid_copy(j, w).start()

    for s in range(4):
        def fill(rows):
            mine[s, rows, :] = parts[r, s, rows, :]

        each_rows(128, 16, fill)
    scatter.advance((0, 1, 2, 3), ())
    for j, (keep, came) in enumerate(((oa_keep, oa_in), (ob_keep, ob_in))):
        next_o[j] = (keep[1].astype(f32) + came[1].astype(f32)).astype(bf16)
        o_hops[j].start()
    summed[...] = gains[...]
    for j in range(4):
        @pl.when(w != j)
        def _():
            wid_copy(j, j).wait_recv()
            summed[...] += over_wid[j]

    for a in range(2):
        for b in range(4):
            @pl.when((r != a) | (n != b))
            def _():
                rest_copy(a, b, r * 4 + n).start()

    for j, keep in enumerate((qa_keep, qb_keep)):
        q_hops[j].wait_recv()
        next_q[j] = (keep[1].astype(f32) + first_q[j, 1].astype(f32)).astype(bf16)
        q_later[j].start()
    scatter.advance((), (0, 1))
    for j, keep in enumerate((qa_keep, qb_keep)):
        q_later[j].wait_recv()
        total = keep[0].astype(f32) + first_q[j, 0].astype(f32) + then_q[j].astype(f32)
        query_out[j * 128 : j * 128 + 128, :] = total[:, 0:512]
        kv[w, j * 128 : j * 128 + 128, :] = total[:, 512:768].astype(bf16)

    def kv_copy(j, slot):
        return pltpu.make_async_remote_copy(
            kv.at[w], kv.at[w], k_s.at[j], k_g.at[slot],
            device_id=(r, n, jnp.int32(j)), device_id_type=MESH,
        )

    def kv_wait(j):
        return pltpu.make_async_remote_copy(
            kv.at[j], kv.at[j], k_s.at[j], k_g.at[j],
            device_id=(r, n, jnp.int32(j)), device_id_type=MESH,
        )

    for j in range(4):
        @pl.when(w != j)
        def _():
            kv_copy(j, w).start()

    scatter.advance((), (2, 3))
    for j, (keep, came) in enumerate(((oa_keep, oa_in), (ob_keep, ob_in))):
        o_hops[j].wait_recv()
        output_out[j * 128 : j * 128 + 128, :] = (
            keep[0].astype(f32) + came[0].astype(f32) + then_o[j].astype(f32)
        )
    mine_block = r * 4 + n
    ga_out[0:1] = summed[pl.ds(mine_block, 1), :]
    ga_out[1:2] = summed[pl.ds(mine_block + 8, 1), :]
    for a in range(2):
        for b in range(4):
            @pl.when((r != a) | (n != b))
            def _():
                slot = a * 4 + b
                rest_copy(a, b, slot).wait_recv()
                ga_out[0:1] += over_rest[slot, pl.ds(mine_block, 1), :]
                ga_out[1:2] += over_rest[slot, pl.ds(mine_block + 8, 1), :]

    scatter.total(acc)

    def last(rows):
        grad = norm_back(hidden[rows, :].astype(f32), gain[...], acc[rows, :])
        grad_out[rows, :] = (grad + gmid[rows, :]).astype(bf16)

    each_rows(hidden.shape[0], 16, last)
    lane = lax.broadcasted_iota(jnp.int32, (256, 128), 1)
    for j in range(4):
        @pl.when(w != j)
        def _():
            kv_wait(j).wait_recv()

        even, odd = kv[j, :, 0:128].astype(f32), kv[j, :, 128:256].astype(f32)
        here = slice(j * 128, j * 128 + 128)
        key_out[:, here] = jnp.where(lane < 64, even, pltpu.roll(odd, 64, 1))
        value_out[:, here] = jnp.where(lane < 64, pltpu.roll(even, 64, 1), odd)
    scatter.sent()
    for hop in q_hops + q_later + o_hops:
        hop.wait_send()
    for j in range(4):
        @pl.when(w != j)
        def _():
            kv_copy(j, w).wait_send()

    for j in range(4):
        @pl.when(w != j)
        def _():
            wid_copy(j, w).wait_send()

    for a in range(2):
        for b in range(4):
            @pl.when((r != a) | (n != b))
            def _():
                rest_copy(a, b, r * 4 + n).wait_send()


def leave(*args):
    shard, width = 128, 2048
    grad = jax.ShapeDtypeStruct((256, 512), f32)
    return comm_call(
        leave_kernel, "leave", 7,
        (jax.ShapeDtypeStruct((shard, width), bf16), jax.ShapeDtypeStruct((8, 256), f32))
        + (grad,) * 4,
        [vmem()] * 13, [vmem()] * 6,
        [pltpu.VMEM((4, shard, width), bf16)]
        + scatter_bufs(shard, width) + scatter_sems()
        + [
            pltpu.VMEM((shard, width), f32),
            pltpu.VMEM((4, 16, 256), f32),
            pltpu.VMEM((16, 256), f32),
            pltpu.VMEM((8, 16, 256), f32),
            pltpu.SemaphoreType.DMA((4,)),
            pltpu.SemaphoreType.DMA((4,)),
            pltpu.SemaphoreType.DMA((8,)),
            pltpu.SemaphoreType.DMA((8,)),
            pltpu.VMEM((2, 2, 128, 768), bf16),
            pltpu.VMEM((2, 128, 768), bf16),
            pltpu.VMEM((2, 128, 768), bf16),
            pltpu.VMEM((2, 128, 512), bf16),
            pltpu.VMEM((2, 128, 512), bf16),
            pltpu.VMEM((4, 256, 256), bf16),
            pltpu.SemaphoreType.DMA((6,)),
            pltpu.SemaphoreType.DMA((6,)),
            pltpu.SemaphoreType.DMA((4,)),
            pltpu.SemaphoreType.DMA((4,)),
        ],
        args, flops=10**10, sent=10**8,
    )


def local_fast(
    hidden_in, doc_lengths, w_query, w_key, w_value, w_output, w_gate, w_up, w_down,
    gain_attn, gain_ffn, grad_out,
):
    r, n, w = spot()
    hidden, grad_top = hidden_in[0], grad_out[0]
    gain_a, gain_f = gain_attn[None], gain_ffn[None]
    def half(weight, axis):
        size = weight.shape[axis] // 2
        return lax.dynamic_slice_in_dim(weight, r * size, size, axis)

    head = (w * 2 + r) * HD
    kv_pack = jnp.concatenate(
        [lax.dynamic_slice_in_dim(w_key, head, HD, 1), lax.dynamic_slice_in_dim(w_value, head, HD, 1)],
        axis=1,
    )
    out_half = half(w_output, 0)
    p1_shard = jnp.concatenate(
        [half(w_query, 1), kv_pack, jnp.concatenate([out_half[:, :256], out_half[:, 256:]], axis=0)],
        axis=1,
    )
    down_half = half(w_down, 0)
    p2_shard = jnp.stack(
        [
            half(w_gate, 1),
            half(w_up, 1),
            jnp.concatenate([down_half[:512], down_half[512:]], axis=1),
        ]
    )
    p1 = lax.all_gather(p1_shard, "nar", axis=0)
    p2 = lax.all_gather(p2_shard, "nar", axis=0)

    token_ids = n * 512 + jnp.arange(512, dtype=jnp.int32)
    doc_start, places = doc_layout(doc_lengths[0], token_ids)
    angles = places.astype(f32)[:, None] * inverse_freq()[None, :]
    cosine, sine = jnp.cos(angles), jnp.sin(angles)
    start_here = (doc_start - (n - 2) * 512).astype(f32)
    tab = jnp.concatenate(
        [cosine] * 4 + [-sine, sine] * 2 + [jnp.broadcast_to(start_here[:, None], (512, 128))],
        axis=1,
    )

    rows, tabs = enter(hidden, gain_a, tab)
    rows3, rows2 = rows.reshape(2, 512, 2048), rows.reshape(1024, 2048)
    q, kv, tops = project(rows3, p1, tabs, grad_top)
    low = tabs[:, ::QUERIES, 256].astype(jnp.int32).reshape(8)
    kv_flat = kv.reshape(2, 1536, 128)
    att, lse = attend(low, q, kv_flat, tabs)
    mid, ffn_rows = middle_stage(att, p1, hidden, gain_f)
    parts, total, gain_f_part, a_send, a_keep, b_send, b_keep, ra_dg, rb_dg = ffn_stage(
        ffn_rows.reshape(1024, 2048), tops, grad_top, p2, gain_f
    )
    gmid, datt, oa_send, oa_keep, ob_send, ob_keep, ra_u, rb_u, la_d, lb_d = branch_stage(
        total, mid, grad_top, gain_f, p1, att.reshape(1024, 256),
        a_send, b_send, a_keep, b_keep, ra_dg, rb_dg,
    )
    (
        dparts, gain_a_part, qa_send, qa_keep, qb_send, qb_keep,
        hidden_out, ra_last, rb_last, oa_came, ob_came,
    ) = unproject(
        q, kv_flat, att, datt, lse, rows2, p1, tabs, gain_a, parts, mid,
        a_keep, b_keep, ra_dg, rb_dg, ra_u, rb_u, oa_send, ob_send,
    )
    gains = jnp.concatenate(
        [gain_f_part.sum(axis=0).reshape(8, 256), gain_a_part.sum(axis=0).reshape(8, 256)], axis=0
    )
    grad_in, gain_sums, grad_query, grad_key, grad_value, output_sum = leave(
        dparts, hidden, gain_a, gmid, gains,
        qa_send, qa_keep, qb_send, qb_keep, oa_keep, ob_keep, oa_came, ob_came,
    )

    def joined(which):
        def half_rows(keep, came, last):
            return keep[0, which].astype(f32) + came.astype(f32) + last.astype(f32)

        a_came, b_came, a_last, b_last = (
            (ra_dg[1, 0], rb_dg[1, 0], ra_last[0], rb_last[0]),
            (ra_u[0], rb_u[0], ra_last[1], rb_last[1]),
            (ra_dg[0, 0], rb_dg[0, 0], la_d, lb_d),
        )[which]
        return jnp.concatenate(
            [half_rows(a_keep, a_came, a_last), half_rows(b_keep, b_came, b_last)], axis=0
        )

    return (
        hidden_out[None],
        grad_in[None],
        grad_query,
        grad_key,
        grad_value,
        output_sum.T,
        joined(0),
        joined(1),
        joined(2).T,
        gain_sums[1],
        gain_sums[0],
    )


def solution(mesh):
    in_specs = (
        P("row", ("nar", "wid"), None),
        P("row", None),
        P("nar", "wid"),
        P("nar", None),
        P("nar", None),
        P("wid", "nar"),
        P("nar", "wid"),
        P("nar", "wid"),
        P("wid", "nar"),
        P(),
        P(),
        P("row", ("nar", "wid"), None),
    )
    out_specs = (
        P("row", ("nar", "wid"), None),
        P("row", ("nar", "wid"), None),
        P(("row", "nar"), "wid"),
        P(("row", "nar"), None),
        P(("row", "nar"), None),
        P("wid", ("row", "nar")),
        P(("row", "nar"), "wid"),
        P(("row", "nar"), "wid"),
        P("wid", ("row", "nar")),
        P(("row", "nar")),
        P(("row", "nar")),
    )
    sizes = dict(mesh.shape)
    fits = sizes == {"row": 2, "nar": 4, "wid": 4}

    def body(*args):
        small = args[0].shape == (1, 128, 2048)
        return (local_fast if fits and small else local)(*args)

    return jax.shard_map(body, mesh=mesh, in_specs=in_specs, out_specs=out_specs, check_vma=False)
```

```python
import math

import jax
import jax.numpy as jnp
from jax import lax
from jax.experimental import pallas as pl
from jax.experimental.pallas import tpu as pltpu
from jax.sharding import PartitionSpec as P

H = 32
KV = 8
HD = 64


norm_eps = 1e-05
masked_score = -1e30


def inverse_freq():
    listed = []
    for pair_index in range(HD // 2):
        base_freq = 500000.0 ** (-2.0 * pair_index / HD)
        wavelength = 2.0 * math.pi / base_freq
        smoothing = (8192.0 / wavelength - 1.0) / 3.0
        blended = (1.0 - smoothing) * base_freq / 32.0 + smoothing * base_freq
        if wavelength < 2048.0:
            listed.append(base_freq)
        elif wavelength > 8192.0:
            listed.append(base_freq / 32.0)
        else:
            listed.append(blended)
    return jnp.asarray(listed, dtype=jnp.float32)


def rotate(values, cosine_table, sine_table):
    half_dim = HD // 2
    first_half = values[..., :half_dim]
    second_half = values[..., half_dim:]
    return jnp.concatenate(
        [
            first_half * cosine_table - second_half * sine_table,
            second_half * cosine_table + first_half * sine_table,
        ],
        axis=-1,
    )


def rotate_back(grads_in, cosine_table, sine_table):
    half_dim = HD // 2
    first_half = grads_in[..., :half_dim]
    second_half = grads_in[..., half_dim:]
    return jnp.concatenate(
        [
            first_half * cosine_table + second_half * sine_table,
            second_half * cosine_table - first_half * sine_table,
        ],
        axis=-1,
    )


def doc_layout(lengths_row, token_ids):
    ends_at = jnp.cumsum(lengths_row, dtype=jnp.int32)
    starts_at = ends_at - lengths_row
    inside = (token_ids[:, None] >= starts_at[None, :]) & (token_ids[:, None] < ends_at[None, :])
    doc_start = jnp.sum(jnp.where(inside, starts_at[None, :], 0), axis=1, dtype=jnp.int32)
    return (doc_start, token_ids - doc_start)


def norm_forward(values, gain_vector):
    root_inv = lax.rsqrt(jnp.mean(values * values, axis=-1, keepdims=True) + norm_eps)
    return (root_inv, (values * root_inv * gain_vector).astype(jnp.bfloat16))


def norm_backward(values, root_inv, gain_vector, grad_normed):
    weighted = grad_normed * gain_vector
    inner_sum = jnp.mean(weighted * values, axis=-1, keepdims=True)
    grad_values = root_inv * weighted - values * (root_inv * root_inv * root_inv) * inner_sum
    gain_term = jnp.sum(grad_normed * values * root_inv, axis=0)
    return (grad_values, gain_term)


def contract_last(left_side, right_side):
    return lax.dot_general(
        left_side, right_side, (((1,), (1,)), ((), ())), preferred_element_type=jnp.float32
    )


def contract_first(left_side, right_side):
    return lax.dot_general(
        left_side, right_side, (((0,), (0,)), ((), ())), preferred_element_type=jnp.float32
    )


def local(
    hidden_in,
    doc_lengths,
    w_query,
    w_key,
    w_value,
    w_output,
    w_gate,
    w_up,
    w_down,
    gain_attn,
    gain_ffn,
    grad_out,
):
    wid_count = lax.axis_size("wid")
    nar_count = lax.axis_size("nar")
    wid_index = lax.axis_index("wid")
    nar_index = lax.axis_index("nar")
    local_tokens = hidden_in.shape[1]
    block_tokens = local_tokens * wid_count
    seq_length = block_tokens * nar_count
    query_heads = w_query.shape[1] // HD
    group_size = H // KV
    kv_local = max(query_heads // group_size, 1)
    heads_per_kv = query_heads // kv_local
    kv_first = wid_index * query_heads // group_size
    query_block = min(512, block_tokens)
    block_count = block_tokens // query_block
    item_count = block_count * query_heads
    attn_scale = HD ** (-0.5)
    query_full, key_full, value_full, output_full, gate_full, up_full, down_full = (
        lax.all_gather(w_query, "nar", axis=0, tiled=True),
        lax.all_gather(w_key, "nar", axis=0, tiled=True),
        lax.all_gather(w_value, "nar", axis=0, tiled=True),
        lax.all_gather(w_output, "nar", axis=1, tiled=True),
        lax.all_gather(w_gate, "nar", axis=0, tiled=True),
        lax.all_gather(w_up, "nar", axis=0, tiled=True),
        lax.all_gather(w_down, "nar", axis=1, tiled=True),
    )
    key_local = lax.dynamic_slice_in_dim(key_full, kv_first * HD, kv_local * HD, 1)
    value_local = lax.dynamic_slice_in_dim(value_full, kv_first * HD, kv_local * HD, 1)
    token_ids = nar_index * block_tokens + jnp.arange(block_tokens, dtype=jnp.int32)
    doc_start, places = doc_layout(doc_lengths[0], token_ids)
    angles = places.astype(jnp.float32)[:, None] * inverse_freq()[None, :]
    cosine_table = jnp.cos(angles)[:, None, :]
    sine_table = jnp.sin(angles)[:, None, :]
    key_ids = jnp.arange(seq_length, dtype=jnp.int32)
    residual = hidden_in[0].astype(jnp.float32)
    root_attn, normed_attn = norm_forward(residual, gain_attn)
    normed_rows = lax.all_gather(normed_attn, "wid", axis=0, tiled=True)
    query_pre = jnp.dot(normed_rows, query_full, preferred_element_type=jnp.float32)
    key_pre = jnp.dot(normed_rows, key_local, preferred_element_type=jnp.float32)
    value_rows = jnp.dot(normed_rows, value_local, preferred_element_type=jnp.float32).astype(
        jnp.bfloat16
    )
    query_rot = (
        rotate(query_pre.reshape(block_tokens, query_heads, HD), cosine_table, sine_table)
        .astype(jnp.bfloat16)
        .reshape(block_tokens, query_heads * HD)
    )
    key_rot = (
        rotate(key_pre.reshape(block_tokens, kv_local, HD), cosine_table, sine_table)
        .astype(jnp.bfloat16)
        .reshape(block_tokens, kv_local * HD)
    )
    key_seq, value_seq = (
        lax.all_gather(key_rot, "nar", axis=0, tiled=True),
        lax.all_gather(value_rows, "nar", axis=0, tiled=True),
    )

    def item_inputs(item_index):
        block_index = item_index // query_heads
        head_index = item_index % query_heads
        kv_index = head_index // heads_per_kv
        row_first = block_index * query_block
        query_part = lax.dynamic_slice(query_rot, (row_first, head_index * HD), (query_block, HD))
        key_head = lax.dynamic_slice_in_dim(key_seq, kv_index * HD, HD, 1)
        value_head = lax.dynamic_slice_in_dim(value_seq, kv_index * HD, HD, 1)
        query_ids = lax.dynamic_slice_in_dim(token_ids, row_first, query_block, 0)
        query_starts = lax.dynamic_slice_in_dim(doc_start, row_first, query_block, 0)
        allowed = (key_ids[None, :] <= query_ids[:, None]) & (
            key_ids[None, :] >= query_starts[:, None]
        )
        scores = contract_last(query_part, key_head) * attn_scale
        return (
            row_first,
            head_index,
            kv_index,
            query_part,
            key_head,
            value_head,
            jnp.where(allowed, scores, masked_score),
        )

    def attend(item_index):
        row_first, head_index, kv_index, query_part, key_head, value_head, scores = item_inputs(
            item_index
        )
        row_max = jnp.max(scores, axis=1, keepdims=True)
        exp_scores = jnp.exp(scores - row_max)
        row_total = jnp.sum(exp_scores, axis=1, keepdims=True)
        probability = (exp_scores / row_total).astype(jnp.bfloat16)
        attended = jnp.dot(probability, value_head, preferred_element_type=jnp.float32)
        return (attended, (row_max + jnp.log(row_total))[:, 0])

    attended_items, logsum_items = lax.map(attend, jnp.arange(item_count, dtype=jnp.int32))
    attended_rows = (
        attended_items.reshape(block_count, query_heads, query_block, HD)
        .transpose(0, 2, 1, 3)
        .reshape(block_tokens, query_heads * HD)
        .astype(jnp.bfloat16)
    )
    rows_here = attended_rows
    branch_attn = lax.psum_scatter(
        jnp.dot(rows_here, output_full, preferred_element_type=jnp.float32),
        "wid",
        scatter_dimension=0,
        tiled=True,
    )
    middle = residual + branch_attn
    root_ffn, normed_ffn = norm_forward(middle, gain_ffn)
    ffn_rows = lax.all_gather(normed_ffn, "wid", axis=0, tiled=True)
    gate_proj = jnp.dot(ffn_rows, gate_full, preferred_element_type=jnp.float32)
    up_proj = jnp.dot(ffn_rows, up_full, preferred_element_type=jnp.float32)
    gate_sigmoid = jax.nn.sigmoid(gate_proj)
    gate_silu = gate_proj * gate_sigmoid
    activated = (gate_silu * up_proj).astype(jnp.bfloat16)
    rows_here = activated
    branch_ffn = lax.psum_scatter(
        jnp.dot(rows_here, down_full, preferred_element_type=jnp.float32).astype(jnp.bfloat16),
        "wid",
        scatter_dimension=0,
        tiled=True,
    ).astype(jnp.float32)
    hidden_out = (middle + branch_ffn).astype(jnp.bfloat16)[None]
    grad_top = grad_out[0]
    grad_rows = lax.all_gather(grad_top, "wid", axis=0, tiled=True)
    grad_activated = contract_last(grad_rows, down_full)
    down_weight_grad = contract_first(activated, grad_rows)
    silu_slope = gate_sigmoid * (1.0 + gate_proj * (1.0 - gate_sigmoid))
    grad_gate_b = (grad_activated * up_proj * silu_slope).astype(jnp.bfloat16)
    grad_up_b = (grad_activated * gate_silu).astype(jnp.bfloat16)
    gate_weight_grad = contract_first(ffn_rows, grad_gate_b)
    up_weight_grad = contract_first(ffn_rows, grad_up_b)
    grad_normed_ffn = lax.psum_scatter(
        contract_last(grad_gate_b, gate_full) + contract_last(grad_up_b, up_full),
        "wid",
        scatter_dimension=0,
        tiled=True,
    )
    grad_middle, gain_ffn_term = norm_backward(middle, root_ffn, gain_ffn, grad_normed_ffn)
    grad_middle = grad_middle + grad_top.astype(jnp.float32)
    grad_branch = grad_middle.astype(jnp.bfloat16)
    branch_rows = lax.all_gather(grad_branch, "wid", axis=0, tiled=True)
    grad_attended = contract_last(branch_rows, output_full).astype(jnp.bfloat16)
    output_weight_grad = contract_first(attended_rows, branch_rows)

    def attend_back(carried, item_index):
        key_grad, value_grad = carried
        row_first, head_index, kv_index, query_part, key_head, value_head, scores = item_inputs(
            item_index
        )
        logsum = lax.dynamic_index_in_dim(logsum_items, item_index, 0, keepdims=False)
        probability = jnp.exp(scores - logsum[:, None])
        grad_part = lax.dynamic_slice(
            grad_attended, (row_first, head_index * HD), (query_block, HD)
        )
        grad_prob = contract_last(grad_part, value_head)
        inner_sum = jnp.sum(probability * grad_prob, axis=1, keepdims=True)
        grad_scores = (probability * (grad_prob - inner_sum)).astype(jnp.bfloat16)
        query_grad = jnp.dot(grad_scores, key_head, preferred_element_type=jnp.float32) * attn_scale
        key_part = contract_first(grad_scores, query_part) * attn_scale
        value_part = contract_first(probability.astype(jnp.bfloat16), grad_part)
        key_old = lax.dynamic_slice_in_dim(key_grad, kv_index * HD, HD, 1)
        key_grad = lax.dynamic_update_slice_in_dim(key_grad, key_old + key_part, kv_index * HD, 1)
        value_old = lax.dynamic_slice_in_dim(value_grad, kv_index * HD, HD, 1)
        value_grad = lax.dynamic_update_slice_in_dim(
            value_grad, value_old + value_part, kv_index * HD, 1
        )
        return ((key_grad, value_grad), query_grad)

    zero_grads = jnp.zeros((seq_length, kv_local * HD), jnp.float32)
    (key_grad_seq, value_grad_seq), query_grad_items = lax.scan(
        attend_back, (zero_grads, zero_grads), jnp.arange(item_count, dtype=jnp.int32)
    )
    key_grad_block, value_grad_block = (
        lax.psum_scatter(
            key_grad_seq.astype(jnp.bfloat16), "nar", scatter_dimension=0, tiled=True
        ).astype(jnp.float32),
        lax.psum_scatter(
            value_grad_seq.astype(jnp.bfloat16), "nar", scatter_dimension=0, tiled=True
        ).astype(jnp.float32),
    )
    query_grad_rows = (
        query_grad_items.reshape(block_count, query_heads, query_block, HD)
        .transpose(0, 2, 1, 3)
        .reshape(block_tokens, query_heads, HD)
    )
    query_grad_b = (
        rotate_back(query_grad_rows, cosine_table, sine_table)
        .astype(jnp.bfloat16)
        .reshape(block_tokens, query_heads * HD)
    )
    key_grad_b = (
        rotate_back(key_grad_block.reshape(block_tokens, kv_local, HD), cosine_table, sine_table)
        .astype(jnp.bfloat16)
        .reshape(block_tokens, kv_local * HD)
    )
    value_grad_b = value_grad_block.astype(jnp.bfloat16)
    query_weight_grad = contract_first(normed_rows, query_grad_b)
    key_weight_grad = contract_first(normed_rows, key_grad_b)
    value_weight_grad = contract_first(normed_rows, value_grad_b)
    grad_normed_attn = lax.psum_scatter(
        (
            contract_last(query_grad_b, query_full)
            + contract_last(key_grad_b, key_local)
            + contract_last(value_grad_b, value_local)
        ).astype(jnp.bfloat16),
        "wid",
        scatter_dimension=0,
        tiled=True,
    ).astype(jnp.float32)
    grad_residual, gain_attn_term = norm_backward(residual, root_attn, gain_attn, grad_normed_attn)
    grad_in = (grad_residual + grad_middle).astype(jnp.bfloat16)[None]
    summed = (
        lax.psum_scatter(
            query_weight_grad.astype(jnp.bfloat16), ("row", "nar"), scatter_dimension=0, tiled=True
        ).astype(jnp.float32),
        lax.psum_scatter(
            key_weight_grad.astype(jnp.bfloat16), ("row", "nar"), scatter_dimension=0, tiled=True
        ).astype(jnp.float32),
        lax.psum_scatter(
            value_weight_grad.astype(jnp.bfloat16), ("row", "nar"), scatter_dimension=0, tiled=True
        ).astype(jnp.float32),
        lax.psum_scatter(
            output_weight_grad.astype(jnp.bfloat16), ("row", "nar"), scatter_dimension=1, tiled=True
        ).astype(jnp.float32),
        lax.psum_scatter(
            gate_weight_grad.astype(jnp.bfloat16), ("row", "nar"), scatter_dimension=0, tiled=True
        ).astype(jnp.float32),
        lax.psum_scatter(
            up_weight_grad.astype(jnp.bfloat16), ("row", "nar"), scatter_dimension=0, tiled=True
        ).astype(jnp.float32),
        lax.psum_scatter(
            down_weight_grad.astype(jnp.bfloat16), ("row", "nar"), scatter_dimension=1, tiled=True
        ).astype(jnp.float32),
        lax.psum_scatter(
            gain_attn_term.astype(jnp.bfloat16), ("row", "nar"), scatter_dimension=0, tiled=True
        ).astype(jnp.float32),
        lax.psum_scatter(
            gain_ffn_term.astype(jnp.bfloat16), ("row", "nar"), scatter_dimension=0, tiled=True
        ).astype(jnp.float32),
    )
    (
        grad_query,
        key_sum,
        value_sum,
        grad_output,
        grad_gate,
        grad_up,
        grad_down,
        gain_attn_sum,
        gain_ffn_sum,
    ) = summed
    key_all, value_all, gain_attn_all, gain_ffn_all = (
        lax.all_gather(key_sum.astype(jnp.bfloat16), "wid", axis=1, tiled=True).astype(
            key_sum.dtype
        ),
        lax.all_gather(value_sum.astype(jnp.bfloat16), "wid", axis=1, tiled=True).astype(
            value_sum.dtype
        ),
        lax.all_gather(gain_attn_sum.astype(jnp.bfloat16), "wid", axis=0, tiled=True).astype(
            gain_attn_sum.dtype
        ),
        lax.all_gather(gain_ffn_sum.astype(jnp.bfloat16), "wid", axis=0, tiled=True).astype(
            gain_ffn_sum.dtype
        ),
    )
    shard_rows = key_sum.shape[0]
    repeats = wid_count * kv_local // KV
    grad_key = key_all.reshape(shard_rows, KV, repeats, HD).sum(axis=2).reshape(shard_rows, KV * HD)
    grad_value = (
        value_all.reshape(shard_rows, KV, repeats, HD).sum(axis=2).reshape(shard_rows, KV * HD)
    )
    grad_gain_attn = gain_attn_all.reshape(wid_count, shard_rows).sum(axis=0)
    grad_gain_ffn = gain_ffn_all.reshape(wid_count, shard_rows).sum(axis=0)
    return (
        hidden_out,
        grad_in,
        grad_query,
        grad_key,
        grad_value,
        grad_output,
        grad_gate,
        grad_up,
        grad_down,
        grad_gain_attn,
        grad_gain_ffn,
    )


MESH = pl.DeviceIdType.MESH
bf16 = jnp.bfloat16
f32 = jnp.float32
VMEM_LIMIT = 60 * 2**20


def spot():
    return lax.axis_index("row"), lax.axis_index("nar"), lax.axis_index("wid")


def greet(partners):
    barrier = pltpu.get_barrier_semaphore()
    total = 0
    for there, device in partners:
        @pl.when(there)
        def _():
            pl.semaphore_signal(barrier, inc=1, device_id=device, device_id_type=MESH)

        total = total + there.astype(jnp.int32)
    pl.semaphore_wait(barrier, total)


def line_partners(r, n, w, wid_count):
    return [
        (w < wid_count - 1, (r, n, jnp.minimum(w + 1, wid_count - 1))),
        (w > 0, (r, n, jnp.maximum(w - 1, 0))),
        (w >= 0, (1 - r, n, w)),
    ]


def each_rows(count, step, body):
    def run(i, carry):
        body(pl.ds(pl.multiple_of(i * step, step), step))
        return carry

    lax.fori_loop(0, count // step, run, 0)


def square_partners(r, n, w):
    return [(n >= 0, over_x(r, n, w)), (n >= 0, over_y(r, n, w))]


def over_x(r, n, w):
    return (r, n + 1 - 2 * (n % 2), w)


def over_y(r, n, w):
    return (r, (n + 2) % 4, w)


def push(source, target, s_s, s_g, device):
    return pltpu.make_async_remote_copy(
        source, target, s_s, s_g, device_id=device, device_id_type=MESH
    )


class Gather:
    def __init__(self, buf, sems, me, wid_count, rows=slice(None), pair=True):
        self.rows, self.both = rows, pair
        self.buf, (self.up_s, self.dn_s, self.pt_s, self.got) = buf, sems
        self.r, self.n, self.w = me
        self.last = wid_count - 1
        self.up = (self.r, self.n, jnp.minimum(self.w + 1, self.last))
        self.dn = (self.r, self.n, jnp.maximum(self.w - 1, 0))
        self.pt = (1 - self.r, self.n, self.w)

    def copy(self, j, sem, device, row=None):
        row = (self.r if self.both else 0) if row is None else row
        return pltpu.make_async_remote_copy(
            self.buf.at[row, j, self.rows],
            self.buf.at[row, j, self.rows],
            sem.at[j],
            self.got.at[row, j],
            device_id=device,
            device_id_type=MESH,
        )

    def pass_on(self, j, go_up, go_dn):
        if go_up:
            @pl.when(self.w < self.last)
            def _():
                self.copy(j, self.up_s, self.up).start()

        if go_dn:
            @pl.when(self.w > 0)
            def _():
                self.copy(j, self.dn_s, self.dn).start()

        if self.both:
            self.copy(j, self.pt_s, self.pt).start()

    def own(self):
        self.pass_on(self.w, True, True)

    def arrive(self, row, j):
        self.copy(j, self.pt_s, self.pt, row).wait_recv()

    def step(self, k):
        below, above = self.w - k, self.w + k

        @pl.when(below >= 0)
        def _():
            self.arrive(None, below)
            self.pass_on(below, True, False)

        @pl.when(above <= self.last)
        def _():
            self.arrive(None, above)
            self.pass_on(above, False, True)

    def advance(self, edge_steps, inner_steps):
        at_end = (self.w == 0) | (self.w == self.last)
        for ends, steps in ((True, edge_steps), (False, inner_steps)):
            if steps:
                @pl.when(at_end if ends else jnp.logical_not(at_end))
                def _():
                    for k in steps:
                        self.step(k)

    def rest(self):
        for j in range(self.last + 1):
            self.arrive(1 - self.r, j)

    def sent(self):
        for j in range(self.last + 1):
            @pl.when((j <= self.w) & (self.w < self.last))
            def _():
                self.copy(j, self.up_s, self.up).wait_send()

            @pl.when((j >= self.w) & (self.w > 0))
            def _():
                self.copy(j, self.dn_s, self.dn).wait_send()

            if self.both:
                self.copy(j, self.pt_s, self.pt).wait_send()


def gather_scratch(shard, width):
    return [pltpu.VMEM((2, 4, shard, width), bf16)] + gather_sems()


def gather_sems():
    return [pltpu.SemaphoreType.DMA((4,))] * 3 + [pltpu.SemaphoreType.DMA((2, 4))]


class Scatter:
    def __init__(self, mine, theirs, bufs, sems, me, wid_count, first=0, count=None):
        self.mine, self.theirs = mine, theirs
        self.from_pt, self.from_up, self.from_dn = bufs
        self.pt_s, self.pt_g, self.up_s, self.up_g, self.dn_s, self.dn_g = sems
        self.r, self.n, self.w = me
        self.first, self.count = first, mine.shape[1] if count is None else count
        self.rows = pl.ds(first, self.count)
        self.last = wid_count - 1
        self.up = (self.r, self.n, jnp.minimum(self.w + 1, self.last))
        self.dn = (self.r, self.n, jnp.maximum(self.w - 1, 0))
        self.pt = (1 - self.r, self.n, self.w)

    def order(self, i):
        low = jnp.where(i == 0, 3, jnp.where(i == 1, 0, jnp.where(i == 2, 2, 1)))
        return jnp.where(self.w < 2, low, 3 - low)

    def send(self, source, target, sent, got, s, device):
        return pltpu.make_async_remote_copy(
            source.at[s, self.rows], target.at[s, self.rows], sent.at[s], got.at[s],
            device_id=device, device_id_type=MESH,
        )

    def pair(self, s):
        return self.send(self.theirs, self.from_pt, self.pt_s, self.pt_g, s, self.pt)

    def climb(self, s):
        return self.send(self.mine, self.from_dn, self.up_s, self.up_g, s, self.up)

    def fall(self, s):
        return self.send(self.mine, self.from_up, self.dn_s, self.dn_g, s, self.dn)

    def each(self, body):
        def run(i, carry):
            body(pl.ds(pl.multiple_of(self.first + i * 16, 16), 16))
            return carry

        lax.fori_loop(0, self.count // 16, run, 0)

    def add(self, s, others):
        def body(rows):
            total = self.mine[s, rows, :].astype(f32)
            for other in others:
                total = total + other[s, rows, :].astype(f32)
            self.mine[s, rows, :] = total.astype(bf16)

        self.each(body)

    def step(self, s):
        self.pair(s).wait_recv()

        @pl.when((s > self.w) & (self.w > 0))
        def _():
            self.climb(s).wait_recv()
            self.add(s, (self.from_pt, self.from_dn))

        @pl.when((s < self.w) & (self.w < self.last))
        def _():
            self.fall(s).wait_recv()
            self.add(s, (self.from_pt, self.from_up))

        @pl.when(((s > self.w) & (self.w == 0)) | ((s < self.w) & (self.w == self.last)))
        def _():
            self.add(s, (self.from_pt,))

        @pl.when(s > self.w)
        def _():
            self.climb(s).start()

        @pl.when(s < self.w)
        def _():
            self.fall(s).start()

    def advance(self, edge_steps, inner_steps):
        for ends, steps in ((True, edge_steps), (False, inner_steps)):
            at_end = (self.w == 0) | (self.w == self.last)

            def body(i, carry):
                self.step(self.order(i))
                return carry

            if steps:
                @pl.when(at_end if ends else jnp.logical_not(at_end))
                def _():
                    lax.fori_loop(steps[0], steps[-1] + 1, body, 0)

    def total(self, out):
        w = self.w

        def first(rows):
            out[rows, :] = self.mine[w, rows, :].astype(f32) + self.from_pt[w, rows, :].astype(f32)

        self.each(first)

        @pl.when(w > 0)
        def _():
            self.climb(w).wait_recv()

            def more(rows):
                out[rows, :] += self.from_dn[w, rows, :].astype(f32)

            self.each(more)

        @pl.when(w < self.last)
        def _():
            self.fall(w).wait_recv()

            def more(rows):
                out[rows, :] += self.from_up[w, rows, :].astype(f32)

            self.each(more)

    def sent(self):
        for s in range(self.last + 1):
            self.pair(s).wait_send()

            @pl.when(s > self.w)
            def _():
                self.climb(s).wait_send()

            @pl.when(s < self.w)
            def _():
                self.fall(s).wait_send()


def scatter_bufs(shard, width):
    return [pltpu.VMEM((4, shard, width), bf16)] * 3


def scatter_sems():
    return [pltpu.SemaphoreType.DMA((4,))] * 6


def vmem():
    return pl.BlockSpec(memory_space=pltpu.VMEM)


def hbm():
    return pl.BlockSpec(memory_space=pl.ANY)


def comm_call(kernel, name, cid, out_shape, in_specs, out_specs, scratch, args, flops=0, sent=0):
    return pl.pallas_call(
        kernel,
        out_shape=out_shape,
        in_specs=in_specs,
        out_specs=out_specs,
        scratch_shapes=scratch,
        compiler_params=pltpu.CompilerParams(
            collective_id=cid, has_side_effects=True, vmem_limit_bytes=VMEM_LIMIT
        ),
        cost_estimate=pl.CostEstimate(flops=flops, bytes_accessed=sent, transcendentals=0),
        name=name,
    )(*args)


def norm_rows(x, gain):
    root = lax.rsqrt(jnp.mean(x * x, axis=-1, keepdims=True) + norm_eps)
    return x * root * gain


def turn(x, cosine, sine):
    lane = lax.broadcasted_iota(jnp.int32, x.shape, 1)
    swapped = jnp.where(lane % 64 < 32, pltpu.roll(x, 96, 1), pltpu.roll(x, 32, 1))
    return x * cosine + swapped * sine


def enter_kernel(hidden, gain, tab, rows_out, tabs_out, buf, up_s, dn_s, pt_s, got, tabs, tab_s, tab_g, out_s):
    me = spot()
    r, n, w = me
    greet(line_partners(r, n, w, 4))
    gather = Gather(buf, (up_s, dn_s, pt_s, got), me, 4)
    tab_copy = pltpu.make_async_remote_copy(
        tab, tabs.at[r], tab_s, tab_g, device_id=(1 - r, n, w), device_id_type=MESH
    )

    def body(rows):
        buf[r, w, rows, :] = norm_rows(hidden[rows, :].astype(f32), gain[...]).astype(bf16)

    each_rows(hidden.shape[0], 16, body)
    gather.own()
    tab_copy.start()

    def keep(rows):
        tabs[r, rows, :] = tab[rows, :]

    each_rows(tab.shape[0], 16, keep)
    for k in (1, 2, 3):
        gather.step(k)
    gather.rest()
    out = pltpu.make_async_copy(buf, rows_out, out_s.at[0])
    out.start()
    tab_copy.wait_recv()
    out_tab = pltpu.make_async_copy(tabs, tabs_out, out_s.at[1])
    out_tab.start()
    gather.sent()
    tab_copy.wait_send()
    out.wait()
    out_tab.wait()


def enter(hidden, gain, tab):
    shard, width = hidden.shape
    return comm_call(
        enter_kernel, "enter", 1,
        (
            jax.ShapeDtypeStruct((2, 4, shard, width), bf16),
            jax.ShapeDtypeStruct((2,) + tab.shape, f32),
        ),
        [vmem()] * 3, [hbm()] * 2,
        gather_scratch(shard, width)
        + [
            pltpu.VMEM((2,) + tab.shape, f32),
            pltpu.SemaphoreType.DMA(()),
            pltpu.SemaphoreType.DMA(()),
            pltpu.SemaphoreType.DMA((2,)),
        ],
        (hidden, gain, tab), flops=10**10, sent=10**8,
    )


def nar_device(r, n, w, by):
    return (r, jnp.clip(n + by, 0, 3), w)


def project_kernel(
    x, p1, tabs, grad_top, q_out, kv_out, tops_out, kv, s_s, s_g, out_s, buf, g0, g1, g2, g3, tops_s
):
    r, n, w = spot()
    greet(
        line_partners(r, n, w, 4)
        + [
            (n >= 1, nar_device(r, n, w, -1)),
            (n >= 2, nar_device(r, n, w, -2)),
            (n <= 2, nar_device(r, n, w, 1)),
            (n <= 1, nar_device(r, n, w, 2)),
        ]
    )
    gather = Gather(buf, (g0, g1, g2, g3), (r, n, w), 4)

    def keep(rows):
        buf[r, w, rows, :] = grad_top[rows, :]

    each_rows(64, 16, keep)
    gather.own()

    def copy(row, slot, by):
        return pltpu.make_async_remote_copy(
            kv.at[row, 2], kv.at[row, slot], s_s.at[row, slot], s_g.at[row, slot],
            device_id=nar_device(r, n, w, by), device_id_type=MESH,
        )

    lane = lax.broadcasted_iota(jnp.int32, (256, 128), 1)
    weight = p1[:, :, 0:384].reshape(2048, 384)
    for row in range(2):
        def tile(i, carry):
            rows = pl.ds(pl.multiple_of(i * 256, 256), 256)
            cosine, sine = tabs[row, rows, 0:128], tabs[row, rows, 128:256]
            pre = jnp.dot(x[row, rows, :], weight, preferred_element_type=f32)
            q_out[row, rows, 0:128] = turn(pre[:, 0:128], cosine, sine).astype(bf16)
            q_out[row, rows, 128:256] = turn(pre[:, 128:256], cosine, sine).astype(bf16)
            both = pre[:, 256:384]
            kv[row, 2, rows, :] = jnp.where(lane < 64, turn(both, cosine, sine), both).astype(bf16)
            return carry

        lax.fori_loop(0, 2, tile, 0)

        @pl.when(n <= 2)
        def _():
            copy(row, 1, 1).start()

        @pl.when(n <= 1)
        def _():
            copy(row, 0, 2).start()

        for slot, least in ((1, 1), (0, 2)):
            @pl.when(n < least)
            def _():
                kv[row, slot] = jnp.zeros((512, 128), bf16)

    for k in (1, 2, 3):
        gather.step(k)
    gather.rest()
    tops_copy = pltpu.make_async_copy(buf, tops_out, tops_s)
    tops_copy.start()
    for row in range(2):
        for slot, least, by in ((1, 1, 1), (0, 2, 2)):
            @pl.when(n >= least)
            def _():
                copy(row, slot, by).wait_recv()

    out = pltpu.make_async_copy(kv, kv_out, out_s)
    out.start()
    for row in range(2):
        @pl.when(n <= 2)
        def _():
            copy(row, 1, 1).wait_send()

        @pl.when(n <= 1)
        def _():
            copy(row, 0, 2).wait_send()

    gather.sent()
    out.wait()
    tops_copy.wait()


def project(x, p1, tabs, grad_top):
    return comm_call(
        project_kernel, "project", 2,
        (
            jax.ShapeDtypeStruct((2, 512, 256), bf16),
            jax.ShapeDtypeStruct((2, 3, 512, 128), bf16),
            jax.ShapeDtypeStruct((2, 4, 64, 2048), bf16),
        ),
        [vmem()] * 4, [vmem(), hbm(), hbm()],
        [
            pltpu.VMEM((2, 3, 512, 128), bf16),
            pltpu.SemaphoreType.DMA((2, 3)),
            pltpu.SemaphoreType.DMA((2, 3)),
            pltpu.SemaphoreType.DMA(()),
        ]
        + gather_scratch(64, 2048)
        + [pltpu.SemaphoreType.DMA(())],
        (x, p1, tabs, grad_top), flops=10**10, sent=10**7,
    )


KEYS = 256
QUERIES = 128


def stack_low(x):
    lane = lax.broadcasted_iota(jnp.int32, (QUERIES, 128), 1)
    zero = jnp.zeros((QUERIES, 128), x.dtype)
    parts = []
    for pair in range(2):
        block = x[:, pair * 128 : pair * 128 + 128]
        parts.append(jnp.where(lane < 64, block, zero))
        parts.append(jnp.where(lane < 64, pltpu.roll(block, 64, 1), zero))
    return jnp.concatenate(parts, axis=0)


def stack_high(x):
    lane = lax.broadcasted_iota(jnp.int32, (QUERIES, 128), 1)
    zero = jnp.zeros((QUERIES, 128), x.dtype)
    parts = []
    for pair in range(2):
        block = x[:, pair * 128 : pair * 128 + 128]
        parts.append(jnp.where(lane >= 64, pltpu.roll(block, 64, 1), zero))
        parts.append(jnp.where(lane >= 64, block, zero))
    return jnp.concatenate(parts, axis=0)


def unstack(x, low):
    lane = lax.broadcasted_iota(jnp.int32, (QUERIES, 128), 1)
    out = []
    for pair in range(2):
        even = x[2 * pair * QUERIES : (2 * pair + 1) * QUERIES]
        odd = x[(2 * pair + 1) * QUERIES : (2 * pair + 2) * QUERIES]
        if low:
            out.append(jnp.where(lane < 64, even, pltpu.roll(odd, 64, 1)))
        else:
            out.append(jnp.where(lane < 64, pltpu.roll(even, 64, 1), odd))
    return jnp.concatenate(out, axis=1)


def allowed_tile(starts, tile, first_query):
    key = lax.broadcasted_iota(jnp.int32, (QUERIES, KEYS), 1) + tile * KEYS
    query = lax.broadcasted_iota(jnp.int32, (QUERIES, KEYS), 0) + first_query
    start = jnp.concatenate([starts] * (KEYS // 128), axis=1)
    ok = (key <= query) & (key.astype(f32) >= start)
    return jnp.concatenate([ok] * 4, axis=0)


def attend_kernel(q, kv, starts, out, lse):
    block = pl.program_id(1)
    first_query = 1024 + block * QUERIES
    query = stack_low(q[0].astype(f32)).astype(bf16)

    def body(step, carry):
        tile = block // 2 + step
        top, total, acc = carry
        both = kv[0, pl.ds(pl.multiple_of(tile * KEYS, KEYS), KEYS), :]
        scores = contract_last(query, both) * 0.125
        ok = allowed_tile(starts[0], tile, first_query)
        scores = jnp.where(ok, scores, masked_score)
        new_top = jnp.maximum(top, jnp.max(scores, axis=1, keepdims=True))
        shrink = jnp.exp(top - new_top)
        part = jnp.exp(scores - new_top)
        total = total * shrink + jnp.sum(part, axis=1, keepdims=True)
        acc = acc * shrink + jnp.dot(part.astype(bf16), both, preferred_element_type=f32)
        return new_top, total, acc

    top, total, acc = lax.fori_loop(
        0, 5, body,
        (
            jnp.full((4 * QUERIES, 1), masked_score, f32),
            jnp.zeros((4 * QUERIES, 1), f32),
            jnp.zeros((4 * QUERIES, 128), f32),
        ),
        unroll=True,
    )
    out[0] = unstack(acc / total, False).astype(bf16)
    lse[0, 0] = jnp.broadcast_to(top + jnp.log(total), (4 * QUERIES, 128))


def attend_specs():
    return [
        pl.BlockSpec((1, QUERIES, 256), lambda i, j: (i, j, 0)),
        pl.BlockSpec((1, 1536, 128), lambda i, j: (i, 0, 0)),
        pl.BlockSpec((1, QUERIES, 128), lambda i, j: (i, j, 2)),
    ]


def attend(q, kv, tabs):
    return pl.pallas_call(
        attend_kernel,
        out_shape=(
            jax.ShapeDtypeStruct((2, 512, 256), bf16),
            jax.ShapeDtypeStruct((2, 4, 4 * QUERIES, 128), f32),
        ),
        grid_spec=pl.GridSpec(
            grid=(2, 4),
            in_specs=attend_specs(),
            out_specs=[
                pl.BlockSpec((1, QUERIES, 256), lambda i, j: (i, j, 0)),
                pl.BlockSpec((1, 1, 4 * QUERIES, 128), lambda i, j: (i, j, 0, 0)),
            ],
        ),
        compiler_params=pltpu.CompilerParams(vmem_limit_bytes=VMEM_LIMIT),
        cost_estimate=pl.CostEstimate(flops=2 * 10**10, bytes_accessed=10**7, transcendentals=10**7),
        name="attend",
    )(q, kv, tabs)


def out_block(p1, nn, half):
    return p1[nn, half * 256 : half * 256 + 256, 384:640]


def middle_kernel(
    att, p1, hidden, gain, mid_out, ffn_out,
    theirs, mine, from_pt, from_up, from_dn, s0, s1, s2, s3, s4, s5, fbuf, h0, h1, h2, h3, out_s,
):
    me = spot()
    r, n, w = me
    greet(line_partners(r, n, w, 4))
    scatter = Scatter(
        mine, theirs, (from_pt, from_up, from_dn), (s0, s1, s2, s3, s4, s5), me, 4
    )
    ffn = Gather(fbuf, (h0, h1, h2, h3), me, 4)
    def shard(i, carry):
        s = scatter.order(i)
        rows = pl.ds(pl.multiple_of(s * 128, 128), 128)
        left = jnp.concatenate([att[1 - r, rows, :], att[r, rows, :]], axis=0)
        for nn in range(4):
            for half in range(2):
                part = jnp.dot(left, out_block(p1, nn, half), preferred_element_type=f32).astype(bf16)
                columns = slice(nn * 512 + half * 256, nn * 512 + half * 256 + 256)
                theirs[s, :, columns] = part[0:128]
                mine[s, :, columns] = part[128:256]
        scatter.pair(s).start()
        return carry

    lax.fori_loop(0, 4, shard, 0)
    scatter.advance((0, 1, 2, 3), (0, 1, 2, 3))
    scatter.total(mid_out)

    def body(rows):
        middle = mid_out[rows, :] + hidden[rows, :].astype(f32)
        mid_out[rows, :] = middle
        fbuf[r, w, rows, :] = norm_rows(middle, gain[...]).astype(bf16)

    each_rows(hidden.shape[0], 16, body)
    ffn.own()
    for k in (1, 2, 3):
        ffn.step(k)
    ffn.rest()
    out_f = pltpu.make_async_copy(fbuf, ffn_out, out_s)
    out_f.start()
    scatter.sent()
    ffn.sent()
    out_f.wait()


def middle_stage(att, p1, hidden, gain):
    shard, width = hidden.shape
    rows = jax.ShapeDtypeStruct((2, 4, shard, width), bf16)
    return comm_call(
        middle_kernel, "middle", 3,
        (jax.ShapeDtypeStruct((shard, width), f32), rows),
        [vmem()] * 4, [vmem(), hbm()],
        [pltpu.VMEM((4, shard, width), bf16)] * 2
        + scatter_bufs(shard, width) + scatter_sems()
        + gather_scratch(shard, width)
        + [pltpu.SemaphoreType.DMA(())],
        (att, p1, hidden, gain), flops=10**10, sent=2 * 10**8,
    )


class Spread:
    def __init__(self, outs, sems, me):
        self.a_send, self.a_keep, self.b_send, self.b_keep = outs
        self.r, self.n, self.w = me
        self.give_s, self.give_g, self.keep_s = sems

    def copies(self, wide, row, place, give):
        for k in range(4):
            block = wide.at[self.n ^ k]
            for part in range(2):
                source = block.at[pl.ds(part * 128, 128)]
                if part == 0:
                    target = (self.a_send if k & 1 else self.a_keep).at[k >> 1]
                else:
                    target = (self.b_send if k >= 2 else self.b_keep).at[k & 1]
                target = place(target)
                at = k * 2 + part
                if give:
                    yield pltpu.make_async_remote_copy(
                        source, target, self.give_s.at[row, at], self.give_g.at[row, at],
                        device_id=(1 - self.r, self.n, self.w), device_id_type=MESH,
                    )
                else:
                    yield pltpu.make_async_copy(source, target, self.keep_s.at[row, at])

    def start(self, *args):
        for copy in self.copies(*args):
            copy.start()

    def wait_send(self, *args):
        for copy in self.copies(*args):
            copy.wait_send()

    def wait_recv(self, *args):
        for copy in self.copies(*args):
            copy.wait_recv()

    def wait(self, *args):
        for copy in self.copies(*args):
            copy.wait()


def spread_sems(count):
    return [pltpu.SemaphoreType.DMA((count, 8))] * 3


def ffn_kernel(
    x, tops_in, grad_top, p2_all, gain,
    part_out, sum_out, gain_out, o0, o1, o2, o3, ra_out, rb_out,
    theirs, mine, from_pt, from_up, from_dn, s0, s1, s2, s3, s4, s5,
    act, dgu, wide, out_s, give_s, give_g, keep_s, p2, in_s, n_s, n_g,
    tops4, h0, h1, h2, h3, tops_s,
):
    me = spot()
    r, n, w = me
    loads = [pltpu.make_async_copy(p2_all.at[:, j], p2.at[j], in_s.at[j]) for j in range(3)]
    loads.append(pltpu.make_async_copy(tops_in, tops4.at[:, :, 0:64], tops_s))
    for load in loads:
        load.start()
    greet(line_partners(r, n, w, 4) + square_partners(r, n, w))
    scatter = Scatter(
        mine, theirs, (from_pt, from_up, from_dn), (s0, s1, s2, s3, s4, s5), me, 4
    )
    late = pl.ds(64, 64)
    gather = Gather(tops4, (h0, h1, h2, h3), me, 4, late)

    def keep(rows):
        tops4[r, w, pl.ds(64 + rows.start, 16), :] = grad_top[pl.ds(64 + rows.start, 16), :]

    each_rows(64, 16, keep)
    gather.own()
    gain_out[...] = jnp.zeros_like(gain_out)
    loads[0].wait()
    loads[1].wait()

    def hidden_tile(i, carry):
        ft, row = i // 2, i % 2
        rows = pl.ds(pl.multiple_of(row * 512, 512), 512)
        columns = pl.ds(pl.multiple_of(ft * 256, 256), 256)
        left = x[rows, :]
        gate = jnp.dot(left, p2[0, :, :, columns].reshape(2048, 256), preferred_element_type=f32)
        up = jnp.dot(left, p2[1, :, :, columns].reshape(2048, 256), preferred_element_type=f32)
        sig = 1.0 / (1.0 + jnp.exp(-gate))
        silu = gate * sig
        act[rows, columns] = (silu * up).astype(bf16)
        dgu[rows, columns] = (up * (sig * (1.0 + gate * (1.0 - sig)))).astype(bf16)
        later = pl.ds(pl.multiple_of(1024 + ft * 256, 256), 256)
        dgu[rows, later] = silu.astype(bf16)
        return carry

    lax.fori_loop(0, 4, hidden_tile, 0)
    gather.step(1)
    lax.fori_loop(4, 8, hidden_tile, 0)
    gather.step(2)
    loads[2].wait()

    def down_tile(dt, carry):
        nn, half = dt // 2, dt % 2
        columns = pl.ds(pl.multiple_of(dt * 256, 256), 256)
        inner = pl.ds(pl.multiple_of(half * 256, 256), 256)
        other = pl.ds(pl.multiple_of(512 + half * 256, 256), 256)
        right = jnp.concatenate([p2[2, nn, :, inner], p2[2, nn, :, other]], axis=0)
        for row, stage in ((0, theirs), (1, mine)):
            part = jnp.dot(act[row * 512 : row * 512 + 512, :], right, preferred_element_type=f32)
            stage[:, :, columns] = part.astype(bf16).reshape(4, 128, 256)
        return carry

    lax.fori_loop(0, 8, down_tile, 0)
    puts = [
        pltpu.make_async_copy(theirs, part_out.at[0], out_s.at[0]),
        pltpu.make_async_copy(mine, part_out.at[1], out_s.at[1]),
    ]
    for put in puts:
        put.start()
    gather.step(3)
    gather.rest()
    loads[3].wait()

    def top_rows(row):
        return tops4[row].reshape(512, 2048)

    def back_tile(ft, carry):
        columns = pl.ds(pl.multiple_of(ft * 256, 256), 256)
        f_rows = pl.ds(pl.multiple_of((ft % 2) * 256, 256), 256)
        f_cols = pl.ds(pl.multiple_of((ft // 2) * 512, 512), 512)
        later = pl.ds(pl.multiple_of(1024 + ft * 256, 256), 256)
        right = jnp.concatenate([p2[2, nn, f_rows, f_cols] for nn in range(4)], axis=1)
        for row in range(2):
            rows = slice(row * 512, row * 512 + 512)
            dact = contract_last(top_rows(row), right)
            dgu[rows, columns] = (dact * dgu[rows, columns].astype(f32)).astype(bf16)
            dgu[rows, later] = (dact * dgu[rows, later].astype(f32)).astype(bf16)
        return carry

    lax.fori_loop(0, 4, back_tile, 0)
    for put in puts:
        put.wait()

    spread = Spread((o0, o1, o2, o3), (give_s, give_g, keep_s), me)
    columns_here = pl.ds(pl.multiple_of(r * 1024, 1024), 1024)
    slots = {2: 0, 0: 1, 1: 0}

    def moved(which, half):
        def place(target):
            return target.at[which, :, columns_here]

        return wide.at[slots[which], half], which, place, half == 0

    def weights(which, between=None):
        for half in range(2):
            d_first = (jnp.where(half == 0, 1 - r, r)) * 1024

            def weight_tile(i, carry):
                d_cols = pl.ds(pl.multiple_of(d_first + i * 256, 256), 256)
                if which < 2:
                    left = x[:, d_cols]
                    right = dgu[:, which * 1024 : which * 1024 + 1024]
                else:
                    left = tops4[:, :, :, d_cols].reshape(1024, 256)
                    right = act[...]
                wide[slots[which], half, i] = contract_first(left, right).astype(bf16)
                return carry

            lax.fori_loop(0, 4, weight_tile, 0)
            spread.start(*moved(which, half))
            if half == 0 and between is not None:
                between()

    def hop(which, at):
        return (
            push(o0.at[:, which], ra_out.at[at], n_s.at[0, at], n_g.at[0, at], over_x(r, n, w)),
            push(o2.at[:, which], rb_out.at[at], n_s.at[1, at], n_g.at[1, at], over_y(r, n, w)),
        )

    hops = hop(2, 0) + hop(0, 1)
    weights(2)
    for i in range(4):
        s = scatter.order(i)
        rows_t = pl.ds(pl.multiple_of((1 - r) * 512 + s * 128, 128), 128)
        rows_m = pl.ds(pl.multiple_of(r * 512 + s * 128, 128), 128)

        def model_tile(dt, carry):
            nn, half = dt // 2, dt % 2
            columns = pl.ds(pl.multiple_of(dt * 256, 256), 256)
            inner = pl.ds(pl.multiple_of(half * 256, 256), 256)
            left = jnp.concatenate([dgu[rows_t, :], dgu[rows_m, :]], axis=0)
            right = jnp.concatenate([p2[0, nn, inner, :], p2[1, nn, inner, :]], axis=1)
            part = contract_last(left, right)
            seen = jnp.concatenate([x[rows_t, columns], x[rows_m, columns]], axis=0)
            terms = part * seen.astype(f32)
            gain_out[:, columns] += jnp.sum(terms.reshape(32, 8, 256), axis=0)
            part = part.astype(bf16)
            theirs[s, :, columns] = part[0:128]
            mine[s, :, columns] = part[128:256]
            return carry

        lax.fori_loop(0, 8, model_tile, 0)
        scatter.pair(s).start()
        if i < 2:
            which = (2, 0)[i]
            spread.wait_recv(*moved(which, 0))
            spread.wait(*moved(which, 1))
            hops[2 * i].start()
            hops[2 * i + 1].start()
        if i == 0:
            weights(0)
            scatter.advance((0,), ())
        elif i > 1:
            scatter.advance((i - 1,), (i - 2,))

    def scale(rows):
        gain_out[rows, :] = gain_out[rows, :] / gain[...]

    each_rows(8, 8, scale)
    spread.wait_send(*moved(2, 0))
    weights(1, lambda: scatter.advance((3,), (2,)))
    scatter.advance((), (3,))
    scatter.total(sum_out)
    scatter.sent()
    gather.sent()
    spread.wait_send(*moved(0, 0))
    spread.wait_recv(*moved(1, 0))
    spread.wait_send(*moved(1, 0))
    spread.wait(*moved(1, 1))
    for hop in hops:
        hop.wait()


def spread_shapes(*dims):
    return (jax.ShapeDtypeStruct((2,) + dims, bf16),) * 4


def ffn_stage(*args):
    shard, width = 128, 2048
    return comm_call(
        ffn_kernel, "ffn", 4,
        (
            jax.ShapeDtypeStruct((2, 4, shard, width), bf16),
            jax.ShapeDtypeStruct((shard, width), f32),
            jax.ShapeDtypeStruct((8, width), f32),
        )
        + spread_shapes(3, 128, width)
        + (jax.ShapeDtypeStruct((2, 2, 128, width), bf16),) * 2,
        [vmem(), hbm(), vmem(), hbm(), vmem()], [hbm(), vmem(), vmem()] + [hbm()] * 6,
        [pltpu.VMEM((4, shard, width), bf16)] * 2
        + scatter_bufs(shard, width) + scatter_sems()
        + [
            pltpu.VMEM((1024, 1024), bf16),
            pltpu.VMEM((1024, 2048), bf16),
            pltpu.VMEM((2, 2, 4, 256, 1024), bf16),
            pltpu.SemaphoreType.DMA((2,)),
        ]
        + spread_sems(3)
        + [pltpu.VMEM((3, 4, 512, 1024), bf16), pltpu.SemaphoreType.DMA((3,))]
        + [pltpu.SemaphoreType.DMA((2, 2))] * 2
        + gather_scratch(shard, width)
        + [pltpu.SemaphoreType.DMA(())],
        args, flops=4 * 10**10, sent=10**8,
    )


def norm_back(values, gain, grad):
    root = lax.rsqrt(jnp.mean(values * values, axis=-1, keepdims=True) + norm_eps)
    weighted = grad * gain
    inner = jnp.mean(weighted * values, axis=-1, keepdims=True)
    return root * weighted - values * (root * root * root) * inner


def branch_kernel(
    total, mid, grad_top, gain, p1, att, a_in, b_in, a_keep, b_keep, a_came, b_came,
    gmid_out, datt_out, o0, o1, o2, o3, ra_out, rb_out, la_out, lb_out,
    buf, g0, g1, g2, g3, wide, give_s, give_g, keep_s, n_s, n_g, kept, came, in_s,
):
    me = spot()
    r, n, w = me
    greet(line_partners(r, n, w, 4) + square_partners(r, n, w))
    gather = Gather(buf, (g0, g1, g2, g3), me, 4)
    hops = [
        push(a_in.at[:, 1], ra_out, n_s.at[0], n_g.at[0], over_x(r, n, w)),
        push(b_in.at[:, 1], rb_out, n_s.at[1], n_g.at[1], over_y(r, n, w)),
        push(kept.at[0], la_out, n_s.at[2], n_g.at[2], over_y(r, n, w)),
        push(kept.at[1], lb_out, n_s.at[3], n_g.at[3], over_x(r, n, w)),
    ]
    loads = []
    for j, (keep, first) in enumerate(((a_keep, a_came), (b_keep, b_came))):
        loads += [
            pltpu.make_async_copy(keep.at[1, 2], kept.at[j], in_s.at[j, 0]),
            pltpu.make_async_copy(first.at[0, 1], came.at[j], in_s.at[j, 1]),
        ]
    for load in loads:
        load.start()
    hops[0].start()
    hops[1].start()

    def body(rows):
        grad = norm_back(mid[rows, :], gain[...], total[rows, :]) + grad_top[rows, :].astype(f32)
        gmid_out[rows, :] = grad
        buf[r, w, rows, :] = grad.astype(bf16)

    each_rows(mid.shape[0], 16, body)
    gather.own()
    for load in loads:
        load.wait()
    for j in range(2):
        def join(rows):
            kept[j, rows, :] = (kept[j, rows, :].astype(f32) + came[j, rows, :].astype(f32)).astype(bf16)

        each_rows(128, 16, join)
        hops[2 + j].start()
    for k in (1, 2, 3):
        gather.step(k)
    gather.rest()
    for row in range(2):
        for pair in range(2):
            left = jnp.concatenate([buf[row, 2 * pair], buf[row, 2 * pair + 1]], axis=0)
            right = jnp.concatenate(
                [out_block(p1, nn, half) for nn in range(4) for half in range(2)], axis=1
            )
            datt_out[row, pair * 256 : pair * 256 + 256, :] = contract_last(left, right).astype(bf16)

    spread = Spread((o0, o1, o2, o3), (give_s, give_g, keep_s), me)

    def moved(half):
        def place(target):
            return target.at[:, pl.ds(pl.multiple_of(r * 256, 256), 256)]

        return wide.at[half], 0, place, half == 0

    for half in range(2):
        d_first = (jnp.where(half == 0, 1 - r, r)) * 1024

        def weight_tile(i, carry):
            columns = pl.ds(pl.multiple_of(d_first + i * 256, 256), 256)
            left = buf[:, :, :, columns].reshape(1024, 256)
            wide[half, i] = contract_first(left, att[...]).astype(bf16)
            return carry

        lax.fori_loop(0, 4, weight_tile, 0)
        spread.start(*moved(half))
    gather.sent()
    spread.wait(*moved(0))
    spread.wait(*moved(1))
    for hop in hops:
        hop.wait()


def branch_stage(*args):
    shard, width = 128, 2048
    return comm_call(
        branch_kernel, "branch", 5,
        (
            jax.ShapeDtypeStruct((shard, width), f32),
            jax.ShapeDtypeStruct((2, 512, 256), bf16),
        )
        + spread_shapes(128, 512)
        + (jax.ShapeDtypeStruct((2, 128, width), bf16),) * 2
        + (jax.ShapeDtypeStruct((128, width), bf16),) * 2,
        [vmem()] * 6 + [hbm()] * 6, [vmem(), vmem()] + [hbm()] * 8,
        gather_scratch(shard, width)
        + [pltpu.VMEM((2, 4, 256, 256), bf16)]
        + spread_sems(1)
        + [pltpu.SemaphoreType.DMA((4,))] * 2
        + [pltpu.VMEM((2, 128, width), bf16)] * 2
        + [pltpu.SemaphoreType.DMA((2, 2))],
        args, flops=10**10, sent=10**8,
    )


def unproject_kernel(
    q, kv, att, grad, lse, x, p1, tabs, gain, parts, mid, a_keep, b_keep, a_gate, b_gate, a_up, b_up, oa_in, ob_in,
    part_out, gain_out, o0, o1, o2, o3, hid_out, ra_out, rb_out, roa_out, rob_out,
    send, recv, both, wide_q, wide_kv, s_s, s_g, give_s, give_g, keep_s,
    mine, from_pt, from_up, from_dn, s0, s1, s2, s3, s4, s5,
    kept, came, acc, in_s, n_s, n_g, m_s, dkv,
):
    me = spot()
    r, n, w = me
    loads = []
    for j, (keep, gate, up) in enumerate(((a_keep, a_gate, a_up), (b_keep, b_gate, b_up))):
        loads += [
            pltpu.make_async_copy(keep.at[1, 0:2], kept.at[j], in_s.at[j, 0]),
            pltpu.make_async_copy(gate.at[1, 1], came.at[j, 0], in_s.at[j, 1]),
            pltpu.make_async_copy(up.at[1], came.at[j, 1], in_s.at[j, 2]),
        ]
    loads.append(pltpu.make_async_copy(parts.at[r], mine, m_s))
    for load in loads:
        load.start()
    greet(
        line_partners(r, n, w, 4)
        + [
            (n >= 1, nar_device(r, n, w, -1)),
            (n >= 2, nar_device(r, n, w, -2)),
            (n <= 2, nar_device(r, n, w, 1)),
            (n <= 1, nar_device(r, n, w, 2)),
        ]
        + square_partners(r, n, w)
    )
    scatter = Scatter(
        mine, parts.at[1 - r], (from_pt, from_up, from_dn), (s0, s1, s2, s3, s4, s5), me, 4
    )
    hops = [
        push(kept.at[0], ra_out, n_s.at[0], n_g.at[0], over_y(r, n, w)),
        push(kept.at[1], rb_out, n_s.at[1], n_g.at[1], over_x(r, n, w)),
        push(oa_in, roa_out, n_s.at[2], n_g.at[2], over_x(r, n, w)),
        push(ob_in, rob_out, n_s.at[3], n_g.at[3], over_y(r, n, w)),
    ]

    def copy(row, slot, by):
        return pltpu.make_async_remote_copy(
            send.at[row, slot], recv.at[row, slot], s_s.at[row, slot], s_g.at[row, slot],
            device_id=nar_device(r, n, w, by), device_id_type=MESH,
        )

    for i in range(4):
        scatter.pair(scatter.order(i)).start()
    for load in loads:
        load.wait()
    for j in range(2):
        for which in range(2):
            def join(rows):
                total = kept[j, which, rows, :].astype(f32) + came[j, which, rows, :].astype(f32)
                kept[j, which, rows, :] = total.astype(bf16)

            each_rows(128, 16, join)
        hops[j].start()
    hops[2].start()
    hops[3].start()
    scatter.advance((0, 1, 2, 3), ())

    def attention(i, carry):
        row, block = i // 4, i % 4
        first_query = 1024 + block * QUERIES
        here = pl.ds(pl.multiple_of(block * QUERIES, QUERIES), QUERIES)

        @pl.when(block == 0)
        def _():
            dkv[row] = jnp.zeros((1536, 128), f32)

        query = stack_low(q[row, here, :].astype(f32)).astype(bf16)
        grads = stack_high(grad[row, here, :].astype(f32))
        inner = jnp.sum(grads * stack_high(att[row, here, :].astype(f32)), axis=1, keepdims=True)
        grads = grads.astype(bf16)
        logsum = jnp.concatenate([lse[row, block]] * (KEYS // 128), axis=1)
        starts = tabs[row, here, 256:384]

        def key_tile(step, dq):
            tile = block // 2 + step
            rows = pl.ds(pl.multiple_of(tile * KEYS, KEYS), KEYS)
            pair = kv[row, rows, :]
            ok = allowed_tile(starts, tile, first_query)
            scores = contract_last(query, pair) * 0.125
            prob = jnp.where(ok, jnp.exp(scores - logsum), 0.0)
            grad_prob = contract_last(grads, pair)
            grad_scores = (prob * (grad_prob - inner)).astype(bf16)
            dkv[row, rows, :] += contract_first(grad_scores, query) * 0.125 + contract_first(
                prob.astype(bf16), grads
            )
            return dq + jnp.dot(grad_scores, pair, preferred_element_type=f32)

        dq = lax.fori_loop(0, 5, key_tile, jnp.zeros((4 * QUERIES, 128), f32), unroll=True)
        flat = unstack(dq, True) * 0.125
        cosine, sine = tabs[row, here, 0:128], -tabs[row, here, 128:256]
        there = pl.ds(pl.multiple_of(i * QUERIES, QUERIES), QUERIES)
        both[there, 0:128] = turn(flat[:, 0:128], cosine, sine).astype(bf16)
        both[there, 128:256] = turn(flat[:, 128:256], cosine, sine).astype(bf16)

        @pl.when(block == 3)
        def _():
            for slot, by in ((1, -1), (0, -2)):
                @pl.when(n >= -by)
                def _():
                    send[row, slot] = dkv[row, slot * 512 : slot * 512 + 512, :].astype(bf16)
                    copy(row, slot, by).start()

        @pl.when(i == 3)
        def _():
            scatter.advance((), (0,))

        return carry

    lax.fori_loop(0, 8, attention, 0)
    scatter.advance((), (1,))

    spread = Spread((o0, o1, o2, o3), (give_s, give_g, keep_s), (r, n, w))

    def moved_q(half):
        def place(target):
            return target.at[:, pl.ds(pl.multiple_of(r * 256, 256), 256)]

        return wide_q.at[half], 0, place, half == 0

    def moved_kv(half):
        def place(target):
            return target.at[:, pl.ds(pl.multiple_of(512 + r * 128, 128), 128)]

        return wide_kv.at[half], 1, place, half == 0

    def weight(half, columns, wide):
        d_first = (jnp.where(half == 0, 1 - r, r)) * 1024

        def tile(i, carry):
            d_cols = pl.ds(pl.multiple_of(d_first + i * 256, 256), 256)
            wide[half, i] = contract_first(x[:, d_cols], both[:, columns]).astype(bf16)
            return carry

        lax.fori_loop(0, 4, tile, 0)

    for half in range(2):
        weight(half, slice(0, 256), wide_q)
        spread.start(*moved_q(half))
    lane = lax.broadcasted_iota(jnp.int32, (128, 128), 1)
    for row in range(2):
        for slot, by in ((1, -1), (0, -2)):
            @pl.when(n <= 3 + by)
            def _():
                copy(row, slot, by).wait_recv()

        def tile(i, carry):
            rows = pl.ds(pl.multiple_of(i * 128, 128), 128)
            total = dkv[row, pl.ds(pl.multiple_of(1024 + i * 128, 128), 128), :]
            zero = jnp.zeros_like(total)
            total = total + jnp.where(n <= 2, recv[row, 1, rows, :].astype(f32), zero)
            total = total + jnp.where(n <= 1, recv[row, 0, rows, :].astype(f32), zero)
            turned = turn(total, tabs[row, rows, 0:128], -tabs[row, rows, 128:256])
            both[pl.ds(pl.multiple_of(row * 512 + i * 128, 128), 128), 256:384] = jnp.where(
                lane < 64, turned, total
            ).astype(bf16)
            return carry

        lax.fori_loop(0, 4, tile, 0)
    for half in range(2):
        weight(half, slice(256, 384), wide_kv)
        spread.start(*moved_kv(half))
    scatter.advance((), (2,))
    gain_out[...] = jnp.zeros_like(gain_out)

    def model_tile(dt, carry):
        nn, half = dt // 2, dt % 2
        columns = pl.ds(pl.multiple_of(dt * 256, 256), 256)
        inner = pl.ds(pl.multiple_of(half * 256, 256), 256)
        right = p1[nn, inner, 0:384]
        for row in range(2):
            for block in range(2):
                first = row * 512 + block * 256
                part = contract_last(both[first : first + 256, :], right)
                terms = part * x[first : first + 256, columns].astype(f32)
                gain_out[:, columns] += jnp.sum(terms.reshape(32, 8, 256), axis=0)
                part_out[row, 2 * block, :, columns] = part[0:128].astype(bf16)
                part_out[row, 2 * block + 1, :, columns] = part[128:256].astype(bf16)
        return carry

    lax.fori_loop(0, 8, model_tile, 0)
    gain_out[...] = gain_out[...] / gain[...]
    scatter.advance((), (3,))
    scatter.total(acc)

    def last(rows):
        hid_out[rows, :] = (acc[rows, :] + mid[rows, :]).astype(bf16)

    each_rows(128, 16, last)
    scatter.sent()
    for row in range(2):
        for slot, by in ((1, -1), (0, -2)):
            @pl.when(n >= -by)
            def _():
                copy(row, slot, by).wait_send()

    for half in range(2):
        spread.wait(*moved_q(half))
        spread.wait(*moved_kv(half))
    for hop in hops:
        hop.wait()


def unproject(*args):
    return comm_call(
        unproject_kernel, "unproject", 6,
        (
            jax.ShapeDtypeStruct((2, 4, 128, 2048), bf16),
            jax.ShapeDtypeStruct((8, 2048), f32),
        )
        + spread_shapes(128, 768)
        + (jax.ShapeDtypeStruct((128, 2048), bf16),)
        + (jax.ShapeDtypeStruct((2, 128, 2048), bf16),) * 2
        + (jax.ShapeDtypeStruct((2, 128, 512), bf16),) * 2,
        [vmem()] * 9 + [hbm(), vmem()] + [hbm()] * 8,
        [vmem(), vmem()] + [hbm()] * 4 + [vmem()] + [hbm()] * 4,
        [
            pltpu.VMEM((2, 2, 512, 128), bf16),
            pltpu.VMEM((2, 2, 512, 128), bf16),
            pltpu.VMEM((1024, 384), bf16),
            pltpu.VMEM((2, 4, 256, 256), bf16),
            pltpu.VMEM((2, 4, 256, 128), bf16),
            pltpu.SemaphoreType.DMA((2, 2)),
            pltpu.SemaphoreType.DMA((2, 2)),
        ]
        + spread_sems(2)
        + [pltpu.VMEM((4, 128, 2048), bf16)]
        + scatter_bufs(128, 2048) + scatter_sems()
        + [
            pltpu.VMEM((2, 2, 128, 2048), bf16),
            pltpu.VMEM((2, 2, 128, 2048), bf16),
            pltpu.VMEM((128, 2048), f32),
            pltpu.SemaphoreType.DMA((2, 3)),
            pltpu.SemaphoreType.DMA((4,)),
            pltpu.SemaphoreType.DMA((4,)),
            pltpu.SemaphoreType.DMA(()),
            pltpu.VMEM((2, 1536, 128), f32),
        ],
        args, flops=10**10, sent=10**7,
    )


def leave_kernel(
    parts, hidden, gain, gmid, gains, qa_send, qa_keep, qb_send, qb_keep, oa_keep, ob_keep, oa_in, ob_in,
    grad_out, ga_out, query_out, key_out, value_out, output_out,
    mine, from_pt, from_up, from_dn, s0, s1, s2, s3, s4, s5,
    acc, over_wid, summed, over_rest, w_s, w_g, t_s, t_g,
    first_q, next_q, then_q, next_o, then_o, kv, n_s, n_g, k0, k1, k2, k3, m_s,
):
    me = spot()
    r, n, w = me
    own_parts = pltpu.make_async_copy(parts.at[r], mine, m_s)
    own_parts.start()
    partners = [(w != j, (r, n, jnp.int32(j))) for j in range(4)]
    partners += [
        ((r != a) | (n != b), (jnp.int32(a), jnp.int32(b), w)) for a in range(2) for b in range(4)
    ]
    greet(partners)
    kv_gather = Gather(kv, (k0, k1, k2, k3), me, 4, pair=False)
    x_side, y_side = over_x(r, n, w), over_y(r, n, w)
    q_hops = [
        push(qa_send, first_q.at[0], n_s.at[0], n_g.at[0], x_side),
        push(qb_send, first_q.at[1], n_s.at[1], n_g.at[1], y_side),
    ]
    q_later = [
        push(next_q.at[0], then_q.at[0], n_s.at[2], n_g.at[2], y_side),
        push(next_q.at[1], then_q.at[1], n_s.at[3], n_g.at[3], x_side),
    ]
    o_hops = [
        push(next_o.at[0], then_o.at[0], n_s.at[4], n_g.at[4], y_side),
        push(next_o.at[1], then_o.at[1], n_s.at[5], n_g.at[5], x_side),
    ]
    for hop in q_hops:
        hop.start()
    scatter = Scatter(
        mine, parts.at[1 - r], (from_pt, from_up, from_dn), (s0, s1, s2, s3, s4, s5), me, 4
    )
    for i in range(4):
        scatter.pair(scatter.order(i)).start()

    def wid_copy(j, slot):
        return pltpu.make_async_remote_copy(
            gains, over_wid.at[slot], w_s.at[j], w_g.at[slot],
            device_id=(r, n, jnp.int32(j)), device_id_type=MESH,
        )

    def rest_copy(a, b, slot):
        return pltpu.make_async_remote_copy(
            summed, over_rest.at[slot], t_s.at[a * 4 + b], t_g.at[slot],
            device_id=(jnp.int32(a), jnp.int32(b), w), device_id_type=MESH,
        )

    for j in range(4):
        @pl.when(w != j)
        def _():
            wid_copy(j, w).start()

    own_parts.wait()
    scatter.advance((0, 1, 2), ())
    for j, (keep, came) in enumerate(((oa_keep, oa_in), (ob_keep, ob_in))):
        next_o[j] = (keep[1].astype(f32) + came[1].astype(f32)).astype(bf16)
        o_hops[j].start()
    summed[...] = gains[...]
    for j in range(4):
        @pl.when(w != j)
        def _():
            wid_copy(j, j).wait_recv()
            summed[...] += over_wid[j]

    for a in range(2):
        for b in range(4):
            @pl.when((r != a) | (n != b))
            def _():
                rest_copy(a, b, r * 4 + n).start()

    for j, keep in enumerate((qa_keep, qb_keep)):
        q_hops[j].wait_recv()
        next_q[j] = (keep[1].astype(f32) + first_q[j, 1].astype(f32)).astype(bf16)
        q_later[j].start()
    scatter.advance((), (0,))
    for j, keep in enumerate((qa_keep, qb_keep)):
        q_later[j].wait_recv()
        total = keep[0].astype(f32) + first_q[j, 0].astype(f32) + then_q[j].astype(f32)
        query_out[j * 128 : j * 128 + 128, :] = total[:, 0:512]
        kv[0, w, j * 128 : j * 128 + 128, :] = total[:, 512:768].astype(bf16)
    kv_gather.own()
    scatter.advance((3,), (1, 2))
    kv_gather.advance((), (1,))
    scatter.advance((), (3,))
    kv_gather.advance((), (2,))
    for j, (keep, came) in enumerate(((oa_keep, oa_in), (ob_keep, ob_in))):
        o_hops[j].wait_recv()
        output_out[j * 128 : j * 128 + 128, :] = (
            keep[0].astype(f32) + came[0].astype(f32) + then_o[j].astype(f32)
        )
    mine_block = r * 4 + n
    ga_out[0:1] = summed[pl.ds(mine_block, 1), :]
    ga_out[1:2] = summed[pl.ds(mine_block + 8, 1), :]
    for a in range(2):
        for b in range(4):
            @pl.when((r != a) | (n != b))
            def _():
                slot = a * 4 + b
                rest_copy(a, b, slot).wait_recv()
                ga_out[0:1] += over_rest[slot, pl.ds(mine_block, 1), :]
                ga_out[1:2] += over_rest[slot, pl.ds(mine_block + 8, 1), :]

    scatter.total(acc)

    def last(rows):
        grad = norm_back(hidden[rows, :].astype(f32), gain[...], acc[rows, :])
        grad_out[rows, :] = (grad + gmid[rows, :]).astype(bf16)

    each_rows(hidden.shape[0], 16, last)
    kv_gather.advance((1, 2, 3), (3,))
    lane = lax.broadcasted_iota(jnp.int32, (256, 128), 1)
    for j in range(4):
        even, odd = kv[0, j, :, 0:128].astype(f32), kv[0, j, :, 128:256].astype(f32)
        here = slice(j * 128, j * 128 + 128)
        key_out[:, here] = jnp.where(lane < 64, even, pltpu.roll(odd, 64, 1))
        value_out[:, here] = jnp.where(lane < 64, pltpu.roll(even, 64, 1), odd)
    scatter.sent()
    kv_gather.sent()
    for hop in q_hops + q_later + o_hops:
        hop.wait_send()
    for j in range(4):
        @pl.when(w != j)
        def _():
            wid_copy(j, w).wait_send()

    for a in range(2):
        for b in range(4):
            @pl.when((r != a) | (n != b))
            def _():
                rest_copy(a, b, r * 4 + n).wait_send()


def leave(*args):
    shard, width = 128, 2048
    grad = jax.ShapeDtypeStruct((256, 512), f32)
    return comm_call(
        leave_kernel, "leave", 7,
        (jax.ShapeDtypeStruct((shard, width), bf16), jax.ShapeDtypeStruct((8, 256), f32))
        + (grad,) * 4,
        [hbm()] + [vmem()] * 12, [vmem()] * 6,
        [pltpu.VMEM((4, shard, width), bf16)]
        + scatter_bufs(shard, width) + scatter_sems()
        + [
            pltpu.VMEM((shard, width), f32),
            pltpu.VMEM((4, 16, 256), f32),
            pltpu.VMEM((16, 256), f32),
            pltpu.VMEM((8, 16, 256), f32),
            pltpu.SemaphoreType.DMA((4,)),
            pltpu.SemaphoreType.DMA((4,)),
            pltpu.SemaphoreType.DMA((8,)),
            pltpu.SemaphoreType.DMA((8,)),
            pltpu.VMEM((2, 2, 128, 768), bf16),
            pltpu.VMEM((2, 128, 768), bf16),
            pltpu.VMEM((2, 128, 768), bf16),
            pltpu.VMEM((2, 128, 512), bf16),
            pltpu.VMEM((2, 128, 512), bf16),
            pltpu.VMEM((1, 4, 256, 256), bf16),
            pltpu.SemaphoreType.DMA((6,)),
            pltpu.SemaphoreType.DMA((6,)),
        ]
        + gather_sems()
        + [pltpu.SemaphoreType.DMA(())],
        args, flops=10**10, sent=10**8,
    )


def local_fast(
    hidden_in, doc_lengths, w_query, w_key, w_value, w_output, w_gate, w_up, w_down,
    gain_attn, gain_ffn, grad_out,
):
    r, n, w = spot()
    hidden, grad_top = hidden_in[0], grad_out[0]
    gain_a, gain_f = gain_attn[None], gain_ffn[None]
    def half(weight, axis):
        size = weight.shape[axis] // 2
        return lax.dynamic_slice_in_dim(weight, r * size, size, axis)

    head = (w * 2 + r) * HD
    kv_pack = jnp.concatenate(
        [lax.dynamic_slice_in_dim(w_key, head, HD, 1), lax.dynamic_slice_in_dim(w_value, head, HD, 1)],
        axis=1,
    )
    out_half = half(w_output, 0)
    p1_shard = jnp.concatenate(
        [half(w_query, 1), kv_pack, jnp.concatenate([out_half[:, :256], out_half[:, 256:]], axis=0)],
        axis=1,
    )
    down_half = half(w_down, 0)
    p2_shard = jnp.stack(
        [
            half(w_gate, 1),
            half(w_up, 1),
            jnp.concatenate([down_half[:512], down_half[512:]], axis=1),
        ]
    )
    p1 = lax.all_gather(p1_shard, "nar", axis=0)
    p2 = lax.all_gather(p2_shard, "nar", axis=0)

    token_ids = n * 512 + jnp.arange(512, dtype=jnp.int32)
    doc_start, places = doc_layout(doc_lengths[0], token_ids)
    angles = places.astype(f32)[:, None] * inverse_freq()[None, :]
    cosine, sine = jnp.cos(angles), jnp.sin(angles)
    start_here = (doc_start - (n - 2) * 512).astype(f32)
    tab = jnp.concatenate(
        [cosine] * 4 + [-sine, sine] * 2 + [jnp.broadcast_to(start_here[:, None], (512, 128))],
        axis=1,
    )

    rows, tabs = enter(hidden, gain_a, tab)
    rows3, rows2 = rows.reshape(2, 512, 2048), rows.reshape(1024, 2048)
    q, kv, tops = project(rows3, p1, tabs, grad_top)
    kv_flat = kv.reshape(2, 1536, 128)
    att, lse = attend(q, kv_flat, tabs)
    mid, ffn_rows = middle_stage(att, p1, hidden, gain_f)
    parts, total, gain_f_part, a_send, a_keep, b_send, b_keep, ra_dg, rb_dg = ffn_stage(
        ffn_rows.reshape(1024, 2048), tops, grad_top, p2, gain_f
    )
    gmid, datt, oa_send, oa_keep, ob_send, ob_keep, ra_u, rb_u, la_d, lb_d = branch_stage(
        total, mid, grad_top, gain_f, p1, att.reshape(1024, 256),
        a_send, b_send, a_keep, b_keep, ra_dg, rb_dg,
    )
    (
        dparts, gain_a_part, qa_send, qa_keep, qb_send, qb_keep,
        hidden_out, ra_last, rb_last, oa_came, ob_came,
    ) = unproject(
        q, kv_flat, att, datt, lse, rows2, p1, tabs, gain_a, parts, mid,
        a_keep, b_keep, ra_dg, rb_dg, ra_u, rb_u, oa_send, ob_send,
    )
    gains = jnp.concatenate(
        [gain_f_part.sum(axis=0).reshape(8, 256), gain_a_part.sum(axis=0).reshape(8, 256)], axis=0
    )
    grad_in, gain_sums, grad_query, grad_key, grad_value, output_sum = leave(
        dparts, hidden, gain_a, gmid, gains,
        qa_send, qa_keep, qb_send, qb_keep, oa_keep, ob_keep, oa_came, ob_came,
    )

    def joined(which):
        def half_rows(keep, came, last):
            return keep[0, which].astype(f32) + came.astype(f32) + last.astype(f32)

        a_came, b_came, a_last, b_last = (
            (ra_dg[1, 0], rb_dg[1, 0], ra_last[0], rb_last[0]),
            (ra_u[0], rb_u[0], ra_last[1], rb_last[1]),
            (ra_dg[0, 0], rb_dg[0, 0], la_d, lb_d),
        )[which]
        return jnp.concatenate(
            [half_rows(a_keep, a_came, a_last), half_rows(b_keep, b_came, b_last)], axis=0
        )

    return (
        hidden_out[None],
        grad_in[None],
        grad_query,
        grad_key,
        grad_value,
        output_sum.T,
        joined(0),
        joined(1),
        joined(2).T,
        gain_sums[1],
        gain_sums[0],
    )


def solution(mesh):
    in_specs = (
        P("row", ("nar", "wid"), None),
        P("row", None),
        P("nar", "wid"),
        P("nar", None),
        P("nar", None),
        P("wid", "nar"),
        P("nar", "wid"),
        P("nar", "wid"),
        P("wid", "nar"),
        P(),
        P(),
        P("row", ("nar", "wid"), None),
    )
    out_specs = (
        P("row", ("nar", "wid"), None),
        P("row", ("nar", "wid"), None),
        P(("row", "nar"), "wid"),
        P(("row", "nar"), None),
        P(("row", "nar"), None),
        P("wid", ("row", "nar")),
        P(("row", "nar"), "wid"),
        P(("row", "nar"), "wid"),
        P("wid", ("row", "nar")),
        P(("row", "nar")),
        P(("row", "nar")),
    )
    sizes = dict(mesh.shape)
    fits = sizes == {"row": 2, "nar": 4, "wid": 4}

    def body(*args):
        small = args[0].shape == (1, 128, 2048)
        return (local_fast if fits and small else local)(*args)

    return jax.shard_map(body, mesh=mesh, in_specs=in_specs, out_specs=out_specs, check_vma=False)
```

```python
import math

import jax
import jax.numpy as jnp
from jax import lax
from jax.experimental import pallas as pl
from jax.experimental.pallas import tpu as pltpu
from jax.sharding import PartitionSpec as P

H = 32
KV = 8
HD = 64


norm_eps = 1e-05
masked_score = -1e30


def inverse_freq():
    listed = []
    for pair_index in range(HD // 2):
        base_freq = 500000.0 ** (-2.0 * pair_index / HD)
        wavelength = 2.0 * math.pi / base_freq
        smoothing = (8192.0 / wavelength - 1.0) / 3.0
        blended = (1.0 - smoothing) * base_freq / 32.0 + smoothing * base_freq
        if wavelength < 2048.0:
            listed.append(base_freq)
        elif wavelength > 8192.0:
            listed.append(base_freq / 32.0)
        else:
            listed.append(blended)
    return jnp.asarray(listed, dtype=jnp.float32)


def rotate(values, cosine_table, sine_table):
    half_dim = HD // 2
    first_half = values[..., :half_dim]
    second_half = values[..., half_dim:]
    return jnp.concatenate(
        [
            first_half * cosine_table - second_half * sine_table,
            second_half * cosine_table + first_half * sine_table,
        ],
        axis=-1,
    )


def rotate_back(grads_in, cosine_table, sine_table):
    half_dim = HD // 2
    first_half = grads_in[..., :half_dim]
    second_half = grads_in[..., half_dim:]
    return jnp.concatenate(
        [
            first_half * cosine_table + second_half * sine_table,
            second_half * cosine_table - first_half * sine_table,
        ],
        axis=-1,
    )


def doc_layout(lengths_row, token_ids):
    ends_at = jnp.cumsum(lengths_row, dtype=jnp.int32)
    starts_at = ends_at - lengths_row
    inside = (token_ids[:, None] >= starts_at[None, :]) & (token_ids[:, None] < ends_at[None, :])
    doc_start = jnp.sum(jnp.where(inside, starts_at[None, :], 0), axis=1, dtype=jnp.int32)
    return (doc_start, token_ids - doc_start)


def norm_forward(values, gain_vector):
    root_inv = lax.rsqrt(jnp.mean(values * values, axis=-1, keepdims=True) + norm_eps)
    return (root_inv, (values * root_inv * gain_vector).astype(jnp.bfloat16))


def norm_backward(values, root_inv, gain_vector, grad_normed):
    weighted = grad_normed * gain_vector
    inner_sum = jnp.mean(weighted * values, axis=-1, keepdims=True)
    grad_values = root_inv * weighted - values * (root_inv * root_inv * root_inv) * inner_sum
    gain_term = jnp.sum(grad_normed * values * root_inv, axis=0)
    return (grad_values, gain_term)


def contract_last(left_side, right_side):
    return lax.dot_general(
        left_side, right_side, (((1,), (1,)), ((), ())), preferred_element_type=jnp.float32
    )


def contract_first(left_side, right_side):
    return lax.dot_general(
        left_side, right_side, (((0,), (0,)), ((), ())), preferred_element_type=jnp.float32
    )


def local(
    hidden_in,
    doc_lengths,
    w_query,
    w_key,
    w_value,
    w_output,
    w_gate,
    w_up,
    w_down,
    gain_attn,
    gain_ffn,
    grad_out,
):
    wid_count = lax.axis_size("wid")
    nar_count = lax.axis_size("nar")
    wid_index = lax.axis_index("wid")
    nar_index = lax.axis_index("nar")
    local_tokens = hidden_in.shape[1]
    block_tokens = local_tokens * wid_count
    seq_length = block_tokens * nar_count
    query_heads = w_query.shape[1] // HD
    group_size = H // KV
    kv_local = max(query_heads // group_size, 1)
    heads_per_kv = query_heads // kv_local
    kv_first = wid_index * query_heads // group_size
    query_block = min(512, block_tokens)
    block_count = block_tokens // query_block
    item_count = block_count * query_heads
    attn_scale = HD ** (-0.5)
    query_full, key_full, value_full, output_full, gate_full, up_full, down_full = (
        lax.all_gather(w_query, "nar", axis=0, tiled=True),
        lax.all_gather(w_key, "nar", axis=0, tiled=True),
        lax.all_gather(w_value, "nar", axis=0, tiled=True),
        lax.all_gather(w_output, "nar", axis=1, tiled=True),
        lax.all_gather(w_gate, "nar", axis=0, tiled=True),
        lax.all_gather(w_up, "nar", axis=0, tiled=True),
        lax.all_gather(w_down, "nar", axis=1, tiled=True),
    )
    key_local = lax.dynamic_slice_in_dim(key_full, kv_first * HD, kv_local * HD, 1)
    value_local = lax.dynamic_slice_in_dim(value_full, kv_first * HD, kv_local * HD, 1)
    token_ids = nar_index * block_tokens + jnp.arange(block_tokens, dtype=jnp.int32)
    doc_start, places = doc_layout(doc_lengths[0], token_ids)
    angles = places.astype(jnp.float32)[:, None] * inverse_freq()[None, :]
    cosine_table = jnp.cos(angles)[:, None, :]
    sine_table = jnp.sin(angles)[:, None, :]
    key_ids = jnp.arange(seq_length, dtype=jnp.int32)
    residual = hidden_in[0].astype(jnp.float32)
    root_attn, normed_attn = norm_forward(residual, gain_attn)
    normed_rows = lax.all_gather(normed_attn, "wid", axis=0, tiled=True)
    query_pre = jnp.dot(normed_rows, query_full, preferred_element_type=jnp.float32)
    key_pre = jnp.dot(normed_rows, key_local, preferred_element_type=jnp.float32)
    value_rows = jnp.dot(normed_rows, value_local, preferred_element_type=jnp.float32).astype(
        jnp.bfloat16
    )
    query_rot = (
        rotate(query_pre.reshape(block_tokens, query_heads, HD), cosine_table, sine_table)
        .astype(jnp.bfloat16)
        .reshape(block_tokens, query_heads * HD)
    )
    key_rot = (
        rotate(key_pre.reshape(block_tokens, kv_local, HD), cosine_table, sine_table)
        .astype(jnp.bfloat16)
        .reshape(block_tokens, kv_local * HD)
    )
    key_seq, value_seq = (
        lax.all_gather(key_rot, "nar", axis=0, tiled=True),
        lax.all_gather(value_rows, "nar", axis=0, tiled=True),
    )

    def item_inputs(item_index):
        block_index = item_index // query_heads
        head_index = item_index % query_heads
        kv_index = head_index // heads_per_kv
        row_first = block_index * query_block
        query_part = lax.dynamic_slice(query_rot, (row_first, head_index * HD), (query_block, HD))
        key_head = lax.dynamic_slice_in_dim(key_seq, kv_index * HD, HD, 1)
        value_head = lax.dynamic_slice_in_dim(value_seq, kv_index * HD, HD, 1)
        query_ids = lax.dynamic_slice_in_dim(token_ids, row_first, query_block, 0)
        query_starts = lax.dynamic_slice_in_dim(doc_start, row_first, query_block, 0)
        allowed = (key_ids[None, :] <= query_ids[:, None]) & (
            key_ids[None, :] >= query_starts[:, None]
        )
        scores = contract_last(query_part, key_head) * attn_scale
        return (
            row_first,
            head_index,
            kv_index,
            query_part,
            key_head,
            value_head,
            jnp.where(allowed, scores, masked_score),
        )

    def attend(item_index):
        row_first, head_index, kv_index, query_part, key_head, value_head, scores = item_inputs(
            item_index
        )
        row_max = jnp.max(scores, axis=1, keepdims=True)
        exp_scores = jnp.exp(scores - row_max)
        row_total = jnp.sum(exp_scores, axis=1, keepdims=True)
        probability = (exp_scores / row_total).astype(jnp.bfloat16)
        attended = jnp.dot(probability, value_head, preferred_element_type=jnp.float32)
        return (attended, (row_max + jnp.log(row_total))[:, 0])

    attended_items, logsum_items = lax.map(attend, jnp.arange(item_count, dtype=jnp.int32))
    attended_rows = (
        attended_items.reshape(block_count, query_heads, query_block, HD)
        .transpose(0, 2, 1, 3)
        .reshape(block_tokens, query_heads * HD)
        .astype(jnp.bfloat16)
    )
    rows_here = attended_rows
    branch_attn = lax.psum_scatter(
        jnp.dot(rows_here, output_full, preferred_element_type=jnp.float32),
        "wid",
        scatter_dimension=0,
        tiled=True,
    )
    middle = residual + branch_attn
    root_ffn, normed_ffn = norm_forward(middle, gain_ffn)
    ffn_rows = lax.all_gather(normed_ffn, "wid", axis=0, tiled=True)
    gate_proj = jnp.dot(ffn_rows, gate_full, preferred_element_type=jnp.float32)
    up_proj = jnp.dot(ffn_rows, up_full, preferred_element_type=jnp.float32)
    gate_sigmoid = jax.nn.sigmoid(gate_proj)
    gate_silu = gate_proj * gate_sigmoid
    activated = (gate_silu * up_proj).astype(jnp.bfloat16)
    rows_here = activated
    branch_ffn = lax.psum_scatter(
        jnp.dot(rows_here, down_full, preferred_element_type=jnp.float32).astype(jnp.bfloat16),
        "wid",
        scatter_dimension=0,
        tiled=True,
    ).astype(jnp.float32)
    hidden_out = (middle + branch_ffn).astype(jnp.bfloat16)[None]
    grad_top = grad_out[0]
    grad_rows = lax.all_gather(grad_top, "wid", axis=0, tiled=True)
    grad_activated = contract_last(grad_rows, down_full)
    down_weight_grad = contract_first(activated, grad_rows)
    silu_slope = gate_sigmoid * (1.0 + gate_proj * (1.0 - gate_sigmoid))
    grad_gate_b = (grad_activated * up_proj * silu_slope).astype(jnp.bfloat16)
    grad_up_b = (grad_activated * gate_silu).astype(jnp.bfloat16)
    gate_weight_grad = contract_first(ffn_rows, grad_gate_b)
    up_weight_grad = contract_first(ffn_rows, grad_up_b)
    grad_normed_ffn = lax.psum_scatter(
        contract_last(grad_gate_b, gate_full) + contract_last(grad_up_b, up_full),
        "wid",
        scatter_dimension=0,
        tiled=True,
    )
    grad_middle, gain_ffn_term = norm_backward(middle, root_ffn, gain_ffn, grad_normed_ffn)
    grad_middle = grad_middle + grad_top.astype(jnp.float32)
    grad_branch = grad_middle.astype(jnp.bfloat16)
    branch_rows = lax.all_gather(grad_branch, "wid", axis=0, tiled=True)
    grad_attended = contract_last(branch_rows, output_full).astype(jnp.bfloat16)
    output_weight_grad = contract_first(attended_rows, branch_rows)

    def attend_back(carried, item_index):
        key_grad, value_grad = carried
        row_first, head_index, kv_index, query_part, key_head, value_head, scores = item_inputs(
            item_index
        )
        logsum = lax.dynamic_index_in_dim(logsum_items, item_index, 0, keepdims=False)
        probability = jnp.exp(scores - logsum[:, None])
        grad_part = lax.dynamic_slice(
            grad_attended, (row_first, head_index * HD), (query_block, HD)
        )
        grad_prob = contract_last(grad_part, value_head)
        inner_sum = jnp.sum(probability * grad_prob, axis=1, keepdims=True)
        grad_scores = (probability * (grad_prob - inner_sum)).astype(jnp.bfloat16)
        query_grad = jnp.dot(grad_scores, key_head, preferred_element_type=jnp.float32) * attn_scale
        key_part = contract_first(grad_scores, query_part) * attn_scale
        value_part = contract_first(probability.astype(jnp.bfloat16), grad_part)
        key_old = lax.dynamic_slice_in_dim(key_grad, kv_index * HD, HD, 1)
        key_grad = lax.dynamic_update_slice_in_dim(key_grad, key_old + key_part, kv_index * HD, 1)
        value_old = lax.dynamic_slice_in_dim(value_grad, kv_index * HD, HD, 1)
        value_grad = lax.dynamic_update_slice_in_dim(
            value_grad, value_old + value_part, kv_index * HD, 1
        )
        return ((key_grad, value_grad), query_grad)

    zero_grads = jnp.zeros((seq_length, kv_local * HD), jnp.float32)
    (key_grad_seq, value_grad_seq), query_grad_items = lax.scan(
        attend_back, (zero_grads, zero_grads), jnp.arange(item_count, dtype=jnp.int32)
    )
    key_grad_block, value_grad_block = (
        lax.psum_scatter(
            key_grad_seq.astype(jnp.bfloat16), "nar", scatter_dimension=0, tiled=True
        ).astype(jnp.float32),
        lax.psum_scatter(
            value_grad_seq.astype(jnp.bfloat16), "nar", scatter_dimension=0, tiled=True
        ).astype(jnp.float32),
    )
    query_grad_rows = (
        query_grad_items.reshape(block_count, query_heads, query_block, HD)
        .transpose(0, 2, 1, 3)
        .reshape(block_tokens, query_heads, HD)
    )
    query_grad_b = (
        rotate_back(query_grad_rows, cosine_table, sine_table)
        .astype(jnp.bfloat16)
        .reshape(block_tokens, query_heads * HD)
    )
    key_grad_b = (
        rotate_back(key_grad_block.reshape(block_tokens, kv_local, HD), cosine_table, sine_table)
        .astype(jnp.bfloat16)
        .reshape(block_tokens, kv_local * HD)
    )
    value_grad_b = value_grad_block.astype(jnp.bfloat16)
    query_weight_grad = contract_first(normed_rows, query_grad_b)
    key_weight_grad = contract_first(normed_rows, key_grad_b)
    value_weight_grad = contract_first(normed_rows, value_grad_b)
    grad_normed_attn = lax.psum_scatter(
        (
            contract_last(query_grad_b, query_full)
            + contract_last(key_grad_b, key_local)
            + contract_last(value_grad_b, value_local)
        ).astype(jnp.bfloat16),
        "wid",
        scatter_dimension=0,
        tiled=True,
    ).astype(jnp.float32)
    grad_residual, gain_attn_term = norm_backward(residual, root_attn, gain_attn, grad_normed_attn)
    grad_in = (grad_residual + grad_middle).astype(jnp.bfloat16)[None]
    summed = (
        lax.psum_scatter(
            query_weight_grad.astype(jnp.bfloat16), ("row", "nar"), scatter_dimension=0, tiled=True
        ).astype(jnp.float32),
        lax.psum_scatter(
            key_weight_grad.astype(jnp.bfloat16), ("row", "nar"), scatter_dimension=0, tiled=True
        ).astype(jnp.float32),
        lax.psum_scatter(
            value_weight_grad.astype(jnp.bfloat16), ("row", "nar"), scatter_dimension=0, tiled=True
        ).astype(jnp.float32),
        lax.psum_scatter(
            output_weight_grad.astype(jnp.bfloat16), ("row", "nar"), scatter_dimension=1, tiled=True
        ).astype(jnp.float32),
        lax.psum_scatter(
            gate_weight_grad.astype(jnp.bfloat16), ("row", "nar"), scatter_dimension=0, tiled=True
        ).astype(jnp.float32),
        lax.psum_scatter(
            up_weight_grad.astype(jnp.bfloat16), ("row", "nar"), scatter_dimension=0, tiled=True
        ).astype(jnp.float32),
        lax.psum_scatter(
            down_weight_grad.astype(jnp.bfloat16), ("row", "nar"), scatter_dimension=1, tiled=True
        ).astype(jnp.float32),
        lax.psum_scatter(
            gain_attn_term.astype(jnp.bfloat16), ("row", "nar"), scatter_dimension=0, tiled=True
        ).astype(jnp.float32),
        lax.psum_scatter(
            gain_ffn_term.astype(jnp.bfloat16), ("row", "nar"), scatter_dimension=0, tiled=True
        ).astype(jnp.float32),
    )
    (
        grad_query,
        key_sum,
        value_sum,
        grad_output,
        grad_gate,
        grad_up,
        grad_down,
        gain_attn_sum,
        gain_ffn_sum,
    ) = summed
    key_all, value_all, gain_attn_all, gain_ffn_all = (
        lax.all_gather(key_sum.astype(jnp.bfloat16), "wid", axis=1, tiled=True).astype(
            key_sum.dtype
        ),
        lax.all_gather(value_sum.astype(jnp.bfloat16), "wid", axis=1, tiled=True).astype(
            value_sum.dtype
        ),
        lax.all_gather(gain_attn_sum.astype(jnp.bfloat16), "wid", axis=0, tiled=True).astype(
            gain_attn_sum.dtype
        ),
        lax.all_gather(gain_ffn_sum.astype(jnp.bfloat16), "wid", axis=0, tiled=True).astype(
            gain_ffn_sum.dtype
        ),
    )
    shard_rows = key_sum.shape[0]
    repeats = wid_count * kv_local // KV
    grad_key = key_all.reshape(shard_rows, KV, repeats, HD).sum(axis=2).reshape(shard_rows, KV * HD)
    grad_value = (
        value_all.reshape(shard_rows, KV, repeats, HD).sum(axis=2).reshape(shard_rows, KV * HD)
    )
    grad_gain_attn = gain_attn_all.reshape(wid_count, shard_rows).sum(axis=0)
    grad_gain_ffn = gain_ffn_all.reshape(wid_count, shard_rows).sum(axis=0)
    return (
        hidden_out,
        grad_in,
        grad_query,
        grad_key,
        grad_value,
        grad_output,
        grad_gate,
        grad_up,
        grad_down,
        grad_gain_attn,
        grad_gain_ffn,
    )


MESH = pl.DeviceIdType.MESH
bf16 = jnp.bfloat16
f32 = jnp.float32
VMEM_LIMIT = 60 * 2**20


def spot():
    return lax.axis_index("row"), lax.axis_index("nar"), lax.axis_index("wid")


def greet(partners):
    barrier = pltpu.get_barrier_semaphore()
    total = 0
    for there, device in partners:
        @pl.when(there)
        def _():
            pl.semaphore_signal(barrier, inc=1, device_id=device, device_id_type=MESH)

        total = total + there.astype(jnp.int32)
    pl.semaphore_wait(barrier, total)


def line_partners(r, n, w, wid_count):
    return [
        (w < wid_count - 1, (r, n, jnp.minimum(w + 1, wid_count - 1))),
        (w > 0, (r, n, jnp.maximum(w - 1, 0))),
        (w >= 0, (1 - r, n, w)),
    ]


def each_rows(count, step, body):
    def run(i, carry):
        body(pl.ds(pl.multiple_of(i * step, step), step))
        return carry

    lax.fori_loop(0, count // step, run, 0)


def square_partners(r, n, w):
    return [(n >= 0, over_x(r, n, w)), (n >= 0, over_y(r, n, w))]


def over_x(r, n, w):
    return (r, n + 1 - 2 * (n % 2), w)


def over_y(r, n, w):
    return (r, (n + 2) % 4, w)


def push(source, target, s_s, s_g, device):
    return pltpu.make_async_remote_copy(
        source, target, s_s, s_g, device_id=device, device_id_type=MESH
    )


class Square:
    def __init__(self, shard, full, sems, me):
        self.shard, self.full = shard, full
        self.sent, self.got = sems
        r, n, w = me
        self.n, self.x, self.y = n, n + 1 - 2 * (n % 2), (n + 2) % 4
        self.by_x, self.by_y = over_x(*me), over_y(*me)
        size = shard.shape[0] // 2
        self.upper, self.lower = pl.ds(0, size), pl.ds(size, size)

    def first(self, k, place):
        return push(
            self.shard, self.full.at[place], self.sent.at[k], self.got.at[k],
            (self.by_x, self.by_y)[k],
        )

    def second(self, k, place):
        part = self.full.at[place, (self.upper, self.lower)[k]]
        return push(
            part, part, self.sent.at[2 + k], self.got.at[2 + k], (self.by_y, self.by_x)[k]
        )

    def start(self):
        self.first(0, self.n).start()
        self.first(1, self.n).start()

    def turn(self):
        self.first(0, self.x).wait_recv()
        self.second(0, self.x).start()
        self.first(1, self.y).wait_recv()
        self.second(1, self.y).start()

    def finish(self):
        for k in range(2):
            self.second(k, 3 - self.n).wait_recv()
            self.first(k, self.n).wait_send()
            self.second(k, (self.x, self.y)[k]).wait_send()


def square_sems():
    return [pltpu.SemaphoreType.DMA((4,))] * 2


def fetch(own, full, target, sems, n):
    copies = [pltpu.make_async_copy(own, target.at[n], sems.at[0])]
    for k, place in enumerate((n + 1 - 2 * (n % 2), (n + 2) % 4, 3 - n)):
        copies.append(pltpu.make_async_copy(full.at[place], target.at[place], sems.at[1 + k]))
    return copies


class Gather:
    def __init__(self, buf, sems, me, wid_count, rows=slice(None), pair=True):
        self.rows, self.both = rows, pair
        self.buf, (self.up_s, self.dn_s, self.pt_s, self.got) = buf, sems
        self.r, self.n, self.w = me
        self.last = wid_count - 1
        self.up = (self.r, self.n, jnp.minimum(self.w + 1, self.last))
        self.dn = (self.r, self.n, jnp.maximum(self.w - 1, 0))
        self.pt = (1 - self.r, self.n, self.w)

    def copy(self, j, sem, device, row=None):
        row = (self.r if self.both else 0) if row is None else row
        return pltpu.make_async_remote_copy(
            self.buf.at[row, j, self.rows],
            self.buf.at[row, j, self.rows],
            sem.at[j],
            self.got.at[row, j],
            device_id=device,
            device_id_type=MESH,
        )

    def pass_on(self, j, go_up, go_dn):
        if go_up:
            @pl.when(self.w < self.last)
            def _():
                self.copy(j, self.up_s, self.up).start()

        if go_dn:
            @pl.when(self.w > 0)
            def _():
                self.copy(j, self.dn_s, self.dn).start()

        if self.both:
            self.copy(j, self.pt_s, self.pt).start()

    def own(self):
        self.pass_on(self.w, True, True)

    def arrive(self, row, j):
        self.copy(j, self.pt_s, self.pt, row).wait_recv()

    def step(self, k):
        below, above = self.w - k, self.w + k

        @pl.when(below >= 0)
        def _():
            self.arrive(None, below)
            self.pass_on(below, True, False)

        @pl.when(above <= self.last)
        def _():
            self.arrive(None, above)
            self.pass_on(above, False, True)

    def advance(self, edge_steps, inner_steps):
        at_end = (self.w == 0) | (self.w == self.last)
        for ends, steps in ((True, edge_steps), (False, inner_steps)):
            if steps:
                @pl.when(at_end if ends else jnp.logical_not(at_end))
                def _():
                    for k in steps:
                        self.step(k)

    def rest(self):
        for j in range(self.last + 1):
            self.arrive(1 - self.r, j)

    def sent(self):
        for j in range(self.last + 1):
            @pl.when((j <= self.w) & (self.w < self.last))
            def _():
                self.copy(j, self.up_s, self.up).wait_send()

            @pl.when((j >= self.w) & (self.w > 0))
            def _():
                self.copy(j, self.dn_s, self.dn).wait_send()

            if self.both:
                self.copy(j, self.pt_s, self.pt).wait_send()


def gather_scratch(shard, width):
    return [pltpu.VMEM((2, 4, shard, width), bf16)] + gather_sems()


def gather_sems():
    return [pltpu.SemaphoreType.DMA((4,))] * 3 + [pltpu.SemaphoreType.DMA((2, 4))]


class Scatter:
    def __init__(self, mine, theirs, bufs, sems, me, wid_count, first=0, count=None):
        self.mine, self.theirs = mine, theirs
        self.from_pt, self.from_up, self.from_dn = bufs
        self.pt_s, self.pt_g, self.up_s, self.up_g, self.dn_s, self.dn_g = sems
        self.r, self.n, self.w = me
        self.first, self.count = first, mine.shape[1] if count is None else count
        self.rows = pl.ds(first, self.count)
        self.last = wid_count - 1
        self.up = (self.r, self.n, jnp.minimum(self.w + 1, self.last))
        self.dn = (self.r, self.n, jnp.maximum(self.w - 1, 0))
        self.pt = (1 - self.r, self.n, self.w)

    def order(self, i):
        low = jnp.where(i == 0, 3, jnp.where(i == 1, 0, jnp.where(i == 2, 2, 1)))
        return jnp.where(self.w < 2, low, 3 - low)

    def send(self, source, target, sent, got, s, device):
        return pltpu.make_async_remote_copy(
            source.at[s, self.rows], target.at[s, self.rows], sent.at[s], got.at[s],
            device_id=device, device_id_type=MESH,
        )

    def pair(self, s):
        return self.send(self.theirs, self.from_pt, self.pt_s, self.pt_g, s, self.pt)

    def climb(self, s):
        return self.send(self.mine, self.from_dn, self.up_s, self.up_g, s, self.up)

    def fall(self, s):
        return self.send(self.mine, self.from_up, self.dn_s, self.dn_g, s, self.dn)

    def each(self, body):
        def run(i, carry):
            body(pl.ds(pl.multiple_of(self.first + i * 16, 16), 16))
            return carry

        lax.fori_loop(0, self.count // 16, run, 0)

    def add(self, s, others):
        def body(rows):
            total = self.mine[s, rows, :].astype(f32)
            for other in others:
                total = total + other[s, rows, :].astype(f32)
            self.mine[s, rows, :] = total.astype(bf16)

        self.each(body)

    def step(self, s):
        self.pair(s).wait_recv()

        @pl.when((s > self.w) & (self.w > 0))
        def _():
            self.climb(s).wait_recv()
            self.add(s, (self.from_pt, self.from_dn))

        @pl.when((s < self.w) & (self.w < self.last))
        def _():
            self.fall(s).wait_recv()
            self.add(s, (self.from_pt, self.from_up))

        @pl.when(((s > self.w) & (self.w == 0)) | ((s < self.w) & (self.w == self.last)))
        def _():
            self.add(s, (self.from_pt,))

        @pl.when(s > self.w)
        def _():
            self.climb(s).start()

        @pl.when(s < self.w)
        def _():
            self.fall(s).start()

    def advance(self, edge_steps, inner_steps):
        for ends, steps in ((True, edge_steps), (False, inner_steps)):
            at_end = (self.w == 0) | (self.w == self.last)

            def body(i, carry):
                self.step(self.order(i))
                return carry

            if steps:
                @pl.when(at_end if ends else jnp.logical_not(at_end))
                def _():
                    lax.fori_loop(steps[0], steps[-1] + 1, body, 0)

    def total(self, out):
        w = self.w

        def first(rows):
            out[rows, :] = self.mine[w, rows, :].astype(f32) + self.from_pt[w, rows, :].astype(f32)

        self.each(first)

        @pl.when(w > 0)
        def _():
            self.climb(w).wait_recv()

            def more(rows):
                out[rows, :] += self.from_dn[w, rows, :].astype(f32)

            self.each(more)

        @pl.when(w < self.last)
        def _():
            self.fall(w).wait_recv()

            def more(rows):
                out[rows, :] += self.from_up[w, rows, :].astype(f32)

            self.each(more)

    def sent(self):
        for s in range(self.last + 1):
            self.pair(s).wait_send()

            @pl.when(s > self.w)
            def _():
                self.climb(s).wait_send()

            @pl.when(s < self.w)
            def _():
                self.fall(s).wait_send()


def scatter_bufs(shard, width):
    return [pltpu.VMEM((4, shard, width), bf16)] * 3


def scatter_sems():
    return [pltpu.SemaphoreType.DMA((4,))] * 6


def vmem():
    return pl.BlockSpec(memory_space=pltpu.VMEM)


def hbm():
    return pl.BlockSpec(memory_space=pl.ANY)


def comm_call(kernel, name, cid, out_shape, in_specs, out_specs, scratch, args, flops=0, sent=0):
    return pl.pallas_call(
        kernel,
        out_shape=out_shape,
        in_specs=in_specs,
        out_specs=out_specs,
        scratch_shapes=scratch,
        compiler_params=pltpu.CompilerParams(
            collective_id=cid, has_side_effects=True, vmem_limit_bytes=VMEM_LIMIT
        ),
        cost_estimate=pl.CostEstimate(flops=flops, bytes_accessed=sent, transcendentals=0),
        name=name,
    )(*args)


def norm_rows(x, gain):
    root = lax.rsqrt(jnp.mean(x * x, axis=-1, keepdims=True) + norm_eps)
    return x * root * gain


def turn(x, cosine, sine):
    lane = lax.broadcasted_iota(jnp.int32, x.shape, 1)
    swapped = jnp.where(lane % 64 < 32, pltpu.roll(x, 96, 1), pltpu.roll(x, 32, 1))
    return x * cosine + swapped * sine


def enter_kernel(
    hidden, gain, tab, p1_own, down_own, rows_out, tabs_out, p1_out, down_out,
    buf, up_s, dn_s, pt_s, got, tabs, tab_s, tab_g, out_s, p1_s, p1_g, down_s, down_g, p1_here, here_s,
):
    me = spot()
    r, n, w = me
    bring = pltpu.make_async_copy(p1_own, p1_here, here_s.at[0])
    bring.start()
    greet(line_partners(r, n, w, 4) + square_partners(r, n, w))
    p1 = Square(p1_own, p1_out, (p1_s, p1_g), me)
    down = Square(down_own.at[0:256], down_out, (down_s, down_g), me)
    p1.start()
    down.start()
    gather = Gather(buf, (up_s, dn_s, pt_s, got), me, 4)
    tab_copy = pltpu.make_async_remote_copy(
        tab, tabs.at[r], tab_s, tab_g, device_id=(1 - r, n, w), device_id_type=MESH
    )

    def body(rows):
        buf[r, w, rows, :] = norm_rows(hidden[rows, :].astype(f32), gain[...]).astype(bf16)

    each_rows(hidden.shape[0], 16, body)
    gather.own()
    tab_copy.start()

    def keep(rows):
        tabs[r, rows, :] = tab[rows, :]

    each_rows(tab.shape[0], 16, keep)
    bring.wait()
    settle = pltpu.make_async_copy(p1_here, p1_out.at[n], here_s.at[1])
    settle.start()
    gather.step(1)
    p1.turn()
    gather.step(2)
    down.turn()
    gather.step(3)
    gather.rest()
    out = pltpu.make_async_copy(buf, rows_out, out_s.at[0])
    out.start()
    tab_copy.wait_recv()
    out_tab = pltpu.make_async_copy(tabs, tabs_out, out_s.at[1])
    out_tab.start()
    gather.sent()
    p1.finish()
    down.finish()
    settle.wait()
    tab_copy.wait_send()
    out.wait()
    out_tab.wait()


def enter(hidden, gain, tab, p1_own, down_own):
    shard, width = hidden.shape
    return comm_call(
        enter_kernel, "enter", 1,
        (
            jax.ShapeDtypeStruct((2, 4, shard, width), bf16),
            jax.ShapeDtypeStruct((2,) + tab.shape, f32),
            jax.ShapeDtypeStruct((4,) + p1_own.shape, bf16),
            jax.ShapeDtypeStruct((4, 256, 1024), bf16),
        ),
        [vmem()] * 3 + [hbm()] * 2, [hbm()] * 4,
        gather_scratch(shard, width)
        + [
            pltpu.VMEM((2,) + tab.shape, f32),
            pltpu.SemaphoreType.DMA(()),
            pltpu.SemaphoreType.DMA(()),
            pltpu.SemaphoreType.DMA((2,)),
        ]
        + square_sems() * 2
        + [pltpu.VMEM(p1_own.shape, bf16), pltpu.SemaphoreType.DMA((2,))],
        (hidden, gain, tab, p1_own, down_own), flops=10**10, sent=10**8,
    )


def nar_device(r, n, w, by):
    return (r, jnp.clip(n + by, 0, 3), w)


def project_kernel(
    x, p1, tabs, grad_top, down_own, q_out, kv_out, tops_out, down_out,
    kv, s_s, s_g, out_s, buf, g0, g1, g2, g3, tops_s, down_s, down_g,
):
    r, n, w = spot()
    greet(
        line_partners(r, n, w, 4)
        + [
            (n >= 1, nar_device(r, n, w, -1)),
            (n >= 2, nar_device(r, n, w, -2)),
            (n <= 2, nar_device(r, n, w, 1)),
            (n <= 1, nar_device(r, n, w, 2)),
        ]
    )
    gather = Gather(buf, (g0, g1, g2, g3), (r, n, w), 4)

    def keep(rows):
        buf[r, w, rows, :] = grad_top[rows, :]

    each_rows(64, 16, keep)
    gather.own()

    def copy(row, slot, by):
        return pltpu.make_async_remote_copy(
            kv.at[row, 2], kv.at[row, slot], s_s.at[row, slot], s_g.at[row, slot],
            device_id=nar_device(r, n, w, by), device_id_type=MESH,
        )

    down = Square(down_own.at[256:512], down_out, (down_s, down_g), (r, n, w))
    lane = lax.broadcasted_iota(jnp.int32, (256, 128), 1)
    weight = p1[:, :, 0:384].reshape(2048, 384)
    for row in range(2):
        def tile(i, carry):
            rows = pl.ds(pl.multiple_of(i * 256, 256), 256)
            cosine, sine = tabs[row, rows, 0:128], tabs[row, rows, 128:256]
            pre = jnp.dot(x[row, rows, :], weight, preferred_element_type=f32)
            q_out[row, rows, 0:128] = turn(pre[:, 0:128], cosine, sine).astype(bf16)
            q_out[row, rows, 128:256] = turn(pre[:, 128:256], cosine, sine).astype(bf16)
            both = pre[:, 256:384]
            kv[row, 2, rows, :] = jnp.where(lane < 64, turn(both, cosine, sine), both).astype(bf16)
            return carry

        lax.fori_loop(0, 2, tile, 0)

        @pl.when(n <= 2)
        def _():
            copy(row, 1, 1).start()

        @pl.when(n <= 1)
        def _():
            copy(row, 0, 2).start()

        for slot, least in ((1, 1), (0, 2)):
            @pl.when(n < least)
            def _():
                kv[row, slot] = jnp.zeros((512, 128), bf16)

    down.start()
    gather.step(1)
    gather.step(2)
    down.turn()
    gather.step(3)
    gather.rest()
    tops_copy = pltpu.make_async_copy(buf, tops_out, tops_s)
    tops_copy.start()
    for row in range(2):
        for slot, least, by in ((1, 1, 1), (0, 2, 2)):
            @pl.when(n >= least)
            def _():
                copy(row, slot, by).wait_recv()

    out = pltpu.make_async_copy(kv, kv_out, out_s)
    out.start()
    for row in range(2):
        @pl.when(n <= 2)
        def _():
            copy(row, 1, 1).wait_send()

        @pl.when(n <= 1)
        def _():
            copy(row, 0, 2).wait_send()

    gather.sent()
    down.finish()
    out.wait()
    tops_copy.wait()


def project(*args):
    return comm_call(
        project_kernel, "project", 2,
        (
            jax.ShapeDtypeStruct((2, 512, 256), bf16),
            jax.ShapeDtypeStruct((2, 3, 512, 128), bf16),
            jax.ShapeDtypeStruct((2, 4, 64, 2048), bf16),
            jax.ShapeDtypeStruct((4, 256, 1024), bf16),
        ),
        [vmem()] * 4 + [hbm()], [vmem(), hbm(), hbm(), hbm()],
        [
            pltpu.VMEM((2, 3, 512, 128), bf16),
            pltpu.SemaphoreType.DMA((2, 3)),
            pltpu.SemaphoreType.DMA((2, 3)),
            pltpu.SemaphoreType.DMA(()),
        ]
        + gather_scratch(64, 2048)
        + [pltpu.SemaphoreType.DMA(())]
        + square_sems(),
        args, flops=10**10, sent=10**7,
    )


KEYS = 256
QUERIES = 128


def stack_low(x):
    lane = lax.broadcasted_iota(jnp.int32, (QUERIES, 128), 1)
    zero = jnp.zeros((QUERIES, 128), x.dtype)
    parts = []
    for pair in range(2):
        block = x[:, pair * 128 : pair * 128 + 128]
        parts.append(jnp.where(lane < 64, block, zero))
        parts.append(jnp.where(lane < 64, pltpu.roll(block, 64, 1), zero))
    return jnp.concatenate(parts, axis=0)


def stack_high(x):
    lane = lax.broadcasted_iota(jnp.int32, (QUERIES, 128), 1)
    zero = jnp.zeros((QUERIES, 128), x.dtype)
    parts = []
    for pair in range(2):
        block = x[:, pair * 128 : pair * 128 + 128]
        parts.append(jnp.where(lane >= 64, pltpu.roll(block, 64, 1), zero))
        parts.append(jnp.where(lane >= 64, block, zero))
    return jnp.concatenate(parts, axis=0)


def unstack(x, low):
    lane = lax.broadcasted_iota(jnp.int32, (QUERIES, 128), 1)
    out = []
    for pair in range(2):
        even = x[2 * pair * QUERIES : (2 * pair + 1) * QUERIES]
        odd = x[(2 * pair + 1) * QUERIES : (2 * pair + 2) * QUERIES]
        if low:
            out.append(jnp.where(lane < 64, even, pltpu.roll(odd, 64, 1)))
        else:
            out.append(jnp.where(lane < 64, pltpu.roll(even, 64, 1), odd))
    return jnp.concatenate(out, axis=1)


def allowed_tile(starts, tile, first_query):
    key = lax.broadcasted_iota(jnp.int32, (QUERIES, KEYS), 1) + tile * KEYS
    query = lax.broadcasted_iota(jnp.int32, (QUERIES, KEYS), 0) + first_query
    start = jnp.concatenate([starts] * (KEYS // 128), axis=1)
    ok = (key <= query) & (key.astype(f32) >= start)
    return jnp.concatenate([ok] * 4, axis=0)


def attend_kernel(q, kv, starts, out, lse):
    block = pl.program_id(1)
    first_query = 1024 + block * QUERIES
    query = stack_low(q[0].astype(f32)).astype(bf16)

    def body(step, carry):
        tile = block // 2 + step
        top, total, acc = carry
        both = kv[0, pl.ds(pl.multiple_of(tile * KEYS, KEYS), KEYS), :]
        scores = contract_last(query, both) * 0.125
        ok = allowed_tile(starts[0], tile, first_query)
        scores = jnp.where(ok, scores, masked_score)
        new_top = jnp.maximum(top, jnp.max(scores, axis=1, keepdims=True))
        shrink = jnp.exp(top - new_top)
        part = jnp.exp(scores - new_top)
        total = total * shrink + jnp.sum(part, axis=1, keepdims=True)
        acc = acc * shrink + jnp.dot(part.astype(bf16), both, preferred_element_type=f32)
        return new_top, total, acc

    top, total, acc = lax.fori_loop(
        0, 5, body,
        (
            jnp.full((4 * QUERIES, 1), masked_score, f32),
            jnp.zeros((4 * QUERIES, 1), f32),
            jnp.zeros((4 * QUERIES, 128), f32),
        ),
        unroll=True,
    )
    out[0] = unstack(acc / total, False).astype(bf16)
    lse[0, 0] = jnp.broadcast_to(top + jnp.log(total), (4 * QUERIES, 128))


def attend_specs():
    return [
        pl.BlockSpec((1, QUERIES, 256), lambda i, j: (i, j, 0)),
        pl.BlockSpec((1, 1536, 128), lambda i, j: (i, 0, 0)),
        pl.BlockSpec((1, QUERIES, 128), lambda i, j: (i, j, 2)),
    ]


def attend(q, kv, tabs):
    return pl.pallas_call(
        attend_kernel,
        out_shape=(
            jax.ShapeDtypeStruct((2, 512, 256), bf16),
            jax.ShapeDtypeStruct((2, 4, 4 * QUERIES, 128), f32),
        ),
        grid_spec=pl.GridSpec(
            grid=(2, 4),
            in_specs=attend_specs(),
            out_specs=[
                pl.BlockSpec((1, QUERIES, 256), lambda i, j: (i, j, 0)),
                pl.BlockSpec((1, 1, 4 * QUERIES, 128), lambda i, j: (i, j, 0, 0)),
            ],
        ),
        compiler_params=pltpu.CompilerParams(vmem_limit_bytes=VMEM_LIMIT),
        cost_estimate=pl.CostEstimate(flops=2 * 10**10, bytes_accessed=10**7, transcendentals=10**7),
        name="attend",
    )(q, kv, tabs)


def out_block(p1, nn, half):
    return p1[nn, half * 256 : half * 256 + 256, 384:640]


def middle_kernel(
    att, p1, hidden, gain, gate_own, up_own, mid_out, ffn_out, gate_out, up_out,
    theirs, mine, from_pt, from_up, from_dn, s0, s1, s2, s3, s4, s5, fbuf, h0, h1, h2, h3, out_s,
    gate_s, gate_g, up_s, up_g,
):
    me = spot()
    r, n, w = me
    greet(line_partners(r, n, w, 4) + square_partners(r, n, w))
    gate = Square(gate_own, gate_out, (gate_s, gate_g), me)
    up = Square(up_own, up_out, (up_s, up_g), me)
    gate.start()
    up.start()
    scatter = Scatter(
        mine, theirs, (from_pt, from_up, from_dn), (s0, s1, s2, s3, s4, s5), me, 4
    )
    ffn = Gather(fbuf, (h0, h1, h2, h3), me, 4)
    def shard(i, carry):
        s = scatter.order(i)
        rows = pl.ds(pl.multiple_of(s * 128, 128), 128)
        left = jnp.concatenate([att[1 - r, rows, :], att[r, rows, :]], axis=0)
        for nn in range(4):
            for half in range(2):
                part = jnp.dot(left, out_block(p1, nn, half), preferred_element_type=f32).astype(bf16)
                columns = slice(nn * 512 + half * 256, nn * 512 + half * 256 + 256)
                theirs[s, :, columns] = part[0:128]
                mine[s, :, columns] = part[128:256]
        scatter.pair(s).start()
        return carry

    lax.fori_loop(0, 4, shard, 0)
    scatter.advance((0, 1, 2, 3), (0, 1, 2, 3))
    scatter.total(mid_out)

    def body(rows):
        middle = mid_out[rows, :] + hidden[rows, :].astype(f32)
        mid_out[rows, :] = middle
        fbuf[r, w, rows, :] = norm_rows(middle, gain[...]).astype(bf16)

    each_rows(hidden.shape[0], 16, body)
    ffn.own()
    gate.turn()
    up.turn()
    for k in (1, 2, 3):
        ffn.step(k)
    ffn.rest()
    out_f = pltpu.make_async_copy(fbuf, ffn_out, out_s)
    out_f.start()
    scatter.sent()
    ffn.sent()
    gate.finish()
    up.finish()
    out_f.wait()


def middle_stage(att, p1, hidden, gain, gate_own, up_own):
    shard, width = hidden.shape
    rows = jax.ShapeDtypeStruct((2, 4, shard, width), bf16)
    return comm_call(
        middle_kernel, "middle", 3,
        (jax.ShapeDtypeStruct((shard, width), f32), rows)
        + (jax.ShapeDtypeStruct((4, 512, 1024), bf16),) * 2,
        [vmem()] * 4 + [hbm()] * 2, [vmem()] + [hbm()] * 3,
        [pltpu.VMEM((4, shard, width), bf16)] * 2
        + scatter_bufs(shard, width) + scatter_sems()
        + gather_scratch(shard, width)
        + [pltpu.SemaphoreType.DMA(())]
        + square_sems() * 2,
        (att, p1, hidden, gain, gate_own, up_own), flops=10**10, sent=2 * 10**8,
    )


class Spread:
    def __init__(self, outs, sems, me):
        self.a_send, self.a_keep, self.b_send, self.b_keep = outs
        self.r, self.n, self.w = me
        self.give_s, self.give_g, self.keep_s = sems

    def copies(self, wide, row, place, give):
        for k in range(4):
            block = wide.at[self.n ^ k]
            for part in range(2):
                source = block.at[pl.ds(part * 128, 128)]
                if part == 0:
                    target = (self.a_send if k & 1 else self.a_keep).at[k >> 1]
                else:
                    target = (self.b_send if k >= 2 else self.b_keep).at[k & 1]
                target = place(target)
                at = k * 2 + part
                if give:
                    yield pltpu.make_async_remote_copy(
                        source, target, self.give_s.at[row, at], self.give_g.at[row, at],
                        device_id=(1 - self.r, self.n, self.w), device_id_type=MESH,
                    )
                else:
                    yield pltpu.make_async_copy(source, target, self.keep_s.at[row, at])

    def start(self, *args):
        for copy in self.copies(*args):
            copy.start()

    def wait_send(self, *args):
        for copy in self.copies(*args):
            copy.wait_send()

    def wait_recv(self, *args):
        for copy in self.copies(*args):
            copy.wait_recv()

    def wait(self, *args):
        for copy in self.copies(*args):
            copy.wait()


def spread_sems(count):
    return [pltpu.SemaphoreType.DMA((count, 8))] * 3


def ffn_kernel(
    x, tops_in, grad_top, gate_own, gate_in, up_own, up_in, down_own, down_a, down_b, gain,
    part_out, sum_out, gain_out, o0, o1, o2, o3, ra_out, rb_out,
    theirs, mine, from_pt, from_up, from_dn, s0, s1, s2, s3, s4, s5,
    act, dgu, wide, out_s, give_s, give_g, keep_s, p2, in_s, n_s, n_g,
    tops4, h0, h1, h2, h3, tops_s,
):
    me = spot()
    r, n, w = me
    loads = [
        fetch(gate_own, gate_in, p2.at[0], in_s.at[0], n),
        fetch(up_own, up_in, p2.at[1], in_s.at[1], n),
        fetch(down_own.at[0:256], down_a, p2.at[2, :, 0:256], in_s.at[2], n)
        + fetch(down_own.at[256:512], down_b, p2.at[2, :, 256:512], in_s.at[3], n),
        [pltpu.make_async_copy(tops_in, tops4.at[:, :, 0:64], tops_s)],
    ]
    for group in loads:
        for load in group:
            load.start()

    def loaded(k):
        for load in loads[k]:
            load.wait()

    greet(line_partners(r, n, w, 4) + square_partners(r, n, w))
    scatter = Scatter(
        mine, theirs, (from_pt, from_up, from_dn), (s0, s1, s2, s3, s4, s5), me, 4
    )
    late = pl.ds(64, 64)
    gather = Gather(tops4, (h0, h1, h2, h3), me, 4, late)

    def keep(rows):
        tops4[r, w, pl.ds(64 + rows.start, 16), :] = grad_top[pl.ds(64 + rows.start, 16), :]

    each_rows(64, 16, keep)
    gather.own()
    gain_out[...] = jnp.zeros_like(gain_out)
    loaded(0)
    loaded(1)

    def hidden_tile(i, carry):
        ft, row = i // 2, i % 2
        rows = pl.ds(pl.multiple_of(row * 512, 512), 512)
        columns = pl.ds(pl.multiple_of(ft * 256, 256), 256)
        left = x[rows, :]
        gate = jnp.dot(left, p2[0, :, :, columns].reshape(2048, 256), preferred_element_type=f32)
        up = jnp.dot(left, p2[1, :, :, columns].reshape(2048, 256), preferred_element_type=f32)
        sig = 1.0 / (1.0 + jnp.exp(-gate))
        silu = gate * sig
        act[rows, columns] = (silu * up).astype(bf16)
        dgu[rows, columns] = (up * (sig * (1.0 + gate * (1.0 - sig)))).astype(bf16)
        later = pl.ds(pl.multiple_of(1024 + ft * 256, 256), 256)
        dgu[rows, later] = silu.astype(bf16)
        return carry

    lax.fori_loop(0, 4, hidden_tile, 0)
    gather.step(1)
    lax.fori_loop(4, 8, hidden_tile, 0)
    gather.step(2)
    loaded(2)

    def down_tile(dt, carry):
        nn, half = dt // 2, dt % 2
        columns = pl.ds(pl.multiple_of(dt * 256, 256), 256)
        inner = pl.ds(pl.multiple_of(half * 256, 256), 256)
        other = pl.ds(pl.multiple_of(512 + half * 256, 256), 256)
        right = jnp.concatenate([p2[2, nn, :, inner], p2[2, nn, :, other]], axis=0)
        for row, stage in ((0, theirs), (1, mine)):
            part = jnp.dot(act[row * 512 : row * 512 + 512, :], right, preferred_element_type=f32)
            stage[:, :, columns] = part.astype(bf16).reshape(4, 128, 256)
        return carry

    lax.fori_loop(0, 8, down_tile, 0)
    puts = [
        pltpu.make_async_copy(theirs, part_out.at[0], out_s.at[0]),
        pltpu.make_async_copy(mine, part_out.at[1], out_s.at[1]),
    ]
    for put in puts:
        put.start()
    gather.step(3)
    gather.rest()
    loaded(3)

    def top_rows(row):
        return tops4[row].reshape(512, 2048)

    def back_tile(ft, carry):
        columns = pl.ds(pl.multiple_of(ft * 256, 256), 256)
        f_rows = pl.ds(pl.multiple_of((ft % 2) * 256, 256), 256)
        f_cols = pl.ds(pl.multiple_of((ft // 2) * 512, 512), 512)
        later = pl.ds(pl.multiple_of(1024 + ft * 256, 256), 256)
        right = jnp.concatenate([p2[2, nn, f_rows, f_cols] for nn in range(4)], axis=1)
        for row in range(2):
            rows = slice(row * 512, row * 512 + 512)
            dact = contract_last(top_rows(row), right)
            dgu[rows, columns] = (dact * dgu[rows, columns].astype(f32)).astype(bf16)
            dgu[rows, later] = (dact * dgu[rows, later].astype(f32)).astype(bf16)
        return carry

    lax.fori_loop(0, 4, back_tile, 0)
    for put in puts:
        put.wait()

    spread = Spread((o0, o1, o2, o3), (give_s, give_g, keep_s), me)
    columns_here = pl.ds(pl.multiple_of(r * 1024, 1024), 1024)
    slots = {2: 0, 0: 1, 1: 0}

    def moved(which, half):
        def place(target):
            return target.at[which, :, columns_here]

        return wide.at[slots[which], half], which, place, half == 0

    def weights(which, between=None):
        for half in range(2):
            d_first = (jnp.where(half == 0, 1 - r, r)) * 1024

            def weight_tile(i, carry):
                d_cols = pl.ds(pl.multiple_of(d_first + i * 256, 256), 256)
                if which < 2:
                    left = x[:, d_cols]
                    right = dgu[:, which * 1024 : which * 1024 + 1024]
                else:
                    left = tops4[:, :, :, d_cols].reshape(1024, 256)
                    right = act[...]
                wide[slots[which], half, i] = contract_first(left, right).astype(bf16)
                return carry

            lax.fori_loop(0, 4, weight_tile, 0)
            spread.start(*moved(which, half))
            if half == 0 and between is not None:
                between()

    def hop(which, at):
        return (
            push(o0.at[:, which], ra_out.at[at], n_s.at[0, at], n_g.at[0, at], over_x(r, n, w)),
            push(o2.at[:, which], rb_out.at[at], n_s.at[1, at], n_g.at[1, at], over_y(r, n, w)),
        )

    hops = hop(2, 0) + hop(0, 1)
    weights(2)
    for i in range(4):
        s = scatter.order(i)
        rows_t = pl.ds(pl.multiple_of((1 - r) * 512 + s * 128, 128), 128)
        rows_m = pl.ds(pl.multiple_of(r * 512 + s * 128, 128), 128)

        def model_tile(dt, carry):
            nn, half = dt // 2, dt % 2
            columns = pl.ds(pl.multiple_of(dt * 256, 256), 256)
            inner = pl.ds(pl.multiple_of(half * 256, 256), 256)
            left = jnp.concatenate([dgu[rows_t, :], dgu[rows_m, :]], axis=0)
            right = jnp.concatenate([p2[0, nn, inner, :], p2[1, nn, inner, :]], axis=1)
            part = contract_last(left, right)
            seen = jnp.concatenate([x[rows_t, columns], x[rows_m, columns]], axis=0)
            terms = part * seen.astype(f32)
            gain_out[:, columns] += jnp.sum(terms.reshape(32, 8, 256), axis=0)
            part = part.astype(bf16)
            theirs[s, :, columns] = part[0:128]
            mine[s, :, columns] = part[128:256]
            return carry

        lax.fori_loop(0, 8, model_tile, 0)
        scatter.pair(s).start()
        if i < 2:
            which = (2, 0)[i]
            spread.wait_recv(*moved(which, 0))
            spread.wait(*moved(which, 1))
            hops[2 * i].start()
            hops[2 * i + 1].start()
        if i == 0:
            weights(0)
            scatter.advance((0,), ())
        elif i > 1:
            scatter.advance((i - 1,), (i - 2,))

    def scale(rows):
        gain_out[rows, :] = gain_out[rows, :] / gain[...]

    each_rows(8, 8, scale)
    spread.wait_send(*moved(2, 0))
    weights(1, lambda: scatter.advance((3,), (2,)))
    scatter.advance((), (3,))
    scatter.total(sum_out)
    scatter.sent()
    gather.sent()
    spread.wait_send(*moved(0, 0))
    spread.wait_recv(*moved(1, 0))
    spread.wait_send(*moved(1, 0))
    spread.wait(*moved(1, 1))
    for hop in hops:
        hop.wait()


def spread_shapes(*dims):
    return (jax.ShapeDtypeStruct((2,) + dims, bf16),) * 4


def ffn_stage(*args):
    shard, width = 128, 2048
    return comm_call(
        ffn_kernel, "ffn", 4,
        (
            jax.ShapeDtypeStruct((2, 4, shard, width), bf16),
            jax.ShapeDtypeStruct((shard, width), f32),
            jax.ShapeDtypeStruct((8, width), f32),
        )
        + spread_shapes(3, 128, width)
        + (jax.ShapeDtypeStruct((2, 2, 128, width), bf16),) * 2,
        [vmem(), hbm(), vmem()] + [hbm()] * 7 + [vmem()], [hbm(), vmem(), vmem()] + [hbm()] * 6,
        [pltpu.VMEM((4, shard, width), bf16)] * 2
        + scatter_bufs(shard, width) + scatter_sems()
        + [
            pltpu.VMEM((1024, 1024), bf16),
            pltpu.VMEM((1024, 2048), bf16),
            pltpu.VMEM((2, 2, 4, 256, 1024), bf16),
            pltpu.SemaphoreType.DMA((2,)),
        ]
        + spread_sems(3)
        + [pltpu.VMEM((3, 4, 512, 1024), bf16), pltpu.SemaphoreType.DMA((4, 4))]
        + [pltpu.SemaphoreType.DMA((2, 2))] * 2
        + gather_scratch(shard, width)
        + [pltpu.SemaphoreType.DMA(())],
        args, flops=4 * 10**10, sent=10**8,
    )


def norm_back(values, gain, grad):
    root = lax.rsqrt(jnp.mean(values * values, axis=-1, keepdims=True) + norm_eps)
    weighted = grad * gain
    inner = jnp.mean(weighted * values, axis=-1, keepdims=True)
    return root * weighted - values * (root * root * root) * inner


def branch_kernel(
    total, mid, grad_top, gain, p1, att, a_in, b_in, a_keep, b_keep, a_came, b_came,
    gmid_out, datt_out, o0, o1, o2, o3, ra_out, rb_out, la_out, lb_out,
    buf, g0, g1, g2, g3, wide, give_s, give_g, keep_s, n_s, n_g, kept, came, in_s,
):
    me = spot()
    r, n, w = me
    greet(line_partners(r, n, w, 4) + square_partners(r, n, w))
    gather = Gather(buf, (g0, g1, g2, g3), me, 4)
    hops = [
        push(a_in.at[:, 1], ra_out, n_s.at[0], n_g.at[0], over_x(r, n, w)),
        push(b_in.at[:, 1], rb_out, n_s.at[1], n_g.at[1], over_y(r, n, w)),
        push(kept.at[0], la_out, n_s.at[2], n_g.at[2], over_y(r, n, w)),
        push(kept.at[1], lb_out, n_s.at[3], n_g.at[3], over_x(r, n, w)),
    ]
    loads = []
    for j, (keep, first) in enumerate(((a_keep, a_came), (b_keep, b_came))):
        loads += [
            pltpu.make_async_copy(keep.at[1, 2], kept.at[j], in_s.at[j, 0]),
            pltpu.make_async_copy(first.at[0, 1], came.at[j], in_s.at[j, 1]),
        ]
    for load in loads:
        load.start()
    hops[0].start()
    hops[1].start()

    def body(rows):
        grad = norm_back(mid[rows, :], gain[...], total[rows, :]) + grad_top[rows, :].astype(f32)
        gmid_out[rows, :] = grad
        buf[r, w, rows, :] = grad.astype(bf16)

    each_rows(mid.shape[0], 16, body)
    gather.own()
    for load in loads:
        load.wait()
    for j in range(2):
        def join(rows):
            kept[j, rows, :] = (kept[j, rows, :].astype(f32) + came[j, rows, :].astype(f32)).astype(bf16)

        each_rows(128, 16, join)
        hops[2 + j].start()
    for k in (1, 2, 3):
        gather.step(k)
    gather.rest()
    for row in range(2):
        for pair in range(2):
            left = jnp.concatenate([buf[row, 2 * pair], buf[row, 2 * pair + 1]], axis=0)
            right = jnp.concatenate(
                [out_block(p1, nn, half) for nn in range(4) for half in range(2)], axis=1
            )
            datt_out[row, pair * 256 : pair * 256 + 256, :] = contract_last(left, right).astype(bf16)

    spread = Spread((o0, o1, o2, o3), (give_s, give_g, keep_s), me)

    def moved(half):
        def place(target):
            return target.at[:, pl.ds(pl.multiple_of(r * 256, 256), 256)]

        return wide.at[half], 0, place, half == 0

    for half in range(2):
        d_first = (jnp.where(half == 0, 1 - r, r)) * 1024

        def weight_tile(i, carry):
            columns = pl.ds(pl.multiple_of(d_first + i * 256, 256), 256)
            left = buf[:, :, :, columns].reshape(1024, 256)
            wide[half, i] = contract_first(left, att[...]).astype(bf16)
            return carry

        lax.fori_loop(0, 4, weight_tile, 0)
        spread.start(*moved(half))
    gather.sent()
    spread.wait(*moved(0))
    spread.wait(*moved(1))
    for hop in hops:
        hop.wait()


def branch_stage(*args):
    shard, width = 128, 2048
    return comm_call(
        branch_kernel, "branch", 5,
        (
            jax.ShapeDtypeStruct((shard, width), f32),
            jax.ShapeDtypeStruct((2, 512, 256), bf16),
        )
        + spread_shapes(128, 512)
        + (jax.ShapeDtypeStruct((2, 128, width), bf16),) * 2
        + (jax.ShapeDtypeStruct((128, width), bf16),) * 2,
        [vmem()] * 6 + [hbm()] * 6, [vmem(), vmem()] + [hbm()] * 8,
        gather_scratch(shard, width)
        + [pltpu.VMEM((2, 4, 256, 256), bf16)]
        + spread_sems(1)
        + [pltpu.SemaphoreType.DMA((4,))] * 2
        + [pltpu.VMEM((2, 128, width), bf16)] * 2
        + [pltpu.SemaphoreType.DMA((2, 2))],
        args, flops=10**10, sent=10**8,
    )


def unproject_kernel(
    q, kv, att, grad, lse, x, p1, tabs, gain, parts, mid, a_keep, b_keep, a_gate, b_gate, a_up, b_up, oa_in, ob_in,
    part_out, gain_out, o0, o1, o2, o3, hid_out, ra_out, rb_out, roa_out, rob_out,
    send, recv, both, wide_q, wide_kv, s_s, s_g, give_s, give_g, keep_s,
    mine, from_pt, from_up, from_dn, s0, s1, s2, s3, s4, s5,
    kept, came, acc, in_s, n_s, n_g, m_s, dkv,
):
    me = spot()
    r, n, w = me
    loads = []
    for j, (keep, gate, up) in enumerate(((a_keep, a_gate, a_up), (b_keep, b_gate, b_up))):
        loads += [
            pltpu.make_async_copy(keep.at[1, 0:2], kept.at[j], in_s.at[j, 0]),
            pltpu.make_async_copy(gate.at[1, 1], came.at[j, 0], in_s.at[j, 1]),
            pltpu.make_async_copy(up.at[1], came.at[j, 1], in_s.at[j, 2]),
        ]
    loads.append(pltpu.make_async_copy(parts.at[r], mine, m_s))
    for load in loads:
        load.start()
    greet(
        line_partners(r, n, w, 4)
        + [
            (n >= 1, nar_device(r, n, w, -1)),
            (n >= 2, nar_device(r, n, w, -2)),
            (n <= 2, nar_device(r, n, w, 1)),
            (n <= 1, nar_device(r, n, w, 2)),
        ]
        + square_partners(r, n, w)
    )
    scatter = Scatter(
        mine, parts.at[1 - r], (from_pt, from_up, from_dn), (s0, s1, s2, s3, s4, s5), me, 4
    )
    hops = [
        push(kept.at[0], ra_out, n_s.at[0], n_g.at[0], over_y(r, n, w)),
        push(kept.at[1], rb_out, n_s.at[1], n_g.at[1], over_x(r, n, w)),
        push(oa_in, roa_out, n_s.at[2], n_g.at[2], over_x(r, n, w)),
        push(ob_in, rob_out, n_s.at[3], n_g.at[3], over_y(r, n, w)),
    ]

    def copy(row, slot, by):
        return pltpu.make_async_remote_copy(
            send.at[row, slot], recv.at[row, slot], s_s.at[row, slot], s_g.at[row, slot],
            device_id=nar_device(r, n, w, by), device_id_type=MESH,
        )

    for i in range(4):
        scatter.pair(scatter.order(i)).start()
    for load in loads:
        load.wait()
    for j in range(2):
        for which in range(2):
            def join(rows):
                total = kept[j, which, rows, :].astype(f32) + came[j, which, rows, :].astype(f32)
                kept[j, which, rows, :] = total.astype(bf16)

            each_rows(128, 16, join)
        hops[j].start()
    hops[2].start()
    hops[3].start()
    scatter.advance((0, 1, 2, 3), ())

    def attention(i, carry):
        row, block = i // 4, i % 4
        first_query = 1024 + block * QUERIES
        here = pl.ds(pl.multiple_of(block * QUERIES, QUERIES), QUERIES)

        @pl.when(block == 0)
        def _():
            dkv[row] = jnp.zeros((1536, 128), f32)

        query = stack_low(q[row, here, :].astype(f32)).astype(bf16)
        grads = stack_high(grad[row, here, :].astype(f32))
        inner = jnp.sum(grads * stack_high(att[row, here, :].astype(f32)), axis=1, keepdims=True)
        grads = grads.astype(bf16)
        logsum = jnp.concatenate([lse[row, block]] * (KEYS // 128), axis=1)
        starts = tabs[row, here, 256:384]

        def key_tile(step, dq):
            tile = block // 2 + step
            rows = pl.ds(pl.multiple_of(tile * KEYS, KEYS), KEYS)
            pair = kv[row, rows, :]
            ok = allowed_tile(starts, tile, first_query)
            scores = contract_last(query, pair) * 0.125
            prob = jnp.where(ok, jnp.exp(scores - logsum), 0.0)
            grad_prob = contract_last(grads, pair)
            grad_scores = (prob * (grad_prob - inner)).astype(bf16)
            dkv[row, rows, :] += contract_first(grad_scores, query) * 0.125 + contract_first(
                prob.astype(bf16), grads
            )
            return dq + jnp.dot(grad_scores, pair, preferred_element_type=f32)

        dq = lax.fori_loop(0, 5, key_tile, jnp.zeros((4 * QUERIES, 128), f32), unroll=True)
        flat = unstack(dq, True) * 0.125
        cosine, sine = tabs[row, here, 0:128], -tabs[row, here, 128:256]
        there = pl.ds(pl.multiple_of(i * QUERIES, QUERIES), QUERIES)
        both[there, 0:128] = turn(flat[:, 0:128], cosine, sine).astype(bf16)
        both[there, 128:256] = turn(flat[:, 128:256], cosine, sine).astype(bf16)

        @pl.when(block == 3)
        def _():
            for slot, by in ((1, -1), (0, -2)):
                @pl.when(n >= -by)
                def _():
                    send[row, slot] = dkv[row, slot * 512 : slot * 512 + 512, :].astype(bf16)
                    copy(row, slot, by).start()

        @pl.when(i == 3)
        def _():
            scatter.advance((), (0,))

        return carry

    lax.fori_loop(0, 8, attention, 0)
    scatter.advance((), (1,))

    spread = Spread((o0, o1, o2, o3), (give_s, give_g, keep_s), (r, n, w))

    def moved_q(half):
        def place(target):
            return target.at[:, pl.ds(pl.multiple_of(r * 256, 256), 256)]

        return wide_q.at[half], 0, place, half == 0

    def moved_kv(half):
        def place(target):
            return target.at[:, pl.ds(pl.multiple_of(512 + r * 128, 128), 128)]

        return wide_kv.at[half], 1, place, half == 0

    def weight(half, columns, wide):
        d_first = (jnp.where(half == 0, 1 - r, r)) * 1024

        def tile(i, carry):
            d_cols = pl.ds(pl.multiple_of(d_first + i * 256, 256), 256)
            wide[half, i] = contract_first(x[:, d_cols], both[:, columns]).astype(bf16)
            return carry

        lax.fori_loop(0, 4, tile, 0)

    for half in range(2):
        weight(half, slice(0, 256), wide_q)
        spread.start(*moved_q(half))
    lane = lax.broadcasted_iota(jnp.int32, (128, 128), 1)
    for row in range(2):
        for slot, by in ((1, -1), (0, -2)):
            @pl.when(n <= 3 + by)
            def _():
                copy(row, slot, by).wait_recv()

        def tile(i, carry):
            rows = pl.ds(pl.multiple_of(i * 128, 128), 128)
            total = dkv[row, pl.ds(pl.multiple_of(1024 + i * 128, 128), 128), :]
            zero = jnp.zeros_like(total)
            total = total + jnp.where(n <= 2, recv[row, 1, rows, :].astype(f32), zero)
            total = total + jnp.where(n <= 1, recv[row, 0, rows, :].astype(f32), zero)
            turned = turn(total, tabs[row, rows, 0:128], -tabs[row, rows, 128:256])
            both[pl.ds(pl.multiple_of(row * 512 + i * 128, 128), 128), 256:384] = jnp.where(
                lane < 64, turned, total
            ).astype(bf16)
            return carry

        lax.fori_loop(0, 4, tile, 0)
    for half in range(2):
        weight(half, slice(256, 384), wide_kv)
        spread.start(*moved_kv(half))
    scatter.advance((), (2,))
    gain_out[...] = jnp.zeros_like(gain_out)

    def model_tile(dt, carry):
        nn, half = dt // 2, dt % 2
        columns = pl.ds(pl.multiple_of(dt * 256, 256), 256)
        inner = pl.ds(pl.multiple_of(half * 256, 256), 256)
        right = p1[nn, inner, 0:384]
        for row in range(2):
            for block in range(2):
                first = row * 512 + block * 256
                part = contract_last(both[first : first + 256, :], right)
                terms = part * x[first : first + 256, columns].astype(f32)
                gain_out[:, columns] += jnp.sum(terms.reshape(32, 8, 256), axis=0)
                part_out[row, 2 * block, :, columns] = part[0:128].astype(bf16)
                part_out[row, 2 * block + 1, :, columns] = part[128:256].astype(bf16)
        return carry

    lax.fori_loop(0, 8, model_tile, 0)
    gain_out[...] = gain_out[...] / gain[...]
    scatter.advance((), (3,))
    scatter.total(acc)

    def last(rows):
        hid_out[rows, :] = (acc[rows, :] + mid[rows, :]).astype(bf16)

    each_rows(128, 16, last)
    scatter.sent()
    for row in range(2):
        for slot, by in ((1, -1), (0, -2)):
            @pl.when(n >= -by)
            def _():
                copy(row, slot, by).wait_send()

    for half in range(2):
        spread.wait(*moved_q(half))
        spread.wait(*moved_kv(half))
    for hop in hops:
        hop.wait()


def unproject(*args):
    return comm_call(
        unproject_kernel, "unproject", 6,
        (
            jax.ShapeDtypeStruct((2, 4, 128, 2048), bf16),
            jax.ShapeDtypeStruct((8, 2048), f32),
        )
        + spread_shapes(128, 768)
        + (jax.ShapeDtypeStruct((128, 2048), bf16),)
        + (jax.ShapeDtypeStruct((2, 128, 2048), bf16),) * 2
        + (jax.ShapeDtypeStruct((2, 128, 512), bf16),) * 2,
        [vmem()] * 9 + [hbm(), vmem()] + [hbm()] * 8,
        [vmem(), vmem()] + [hbm()] * 4 + [vmem()] + [hbm()] * 4,
        [
            pltpu.VMEM((2, 2, 512, 128), bf16),
            pltpu.VMEM((2, 2, 512, 128), bf16),
            pltpu.VMEM((1024, 384), bf16),
            pltpu.VMEM((2, 4, 256, 256), bf16),
            pltpu.VMEM((2, 4, 256, 128), bf16),
            pltpu.SemaphoreType.DMA((2, 2)),
            pltpu.SemaphoreType.DMA((2, 2)),
        ]
        + spread_sems(2)
        + [pltpu.VMEM((4, 128, 2048), bf16)]
        + scatter_bufs(128, 2048) + scatter_sems()
        + [
            pltpu.VMEM((2, 2, 128, 2048), bf16),
            pltpu.VMEM((2, 2, 128, 2048), bf16),
            pltpu.VMEM((128, 2048), f32),
            pltpu.SemaphoreType.DMA((2, 3)),
            pltpu.SemaphoreType.DMA((4,)),
            pltpu.SemaphoreType.DMA((4,)),
            pltpu.SemaphoreType.DMA(()),
            pltpu.VMEM((2, 1536, 128), f32),
        ],
        args, flops=10**10, sent=10**7,
    )


def leave_kernel(
    parts, hidden, gain, gmid, gains, qa_send, qa_keep, qb_send, qb_keep, oa_keep, ob_keep, oa_in, ob_in,
    grad_out, ga_out, query_out, key_out, value_out, output_out,
    mine, from_pt, from_up, from_dn, s0, s1, s2, s3, s4, s5,
    acc, over_wid, summed, over_rest, w_s, w_g, t_s, t_g,
    first_q, next_q, then_q, next_o, then_o, kv, n_s, n_g, k0, k1, k2, k3, m_s,
):
    me = spot()
    r, n, w = me
    own_parts = pltpu.make_async_copy(parts.at[r], mine, m_s)
    own_parts.start()
    partners = [(w != j, (r, n, jnp.int32(j))) for j in range(4)]
    partners += [
        ((r != a) | (n != b), (jnp.int32(a), jnp.int32(b), w)) for a in range(2) for b in range(4)
    ]
    greet(partners)
    kv_gather = Gather(kv, (k0, k1, k2, k3), me, 4, pair=False)
    x_side, y_side = over_x(r, n, w), over_y(r, n, w)
    q_hops = [
        push(qa_send, first_q.at[0], n_s.at[0], n_g.at[0], x_side),
        push(qb_send, first_q.at[1], n_s.at[1], n_g.at[1], y_side),
    ]
    q_later = [
        push(next_q.at[0], then_q.at[0], n_s.at[2], n_g.at[2], y_side),
        push(next_q.at[1], then_q.at[1], n_s.at[3], n_g.at[3], x_side),
    ]
    o_hops = [
        push(next_o.at[0], then_o.at[0], n_s.at[4], n_g.at[4], y_side),
        push(next_o.at[1], then_o.at[1], n_s.at[5], n_g.at[5], x_side),
    ]
    for hop in q_hops:
        hop.start()
    scatter = Scatter(
        mine, parts.at[1 - r], (from_pt, from_up, from_dn), (s0, s1, s2, s3, s4, s5), me, 4
    )
    for i in range(4):
        scatter.pair(scatter.order(i)).start()

    def wid_copy(j, slot):
        return pltpu.make_async_remote_copy(
            gains, over_wid.at[slot], w_s.at[j], w_g.at[slot],
            device_id=(r, n, jnp.int32(j)), device_id_type=MESH,
        )

    def rest_copy(a, b, slot):
        return pltpu.make_async_remote_copy(
            summed, over_rest.at[slot], t_s.at[a * 4 + b], t_g.at[slot],
            device_id=(jnp.int32(a), jnp.int32(b), w), device_id_type=MESH,
        )

    for j in range(4):
        @pl.when(w != j)
        def _():
            wid_copy(j, w).start()

    own_parts.wait()
    scatter.advance((0, 1, 2), ())
    for j, (keep, came) in enumerate(((oa_keep, oa_in), (ob_keep, ob_in))):
        next_o[j] = (keep[1].astype(f32) + came[1].astype(f32)).astype(bf16)
        o_hops[j].start()
    summed[...] = gains[...]
    for j in range(4):
        @pl.when(w != j)
        def _():
            wid_copy(j, j).wait_recv()
            summed[...] += over_wid[j]

    for a in range(2):
        for b in range(4):
            @pl.when((r != a) | (n != b))
            def _():
                rest_copy(a, b, r * 4 + n).start()

    for j, keep in enumerate((qa_keep, qb_keep)):
        q_hops[j].wait_recv()
        next_q[j] = (keep[1].astype(f32) + first_q[j, 1].astype(f32)).astype(bf16)
        q_later[j].start()
    scatter.advance((), (0,))
    for j, keep in enumerate((qa_keep, qb_keep)):
        q_later[j].wait_recv()
        total = keep[0].astype(f32) + first_q[j, 0].astype(f32) + then_q[j].astype(f32)
        query_out[j * 128 : j * 128 + 128, :] = total[:, 0:512]
        kv[0, w, j * 128 : j * 128 + 128, :] = total[:, 512:768].astype(bf16)
    kv_gather.own()
    scatter.advance((3,), (1, 2))
    kv_gather.advance((), (1,))
    scatter.advance((), (3,))
    kv_gather.advance((), (2,))
    for j, (keep, came) in enumerate(((oa_keep, oa_in), (ob_keep, ob_in))):
        o_hops[j].wait_recv()
        output_out[j * 128 : j * 128 + 128, :] = (
            keep[0].astype(f32) + came[0].astype(f32) + then_o[j].astype(f32)
        )
    mine_block = r * 4 + n
    ga_out[0:1] = summed[pl.ds(mine_block, 1), :]
    ga_out[1:2] = summed[pl.ds(mine_block + 8, 1), :]
    for a in range(2):
        for b in range(4):
            @pl.when((r != a) | (n != b))
            def _():
                slot = a * 4 + b
                rest_copy(a, b, slot).wait_recv()
                ga_out[0:1] += over_rest[slot, pl.ds(mine_block, 1), :]
                ga_out[1:2] += over_rest[slot, pl.ds(mine_block + 8, 1), :]

    scatter.total(acc)

    def last(rows):
        grad = norm_back(hidden[rows, :].astype(f32), gain[...], acc[rows, :])
        grad_out[rows, :] = (grad + gmid[rows, :]).astype(bf16)

    each_rows(hidden.shape[0], 16, last)
    kv_gather.advance((1, 2, 3), (3,))
    lane = lax.broadcasted_iota(jnp.int32, (256, 128), 1)
    for j in range(4):
        even, odd = kv[0, j, :, 0:128].astype(f32), kv[0, j, :, 128:256].astype(f32)
        here = slice(j * 128, j * 128 + 128)
        key_out[:, here] = jnp.where(lane < 64, even, pltpu.roll(odd, 64, 1))
        value_out[:, here] = jnp.where(lane < 64, pltpu.roll(even, 64, 1), odd)
    scatter.sent()
    kv_gather.sent()
    for hop in q_hops + q_later + o_hops:
        hop.wait_send()
    for j in range(4):
        @pl.when(w != j)
        def _():
            wid_copy(j, w).wait_send()

    for a in range(2):
        for b in range(4):
            @pl.when((r != a) | (n != b))
            def _():
                rest_copy(a, b, r * 4 + n).wait_send()


def leave(*args):
    shard, width = 128, 2048
    grad = jax.ShapeDtypeStruct((256, 512), f32)
    return comm_call(
        leave_kernel, "leave", 7,
        (jax.ShapeDtypeStruct((shard, width), bf16), jax.ShapeDtypeStruct((8, 256), f32))
        + (grad,) * 4,
        [hbm()] + [vmem()] * 12, [vmem()] * 6,
        [pltpu.VMEM((4, shard, width), bf16)]
        + scatter_bufs(shard, width) + scatter_sems()
        + [
            pltpu.VMEM((shard, width), f32),
            pltpu.VMEM((4, 16, 256), f32),
            pltpu.VMEM((16, 256), f32),
            pltpu.VMEM((8, 16, 256), f32),
            pltpu.SemaphoreType.DMA((4,)),
            pltpu.SemaphoreType.DMA((4,)),
            pltpu.SemaphoreType.DMA((8,)),
            pltpu.SemaphoreType.DMA((8,)),
            pltpu.VMEM((2, 2, 128, 768), bf16),
            pltpu.VMEM((2, 128, 768), bf16),
            pltpu.VMEM((2, 128, 768), bf16),
            pltpu.VMEM((2, 128, 512), bf16),
            pltpu.VMEM((2, 128, 512), bf16),
            pltpu.VMEM((1, 4, 256, 256), bf16),
            pltpu.SemaphoreType.DMA((6,)),
            pltpu.SemaphoreType.DMA((6,)),
        ]
        + gather_sems()
        + [pltpu.SemaphoreType.DMA(())],
        args, flops=10**10, sent=10**8,
    )


def local_fast(
    hidden_in, doc_lengths, w_query, w_key, w_value, w_output, w_gate, w_up, w_down,
    gain_attn, gain_ffn, grad_out,
):
    r, n, w = spot()
    hidden, grad_top = hidden_in[0], grad_out[0]
    gain_a, gain_f = gain_attn[None], gain_ffn[None]
    def half(weight, axis):
        size = weight.shape[axis] // 2
        return lax.dynamic_slice_in_dim(weight, r * size, size, axis)

    head = (w * 2 + r) * HD
    kv_pack = jnp.concatenate(
        [lax.dynamic_slice_in_dim(w_key, head, HD, 1), lax.dynamic_slice_in_dim(w_value, head, HD, 1)],
        axis=1,
    )
    out_half = half(w_output, 0)
    p1_shard = jnp.concatenate(
        [half(w_query, 1), kv_pack, jnp.concatenate([out_half[:, :256], out_half[:, 256:]], axis=0)],
        axis=1,
    )
    down_half = half(w_down, 0)
    gate_own, up_own = half(w_gate, 1), half(w_up, 1)
    down_own = jnp.concatenate([down_half[:512], down_half[512:]], axis=1)

    token_ids = n * 512 + jnp.arange(512, dtype=jnp.int32)
    doc_start, places = doc_layout(doc_lengths[0], token_ids)
    angles = places.astype(f32)[:, None] * inverse_freq()[None, :]
    cosine, sine = jnp.cos(angles), jnp.sin(angles)
    start_here = (doc_start - (n - 2) * 512).astype(f32)
    tab = jnp.concatenate(
        [cosine] * 4 + [-sine, sine] * 2 + [jnp.broadcast_to(start_here[:, None], (512, 128))],
        axis=1,
    )

    rows, tabs, p1, down_a = enter(hidden, gain_a, tab, p1_shard, down_own)
    rows3, rows2 = rows.reshape(2, 512, 2048), rows.reshape(1024, 2048)
    q, kv, tops, down_b = project(rows3, p1, tabs, grad_top, down_own)
    kv_flat = kv.reshape(2, 1536, 128)
    att, lse = attend(q, kv_flat, tabs)
    mid, ffn_rows, gate_all, up_all = middle_stage(att, p1, hidden, gain_f, gate_own, up_own)
    parts, total, gain_f_part, a_send, a_keep, b_send, b_keep, ra_dg, rb_dg = ffn_stage(
        ffn_rows.reshape(1024, 2048), tops, grad_top,
        gate_own, gate_all, up_own, up_all, down_own, down_a, down_b, gain_f,
    )
    gmid, datt, oa_send, oa_keep, ob_send, ob_keep, ra_u, rb_u, la_d, lb_d = branch_stage(
        total, mid, grad_top, gain_f, p1, att.reshape(1024, 256),
        a_send, b_send, a_keep, b_keep, ra_dg, rb_dg,
    )
    (
        dparts, gain_a_part, qa_send, qa_keep, qb_send, qb_keep,
        hidden_out, ra_last, rb_last, oa_came, ob_came,
    ) = unproject(
        q, kv_flat, att, datt, lse, rows2, p1, tabs, gain_a, parts, mid,
        a_keep, b_keep, ra_dg, rb_dg, ra_u, rb_u, oa_send, ob_send,
    )
    gains = jnp.concatenate(
        [gain_f_part.sum(axis=0).reshape(8, 256), gain_a_part.sum(axis=0).reshape(8, 256)], axis=0
    )
    grad_in, gain_sums, grad_query, grad_key, grad_value, output_sum = leave(
        dparts, hidden, gain_a, gmid, gains,
        qa_send, qa_keep, qb_send, qb_keep, oa_keep, ob_keep, oa_came, ob_came,
    )

    def joined(which):
        def half_rows(keep, came, last):
            return keep[0, which].astype(f32) + came.astype(f32) + last.astype(f32)

        a_came, b_came, a_last, b_last = (
            (ra_dg[1, 0], rb_dg[1, 0], ra_last[0], rb_last[0]),
            (ra_u[0], rb_u[0], ra_last[1], rb_last[1]),
            (ra_dg[0, 0], rb_dg[0, 0], la_d, lb_d),
        )[which]
        return jnp.concatenate(
            [half_rows(a_keep, a_came, a_last), half_rows(b_keep, b_came, b_last)], axis=0
        )

    return (
        hidden_out[None],
        grad_in[None],
        grad_query,
        grad_key,
        grad_value,
        output_sum.T,
        joined(0),
        joined(1),
        joined(2).T,
        gain_sums[1],
        gain_sums[0],
    )


def solution(mesh):
    in_specs = (
        P("row", ("nar", "wid"), None),
        P("row", None),
        P("nar", "wid"),
        P("nar", None),
        P("nar", None),
        P("wid", "nar"),
        P("nar", "wid"),
        P("nar", "wid"),
        P("wid", "nar"),
        P(),
        P(),
        P("row", ("nar", "wid"), None),
    )
    out_specs = (
        P("row", ("nar", "wid"), None),
        P("row", ("nar", "wid"), None),
        P(("row", "nar"), "wid"),
        P(("row", "nar"), None),
        P(("row", "nar"), None),
        P("wid", ("row", "nar")),
        P(("row", "nar"), "wid"),
        P(("row", "nar"), "wid"),
        P("wid", ("row", "nar")),
        P(("row", "nar")),
        P(("row", "nar")),
    )
    sizes = dict(mesh.shape)
    fits = sizes == {"row": 2, "nar": 4, "wid": 4}

    def body(*args):
        small = args[0].shape == (1, 128, 2048)
        return (local_fast if fits and small else local)(*args)

    return jax.shard_map(body, mesh=mesh, in_specs=in_specs, out_specs=out_specs, check_vma=False)
```

```python
import math

import jax
import jax.numpy as jnp
from jax import lax
from jax.experimental import pallas as pl
from jax.experimental.pallas import tpu as pltpu
from jax.sharding import PartitionSpec as P

H = 32
KV = 8
HD = 64


norm_eps = 1e-05
masked_score = -1e30


def inverse_freq():
    listed = []
    for pair_index in range(HD // 2):
        base_freq = 500000.0 ** (-2.0 * pair_index / HD)
        wavelength = 2.0 * math.pi / base_freq
        smoothing = (8192.0 / wavelength - 1.0) / 3.0
        blended = (1.0 - smoothing) * base_freq / 32.0 + smoothing * base_freq
        if wavelength < 2048.0:
            listed.append(base_freq)
        elif wavelength > 8192.0:
            listed.append(base_freq / 32.0)
        else:
            listed.append(blended)
    return jnp.asarray(listed, dtype=jnp.float32)


def rotate(values, cosine_table, sine_table):
    half_dim = HD // 2
    first_half = values[..., :half_dim]
    second_half = values[..., half_dim:]
    return jnp.concatenate(
        [
            first_half * cosine_table - second_half * sine_table,
            second_half * cosine_table + first_half * sine_table,
        ],
        axis=-1,
    )


def rotate_back(grads_in, cosine_table, sine_table):
    half_dim = HD // 2
    first_half = grads_in[..., :half_dim]
    second_half = grads_in[..., half_dim:]
    return jnp.concatenate(
        [
            first_half * cosine_table + second_half * sine_table,
            second_half * cosine_table - first_half * sine_table,
        ],
        axis=-1,
    )


def doc_layout(lengths_row, token_ids):
    ends_at = jnp.cumsum(lengths_row, dtype=jnp.int32)
    starts_at = ends_at - lengths_row
    inside = (token_ids[:, None] >= starts_at[None, :]) & (token_ids[:, None] < ends_at[None, :])
    doc_start = jnp.sum(jnp.where(inside, starts_at[None, :], 0), axis=1, dtype=jnp.int32)
    return (doc_start, token_ids - doc_start)


def norm_forward(values, gain_vector):
    root_inv = lax.rsqrt(jnp.mean(values * values, axis=-1, keepdims=True) + norm_eps)
    return (root_inv, (values * root_inv * gain_vector).astype(jnp.bfloat16))


def norm_backward(values, root_inv, gain_vector, grad_normed):
    weighted = grad_normed * gain_vector
    inner_sum = jnp.mean(weighted * values, axis=-1, keepdims=True)
    grad_values = root_inv * weighted - values * (root_inv * root_inv * root_inv) * inner_sum
    gain_term = jnp.sum(grad_normed * values * root_inv, axis=0)
    return (grad_values, gain_term)


def contract_last(left_side, right_side):
    return lax.dot_general(
        left_side, right_side, (((1,), (1,)), ((), ())), preferred_element_type=jnp.float32
    )


def contract_first(left_side, right_side):
    return lax.dot_general(
        left_side, right_side, (((0,), (0,)), ((), ())), preferred_element_type=jnp.float32
    )


def local(
    hidden_in,
    doc_lengths,
    w_query,
    w_key,
    w_value,
    w_output,
    w_gate,
    w_up,
    w_down,
    gain_attn,
    gain_ffn,
    grad_out,
):
    wid_count = lax.axis_size("wid")
    nar_count = lax.axis_size("nar")
    wid_index = lax.axis_index("wid")
    nar_index = lax.axis_index("nar")
    local_tokens = hidden_in.shape[1]
    block_tokens = local_tokens * wid_count
    seq_length = block_tokens * nar_count
    query_heads = w_query.shape[1] // HD
    group_size = H // KV
    kv_local = max(query_heads // group_size, 1)
    heads_per_kv = query_heads // kv_local
    kv_first = wid_index * query_heads // group_size
    query_block = min(512, block_tokens)
    block_count = block_tokens // query_block
    item_count = block_count * query_heads
    attn_scale = HD ** (-0.5)
    query_full, key_full, value_full, output_full, gate_full, up_full, down_full = (
        lax.all_gather(w_query, "nar", axis=0, tiled=True),
        lax.all_gather(w_key, "nar", axis=0, tiled=True),
        lax.all_gather(w_value, "nar", axis=0, tiled=True),
        lax.all_gather(w_output, "nar", axis=1, tiled=True),
        lax.all_gather(w_gate, "nar", axis=0, tiled=True),
        lax.all_gather(w_up, "nar", axis=0, tiled=True),
        lax.all_gather(w_down, "nar", axis=1, tiled=True),
    )
    key_local = lax.dynamic_slice_in_dim(key_full, kv_first * HD, kv_local * HD, 1)
    value_local = lax.dynamic_slice_in_dim(value_full, kv_first * HD, kv_local * HD, 1)
    token_ids = nar_index * block_tokens + jnp.arange(block_tokens, dtype=jnp.int32)
    doc_start, places = doc_layout(doc_lengths[0], token_ids)
    angles = places.astype(jnp.float32)[:, None] * inverse_freq()[None, :]
    cosine_table = jnp.cos(angles)[:, None, :]
    sine_table = jnp.sin(angles)[:, None, :]
    key_ids = jnp.arange(seq_length, dtype=jnp.int32)
    residual = hidden_in[0].astype(jnp.float32)
    root_attn, normed_attn = norm_forward(residual, gain_attn)
    normed_rows = lax.all_gather(normed_attn, "wid", axis=0, tiled=True)
    query_pre = jnp.dot(normed_rows, query_full, preferred_element_type=jnp.float32)
    key_pre = jnp.dot(normed_rows, key_local, preferred_element_type=jnp.float32)
    value_rows = jnp.dot(normed_rows, value_local, preferred_element_type=jnp.float32).astype(
        jnp.bfloat16
    )
    query_rot = (
        rotate(query_pre.reshape(block_tokens, query_heads, HD), cosine_table, sine_table)
        .astype(jnp.bfloat16)
        .reshape(block_tokens, query_heads * HD)
    )
    key_rot = (
        rotate(key_pre.reshape(block_tokens, kv_local, HD), cosine_table, sine_table)
        .astype(jnp.bfloat16)
        .reshape(block_tokens, kv_local * HD)
    )
    key_seq, value_seq = (
        lax.all_gather(key_rot, "nar", axis=0, tiled=True),
        lax.all_gather(value_rows, "nar", axis=0, tiled=True),
    )

    def item_inputs(item_index):
        block_index = item_index // query_heads
        head_index = item_index % query_heads
        kv_index = head_index // heads_per_kv
        row_first = block_index * query_block
        query_part = lax.dynamic_slice(query_rot, (row_first, head_index * HD), (query_block, HD))
        key_head = lax.dynamic_slice_in_dim(key_seq, kv_index * HD, HD, 1)
        value_head = lax.dynamic_slice_in_dim(value_seq, kv_index * HD, HD, 1)
        query_ids = lax.dynamic_slice_in_dim(token_ids, row_first, query_block, 0)
        query_starts = lax.dynamic_slice_in_dim(doc_start, row_first, query_block, 0)
        allowed = (key_ids[None, :] <= query_ids[:, None]) & (
            key_ids[None, :] >= query_starts[:, None]
        )
        scores = contract_last(query_part, key_head) * attn_scale
        return (
            row_first,
            head_index,
            kv_index,
            query_part,
            key_head,
            value_head,
            jnp.where(allowed, scores, masked_score),
        )

    def attend(item_index):
        row_first, head_index, kv_index, query_part, key_head, value_head, scores = item_inputs(
            item_index
        )
        row_max = jnp.max(scores, axis=1, keepdims=True)
        exp_scores = jnp.exp(scores - row_max)
        row_total = jnp.sum(exp_scores, axis=1, keepdims=True)
        probability = (exp_scores / row_total).astype(jnp.bfloat16)
        attended = jnp.dot(probability, value_head, preferred_element_type=jnp.float32)
        return (attended, (row_max + jnp.log(row_total))[:, 0])

    attended_items, logsum_items = lax.map(attend, jnp.arange(item_count, dtype=jnp.int32))
    attended_rows = (
        attended_items.reshape(block_count, query_heads, query_block, HD)
        .transpose(0, 2, 1, 3)
        .reshape(block_tokens, query_heads * HD)
        .astype(jnp.bfloat16)
    )
    rows_here = attended_rows
    branch_attn = lax.psum_scatter(
        jnp.dot(rows_here, output_full, preferred_element_type=jnp.float32),
        "wid",
        scatter_dimension=0,
        tiled=True,
    )
    middle = residual + branch_attn
    root_ffn, normed_ffn = norm_forward(middle, gain_ffn)
    ffn_rows = lax.all_gather(normed_ffn, "wid", axis=0, tiled=True)
    gate_proj = jnp.dot(ffn_rows, gate_full, preferred_element_type=jnp.float32)
    up_proj = jnp.dot(ffn_rows, up_full, preferred_element_type=jnp.float32)
    gate_sigmoid = jax.nn.sigmoid(gate_proj)
    gate_silu = gate_proj * gate_sigmoid
    activated = (gate_silu * up_proj).astype(jnp.bfloat16)
    rows_here = activated
    branch_ffn = lax.psum_scatter(
        jnp.dot(rows_here, down_full, preferred_element_type=jnp.float32).astype(jnp.bfloat16),
        "wid",
        scatter_dimension=0,
        tiled=True,
    ).astype(jnp.float32)
    hidden_out = (middle + branch_ffn).astype(jnp.bfloat16)[None]
    grad_top = grad_out[0]
    grad_rows = lax.all_gather(grad_top, "wid", axis=0, tiled=True)
    grad_activated = contract_last(grad_rows, down_full)
    down_weight_grad = contract_first(activated, grad_rows)
    silu_slope = gate_sigmoid * (1.0 + gate_proj * (1.0 - gate_sigmoid))
    grad_gate_b = (grad_activated * up_proj * silu_slope).astype(jnp.bfloat16)
    grad_up_b = (grad_activated * gate_silu).astype(jnp.bfloat16)
    gate_weight_grad = contract_first(ffn_rows, grad_gate_b)
    up_weight_grad = contract_first(ffn_rows, grad_up_b)
    grad_normed_ffn = lax.psum_scatter(
        contract_last(grad_gate_b, gate_full) + contract_last(grad_up_b, up_full),
        "wid",
        scatter_dimension=0,
        tiled=True,
    )
    grad_middle, gain_ffn_term = norm_backward(middle, root_ffn, gain_ffn, grad_normed_ffn)
    grad_middle = grad_middle + grad_top.astype(jnp.float32)
    grad_branch = grad_middle.astype(jnp.bfloat16)
    branch_rows = lax.all_gather(grad_branch, "wid", axis=0, tiled=True)
    grad_attended = contract_last(branch_rows, output_full).astype(jnp.bfloat16)
    output_weight_grad = contract_first(attended_rows, branch_rows)

    def attend_back(carried, item_index):
        key_grad, value_grad = carried
        row_first, head_index, kv_index, query_part, key_head, value_head, scores = item_inputs(
            item_index
        )
        logsum = lax.dynamic_index_in_dim(logsum_items, item_index, 0, keepdims=False)
        probability = jnp.exp(scores - logsum[:, None])
        grad_part = lax.dynamic_slice(
            grad_attended, (row_first, head_index * HD), (query_block, HD)
        )
        grad_prob = contract_last(grad_part, value_head)
        inner_sum = jnp.sum(probability * grad_prob, axis=1, keepdims=True)
        grad_scores = (probability * (grad_prob - inner_sum)).astype(jnp.bfloat16)
        query_grad = jnp.dot(grad_scores, key_head, preferred_element_type=jnp.float32) * attn_scale
        key_part = contract_first(grad_scores, query_part) * attn_scale
        value_part = contract_first(probability.astype(jnp.bfloat16), grad_part)
        key_old = lax.dynamic_slice_in_dim(key_grad, kv_index * HD, HD, 1)
        key_grad = lax.dynamic_update_slice_in_dim(key_grad, key_old + key_part, kv_index * HD, 1)
        value_old = lax.dynamic_slice_in_dim(value_grad, kv_index * HD, HD, 1)
        value_grad = lax.dynamic_update_slice_in_dim(
            value_grad, value_old + value_part, kv_index * HD, 1
        )
        return ((key_grad, value_grad), query_grad)

    zero_grads = jnp.zeros((seq_length, kv_local * HD), jnp.float32)
    (key_grad_seq, value_grad_seq), query_grad_items = lax.scan(
        attend_back, (zero_grads, zero_grads), jnp.arange(item_count, dtype=jnp.int32)
    )
    key_grad_block, value_grad_block = (
        lax.psum_scatter(
            key_grad_seq.astype(jnp.bfloat16), "nar", scatter_dimension=0, tiled=True
        ).astype(jnp.float32),
        lax.psum_scatter(
            value_grad_seq.astype(jnp.bfloat16), "nar", scatter_dimension=0, tiled=True
        ).astype(jnp.float32),
    )
    query_grad_rows = (
        query_grad_items.reshape(block_count, query_heads, query_block, HD)
        .transpose(0, 2, 1, 3)
        .reshape(block_tokens, query_heads, HD)
    )
    query_grad_b = (
        rotate_back(query_grad_rows, cosine_table, sine_table)
        .astype(jnp.bfloat16)
        .reshape(block_tokens, query_heads * HD)
    )
    key_grad_b = (
        rotate_back(key_grad_block.reshape(block_tokens, kv_local, HD), cosine_table, sine_table)
        .astype(jnp.bfloat16)
        .reshape(block_tokens, kv_local * HD)
    )
    value_grad_b = value_grad_block.astype(jnp.bfloat16)
    query_weight_grad = contract_first(normed_rows, query_grad_b)
    key_weight_grad = contract_first(normed_rows, key_grad_b)
    value_weight_grad = contract_first(normed_rows, value_grad_b)
    grad_normed_attn = lax.psum_scatter(
        (
            contract_last(query_grad_b, query_full)
            + contract_last(key_grad_b, key_local)
            + contract_last(value_grad_b, value_local)
        ).astype(jnp.bfloat16),
        "wid",
        scatter_dimension=0,
        tiled=True,
    ).astype(jnp.float32)
    grad_residual, gain_attn_term = norm_backward(residual, root_attn, gain_attn, grad_normed_attn)
    grad_in = (grad_residual + grad_middle).astype(jnp.bfloat16)[None]
    summed = (
        lax.psum_scatter(
            query_weight_grad.astype(jnp.bfloat16), ("row", "nar"), scatter_dimension=0, tiled=True
        ).astype(jnp.float32),
        lax.psum_scatter(
            key_weight_grad.astype(jnp.bfloat16), ("row", "nar"), scatter_dimension=0, tiled=True
        ).astype(jnp.float32),
        lax.psum_scatter(
            value_weight_grad.astype(jnp.bfloat16), ("row", "nar"), scatter_dimension=0, tiled=True
        ).astype(jnp.float32),
        lax.psum_scatter(
            output_weight_grad.astype(jnp.bfloat16), ("row", "nar"), scatter_dimension=1, tiled=True
        ).astype(jnp.float32),
        lax.psum_scatter(
            gate_weight_grad.astype(jnp.bfloat16), ("row", "nar"), scatter_dimension=0, tiled=True
        ).astype(jnp.float32),
        lax.psum_scatter(
            up_weight_grad.astype(jnp.bfloat16), ("row", "nar"), scatter_dimension=0, tiled=True
        ).astype(jnp.float32),
        lax.psum_scatter(
            down_weight_grad.astype(jnp.bfloat16), ("row", "nar"), scatter_dimension=1, tiled=True
        ).astype(jnp.float32),
        lax.psum_scatter(
            gain_attn_term.astype(jnp.bfloat16), ("row", "nar"), scatter_dimension=0, tiled=True
        ).astype(jnp.float32),
        lax.psum_scatter(
            gain_ffn_term.astype(jnp.bfloat16), ("row", "nar"), scatter_dimension=0, tiled=True
        ).astype(jnp.float32),
    )
    (
        grad_query,
        key_sum,
        value_sum,
        grad_output,
        grad_gate,
        grad_up,
        grad_down,
        gain_attn_sum,
        gain_ffn_sum,
    ) = summed
    key_all, value_all, gain_attn_all, gain_ffn_all = (
        lax.all_gather(key_sum.astype(jnp.bfloat16), "wid", axis=1, tiled=True).astype(
            key_sum.dtype
        ),
        lax.all_gather(value_sum.astype(jnp.bfloat16), "wid", axis=1, tiled=True).astype(
            value_sum.dtype
        ),
        lax.all_gather(gain_attn_sum.astype(jnp.bfloat16), "wid", axis=0, tiled=True).astype(
            gain_attn_sum.dtype
        ),
        lax.all_gather(gain_ffn_sum.astype(jnp.bfloat16), "wid", axis=0, tiled=True).astype(
            gain_ffn_sum.dtype
        ),
    )
    shard_rows = key_sum.shape[0]
    repeats = wid_count * kv_local // KV
    grad_key = key_all.reshape(shard_rows, KV, repeats, HD).sum(axis=2).reshape(shard_rows, KV * HD)
    grad_value = (
        value_all.reshape(shard_rows, KV, repeats, HD).sum(axis=2).reshape(shard_rows, KV * HD)
    )
    grad_gain_attn = gain_attn_all.reshape(wid_count, shard_rows).sum(axis=0)
    grad_gain_ffn = gain_ffn_all.reshape(wid_count, shard_rows).sum(axis=0)
    return (
        hidden_out,
        grad_in,
        grad_query,
        grad_key,
        grad_value,
        grad_output,
        grad_gate,
        grad_up,
        grad_down,
        grad_gain_attn,
        grad_gain_ffn,
    )


MESH = pl.DeviceIdType.MESH
bf16 = jnp.bfloat16
f32 = jnp.float32
VMEM_LIMIT = 60 * 2**20


def spot():
    return lax.axis_index("row"), lax.axis_index("nar"), lax.axis_index("wid")


def greet(partners):
    barrier = pltpu.get_barrier_semaphore()
    total = 0
    for there, device in partners:
        @pl.when(there)
        def _():
            pl.semaphore_signal(barrier, inc=1, device_id=device, device_id_type=MESH)

        total = total + there.astype(jnp.int32)
    pl.semaphore_wait(barrier, total)


def line_partners(r, n, w, wid_count):
    return [
        (w < wid_count - 1, (r, n, jnp.minimum(w + 1, wid_count - 1))),
        (w > 0, (r, n, jnp.maximum(w - 1, 0))),
        (w >= 0, (1 - r, n, w)),
    ]


def each_rows(count, step, body):
    def run(i, carry):
        body(pl.ds(pl.multiple_of(i * step, step), step))
        return carry

    lax.fori_loop(0, count // step, run, 0)


def square_partners(r, n, w):
    return [(n >= 0, over_x(r, n, w)), (n >= 0, over_y(r, n, w))]


def over_x(r, n, w):
    return (r, n + 1 - 2 * (n % 2), w)


def over_y(r, n, w):
    return (r, (n + 2) % 4, w)


def push(source, target, s_s, s_g, device):
    return pltpu.make_async_remote_copy(
        source, target, s_s, s_g, device_id=device, device_id_type=MESH
    )


class Square:
    def __init__(self, shard, full, sems, me):
        self.shard, self.full = shard, full
        self.sent, self.got = sems
        r, n, w = me
        self.n, self.x, self.y = n, n + 1 - 2 * (n % 2), (n + 2) % 4
        self.by_x, self.by_y = over_x(*me), over_y(*me)
        size = shard.shape[0] // 2
        self.upper, self.lower = pl.ds(0, size), pl.ds(size, size)

    def first(self, k, place):
        return push(
            self.shard, self.full.at[place], self.sent.at[k], self.got.at[k],
            (self.by_x, self.by_y)[k],
        )

    def second(self, k, place):
        part = self.full.at[place, (self.upper, self.lower)[k]]
        return push(
            part, part, self.sent.at[2 + k], self.got.at[2 + k], (self.by_y, self.by_x)[k]
        )

    def start(self):
        self.first(0, self.n).start()
        self.first(1, self.n).start()

    def turn(self):
        self.first(0, self.x).wait_recv()
        self.second(0, self.x).start()
        self.first(1, self.y).wait_recv()
        self.second(1, self.y).start()

    def finish(self):
        for k in range(2):
            self.second(k, 3 - self.n).wait_recv()
            self.first(k, self.n).wait_send()
            self.second(k, (self.x, self.y)[k]).wait_send()


def square_sems():
    return [pltpu.SemaphoreType.DMA((4,))] * 2


def fetch(own, full, target, sems, n):
    copies = [pltpu.make_async_copy(own, target.at[n], sems.at[0])]
    for k, place in enumerate((n + 1 - 2 * (n % 2), (n + 2) % 4, 3 - n)):
        copies.append(pltpu.make_async_copy(full.at[place], target.at[place], sems.at[1 + k]))
    return copies


class Gather:
    def __init__(self, buf, sems, me, wid_count, rows=slice(None), pair=True):
        self.rows, self.both = rows, pair
        self.buf, (self.up_s, self.dn_s, self.pt_s, self.got) = buf, sems
        self.r, self.n, self.w = me
        self.last = wid_count - 1
        self.up = (self.r, self.n, jnp.minimum(self.w + 1, self.last))
        self.dn = (self.r, self.n, jnp.maximum(self.w - 1, 0))
        self.pt = (1 - self.r, self.n, self.w)

    def copy(self, j, sem, device, row=None):
        row = (self.r if self.both else 0) if row is None else row
        return pltpu.make_async_remote_copy(
            self.buf.at[row, j, self.rows],
            self.buf.at[row, j, self.rows],
            sem.at[j],
            self.got.at[row, j],
            device_id=device,
            device_id_type=MESH,
        )

    def pass_on(self, j, go_up, go_dn):
        if go_up:
            @pl.when(self.w < self.last)
            def _():
                self.copy(j, self.up_s, self.up).start()

        if go_dn:
            @pl.when(self.w > 0)
            def _():
                self.copy(j, self.dn_s, self.dn).start()

        if self.both:
            self.copy(j, self.pt_s, self.pt).start()

    def own(self):
        self.pass_on(self.w, True, True)

    def arrive(self, row, j):
        self.copy(j, self.pt_s, self.pt, row).wait_recv()

    def step(self, k):
        below, above = self.w - k, self.w + k

        @pl.when(below >= 0)
        def _():
            self.arrive(None, below)
            self.pass_on(below, True, False)

        @pl.when(above <= self.last)
        def _():
            self.arrive(None, above)
            self.pass_on(above, False, True)

    def advance(self, edge_steps, inner_steps):
        at_end = (self.w == 0) | (self.w == self.last)
        for ends, steps in ((True, edge_steps), (False, inner_steps)):
            if steps:
                @pl.when(at_end if ends else jnp.logical_not(at_end))
                def _():
                    for k in steps:
                        self.step(k)

    def rest(self):
        for j in range(self.last + 1):
            self.arrive(1 - self.r, j)

    def sent(self):
        for j in range(self.last + 1):
            @pl.when((j <= self.w) & (self.w < self.last))
            def _():
                self.copy(j, self.up_s, self.up).wait_send()

            @pl.when((j >= self.w) & (self.w > 0))
            def _():
                self.copy(j, self.dn_s, self.dn).wait_send()

            if self.both:
                self.copy(j, self.pt_s, self.pt).wait_send()


def gather_scratch(shard, width):
    return [pltpu.VMEM((2, 4, shard, width), bf16)] + gather_sems()


def gather_sems():
    return [pltpu.SemaphoreType.DMA((4,))] * 3 + [pltpu.SemaphoreType.DMA((2, 4))]


class Scatter:
    def __init__(self, mine, theirs, bufs, sems, me, wid_count, first=0, count=None):
        self.mine, self.theirs = mine, theirs
        self.from_pt, self.from_up, self.from_dn = bufs
        self.pt_s, self.pt_g, self.up_s, self.up_g, self.dn_s, self.dn_g = sems
        self.r, self.n, self.w = me
        self.first, self.count = first, mine.shape[1] if count is None else count
        self.rows = pl.ds(first, self.count)
        self.last = wid_count - 1
        self.up = (self.r, self.n, jnp.minimum(self.w + 1, self.last))
        self.dn = (self.r, self.n, jnp.maximum(self.w - 1, 0))
        self.pt = (1 - self.r, self.n, self.w)

    def order(self, i):
        low = jnp.where(i == 0, 3, jnp.where(i == 1, 0, jnp.where(i == 2, 2, 1)))
        return jnp.where(self.w < 2, low, 3 - low)

    def send(self, source, target, sent, got, s, device):
        return pltpu.make_async_remote_copy(
            source.at[s, self.rows], target.at[s, self.rows], sent.at[s], got.at[s],
            device_id=device, device_id_type=MESH,
        )

    def pair(self, s):
        return self.send(self.theirs, self.from_pt, self.pt_s, self.pt_g, s, self.pt)

    def climb(self, s):
        return self.send(self.mine, self.from_dn, self.up_s, self.up_g, s, self.up)

    def fall(self, s):
        return self.send(self.mine, self.from_up, self.dn_s, self.dn_g, s, self.dn)

    def each(self, body):
        def run(i, carry):
            body(pl.ds(pl.multiple_of(self.first + i * 16, 16), 16))
            return carry

        lax.fori_loop(0, self.count // 16, run, 0)

    def add(self, s, others):
        def body(rows):
            total = self.mine[s, rows, :].astype(f32)
            for other in others:
                total = total + other[s, rows, :].astype(f32)
            self.mine[s, rows, :] = total.astype(bf16)

        self.each(body)

    def step(self, s):
        self.pair(s).wait_recv()

        @pl.when((s > self.w) & (self.w > 0))
        def _():
            self.climb(s).wait_recv()
            self.add(s, (self.from_pt, self.from_dn))

        @pl.when((s < self.w) & (self.w < self.last))
        def _():
            self.fall(s).wait_recv()
            self.add(s, (self.from_pt, self.from_up))

        @pl.when(((s > self.w) & (self.w == 0)) | ((s < self.w) & (self.w == self.last)))
        def _():
            self.add(s, (self.from_pt,))

        @pl.when(s > self.w)
        def _():
            self.climb(s).start()

        @pl.when(s < self.w)
        def _():
            self.fall(s).start()

    def advance(self, edge_steps, inner_steps):
        for ends, steps in ((True, edge_steps), (False, inner_steps)):
            at_end = (self.w == 0) | (self.w == self.last)

            def body(i, carry):
                self.step(self.order(i))
                return carry

            if steps:
                @pl.when(at_end if ends else jnp.logical_not(at_end))
                def _():
                    lax.fori_loop(steps[0], steps[-1] + 1, body, 0)

    def total(self, out):
        w = self.w

        def first(rows):
            out[rows, :] = self.mine[w, rows, :].astype(f32) + self.from_pt[w, rows, :].astype(f32)

        self.each(first)

        @pl.when(w > 0)
        def _():
            self.climb(w).wait_recv()

            def more(rows):
                out[rows, :] += self.from_dn[w, rows, :].astype(f32)

            self.each(more)

        @pl.when(w < self.last)
        def _():
            self.fall(w).wait_recv()

            def more(rows):
                out[rows, :] += self.from_up[w, rows, :].astype(f32)

            self.each(more)

    def sent(self):
        for s in range(self.last + 1):
            self.pair(s).wait_send()

            @pl.when(s > self.w)
            def _():
                self.climb(s).wait_send()

            @pl.when(s < self.w)
            def _():
                self.fall(s).wait_send()


def scatter_bufs(shard, width):
    return [pltpu.VMEM((4, shard, width), bf16)] * 3


def scatter_sems():
    return [pltpu.SemaphoreType.DMA((4,))] * 6


def vmem():
    return pl.BlockSpec(memory_space=pltpu.VMEM)


def hbm():
    return pl.BlockSpec(memory_space=pl.ANY)


def comm_call(kernel, name, cid, out_shape, in_specs, out_specs, scratch, args, flops=0, sent=0):
    return pl.pallas_call(
        kernel,
        out_shape=out_shape,
        in_specs=in_specs,
        out_specs=out_specs,
        scratch_shapes=scratch,
        compiler_params=pltpu.CompilerParams(
            collective_id=cid, has_side_effects=True, vmem_limit_bytes=VMEM_LIMIT
        ),
        cost_estimate=pl.CostEstimate(flops=flops, bytes_accessed=sent, transcendentals=0),
        name=name,
    )(*args)


def norm_rows(x, gain):
    root = lax.rsqrt(jnp.mean(x * x, axis=-1, keepdims=True) + norm_eps)
    return x * root * gain


def turn(x, cosine, sine):
    lane = lax.broadcasted_iota(jnp.int32, x.shape, 1)
    swapped = jnp.where(lane % 64 < 32, pltpu.roll(x, 96, 1), pltpu.roll(x, 32, 1))
    return x * cosine + swapped * sine


def enter_kernel(
    hidden, gain, tab, p1_own, down_own, rows_out, tabs_out, p1_out, down_out,
    buf, up_s, dn_s, pt_s, got, tabs, tab_s, tab_g, out_s, p1_s, p1_g, down_s, down_g, p1_here, here_s,
):
    me = spot()
    r, n, w = me
    bring = pltpu.make_async_copy(p1_own, p1_here, here_s.at[0])
    bring.start()
    greet(line_partners(r, n, w, 4) + square_partners(r, n, w))
    p1 = Square(p1_own, p1_out, (p1_s, p1_g), me)
    down = Square(down_own.at[0:256], down_out, (down_s, down_g), me)
    p1.start()
    down.start()
    gather = Gather(buf, (up_s, dn_s, pt_s, got), me, 4)
    tab_copy = pltpu.make_async_remote_copy(
        tab, tabs.at[r], tab_s, tab_g, device_id=(1 - r, n, w), device_id_type=MESH
    )

    def body(rows):
        buf[r, w, rows, :] = norm_rows(hidden[rows, :].astype(f32), gain[...]).astype(bf16)

    each_rows(hidden.shape[0], 16, body)
    gather.own()
    tab_copy.start()

    def keep(rows):
        tabs[r, rows, :] = tab[rows, :]

    each_rows(tab.shape[0], 16, keep)
    bring.wait()
    settle = pltpu.make_async_copy(p1_here, p1_out.at[n], here_s.at[1])
    settle.start()
    gather.step(1)
    p1.turn()
    gather.step(2)
    down.turn()
    gather.step(3)
    gather.rest()
    out = pltpu.make_async_copy(buf, rows_out, out_s.at[0])
    out.start()
    tab_copy.wait_recv()
    out_tab = pltpu.make_async_copy(tabs, tabs_out, out_s.at[1])
    out_tab.start()
    gather.sent()
    p1.finish()
    down.finish()
    settle.wait()
    tab_copy.wait_send()
    out.wait()
    out_tab.wait()


def enter(hidden, gain, tab, p1_own, down_own):
    shard, width = hidden.shape
    return comm_call(
        enter_kernel, "enter", 1,
        (
            jax.ShapeDtypeStruct((2, 4, shard, width), bf16),
            jax.ShapeDtypeStruct((2,) + tab.shape, f32),
            jax.ShapeDtypeStruct((4,) + p1_own.shape, bf16),
            jax.ShapeDtypeStruct((4, 256, 1024), bf16),
        ),
        [vmem()] * 3 + [hbm()] * 2, [hbm()] * 4,
        gather_scratch(shard, width)
        + [
            pltpu.VMEM((2,) + tab.shape, f32),
            pltpu.SemaphoreType.DMA(()),
            pltpu.SemaphoreType.DMA(()),
            pltpu.SemaphoreType.DMA((2,)),
        ]
        + square_sems() * 2
        + [pltpu.VMEM(p1_own.shape, bf16), pltpu.SemaphoreType.DMA((2,))],
        (hidden, gain, tab, p1_own, down_own), flops=10**10, sent=10**8,
    )


def nar_device(r, n, w, by):
    return (r, jnp.clip(n + by, 0, 3), w)


def project_kernel(
    x, p1, tabs, grad_top, q_out, kv_out, tops_out, kv, s_s, s_g, out_s, buf, g0, g1, g2, g3, tops_s
):
    r, n, w = spot()
    greet(
        line_partners(r, n, w, 4)
        + [
            (n >= 1, nar_device(r, n, w, -1)),
            (n >= 2, nar_device(r, n, w, -2)),
            (n <= 2, nar_device(r, n, w, 1)),
            (n <= 1, nar_device(r, n, w, 2)),
        ]
    )
    gather = Gather(buf, (g0, g1, g2, g3), (r, n, w), 4)

    def keep(rows):
        buf[r, w, rows, :] = grad_top[rows, :]

    each_rows(64, 16, keep)
    gather.own()

    def copy(row, slot, by):
        return pltpu.make_async_remote_copy(
            kv.at[row, 2], kv.at[row, slot], s_s.at[row, slot], s_g.at[row, slot],
            device_id=nar_device(r, n, w, by), device_id_type=MESH,
        )

    lane = lax.broadcasted_iota(jnp.int32, (256, 128), 1)
    weight = p1[:, :, 0:384].reshape(2048, 384)
    for row in range(2):
        def tile(i, carry):
            rows = pl.ds(pl.multiple_of(i * 256, 256), 256)
            cosine, sine = tabs[row, rows, 0:128], tabs[row, rows, 128:256]
            pre = jnp.dot(x[row, rows, :], weight, preferred_element_type=f32)
            q_out[row, rows, 0:128] = turn(pre[:, 0:128], cosine, sine).astype(bf16)
            q_out[row, rows, 128:256] = turn(pre[:, 128:256], cosine, sine).astype(bf16)
            both = pre[:, 256:384]
            kv[row, 2, rows, :] = jnp.where(lane < 64, turn(both, cosine, sine), both).astype(bf16)
            return carry

        lax.fori_loop(0, 2, tile, 0)

        @pl.when(n <= 2)
        def _():
            copy(row, 1, 1).start()

        @pl.when(n <= 1)
        def _():
            copy(row, 0, 2).start()

        for slot, least in ((1, 1), (0, 2)):
            @pl.when(n < least)
            def _():
                kv[row, slot] = jnp.zeros((512, 128), bf16)

    for k in (1, 2, 3):
        gather.step(k)
    gather.rest()
    tops_copy = pltpu.make_async_copy(buf, tops_out, tops_s)
    tops_copy.start()
    for row in range(2):
        for slot, least, by in ((1, 1, 1), (0, 2, 2)):
            @pl.when(n >= least)
            def _():
                copy(row, slot, by).wait_recv()

    out = pltpu.make_async_copy(kv, kv_out, out_s)
    out.start()
    for row in range(2):
        @pl.when(n <= 2)
        def _():
            copy(row, 1, 1).wait_send()

        @pl.when(n <= 1)
        def _():
            copy(row, 0, 2).wait_send()

    gather.sent()
    out.wait()
    tops_copy.wait()


def project(x, p1, tabs, grad_top):
    return comm_call(
        project_kernel, "project", 2,
        (
            jax.ShapeDtypeStruct((2, 512, 256), bf16),
            jax.ShapeDtypeStruct((2, 3, 512, 128), bf16),
            jax.ShapeDtypeStruct((2, 4, 64, 2048), bf16),
        ),
        [vmem()] * 4, [vmem(), hbm(), hbm()],
        [
            pltpu.VMEM((2, 3, 512, 128), bf16),
            pltpu.SemaphoreType.DMA((2, 3)),
            pltpu.SemaphoreType.DMA((2, 3)),
            pltpu.SemaphoreType.DMA(()),
        ]
        + gather_scratch(64, 2048)
        + [pltpu.SemaphoreType.DMA(())],
        (x, p1, tabs, grad_top), flops=10**10, sent=10**7,
    )


KEYS = 256
QUERIES = 128


def stack_low(x):
    lane = lax.broadcasted_iota(jnp.int32, (QUERIES, 128), 1)
    zero = jnp.zeros((QUERIES, 128), x.dtype)
    parts = []
    for pair in range(2):
        block = x[:, pair * 128 : pair * 128 + 128]
        parts.append(jnp.where(lane < 64, block, zero))
        parts.append(jnp.where(lane < 64, pltpu.roll(block, 64, 1), zero))
    return jnp.concatenate(parts, axis=0)


def stack_high(x):
    lane = lax.broadcasted_iota(jnp.int32, (QUERIES, 128), 1)
    zero = jnp.zeros((QUERIES, 128), x.dtype)
    parts = []
    for pair in range(2):
        block = x[:, pair * 128 : pair * 128 + 128]
        parts.append(jnp.where(lane >= 64, pltpu.roll(block, 64, 1), zero))
        parts.append(jnp.where(lane >= 64, block, zero))
    return jnp.concatenate(parts, axis=0)


def unstack(x, low):
    lane = lax.broadcasted_iota(jnp.int32, (QUERIES, 128), 1)
    out = []
    for pair in range(2):
        even = x[2 * pair * QUERIES : (2 * pair + 1) * QUERIES]
        odd = x[(2 * pair + 1) * QUERIES : (2 * pair + 2) * QUERIES]
        if low:
            out.append(jnp.where(lane < 64, even, pltpu.roll(odd, 64, 1)))
        else:
            out.append(jnp.where(lane < 64, pltpu.roll(even, 64, 1), odd))
    return jnp.concatenate(out, axis=1)


def allowed_tile(starts, tile, first_query):
    key = lax.broadcasted_iota(jnp.int32, (QUERIES, KEYS), 1) + tile * KEYS
    query = lax.broadcasted_iota(jnp.int32, (QUERIES, KEYS), 0) + first_query
    start = jnp.concatenate([starts] * (KEYS // 128), axis=1)
    ok = (key <= query) & (key.astype(f32) >= start)
    return jnp.concatenate([ok] * 4, axis=0)


def attend_block(q, kv, starts, first_query):
    query = stack_low(q.astype(f32)).astype(bf16)

    def body(step, carry):
        tile = (first_query - 1024) // KEYS + step
        top, total, acc = carry
        both = kv[pl.ds(pl.multiple_of(tile * KEYS, KEYS), KEYS), :]
        scores = contract_last(query, both) * 0.125
        ok = allowed_tile(starts, tile, first_query)
        scores = jnp.where(ok, scores, masked_score)
        new_top = jnp.maximum(top, jnp.max(scores, axis=1, keepdims=True))
        shrink = jnp.exp(top - new_top)
        part = jnp.exp(scores - new_top)
        total = total * shrink + jnp.sum(part, axis=1, keepdims=True)
        acc = acc * shrink + jnp.dot(part.astype(bf16), both, preferred_element_type=f32)
        return new_top, total, acc

    top, total, acc = lax.fori_loop(
        0, 5, body,
        (
            jnp.full((4 * QUERIES, 1), masked_score, f32),
            jnp.zeros((4 * QUERIES, 1), f32),
            jnp.zeros((4 * QUERIES, 128), f32),
        ),
        unroll=True,
    )
    logsum = jnp.broadcast_to(top + jnp.log(total), (4 * QUERIES, 128))
    return unstack(acc / total, False).astype(bf16), logsum


def out_block(p1, nn, half):
    return p1[nn, half * 256 : half * 256 + 256, 384:640]


def middle_kernel(
    q, kv, tabs, p1, hidden, gain, gate_own, up_own, down_own,
    att, lse, mid_out, ffn_out, gate_out, up_out, down_out,
    theirs, mine, from_pt, from_up, from_dn, s0, s1, s2, s3, s4, s5, fbuf, h0, h1, h2, h3, out_s,
    gate_s, gate_g, up_s, up_g, down_s, down_g,
):
    me = spot()
    r, n, w = me
    greet(line_partners(r, n, w, 4) + square_partners(r, n, w))
    gate = Square(gate_own, gate_out, (gate_s, gate_g), me)
    up = Square(up_own, up_out, (up_s, up_g), me)
    gate.start()
    up.start()
    down = Square(down_own.at[256:512], down_out, (down_s, down_g), me)
    down.start()
    scatter = Scatter(
        mine, theirs, (from_pt, from_up, from_dn), (s0, s1, s2, s3, s4, s5), me, 4
    )
    ffn = Gather(fbuf, (h0, h1, h2, h3), me, 4)
    def shard(i, carry):
        s = scatter.order(i)
        rows = pl.ds(pl.multiple_of(s * 128, 128), 128)
        for row in range(2):
            att[row, rows, :], lse[row, s] = attend_block(
                q[row, rows, :], kv.at[row], tabs[row, rows, 256:384], 1024 + s * 128
            )

        @pl.when((i >= 1) & ((w == 0) | (w == 3)))
        def _():
            scatter.step(scatter.order(i - 1))

        left = jnp.concatenate([att[1 - r, rows, :], att[r, rows, :]], axis=0)
        for nn in range(4):
            for half in range(2):
                part = jnp.dot(left, out_block(p1, nn, half), preferred_element_type=f32).astype(bf16)
                columns = slice(nn * 512 + half * 256, nn * 512 + half * 256 + 256)
                theirs[s, :, columns] = part[0:128]
                mine[s, :, columns] = part[128:256]
        scatter.pair(s).start()
        return carry

    lax.fori_loop(0, 4, shard, 0)
    scatter.advance((3,), (0, 1, 2, 3))
    scatter.total(mid_out)

    def body(rows):
        middle = mid_out[rows, :] + hidden[rows, :].astype(f32)
        mid_out[rows, :] = middle
        fbuf[r, w, rows, :] = norm_rows(middle, gain[...]).astype(bf16)

    each_rows(hidden.shape[0], 16, body)
    ffn.own()
    gate.turn()
    up.turn()
    ffn.step(1)
    down.turn()
    ffn.step(2)
    ffn.step(3)
    ffn.rest()
    out_f = pltpu.make_async_copy(fbuf, ffn_out, out_s)
    out_f.start()
    scatter.sent()
    ffn.sent()
    gate.finish()
    up.finish()
    down.finish()
    out_f.wait()


def middle_stage(q, kv, tabs, p1, hidden, gain, *weights):
    shard, width = hidden.shape
    rows = jax.ShapeDtypeStruct((2, 4, shard, width), bf16)
    return comm_call(
        middle_kernel, "middle", 3,
        (
            jax.ShapeDtypeStruct((2, 512, 256), bf16),
            jax.ShapeDtypeStruct((2, 4, 4 * QUERIES, 128), f32),
            jax.ShapeDtypeStruct((shard, width), f32),
            rows,
        )
        + (jax.ShapeDtypeStruct((4, 512, 1024), bf16),) * 2
        + (jax.ShapeDtypeStruct((4, 256, 1024), bf16),),
        [vmem()] * 6 + [hbm()] * 3, [vmem()] * 3 + [hbm()] * 4,
        [pltpu.VMEM((4, shard, width), bf16)] * 2
        + scatter_bufs(shard, width) + scatter_sems()
        + gather_scratch(shard, width)
        + [pltpu.SemaphoreType.DMA(())]
        + square_sems() * 3,
        (q, kv, tabs, p1, hidden, gain, *weights), flops=10**10, sent=2 * 10**8,
    )


class Spread:
    def __init__(self, outs, sems, me):
        self.a_send, self.a_keep, self.b_send, self.b_keep = outs
        self.r, self.n, self.w = me
        self.give_s, self.give_g, self.keep_s = sems

    def copies(self, wide, row, place, give):
        for k in range(4):
            block = wide.at[self.n ^ k]
            for part in range(2):
                source = block.at[pl.ds(part * 128, 128)]
                if part == 0:
                    target = (self.a_send if k & 1 else self.a_keep).at[k >> 1]
                else:
                    target = (self.b_send if k >= 2 else self.b_keep).at[k & 1]
                target = place(target)
                at = k * 2 + part
                if give:
                    yield pltpu.make_async_remote_copy(
                        source, target, self.give_s.at[row, at], self.give_g.at[row, at],
                        device_id=(1 - self.r, self.n, self.w), device_id_type=MESH,
                    )
                else:
                    yield pltpu.make_async_copy(source, target, self.keep_s.at[row, at])

    def start(self, *args):
        for copy in self.copies(*args):
            copy.start()

    def wait_send(self, *args):
        for copy in self.copies(*args):
            copy.wait_send()

    def wait_recv(self, *args):
        for copy in self.copies(*args):
            copy.wait_recv()

    def wait(self, *args):
        for copy in self.copies(*args):
            copy.wait()


def spread_sems(count):
    return [pltpu.SemaphoreType.DMA((count, 8))] * 3


def ffn_kernel(
    x, tops_in, grad_top, gate_own, gate_in, up_own, up_in, down_own, down_a, down_b, gain,
    part_out, sum_out, gain_out, o0, o1, o2, o3, ra_out, rb_out,
    theirs, mine, from_pt, from_up, from_dn, s0, s1, s2, s3, s4, s5,
    act, dgu, wide, out_s, give_s, give_g, keep_s, p2, in_s, n_s, n_g,
    tops4, h0, h1, h2, h3, tops_s,
):
    me = spot()
    r, n, w = me
    loads = [
        fetch(gate_own, gate_in, p2.at[0], in_s.at[0], n),
        fetch(up_own, up_in, p2.at[1], in_s.at[1], n),
        fetch(down_own.at[0:256], down_a, p2.at[2, :, 0:256], in_s.at[2], n)
        + fetch(down_own.at[256:512], down_b, p2.at[2, :, 256:512], in_s.at[3], n),
        [pltpu.make_async_copy(tops_in, tops4.at[:, :, 0:64], tops_s)],
    ]
    for group in loads:
        for load in group:
            load.start()

    def loaded(k):
        for load in loads[k]:
            load.wait()

    greet(line_partners(r, n, w, 4) + square_partners(r, n, w))
    scatter = Scatter(
        mine, theirs, (from_pt, from_up, from_dn), (s0, s1, s2, s3, s4, s5), me, 4
    )
    late = pl.ds(64, 64)
    gather = Gather(tops4, (h0, h1, h2, h3), me, 4, late)

    def keep(rows):
        tops4[r, w, pl.ds(64 + rows.start, 16), :] = grad_top[pl.ds(64 + rows.start, 16), :]

    each_rows(64, 16, keep)
    gather.own()
    gain_out[...] = jnp.zeros_like(gain_out)
    loaded(0)
    loaded(1)

    def hidden_tile(i, carry):
        ft, row = i // 2, i % 2
        rows = pl.ds(pl.multiple_of(row * 512, 512), 512)
        columns = pl.ds(pl.multiple_of(ft * 256, 256), 256)
        left = x[rows, :]
        gate = jnp.dot(left, p2[0, :, :, columns].reshape(2048, 256), preferred_element_type=f32)
        up = jnp.dot(left, p2[1, :, :, columns].reshape(2048, 256), preferred_element_type=f32)
        sig = 1.0 / (1.0 + jnp.exp(-gate))
        silu = gate * sig
        act[rows, columns] = (silu * up).astype(bf16)
        dgu[rows, columns] = (up * (sig * (1.0 + gate * (1.0 - sig)))).astype(bf16)
        later = pl.ds(pl.multiple_of(1024 + ft * 256, 256), 256)
        dgu[rows, later] = silu.astype(bf16)
        return carry

    lax.fori_loop(0, 4, hidden_tile, 0)
    gather.step(1)
    lax.fori_loop(4, 8, hidden_tile, 0)
    gather.step(2)
    loaded(2)

    def down_tile(dt, carry):
        nn, half = dt // 2, dt % 2
        columns = pl.ds(pl.multiple_of(dt * 256, 256), 256)
        inner = pl.ds(pl.multiple_of(half * 256, 256), 256)
        other = pl.ds(pl.multiple_of(512 + half * 256, 256), 256)
        right = jnp.concatenate([p2[2, nn, :, inner], p2[2, nn, :, other]], axis=0)
        for row, stage in ((0, theirs), (1, mine)):
            part = jnp.dot(act[row * 512 : row * 512 + 512, :], right, preferred_element_type=f32)
            stage[:, :, columns] = part.astype(bf16).reshape(4, 128, 256)
        return carry

    lax.fori_loop(0, 8, down_tile, 0)
    puts = [
        pltpu.make_async_copy(theirs, part_out.at[0], out_s.at[0]),
        pltpu.make_async_copy(mine, part_out.at[1], out_s.at[1]),
    ]
    for put in puts:
        put.start()
    gather.step(3)
    gather.rest()
    loaded(3)

    def top_rows(row):
        return tops4[row].reshape(512, 2048)

    def back_tile(ft, carry):
        columns = pl.ds(pl.multiple_of(ft * 256, 256), 256)
        f_rows = pl.ds(pl.multiple_of((ft % 2) * 256, 256), 256)
        f_cols = pl.ds(pl.multiple_of((ft // 2) * 512, 512), 512)
        later = pl.ds(pl.multiple_of(1024 + ft * 256, 256), 256)
        right = jnp.concatenate([p2[2, nn, f_rows, f_cols] for nn in range(4)], axis=1)
        for row in range(2):
            rows = slice(row * 512, row * 512 + 512)
            dact = contract_last(top_rows(row), right)
            dgu[rows, columns] = (dact * dgu[rows, columns].astype(f32)).astype(bf16)
            dgu[rows, later] = (dact * dgu[rows, later].astype(f32)).astype(bf16)
        return carry

    lax.fori_loop(0, 4, back_tile, 0)
    for put in puts:
        put.wait()

    spread = Spread((o0, o1, o2, o3), (give_s, give_g, keep_s), me)
    columns_here = pl.ds(pl.multiple_of(r * 1024, 1024), 1024)
    slots = {2: 0, 0: 1, 1: 0}

    def moved(which, half):
        def place(target):
            return target.at[which, :, columns_here]

        return wide.at[slots[which], half], which, place, half == 0

    def weights(which, between=None):
        for half in range(2):
            d_first = (jnp.where(half == 0, 1 - r, r)) * 1024

            def weight_tile(i, carry):
                d_cols = pl.ds(pl.multiple_of(d_first + i * 256, 256), 256)
                if which < 2:
                    left = x[:, d_cols]
                    right = dgu[:, which * 1024 : which * 1024 + 1024]
                else:
                    left = tops4[:, :, :, d_cols].reshape(1024, 256)
                    right = act[...]
                wide[slots[which], half, i] = contract_first(left, right).astype(bf16)
                return carry

            lax.fori_loop(0, 4, weight_tile, 0)
            spread.start(*moved(which, half))
            if half == 0 and between is not None:
                between()

    def hop(which, at):
        return (
            push(o0.at[:, which], ra_out.at[at], n_s.at[0, at], n_g.at[0, at], over_x(r, n, w)),
            push(o2.at[:, which], rb_out.at[at], n_s.at[1, at], n_g.at[1, at], over_y(r, n, w)),
        )

    hops = hop(2, 0) + hop(0, 1)
    weights(2)
    for i in range(4):
        s = scatter.order(i)
        rows_t = pl.ds(pl.multiple_of((1 - r) * 512 + s * 128, 128), 128)
        rows_m = pl.ds(pl.multiple_of(r * 512 + s * 128, 128), 128)

        def model_tile(dt, carry):
            nn, half = dt // 2, dt % 2
            columns = pl.ds(pl.multiple_of(dt * 256, 256), 256)
            inner = pl.ds(pl.multiple_of(half * 256, 256), 256)
            left = jnp.concatenate([dgu[rows_t, :], dgu[rows_m, :]], axis=0)
            right = jnp.concatenate([p2[0, nn, inner, :], p2[1, nn, inner, :]], axis=1)
            part = contract_last(left, right)
            seen = jnp.concatenate([x[rows_t, columns], x[rows_m, columns]], axis=0)
            terms = part * seen.astype(f32)
            gain_out[:, columns] += jnp.sum(terms.reshape(32, 8, 256), axis=0)
            part = part.astype(bf16)
            theirs[s, :, columns] = part[0:128]
            mine[s, :, columns] = part[128:256]
            return carry

        lax.fori_loop(0, 8, model_tile, 0)
        scatter.pair(s).start()
        if i < 2:
            which = (2, 0)[i]
            spread.wait_recv(*moved(which, 0))
            spread.wait(*moved(which, 1))
            hops[2 * i].start()
            hops[2 * i + 1].start()
        if i == 0:
            weights(0)
            scatter.advance((0,), ())
        elif i > 1:
            scatter.advance((i - 1,), (i - 2,))

    def scale(rows):
        gain_out[rows, :] = gain_out[rows, :] / gain[...]

    each_rows(8, 8, scale)
    spread.wait_send(*moved(2, 0))
    weights(1, lambda: scatter.advance((3,), (2,)))
    scatter.advance((), (3,))
    scatter.total(sum_out)
    scatter.sent()
    gather.sent()
    spread.wait_send(*moved(0, 0))
    spread.wait_recv(*moved(1, 0))
    spread.wait_send(*moved(1, 0))
    spread.wait(*moved(1, 1))
    for hop in hops:
        hop.wait()


def spread_shapes(*dims):
    return (jax.ShapeDtypeStruct((2,) + dims, bf16),) * 4


def ffn_stage(*args):
    shard, width = 128, 2048
    return comm_call(
        ffn_kernel, "ffn", 4,
        (
            jax.ShapeDtypeStruct((2, 4, shard, width), bf16),
            jax.ShapeDtypeStruct((shard, width), f32),
            jax.ShapeDtypeStruct((8, width), f32),
        )
        + spread_shapes(3, 128, width)
        + (jax.ShapeDtypeStruct((2, 2, 128, width), bf16),) * 2,
        [vmem(), hbm(), vmem()] + [hbm()] * 7 + [vmem()], [hbm(), vmem(), vmem()] + [hbm()] * 6,
        [pltpu.VMEM((4, shard, width), bf16)] * 2
        + scatter_bufs(shard, width) + scatter_sems()
        + [
            pltpu.VMEM((1024, 1024), bf16),
            pltpu.VMEM((1024, 2048), bf16),
            pltpu.VMEM((2, 2, 4, 256, 1024), bf16),
            pltpu.SemaphoreType.DMA((2,)),
        ]
        + spread_sems(3)
        + [pltpu.VMEM((3, 4, 512, 1024), bf16), pltpu.SemaphoreType.DMA((4, 4))]
        + [pltpu.SemaphoreType.DMA((2, 2))] * 2
        + gather_scratch(shard, width)
        + [pltpu.SemaphoreType.DMA(())],
        args, flops=4 * 10**10, sent=10**8,
    )


def norm_back(values, gain, grad):
    root = lax.rsqrt(jnp.mean(values * values, axis=-1, keepdims=True) + norm_eps)
    weighted = grad * gain
    inner = jnp.mean(weighted * values, axis=-1, keepdims=True)
    return root * weighted - values * (root * root * root) * inner


def branch_kernel(
    total, mid, grad_top, gain, p1, att, a_in, b_in, a_keep, b_keep, a_came, b_came,
    gmid_out, datt_out, o0, o1, o2, o3, ra_out, rb_out, la_out, lb_out,
    buf, g0, g1, g2, g3, wide, give_s, give_g, keep_s, n_s, n_g, kept, came, in_s,
):
    me = spot()
    r, n, w = me
    greet(line_partners(r, n, w, 4) + square_partners(r, n, w))
    gather = Gather(buf, (g0, g1, g2, g3), me, 4)
    hops = [
        push(a_in.at[:, 1], ra_out, n_s.at[0], n_g.at[0], over_x(r, n, w)),
        push(b_in.at[:, 1], rb_out, n_s.at[1], n_g.at[1], over_y(r, n, w)),
        push(kept.at[0], la_out, n_s.at[2], n_g.at[2], over_y(r, n, w)),
        push(kept.at[1], lb_out, n_s.at[3], n_g.at[3], over_x(r, n, w)),
    ]
    loads = []
    for j, (keep, first) in enumerate(((a_keep, a_came), (b_keep, b_came))):
        loads += [
            pltpu.make_async_copy(keep.at[1, 2], kept.at[j], in_s.at[j, 0]),
            pltpu.make_async_copy(first.at[0, 1], came.at[j], in_s.at[j, 1]),
        ]
    for load in loads:
        load.start()
    hops[0].start()
    hops[1].start()

    def body(rows):
        grad = norm_back(mid[rows, :], gain[...], total[rows, :]) + grad_top[rows, :].astype(f32)
        gmid_out[rows, :] = grad
        buf[r, w, rows, :] = grad.astype(bf16)

    each_rows(mid.shape[0], 16, body)
    gather.own()
    for load in loads:
        load.wait()
    for j in range(2):
        def join(rows):
            kept[j, rows, :] = (kept[j, rows, :].astype(f32) + came[j, rows, :].astype(f32)).astype(bf16)

        each_rows(128, 16, join)
        hops[2 + j].start()
    for k in (1, 2, 3):
        gather.step(k)
    gather.rest()
    for row in range(2):
        for pair in range(2):
            left = jnp.concatenate([buf[row, 2 * pair], buf[row, 2 * pair + 1]], axis=0)
            right = jnp.concatenate(
                [out_block(p1, nn, half) for nn in range(4) for half in range(2)], axis=1
            )
            datt_out[row, pair * 256 : pair * 256 + 256, :] = contract_last(left, right).astype(bf16)

    spread = Spread((o0, o1, o2, o3), (give_s, give_g, keep_s), me)

    def moved(half):
        def place(target):
            return target.at[:, pl.ds(pl.multiple_of(r * 256, 256), 256)]

        return wide.at[half], 0, place, half == 0

    for half in range(2):
        d_first = (jnp.where(half == 0, 1 - r, r)) * 1024

        def weight_tile(i, carry):
            columns = pl.ds(pl.multiple_of(d_first + i * 256, 256), 256)
            left = buf[:, :, :, columns].reshape(1024, 256)
            wide[half, i] = contract_first(left, att[...]).astype(bf16)
            return carry

        lax.fori_loop(0, 4, weight_tile, 0)
        spread.start(*moved(half))
    gather.sent()
    spread.wait(*moved(0))
    spread.wait(*moved(1))
    for hop in hops:
        hop.wait()


def branch_stage(*args):
    shard, width = 128, 2048
    return comm_call(
        branch_kernel, "branch", 5,
        (
            jax.ShapeDtypeStruct((shard, width), f32),
            jax.ShapeDtypeStruct((2, 512, 256), bf16),
        )
        + spread_shapes(128, 512)
        + (jax.ShapeDtypeStruct((2, 128, width), bf16),) * 2
        + (jax.ShapeDtypeStruct((128, width), bf16),) * 2,
        [vmem()] * 6 + [hbm()] * 6, [vmem(), vmem()] + [hbm()] * 8,
        gather_scratch(shard, width)
        + [pltpu.VMEM((2, 4, 256, 256), bf16)]
        + spread_sems(1)
        + [pltpu.SemaphoreType.DMA((4,))] * 2
        + [pltpu.VMEM((2, 128, width), bf16)] * 2
        + [pltpu.SemaphoreType.DMA((2, 2))],
        args, flops=10**10, sent=10**8,
    )


def unproject_kernel(
    q, kv, att, grad, lse, x, p1, tabs, gain, parts, mid, a_keep, b_keep, a_gate, b_gate, a_up, b_up, oa_in, ob_in,
    part_out, gain_out, o0, o1, o2, o3, hid_out, ra_out, rb_out, roa_out, rob_out,
    send, recv, both, wide_q, wide_kv, s_s, s_g, give_s, give_g, keep_s,
    mine, from_pt, from_up, from_dn, s0, s1, s2, s3, s4, s5,
    kept, came, acc, in_s, n_s, n_g, m_s, dkv,
):
    me = spot()
    r, n, w = me
    loads = []
    for j, (keep, gate, up) in enumerate(((a_keep, a_gate, a_up), (b_keep, b_gate, b_up))):
        loads += [
            pltpu.make_async_copy(keep.at[1, 0:2], kept.at[j], in_s.at[j, 0]),
            pltpu.make_async_copy(gate.at[1, 1], came.at[j, 0], in_s.at[j, 1]),
            pltpu.make_async_copy(up.at[1], came.at[j, 1], in_s.at[j, 2]),
        ]
    loads.append(pltpu.make_async_copy(parts.at[r], mine, m_s))
    for load in loads:
        load.start()
    greet(
        line_partners(r, n, w, 4)
        + [
            (n >= 1, nar_device(r, n, w, -1)),
            (n >= 2, nar_device(r, n, w, -2)),
            (n <= 2, nar_device(r, n, w, 1)),
            (n <= 1, nar_device(r, n, w, 2)),
        ]
        + square_partners(r, n, w)
    )
    scatter = Scatter(
        mine, parts.at[1 - r], (from_pt, from_up, from_dn), (s0, s1, s2, s3, s4, s5), me, 4
    )
    hops = [
        push(kept.at[0], ra_out, n_s.at[0], n_g.at[0], over_y(r, n, w)),
        push(kept.at[1], rb_out, n_s.at[1], n_g.at[1], over_x(r, n, w)),
        push(oa_in, roa_out, n_s.at[2], n_g.at[2], over_x(r, n, w)),
        push(ob_in, rob_out, n_s.at[3], n_g.at[3], over_y(r, n, w)),
    ]

    def copy(row, slot, by):
        return pltpu.make_async_remote_copy(
            send.at[row, slot], recv.at[row, slot], s_s.at[row, slot], s_g.at[row, slot],
            device_id=nar_device(r, n, w, by), device_id_type=MESH,
        )

    for i in range(4):
        scatter.pair(scatter.order(i)).start()
    for load in loads:
        load.wait()
    for j in range(2):
        for which in range(2):
            def join(rows):
                total = kept[j, which, rows, :].astype(f32) + came[j, which, rows, :].astype(f32)
                kept[j, which, rows, :] = total.astype(bf16)

            each_rows(128, 16, join)
        hops[j].start()
    hops[2].start()
    hops[3].start()
    scatter.advance((0, 1, 2, 3), ())

    def attention(i, carry):
        row, block = i // 4, i % 4
        first_query = 1024 + block * QUERIES
        here = pl.ds(pl.multiple_of(block * QUERIES, QUERIES), QUERIES)

        @pl.when(block == 0)
        def _():
            dkv[row] = jnp.zeros((1536, 128), f32)

        query = stack_low(q[row, here, :].astype(f32)).astype(bf16)
        grads = stack_high(grad[row, here, :].astype(f32))
        inner = jnp.sum(grads * stack_high(att[row, here, :].astype(f32)), axis=1, keepdims=True)
        grads = grads.astype(bf16)
        logsum = jnp.concatenate([lse[row, block]] * (KEYS // 128), axis=1)
        starts = tabs[row, here, 256:384]

        def key_tile(step, dq):
            tile = block // 2 + step
            rows = pl.ds(pl.multiple_of(tile * KEYS, KEYS), KEYS)
            pair = kv[row, rows, :]
            ok = allowed_tile(starts, tile, first_query)
            scores = contract_last(query, pair) * 0.125
            prob = jnp.where(ok, jnp.exp(scores - logsum), 0.0)
            grad_prob = contract_last(grads, pair)
            grad_scores = (prob * (grad_prob - inner)).astype(bf16)
            dkv[row, rows, :] += contract_first(grad_scores, query) * 0.125 + contract_first(
                prob.astype(bf16), grads
            )
            return dq + jnp.dot(grad_scores, pair, preferred_element_type=f32)

        dq = lax.fori_loop(0, 5, key_tile, jnp.zeros((4 * QUERIES, 128), f32), unroll=True)
        flat = unstack(dq, True) * 0.125
        cosine, sine = tabs[row, here, 0:128], -tabs[row, here, 128:256]
        there = pl.ds(pl.multiple_of(i * QUERIES, QUERIES), QUERIES)
        both[there, 0:128] = turn(flat[:, 0:128], cosine, sine).astype(bf16)
        both[there, 128:256] = turn(flat[:, 128:256], cosine, sine).astype(bf16)

        @pl.when(block == 3)
        def _():
            for slot, by in ((1, -1), (0, -2)):
                @pl.when(n >= -by)
                def _():
                    send[row, slot] = dkv[row, slot * 512 : slot * 512 + 512, :].astype(bf16)
                    copy(row, slot, by).start()

        @pl.when(i == 3)
        def _():
            scatter.advance((), (0,))

        return carry

    lax.fori_loop(0, 8, attention, 0)
    scatter.advance((), (1,))

    spread = Spread((o0, o1, o2, o3), (give_s, give_g, keep_s), (r, n, w))

    def moved_q(half):
        def place(target):
            return target.at[:, pl.ds(pl.multiple_of(r * 256, 256), 256)]

        return wide_q.at[half], 0, place, half == 0

    def moved_kv(half):
        def place(target):
            return target.at[:, pl.ds(pl.multiple_of(512 + r * 128, 128), 128)]

        return wide_kv.at[half], 1, place, half == 0

    def weight(half, columns, wide):
        d_first = (jnp.where(half == 0, 1 - r, r)) * 1024

        def tile(i, carry):
            d_cols = pl.ds(pl.multiple_of(d_first + i * 256, 256), 256)
            wide[half, i] = contract_first(x[:, d_cols], both[:, columns]).astype(bf16)
            return carry

        lax.fori_loop(0, 4, tile, 0)

    for half in range(2):
        weight(half, slice(0, 256), wide_q)
        spread.start(*moved_q(half))
    lane = lax.broadcasted_iota(jnp.int32, (128, 128), 1)
    for row in range(2):
        for slot, by in ((1, -1), (0, -2)):
            @pl.when(n <= 3 + by)
            def _():
                copy(row, slot, by).wait_recv()

        def tile(i, carry):
            rows = pl.ds(pl.multiple_of(i * 128, 128), 128)
            total = dkv[row, pl.ds(pl.multiple_of(1024 + i * 128, 128), 128), :]
            zero = jnp.zeros_like(total)
            total = total + jnp.where(n <= 2, recv[row, 1, rows, :].astype(f32), zero)
            total = total + jnp.where(n <= 1, recv[row, 0, rows, :].astype(f32), zero)
            turned = turn(total, tabs[row, rows, 0:128], -tabs[row, rows, 128:256])
            both[pl.ds(pl.multiple_of(row * 512 + i * 128, 128), 128), 256:384] = jnp.where(
                lane < 64, turned, total
            ).astype(bf16)
            return carry

        lax.fori_loop(0, 4, tile, 0)
    for half in range(2):
        weight(half, slice(256, 384), wide_kv)
        spread.start(*moved_kv(half))
    scatter.advance((), (2,))
    gain_out[...] = jnp.zeros_like(gain_out)

    def model_tile(dt, carry):
        nn, half = dt // 2, dt % 2
        columns = pl.ds(pl.multiple_of(dt * 256, 256), 256)
        inner = pl.ds(pl.multiple_of(half * 256, 256), 256)
        right = p1[nn, inner, 0:384]
        for row in range(2):
            for block in range(2):
                first = row * 512 + block * 256
                part = contract_last(both[first : first + 256, :], right)
                terms = part * x[first : first + 256, columns].astype(f32)
                gain_out[:, columns] += jnp.sum(terms.reshape(32, 8, 256), axis=0)
                part_out[row, 2 * block, :, columns] = part[0:128].astype(bf16)
                part_out[row, 2 * block + 1, :, columns] = part[128:256].astype(bf16)
        return carry

    lax.fori_loop(0, 8, model_tile, 0)
    gain_out[...] = gain_out[...] / gain[...]
    scatter.advance((), (3,))
    scatter.total(acc)

    def last(rows):
        hid_out[rows, :] = (acc[rows, :] + mid[rows, :]).astype(bf16)

    each_rows(128, 16, last)
    scatter.sent()
    for row in range(2):
        for slot, by in ((1, -1), (0, -2)):
            @pl.when(n >= -by)
            def _():
                copy(row, slot, by).wait_send()

    for half in range(2):
        spread.wait(*moved_q(half))
        spread.wait(*moved_kv(half))
    for hop in hops:
        hop.wait()


def unproject(*args):
    return comm_call(
        unproject_kernel, "unproject", 6,
        (
            jax.ShapeDtypeStruct((2, 4, 128, 2048), bf16),
            jax.ShapeDtypeStruct((8, 2048), f32),
        )
        + spread_shapes(128, 768)
        + (jax.ShapeDtypeStruct((128, 2048), bf16),)
        + (jax.ShapeDtypeStruct((2, 128, 2048), bf16),) * 2
        + (jax.ShapeDtypeStruct((2, 128, 512), bf16),) * 2,
        [vmem()] * 9 + [hbm(), vmem()] + [hbm()] * 8,
        [vmem(), vmem()] + [hbm()] * 4 + [vmem()] + [hbm()] * 4,
        [
            pltpu.VMEM((2, 2, 512, 128), bf16),
            pltpu.VMEM((2, 2, 512, 128), bf16),
            pltpu.VMEM((1024, 384), bf16),
            pltpu.VMEM((2, 4, 256, 256), bf16),
            pltpu.VMEM((2, 4, 256, 128), bf16),
            pltpu.SemaphoreType.DMA((2, 2)),
            pltpu.SemaphoreType.DMA((2, 2)),
        ]
        + spread_sems(2)
        + [pltpu.VMEM((4, 128, 2048), bf16)]
        + scatter_bufs(128, 2048) + scatter_sems()
        + [
            pltpu.VMEM((2, 2, 128, 2048), bf16),
            pltpu.VMEM((2, 2, 128, 2048), bf16),
            pltpu.VMEM((128, 2048), f32),
            pltpu.SemaphoreType.DMA((2, 3)),
            pltpu.SemaphoreType.DMA((4,)),
            pltpu.SemaphoreType.DMA((4,)),
            pltpu.SemaphoreType.DMA(()),
            pltpu.VMEM((2, 1536, 128), f32),
        ],
        args, flops=10**10, sent=10**7,
    )


def leave_kernel(
    parts, hidden, gain, gmid, gains, qa_send, qa_keep, qb_send, qb_keep, oa_keep, ob_keep, oa_in, ob_in,
    grad_out, ga_out, query_out, key_out, value_out, output_out,
    mine, from_pt, from_up, from_dn, s0, s1, s2, s3, s4, s5,
    acc, over_wid, summed, over_rest, w_s, w_g, t_s, t_g,
    first_q, next_q, then_q, next_o, then_o, kv, n_s, n_g, k0, k1, k2, k3, m_s,
):
    me = spot()
    r, n, w = me
    own_parts = pltpu.make_async_copy(parts.at[r], mine, m_s)
    own_parts.start()
    partners = [(w != j, (r, n, jnp.int32(j))) for j in range(4)]
    partners += [
        ((r != a) | (n != b), (jnp.int32(a), jnp.int32(b), w)) for a in range(2) for b in range(4)
    ]
    greet(partners)
    kv_gather = Gather(kv, (k0, k1, k2, k3), me, 4, pair=False)
    x_side, y_side = over_x(r, n, w), over_y(r, n, w)
    q_hops = [
        push(qa_send, first_q.at[0], n_s.at[0], n_g.at[0], x_side),
        push(qb_send, first_q.at[1], n_s.at[1], n_g.at[1], y_side),
    ]
    q_later = [
        push(next_q.at[0], then_q.at[0], n_s.at[2], n_g.at[2], y_side),
        push(next_q.at[1], then_q.at[1], n_s.at[3], n_g.at[3], x_side),
    ]
    o_hops = [
        push(next_o.at[0], then_o.at[0], n_s.at[4], n_g.at[4], y_side),
        push(next_o.at[1], then_o.at[1], n_s.at[5], n_g.at[5], x_side),
    ]
    for hop in q_hops:
        hop.start()
    scatter = Scatter(
        mine, parts.at[1 - r], (from_pt, from_up, from_dn), (s0, s1, s2, s3, s4, s5), me, 4
    )
    for i in range(4):
        scatter.pair(scatter.order(i)).start()

    def wid_copy(j, slot):
        return pltpu.make_async_remote_copy(
            gains, over_wid.at[slot], w_s.at[j], w_g.at[slot],
            device_id=(r, n, jnp.int32(j)), device_id_type=MESH,
        )

    def rest_copy(a, b, slot):
        return pltpu.make_async_remote_copy(
            summed, over_rest.at[slot], t_s.at[a * 4 + b], t_g.at[slot],
            device_id=(jnp.int32(a), jnp.int32(b), w), device_id_type=MESH,
        )

    for j in range(4):
        @pl.when(w != j)
        def _():
            wid_copy(j, w).start()

    own_parts.wait()
    scatter.advance((0, 1, 2), ())
    for j, (keep, came) in enumerate(((oa_keep, oa_in), (ob_keep, ob_in))):
        next_o[j] = (keep[1].astype(f32) + came[1].astype(f32)).astype(bf16)
        o_hops[j].start()
    summed[...] = gains[...]
    for j in range(4):
        @pl.when(w != j)
        def _():
            wid_copy(j, j).wait_recv()
            summed[...] += over_wid[j]

    for a in range(2):
        for b in range(4):
            @pl.when((r != a) | (n != b))
            def _():
                rest_copy(a, b, r * 4 + n).start()

    for j, keep in enumerate((qa_keep, qb_keep)):
        q_hops[j].wait_recv()
        next_q[j] = (keep[1].astype(f32) + first_q[j, 1].astype(f32)).astype(bf16)
        q_later[j].start()
    scatter.advance((), (0,))
    for j, keep in enumerate((qa_keep, qb_keep)):
        q_later[j].wait_recv()
        total = keep[0].astype(f32) + first_q[j, 0].astype(f32) + then_q[j].astype(f32)
        query_out[j * 128 : j * 128 + 128, :] = total[:, 0:512]
        kv[0, w, j * 128 : j * 128 + 128, :] = total[:, 512:768].astype(bf16)
    kv_gather.own()
    scatter.advance((3,), (1, 2))
    kv_gather.advance((), (1,))
    scatter.advance((), (3,))
    kv_gather.advance((), (2,))
    for j, (keep, came) in enumerate(((oa_keep, oa_in), (ob_keep, ob_in))):
        o_hops[j].wait_recv()
        output_out[j * 128 : j * 128 + 128, :] = (
            keep[0].astype(f32) + came[0].astype(f32) + then_o[j].astype(f32)
        )
    mine_block = r * 4 + n
    ga_out[0:1] = summed[pl.ds(mine_block, 1), :]
    ga_out[1:2] = summed[pl.ds(mine_block + 8, 1), :]
    for a in range(2):
        for b in range(4):
            @pl.when((r != a) | (n != b))
            def _():
                slot = a * 4 + b
                rest_copy(a, b, slot).wait_recv()
                ga_out[0:1] += over_rest[slot, pl.ds(mine_block, 1), :]
                ga_out[1:2] += over_rest[slot, pl.ds(mine_block + 8, 1), :]

    scatter.total(acc)

    def last(rows):
        grad = norm_back(hidden[rows, :].astype(f32), gain[...], acc[rows, :])
        grad_out[rows, :] = (grad + gmid[rows, :]).astype(bf16)

    each_rows(hidden.shape[0], 16, last)
    kv_gather.advance((1, 2, 3), (3,))
    lane = lax.broadcasted_iota(jnp.int32, (256, 128), 1)
    for j in range(4):
        even, odd = kv[0, j, :, 0:128].astype(f32), kv[0, j, :, 128:256].astype(f32)
        here = slice(j * 128, j * 128 + 128)
        key_out[:, here] = jnp.where(lane < 64, even, pltpu.roll(odd, 64, 1))
        value_out[:, here] = jnp.where(lane < 64, pltpu.roll(even, 64, 1), odd)
    scatter.sent()
    kv_gather.sent()
    for hop in q_hops + q_later + o_hops:
        hop.wait_send()
    for j in range(4):
        @pl.when(w != j)
        def _():
            wid_copy(j, w).wait_send()

    for a in range(2):
        for b in range(4):
            @pl.when((r != a) | (n != b))
            def _():
                rest_copy(a, b, r * 4 + n).wait_send()


def leave(*args):
    shard, width = 128, 2048
    grad = jax.ShapeDtypeStruct((256, 512), f32)
    return comm_call(
        leave_kernel, "leave", 7,
        (jax.ShapeDtypeStruct((shard, width), bf16), jax.ShapeDtypeStruct((8, 256), f32))
        + (grad,) * 4,
        [hbm()] + [vmem()] * 12, [vmem()] * 6,
        [pltpu.VMEM((4, shard, width), bf16)]
        + scatter_bufs(shard, width) + scatter_sems()
        + [
            pltpu.VMEM((shard, width), f32),
            pltpu.VMEM((4, 16, 256), f32),
            pltpu.VMEM((16, 256), f32),
            pltpu.VMEM((8, 16, 256), f32),
            pltpu.SemaphoreType.DMA((4,)),
            pltpu.SemaphoreType.DMA((4,)),
            pltpu.SemaphoreType.DMA((8,)),
            pltpu.SemaphoreType.DMA((8,)),
            pltpu.VMEM((2, 2, 128, 768), bf16),
            pltpu.VMEM((2, 128, 768), bf16),
            pltpu.VMEM((2, 128, 768), bf16),
            pltpu.VMEM((2, 128, 512), bf16),
            pltpu.VMEM((2, 128, 512), bf16),
            pltpu.VMEM((1, 4, 256, 256), bf16),
            pltpu.SemaphoreType.DMA((6,)),
            pltpu.SemaphoreType.DMA((6,)),
        ]
        + gather_sems()
        + [pltpu.SemaphoreType.DMA(())],
        args, flops=10**10, sent=10**8,
    )


def local_fast(
    hidden_in, doc_lengths, w_query, w_key, w_value, w_output, w_gate, w_up, w_down,
    gain_attn, gain_ffn, grad_out,
):
    r, n, w = spot()
    hidden, grad_top = hidden_in[0], grad_out[0]
    gain_a, gain_f = gain_attn[None], gain_ffn[None]
    def half(weight, axis):
        size = weight.shape[axis] // 2
        return lax.dynamic_slice_in_dim(weight, r * size, size, axis)

    head = (w * 2 + r) * HD
    kv_pack = jnp.concatenate(
        [lax.dynamic_slice_in_dim(w_key, head, HD, 1), lax.dynamic_slice_in_dim(w_value, head, HD, 1)],
        axis=1,
    )
    out_half = half(w_output, 0)
    p1_shard = jnp.concatenate(
        [half(w_query, 1), kv_pack, jnp.concatenate([out_half[:, :256], out_half[:, 256:]], axis=0)],
        axis=1,
    )
    down_half = half(w_down, 0)
    gate_own, up_own = half(w_gate, 1), half(w_up, 1)
    down_own = jnp.concatenate([down_half[:512], down_half[512:]], axis=1)

    token_ids = n * 512 + jnp.arange(512, dtype=jnp.int32)
    doc_start, places = doc_layout(doc_lengths[0], token_ids)
    angles = places.astype(f32)[:, None] * inverse_freq()[None, :]
    cosine, sine = jnp.cos(angles), jnp.sin(angles)
    start_here = (doc_start - (n - 2) * 512).astype(f32)
    tab = jnp.concatenate(
        [cosine] * 4 + [-sine, sine] * 2 + [jnp.broadcast_to(start_here[:, None], (512, 128))],
        axis=1,
    )

    rows, tabs, p1, down_a = enter(hidden, gain_a, tab, p1_shard, down_own)
    rows3, rows2 = rows.reshape(2, 512, 2048), rows.reshape(1024, 2048)
    q, kv, tops = project(rows3, p1, tabs, grad_top)
    kv_flat = kv.reshape(2, 1536, 128)
    att, lse, mid, ffn_rows, gate_all, up_all, down_b = middle_stage(
        q, kv_flat, tabs, p1, hidden, gain_f, gate_own, up_own, down_own
    )
    parts, total, gain_f_part, a_send, a_keep, b_send, b_keep, ra_dg, rb_dg = ffn_stage(
        ffn_rows.reshape(1024, 2048), tops, grad_top,
        gate_own, gate_all, up_own, up_all, down_own, down_a, down_b, gain_f,
    )
    gmid, datt, oa_send, oa_keep, ob_send, ob_keep, ra_u, rb_u, la_d, lb_d = branch_stage(
        total, mid, grad_top, gain_f, p1, att.reshape(1024, 256),
        a_send, b_send, a_keep, b_keep, ra_dg, rb_dg,
    )
    (
        dparts, gain_a_part, qa_send, qa_keep, qb_send, qb_keep,
        hidden_out, ra_last, rb_last, oa_came, ob_came,
    ) = unproject(
        q, kv_flat, att, datt, lse, rows2, p1, tabs, gain_a, parts, mid,
        a_keep, b_keep, ra_dg, rb_dg, ra_u, rb_u, oa_send, ob_send,
    )
    gains = jnp.concatenate(
        [gain_f_part.sum(axis=0).reshape(8, 256), gain_a_part.sum(axis=0).reshape(8, 256)], axis=0
    )
    grad_in, gain_sums, grad_query, grad_key, grad_value, output_sum = leave(
        dparts, hidden, gain_a, gmid, gains,
        qa_send, qa_keep, qb_send, qb_keep, oa_keep, ob_keep, oa_came, ob_came,
    )

    def joined(which):
        def half_rows(keep, came, last):
            return keep[0, which].astype(f32) + came.astype(f32) + last.astype(f32)

        a_came, b_came, a_last, b_last = (
            (ra_dg[1, 0], rb_dg[1, 0], ra_last[0], rb_last[0]),
            (ra_u[0], rb_u[0], ra_last[1], rb_last[1]),
            (ra_dg[0, 0], rb_dg[0, 0], la_d, lb_d),
        )[which]
        return jnp.concatenate(
            [half_rows(a_keep, a_came, a_last), half_rows(b_keep, b_came, b_last)], axis=0
        )

    return (
        hidden_out[None],
        grad_in[None],
        grad_query,
        grad_key,
        grad_value,
        output_sum.T,
        joined(0),
        joined(1),
        joined(2).T,
        gain_sums[1],
        gain_sums[0],
    )


def solution(mesh):
    in_specs = (
        P("row", ("nar", "wid"), None),
        P("row", None),
        P("nar", "wid"),
        P("nar", None),
        P("nar", None),
        P("wid", "nar"),
        P("nar", "wid"),
        P("nar", "wid"),
        P("wid", "nar"),
        P(),
        P(),
        P("row", ("nar", "wid"), None),
    )
    out_specs = (
        P("row", ("nar", "wid"), None),
        P("row", ("nar", "wid"), None),
        P(("row", "nar"), "wid"),
        P(("row", "nar"), None),
        P(("row", "nar"), None),
        P("wid", ("row", "nar")),
        P(("row", "nar"), "wid"),
        P(("row", "nar"), "wid"),
        P("wid", ("row", "nar")),
        P(("row", "nar")),
        P(("row", "nar")),
    )
    sizes = dict(mesh.shape)
    fits = sizes == {"row": 2, "nar": 4, "wid": 4}

    def body(*args):
        small = args[0].shape == (1, 128, 2048)
        return (local_fast if fits and small else local)(*args)

    return jax.shard_map(body, mesh=mesh, in_specs=in_specs, out_specs=out_specs, check_vma=False)
```

```python
import math

import jax
import jax.numpy as jnp
from jax import lax
from jax.experimental import pallas as pl
from jax.experimental.pallas import tpu as pltpu
from jax.sharding import PartitionSpec as P

H = 32
KV = 8
HD = 64


norm_eps = 1e-05
masked_score = -1e30


def inverse_freq():
    listed = []
    for pair_index in range(HD // 2):
        base_freq = 500000.0 ** (-2.0 * pair_index / HD)
        wavelength = 2.0 * math.pi / base_freq
        smoothing = (8192.0 / wavelength - 1.0) / 3.0
        blended = (1.0 - smoothing) * base_freq / 32.0 + smoothing * base_freq
        if wavelength < 2048.0:
            listed.append(base_freq)
        elif wavelength > 8192.0:
            listed.append(base_freq / 32.0)
        else:
            listed.append(blended)
    return jnp.asarray(listed, dtype=jnp.float32)


def rotate(values, cosine_table, sine_table):
    half_dim = HD // 2
    first_half = values[..., :half_dim]
    second_half = values[..., half_dim:]
    return jnp.concatenate(
        [
            first_half * cosine_table - second_half * sine_table,
            second_half * cosine_table + first_half * sine_table,
        ],
        axis=-1,
    )


def rotate_back(grads_in, cosine_table, sine_table):
    half_dim = HD // 2
    first_half = grads_in[..., :half_dim]
    second_half = grads_in[..., half_dim:]
    return jnp.concatenate(
        [
            first_half * cosine_table + second_half * sine_table,
            second_half * cosine_table - first_half * sine_table,
        ],
        axis=-1,
    )


def doc_layout(lengths_row, token_ids):
    ends_at = jnp.cumsum(lengths_row, dtype=jnp.int32)
    starts_at = ends_at - lengths_row
    inside = (token_ids[:, None] >= starts_at[None, :]) & (token_ids[:, None] < ends_at[None, :])
    doc_start = jnp.sum(jnp.where(inside, starts_at[None, :], 0), axis=1, dtype=jnp.int32)
    return (doc_start, token_ids - doc_start)


def norm_forward(values, gain_vector):
    root_inv = lax.rsqrt(jnp.mean(values * values, axis=-1, keepdims=True) + norm_eps)
    return (root_inv, (values * root_inv * gain_vector).astype(jnp.bfloat16))


def norm_backward(values, root_inv, gain_vector, grad_normed):
    weighted = grad_normed * gain_vector
    inner_sum = jnp.mean(weighted * values, axis=-1, keepdims=True)
    grad_values = root_inv * weighted - values * (root_inv * root_inv * root_inv) * inner_sum
    gain_term = jnp.sum(grad_normed * values * root_inv, axis=0)
    return (grad_values, gain_term)


def contract_last(left_side, right_side):
    return lax.dot_general(
        left_side, right_side, (((1,), (1,)), ((), ())), preferred_element_type=jnp.float32
    )


def contract_first(left_side, right_side):
    return lax.dot_general(
        left_side, right_side, (((0,), (0,)), ((), ())), preferred_element_type=jnp.float32
    )


def local(
    hidden_in,
    doc_lengths,
    w_query,
    w_key,
    w_value,
    w_output,
    w_gate,
    w_up,
    w_down,
    gain_attn,
    gain_ffn,
    grad_out,
):
    wid_count = lax.axis_size("wid")
    nar_count = lax.axis_size("nar")
    wid_index = lax.axis_index("wid")
    nar_index = lax.axis_index("nar")
    local_tokens = hidden_in.shape[1]
    block_tokens = local_tokens * wid_count
    seq_length = block_tokens * nar_count
    query_heads = w_query.shape[1] // HD
    group_size = H // KV
    kv_local = max(query_heads // group_size, 1)
    heads_per_kv = query_heads // kv_local
    kv_first = wid_index * query_heads // group_size
    query_block = min(512, block_tokens)
    block_count = block_tokens // query_block
    item_count = block_count * query_heads
    attn_scale = HD ** (-0.5)
    query_full, key_full, value_full, output_full, gate_full, up_full, down_full = (
        lax.all_gather(w_query, "nar", axis=0, tiled=True),
        lax.all_gather(w_key, "nar", axis=0, tiled=True),
        lax.all_gather(w_value, "nar", axis=0, tiled=True),
        lax.all_gather(w_output, "nar", axis=1, tiled=True),
        lax.all_gather(w_gate, "nar", axis=0, tiled=True),
        lax.all_gather(w_up, "nar", axis=0, tiled=True),
        lax.all_gather(w_down, "nar", axis=1, tiled=True),
    )
    key_local = lax.dynamic_slice_in_dim(key_full, kv_first * HD, kv_local * HD, 1)
    value_local = lax.dynamic_slice_in_dim(value_full, kv_first * HD, kv_local * HD, 1)
    token_ids = nar_index * block_tokens + jnp.arange(block_tokens, dtype=jnp.int32)
    doc_start, places = doc_layout(doc_lengths[0], token_ids)
    angles = places.astype(jnp.float32)[:, None] * inverse_freq()[None, :]
    cosine_table = jnp.cos(angles)[:, None, :]
    sine_table = jnp.sin(angles)[:, None, :]
    key_ids = jnp.arange(seq_length, dtype=jnp.int32)
    residual = hidden_in[0].astype(jnp.float32)
    root_attn, normed_attn = norm_forward(residual, gain_attn)
    normed_rows = lax.all_gather(normed_attn, "wid", axis=0, tiled=True)
    query_pre = jnp.dot(normed_rows, query_full, preferred_element_type=jnp.float32)
    key_pre = jnp.dot(normed_rows, key_local, preferred_element_type=jnp.float32)
    value_rows = jnp.dot(normed_rows, value_local, preferred_element_type=jnp.float32).astype(
        jnp.bfloat16
    )
    query_rot = (
        rotate(query_pre.reshape(block_tokens, query_heads, HD), cosine_table, sine_table)
        .astype(jnp.bfloat16)
        .reshape(block_tokens, query_heads * HD)
    )
    key_rot = (
        rotate(key_pre.reshape(block_tokens, kv_local, HD), cosine_table, sine_table)
        .astype(jnp.bfloat16)
        .reshape(block_tokens, kv_local * HD)
    )
    key_seq, value_seq = (
        lax.all_gather(key_rot, "nar", axis=0, tiled=True),
        lax.all_gather(value_rows, "nar", axis=0, tiled=True),
    )

    def item_inputs(item_index):
        block_index = item_index // query_heads
        head_index = item_index % query_heads
        kv_index = head_index // heads_per_kv
        row_first = block_index * query_block
        query_part = lax.dynamic_slice(query_rot, (row_first, head_index * HD), (query_block, HD))
        key_head = lax.dynamic_slice_in_dim(key_seq, kv_index * HD, HD, 1)
        value_head = lax.dynamic_slice_in_dim(value_seq, kv_index * HD, HD, 1)
        query_ids = lax.dynamic_slice_in_dim(token_ids, row_first, query_block, 0)
        query_starts = lax.dynamic_slice_in_dim(doc_start, row_first, query_block, 0)
        allowed = (key_ids[None, :] <= query_ids[:, None]) & (
            key_ids[None, :] >= query_starts[:, None]
        )
        scores = contract_last(query_part, key_head) * attn_scale
        return (
            row_first,
            head_index,
            kv_index,
            query_part,
            key_head,
            value_head,
            jnp.where(allowed, scores, masked_score),
        )

    def attend(item_index):
        row_first, head_index, kv_index, query_part, key_head, value_head, scores = item_inputs(
            item_index
        )
        row_max = jnp.max(scores, axis=1, keepdims=True)
        exp_scores = jnp.exp(scores - row_max)
        row_total = jnp.sum(exp_scores, axis=1, keepdims=True)
        probability = (exp_scores / row_total).astype(jnp.bfloat16)
        attended = jnp.dot(probability, value_head, preferred_element_type=jnp.float32)
        return (attended, (row_max + jnp.log(row_total))[:, 0])

    attended_items, logsum_items = lax.map(attend, jnp.arange(item_count, dtype=jnp.int32))
    attended_rows = (
        attended_items.reshape(block_count, query_heads, query_block, HD)
        .transpose(0, 2, 1, 3)
        .reshape(block_tokens, query_heads * HD)
        .astype(jnp.bfloat16)
    )
    rows_here = attended_rows
    branch_attn = lax.psum_scatter(
        jnp.dot(rows_here, output_full, preferred_element_type=jnp.float32),
        "wid",
        scatter_dimension=0,
        tiled=True,
    )
    middle = residual + branch_attn
    root_ffn, normed_ffn = norm_forward(middle, gain_ffn)
    ffn_rows = lax.all_gather(normed_ffn, "wid", axis=0, tiled=True)
    gate_proj = jnp.dot(ffn_rows, gate_full, preferred_element_type=jnp.float32)
    up_proj = jnp.dot(ffn_rows, up_full, preferred_element_type=jnp.float32)
    gate_sigmoid = jax.nn.sigmoid(gate_proj)
    gate_silu = gate_proj * gate_sigmoid
    activated = (gate_silu * up_proj).astype(jnp.bfloat16)
    rows_here = activated
    branch_ffn = lax.psum_scatter(
        jnp.dot(rows_here, down_full, preferred_element_type=jnp.float32).astype(jnp.bfloat16),
        "wid",
        scatter_dimension=0,
        tiled=True,
    ).astype(jnp.float32)
    hidden_out = (middle + branch_ffn).astype(jnp.bfloat16)[None]
    grad_top = grad_out[0]
    grad_rows = lax.all_gather(grad_top, "wid", axis=0, tiled=True)
    grad_activated = contract_last(grad_rows, down_full)
    down_weight_grad = contract_first(activated, grad_rows)
    silu_slope = gate_sigmoid * (1.0 + gate_proj * (1.0 - gate_sigmoid))
    grad_gate_b = (grad_activated * up_proj * silu_slope).astype(jnp.bfloat16)
    grad_up_b = (grad_activated * gate_silu).astype(jnp.bfloat16)
    gate_weight_grad = contract_first(ffn_rows, grad_gate_b)
    up_weight_grad = contract_first(ffn_rows, grad_up_b)
    grad_normed_ffn = lax.psum_scatter(
        contract_last(grad_gate_b, gate_full) + contract_last(grad_up_b, up_full),
        "wid",
        scatter_dimension=0,
        tiled=True,
    )
    grad_middle, gain_ffn_term = norm_backward(middle, root_ffn, gain_ffn, grad_normed_ffn)
    grad_middle = grad_middle + grad_top.astype(jnp.float32)
    grad_branch = grad_middle.astype(jnp.bfloat16)
    branch_rows = lax.all_gather(grad_branch, "wid", axis=0, tiled=True)
    grad_attended = contract_last(branch_rows, output_full).astype(jnp.bfloat16)
    output_weight_grad = contract_first(attended_rows, branch_rows)

    def attend_back(carried, item_index):
        key_grad, value_grad = carried
        row_first, head_index, kv_index, query_part, key_head, value_head, scores = item_inputs(
            item_index
        )
        logsum = lax.dynamic_index_in_dim(logsum_items, item_index, 0, keepdims=False)
        probability = jnp.exp(scores - logsum[:, None])
        grad_part = lax.dynamic_slice(
            grad_attended, (row_first, head_index * HD), (query_block, HD)
        )
        grad_prob = contract_last(grad_part, value_head)
        inner_sum = jnp.sum(probability * grad_prob, axis=1, keepdims=True)
        grad_scores = (probability * (grad_prob - inner_sum)).astype(jnp.bfloat16)
        query_grad = jnp.dot(grad_scores, key_head, preferred_element_type=jnp.float32) * attn_scale
        key_part = contract_first(grad_scores, query_part) * attn_scale
        value_part = contract_first(probability.astype(jnp.bfloat16), grad_part)
        key_old = lax.dynamic_slice_in_dim(key_grad, kv_index * HD, HD, 1)
        key_grad = lax.dynamic_update_slice_in_dim(key_grad, key_old + key_part, kv_index * HD, 1)
        value_old = lax.dynamic_slice_in_dim(value_grad, kv_index * HD, HD, 1)
        value_grad = lax.dynamic_update_slice_in_dim(
            value_grad, value_old + value_part, kv_index * HD, 1
        )
        return ((key_grad, value_grad), query_grad)

    zero_grads = jnp.zeros((seq_length, kv_local * HD), jnp.float32)
    (key_grad_seq, value_grad_seq), query_grad_items = lax.scan(
        attend_back, (zero_grads, zero_grads), jnp.arange(item_count, dtype=jnp.int32)
    )
    key_grad_block, value_grad_block = (
        lax.psum_scatter(
            key_grad_seq.astype(jnp.bfloat16), "nar", scatter_dimension=0, tiled=True
        ).astype(jnp.float32),
        lax.psum_scatter(
            value_grad_seq.astype(jnp.bfloat16), "nar", scatter_dimension=0, tiled=True
        ).astype(jnp.float32),
    )
    query_grad_rows = (
        query_grad_items.reshape(block_count, query_heads, query_block, HD)
        .transpose(0, 2, 1, 3)
        .reshape(block_tokens, query_heads, HD)
    )
    query_grad_b = (
        rotate_back(query_grad_rows, cosine_table, sine_table)
        .astype(jnp.bfloat16)
        .reshape(block_tokens, query_heads * HD)
    )
    key_grad_b = (
        rotate_back(key_grad_block.reshape(block_tokens, kv_local, HD), cosine_table, sine_table)
        .astype(jnp.bfloat16)
        .reshape(block_tokens, kv_local * HD)
    )
    value_grad_b = value_grad_block.astype(jnp.bfloat16)
    query_weight_grad = contract_first(normed_rows, query_grad_b)
    key_weight_grad = contract_first(normed_rows, key_grad_b)
    value_weight_grad = contract_first(normed_rows, value_grad_b)
    grad_normed_attn = lax.psum_scatter(
        (
            contract_last(query_grad_b, query_full)
            + contract_last(key_grad_b, key_local)
            + contract_last(value_grad_b, value_local)
        ).astype(jnp.bfloat16),
        "wid",
        scatter_dimension=0,
        tiled=True,
    ).astype(jnp.float32)
    grad_residual, gain_attn_term = norm_backward(residual, root_attn, gain_attn, grad_normed_attn)
    grad_in = (grad_residual + grad_middle).astype(jnp.bfloat16)[None]
    summed = (
        lax.psum_scatter(
            query_weight_grad.astype(jnp.bfloat16), ("row", "nar"), scatter_dimension=0, tiled=True
        ).astype(jnp.float32),
        lax.psum_scatter(
            key_weight_grad.astype(jnp.bfloat16), ("row", "nar"), scatter_dimension=0, tiled=True
        ).astype(jnp.float32),
        lax.psum_scatter(
            value_weight_grad.astype(jnp.bfloat16), ("row", "nar"), scatter_dimension=0, tiled=True
        ).astype(jnp.float32),
        lax.psum_scatter(
            output_weight_grad.astype(jnp.bfloat16), ("row", "nar"), scatter_dimension=1, tiled=True
        ).astype(jnp.float32),
        lax.psum_scatter(
            gate_weight_grad.astype(jnp.bfloat16), ("row", "nar"), scatter_dimension=0, tiled=True
        ).astype(jnp.float32),
        lax.psum_scatter(
            up_weight_grad.astype(jnp.bfloat16), ("row", "nar"), scatter_dimension=0, tiled=True
        ).astype(jnp.float32),
        lax.psum_scatter(
            down_weight_grad.astype(jnp.bfloat16), ("row", "nar"), scatter_dimension=1, tiled=True
        ).astype(jnp.float32),
        lax.psum_scatter(
            gain_attn_term.astype(jnp.bfloat16), ("row", "nar"), scatter_dimension=0, tiled=True
        ).astype(jnp.float32),
        lax.psum_scatter(
            gain_ffn_term.astype(jnp.bfloat16), ("row", "nar"), scatter_dimension=0, tiled=True
        ).astype(jnp.float32),
    )
    (
        grad_query,
        key_sum,
        value_sum,
        grad_output,
        grad_gate,
        grad_up,
        grad_down,
        gain_attn_sum,
        gain_ffn_sum,
    ) = summed
    key_all, value_all, gain_attn_all, gain_ffn_all = (
        lax.all_gather(key_sum.astype(jnp.bfloat16), "wid", axis=1, tiled=True).astype(
            key_sum.dtype
        ),
        lax.all_gather(value_sum.astype(jnp.bfloat16), "wid", axis=1, tiled=True).astype(
            value_sum.dtype
        ),
        lax.all_gather(gain_attn_sum.astype(jnp.bfloat16), "wid", axis=0, tiled=True).astype(
            gain_attn_sum.dtype
        ),
        lax.all_gather(gain_ffn_sum.astype(jnp.bfloat16), "wid", axis=0, tiled=True).astype(
            gain_ffn_sum.dtype
        ),
    )
    shard_rows = key_sum.shape[0]
    repeats = wid_count * kv_local // KV
    grad_key = key_all.reshape(shard_rows, KV, repeats, HD).sum(axis=2).reshape(shard_rows, KV * HD)
    grad_value = (
        value_all.reshape(shard_rows, KV, repeats, HD).sum(axis=2).reshape(shard_rows, KV * HD)
    )
    grad_gain_attn = gain_attn_all.reshape(wid_count, shard_rows).sum(axis=0)
    grad_gain_ffn = gain_ffn_all.reshape(wid_count, shard_rows).sum(axis=0)
    return (
        hidden_out,
        grad_in,
        grad_query,
        grad_key,
        grad_value,
        grad_output,
        grad_gate,
        grad_up,
        grad_down,
        grad_gain_attn,
        grad_gain_ffn,
    )


MESH = pl.DeviceIdType.MESH
bf16 = jnp.bfloat16
f32 = jnp.float32
VMEM_LIMIT = 60 * 2**20


def spot():
    return lax.axis_index("row"), lax.axis_index("nar"), lax.axis_index("wid")


def greet(partners):
    barrier = pltpu.get_barrier_semaphore()
    total = 0
    for there, device in partners:
        @pl.when(there)
        def _():
            pl.semaphore_signal(barrier, inc=1, device_id=device, device_id_type=MESH)

        total = total + there.astype(jnp.int32)
    pl.semaphore_wait(barrier, total)


def line_partners(r, n, w, wid_count):
    return [
        (w < wid_count - 1, (r, n, jnp.minimum(w + 1, wid_count - 1))),
        (w > 0, (r, n, jnp.maximum(w - 1, 0))),
        (w >= 0, (1 - r, n, w)),
    ]


def each_rows(count, step, body):
    def run(i, carry):
        body(pl.ds(pl.multiple_of(i * step, step), step))
        return carry

    lax.fori_loop(0, count // step, run, 0)


def square_partners(r, n, w):
    return [(n >= 0, over_x(r, n, w)), (n >= 0, over_y(r, n, w))]


def over_x(r, n, w):
    return (r, n + 1 - 2 * (n % 2), w)


def over_y(r, n, w):
    return (r, (n + 2) % 4, w)


def push(source, target, s_s, s_g, device):
    return pltpu.make_async_remote_copy(
        source, target, s_s, s_g, device_id=device, device_id_type=MESH
    )


class Square:
    def __init__(self, shard, full, sems, me):
        self.shard, self.full = shard, full
        self.sent, self.got = sems
        r, n, w = me
        self.n, self.x, self.y = n, n + 1 - 2 * (n % 2), (n + 2) % 4
        self.by_x, self.by_y = over_x(*me), over_y(*me)
        size = shard.shape[0] // 2
        self.upper, self.lower = pl.ds(0, size), pl.ds(size, size)

    def first(self, k, place):
        return push(
            self.shard, self.full.at[place], self.sent.at[k], self.got.at[k],
            (self.by_x, self.by_y)[k],
        )

    def second(self, k, place):
        part = self.full.at[place, (self.upper, self.lower)[k]]
        return push(
            part, part, self.sent.at[2 + k], self.got.at[2 + k], (self.by_y, self.by_x)[k]
        )

    def start(self):
        self.first(0, self.n).start()
        self.first(1, self.n).start()

    def turn(self):
        self.first(0, self.x).wait_recv()
        self.second(0, self.x).start()
        self.first(1, self.y).wait_recv()
        self.second(1, self.y).start()

    def finish(self):
        for k in range(2):
            self.second(k, 3 - self.n).wait_recv()
            self.first(k, self.n).wait_send()
            self.second(k, (self.x, self.y)[k]).wait_send()


def square_sems():
    return [pltpu.SemaphoreType.DMA((4,))] * 2


def fetch(own, full, target, sems, n):
    copies = [pltpu.make_async_copy(own, target.at[n], sems.at[0])]
    for k, place in enumerate((n + 1 - 2 * (n % 2), (n + 2) % 4, 3 - n)):
        copies.append(pltpu.make_async_copy(full.at[place], target.at[place], sems.at[1 + k]))
    return copies


class Gather:
    def __init__(self, buf, sems, me, wid_count, rows=slice(None), pair=True):
        self.rows, self.both = rows, pair
        self.buf, (self.up_s, self.dn_s, self.pt_s, self.got) = buf, sems
        self.r, self.n, self.w = me
        self.last = wid_count - 1
        self.up = (self.r, self.n, jnp.minimum(self.w + 1, self.last))
        self.dn = (self.r, self.n, jnp.maximum(self.w - 1, 0))
        self.pt = (1 - self.r, self.n, self.w)

    def copy(self, j, sem, device, row=None):
        row = (self.r if self.both else 0) if row is None else row
        return pltpu.make_async_remote_copy(
            self.buf.at[row, j, self.rows],
            self.buf.at[row, j, self.rows],
            sem.at[j],
            self.got.at[row, j],
            device_id=device,
            device_id_type=MESH,
        )

    def pass_on(self, j, go_up, go_dn):
        if go_up:
            @pl.when(self.w < self.last)
            def _():
                self.copy(j, self.up_s, self.up).start()

        if go_dn:
            @pl.when(self.w > 0)
            def _():
                self.copy(j, self.dn_s, self.dn).start()

        if self.both:
            self.copy(j, self.pt_s, self.pt).start()

    def own(self):
        self.pass_on(self.w, True, True)

    def arrive(self, row, j):
        self.copy(j, self.pt_s, self.pt, row).wait_recv()

    def step(self, k):
        below, above = self.w - k, self.w + k

        @pl.when(below >= 0)
        def _():
            self.arrive(None, below)
            self.pass_on(below, True, False)

        @pl.when(above <= self.last)
        def _():
            self.arrive(None, above)
            self.pass_on(above, False, True)

    def advance(self, edge_steps, inner_steps):
        at_end = (self.w == 0) | (self.w == self.last)
        for ends, steps in ((True, edge_steps), (False, inner_steps)):
            if steps:
                @pl.when(at_end if ends else jnp.logical_not(at_end))
                def _():
                    for k in steps:
                        self.step(k)

    def rest(self):
        for j in range(self.last + 1):
            self.arrive(1 - self.r, j)

    def sent(self):
        for j in range(self.last + 1):
            @pl.when((j <= self.w) & (self.w < self.last))
            def _():
                self.copy(j, self.up_s, self.up).wait_send()

            @pl.when((j >= self.w) & (self.w > 0))
            def _():
                self.copy(j, self.dn_s, self.dn).wait_send()

            if self.both:
                self.copy(j, self.pt_s, self.pt).wait_send()


def gather_scratch(shard, width):
    return [pltpu.VMEM((2, 4, shard, width), bf16)] + gather_sems()


def gather_sems():
    return [pltpu.SemaphoreType.DMA((4,))] * 3 + [pltpu.SemaphoreType.DMA((2, 4))]


class Scatter:
    def __init__(self, mine, theirs, bufs, sems, me, wid_count, first=0, count=None):
        self.mine, self.theirs = mine, theirs
        self.from_pt, self.from_up, self.from_dn = bufs
        self.pt_s, self.pt_g, self.up_s, self.up_g, self.dn_s, self.dn_g = sems
        self.r, self.n, self.w = me
        self.first, self.count = first, mine.shape[1] if count is None else count
        self.rows = pl.ds(first, self.count)
        self.last = wid_count - 1
        self.up = (self.r, self.n, jnp.minimum(self.w + 1, self.last))
        self.dn = (self.r, self.n, jnp.maximum(self.w - 1, 0))
        self.pt = (1 - self.r, self.n, self.w)

    def order(self, i):
        low = jnp.where(i == 0, 3, jnp.where(i == 1, 0, jnp.where(i == 2, 2, 1)))
        return jnp.where(self.w < 2, low, 3 - low)

    def send(self, source, target, sent, got, s, device):
        return pltpu.make_async_remote_copy(
            source.at[s, self.rows], target.at[s, self.rows], sent.at[s], got.at[s],
            device_id=device, device_id_type=MESH,
        )

    def pair(self, s):
        return self.send(self.theirs, self.from_pt, self.pt_s, self.pt_g, s, self.pt)

    def climb(self, s):
        return self.send(self.mine, self.from_dn, self.up_s, self.up_g, s, self.up)

    def fall(self, s):
        return self.send(self.mine, self.from_up, self.dn_s, self.dn_g, s, self.dn)

    def each(self, body):
        def run(i, carry):
            body(pl.ds(pl.multiple_of(self.first + i * 16, 16), 16))
            return carry

        lax.fori_loop(0, self.count // 16, run, 0)

    def add(self, s, others):
        def body(rows):
            total = self.mine[s, rows, :].astype(f32)
            for other in others:
                total = total + other[s, rows, :].astype(f32)
            self.mine[s, rows, :] = total.astype(bf16)

        self.each(body)

    def step(self, s):
        self.pair(s).wait_recv()

        @pl.when((s > self.w) & (self.w > 0))
        def _():
            self.climb(s).wait_recv()
            self.add(s, (self.from_pt, self.from_dn))

        @pl.when((s < self.w) & (self.w < self.last))
        def _():
            self.fall(s).wait_recv()
            self.add(s, (self.from_pt, self.from_up))

        @pl.when(((s > self.w) & (self.w == 0)) | ((s < self.w) & (self.w == self.last)))
        def _():
            self.add(s, (self.from_pt,))

        @pl.when(s > self.w)
        def _():
            self.climb(s).start()

        @pl.when(s < self.w)
        def _():
            self.fall(s).start()

    def advance(self, edge_steps, inner_steps):
        for ends, steps in ((True, edge_steps), (False, inner_steps)):
            at_end = (self.w == 0) | (self.w == self.last)

            def body(i, carry):
                self.step(self.order(i))
                return carry

            if steps:
                @pl.when(at_end if ends else jnp.logical_not(at_end))
                def _():
                    lax.fori_loop(steps[0], steps[-1] + 1, body, 0)

    def total(self, out):
        w = self.w

        def first(rows):
            out[rows, :] = self.mine[w, rows, :].astype(f32) + self.from_pt[w, rows, :].astype(f32)

        self.each(first)

        @pl.when(w > 0)
        def _():
            self.climb(w).wait_recv()

            def more(rows):
                out[rows, :] += self.from_dn[w, rows, :].astype(f32)

            self.each(more)

        @pl.when(w < self.last)
        def _():
            self.fall(w).wait_recv()

            def more(rows):
                out[rows, :] += self.from_up[w, rows, :].astype(f32)

            self.each(more)

    def sent(self):
        for s in range(self.last + 1):
            self.pair(s).wait_send()

            @pl.when(s > self.w)
            def _():
                self.climb(s).wait_send()

            @pl.when(s < self.w)
            def _():
                self.fall(s).wait_send()


def scatter_bufs(shard, width):
    return [pltpu.VMEM((4, shard, width), bf16)] * 3


def scatter_sems():
    return [pltpu.SemaphoreType.DMA((4,))] * 6


def vmem():
    return pl.BlockSpec(memory_space=pltpu.VMEM)


def hbm():
    return pl.BlockSpec(memory_space=pl.ANY)


def comm_call(kernel, name, cid, out_shape, in_specs, out_specs, scratch, args, flops=0, sent=0):
    return pl.pallas_call(
        kernel,
        out_shape=out_shape,
        in_specs=in_specs,
        out_specs=out_specs,
        scratch_shapes=scratch,
        compiler_params=pltpu.CompilerParams(
            collective_id=cid, has_side_effects=True, vmem_limit_bytes=VMEM_LIMIT
        ),
        cost_estimate=pl.CostEstimate(flops=flops, bytes_accessed=sent, transcendentals=0),
        name=name,
    )(*args)


def norm_rows(x, gain):
    root = lax.rsqrt(jnp.mean(x * x, axis=-1, keepdims=True) + norm_eps)
    return x * root * gain


def turn(x, cosine, sine):
    lane = lax.broadcasted_iota(jnp.int32, x.shape, 1)
    swapped = jnp.where(lane % 64 < 32, pltpu.roll(x, 96, 1), pltpu.roll(x, 32, 1))
    return x * cosine + swapped * sine


def nar_device(r, n, w, by):
    return (r, jnp.clip(n + by, 0, 3), w)


def enter_kernel(
    hidden, gain, tab, grad_top, p1_own, down_own,
    q_out, rows_out, tabs_out, p1_out, down_out, kv_out, tops_out,
    buf, up_s, dn_s, pt_s, got, tbuf, h0, h1, h2, h3, tabs, p1, kv,
    tab_s, tab_g, out_s, p1_s, p1_g, down_s, down_g, s_s, s_g,
):
    me = spot()
    r, n, w = me
    bring = pltpu.make_async_copy(p1_own, p1.at[n], out_s.at[0])
    bring.start()
    greet(
        line_partners(r, n, w, 4)
        + [
            (n >= 1, nar_device(r, n, w, -1)),
            (n >= 2, nar_device(r, n, w, -2)),
            (n <= 2, nar_device(r, n, w, 1)),
            (n <= 1, nar_device(r, n, w, 2)),
        ]
    )
    p1_square = Square(p1_own, p1, (p1_s, p1_g), me)
    down = Square(down_own.at[0:256], down_out, (down_s, down_g), me)
    p1_square.start()
    down.start()
    gather = Gather(buf, (up_s, dn_s, pt_s, got), me, 4)
    tops = Gather(tbuf, (h0, h1, h2, h3), me, 4)
    tab_copy = pltpu.make_async_remote_copy(
        tab, tabs.at[r], tab_s, tab_g, device_id=(1 - r, n, w), device_id_type=MESH
    )

    def body(rows):
        buf[r, w, rows, :] = norm_rows(hidden[rows, :].astype(f32), gain[...]).astype(bf16)

    each_rows(hidden.shape[0], 16, body)
    gather.own()
    tab_copy.start()

    def keep(rows):
        tabs[r, rows, :] = tab[rows, :]

    each_rows(tab.shape[0], 16, keep)

    def keep_top(rows):
        tbuf[r, w, rows, :] = grad_top[rows, :]

    each_rows(64, 16, keep_top)
    gather.step(1)
    p1_square.turn()
    gather.step(2)
    tops.own()
    down.turn()
    gather.step(3)
    gather.rest()
    tab_copy.wait_recv()
    p1_square.finish()
    bring.wait()
    outs = [
        pltpu.make_async_copy(buf, rows_out, out_s.at[1]),
        pltpu.make_async_copy(tabs, tabs_out, out_s.at[2]),
        pltpu.make_async_copy(p1, p1_out, out_s.at[3]),
    ]
    for out in outs:
        out.start()
    tops.step(1)

    def copy(row, slot, by):
        return pltpu.make_async_remote_copy(
            kv.at[row, 2], kv.at[row, slot], s_s.at[row, slot], s_g.at[row, slot],
            device_id=nar_device(r, n, w, by), device_id_type=MESH,
        )

    lane = lax.broadcasted_iota(jnp.int32, (256, 128), 1)
    weight = p1[:, :, 0:384].reshape(2048, 384)
    for row in range(2):
        def tile(i, carry):
            rows = pl.ds(pl.multiple_of(i * 256, 256), 256)
            cosine, sine = tabs[row, rows, 0:128], tabs[row, rows, 128:256]
            left = buf[row, pl.ds(i * 2, 2)].reshape(256, 2048)
            pre = jnp.dot(left, weight, preferred_element_type=f32)
            q_out[row, rows, 0:128] = turn(pre[:, 0:128], cosine, sine).astype(bf16)
            q_out[row, rows, 128:256] = turn(pre[:, 128:256], cosine, sine).astype(bf16)
            both = pre[:, 256:384]
            kv[row, 2, rows, :] = jnp.where(lane < 64, turn(both, cosine, sine), both).astype(bf16)
            return carry

        lax.fori_loop(0, 2, tile, 0)

        @pl.when(n <= 2)
        def _():
            copy(row, 1, 1).start()

        @pl.when(n <= 1)
        def _():
            copy(row, 0, 2).start()

        for slot, least in ((1, 1), (0, 2)):
            @pl.when(n < least)
            def _():
                kv[row, slot] = jnp.zeros((512, 128), bf16)

    tops.step(2)
    for row in range(2):
        for slot, least, by in ((1, 1, 1), (0, 2, 2)):
            @pl.when(n >= least)
            def _():
                copy(row, slot, by).wait_recv()

    outs.append(pltpu.make_async_copy(kv, kv_out, out_s.at[4]))
    outs[3].start()
    tops.step(3)
    tops.rest()
    outs.append(pltpu.make_async_copy(tbuf, tops_out, out_s.at[5]))
    outs[4].start()
    for row in range(2):
        @pl.when(n <= 2)
        def _():
            copy(row, 1, 1).wait_send()

        @pl.when(n <= 1)
        def _():
            copy(row, 0, 2).wait_send()

    gather.sent()
    tops.sent()
    tab_copy.wait_send()
    down.finish()
    for out in outs:
        out.wait()


def enter(hidden, gain, tab, grad_top, p1_own, down_own):
    shard, width = hidden.shape
    return comm_call(
        enter_kernel, "enter", 1,
        (
            jax.ShapeDtypeStruct((2, 512, 256), bf16),
            jax.ShapeDtypeStruct((2, 4, shard, width), bf16),
            jax.ShapeDtypeStruct((2,) + tab.shape, f32),
            jax.ShapeDtypeStruct((4,) + p1_own.shape, bf16),
            jax.ShapeDtypeStruct((4, 256, 1024), bf16),
            jax.ShapeDtypeStruct((2, 3, 512, 128), bf16),
            jax.ShapeDtypeStruct((2, 4, 64, width), bf16),
        ),
        [vmem()] * 4 + [hbm()] * 2, [vmem()] + [hbm()] * 6,
        gather_scratch(shard, width)
        + gather_scratch(64, width)
        + [
            pltpu.VMEM((2,) + tab.shape, f32),
            pltpu.VMEM((4,) + p1_own.shape, bf16),
            pltpu.VMEM((2, 3, 512, 128), bf16),
            pltpu.SemaphoreType.DMA(()),
            pltpu.SemaphoreType.DMA(()),
            pltpu.SemaphoreType.DMA((6,)),
        ]
        + square_sems() * 2
        + [pltpu.SemaphoreType.DMA((2, 3))] * 2,
        (hidden, gain, tab, grad_top, p1_own, down_own), flops=10**10, sent=10**8,
    )


KEYS = 256
QUERIES = 128


def stack_low(x):
    lane = lax.broadcasted_iota(jnp.int32, (QUERIES, 128), 1)
    zero = jnp.zeros((QUERIES, 128), x.dtype)
    parts = []
    for pair in range(2):
        block = x[:, pair * 128 : pair * 128 + 128]
        parts.append(jnp.where(lane < 64, block, zero))
        parts.append(jnp.where(lane < 64, pltpu.roll(block, 64, 1), zero))
    return jnp.concatenate(parts, axis=0)


def stack_high(x):
    lane = lax.broadcasted_iota(jnp.int32, (QUERIES, 128), 1)
    zero = jnp.zeros((QUERIES, 128), x.dtype)
    parts = []
    for pair in range(2):
        block = x[:, pair * 128 : pair * 128 + 128]
        parts.append(jnp.where(lane >= 64, pltpu.roll(block, 64, 1), zero))
        parts.append(jnp.where(lane >= 64, block, zero))
    return jnp.concatenate(parts, axis=0)


def unstack(x, low):
    lane = lax.broadcasted_iota(jnp.int32, (QUERIES, 128), 1)
    out = []
    for pair in range(2):
        even = x[2 * pair * QUERIES : (2 * pair + 1) * QUERIES]
        odd = x[(2 * pair + 1) * QUERIES : (2 * pair + 2) * QUERIES]
        if low:
            out.append(jnp.where(lane < 64, even, pltpu.roll(odd, 64, 1)))
        else:
            out.append(jnp.where(lane < 64, pltpu.roll(even, 64, 1), odd))
    return jnp.concatenate(out, axis=1)


def allowed_tile(starts, tile, first_query):
    key = lax.broadcasted_iota(jnp.int32, (QUERIES, KEYS), 1) + tile * KEYS
    query = lax.broadcasted_iota(jnp.int32, (QUERIES, KEYS), 0) + first_query
    start = jnp.concatenate([starts] * (KEYS // 128), axis=1)
    ok = (key <= query) & (key.astype(f32) >= start)
    return jnp.concatenate([ok] * 4, axis=0)


def attend_block(q, kv, starts, first_query):
    query = stack_low(q.astype(f32)).astype(bf16)

    def body(step, carry):
        tile = (first_query - 1024) // KEYS + step
        top, total, acc = carry
        both = kv[pl.ds(pl.multiple_of(tile * KEYS, KEYS), KEYS), :]
        scores = contract_last(query, both) * 0.125
        ok = allowed_tile(starts, tile, first_query)
        scores = jnp.where(ok, scores, masked_score)
        new_top = jnp.maximum(top, jnp.max(scores, axis=1, keepdims=True))
        shrink = jnp.exp(top - new_top)
        part = jnp.exp(scores - new_top)
        total = total * shrink + jnp.sum(part, axis=1, keepdims=True)
        acc = acc * shrink + jnp.dot(part.astype(bf16), both, preferred_element_type=f32)
        return new_top, total, acc

    top, total, acc = lax.fori_loop(
        0, 5, body,
        (
            jnp.full((4 * QUERIES, 1), masked_score, f32),
            jnp.zeros((4 * QUERIES, 1), f32),
            jnp.zeros((4 * QUERIES, 128), f32),
        ),
        unroll=True,
    )
    logsum = jnp.broadcast_to(top + jnp.log(total), (4 * QUERIES, 128))
    return unstack(acc / total, False).astype(bf16), logsum


def out_block(p1, nn, half):
    return p1[nn, half * 256 : half * 256 + 256, 384:640]


def middle_kernel(
    q, kv, tabs, p1, hidden, gain, gate_own, up_own, down_own,
    att, lse, mid_out, ffn_out, gate_out, up_out, down_out,
    theirs, mine, from_pt, from_up, from_dn, s0, s1, s2, s3, s4, s5, fbuf, h0, h1, h2, h3, out_s,
    gate_s, gate_g, up_s, up_g, down_s, down_g,
):
    me = spot()
    r, n, w = me
    greet(line_partners(r, n, w, 4) + square_partners(r, n, w))
    gate = Square(gate_own, gate_out, (gate_s, gate_g), me)
    up = Square(up_own, up_out, (up_s, up_g), me)
    gate.start()
    up.start()
    down = Square(down_own.at[256:512], down_out, (down_s, down_g), me)
    down.start()
    scatter = Scatter(
        mine, theirs, (from_pt, from_up, from_dn), (s0, s1, s2, s3, s4, s5), me, 4
    )
    ffn = Gather(fbuf, (h0, h1, h2, h3), me, 4)
    def shard(i, carry):
        s = scatter.order(i)
        rows = pl.ds(pl.multiple_of(s * 128, 128), 128)
        for row in range(2):
            att[row, rows, :], lse[row, s] = attend_block(
                q[row, rows, :], kv.at[row], tabs[row, rows, 256:384], 1024 + s * 128
            )

        @pl.when((i >= 1) & ((w == 0) | (w == 3)))
        def _():
            scatter.step(scatter.order(i - 1))

        left = jnp.concatenate([att[1 - r, rows, :], att[r, rows, :]], axis=0)
        for nn in range(4):
            for half in range(2):
                part = jnp.dot(left, out_block(p1, nn, half), preferred_element_type=f32).astype(bf16)
                columns = slice(nn * 512 + half * 256, nn * 512 + half * 256 + 256)
                theirs[s, :, columns] = part[0:128]
                mine[s, :, columns] = part[128:256]
        scatter.pair(s).start()
        return carry

    lax.fori_loop(0, 4, shard, 0)
    scatter.advance((3,), (0, 1, 2, 3))
    scatter.total(mid_out)

    def body(rows):
        middle = mid_out[rows, :] + hidden[rows, :].astype(f32)
        mid_out[rows, :] = middle
        fbuf[r, w, rows, :] = norm_rows(middle, gain[...]).astype(bf16)

    each_rows(hidden.shape[0], 16, body)
    ffn.own()
    gate.turn()
    up.turn()
    ffn.step(1)
    down.turn()
    ffn.step(2)
    ffn.step(3)
    ffn.rest()
    out_f = pltpu.make_async_copy(fbuf, ffn_out, out_s)
    out_f.start()
    scatter.sent()
    ffn.sent()
    gate.finish()
    up.finish()
    down.finish()
    out_f.wait()


def middle_stage(q, kv, tabs, p1, hidden, gain, *weights):
    shard, width = hidden.shape
    rows = jax.ShapeDtypeStruct((2, 4, shard, width), bf16)
    return comm_call(
        middle_kernel, "middle", 3,
        (
            jax.ShapeDtypeStruct((2, 512, 256), bf16),
            jax.ShapeDtypeStruct((2, 4, 4 * QUERIES, 128), f32),
            jax.ShapeDtypeStruct((shard, width), f32),
            rows,
        )
        + (jax.ShapeDtypeStruct((4, 512, 1024), bf16),) * 2
        + (jax.ShapeDtypeStruct((4, 256, 1024), bf16),),
        [vmem()] * 6 + [hbm()] * 3, [vmem()] * 3 + [hbm()] * 4,
        [pltpu.VMEM((4, shard, width), bf16)] * 2
        + scatter_bufs(shard, width) + scatter_sems()
        + gather_scratch(shard, width)
        + [pltpu.SemaphoreType.DMA(())]
        + square_sems() * 3,
        (q, kv, tabs, p1, hidden, gain, *weights), flops=10**10, sent=2 * 10**8,
    )


class Spread:
    def __init__(self, outs, sems, me):
        self.a_send, self.a_keep, self.b_send, self.b_keep = outs
        self.r, self.n, self.w = me
        self.give_s, self.give_g, self.keep_s = sems

    def copies(self, wide, row, place, give):
        for k in range(4):
            block = wide.at[self.n ^ k]
            for part in range(2):
                source = block.at[pl.ds(part * 128, 128)]
                if part == 0:
                    target = (self.a_send if k & 1 else self.a_keep).at[k >> 1]
                else:
                    target = (self.b_send if k >= 2 else self.b_keep).at[k & 1]
                target = place(target)
                at = k * 2 + part
                if give:
                    yield pltpu.make_async_remote_copy(
                        source, target, self.give_s.at[row, at], self.give_g.at[row, at],
                        device_id=(1 - self.r, self.n, self.w), device_id_type=MESH,
                    )
                else:
                    yield pltpu.make_async_copy(source, target, self.keep_s.at[row, at])

    def start(self, *args):
        for copy in self.copies(*args):
            copy.start()

    def wait_send(self, *args):
        for copy in self.copies(*args):
            copy.wait_send()

    def wait_recv(self, *args):
        for copy in self.copies(*args):
            copy.wait_recv()

    def wait(self, *args):
        for copy in self.copies(*args):
            copy.wait()


def spread_sems(count):
    return [pltpu.SemaphoreType.DMA((count, 8))] * 3


def ffn_kernel(
    x, tops_in, grad_top, gate_own, gate_in, up_own, up_in, down_own, down_a, down_b, gain,
    part_out, sum_out, gain_out, o0, o1, o2, o3, ra_out, rb_out,
    theirs, mine, from_pt, from_up, from_dn, s0, s1, s2, s3, s4, s5,
    act, dgu, wide, out_s, give_s, give_g, keep_s, p2, in_s, n_s, n_g,
    tops4, h0, h1, h2, h3, tops_s,
):
    me = spot()
    r, n, w = me
    loads = [
        fetch(gate_own, gate_in, p2.at[0], in_s.at[0], n),
        fetch(up_own, up_in, p2.at[1], in_s.at[1], n),
        fetch(down_own.at[0:256], down_a, p2.at[2, :, 0:256], in_s.at[2], n)
        + fetch(down_own.at[256:512], down_b, p2.at[2, :, 256:512], in_s.at[3], n),
        [pltpu.make_async_copy(tops_in, tops4.at[:, :, 0:64], tops_s)],
    ]
    for group in loads:
        for load in group:
            load.start()

    def loaded(k):
        for load in loads[k]:
            load.wait()

    greet(line_partners(r, n, w, 4) + square_partners(r, n, w))
    scatter = Scatter(
        mine, theirs, (from_pt, from_up, from_dn), (s0, s1, s2, s3, s4, s5), me, 4
    )
    late = pl.ds(64, 64)
    gather = Gather(tops4, (h0, h1, h2, h3), me, 4, late)

    def keep(rows):
        tops4[r, w, pl.ds(64 + rows.start, 16), :] = grad_top[pl.ds(64 + rows.start, 16), :]

    each_rows(64, 16, keep)
    gather.own()
    gain_out[...] = jnp.zeros_like(gain_out)
    loaded(0)
    loaded(1)

    def hidden_tile(i, carry):
        ft, row = i // 2, i % 2
        rows = pl.ds(pl.multiple_of(row * 512, 512), 512)
        columns = pl.ds(pl.multiple_of(ft * 256, 256), 256)
        left = x[rows, :]
        gate = jnp.dot(left, p2[0, :, :, columns].reshape(2048, 256), preferred_element_type=f32)
        up = jnp.dot(left, p2[1, :, :, columns].reshape(2048, 256), preferred_element_type=f32)
        sig = 1.0 / (1.0 + jnp.exp(-gate))
        silu = gate * sig
        act[rows, columns] = (silu * up).astype(bf16)
        dgu[rows, columns] = (up * (sig * (1.0 + gate * (1.0 - sig)))).astype(bf16)
        later = pl.ds(pl.multiple_of(1024 + ft * 256, 256), 256)
        dgu[rows, later] = silu.astype(bf16)
        return carry

    lax.fori_loop(0, 4, hidden_tile, 0)
    gather.step(1)
    lax.fori_loop(4, 8, hidden_tile, 0)
    gather.step(2)
    loaded(2)

    def down_tile(dt, carry):
        nn, half = dt // 2, dt % 2
        columns = pl.ds(pl.multiple_of(dt * 256, 256), 256)
        inner = pl.ds(pl.multiple_of(half * 256, 256), 256)
        other = pl.ds(pl.multiple_of(512 + half * 256, 256), 256)
        right = jnp.concatenate([p2[2, nn, :, inner], p2[2, nn, :, other]], axis=0)
        for row, stage in ((0, theirs), (1, mine)):
            part = jnp.dot(act[row * 512 : row * 512 + 512, :], right, preferred_element_type=f32)
            stage[:, :, columns] = part.astype(bf16).reshape(4, 128, 256)
        return carry

    lax.fori_loop(0, 8, down_tile, 0)
    puts = [
        pltpu.make_async_copy(theirs, part_out.at[0], out_s.at[0]),
        pltpu.make_async_copy(mine, part_out.at[1], out_s.at[1]),
    ]
    for put in puts:
        put.start()
    gather.step(3)
    gather.rest()
    loaded(3)

    def top_rows(row):
        return tops4[row].reshape(512, 2048)

    def back_tile(ft, carry):
        columns = pl.ds(pl.multiple_of(ft * 256, 256), 256)
        f_rows = pl.ds(pl.multiple_of((ft % 2) * 256, 256), 256)
        f_cols = pl.ds(pl.multiple_of((ft // 2) * 512, 512), 512)
        later = pl.ds(pl.multiple_of(1024 + ft * 256, 256), 256)
        right = jnp.concatenate([p2[2, nn, f_rows, f_cols] for nn in range(4)], axis=1)
        for row in range(2):
            rows = slice(row * 512, row * 512 + 512)
            dact = contract_last(top_rows(row), right)
            dgu[rows, columns] = (dact * dgu[rows, columns].astype(f32)).astype(bf16)
            dgu[rows, later] = (dact * dgu[rows, later].astype(f32)).astype(bf16)
        return carry

    lax.fori_loop(0, 4, back_tile, 0)
    for put in puts:
        put.wait()

    spread = Spread((o0, o1, o2, o3), (give_s, give_g, keep_s), me)
    columns_here = pl.ds(pl.multiple_of(r * 1024, 1024), 1024)
    slots = {2: 0, 0: 1, 1: 0}

    def moved(which, half):
        def place(target):
            return target.at[which, :, columns_here]

        return wide.at[slots[which], half], which, place, half == 0

    def weights(which, between=None):
        for half in range(2):
            d_first = (jnp.where(half == 0, 1 - r, r)) * 1024

            def weight_tile(i, carry):
                d_cols = pl.ds(pl.multiple_of(d_first + i * 256, 256), 256)
                if which < 2:
                    left = x[:, d_cols]
                    right = dgu[:, which * 1024 : which * 1024 + 1024]
                else:
                    left = tops4[:, :, :, d_cols].reshape(1024, 256)
                    right = act[...]
                wide[slots[which], half, i] = contract_first(left, right).astype(bf16)
                return carry

            lax.fori_loop(0, 4, weight_tile, 0)
            spread.start(*moved(which, half))
            if half == 0 and between is not None:
                between()

    def hop(which, at):
        return (
            push(o0.at[:, which], ra_out.at[at], n_s.at[0, at], n_g.at[0, at], over_x(r, n, w)),
            push(o2.at[:, which], rb_out.at[at], n_s.at[1, at], n_g.at[1, at], over_y(r, n, w)),
        )

    hops = hop(2, 0) + hop(0, 1)
    weights(2)
    for i in range(4):
        s = scatter.order(i)
        rows_t = pl.ds(pl.multiple_of((1 - r) * 512 + s * 128, 128), 128)
        rows_m = pl.ds(pl.multiple_of(r * 512 + s * 128, 128), 128)

        def model_tile(dt, carry):
            nn, half = dt // 2, dt % 2
            columns = pl.ds(pl.multiple_of(dt * 256, 256), 256)
            inner = pl.ds(pl.multiple_of(half * 256, 256), 256)
            left = jnp.concatenate([dgu[rows_t, :], dgu[rows_m, :]], axis=0)
            right = jnp.concatenate([p2[0, nn, inner, :], p2[1, nn, inner, :]], axis=1)
            part = contract_last(left, right)
            seen = jnp.concatenate([x[rows_t, columns], x[rows_m, columns]], axis=0)
            terms = part * seen.astype(f32)
            gain_out[:, columns] += jnp.sum(terms.reshape(32, 8, 256), axis=0)
            part = part.astype(bf16)
            theirs[s, :, columns] = part[0:128]
            mine[s, :, columns] = part[128:256]
            return carry

        lax.fori_loop(0, 8, model_tile, 0)
        scatter.pair(s).start()
        if i < 2:
            which = (2, 0)[i]
            spread.wait_recv(*moved(which, 0))
            spread.wait(*moved(which, 1))
            hops[2 * i].start()
            hops[2 * i + 1].start()
        if i == 0:
            weights(0)
            scatter.advance((0,), ())
        elif i > 1:
            scatter.advance((i - 1,), (i - 2,))

    def scale(rows):
        gain_out[rows, :] = gain_out[rows, :] / gain[...]

    each_rows(8, 8, scale)
    spread.wait_send(*moved(2, 0))
    weights(1, lambda: scatter.advance((3,), (2,)))
    scatter.advance((), (3,))
    scatter.total(sum_out)
    scatter.sent()
    gather.sent()
    spread.wait_send(*moved(0, 0))
    spread.wait_recv(*moved(1, 0))
    spread.wait_send(*moved(1, 0))
    spread.wait(*moved(1, 1))
    for hop in hops:
        hop.wait()


def spread_shapes(*dims):
    return (jax.ShapeDtypeStruct((2,) + dims, bf16),) * 4


def ffn_stage(*args):
    shard, width = 128, 2048
    return comm_call(
        ffn_kernel, "ffn", 4,
        (
            jax.ShapeDtypeStruct((2, 4, shard, width), bf16),
            jax.ShapeDtypeStruct((shard, width), f32),
            jax.ShapeDtypeStruct((8, width), f32),
        )
        + spread_shapes(3, 128, width)
        + (jax.ShapeDtypeStruct((2, 2, 128, width), bf16),) * 2,
        [vmem(), hbm(), vmem()] + [hbm()] * 7 + [vmem()], [hbm(), vmem(), vmem()] + [hbm()] * 6,
        [pltpu.VMEM((4, shard, width), bf16)] * 2
        + scatter_bufs(shard, width) + scatter_sems()
        + [
            pltpu.VMEM((1024, 1024), bf16),
            pltpu.VMEM((1024, 2048), bf16),
            pltpu.VMEM((2, 2, 4, 256, 1024), bf16),
            pltpu.SemaphoreType.DMA((2,)),
        ]
        + spread_sems(3)
        + [pltpu.VMEM((3, 4, 512, 1024), bf16), pltpu.SemaphoreType.DMA((4, 4))]
        + [pltpu.SemaphoreType.DMA((2, 2))] * 2
        + gather_scratch(shard, width)
        + [pltpu.SemaphoreType.DMA(())],
        args, flops=4 * 10**10, sent=10**8,
    )


def norm_back(values, gain, grad):
    root = lax.rsqrt(jnp.mean(values * values, axis=-1, keepdims=True) + norm_eps)
    weighted = grad * gain
    inner = jnp.mean(weighted * values, axis=-1, keepdims=True)
    return root * weighted - values * (root * root * root) * inner


def branch_kernel(
    total, mid, grad_top, gain, p1, att, a_in, b_in, a_keep, b_keep, a_came, b_came,
    gmid_out, datt_out, o0, o1, o2, o3, ra_out, rb_out, la_out, lb_out,
    buf, g0, g1, g2, g3, wide, give_s, give_g, keep_s, n_s, n_g, kept, came, in_s,
):
    me = spot()
    r, n, w = me
    greet(line_partners(r, n, w, 4) + square_partners(r, n, w))
    gather = Gather(buf, (g0, g1, g2, g3), me, 4)
    hops = [
        push(a_in.at[:, 1], ra_out, n_s.at[0], n_g.at[0], over_x(r, n, w)),
        push(b_in.at[:, 1], rb_out, n_s.at[1], n_g.at[1], over_y(r, n, w)),
        push(kept.at[0], la_out, n_s.at[2], n_g.at[2], over_y(r, n, w)),
        push(kept.at[1], lb_out, n_s.at[3], n_g.at[3], over_x(r, n, w)),
    ]
    loads = []
    for j, (keep, first) in enumerate(((a_keep, a_came), (b_keep, b_came))):
        loads += [
            pltpu.make_async_copy(keep.at[1, 2], kept.at[j], in_s.at[j, 0]),
            pltpu.make_async_copy(first.at[0, 1], came.at[j], in_s.at[j, 1]),
        ]
    for load in loads:
        load.start()
    hops[0].start()
    hops[1].start()

    def body(rows):
        grad = norm_back(mid[rows, :], gain[...], total[rows, :]) + grad_top[rows, :].astype(f32)
        gmid_out[rows, :] = grad
        buf[r, w, rows, :] = grad.astype(bf16)

    each_rows(mid.shape[0], 16, body)
    gather.own()
    for load in loads:
        load.wait()
    for j in range(2):
        def join(rows):
            kept[j, rows, :] = (kept[j, rows, :].astype(f32) + came[j, rows, :].astype(f32)).astype(bf16)

        each_rows(128, 16, join)
        hops[2 + j].start()
    for k in (1, 2, 3):
        gather.step(k)
    gather.rest()
    for row in range(2):
        for pair in range(2):
            left = jnp.concatenate([buf[row, 2 * pair], buf[row, 2 * pair + 1]], axis=0)
            right = jnp.concatenate(
                [out_block(p1, nn, half) for nn in range(4) for half in range(2)], axis=1
            )
            datt_out[row, pair * 256 : pair * 256 + 256, :] = contract_last(left, right).astype(bf16)

    spread = Spread((o0, o1, o2, o3), (give_s, give_g, keep_s), me)

    def moved(half):
        def place(target):
            return target.at[:, pl.ds(pl.multiple_of(r * 256, 256), 256)]

        return wide.at[half], 0, place, half == 0

    for half in range(2):
        d_first = (jnp.where(half == 0, 1 - r, r)) * 1024

        def weight_tile(i, carry):
            columns = pl.ds(pl.multiple_of(d_first + i * 256, 256), 256)
            left = buf[:, :, :, columns].reshape(1024, 256)
            wide[half, i] = contract_first(left, att[...]).astype(bf16)
            return carry

        lax.fori_loop(0, 4, weight_tile, 0)
        spread.start(*moved(half))
    gather.sent()
    spread.wait(*moved(0))
    spread.wait(*moved(1))
    for hop in hops:
        hop.wait()


def branch_stage(*args):
    shard, width = 128, 2048
    return comm_call(
        branch_kernel, "branch", 5,
        (
            jax.ShapeDtypeStruct((shard, width), f32),
            jax.ShapeDtypeStruct((2, 512, 256), bf16),
        )
        + spread_shapes(128, 512)
        + (jax.ShapeDtypeStruct((2, 128, width), bf16),) * 2
        + (jax.ShapeDtypeStruct((128, width), bf16),) * 2,
        [vmem()] * 6 + [hbm()] * 6, [vmem(), vmem()] + [hbm()] * 8,
        gather_scratch(shard, width)
        + [pltpu.VMEM((2, 4, 256, 256), bf16)]
        + spread_sems(1)
        + [pltpu.SemaphoreType.DMA((4,))] * 2
        + [pltpu.VMEM((2, 128, width), bf16)] * 2
        + [pltpu.SemaphoreType.DMA((2, 2))],
        args, flops=10**10, sent=10**8,
    )


def unproject_kernel(
    q, kv, att, grad, lse, x, p1, tabs, gain, parts, mid, a_keep, b_keep, a_gate, b_gate, a_up, b_up, oa_in, ob_in,
    part_out, gain_out, o0, o1, o2, o3, hid_out, ra_out, rb_out, roa_out, rob_out,
    send, recv, both, wide_q, wide_kv, s_s, s_g, give_s, give_g, keep_s,
    mine, from_pt, from_up, from_dn, s0, s1, s2, s3, s4, s5,
    kept, came, acc, in_s, n_s, n_g, m_s, dkv,
):
    me = spot()
    r, n, w = me
    loads = []
    for j, (keep, gate, up) in enumerate(((a_keep, a_gate, a_up), (b_keep, b_gate, b_up))):
        loads += [
            pltpu.make_async_copy(keep.at[1, 0:2], kept.at[j], in_s.at[j, 0]),
            pltpu.make_async_copy(gate.at[1, 1], came.at[j, 0], in_s.at[j, 1]),
            pltpu.make_async_copy(up.at[1], came.at[j, 1], in_s.at[j, 2]),
        ]
    loads.append(pltpu.make_async_copy(parts.at[r], mine, m_s))
    for load in loads:
        load.start()
    greet(
        line_partners(r, n, w, 4)
        + [
            (n >= 1, nar_device(r, n, w, -1)),
            (n >= 2, nar_device(r, n, w, -2)),
            (n <= 2, nar_device(r, n, w, 1)),
            (n <= 1, nar_device(r, n, w, 2)),
        ]
        + square_partners(r, n, w)
    )
    scatter = Scatter(
        mine, parts.at[1 - r], (from_pt, from_up, from_dn), (s0, s1, s2, s3, s4, s5), me, 4
    )
    hops = [
        push(kept.at[0], ra_out, n_s.at[0], n_g.at[0], over_y(r, n, w)),
        push(kept.at[1], rb_out, n_s.at[1], n_g.at[1], over_x(r, n, w)),
        push(oa_in, roa_out, n_s.at[2], n_g.at[2], over_x(r, n, w)),
        push(ob_in, rob_out, n_s.at[3], n_g.at[3], over_y(r, n, w)),
    ]

    def copy(row, slot, by):
        return pltpu.make_async_remote_copy(
            send.at[row, slot], recv.at[row, slot], s_s.at[row, slot], s_g.at[row, slot],
            device_id=nar_device(r, n, w, by), device_id_type=MESH,
        )

    for i in range(4):
        scatter.pair(scatter.order(i)).start()
    for load in loads:
        load.wait()
    for j in range(2):
        for which in range(2):
            def join(rows):
                total = kept[j, which, rows, :].astype(f32) + came[j, which, rows, :].astype(f32)
                kept[j, which, rows, :] = total.astype(bf16)

            each_rows(128, 16, join)
        hops[j].start()
    hops[2].start()
    hops[3].start()
    scatter.advance((0, 1, 2, 3), ())

    def attention(i, carry):
        row, block = i // 4, i % 4
        first_query = 1024 + block * QUERIES
        here = pl.ds(pl.multiple_of(block * QUERIES, QUERIES), QUERIES)

        @pl.when(block == 0)
        def _():
            dkv[row] = jnp.zeros((1536, 128), f32)

        query = stack_low(q[row, here, :].astype(f32)).astype(bf16)
        grads = stack_high(grad[row, here, :].astype(f32))
        inner = jnp.sum(grads * stack_high(att[row, here, :].astype(f32)), axis=1, keepdims=True)
        grads = grads.astype(bf16)
        logsum = jnp.concatenate([lse[row, block]] * (KEYS // 128), axis=1)
        starts = tabs[row, here, 256:384]

        def key_tile(step, dq):
            tile = block // 2 + step
            rows = pl.ds(pl.multiple_of(tile * KEYS, KEYS), KEYS)
            pair = kv[row, rows, :]
            ok = allowed_tile(starts, tile, first_query)
            scores = contract_last(query, pair) * 0.125
            prob = jnp.where(ok, jnp.exp(scores - logsum), 0.0)
            grad_prob = contract_last(grads, pair)
            grad_scores = (prob * (grad_prob - inner)).astype(bf16)
            dkv[row, rows, :] += contract_first(grad_scores, query) * 0.125 + contract_first(
                prob.astype(bf16), grads
            )
            return dq + jnp.dot(grad_scores, pair, preferred_element_type=f32)

        dq = lax.fori_loop(0, 5, key_tile, jnp.zeros((4 * QUERIES, 128), f32), unroll=True)
        flat = unstack(dq, True) * 0.125
        cosine, sine = tabs[row, here, 0:128], -tabs[row, here, 128:256]
        there = pl.ds(pl.multiple_of(i * QUERIES, QUERIES), QUERIES)
        both[there, 0:128] = turn(flat[:, 0:128], cosine, sine).astype(bf16)
        both[there, 128:256] = turn(flat[:, 128:256], cosine, sine).astype(bf16)

        @pl.when(block == 3)
        def _():
            for slot, by in ((1, -1), (0, -2)):
                @pl.when(n >= -by)
                def _():
                    send[row, slot] = dkv[row, slot * 512 : slot * 512 + 512, :].astype(bf16)
                    copy(row, slot, by).start()

        @pl.when(i == 3)
        def _():
            scatter.advance((), (0,))

        return carry

    lax.fori_loop(0, 8, attention, 0)
    scatter.advance((), (1,))

    spread = Spread((o0, o1, o2, o3), (give_s, give_g, keep_s), (r, n, w))

    def moved_q(half):
        def place(target):
            return target.at[:, pl.ds(pl.multiple_of(r * 256, 256), 256)]

        return wide_q.at[half], 0, place, half == 0

    def moved_kv(half):
        def place(target):
            return target.at[:, pl.ds(pl.multiple_of(512 + r * 128, 128), 128)]

        return wide_kv.at[half], 1, place, half == 0

    def weight(half, columns, wide):
        d_first = (jnp.where(half == 0, 1 - r, r)) * 1024

        def tile(i, carry):
            d_cols = pl.ds(pl.multiple_of(d_first + i * 256, 256), 256)
            wide[half, i] = contract_first(x[:, d_cols], both[:, columns]).astype(bf16)
            return carry

        lax.fori_loop(0, 4, tile, 0)

    for half in range(2):
        weight(half, slice(0, 256), wide_q)
        spread.start(*moved_q(half))
    lane = lax.broadcasted_iota(jnp.int32, (128, 128), 1)
    for row in range(2):
        for slot, by in ((1, -1), (0, -2)):
            @pl.when(n <= 3 + by)
            def _():
                copy(row, slot, by).wait_recv()

        def tile(i, carry):
            rows = pl.ds(pl.multiple_of(i * 128, 128), 128)
            total = dkv[row, pl.ds(pl.multiple_of(1024 + i * 128, 128), 128), :]
            zero = jnp.zeros_like(total)
            total = total + jnp.where(n <= 2, recv[row, 1, rows, :].astype(f32), zero)
            total = total + jnp.where(n <= 1, recv[row, 0, rows, :].astype(f32), zero)
            turned = turn(total, tabs[row, rows, 0:128], -tabs[row, rows, 128:256])
            both[pl.ds(pl.multiple_of(row * 512 + i * 128, 128), 128), 256:384] = jnp.where(
                lane < 64, turned, total
            ).astype(bf16)
            return carry

        lax.fori_loop(0, 4, tile, 0)
    for half in range(2):
        weight(half, slice(256, 384), wide_kv)
        spread.start(*moved_kv(half))
    scatter.advance((), (2,))
    gain_out[...] = jnp.zeros_like(gain_out)

    def model_tile(dt, carry):
        nn, half = dt // 2, dt % 2
        columns = pl.ds(pl.multiple_of(dt * 256, 256), 256)
        inner = pl.ds(pl.multiple_of(half * 256, 256), 256)
        right = p1[nn, inner, 0:384]
        for row in range(2):
            for block in range(2):
                first = row * 512 + block * 256
                part = contract_last(both[first : first + 256, :], right)
                terms = part * x[first : first + 256, columns].astype(f32)
                gain_out[:, columns] += jnp.sum(terms.reshape(32, 8, 256), axis=0)
                part_out[row, 2 * block, :, columns] = part[0:128].astype(bf16)
                part_out[row, 2 * block + 1, :, columns] = part[128:256].astype(bf16)
        return carry

    lax.fori_loop(0, 8, model_tile, 0)
    gain_out[...] = gain_out[...] / gain[...]
    scatter.advance((), (3,))
    scatter.total(acc)

    def last(rows):
        hid_out[rows, :] = (acc[rows, :] + mid[rows, :]).astype(bf16)

    each_rows(128, 16, last)
    scatter.sent()
    for row in range(2):
        for slot, by in ((1, -1), (0, -2)):
            @pl.when(n >= -by)
            def _():
                copy(row, slot, by).wait_send()

    for half in range(2):
        spread.wait(*moved_q(half))
        spread.wait(*moved_kv(half))
    for hop in hops:
        hop.wait()


def unproject(*args):
    return comm_call(
        unproject_kernel, "unproject", 6,
        (
            jax.ShapeDtypeStruct((2, 4, 128, 2048), bf16),
            jax.ShapeDtypeStruct((8, 2048), f32),
        )
        + spread_shapes(128, 768)
        + (jax.ShapeDtypeStruct((128, 2048), bf16),)
        + (jax.ShapeDtypeStruct((2, 128, 2048), bf16),) * 2
        + (jax.ShapeDtypeStruct((2, 128, 512), bf16),) * 2,
        [vmem()] * 9 + [hbm(), vmem()] + [hbm()] * 8,
        [vmem(), vmem()] + [hbm()] * 4 + [vmem()] + [hbm()] * 4,
        [
            pltpu.VMEM((2, 2, 512, 128), bf16),
            pltpu.VMEM((2, 2, 512, 128), bf16),
            pltpu.VMEM((1024, 384), bf16),
            pltpu.VMEM((2, 4, 256, 256), bf16),
            pltpu.VMEM((2, 4, 256, 128), bf16),
            pltpu.SemaphoreType.DMA((2, 2)),
            pltpu.SemaphoreType.DMA((2, 2)),
        ]
        + spread_sems(2)
        + [pltpu.VMEM((4, 128, 2048), bf16)]
        + scatter_bufs(128, 2048) + scatter_sems()
        + [
            pltpu.VMEM((2, 2, 128, 2048), bf16),
            pltpu.VMEM((2, 2, 128, 2048), bf16),
            pltpu.VMEM((128, 2048), f32),
            pltpu.SemaphoreType.DMA((2, 3)),
            pltpu.SemaphoreType.DMA((4,)),
            pltpu.SemaphoreType.DMA((4,)),
            pltpu.SemaphoreType.DMA(()),
            pltpu.VMEM((2, 1536, 128), f32),
        ],
        args, flops=10**10, sent=10**7,
    )


def leave_kernel(
    parts, hidden, gain, gmid, gains, qa_send, qa_keep, qb_send, qb_keep, oa_keep, ob_keep, oa_in, ob_in,
    grad_out, ga_out, query_out, key_out, value_out, output_out,
    mine, from_pt, from_up, from_dn, s0, s1, s2, s3, s4, s5,
    acc, over_wid, summed, over_rest, w_s, w_g, t_s, t_g,
    first_q, next_q, then_q, next_o, then_o, kv, n_s, n_g, k0, k1, k2, k3, m_s,
):
    me = spot()
    r, n, w = me
    own_parts = pltpu.make_async_copy(parts.at[r], mine, m_s)
    own_parts.start()
    partners = [(w != j, (r, n, jnp.int32(j))) for j in range(4)]
    partners += [
        ((r != a) | (n != b), (jnp.int32(a), jnp.int32(b), w)) for a in range(2) for b in range(4)
    ]
    greet(partners)
    kv_gather = Gather(kv, (k0, k1, k2, k3), me, 4, pair=False)
    x_side, y_side = over_x(r, n, w), over_y(r, n, w)
    q_hops = [
        push(qa_send, first_q.at[0], n_s.at[0], n_g.at[0], x_side),
        push(qb_send, first_q.at[1], n_s.at[1], n_g.at[1], y_side),
    ]
    q_later = [
        push(next_q.at[0], then_q.at[0], n_s.at[2], n_g.at[2], y_side),
        push(next_q.at[1], then_q.at[1], n_s.at[3], n_g.at[3], x_side),
    ]
    o_hops = [
        push(next_o.at[0], then_o.at[0], n_s.at[4], n_g.at[4], y_side),
        push(next_o.at[1], then_o.at[1], n_s.at[5], n_g.at[5], x_side),
    ]
    for hop in q_hops:
        hop.start()
    scatter = Scatter(
        mine, parts.at[1 - r], (from_pt, from_up, from_dn), (s0, s1, s2, s3, s4, s5), me, 4
    )
    for i in range(4):
        scatter.pair(scatter.order(i)).start()

    def wid_copy(j, slot):
        return pltpu.make_async_remote_copy(
            gains, over_wid.at[slot], w_s.at[j], w_g.at[slot],
            device_id=(r, n, jnp.int32(j)), device_id_type=MESH,
        )

    def rest_copy(a, b, slot):
        return pltpu.make_async_remote_copy(
            summed, over_rest.at[slot], t_s.at[a * 4 + b], t_g.at[slot],
            device_id=(jnp.int32(a), jnp.int32(b), w), device_id_type=MESH,
        )

    for j in range(4):
        @pl.when(w != j)
        def _():
            wid_copy(j, w).start()

    own_parts.wait()
    scatter.advance((0, 1, 2), ())
    for j, (keep, came) in enumerate(((oa_keep, oa_in), (ob_keep, ob_in))):
        next_o[j] = (keep[1].astype(f32) + came[1].astype(f32)).astype(bf16)
        o_hops[j].start()
    summed[...] = gains[...]
    for j in range(4):
        @pl.when(w != j)
        def _():
            wid_copy(j, j).wait_recv()
            summed[...] += over_wid[j]

    for a in range(2):
        for b in range(4):
            @pl.when((r != a) | (n != b))
            def _():
                rest_copy(a, b, r * 4 + n).start()

    for j, keep in enumerate((qa_keep, qb_keep)):
        q_hops[j].wait_recv()
        next_q[j] = (keep[1].astype(f32) + first_q[j, 1].astype(f32)).astype(bf16)
        q_later[j].start()
    scatter.advance((), (0,))
    for j, keep in enumerate((qa_keep, qb_keep)):
        q_later[j].wait_recv()
        total = keep[0].astype(f32) + first_q[j, 0].astype(f32) + then_q[j].astype(f32)
        query_out[j * 128 : j * 128 + 128, :] = total[:, 0:512]
        kv[0, w, j * 128 : j * 128 + 128, :] = total[:, 512:768].astype(bf16)
    kv_gather.own()
    scatter.advance((3,), (1, 2))
    kv_gather.advance((), (1,))
    scatter.advance((), (3,))
    kv_gather.advance((), (2,))
    for j, (keep, came) in enumerate(((oa_keep, oa_in), (ob_keep, ob_in))):
        o_hops[j].wait_recv()
        output_out[j * 128 : j * 128 + 128, :] = (
            keep[0].astype(f32) + came[0].astype(f32) + then_o[j].astype(f32)
        )
    mine_block = r * 4 + n
    ga_out[0:1] = summed[pl.ds(mine_block, 1), :]
    ga_out[1:2] = summed[pl.ds(mine_block + 8, 1), :]
    for a in range(2):
        for b in range(4):
            @pl.when((r != a) | (n != b))
            def _():
                slot = a * 4 + b
                rest_copy(a, b, slot).wait_recv()
                ga_out[0:1] += over_rest[slot, pl.ds(mine_block, 1), :]
                ga_out[1:2] += over_rest[slot, pl.ds(mine_block + 8, 1), :]

    scatter.total(acc)

    def last(rows):
        grad = norm_back(hidden[rows, :].astype(f32), gain[...], acc[rows, :])
        grad_out[rows, :] = (grad + gmid[rows, :]).astype(bf16)

    each_rows(hidden.shape[0], 16, last)
    kv_gather.advance((1, 2, 3), (3,))
    lane = lax.broadcasted_iota(jnp.int32, (256, 128), 1)
    for j in range(4):
        even, odd = kv[0, j, :, 0:128].astype(f32), kv[0, j, :, 128:256].astype(f32)
        here = slice(j * 128, j * 128 + 128)
        key_out[:, here] = jnp.where(lane < 64, even, pltpu.roll(odd, 64, 1))
        value_out[:, here] = jnp.where(lane < 64, pltpu.roll(even, 64, 1), odd)
    scatter.sent()
    kv_gather.sent()
    for hop in q_hops + q_later + o_hops:
        hop.wait_send()
    for j in range(4):
        @pl.when(w != j)
        def _():
            wid_copy(j, w).wait_send()

    for a in range(2):
        for b in range(4):
            @pl.when((r != a) | (n != b))
            def _():
                rest_copy(a, b, r * 4 + n).wait_send()


def leave(*args):
    shard, width = 128, 2048
    grad = jax.ShapeDtypeStruct((256, 512), f32)
    return comm_call(
        leave_kernel, "leave", 7,
        (jax.ShapeDtypeStruct((shard, width), bf16), jax.ShapeDtypeStruct((8, 256), f32))
        + (grad,) * 4,
        [hbm()] + [vmem()] * 12, [vmem()] * 6,
        [pltpu.VMEM((4, shard, width), bf16)]
        + scatter_bufs(shard, width) + scatter_sems()
        + [
            pltpu.VMEM((shard, width), f32),
            pltpu.VMEM((4, 16, 256), f32),
            pltpu.VMEM((16, 256), f32),
            pltpu.VMEM((8, 16, 256), f32),
            pltpu.SemaphoreType.DMA((4,)),
            pltpu.SemaphoreType.DMA((4,)),
            pltpu.SemaphoreType.DMA((8,)),
            pltpu.SemaphoreType.DMA((8,)),
            pltpu.VMEM((2, 2, 128, 768), bf16),
            pltpu.VMEM((2, 128, 768), bf16),
            pltpu.VMEM((2, 128, 768), bf16),
            pltpu.VMEM((2, 128, 512), bf16),
            pltpu.VMEM((2, 128, 512), bf16),
            pltpu.VMEM((1, 4, 256, 256), bf16),
            pltpu.SemaphoreType.DMA((6,)),
            pltpu.SemaphoreType.DMA((6,)),
        ]
        + gather_sems()
        + [pltpu.SemaphoreType.DMA(())],
        args, flops=10**10, sent=10**8,
    )


def local_fast(
    hidden_in, doc_lengths, w_query, w_key, w_value, w_output, w_gate, w_up, w_down,
    gain_attn, gain_ffn, grad_out,
):
    r, n, w = spot()
    hidden, grad_top = hidden_in[0], grad_out[0]
    gain_a, gain_f = gain_attn[None], gain_ffn[None]
    def half(weight, axis):
        size = weight.shape[axis] // 2
        return lax.dynamic_slice_in_dim(weight, r * size, size, axis)

    head = (w * 2 + r) * HD
    kv_pack = jnp.concatenate(
        [lax.dynamic_slice_in_dim(w_key, head, HD, 1), lax.dynamic_slice_in_dim(w_value, head, HD, 1)],
        axis=1,
    )
    out_half = half(w_output, 0)
    p1_shard = jnp.concatenate(
        [half(w_query, 1), kv_pack, jnp.concatenate([out_half[:, :256], out_half[:, 256:]], axis=0)],
        axis=1,
    )
    down_half = half(w_down, 0)
    gate_own, up_own = half(w_gate, 1), half(w_up, 1)
    down_own = jnp.concatenate([down_half[:512], down_half[512:]], axis=1)

    token_ids = n * 512 + jnp.arange(512, dtype=jnp.int32)
    doc_start, places = doc_layout(doc_lengths[0], token_ids)
    angles = places.astype(f32)[:, None] * inverse_freq()[None, :]
    cosine, sine = jnp.cos(angles), jnp.sin(angles)
    start_here = (doc_start - (n - 2) * 512).astype(f32)
    tab = jnp.concatenate(
        [cosine] * 4 + [-sine, sine] * 2 + [jnp.broadcast_to(start_here[:, None], (512, 128))],
        axis=1,
    )

    q, rows, tabs, p1, down_a, kv, tops = enter(
        hidden, gain_a, tab, grad_top, p1_shard, down_own
    )
    rows2 = rows.reshape(1024, 2048)
    kv_flat = kv.reshape(2, 1536, 128)
    att, lse, mid, ffn_rows, gate_all, up_all, down_b = middle_stage(
        q, kv_flat, tabs, p1, hidden, gain_f, gate_own, up_own, down_own
    )
    parts, total, gain_f_part, a_send, a_keep, b_send, b_keep, ra_dg, rb_dg = ffn_stage(
        ffn_rows.reshape(1024, 2048), tops, grad_top,
        gate_own, gate_all, up_own, up_all, down_own, down_a, down_b, gain_f,
    )
    gmid, datt, oa_send, oa_keep, ob_send, ob_keep, ra_u, rb_u, la_d, lb_d = branch_stage(
        total, mid, grad_top, gain_f, p1, att.reshape(1024, 256),
        a_send, b_send, a_keep, b_keep, ra_dg, rb_dg,
    )
    (
        dparts, gain_a_part, qa_send, qa_keep, qb_send, qb_keep,
        hidden_out, ra_last, rb_last, oa_came, ob_came,
    ) = unproject(
        q, kv_flat, att, datt, lse, rows2, p1, tabs, gain_a, parts, mid,
        a_keep, b_keep, ra_dg, rb_dg, ra_u, rb_u, oa_send, ob_send,
    )
    gains = jnp.concatenate(
        [gain_f_part.sum(axis=0).reshape(8, 256), gain_a_part.sum(axis=0).reshape(8, 256)], axis=0
    )
    grad_in, gain_sums, grad_query, grad_key, grad_value, output_sum = leave(
        dparts, hidden, gain_a, gmid, gains,
        qa_send, qa_keep, qb_send, qb_keep, oa_keep, ob_keep, oa_came, ob_came,
    )

    def joined(which):
        def half_rows(keep, came, last):
            return keep[0, which].astype(f32) + came.astype(f32) + last.astype(f32)

        a_came, b_came, a_last, b_last = (
            (ra_dg[1, 0], rb_dg[1, 0], ra_last[0], rb_last[0]),
            (ra_u[0], rb_u[0], ra_last[1], rb_last[1]),
            (ra_dg[0, 0], rb_dg[0, 0], la_d, lb_d),
        )[which]
        return jnp.concatenate(
            [half_rows(a_keep, a_came, a_last), half_rows(b_keep, b_came, b_last)], axis=0
        )

    return (
        hidden_out[None],
        grad_in[None],
        grad_query,
        grad_key,
        grad_value,
        output_sum.T,
        joined(0),
        joined(1),
        joined(2).T,
        gain_sums[1],
        gain_sums[0],
    )


def solution(mesh):
    in_specs = (
        P("row", ("nar", "wid"), None),
        P("row", None),
        P("nar", "wid"),
        P("nar", None),
        P("nar", None),
        P("wid", "nar"),
        P("nar", "wid"),
        P("nar", "wid"),
        P("wid", "nar"),
        P(),
        P(),
        P("row", ("nar", "wid"), None),
    )
    out_specs = (
        P("row", ("nar", "wid"), None),
        P("row", ("nar", "wid"), None),
        P(("row", "nar"), "wid"),
        P(("row", "nar"), None),
        P(("row", "nar"), None),
        P("wid", ("row", "nar")),
        P(("row", "nar"), "wid"),
        P(("row", "nar"), "wid"),
        P("wid", ("row", "nar")),
        P(("row", "nar")),
        P(("row", "nar")),
    )
    sizes = dict(mesh.shape)
    fits = sizes == {"row": 2, "nar": 4, "wid": 4}

    def body(*args):
        small = args[0].shape == (1, 128, 2048)
        return (local_fast if fits and small else local)(*args)

    return jax.shard_map(body, mesh=mesh, in_specs=in_specs, out_specs=out_specs, check_vma=False)
```

```python
import math

import jax
import jax.numpy as jnp
from jax import lax
from jax.experimental import pallas as pl
from jax.experimental.pallas import tpu as pltpu
from jax.sharding import PartitionSpec as P

H = 32
KV = 8
HD = 64


norm_eps = 1e-05
masked_score = -1e30


def inverse_freq():
    listed = []
    for pair_index in range(HD // 2):
        base_freq = 500000.0 ** (-2.0 * pair_index / HD)
        wavelength = 2.0 * math.pi / base_freq
        smoothing = (8192.0 / wavelength - 1.0) / 3.0
        blended = (1.0 - smoothing) * base_freq / 32.0 + smoothing * base_freq
        if wavelength < 2048.0:
            listed.append(base_freq)
        elif wavelength > 8192.0:
            listed.append(base_freq / 32.0)
        else:
            listed.append(blended)
    return jnp.asarray(listed, dtype=jnp.float32)


def rotate(values, cosine_table, sine_table):
    half_dim = HD // 2
    first_half = values[..., :half_dim]
    second_half = values[..., half_dim:]
    return jnp.concatenate(
        [
            first_half * cosine_table - second_half * sine_table,
            second_half * cosine_table + first_half * sine_table,
        ],
        axis=-1,
    )


def rotate_back(grads_in, cosine_table, sine_table):
    half_dim = HD // 2
    first_half = grads_in[..., :half_dim]
    second_half = grads_in[..., half_dim:]
    return jnp.concatenate(
        [
            first_half * cosine_table + second_half * sine_table,
            second_half * cosine_table - first_half * sine_table,
        ],
        axis=-1,
    )


def doc_layout(lengths_row, token_ids):
    ends_at = jnp.cumsum(lengths_row, dtype=jnp.int32)
    starts_at = ends_at - lengths_row
    inside = (token_ids[:, None] >= starts_at[None, :]) & (token_ids[:, None] < ends_at[None, :])
    doc_start = jnp.sum(jnp.where(inside, starts_at[None, :], 0), axis=1, dtype=jnp.int32)
    return (doc_start, token_ids - doc_start)


def norm_forward(values, gain_vector):
    root_inv = lax.rsqrt(jnp.mean(values * values, axis=-1, keepdims=True) + norm_eps)
    return (root_inv, (values * root_inv * gain_vector).astype(jnp.bfloat16))


def norm_backward(values, root_inv, gain_vector, grad_normed):
    weighted = grad_normed * gain_vector
    inner_sum = jnp.mean(weighted * values, axis=-1, keepdims=True)
    grad_values = root_inv * weighted - values * (root_inv * root_inv * root_inv) * inner_sum
    gain_term = jnp.sum(grad_normed * values * root_inv, axis=0)
    return (grad_values, gain_term)


def contract_last(left_side, right_side):
    return lax.dot_general(
        left_side, right_side, (((1,), (1,)), ((), ())), preferred_element_type=jnp.float32
    )


def contract_first(left_side, right_side):
    return lax.dot_general(
        left_side, right_side, (((0,), (0,)), ((), ())), preferred_element_type=jnp.float32
    )


def local(
    hidden_in,
    doc_lengths,
    w_query,
    w_key,
    w_value,
    w_output,
    w_gate,
    w_up,
    w_down,
    gain_attn,
    gain_ffn,
    grad_out,
):
    wid_count = lax.axis_size("wid")
    nar_count = lax.axis_size("nar")
    wid_index = lax.axis_index("wid")
    nar_index = lax.axis_index("nar")
    local_tokens = hidden_in.shape[1]
    block_tokens = local_tokens * wid_count
    seq_length = block_tokens * nar_count
    query_heads = w_query.shape[1] // HD
    group_size = H // KV
    kv_local = max(query_heads // group_size, 1)
    heads_per_kv = query_heads // kv_local
    kv_first = wid_index * query_heads // group_size
    query_block = min(512, block_tokens)
    block_count = block_tokens // query_block
    item_count = block_count * query_heads
    attn_scale = HD ** (-0.5)
    query_full, key_full, value_full, output_full, gate_full, up_full, down_full = (
        lax.all_gather(w_query, "nar", axis=0, tiled=True),
        lax.all_gather(w_key, "nar", axis=0, tiled=True),
        lax.all_gather(w_value, "nar", axis=0, tiled=True),
        lax.all_gather(w_output, "nar", axis=1, tiled=True),
        lax.all_gather(w_gate, "nar", axis=0, tiled=True),
        lax.all_gather(w_up, "nar", axis=0, tiled=True),
        lax.all_gather(w_down, "nar", axis=1, tiled=True),
    )
    key_local = lax.dynamic_slice_in_dim(key_full, kv_first * HD, kv_local * HD, 1)
    value_local = lax.dynamic_slice_in_dim(value_full, kv_first * HD, kv_local * HD, 1)
    token_ids = nar_index * block_tokens + jnp.arange(block_tokens, dtype=jnp.int32)
    doc_start, places = doc_layout(doc_lengths[0], token_ids)
    angles = places.astype(jnp.float32)[:, None] * inverse_freq()[None, :]
    cosine_table = jnp.cos(angles)[:, None, :]
    sine_table = jnp.sin(angles)[:, None, :]
    key_ids = jnp.arange(seq_length, dtype=jnp.int32)
    residual = hidden_in[0].astype(jnp.float32)
    root_attn, normed_attn = norm_forward(residual, gain_attn)
    normed_rows = lax.all_gather(normed_attn, "wid", axis=0, tiled=True)
    query_pre = jnp.dot(normed_rows, query_full, preferred_element_type=jnp.float32)
    key_pre = jnp.dot(normed_rows, key_local, preferred_element_type=jnp.float32)
    value_rows = jnp.dot(normed_rows, value_local, preferred_element_type=jnp.float32).astype(
        jnp.bfloat16
    )
    query_rot = (
        rotate(query_pre.reshape(block_tokens, query_heads, HD), cosine_table, sine_table)
        .astype(jnp.bfloat16)
        .reshape(block_tokens, query_heads * HD)
    )
    key_rot = (
        rotate(key_pre.reshape(block_tokens, kv_local, HD), cosine_table, sine_table)
        .astype(jnp.bfloat16)
        .reshape(block_tokens, kv_local * HD)
    )
    key_seq, value_seq = (
        lax.all_gather(key_rot, "nar", axis=0, tiled=True),
        lax.all_gather(value_rows, "nar", axis=0, tiled=True),
    )

    def item_inputs(item_index):
        block_index = item_index // query_heads
        head_index = item_index % query_heads
        kv_index = head_index // heads_per_kv
        row_first = block_index * query_block
        query_part = lax.dynamic_slice(query_rot, (row_first, head_index * HD), (query_block, HD))
        key_head = lax.dynamic_slice_in_dim(key_seq, kv_index * HD, HD, 1)
        value_head = lax.dynamic_slice_in_dim(value_seq, kv_index * HD, HD, 1)
        query_ids = lax.dynamic_slice_in_dim(token_ids, row_first, query_block, 0)
        query_starts = lax.dynamic_slice_in_dim(doc_start, row_first, query_block, 0)
        allowed = (key_ids[None, :] <= query_ids[:, None]) & (
            key_ids[None, :] >= query_starts[:, None]
        )
        scores = contract_last(query_part, key_head) * attn_scale
        return (
            row_first,
            head_index,
            kv_index,
            query_part,
            key_head,
            value_head,
            jnp.where(allowed, scores, masked_score),
        )

    def attend(item_index):
        row_first, head_index, kv_index, query_part, key_head, value_head, scores = item_inputs(
            item_index
        )
        row_max = jnp.max(scores, axis=1, keepdims=True)
        exp_scores = jnp.exp(scores - row_max)
        row_total = jnp.sum(exp_scores, axis=1, keepdims=True)
        probability = (exp_scores / row_total).astype(jnp.bfloat16)
        attended = jnp.dot(probability, value_head, preferred_element_type=jnp.float32)
        return (attended, (row_max + jnp.log(row_total))[:, 0])

    attended_items, logsum_items = lax.map(attend, jnp.arange(item_count, dtype=jnp.int32))
    attended_rows = (
        attended_items.reshape(block_count, query_heads, query_block, HD)
        .transpose(0, 2, 1, 3)
        .reshape(block_tokens, query_heads * HD)
        .astype(jnp.bfloat16)
    )
    rows_here = attended_rows
    branch_attn = lax.psum_scatter(
        jnp.dot(rows_here, output_full, preferred_element_type=jnp.float32),
        "wid",
        scatter_dimension=0,
        tiled=True,
    )
    middle = residual + branch_attn
    root_ffn, normed_ffn = norm_forward(middle, gain_ffn)
    ffn_rows = lax.all_gather(normed_ffn, "wid", axis=0, tiled=True)
    gate_proj = jnp.dot(ffn_rows, gate_full, preferred_element_type=jnp.float32)
    up_proj = jnp.dot(ffn_rows, up_full, preferred_element_type=jnp.float32)
    gate_sigmoid = jax.nn.sigmoid(gate_proj)
    gate_silu = gate_proj * gate_sigmoid
    activated = (gate_silu * up_proj).astype(jnp.bfloat16)
    rows_here = activated
    branch_ffn = lax.psum_scatter(
        jnp.dot(rows_here, down_full, preferred_element_type=jnp.float32).astype(jnp.bfloat16),
        "wid",
        scatter_dimension=0,
        tiled=True,
    ).astype(jnp.float32)
    hidden_out = (middle + branch_ffn).astype(jnp.bfloat16)[None]
    grad_top = grad_out[0]
    grad_rows = lax.all_gather(grad_top, "wid", axis=0, tiled=True)
    grad_activated = contract_last(grad_rows, down_full)
    down_weight_grad = contract_first(activated, grad_rows)
    silu_slope = gate_sigmoid * (1.0 + gate_proj * (1.0 - gate_sigmoid))
    grad_gate_b = (grad_activated * up_proj * silu_slope).astype(jnp.bfloat16)
    grad_up_b = (grad_activated * gate_silu).astype(jnp.bfloat16)
    gate_weight_grad = contract_first(ffn_rows, grad_gate_b)
    up_weight_grad = contract_first(ffn_rows, grad_up_b)
    grad_normed_ffn = lax.psum_scatter(
        contract_last(grad_gate_b, gate_full) + contract_last(grad_up_b, up_full),
        "wid",
        scatter_dimension=0,
        tiled=True,
    )
    grad_middle, gain_ffn_term = norm_backward(middle, root_ffn, gain_ffn, grad_normed_ffn)
    grad_middle = grad_middle + grad_top.astype(jnp.float32)
    grad_branch = grad_middle.astype(jnp.bfloat16)
    branch_rows = lax.all_gather(grad_branch, "wid", axis=0, tiled=True)
    grad_attended = contract_last(branch_rows, output_full).astype(jnp.bfloat16)
    output_weight_grad = contract_first(attended_rows, branch_rows)

    def attend_back(carried, item_index):
        key_grad, value_grad = carried
        row_first, head_index, kv_index, query_part, key_head, value_head, scores = item_inputs(
            item_index
        )
        logsum = lax.dynamic_index_in_dim(logsum_items, item_index, 0, keepdims=False)
        probability = jnp.exp(scores - logsum[:, None])
        grad_part = lax.dynamic_slice(
            grad_attended, (row_first, head_index * HD), (query_block, HD)
        )
        grad_prob = contract_last(grad_part, value_head)
        inner_sum = jnp.sum(probability * grad_prob, axis=1, keepdims=True)
        grad_scores = (probability * (grad_prob - inner_sum)).astype(jnp.bfloat16)
        query_grad = jnp.dot(grad_scores, key_head, preferred_element_type=jnp.float32) * attn_scale
        key_part = contract_first(grad_scores, query_part) * attn_scale
        value_part = contract_first(probability.astype(jnp.bfloat16), grad_part)
        key_old = lax.dynamic_slice_in_dim(key_grad, kv_index * HD, HD, 1)
        key_grad = lax.dynamic_update_slice_in_dim(key_grad, key_old + key_part, kv_index * HD, 1)
        value_old = lax.dynamic_slice_in_dim(value_grad, kv_index * HD, HD, 1)
        value_grad = lax.dynamic_update_slice_in_dim(
            value_grad, value_old + value_part, kv_index * HD, 1
        )
        return ((key_grad, value_grad), query_grad)

    zero_grads = jnp.zeros((seq_length, kv_local * HD), jnp.float32)
    (key_grad_seq, value_grad_seq), query_grad_items = lax.scan(
        attend_back, (zero_grads, zero_grads), jnp.arange(item_count, dtype=jnp.int32)
    )
    key_grad_block, value_grad_block = (
        lax.psum_scatter(
            key_grad_seq.astype(jnp.bfloat16), "nar", scatter_dimension=0, tiled=True
        ).astype(jnp.float32),
        lax.psum_scatter(
            value_grad_seq.astype(jnp.bfloat16), "nar", scatter_dimension=0, tiled=True
        ).astype(jnp.float32),
    )
    query_grad_rows = (
        query_grad_items.reshape(block_count, query_heads, query_block, HD)
        .transpose(0, 2, 1, 3)
        .reshape(block_tokens, query_heads, HD)
    )
    query_grad_b = (
        rotate_back(query_grad_rows, cosine_table, sine_table)
        .astype(jnp.bfloat16)
        .reshape(block_tokens, query_heads * HD)
    )
    key_grad_b = (
        rotate_back(key_grad_block.reshape(block_tokens, kv_local, HD), cosine_table, sine_table)
        .astype(jnp.bfloat16)
        .reshape(block_tokens, kv_local * HD)
    )
    value_grad_b = value_grad_block.astype(jnp.bfloat16)
    query_weight_grad = contract_first(normed_rows, query_grad_b)
    key_weight_grad = contract_first(normed_rows, key_grad_b)
    value_weight_grad = contract_first(normed_rows, value_grad_b)
    grad_normed_attn = lax.psum_scatter(
        (
            contract_last(query_grad_b, query_full)
            + contract_last(key_grad_b, key_local)
            + contract_last(value_grad_b, value_local)
        ).astype(jnp.bfloat16),
        "wid",
        scatter_dimension=0,
        tiled=True,
    ).astype(jnp.float32)
    grad_residual, gain_attn_term = norm_backward(residual, root_attn, gain_attn, grad_normed_attn)
    grad_in = (grad_residual + grad_middle).astype(jnp.bfloat16)[None]
    summed = (
        lax.psum_scatter(
            query_weight_grad.astype(jnp.bfloat16), ("row", "nar"), scatter_dimension=0, tiled=True
        ).astype(jnp.float32),
        lax.psum_scatter(
            key_weight_grad.astype(jnp.bfloat16), ("row", "nar"), scatter_dimension=0, tiled=True
        ).astype(jnp.float32),
        lax.psum_scatter(
            value_weight_grad.astype(jnp.bfloat16), ("row", "nar"), scatter_dimension=0, tiled=True
        ).astype(jnp.float32),
        lax.psum_scatter(
            output_weight_grad.astype(jnp.bfloat16), ("row", "nar"), scatter_dimension=1, tiled=True
        ).astype(jnp.float32),
        lax.psum_scatter(
            gate_weight_grad.astype(jnp.bfloat16), ("row", "nar"), scatter_dimension=0, tiled=True
        ).astype(jnp.float32),
        lax.psum_scatter(
            up_weight_grad.astype(jnp.bfloat16), ("row", "nar"), scatter_dimension=0, tiled=True
        ).astype(jnp.float32),
        lax.psum_scatter(
            down_weight_grad.astype(jnp.bfloat16), ("row", "nar"), scatter_dimension=1, tiled=True
        ).astype(jnp.float32),
        lax.psum_scatter(
            gain_attn_term.astype(jnp.bfloat16), ("row", "nar"), scatter_dimension=0, tiled=True
        ).astype(jnp.float32),
        lax.psum_scatter(
            gain_ffn_term.astype(jnp.bfloat16), ("row", "nar"), scatter_dimension=0, tiled=True
        ).astype(jnp.float32),
    )
    (
        grad_query,
        key_sum,
        value_sum,
        grad_output,
        grad_gate,
        grad_up,
        grad_down,
        gain_attn_sum,
        gain_ffn_sum,
    ) = summed
    key_all, value_all, gain_attn_all, gain_ffn_all = (
        lax.all_gather(key_sum.astype(jnp.bfloat16), "wid", axis=1, tiled=True).astype(
            key_sum.dtype
        ),
        lax.all_gather(value_sum.astype(jnp.bfloat16), "wid", axis=1, tiled=True).astype(
            value_sum.dtype
        ),
        lax.all_gather(gain_attn_sum.astype(jnp.bfloat16), "wid", axis=0, tiled=True).astype(
            gain_attn_sum.dtype
        ),
        lax.all_gather(gain_ffn_sum.astype(jnp.bfloat16), "wid", axis=0, tiled=True).astype(
            gain_ffn_sum.dtype
        ),
    )
    shard_rows = key_sum.shape[0]
    repeats = wid_count * kv_local // KV
    grad_key = key_all.reshape(shard_rows, KV, repeats, HD).sum(axis=2).reshape(shard_rows, KV * HD)
    grad_value = (
        value_all.reshape(shard_rows, KV, repeats, HD).sum(axis=2).reshape(shard_rows, KV * HD)
    )
    grad_gain_attn = gain_attn_all.reshape(wid_count, shard_rows).sum(axis=0)
    grad_gain_ffn = gain_ffn_all.reshape(wid_count, shard_rows).sum(axis=0)
    return (
        hidden_out,
        grad_in,
        grad_query,
        grad_key,
        grad_value,
        grad_output,
        grad_gate,
        grad_up,
        grad_down,
        grad_gain_attn,
        grad_gain_ffn,
    )


MESH = pl.DeviceIdType.MESH
bf16 = jnp.bfloat16
f32 = jnp.float32
VMEM_LIMIT = 60 * 2**20


def spot():
    return lax.axis_index("row"), lax.axis_index("nar"), lax.axis_index("wid")


def greet(partners):
    barrier = pltpu.get_barrier_semaphore()
    total = 0
    for there, device in partners:
        @pl.when(there)
        def _():
            pl.semaphore_signal(barrier, inc=1, device_id=device, device_id_type=MESH)

        total = total + there.astype(jnp.int32)
    pl.semaphore_wait(barrier, total)


def line_partners(r, n, w, wid_count):
    return [
        (w < wid_count - 1, (r, n, jnp.minimum(w + 1, wid_count - 1))),
        (w > 0, (r, n, jnp.maximum(w - 1, 0))),
        (w >= 0, (1 - r, n, w)),
    ]


def each_rows(count, step, body):
    def run(i, carry):
        body(pl.ds(pl.multiple_of(i * step, step), step))
        return carry

    lax.fori_loop(0, count // step, run, 0)


def square_partners(r, n, w):
    return [(n >= 0, over_x(r, n, w)), (n >= 0, over_y(r, n, w))]


def over_x(r, n, w):
    return (r, n + 1 - 2 * (n % 2), w)


def over_y(r, n, w):
    return (r, (n + 2) % 4, w)


def push(source, target, s_s, s_g, device):
    return pltpu.make_async_remote_copy(
        source, target, s_s, s_g, device_id=device, device_id_type=MESH
    )


class Square:
    def __init__(self, shard, full, sems, me):
        self.shard, self.full = shard, full
        self.sent, self.got = sems
        r, n, w = me
        self.n, self.x, self.y = n, n + 1 - 2 * (n % 2), (n + 2) % 4
        self.by_x, self.by_y = over_x(*me), over_y(*me)
        size = shard.shape[0] // 2
        self.upper, self.lower = pl.ds(0, size), pl.ds(size, size)

    def first(self, k, place):
        return push(
            self.shard, self.full.at[place], self.sent.at[k], self.got.at[k],
            (self.by_x, self.by_y)[k],
        )

    def second(self, k, place):
        part = self.full.at[place, (self.upper, self.lower)[k]]
        return push(
            part, part, self.sent.at[2 + k], self.got.at[2 + k], (self.by_y, self.by_x)[k]
        )

    def start(self):
        self.first(0, self.n).start()
        self.first(1, self.n).start()

    def turn(self):
        self.first(0, self.x).wait_recv()
        self.second(0, self.x).start()
        self.first(1, self.y).wait_recv()
        self.second(1, self.y).start()

    def finish(self):
        for k in range(2):
            self.second(k, 3 - self.n).wait_recv()
            self.first(k, self.n).wait_send()
            self.second(k, (self.x, self.y)[k]).wait_send()


def square_sems():
    return [pltpu.SemaphoreType.DMA((4,))] * 2


def fetch(own, full, target, sems, n):
    copies = [pltpu.make_async_copy(own, target.at[n], sems.at[0])]
    for k, place in enumerate((n + 1 - 2 * (n % 2), (n + 2) % 4, 3 - n)):
        copies.append(pltpu.make_async_copy(full.at[place], target.at[place], sems.at[1 + k]))
    return copies


class Gather:
    def __init__(self, buf, sems, me, wid_count, rows=slice(None), pair=True):
        self.rows, self.both = rows, pair
        self.buf, (self.up_s, self.dn_s, self.pt_s, self.got) = buf, sems
        self.r, self.n, self.w = me
        self.last = wid_count - 1
        self.up = (self.r, self.n, jnp.minimum(self.w + 1, self.last))
        self.dn = (self.r, self.n, jnp.maximum(self.w - 1, 0))
        self.pt = (1 - self.r, self.n, self.w)

    def copy(self, j, sem, device, row=None):
        row = (self.r if self.both else 0) if row is None else row
        return pltpu.make_async_remote_copy(
            self.buf.at[row, j, self.rows],
            self.buf.at[row, j, self.rows],
            sem.at[j],
            self.got.at[row, j],
            device_id=device,
            device_id_type=MESH,
        )

    def pass_on(self, j, go_up, go_dn):
        if go_up:
            @pl.when(self.w < self.last)
            def _():
                self.copy(j, self.up_s, self.up).start()

        if go_dn:
            @pl.when(self.w > 0)
            def _():
                self.copy(j, self.dn_s, self.dn).start()

        if self.both:
            self.copy(j, self.pt_s, self.pt).start()

    def own(self):
        self.pass_on(self.w, True, True)

    def arrive(self, row, j):
        self.copy(j, self.pt_s, self.pt, row).wait_recv()

    def step(self, k):
        below, above = self.w - k, self.w + k

        @pl.when(below >= 0)
        def _():
            self.arrive(None, below)
            self.pass_on(below, True, False)

        @pl.when(above <= self.last)
        def _():
            self.arrive(None, above)
            self.pass_on(above, False, True)

    def advance(self, edge_steps, inner_steps):
        at_end = (self.w == 0) | (self.w == self.last)
        for ends, steps in ((True, edge_steps), (False, inner_steps)):
            if steps:
                @pl.when(at_end if ends else jnp.logical_not(at_end))
                def _():
                    for k in steps:
                        self.step(k)

    def rest(self):
        for j in range(self.last + 1):
            self.arrive(1 - self.r, j)

    def sent(self):
        for j in range(self.last + 1):
            @pl.when((j <= self.w) & (self.w < self.last))
            def _():
                self.copy(j, self.up_s, self.up).wait_send()

            @pl.when((j >= self.w) & (self.w > 0))
            def _():
                self.copy(j, self.dn_s, self.dn).wait_send()

            if self.both:
                self.copy(j, self.pt_s, self.pt).wait_send()


def gather_scratch(shard, width):
    return [pltpu.VMEM((2, 4, shard, width), bf16)] + gather_sems()


def gather_sems():
    return [pltpu.SemaphoreType.DMA((4,))] * 3 + [pltpu.SemaphoreType.DMA((2, 4))]


class Scatter:
    def __init__(self, mine, theirs, bufs, sems, me, wid_count, first=0, count=None):
        self.mine, self.theirs = mine, theirs
        self.from_pt, self.from_up, self.from_dn = bufs
        self.pt_s, self.pt_g, self.up_s, self.up_g, self.dn_s, self.dn_g = sems
        self.r, self.n, self.w = me
        self.first, self.count = first, mine.shape[1] if count is None else count
        self.rows = pl.ds(first, self.count)
        self.last = wid_count - 1
        self.up = (self.r, self.n, jnp.minimum(self.w + 1, self.last))
        self.dn = (self.r, self.n, jnp.maximum(self.w - 1, 0))
        self.pt = (1 - self.r, self.n, self.w)

    def order(self, i):
        low = jnp.where(i == 0, 3, jnp.where(i == 1, 0, jnp.where(i == 2, 2, 1)))
        return jnp.where(self.w < 2, low, 3 - low)

    def send(self, source, target, sent, got, s, device):
        return pltpu.make_async_remote_copy(
            source.at[s, self.rows], target.at[s, self.rows], sent.at[s], got.at[s],
            device_id=device, device_id_type=MESH,
        )

    def pair(self, s):
        return self.send(self.theirs, self.from_pt, self.pt_s, self.pt_g, s, self.pt)

    def climb(self, s):
        return self.send(self.mine, self.from_dn, self.up_s, self.up_g, s, self.up)

    def fall(self, s):
        return self.send(self.mine, self.from_up, self.dn_s, self.dn_g, s, self.dn)

    def each(self, body):
        def run(i, carry):
            body(pl.ds(pl.multiple_of(self.first + i * 16, 16), 16))
            return carry

        lax.fori_loop(0, self.count // 16, run, 0)

    def add(self, s, others):
        def body(rows):
            total = self.mine[s, rows, :].astype(f32)
            for other in others:
                total = total + other[s, rows, :].astype(f32)
            self.mine[s, rows, :] = total.astype(bf16)

        self.each(body)

    def step(self, s):
        self.pair(s).wait_recv()

        @pl.when((s > self.w) & (self.w > 0))
        def _():
            self.climb(s).wait_recv()
            self.add(s, (self.from_pt, self.from_dn))

        @pl.when((s < self.w) & (self.w < self.last))
        def _():
            self.fall(s).wait_recv()
            self.add(s, (self.from_pt, self.from_up))

        @pl.when(((s > self.w) & (self.w == 0)) | ((s < self.w) & (self.w == self.last)))
        def _():
            self.add(s, (self.from_pt,))

        @pl.when(s > self.w)
        def _():
            self.climb(s).start()

        @pl.when(s < self.w)
        def _():
            self.fall(s).start()

    def advance(self, edge_steps, inner_steps):
        for ends, steps in ((True, edge_steps), (False, inner_steps)):
            at_end = (self.w == 0) | (self.w == self.last)

            def body(i, carry):
                self.step(self.order(i))
                return carry

            if steps:
                @pl.when(at_end if ends else jnp.logical_not(at_end))
                def _():
                    lax.fori_loop(steps[0], steps[-1] + 1, body, 0)

    def total(self, out):
        w = self.w

        def first(rows):
            out[rows, :] = self.mine[w, rows, :].astype(f32) + self.from_pt[w, rows, :].astype(f32)

        self.each(first)

        @pl.when(w > 0)
        def _():
            self.climb(w).wait_recv()

            def more(rows):
                out[rows, :] += self.from_dn[w, rows, :].astype(f32)

            self.each(more)

        @pl.when(w < self.last)
        def _():
            self.fall(w).wait_recv()

            def more(rows):
                out[rows, :] += self.from_up[w, rows, :].astype(f32)

            self.each(more)

    def sent(self):
        for s in range(self.last + 1):
            self.pair(s).wait_send()

            @pl.when(s > self.w)
            def _():
                self.climb(s).wait_send()

            @pl.when(s < self.w)
            def _():
                self.fall(s).wait_send()


def scatter_bufs(shard, width):
    return [pltpu.VMEM((4, shard, width), bf16)] * 3


def scatter_sems():
    return [pltpu.SemaphoreType.DMA((4,))] * 6


def vmem():
    return pl.BlockSpec(memory_space=pltpu.VMEM)


def hbm():
    return pl.BlockSpec(memory_space=pl.ANY)


def comm_call(kernel, name, cid, out_shape, in_specs, out_specs, scratch, args, flops=0, sent=0):
    return pl.pallas_call(
        kernel,
        out_shape=out_shape,
        in_specs=in_specs,
        out_specs=out_specs,
        scratch_shapes=scratch,
        compiler_params=pltpu.CompilerParams(
            collective_id=cid, has_side_effects=True, vmem_limit_bytes=VMEM_LIMIT
        ),
        cost_estimate=pl.CostEstimate(flops=flops, bytes_accessed=sent, transcendentals=0),
        name=name,
    )(*args)


def norm_rows(x, gain):
    root = lax.rsqrt(jnp.mean(x * x, axis=-1, keepdims=True) + norm_eps)
    return x * root * gain


def turn(x, cosine, sine):
    lane = lax.broadcasted_iota(jnp.int32, x.shape, 1)
    swapped = jnp.where(lane % 64 < 32, pltpu.roll(x, 96, 1), pltpu.roll(x, 32, 1))
    return x * cosine + swapped * sine


def nar_device(r, n, w, by):
    return (r, jnp.clip(n + by, 0, 3), w)


def enter_kernel(
    hidden, gain, tab, grad_top, p1_own, down_own,
    q_out, rows_out, tabs_out, p1_out, down_out, kv_out, tops_out,
    buf, up_s, dn_s, pt_s, got, tbuf, h0, h1, h2, h3, tabs, p1, kv,
    tab_s, tab_g, out_s, p1_s, p1_g, down_s, down_g, s_s, s_g,
):
    me = spot()
    r, n, w = me
    bring = pltpu.make_async_copy(p1_own, p1.at[n], out_s.at[0])
    bring.start()
    greet(
        line_partners(r, n, w, 4)
        + [
            (n >= 1, nar_device(r, n, w, -1)),
            (n >= 2, nar_device(r, n, w, -2)),
            (n <= 2, nar_device(r, n, w, 1)),
            (n <= 1, nar_device(r, n, w, 2)),
        ]
    )
    p1_square = Square(p1_own, p1, (p1_s, p1_g), me)
    down = Square(down_own.at[0:256], down_out, (down_s, down_g), me)
    p1_square.start()
    down.start()
    gather = Gather(buf, (up_s, dn_s, pt_s, got), me, 4)
    tops = Gather(tbuf, (h0, h1, h2, h3), me, 4)
    tab_copy = pltpu.make_async_remote_copy(
        tab, tabs.at[r], tab_s, tab_g, device_id=(1 - r, n, w), device_id_type=MESH
    )

    def body(rows):
        buf[r, w, rows, :] = norm_rows(hidden[rows, :].astype(f32), gain[...]).astype(bf16)

    each_rows(hidden.shape[0], 16, body)
    gather.own()
    tab_copy.start()

    def keep(rows):
        tabs[r, rows, :] = tab[rows, :]

    each_rows(tab.shape[0], 16, keep)

    def keep_top(rows):
        tbuf[r, w, rows, :] = grad_top[rows, :]

    each_rows(64, 16, keep_top)
    gather.step(1)
    p1_square.turn()
    gather.step(2)
    tops.own()
    down.turn()
    gather.step(3)
    gather.rest()
    tab_copy.wait_recv()
    p1_square.finish()
    bring.wait()
    outs = [
        pltpu.make_async_copy(buf, rows_out, out_s.at[1]),
        pltpu.make_async_copy(tabs, tabs_out, out_s.at[2]),
        pltpu.make_async_copy(p1, p1_out, out_s.at[3]),
    ]
    for out in outs:
        out.start()
    tops.step(1)

    def copy(row, slot, by):
        return pltpu.make_async_remote_copy(
            kv.at[row, 2], kv.at[row, slot], s_s.at[row, slot], s_g.at[row, slot],
            device_id=nar_device(r, n, w, by), device_id_type=MESH,
        )

    lane = lax.broadcasted_iota(jnp.int32, (256, 128), 1)
    weight = p1[:, :, 0:384].reshape(2048, 384)
    for row in range(2):
        def tile(i, carry):
            rows = pl.ds(pl.multiple_of(i * 256, 256), 256)
            cosine, sine = tabs[row, rows, 0:128], tabs[row, rows, 128:256]
            left = buf[row, pl.ds(i * 2, 2)].reshape(256, 2048)
            pre = jnp.dot(left, weight, preferred_element_type=f32)
            q_out[row, rows, 0:128] = turn(pre[:, 0:128], cosine, sine).astype(bf16)
            q_out[row, rows, 128:256] = turn(pre[:, 128:256], cosine, sine).astype(bf16)
            both = pre[:, 256:384]
            kv[row, 2, rows, :] = jnp.where(lane < 64, turn(both, cosine, sine), both).astype(bf16)
            return carry

        lax.fori_loop(0, 2, tile, 0)

        @pl.when(n <= 2)
        def _():
            copy(row, 1, 1).start()

        @pl.when(n <= 1)
        def _():
            copy(row, 0, 2).start()

        for slot, least in ((1, 1), (0, 2)):
            @pl.when(n < least)
            def _():
                kv[row, slot] = jnp.zeros((512, 128), bf16)

    tops.step(2)
    for row in range(2):
        for slot, least, by in ((1, 1, 1), (0, 2, 2)):
            @pl.when(n >= least)
            def _():
                copy(row, slot, by).wait_recv()

    outs.append(pltpu.make_async_copy(kv, kv_out, out_s.at[4]))
    outs[3].start()
    tops.step(3)
    tops.rest()
    outs.append(pltpu.make_async_copy(tbuf, tops_out, out_s.at[5]))
    outs[4].start()
    for row in range(2):
        @pl.when(n <= 2)
        def _():
            copy(row, 1, 1).wait_send()

        @pl.when(n <= 1)
        def _():
            copy(row, 0, 2).wait_send()

    gather.sent()
    tops.sent()
    tab_copy.wait_send()
    down.finish()
    for out in outs:
        out.wait()


def enter(hidden, gain, tab, grad_top, p1_own, down_own):
    shard, width = hidden.shape
    return comm_call(
        enter_kernel, "enter", 1,
        (
            jax.ShapeDtypeStruct((2, 512, 256), bf16),
            jax.ShapeDtypeStruct((2, 4, shard, width), bf16),
            jax.ShapeDtypeStruct((2,) + tab.shape, f32),
            jax.ShapeDtypeStruct((4,) + p1_own.shape, bf16),
            jax.ShapeDtypeStruct((4, 256, 1024), bf16),
            jax.ShapeDtypeStruct((2, 3, 512, 128), bf16),
            jax.ShapeDtypeStruct((2, 4, 64, width), bf16),
        ),
        [vmem()] * 4 + [hbm()] * 2, [vmem()] + [hbm()] * 6,
        gather_scratch(shard, width)
        + gather_scratch(64, width)
        + [
            pltpu.VMEM((2,) + tab.shape, f32),
            pltpu.VMEM((4,) + p1_own.shape, bf16),
            pltpu.VMEM((2, 3, 512, 128), bf16),
            pltpu.SemaphoreType.DMA(()),
            pltpu.SemaphoreType.DMA(()),
            pltpu.SemaphoreType.DMA((6,)),
        ]
        + square_sems() * 2
        + [pltpu.SemaphoreType.DMA((2, 3))] * 2,
        (hidden, gain, tab, grad_top, p1_own, down_own), flops=10**10, sent=10**8,
    )


KEYS = 256
QUERIES = 128


def stack_low(x):
    lane = lax.broadcasted_iota(jnp.int32, (QUERIES, 128), 1)
    zero = jnp.zeros((QUERIES, 128), x.dtype)
    parts = []
    for pair in range(2):
        block = x[:, pair * 128 : pair * 128 + 128]
        parts.append(jnp.where(lane < 64, block, zero))
        parts.append(jnp.where(lane < 64, pltpu.roll(block, 64, 1), zero))
    return jnp.concatenate(parts, axis=0)


def stack_high(x):
    lane = lax.broadcasted_iota(jnp.int32, (QUERIES, 128), 1)
    zero = jnp.zeros((QUERIES, 128), x.dtype)
    parts = []
    for pair in range(2):
        block = x[:, pair * 128 : pair * 128 + 128]
        parts.append(jnp.where(lane >= 64, pltpu.roll(block, 64, 1), zero))
        parts.append(jnp.where(lane >= 64, block, zero))
    return jnp.concatenate(parts, axis=0)


def unstack(x, low):
    lane = lax.broadcasted_iota(jnp.int32, (QUERIES, 128), 1)
    out = []
    for pair in range(2):
        even = x[2 * pair * QUERIES : (2 * pair + 1) * QUERIES]
        odd = x[(2 * pair + 1) * QUERIES : (2 * pair + 2) * QUERIES]
        if low:
            out.append(jnp.where(lane < 64, even, pltpu.roll(odd, 64, 1)))
        else:
            out.append(jnp.where(lane < 64, pltpu.roll(even, 64, 1), odd))
    return jnp.concatenate(out, axis=1)


def allowed_tile(starts, tile, first_query):
    key = lax.broadcasted_iota(jnp.int32, (QUERIES, KEYS), 1) + tile * KEYS
    query = lax.broadcasted_iota(jnp.int32, (QUERIES, KEYS), 0) + first_query
    start = jnp.concatenate([starts] * (KEYS // 128), axis=1)
    ok = (key <= query) & (key.astype(f32) >= start)
    return jnp.concatenate([ok] * 4, axis=0)


def attend_block(q, kv, starts, first_query):
    query = stack_low(q.astype(f32)).astype(bf16)

    def body(step, carry):
        tile = (first_query - 1024) // KEYS + step
        top, total, acc = carry
        both = kv[pl.ds(pl.multiple_of(tile * KEYS, KEYS), KEYS), :]
        scores = contract_last(query, both) * 0.125
        ok = allowed_tile(starts, tile, first_query)
        scores = jnp.where(ok, scores, masked_score)
        new_top = jnp.maximum(top, jnp.max(scores, axis=1, keepdims=True))
        shrink = jnp.exp(top - new_top)
        part = jnp.exp(scores - new_top)
        total = total * shrink + jnp.sum(part, axis=1, keepdims=True)
        acc = acc * shrink + jnp.dot(part.astype(bf16), both, preferred_element_type=f32)
        return new_top, total, acc

    top, total, acc = lax.fori_loop(
        0, 5, body,
        (
            jnp.full((4 * QUERIES, 1), masked_score, f32),
            jnp.zeros((4 * QUERIES, 1), f32),
            jnp.zeros((4 * QUERIES, 128), f32),
        ),
        unroll=True,
    )
    logsum = jnp.broadcast_to(top + jnp.log(total), (4 * QUERIES, 128))
    return unstack(acc / total, False).astype(bf16), logsum


def out_block(p1, nn, half):
    return p1[nn, half * 256 : half * 256 + 256, 384:640]


def middle_kernel(
    q, kv, tabs, p1, hidden, gain, gate_own, up_own, down_own,
    att, lse, mid_out, ffn_out, gate_out, up_out, down_out,
    theirs, mine, from_pt, from_up, from_dn, s0, s1, s2, s3, s4, s5, fbuf, h0, h1, h2, h3, out_s,
    gate_s, gate_g, up_s, up_g, down_s, down_g,
):
    me = spot()
    r, n, w = me
    greet(line_partners(r, n, w, 4) + square_partners(r, n, w))
    gate = Square(gate_own, gate_out, (gate_s, gate_g), me)
    up = Square(up_own, up_out, (up_s, up_g), me)
    gate.start()
    up.start()
    down = Square(down_own.at[256:512], down_out, (down_s, down_g), me)
    down.start()
    scatter = Scatter(
        mine, theirs, (from_pt, from_up, from_dn), (s0, s1, s2, s3, s4, s5), me, 4
    )
    ffn = Gather(fbuf, (h0, h1, h2, h3), me, 4)
    def shard(i, carry):
        s = scatter.order(i)
        rows = pl.ds(pl.multiple_of(s * 128, 128), 128)
        for row in range(2):
            att[row, rows, :], lse[row, s] = attend_block(
                q[row, rows, :], kv.at[row], tabs[row, rows, 256:384], 1024 + s * 128
            )

        @pl.when((i >= 1) & ((w == 0) | (w == 3)))
        def _():
            scatter.step(scatter.order(i - 1))

        left = jnp.concatenate([att[1 - r, rows, :], att[r, rows, :]], axis=0)
        for nn in range(4):
            for half in range(2):
                part = jnp.dot(left, out_block(p1, nn, half), preferred_element_type=f32).astype(bf16)
                columns = slice(nn * 512 + half * 256, nn * 512 + half * 256 + 256)
                theirs[s, :, columns] = part[0:128]
                mine[s, :, columns] = part[128:256]
        scatter.pair(s).start()
        return carry

    lax.fori_loop(0, 4, shard, 0)
    scatter.advance((3,), (0, 1, 2, 3))
    scatter.total(mid_out)

    def body(rows):
        middle = mid_out[rows, :] + hidden[rows, :].astype(f32)
        mid_out[rows, :] = middle
        fbuf[r, w, rows, :] = norm_rows(middle, gain[...]).astype(bf16)

    each_rows(hidden.shape[0], 16, body)
    ffn.own()
    gate.turn()
    up.turn()
    ffn.step(1)
    down.turn()
    ffn.step(2)
    ffn.step(3)
    ffn.rest()
    out_f = pltpu.make_async_copy(fbuf, ffn_out, out_s)
    out_f.start()
    scatter.sent()
    ffn.sent()
    gate.finish()
    up.finish()
    down.finish()
    out_f.wait()


def middle_stage(q, kv, tabs, p1, hidden, gain, *weights):
    shard, width = hidden.shape
    rows = jax.ShapeDtypeStruct((2, 4, shard, width), bf16)
    return comm_call(
        middle_kernel, "middle", 3,
        (
            jax.ShapeDtypeStruct((2, 512, 256), bf16),
            jax.ShapeDtypeStruct((2, 4, 4 * QUERIES, 128), f32),
            jax.ShapeDtypeStruct((shard, width), f32),
            rows,
        )
        + (jax.ShapeDtypeStruct((4, 512, 1024), bf16),) * 2
        + (jax.ShapeDtypeStruct((4, 256, 1024), bf16),),
        [vmem()] * 6 + [hbm()] * 3, [vmem()] * 3 + [hbm()] * 4,
        [pltpu.VMEM((4, shard, width), bf16)] * 2
        + scatter_bufs(shard, width) + scatter_sems()
        + gather_scratch(shard, width)
        + [pltpu.SemaphoreType.DMA(())]
        + square_sems() * 3,
        (q, kv, tabs, p1, hidden, gain, *weights), flops=10**10, sent=2 * 10**8,
    )


class Spread:
    def __init__(self, outs, sems, me):
        self.a_send, self.a_keep, self.b_send, self.b_keep = outs
        self.r, self.n, self.w = me
        self.give_s, self.give_g, self.keep_s = sems

    def copies(self, wide, row, place, give):
        for k in range(4):
            block = wide.at[self.n ^ k]
            for part in range(2):
                source = block.at[pl.ds(part * 128, 128)]
                if part == 0:
                    target = (self.a_send if k & 1 else self.a_keep).at[k >> 1]
                else:
                    target = (self.b_send if k >= 2 else self.b_keep).at[k & 1]
                target = place(target)
                at = k * 2 + part
                if give:
                    yield pltpu.make_async_remote_copy(
                        source, target, self.give_s.at[row, at], self.give_g.at[row, at],
                        device_id=(1 - self.r, self.n, self.w), device_id_type=MESH,
                    )
                else:
                    yield pltpu.make_async_copy(source, target, self.keep_s.at[row, at])

    def start(self, *args):
        for copy in self.copies(*args):
            copy.start()

    def wait_send(self, *args):
        for copy in self.copies(*args):
            copy.wait_send()

    def wait_recv(self, *args):
        for copy in self.copies(*args):
            copy.wait_recv()

    def wait(self, *args):
        for copy in self.copies(*args):
            copy.wait()


def spread_sems(count):
    return [pltpu.SemaphoreType.DMA((count, 8))] * 3


def ffn_kernel(
    x, tops_in, grad_top, gate_own, gate_in, up_own, up_in, down_own, down_a, down_b, gain,
    part_out, sum_out, gain_out, o0, o1, o2, o3, ra_out, rb_out,
    theirs, mine, from_pt, from_up, from_dn, s0, s1, s2, s3, s4, s5,
    act, dgu, wide, out_s, give_s, give_g, keep_s, p2, in_s, n_s, n_g,
    tops4, h0, h1, h2, h3, tops_s,
):
    me = spot()
    r, n, w = me
    loads = [
        fetch(gate_own, gate_in, p2.at[0], in_s.at[0], n),
        fetch(up_own, up_in, p2.at[1], in_s.at[1], n),
        fetch(down_own.at[0:256], down_a, p2.at[2, :, 0:256], in_s.at[2], n)
        + fetch(down_own.at[256:512], down_b, p2.at[2, :, 256:512], in_s.at[3], n),
        [pltpu.make_async_copy(tops_in, tops4.at[:, :, 0:64], tops_s)],
    ]
    for group in loads:
        for load in group:
            load.start()

    def loaded(k):
        for load in loads[k]:
            load.wait()

    greet(line_partners(r, n, w, 4) + square_partners(r, n, w))
    scatter = Scatter(
        mine, theirs, (from_pt, from_up, from_dn), (s0, s1, s2, s3, s4, s5), me, 4
    )
    late = pl.ds(64, 64)
    gather = Gather(tops4, (h0, h1, h2, h3), me, 4, late)

    def keep(rows):
        tops4[r, w, pl.ds(64 + rows.start, 16), :] = grad_top[pl.ds(64 + rows.start, 16), :]

    each_rows(64, 16, keep)
    gather.own()
    gain_out[...] = jnp.zeros_like(gain_out)
    loaded(0)
    loaded(1)

    def hidden_tile(i, carry):
        ft, row = i // 2, i % 2
        rows = pl.ds(pl.multiple_of(row * 512, 512), 512)
        columns = pl.ds(pl.multiple_of(ft * 256, 256), 256)
        left = x[rows, :]
        gate = jnp.dot(left, p2[0, :, :, columns].reshape(2048, 256), preferred_element_type=f32)
        up = jnp.dot(left, p2[1, :, :, columns].reshape(2048, 256), preferred_element_type=f32)
        sig = 1.0 / (1.0 + jnp.exp(-gate))
        silu = gate * sig
        act[rows, columns] = (silu * up).astype(bf16)
        dgu[rows, columns] = (up * (sig * (1.0 + gate * (1.0 - sig)))).astype(bf16)
        later = pl.ds(pl.multiple_of(1024 + ft * 256, 256), 256)
        dgu[rows, later] = silu.astype(bf16)
        return carry

    lax.fori_loop(0, 4, hidden_tile, 0)
    gather.step(1)
    lax.fori_loop(4, 8, hidden_tile, 0)
    gather.step(2)
    loaded(2)

    def down_tile(dt, carry):
        nn, half = dt // 2, dt % 2
        columns = pl.ds(pl.multiple_of(dt * 256, 256), 256)
        inner = pl.ds(pl.multiple_of(half * 256, 256), 256)
        other = pl.ds(pl.multiple_of(512 + half * 256, 256), 256)
        right = jnp.concatenate([p2[2, nn, :, inner], p2[2, nn, :, other]], axis=0)
        for row, stage in ((0, theirs), (1, mine)):
            part = jnp.dot(act[row * 512 : row * 512 + 512, :], right, preferred_element_type=f32)
            stage[:, :, columns] = part.astype(bf16).reshape(4, 128, 256)
        return carry

    lax.fori_loop(0, 8, down_tile, 0)
    puts = [
        pltpu.make_async_copy(theirs, part_out.at[0], out_s.at[0]),
        pltpu.make_async_copy(mine, part_out.at[1], out_s.at[1]),
    ]
    for put in puts:
        put.start()
    gather.step(3)
    gather.rest()
    loaded(3)

    def top_rows(row):
        return tops4[row].reshape(512, 2048)

    def back_tile(ft, carry):
        columns = pl.ds(pl.multiple_of(ft * 256, 256), 256)
        f_rows = pl.ds(pl.multiple_of((ft % 2) * 256, 256), 256)
        f_cols = pl.ds(pl.multiple_of((ft // 2) * 512, 512), 512)
        later = pl.ds(pl.multiple_of(1024 + ft * 256, 256), 256)
        right = jnp.concatenate([p2[2, nn, f_rows, f_cols] for nn in range(4)], axis=1)
        for row in range(2):
            rows = slice(row * 512, row * 512 + 512)
            dact = contract_last(top_rows(row), right)
            dgu[rows, columns] = (dact * dgu[rows, columns].astype(f32)).astype(bf16)
            dgu[rows, later] = (dact * dgu[rows, later].astype(f32)).astype(bf16)
        return carry

    lax.fori_loop(0, 4, back_tile, 0)
    for put in puts:
        put.wait()

    spread = Spread((o0, o1, o2, o3), (give_s, give_g, keep_s), me)
    columns_here = pl.ds(pl.multiple_of(r * 1024, 1024), 1024)
    slots = {2: 0, 0: 1, 1: 0}

    def moved(which, half):
        def place(target):
            return target.at[which, :, columns_here]

        return wide.at[slots[which], half], which, place, half == 0

    def weights(which, between=None):
        for half in range(2):
            d_first = (jnp.where(half == 0, 1 - r, r)) * 1024

            def weight_tile(i, carry):
                d_cols = pl.ds(pl.multiple_of(d_first + i * 256, 256), 256)
                if which < 2:
                    left = x[:, d_cols]
                    right = dgu[:, which * 1024 : which * 1024 + 1024]
                else:
                    left = tops4[:, :, :, d_cols].reshape(1024, 256)
                    right = act[...]
                wide[slots[which], half, i] = contract_first(left, right).astype(bf16)
                return carry

            lax.fori_loop(0, 4, weight_tile, 0)
            spread.start(*moved(which, half))
            if half == 0 and between is not None:
                between()

    def hop(which, at):
        return (
            push(o0.at[:, which], ra_out.at[at], n_s.at[0, at], n_g.at[0, at], over_x(r, n, w)),
            push(o2.at[:, which], rb_out.at[at], n_s.at[1, at], n_g.at[1, at], over_y(r, n, w)),
        )

    hops = hop(2, 0) + hop(0, 1)
    weights(2)
    for i in range(4):
        s = scatter.order(i)
        rows_t = pl.ds(pl.multiple_of((1 - r) * 512 + s * 128, 128), 128)
        rows_m = pl.ds(pl.multiple_of(r * 512 + s * 128, 128), 128)

        def model_tile(dt, carry):
            nn, half = dt // 2, dt % 2
            columns = pl.ds(pl.multiple_of(dt * 256, 256), 256)
            inner = pl.ds(pl.multiple_of(half * 256, 256), 256)
            left = jnp.concatenate([dgu[rows_t, :], dgu[rows_m, :]], axis=0)
            right = jnp.concatenate([p2[0, nn, inner, :], p2[1, nn, inner, :]], axis=1)
            part = contract_last(left, right)
            seen = jnp.concatenate([x[rows_t, columns], x[rows_m, columns]], axis=0)
            terms = part * seen.astype(f32)
            gain_out[:, columns] += jnp.sum(terms.reshape(32, 8, 256), axis=0)
            part = part.astype(bf16)
            theirs[s, :, columns] = part[0:128]
            mine[s, :, columns] = part[128:256]
            return carry

        lax.fori_loop(0, 8, model_tile, 0)
        scatter.pair(s).start()
        if i < 2:
            which = (2, 0)[i]
            spread.wait_recv(*moved(which, 0))
            spread.wait(*moved(which, 1))
            hops[2 * i].start()
            hops[2 * i + 1].start()
        if i == 0:
            weights(0)
            scatter.advance((0,), ())
        elif i > 1:
            scatter.advance((i - 1,), (i - 2,))

    def scale(rows):
        gain_out[rows, :] = gain_out[rows, :] / gain[...]

    each_rows(8, 8, scale)
    spread.wait_send(*moved(2, 0))
    weights(1, lambda: scatter.advance((3,), (2,)))
    scatter.advance((), (3,))
    scatter.total(sum_out)
    scatter.sent()
    gather.sent()
    spread.wait_send(*moved(0, 0))
    spread.wait_recv(*moved(1, 0))
    spread.wait_send(*moved(1, 0))
    spread.wait(*moved(1, 1))
    for hop in hops:
        hop.wait()


def spread_shapes(*dims):
    return (jax.ShapeDtypeStruct((2,) + dims, bf16),) * 4


def ffn_stage(*args):
    shard, width = 128, 2048
    return comm_call(
        ffn_kernel, "ffn", 4,
        (
            jax.ShapeDtypeStruct((2, 4, shard, width), bf16),
            jax.ShapeDtypeStruct((shard, width), f32),
            jax.ShapeDtypeStruct((8, width), f32),
        )
        + spread_shapes(3, 128, width)
        + (jax.ShapeDtypeStruct((2, 2, 128, width), bf16),) * 2,
        [vmem(), hbm(), vmem()] + [hbm()] * 7 + [vmem()], [hbm(), vmem(), vmem()] + [hbm()] * 6,
        [pltpu.VMEM((4, shard, width), bf16)] * 2
        + scatter_bufs(shard, width) + scatter_sems()
        + [
            pltpu.VMEM((1024, 1024), bf16),
            pltpu.VMEM((1024, 2048), bf16),
            pltpu.VMEM((2, 2, 4, 256, 1024), bf16),
            pltpu.SemaphoreType.DMA((2,)),
        ]
        + spread_sems(3)
        + [pltpu.VMEM((3, 4, 512, 1024), bf16), pltpu.SemaphoreType.DMA((4, 4))]
        + [pltpu.SemaphoreType.DMA((2, 2))] * 2
        + gather_scratch(shard, width)
        + [pltpu.SemaphoreType.DMA(())],
        args, flops=4 * 10**10, sent=10**8,
    )


def norm_back(values, gain, grad):
    root = lax.rsqrt(jnp.mean(values * values, axis=-1, keepdims=True) + norm_eps)
    weighted = grad * gain
    inner = jnp.mean(weighted * values, axis=-1, keepdims=True)
    return root * weighted - values * (root * root * root) * inner


def back_kernel(
    total, mid, grad_top, gain_f, p1, att, q, kv, lse, x, tabs, gain,
    parts, a_send, b_send, a_keep, b_keep, a_came, b_came,
    gmid_out, part_out, gain_out, hid_out, o0, o1, o2, o3, oa_out, ob_out,
    q0, q1, q2, q3, ua_out, ub_out, la_out, lb_out,
    buf, g0, g1, g2, g3, grad, wide, give_s, give_g, keep_s,
    send, recv, both, wide_q, wide_kv, s_s, s_g, qgive_s, qgive_g, qkeep_s,
    mine, from_pt, from_up, from_dn, s0, s1, s2, s3, s4, s5,
    kept, came, acc, in_s, n_s, n_g, m_s, dkv,
):
    me = spot()
    r, n, w = me
    x_side, y_side = over_x(r, n, w), over_y(r, n, w)
    loads = [pltpu.make_async_copy(parts.at[r], mine, m_s)]
    for j, (keep, first) in enumerate(((a_keep, a_came), (b_keep, b_came))):
        loads += [
            pltpu.make_async_copy(keep.at[1], kept.at[j], in_s.at[j, 0]),
            pltpu.make_async_copy(first.at[1, 1], came.at[j, 0], in_s.at[j, 1]),
            pltpu.make_async_copy(first.at[0, 1], came.at[j, 2], in_s.at[j, 2]),
        ]
    for load in loads:
        load.start()
    greet(
        line_partners(r, n, w, 4)
        + [
            (n >= 1, nar_device(r, n, w, -1)),
            (n >= 2, nar_device(r, n, w, -2)),
            (n <= 2, nar_device(r, n, w, 1)),
            (n <= 1, nar_device(r, n, w, 2)),
        ]
    )
    scatter = Scatter(
        mine, parts.at[1 - r], (from_pt, from_up, from_dn), (s0, s1, s2, s3, s4, s5), me, 4
    )
    gather = Gather(buf, (g0, g1, g2, g3), me, 4)

    def hop(k, source, target, device):
        return push(source, target, n_s.at[k], n_g.at[k], device)

    up_hops = [
        hop(0, a_send.at[:, 1], ua_out, x_side),
        hop(1, b_send.at[:, 1], ub_out, y_side),
    ]
    last_hops = [
        [
            hop(2 + which, kept.at[0, which], la_out.at[which], y_side),
            hop(5 + which, kept.at[1, which], lb_out.at[which], x_side),
        ]
        for which in range(3)
    ]
    o_hops = [hop(8, o0, oa_out, x_side), hop(9, o2, ob_out, y_side)]
    for one in up_hops:
        one.start()

    def body(rows):
        got = norm_back(mid[rows, :], gain_f[...], total[rows, :]) + grad_top[rows, :].astype(f32)
        gmid_out[rows, :] = got
        buf[r, w, rows, :] = got.astype(bf16)

    each_rows(mid.shape[0], 16, body)
    gather.own()
    for load in loads:
        load.wait()

    def join(which):
        for j in range(2):
            def add(rows):
                one = kept[j, which, rows, :].astype(f32) + came[j, which, rows, :].astype(f32)
                kept[j, which, rows, :] = one.astype(bf16)

            each_rows(128, 16, add)
            last_hops[which][j].start()

    join(2)
    join(0)
    for i in range(4):
        scatter.pair(scatter.order(i)).start()
    for k in (1, 2, 3):
        gather.step(k)
    gather.rest()
    scatter.advance((0, 1, 2, 3), ())
    for row in range(2):
        for pair in range(2):
            left = jnp.concatenate([buf[row, 2 * pair], buf[row, 2 * pair + 1]], axis=0)
            right = jnp.concatenate(
                [out_block(p1, nn, half) for nn in range(4) for half in range(2)], axis=1
            )
            grad[row, pair * 256 : pair * 256 + 256, :] = contract_last(left, right).astype(bf16)

    def copy(row, slot, by):
        return pltpu.make_async_remote_copy(
            send.at[row, slot], recv.at[row, slot], s_s.at[row, slot], s_g.at[row, slot],
            device_id=nar_device(r, n, w, by), device_id_type=MESH,
        )

    def attention(i, carry):
        row, block = i // 4, i % 4
        first_query = 1024 + block * QUERIES
        here = pl.ds(pl.multiple_of(block * QUERIES, QUERIES), QUERIES)

        @pl.when(block == 0)
        def _():
            dkv[row] = jnp.zeros((1536, 128), f32)

        query = stack_low(q[row, here, :].astype(f32)).astype(bf16)
        grads = stack_high(grad[row, here, :].astype(f32))
        inner = jnp.sum(grads * stack_high(att[row, here, :].astype(f32)), axis=1, keepdims=True)
        grads = grads.astype(bf16)
        logsum = jnp.concatenate([lse[row, block]] * (KEYS // 128), axis=1)
        starts = tabs[row, here, 256:384]

        def key_tile(step, dq):
            tile = block // 2 + step
            rows = pl.ds(pl.multiple_of(tile * KEYS, KEYS), KEYS)
            pair = kv[row, rows, :]
            ok = allowed_tile(starts, tile, first_query)
            scores = contract_last(query, pair) * 0.125
            prob = jnp.where(ok, jnp.exp(scores - logsum), 0.0)
            grad_prob = contract_last(grads, pair)
            grad_scores = (prob * (grad_prob - inner)).astype(bf16)
            dkv[row, rows, :] += contract_first(grad_scores, query) * 0.125 + contract_first(
                prob.astype(bf16), grads
            )
            return dq + jnp.dot(grad_scores, pair, preferred_element_type=f32)

        dq = lax.fori_loop(0, 5, key_tile, jnp.zeros((4 * QUERIES, 128), f32), unroll=True)
        flat = unstack(dq, True) * 0.125
        cosine, sine = tabs[row, here, 0:128], -tabs[row, here, 128:256]
        there = pl.ds(pl.multiple_of(i * QUERIES, QUERIES), QUERIES)
        both[there, 0:128] = turn(flat[:, 0:128], cosine, sine).astype(bf16)
        both[there, 128:256] = turn(flat[:, 128:256], cosine, sine).astype(bf16)

        @pl.when(block == 3)
        def _():
            for slot, by in ((1, -1), (0, -2)):
                @pl.when(n >= -by)
                def _():
                    send[row, slot] = dkv[row, slot * 512 : slot * 512 + 512, :].astype(bf16)
                    copy(row, slot, by).start()

        @pl.when(i == 3)
        def _():
            scatter.advance((), (0,))

        return carry

    lax.fori_loop(0, 8, attention, 0)
    scatter.advance((), (1,))

    fresh = []
    for j, first in enumerate((ua_out, ub_out)):
        up_hops[j].wait_recv()
        fresh.append(pltpu.make_async_copy(first.at[1], came.at[j, 1], in_s.at[j, 3]))
        fresh[j].start()
    for load in fresh:
        load.wait()
    join(1)

    spread_o = Spread((o0, o1, o2, o3), (give_s, give_g, keep_s), me)
    spread = Spread((q0, q1, q2, q3), (qgive_s, qgive_g, qkeep_s), me)

    def moved_o(half):
        def place(target):
            return target.at[:, pl.ds(pl.multiple_of(r * 256, 256), 256)]

        return wide.at[half], 0, place, half == 0

    for half in range(2):
        d_first = (jnp.where(half == 0, 1 - r, r)) * 1024

        def weight_tile(i, carry):
            columns = pl.ds(pl.multiple_of(d_first + i * 256, 256), 256)
            left = buf[:, :, :, columns].reshape(1024, 256)
            wide[half, i] = contract_first(left, att[...].reshape(1024, 256)).astype(bf16)
            return carry

        lax.fori_loop(0, 4, weight_tile, 0)
        spread_o.start(*moved_o(half))

    def moved_q(half):
        def place(target):
            return target.at[:, pl.ds(pl.multiple_of(r * 256, 256), 256)]

        return wide_q.at[half], 0, place, half == 0

    def moved_kv(half):
        def place(target):
            return target.at[:, pl.ds(pl.multiple_of(512 + r * 128, 128), 128)]

        return wide_kv.at[half], 1, place, half == 0

    def weight(half, columns, wide):
        d_first = (jnp.where(half == 0, 1 - r, r)) * 1024

        def tile(i, carry):
            d_cols = pl.ds(pl.multiple_of(d_first + i * 256, 256), 256)
            wide[half, i] = contract_first(x[:, d_cols], both[:, columns]).astype(bf16)
            return carry

        lax.fori_loop(0, 4, tile, 0)

    for half in range(2):
        weight(half, slice(0, 256), wide_q)
        spread.start(*moved_q(half))
    lane = lax.broadcasted_iota(jnp.int32, (128, 128), 1)
    for row in range(2):
        for slot, by in ((1, -1), (0, -2)):
            @pl.when(n <= 3 + by)
            def _():
                copy(row, slot, by).wait_recv()

        def tile(i, carry):
            rows = pl.ds(pl.multiple_of(i * 128, 128), 128)
            total = dkv[row, pl.ds(pl.multiple_of(1024 + i * 128, 128), 128), :]
            zero = jnp.zeros_like(total)
            total = total + jnp.where(n <= 2, recv[row, 1, rows, :].astype(f32), zero)
            total = total + jnp.where(n <= 1, recv[row, 0, rows, :].astype(f32), zero)
            turned = turn(total, tabs[row, rows, 0:128], -tabs[row, rows, 128:256])
            both[pl.ds(pl.multiple_of(row * 512 + i * 128, 128), 128), 256:384] = jnp.where(
                lane < 64, turned, total
            ).astype(bf16)
            return carry

        lax.fori_loop(0, 4, tile, 0)
    for half in range(2):
        weight(half, slice(256, 384), wide_kv)
        spread.start(*moved_kv(half))
    scatter.advance((), (2,))
    spread_o.wait_recv(*moved_o(0))
    spread_o.wait(*moved_o(1))
    for one in o_hops:
        one.start()
    gain_out[...] = jnp.zeros_like(gain_out)

    def model_tile(dt, carry):
        nn, half = dt // 2, dt % 2
        columns = pl.ds(pl.multiple_of(dt * 256, 256), 256)
        inner = pl.ds(pl.multiple_of(half * 256, 256), 256)
        right = p1[nn, inner, 0:384]
        for row in range(2):
            for block in range(2):
                first = row * 512 + block * 256
                part = contract_last(both[first : first + 256, :], right)
                terms = part * x[first : first + 256, columns].astype(f32)
                gain_out[:, columns] += jnp.sum(terms.reshape(32, 8, 256), axis=0)
                part_out[row, 2 * block, :, columns] = part[0:128].astype(bf16)
                part_out[row, 2 * block + 1, :, columns] = part[128:256].astype(bf16)
        return carry

    lax.fori_loop(0, 8, model_tile, 0)
    gain_out[...] = gain_out[...] / gain[...]
    scatter.advance((), (3,))
    scatter.total(acc)

    def last(rows):
        hid_out[rows, :] = (acc[rows, :] + mid[rows, :]).astype(bf16)

    each_rows(128, 16, last)
    scatter.sent()
    for row in range(2):
        for slot, by in ((1, -1), (0, -2)):
            @pl.when(n >= -by)
            def _():
                copy(row, slot, by).wait_send()

    for half in range(2):
        spread.wait(*moved_q(half))
        spread.wait(*moved_kv(half))
    spread_o.wait_send(*moved_o(0))
    gather.sent()
    for one in up_hops:
        one.wait_send()
    for one in last_hops[0] + last_hops[1] + last_hops[2] + o_hops:
        one.wait()


def back(*args):
    shard, width = 128, 2048
    return comm_call(
        back_kernel, "back", 5,
        (
            jax.ShapeDtypeStruct((shard, width), f32),
            jax.ShapeDtypeStruct((2, 4, shard, width), bf16),
            jax.ShapeDtypeStruct((8, width), f32),
            jax.ShapeDtypeStruct((shard, width), bf16),
        )
        + spread_shapes(128, 512)
        + (jax.ShapeDtypeStruct((2, 128, 512), bf16),) * 2
        + spread_shapes(128, 768)
        + (jax.ShapeDtypeStruct((2, 128, width), bf16),) * 2
        + (jax.ShapeDtypeStruct((3, 128, width), bf16),) * 2,
        [vmem()] * 12 + [hbm()] * 7, [vmem()] * 4 + [hbm()] * 14,
        gather_scratch(shard, width)
        + [pltpu.VMEM((2, 512, 256), bf16), pltpu.VMEM((2, 4, 256, 256), bf16)]
        + spread_sems(1)
        + [
            pltpu.VMEM((2, 2, 512, 128), bf16),
            pltpu.VMEM((2, 2, 512, 128), bf16),
            pltpu.VMEM((1024, 384), bf16),
            pltpu.VMEM((2, 4, 256, 256), bf16),
            pltpu.VMEM((2, 4, 256, 128), bf16),
            pltpu.SemaphoreType.DMA((2, 2)),
            pltpu.SemaphoreType.DMA((2, 2)),
        ]
        + spread_sems(2)
        + [pltpu.VMEM((4, shard, width), bf16)]
        + scatter_bufs(shard, width) + scatter_sems()
        + [
            pltpu.VMEM((2, 3, shard, width), bf16),
            pltpu.VMEM((2, 3, shard, width), bf16),
            pltpu.VMEM((shard, width), f32),
            pltpu.SemaphoreType.DMA((2, 4)),
            pltpu.SemaphoreType.DMA((10,)),
            pltpu.SemaphoreType.DMA((10,)),
            pltpu.SemaphoreType.DMA(()),
            pltpu.VMEM((2, 1536, 128), f32),
        ],
        args, flops=10**10, sent=10**8,
    )


def leave_kernel(
    parts, hidden, gain, gmid, gains, qa_send, qa_keep, qb_send, qb_keep, oa_keep, ob_keep, oa_in, ob_in,
    grad_out, ga_out, query_out, key_out, value_out, output_out,
    mine, from_pt, from_up, from_dn, s0, s1, s2, s3, s4, s5,
    acc, over_wid, summed, over_rest, w_s, w_g, t_s, t_g,
    first_q, next_q, then_q, next_o, then_o, kv, n_s, n_g, k0, k1, k2, k3, m_s,
):
    me = spot()
    r, n, w = me
    own_parts = pltpu.make_async_copy(parts.at[r], mine, m_s)
    own_parts.start()
    partners = [(w != j, (r, n, jnp.int32(j))) for j in range(4)]
    partners += [
        ((r != a) | (n != b), (jnp.int32(a), jnp.int32(b), w)) for a in range(2) for b in range(4)
    ]
    greet(partners)
    kv_gather = Gather(kv, (k0, k1, k2, k3), me, 4, pair=False)
    x_side, y_side = over_x(r, n, w), over_y(r, n, w)
    q_hops = [
        push(qa_send, first_q.at[0], n_s.at[0], n_g.at[0], x_side),
        push(qb_send, first_q.at[1], n_s.at[1], n_g.at[1], y_side),
    ]
    q_later = [
        push(next_q.at[0], then_q.at[0], n_s.at[2], n_g.at[2], y_side),
        push(next_q.at[1], then_q.at[1], n_s.at[3], n_g.at[3], x_side),
    ]
    o_hops = [
        push(next_o.at[0], then_o.at[0], n_s.at[4], n_g.at[4], y_side),
        push(next_o.at[1], then_o.at[1], n_s.at[5], n_g.at[5], x_side),
    ]
    for hop in q_hops:
        hop.start()
    scatter = Scatter(
        mine, parts.at[1 - r], (from_pt, from_up, from_dn), (s0, s1, s2, s3, s4, s5), me, 4
    )
    for i in range(4):
        scatter.pair(scatter.order(i)).start()

    def wid_copy(j, slot):
        return pltpu.make_async_remote_copy(
            gains, over_wid.at[slot], w_s.at[j], w_g.at[slot],
            device_id=(r, n, jnp.int32(j)), device_id_type=MESH,
        )

    def rest_copy(a, b, slot):
        return pltpu.make_async_remote_copy(
            summed, over_rest.at[slot], t_s.at[a * 4 + b], t_g.at[slot],
            device_id=(jnp.int32(a), jnp.int32(b), w), device_id_type=MESH,
        )

    for j in range(4):
        @pl.when(w != j)
        def _():
            wid_copy(j, w).start()

    own_parts.wait()
    scatter.advance((0, 1, 2), ())
    for j, (keep, came) in enumerate(((oa_keep, oa_in), (ob_keep, ob_in))):
        next_o[j] = (keep[1].astype(f32) + came[1].astype(f32)).astype(bf16)
        o_hops[j].start()
    summed[...] = gains[...]
    for j in range(4):
        @pl.when(w != j)
        def _():
            wid_copy(j, j).wait_recv()
            summed[...] += over_wid[j]

    for a in range(2):
        for b in range(4):
            @pl.when((r != a) | (n != b))
            def _():
                rest_copy(a, b, r * 4 + n).start()

    for j, keep in enumerate((qa_keep, qb_keep)):
        q_hops[j].wait_recv()
        next_q[j] = (keep[1].astype(f32) + first_q[j, 1].astype(f32)).astype(bf16)
        q_later[j].start()
    scatter.advance((), (0,))
    for j, keep in enumerate((qa_keep, qb_keep)):
        q_later[j].wait_recv()
        total = keep[0].astype(f32) + first_q[j, 0].astype(f32) + then_q[j].astype(f32)
        query_out[j * 128 : j * 128 + 128, :] = total[:, 0:512]
        kv[0, w, j * 128 : j * 128 + 128, :] = total[:, 512:768].astype(bf16)
    kv_gather.own()
    scatter.advance((3,), (1, 2))
    kv_gather.advance((), (1,))
    scatter.advance((), (3,))
    kv_gather.advance((), (2,))
    for j, (keep, came) in enumerate(((oa_keep, oa_in), (ob_keep, ob_in))):
        o_hops[j].wait_recv()
        output_out[j * 128 : j * 128 + 128, :] = (
            keep[0].astype(f32) + came[0].astype(f32) + then_o[j].astype(f32)
        )
    mine_block = r * 4 + n
    ga_out[0:1] = summed[pl.ds(mine_block, 1), :]
    ga_out[1:2] = summed[pl.ds(mine_block + 8, 1), :]
    for a in range(2):
        for b in range(4):
            @pl.when((r != a) | (n != b))
            def _():
                slot = a * 4 + b
                rest_copy(a, b, slot).wait_recv()
                ga_out[0:1] += over_rest[slot, pl.ds(mine_block, 1), :]
                ga_out[1:2] += over_rest[slot, pl.ds(mine_block + 8, 1), :]

    scatter.total(acc)

    def last(rows):
        grad = norm_back(hidden[rows, :].astype(f32), gain[...], acc[rows, :])
        grad_out[rows, :] = (grad + gmid[rows, :]).astype(bf16)

    each_rows(hidden.shape[0], 16, last)
    kv_gather.advance((1, 2, 3), (3,))
    lane = lax.broadcasted_iota(jnp.int32, (256, 128), 1)
    for j in range(4):
        even, odd = kv[0, j, :, 0:128].astype(f32), kv[0, j, :, 128:256].astype(f32)
        here = slice(j * 128, j * 128 + 128)
        key_out[:, here] = jnp.where(lane < 64, even, pltpu.roll(odd, 64, 1))
        value_out[:, here] = jnp.where(lane < 64, pltpu.roll(even, 64, 1), odd)
    scatter.sent()
    kv_gather.sent()
    for hop in q_hops + q_later + o_hops:
        hop.wait_send()
    for j in range(4):
        @pl.when(w != j)
        def _():
            wid_copy(j, w).wait_send()

    for a in range(2):
        for b in range(4):
            @pl.when((r != a) | (n != b))
            def _():
                rest_copy(a, b, r * 4 + n).wait_send()


def leave(*args):
    shard, width = 128, 2048
    grad = jax.ShapeDtypeStruct((256, 512), f32)
    return comm_call(
        leave_kernel, "leave", 7,
        (jax.ShapeDtypeStruct((shard, width), bf16), jax.ShapeDtypeStruct((8, 256), f32))
        + (grad,) * 4,
        [hbm()] + [vmem()] * 12, [vmem()] * 6,
        [pltpu.VMEM((4, shard, width), bf16)]
        + scatter_bufs(shard, width) + scatter_sems()
        + [
            pltpu.VMEM((shard, width), f32),
            pltpu.VMEM((4, 16, 256), f32),
            pltpu.VMEM((16, 256), f32),
            pltpu.VMEM((8, 16, 256), f32),
            pltpu.SemaphoreType.DMA((4,)),
            pltpu.SemaphoreType.DMA((4,)),
            pltpu.SemaphoreType.DMA((8,)),
            pltpu.SemaphoreType.DMA((8,)),
            pltpu.VMEM((2, 2, 128, 768), bf16),
            pltpu.VMEM((2, 128, 768), bf16),
            pltpu.VMEM((2, 128, 768), bf16),
            pltpu.VMEM((2, 128, 512), bf16),
            pltpu.VMEM((2, 128, 512), bf16),
            pltpu.VMEM((1, 4, 256, 256), bf16),
            pltpu.SemaphoreType.DMA((6,)),
            pltpu.SemaphoreType.DMA((6,)),
        ]
        + gather_sems()
        + [pltpu.SemaphoreType.DMA(())],
        args, flops=10**10, sent=10**8,
    )


def local_fast(
    hidden_in, doc_lengths, w_query, w_key, w_value, w_output, w_gate, w_up, w_down,
    gain_attn, gain_ffn, grad_out,
):
    r, n, w = spot()
    hidden, grad_top = hidden_in[0], grad_out[0]
    gain_a, gain_f = gain_attn[None], gain_ffn[None]
    def half(weight, axis):
        size = weight.shape[axis] // 2
        return lax.dynamic_slice_in_dim(weight, r * size, size, axis)

    head = (w * 2 + r) * HD
    kv_pack = jnp.concatenate(
        [lax.dynamic_slice_in_dim(w_key, head, HD, 1), lax.dynamic_slice_in_dim(w_value, head, HD, 1)],
        axis=1,
    )
    out_half = half(w_output, 0)
    p1_shard = jnp.concatenate(
        [half(w_query, 1), kv_pack, jnp.concatenate([out_half[:, :256], out_half[:, 256:]], axis=0)],
        axis=1,
    )
    down_half = half(w_down, 0)
    gate_own, up_own = half(w_gate, 1), half(w_up, 1)
    down_own = jnp.concatenate([down_half[:512], down_half[512:]], axis=1)

    token_ids = n * 512 + jnp.arange(512, dtype=jnp.int32)
    doc_start, places = doc_layout(doc_lengths[0], token_ids)
    angles = places.astype(f32)[:, None] * inverse_freq()[None, :]
    cosine, sine = jnp.cos(angles), jnp.sin(angles)
    start_here = (doc_start - (n - 2) * 512).astype(f32)
    tab = jnp.concatenate(
        [cosine] * 4 + [-sine, sine] * 2 + [jnp.broadcast_to(start_here[:, None], (512, 128))],
        axis=1,
    )

    q, rows, tabs, p1, down_a, kv, tops = enter(
        hidden, gain_a, tab, grad_top, p1_shard, down_own
    )
    rows2 = rows.reshape(1024, 2048)
    kv_flat = kv.reshape(2, 1536, 128)
    att, lse, mid, ffn_rows, gate_all, up_all, down_b = middle_stage(
        q, kv_flat, tabs, p1, hidden, gain_f, gate_own, up_own, down_own
    )
    parts, total, gain_f_part, a_send, a_keep, b_send, b_keep, ra_dg, rb_dg = ffn_stage(
        ffn_rows.reshape(1024, 2048), tops, grad_top,
        gate_own, gate_all, up_own, up_all, down_own, down_a, down_b, gain_f,
    )
    (
        gmid, dparts, gain_a_part, hidden_out, _, oa_keep, _, ob_keep, oa_came, ob_came,
        qa_send, qa_keep, qb_send, qb_keep, ra_u, rb_u, a_last, b_last,
    ) = back(
        total, mid, grad_top, gain_f, p1, att, q, kv_flat, lse, rows2, tabs, gain_a,
        parts, a_send, b_send, a_keep, b_keep, ra_dg, rb_dg,
    )
    gains = jnp.concatenate(
        [gain_f_part.sum(axis=0).reshape(8, 256), gain_a_part.sum(axis=0).reshape(8, 256)], axis=0
    )
    grad_in, gain_sums, grad_query, grad_key, grad_value, output_sum = leave(
        dparts, hidden, gain_a, gmid, gains,
        qa_send, qa_keep, qb_send, qb_keep, oa_keep, ob_keep, oa_came, ob_came,
    )

    def joined(which):
        def half_rows(keep, came, last):
            return keep[0, which].astype(f32) + came.astype(f32) + last.astype(f32)

        a_came, b_came = (
            (ra_dg[1, 0], rb_dg[1, 0]), (ra_u[0], rb_u[0]), (ra_dg[0, 0], rb_dg[0, 0])
        )[which]
        return jnp.concatenate(
            [half_rows(a_keep, a_came, a_last[which]), half_rows(b_keep, b_came, b_last[which])], axis=0
        )

    return (
        hidden_out[None],
        grad_in[None],
        grad_query,
        grad_key,
        grad_value,
        output_sum.T,
        joined(0),
        joined(1),
        joined(2).T,
        gain_sums[1],
        gain_sums[0],
    )


def solution(mesh):
    in_specs = (
        P("row", ("nar", "wid"), None),
        P("row", None),
        P("nar", "wid"),
        P("nar", None),
        P("nar", None),
        P("wid", "nar"),
        P("nar", "wid"),
        P("nar", "wid"),
        P("wid", "nar"),
        P(),
        P(),
        P("row", ("nar", "wid"), None),
    )
    out_specs = (
        P("row", ("nar", "wid"), None),
        P("row", ("nar", "wid"), None),
        P(("row", "nar"), "wid"),
        P(("row", "nar"), None),
        P(("row", "nar"), None),
        P("wid", ("row", "nar")),
        P(("row", "nar"), "wid"),
        P(("row", "nar"), "wid"),
        P("wid", ("row", "nar")),
        P(("row", "nar")),
        P(("row", "nar")),
    )
    sizes = dict(mesh.shape)
    fits = sizes == {"row": 2, "nar": 4, "wid": 4}

    def body(*args):
        small = args[0].shape == (1, 128, 2048)
        return (local_fast if fits and small else local)(*args)

    return jax.shard_map(body, mesh=mesh, in_specs=in_specs, out_specs=out_specs, check_vma=False)
```

```python
import math

import jax
import jax.numpy as jnp
from jax import lax
from jax.experimental import pallas as pl
from jax.experimental.pallas import tpu as pltpu
from jax.sharding import PartitionSpec as P

H = 32
KV = 8
HD = 64


norm_eps = 1e-05
masked_score = -1e30


def inverse_freq():
    listed = []
    for pair_index in range(HD // 2):
        base_freq = 500000.0 ** (-2.0 * pair_index / HD)
        wavelength = 2.0 * math.pi / base_freq
        smoothing = (8192.0 / wavelength - 1.0) / 3.0
        blended = (1.0 - smoothing) * base_freq / 32.0 + smoothing * base_freq
        if wavelength < 2048.0:
            listed.append(base_freq)
        elif wavelength > 8192.0:
            listed.append(base_freq / 32.0)
        else:
            listed.append(blended)
    return jnp.asarray(listed, dtype=jnp.float32)


def rotate(values, cosine_table, sine_table):
    half_dim = HD // 2
    first_half = values[..., :half_dim]
    second_half = values[..., half_dim:]
    return jnp.concatenate(
        [
            first_half * cosine_table - second_half * sine_table,
            second_half * cosine_table + first_half * sine_table,
        ],
        axis=-1,
    )


def rotate_back(grads_in, cosine_table, sine_table):
    half_dim = HD // 2
    first_half = grads_in[..., :half_dim]
    second_half = grads_in[..., half_dim:]
    return jnp.concatenate(
        [
            first_half * cosine_table + second_half * sine_table,
            second_half * cosine_table - first_half * sine_table,
        ],
        axis=-1,
    )


def doc_layout(lengths_row, token_ids):
    ends_at = jnp.cumsum(lengths_row, dtype=jnp.int32)
    starts_at = ends_at - lengths_row
    inside = (token_ids[:, None] >= starts_at[None, :]) & (token_ids[:, None] < ends_at[None, :])
    doc_start = jnp.sum(jnp.where(inside, starts_at[None, :], 0), axis=1, dtype=jnp.int32)
    return (doc_start, token_ids - doc_start)


def norm_forward(values, gain_vector):
    root_inv = lax.rsqrt(jnp.mean(values * values, axis=-1, keepdims=True) + norm_eps)
    return (root_inv, (values * root_inv * gain_vector).astype(jnp.bfloat16))


def norm_backward(values, root_inv, gain_vector, grad_normed):
    weighted = grad_normed * gain_vector
    inner_sum = jnp.mean(weighted * values, axis=-1, keepdims=True)
    grad_values = root_inv * weighted - values * (root_inv * root_inv * root_inv) * inner_sum
    gain_term = jnp.sum(grad_normed * values * root_inv, axis=0)
    return (grad_values, gain_term)


def contract_last(left_side, right_side):
    return lax.dot_general(
        left_side, right_side, (((1,), (1,)), ((), ())), preferred_element_type=jnp.float32
    )


def contract_first(left_side, right_side):
    return lax.dot_general(
        left_side, right_side, (((0,), (0,)), ((), ())), preferred_element_type=jnp.float32
    )


def local(
    hidden_in,
    doc_lengths,
    w_query,
    w_key,
    w_value,
    w_output,
    w_gate,
    w_up,
    w_down,
    gain_attn,
    gain_ffn,
    grad_out,
):
    wid_count = lax.axis_size("wid")
    nar_count = lax.axis_size("nar")
    wid_index = lax.axis_index("wid")
    nar_index = lax.axis_index("nar")
    local_tokens = hidden_in.shape[1]
    block_tokens = local_tokens * wid_count
    seq_length = block_tokens * nar_count
    query_heads = w_query.shape[1] // HD
    group_size = H // KV
    kv_local = max(query_heads // group_size, 1)
    heads_per_kv = query_heads // kv_local
    kv_first = wid_index * query_heads // group_size
    query_block = min(512, block_tokens)
    block_count = block_tokens // query_block
    item_count = block_count * query_heads
    attn_scale = HD ** (-0.5)
    query_full, key_full, value_full, output_full, gate_full, up_full, down_full = (
        lax.all_gather(w_query, "nar", axis=0, tiled=True),
        lax.all_gather(w_key, "nar", axis=0, tiled=True),
        lax.all_gather(w_value, "nar", axis=0, tiled=True),
        lax.all_gather(w_output, "nar", axis=1, tiled=True),
        lax.all_gather(w_gate, "nar", axis=0, tiled=True),
        lax.all_gather(w_up, "nar", axis=0, tiled=True),
        lax.all_gather(w_down, "nar", axis=1, tiled=True),
    )
    key_local = lax.dynamic_slice_in_dim(key_full, kv_first * HD, kv_local * HD, 1)
    value_local = lax.dynamic_slice_in_dim(value_full, kv_first * HD, kv_local * HD, 1)
    token_ids = nar_index * block_tokens + jnp.arange(block_tokens, dtype=jnp.int32)
    doc_start, places = doc_layout(doc_lengths[0], token_ids)
    angles = places.astype(jnp.float32)[:, None] * inverse_freq()[None, :]
    cosine_table = jnp.cos(angles)[:, None, :]
    sine_table = jnp.sin(angles)[:, None, :]
    key_ids = jnp.arange(seq_length, dtype=jnp.int32)
    residual = hidden_in[0].astype(jnp.float32)
    root_attn, normed_attn = norm_forward(residual, gain_attn)
    normed_rows = lax.all_gather(normed_attn, "wid", axis=0, tiled=True)
    query_pre = jnp.dot(normed_rows, query_full, preferred_element_type=jnp.float32)
    key_pre = jnp.dot(normed_rows, key_local, preferred_element_type=jnp.float32)
    value_rows = jnp.dot(normed_rows, value_local, preferred_element_type=jnp.float32).astype(
        jnp.bfloat16
    )
    query_rot = (
        rotate(query_pre.reshape(block_tokens, query_heads, HD), cosine_table, sine_table)
        .astype(jnp.bfloat16)
        .reshape(block_tokens, query_heads * HD)
    )
    key_rot = (
        rotate(key_pre.reshape(block_tokens, kv_local, HD), cosine_table, sine_table)
        .astype(jnp.bfloat16)
        .reshape(block_tokens, kv_local * HD)
    )
    key_seq, value_seq = (
        lax.all_gather(key_rot, "nar", axis=0, tiled=True),
        lax.all_gather(value_rows, "nar", axis=0, tiled=True),
    )

    def item_inputs(item_index):
        block_index = item_index // query_heads
        head_index = item_index % query_heads
        kv_index = head_index // heads_per_kv
        row_first = block_index * query_block
        query_part = lax.dynamic_slice(query_rot, (row_first, head_index * HD), (query_block, HD))
        key_head = lax.dynamic_slice_in_dim(key_seq, kv_index * HD, HD, 1)
        value_head = lax.dynamic_slice_in_dim(value_seq, kv_index * HD, HD, 1)
        query_ids = lax.dynamic_slice_in_dim(token_ids, row_first, query_block, 0)
        query_starts = lax.dynamic_slice_in_dim(doc_start, row_first, query_block, 0)
        allowed = (key_ids[None, :] <= query_ids[:, None]) & (
            key_ids[None, :] >= query_starts[:, None]
        )
        scores = contract_last(query_part, key_head) * attn_scale
        return (
            row_first,
            head_index,
            kv_index,
            query_part,
            key_head,
            value_head,
            jnp.where(allowed, scores, masked_score),
        )

    def attend(item_index):
        row_first, head_index, kv_index, query_part, key_head, value_head, scores = item_inputs(
            item_index
        )
        row_max = jnp.max(scores, axis=1, keepdims=True)
        exp_scores = jnp.exp(scores - row_max)
        row_total = jnp.sum(exp_scores, axis=1, keepdims=True)
        probability = (exp_scores / row_total).astype(jnp.bfloat16)
        attended = jnp.dot(probability, value_head, preferred_element_type=jnp.float32)
        return (attended, (row_max + jnp.log(row_total))[:, 0])

    attended_items, logsum_items = lax.map(attend, jnp.arange(item_count, dtype=jnp.int32))
    attended_rows = (
        attended_items.reshape(block_count, query_heads, query_block, HD)
        .transpose(0, 2, 1, 3)
        .reshape(block_tokens, query_heads * HD)
        .astype(jnp.bfloat16)
    )
    rows_here = attended_rows
    branch_attn = lax.psum_scatter(
        jnp.dot(rows_here, output_full, preferred_element_type=jnp.float32),
        "wid",
        scatter_dimension=0,
        tiled=True,
    )
    middle = residual + branch_attn
    root_ffn, normed_ffn = norm_forward(middle, gain_ffn)
    ffn_rows = lax.all_gather(normed_ffn, "wid", axis=0, tiled=True)
    gate_proj = jnp.dot(ffn_rows, gate_full, preferred_element_type=jnp.float32)
    up_proj = jnp.dot(ffn_rows, up_full, preferred_element_type=jnp.float32)
    gate_sigmoid = jax.nn.sigmoid(gate_proj)
    gate_silu = gate_proj * gate_sigmoid
    activated = (gate_silu * up_proj).astype(jnp.bfloat16)
    rows_here = activated
    branch_ffn = lax.psum_scatter(
        jnp.dot(rows_here, down_full, preferred_element_type=jnp.float32).astype(jnp.bfloat16),
        "wid",
        scatter_dimension=0,
        tiled=True,
    ).astype(jnp.float32)
    hidden_out = (middle + branch_ffn).astype(jnp.bfloat16)[None]
    grad_top = grad_out[0]
    grad_rows = lax.all_gather(grad_top, "wid", axis=0, tiled=True)
    grad_activated = contract_last(grad_rows, down_full)
    down_weight_grad = contract_first(activated, grad_rows)
    silu_slope = gate_sigmoid * (1.0 + gate_proj * (1.0 - gate_sigmoid))
    grad_gate_b = (grad_activated * up_proj * silu_slope).astype(jnp.bfloat16)
    grad_up_b = (grad_activated * gate_silu).astype(jnp.bfloat16)
    gate_weight_grad = contract_first(ffn_rows, grad_gate_b)
    up_weight_grad = contract_first(ffn_rows, grad_up_b)
    grad_normed_ffn = lax.psum_scatter(
        contract_last(grad_gate_b, gate_full) + contract_last(grad_up_b, up_full),
        "wid",
        scatter_dimension=0,
        tiled=True,
    )
    grad_middle, gain_ffn_term = norm_backward(middle, root_ffn, gain_ffn, grad_normed_ffn)
    grad_middle = grad_middle + grad_top.astype(jnp.float32)
    grad_branch = grad_middle.astype(jnp.bfloat16)
    branch_rows = lax.all_gather(grad_branch, "wid", axis=0, tiled=True)
    grad_attended = contract_last(branch_rows, output_full).astype(jnp.bfloat16)
    output_weight_grad = contract_first(attended_rows, branch_rows)

    def attend_back(carried, item_index):
        key_grad, value_grad = carried
        row_first, head_index, kv_index, query_part, key_head, value_head, scores = item_inputs(
            item_index
        )
        logsum = lax.dynamic_index_in_dim(logsum_items, item_index, 0, keepdims=False)
        probability = jnp.exp(scores - logsum[:, None])
        grad_part = lax.dynamic_slice(
            grad_attended, (row_first, head_index * HD), (query_block, HD)
        )
        grad_prob = contract_last(grad_part, value_head)
        inner_sum = jnp.sum(probability * grad_prob, axis=1, keepdims=True)
        grad_scores = (probability * (grad_prob - inner_sum)).astype(jnp.bfloat16)
        query_grad = jnp.dot(grad_scores, key_head, preferred_element_type=jnp.float32) * attn_scale
        key_part = contract_first(grad_scores, query_part) * attn_scale
        value_part = contract_first(probability.astype(jnp.bfloat16), grad_part)
        key_old = lax.dynamic_slice_in_dim(key_grad, kv_index * HD, HD, 1)
        key_grad = lax.dynamic_update_slice_in_dim(key_grad, key_old + key_part, kv_index * HD, 1)
        value_old = lax.dynamic_slice_in_dim(value_grad, kv_index * HD, HD, 1)
        value_grad = lax.dynamic_update_slice_in_dim(
            value_grad, value_old + value_part, kv_index * HD, 1
        )
        return ((key_grad, value_grad), query_grad)

    zero_grads = jnp.zeros((seq_length, kv_local * HD), jnp.float32)
    (key_grad_seq, value_grad_seq), query_grad_items = lax.scan(
        attend_back, (zero_grads, zero_grads), jnp.arange(item_count, dtype=jnp.int32)
    )
    key_grad_block, value_grad_block = (
        lax.psum_scatter(
            key_grad_seq.astype(jnp.bfloat16), "nar", scatter_dimension=0, tiled=True
        ).astype(jnp.float32),
        lax.psum_scatter(
            value_grad_seq.astype(jnp.bfloat16), "nar", scatter_dimension=0, tiled=True
        ).astype(jnp.float32),
    )
    query_grad_rows = (
        query_grad_items.reshape(block_count, query_heads, query_block, HD)
        .transpose(0, 2, 1, 3)
        .reshape(block_tokens, query_heads, HD)
    )
    query_grad_b = (
        rotate_back(query_grad_rows, cosine_table, sine_table)
        .astype(jnp.bfloat16)
        .reshape(block_tokens, query_heads * HD)
    )
    key_grad_b = (
        rotate_back(key_grad_block.reshape(block_tokens, kv_local, HD), cosine_table, sine_table)
        .astype(jnp.bfloat16)
        .reshape(block_tokens, kv_local * HD)
    )
    value_grad_b = value_grad_block.astype(jnp.bfloat16)
    query_weight_grad = contract_first(normed_rows, query_grad_b)
    key_weight_grad = contract_first(normed_rows, key_grad_b)
    value_weight_grad = contract_first(normed_rows, value_grad_b)
    grad_normed_attn = lax.psum_scatter(
        (
            contract_last(query_grad_b, query_full)
            + contract_last(key_grad_b, key_local)
            + contract_last(value_grad_b, value_local)
        ).astype(jnp.bfloat16),
        "wid",
        scatter_dimension=0,
        tiled=True,
    ).astype(jnp.float32)
    grad_residual, gain_attn_term = norm_backward(residual, root_attn, gain_attn, grad_normed_attn)
    grad_in = (grad_residual + grad_middle).astype(jnp.bfloat16)[None]
    summed = (
        lax.psum_scatter(
            query_weight_grad.astype(jnp.bfloat16), ("row", "nar"), scatter_dimension=0, tiled=True
        ).astype(jnp.float32),
        lax.psum_scatter(
            key_weight_grad.astype(jnp.bfloat16), ("row", "nar"), scatter_dimension=0, tiled=True
        ).astype(jnp.float32),
        lax.psum_scatter(
            value_weight_grad.astype(jnp.bfloat16), ("row", "nar"), scatter_dimension=0, tiled=True
        ).astype(jnp.float32),
        lax.psum_scatter(
            output_weight_grad.astype(jnp.bfloat16), ("row", "nar"), scatter_dimension=1, tiled=True
        ).astype(jnp.float32),
        lax.psum_scatter(
            gate_weight_grad.astype(jnp.bfloat16), ("row", "nar"), scatter_dimension=0, tiled=True
        ).astype(jnp.float32),
        lax.psum_scatter(
            up_weight_grad.astype(jnp.bfloat16), ("row", "nar"), scatter_dimension=0, tiled=True
        ).astype(jnp.float32),
        lax.psum_scatter(
            down_weight_grad.astype(jnp.bfloat16), ("row", "nar"), scatter_dimension=1, tiled=True
        ).astype(jnp.float32),
        lax.psum_scatter(
            gain_attn_term.astype(jnp.bfloat16), ("row", "nar"), scatter_dimension=0, tiled=True
        ).astype(jnp.float32),
        lax.psum_scatter(
            gain_ffn_term.astype(jnp.bfloat16), ("row", "nar"), scatter_dimension=0, tiled=True
        ).astype(jnp.float32),
    )
    (
        grad_query,
        key_sum,
        value_sum,
        grad_output,
        grad_gate,
        grad_up,
        grad_down,
        gain_attn_sum,
        gain_ffn_sum,
    ) = summed
    key_all, value_all, gain_attn_all, gain_ffn_all = (
        lax.all_gather(key_sum.astype(jnp.bfloat16), "wid", axis=1, tiled=True).astype(
            key_sum.dtype
        ),
        lax.all_gather(value_sum.astype(jnp.bfloat16), "wid", axis=1, tiled=True).astype(
            value_sum.dtype
        ),
        lax.all_gather(gain_attn_sum.astype(jnp.bfloat16), "wid", axis=0, tiled=True).astype(
            gain_attn_sum.dtype
        ),
        lax.all_gather(gain_ffn_sum.astype(jnp.bfloat16), "wid", axis=0, tiled=True).astype(
            gain_ffn_sum.dtype
        ),
    )
    shard_rows = key_sum.shape[0]
    repeats = wid_count * kv_local // KV
    grad_key = key_all.reshape(shard_rows, KV, repeats, HD).sum(axis=2).reshape(shard_rows, KV * HD)
    grad_value = (
        value_all.reshape(shard_rows, KV, repeats, HD).sum(axis=2).reshape(shard_rows, KV * HD)
    )
    grad_gain_attn = gain_attn_all.reshape(wid_count, shard_rows).sum(axis=0)
    grad_gain_ffn = gain_ffn_all.reshape(wid_count, shard_rows).sum(axis=0)
    return (
        hidden_out,
        grad_in,
        grad_query,
        grad_key,
        grad_value,
        grad_output,
        grad_gate,
        grad_up,
        grad_down,
        grad_gain_attn,
        grad_gain_ffn,
    )


MESH = pl.DeviceIdType.MESH
bf16 = jnp.bfloat16
f32 = jnp.float32
VMEM_LIMIT = 60 * 2**20


def spot():
    return lax.axis_index("row"), lax.axis_index("nar"), lax.axis_index("wid")


def greet(partners):
    barrier = pltpu.get_barrier_semaphore()
    total = 0
    for there, device in partners:
        @pl.when(there)
        def _():
            pl.semaphore_signal(barrier, inc=1, device_id=device, device_id_type=MESH)

        total = total + there.astype(jnp.int32)
    pl.semaphore_wait(barrier, total)


def line_partners(r, n, w, wid_count):
    return [
        (w < wid_count - 1, (r, n, jnp.minimum(w + 1, wid_count - 1))),
        (w > 0, (r, n, jnp.maximum(w - 1, 0))),
        (w >= 0, (1 - r, n, w)),
    ]


def each_rows(count, step, body):
    def run(i, carry):
        body(pl.ds(pl.multiple_of(i * step, step), step))
        return carry

    lax.fori_loop(0, count // step, run, 0)


def square_partners(r, n, w):
    return [(n >= 0, over_x(r, n, w)), (n >= 0, over_y(r, n, w))]


def over_x(r, n, w):
    return (r, n + 1 - 2 * (n % 2), w)


def over_y(r, n, w):
    return (r, (n + 2) % 4, w)


def push(source, target, s_s, s_g, device):
    return pltpu.make_async_remote_copy(
        source, target, s_s, s_g, device_id=device, device_id_type=MESH
    )


class Square:
    def __init__(self, shard, full, sems, me):
        self.shard, self.full = shard, full
        self.sent, self.got = sems
        r, n, w = me
        self.n, self.x, self.y = n, n + 1 - 2 * (n % 2), (n + 2) % 4
        self.by_x, self.by_y = over_x(*me), over_y(*me)
        size = shard.shape[0] // 2
        self.upper, self.lower = pl.ds(0, size), pl.ds(size, size)

    def first(self, k, place):
        return push(
            self.shard, self.full.at[place], self.sent.at[k], self.got.at[k],
            (self.by_x, self.by_y)[k],
        )

    def second(self, k, place):
        part = self.full.at[place, (self.upper, self.lower)[k]]
        return push(
            part, part, self.sent.at[2 + k], self.got.at[2 + k], (self.by_y, self.by_x)[k]
        )

    def start(self):
        self.first(0, self.n).start()
        self.first(1, self.n).start()

    def turn(self):
        self.first(0, self.x).wait_recv()
        self.second(0, self.x).start()
        self.first(1, self.y).wait_recv()
        self.second(1, self.y).start()

    def finish(self):
        for k in range(2):
            self.second(k, 3 - self.n).wait_recv()
            self.first(k, self.n).wait_send()
            self.second(k, (self.x, self.y)[k]).wait_send()


def square_sems():
    return [pltpu.SemaphoreType.DMA((4,))] * 2


def fetch(own, full, target, sems, n):
    copies = [pltpu.make_async_copy(own, target.at[n], sems.at[0])]
    for k, place in enumerate((n + 1 - 2 * (n % 2), (n + 2) % 4, 3 - n)):
        copies.append(pltpu.make_async_copy(full.at[place], target.at[place], sems.at[1 + k]))
    return copies


class Gather:
    def __init__(self, buf, sems, me, wid_count, rows=slice(None), pair=True):
        self.rows, self.both = rows, pair
        self.buf, (self.up_s, self.dn_s, self.pt_s, self.got) = buf, sems
        self.r, self.n, self.w = me
        self.last = wid_count - 1
        self.up = (self.r, self.n, jnp.minimum(self.w + 1, self.last))
        self.dn = (self.r, self.n, jnp.maximum(self.w - 1, 0))
        self.pt = (1 - self.r, self.n, self.w)

    def copy(self, j, sem, device, row=None):
        row = (self.r if self.both else 0) if row is None else row
        return pltpu.make_async_remote_copy(
            self.buf.at[row, j, self.rows],
            self.buf.at[row, j, self.rows],
            sem.at[j],
            self.got.at[row, j],
            device_id=device,
            device_id_type=MESH,
        )

    def pass_on(self, j, go_up, go_dn):
        if go_up:
            @pl.when(self.w < self.last)
            def _():
                self.copy(j, self.up_s, self.up).start()

        if go_dn:
            @pl.when(self.w > 0)
            def _():
                self.copy(j, self.dn_s, self.dn).start()

        if self.both:
            self.copy(j, self.pt_s, self.pt).start()

    def own(self):
        self.pass_on(self.w, True, True)

    def arrive(self, row, j):
        self.copy(j, self.pt_s, self.pt, row).wait_recv()

    def step(self, k):
        below, above = self.w - k, self.w + k

        @pl.when(below >= 0)
        def _():
            self.arrive(None, below)
            self.pass_on(below, True, False)

        @pl.when(above <= self.last)
        def _():
            self.arrive(None, above)
            self.pass_on(above, False, True)

    def advance(self, edge_steps, inner_steps):
        at_end = (self.w == 0) | (self.w == self.last)
        for ends, steps in ((True, edge_steps), (False, inner_steps)):
            if steps:
                @pl.when(at_end if ends else jnp.logical_not(at_end))
                def _():
                    for k in steps:
                        self.step(k)

    def rest(self):
        for j in range(self.last + 1):
            self.arrive(1 - self.r, j)

    def sent(self):
        for j in range(self.last + 1):
            @pl.when((j <= self.w) & (self.w < self.last))
            def _():
                self.copy(j, self.up_s, self.up).wait_send()

            @pl.when((j >= self.w) & (self.w > 0))
            def _():
                self.copy(j, self.dn_s, self.dn).wait_send()

            if self.both:
                self.copy(j, self.pt_s, self.pt).wait_send()


def gather_scratch(shard, width):
    return [pltpu.VMEM((2, 4, shard, width), bf16)] + gather_sems()


def gather_sems():
    return [pltpu.SemaphoreType.DMA((4,))] * 3 + [pltpu.SemaphoreType.DMA((2, 4))]


class Scatter:
    def __init__(self, mine, theirs, bufs, sems, me, wid_count, first=0, count=None):
        self.mine, self.theirs = mine, theirs
        self.from_pt, self.from_up, self.from_dn = bufs
        self.pt_s, self.pt_g, self.up_s, self.up_g, self.dn_s, self.dn_g = sems
        self.r, self.n, self.w = me
        self.first, self.count = first, mine.shape[1] if count is None else count
        self.rows = pl.ds(first, self.count)
        self.last = wid_count - 1
        self.up = (self.r, self.n, jnp.minimum(self.w + 1, self.last))
        self.dn = (self.r, self.n, jnp.maximum(self.w - 1, 0))
        self.pt = (1 - self.r, self.n, self.w)

    def order(self, i):
        low = jnp.where(i == 0, 3, jnp.where(i == 1, 0, jnp.where(i == 2, 2, 1)))
        return jnp.where(self.w < 2, low, 3 - low)

    def send(self, source, target, sent, got, s, device):
        return pltpu.make_async_remote_copy(
            source.at[s, self.rows], target.at[s, self.rows], sent.at[s], got.at[s],
            device_id=device, device_id_type=MESH,
        )

    def pair(self, s):
        return self.send(self.theirs, self.from_pt, self.pt_s, self.pt_g, s, self.pt)

    def climb(self, s):
        return self.send(self.mine, self.from_dn, self.up_s, self.up_g, s, self.up)

    def fall(self, s):
        return self.send(self.mine, self.from_up, self.dn_s, self.dn_g, s, self.dn)

    def each(self, body):
        def run(i, carry):
            body(pl.ds(pl.multiple_of(self.first + i * 16, 16), 16))
            return carry

        lax.fori_loop(0, self.count // 16, run, 0)

    def add(self, s, others):
        def body(rows):
            total = self.mine[s, rows, :].astype(f32)
            for other in others:
                total = total + other[s, rows, :].astype(f32)
            self.mine[s, rows, :] = total.astype(bf16)

        self.each(body)

    def step(self, s):
        self.pair(s).wait_recv()

        @pl.when((s > self.w) & (self.w > 0))
        def _():
            self.climb(s).wait_recv()
            self.add(s, (self.from_pt, self.from_dn))

        @pl.when((s < self.w) & (self.w < self.last))
        def _():
            self.fall(s).wait_recv()
            self.add(s, (self.from_pt, self.from_up))

        @pl.when(((s > self.w) & (self.w == 0)) | ((s < self.w) & (self.w == self.last)))
        def _():
            self.add(s, (self.from_pt,))

        @pl.when(s > self.w)
        def _():
            self.climb(s).start()

        @pl.when(s < self.w)
        def _():
            self.fall(s).start()

    def advance(self, edge_steps, inner_steps):
        for ends, steps in ((True, edge_steps), (False, inner_steps)):
            at_end = (self.w == 0) | (self.w == self.last)

            def body(i, carry):
                self.step(self.order(i))
                return carry

            if steps:
                @pl.when(at_end if ends else jnp.logical_not(at_end))
                def _():
                    lax.fori_loop(steps[0], steps[-1] + 1, body, 0)

    def total(self, out):
        w = self.w

        def first(rows):
            out[rows, :] = self.mine[w, rows, :].astype(f32) + self.from_pt[w, rows, :].astype(f32)

        self.each(first)

        @pl.when(w > 0)
        def _():
            self.climb(w).wait_recv()

            def more(rows):
                out[rows, :] += self.from_dn[w, rows, :].astype(f32)

            self.each(more)

        @pl.when(w < self.last)
        def _():
            self.fall(w).wait_recv()

            def more(rows):
                out[rows, :] += self.from_up[w, rows, :].astype(f32)

            self.each(more)

    def sent(self):
        for s in range(self.last + 1):
            self.pair(s).wait_send()

            @pl.when(s > self.w)
            def _():
                self.climb(s).wait_send()

            @pl.when(s < self.w)
            def _():
                self.fall(s).wait_send()


def scatter_bufs(shard, width):
    return [pltpu.VMEM((4, shard, width), bf16)] * 3


def scatter_sems():
    return [pltpu.SemaphoreType.DMA((4,))] * 6


def vmem():
    return pl.BlockSpec(memory_space=pltpu.VMEM)


def hbm():
    return pl.BlockSpec(memory_space=pl.ANY)


def comm_call(kernel, name, cid, out_shape, in_specs, out_specs, scratch, args, flops=0, sent=0):
    return pl.pallas_call(
        kernel,
        out_shape=out_shape,
        in_specs=in_specs,
        out_specs=out_specs,
        scratch_shapes=scratch,
        compiler_params=pltpu.CompilerParams(
            collective_id=cid, has_side_effects=True, vmem_limit_bytes=VMEM_LIMIT
        ),
        cost_estimate=pl.CostEstimate(flops=flops, bytes_accessed=sent, transcendentals=0),
        name=name,
    )(*args)


def norm_rows(x, gain):
    root = lax.rsqrt(jnp.mean(x * x, axis=-1, keepdims=True) + norm_eps)
    return x * root * gain


def turn(x, cosine, sine):
    lane = lax.broadcasted_iota(jnp.int32, x.shape, 1)
    swapped = jnp.where(lane % 64 < 32, pltpu.roll(x, 96, 1), pltpu.roll(x, 32, 1))
    return x * cosine + swapped * sine


def nar_device(r, n, w, by):
    return (r, jnp.clip(n + by, 0, 3), w)


def enter_kernel(
    hidden, gain, tab, grad_top, p1_own, down_own,
    q_out, rows_out, tabs_out, p1_out, down_out, kv_out, tops_out,
    buf, up_s, dn_s, pt_s, got, tbuf, h0, h1, h2, h3, tabs, p1, kv,
    tab_s, tab_g, out_s, p1_s, p1_g, down_s, down_g, s_s, s_g,
):
    me = spot()
    r, n, w = me
    bring = pltpu.make_async_copy(p1_own, p1.at[n], out_s.at[0])
    bring.start()
    greet(
        line_partners(r, n, w, 4)
        + [
            (n >= 1, nar_device(r, n, w, -1)),
            (n >= 2, nar_device(r, n, w, -2)),
            (n <= 2, nar_device(r, n, w, 1)),
            (n <= 1, nar_device(r, n, w, 2)),
        ]
    )
    p1_square = Square(p1_own, p1, (p1_s, p1_g), me)
    down = Square(down_own.at[0:256], down_out, (down_s, down_g), me)
    p1_square.start()
    down.start()
    gather = Gather(buf, (up_s, dn_s, pt_s, got), me, 4)
    tops = Gather(tbuf, (h0, h1, h2, h3), me, 4)
    tab_copy = pltpu.make_async_remote_copy(
        tab, tabs.at[r], tab_s, tab_g, device_id=(1 - r, n, w), device_id_type=MESH
    )

    def body(rows):
        buf[r, w, rows, :] = norm_rows(hidden[rows, :].astype(f32), gain[...]).astype(bf16)

    each_rows(hidden.shape[0], 16, body)
    gather.own()
    tab_copy.start()

    def keep(rows):
        tabs[r, rows, :] = tab[rows, :]

    each_rows(tab.shape[0], 16, keep)

    def keep_top(rows):
        tbuf[r, w, rows, :] = grad_top[rows, :]

    each_rows(64, 16, keep_top)
    gather.step(1)
    p1_square.turn()
    gather.step(2)
    tops.own()
    down.turn()
    gather.step(3)
    gather.rest()
    tab_copy.wait_recv()
    p1_square.finish()
    bring.wait()
    outs = [
        pltpu.make_async_copy(buf, rows_out, out_s.at[1]),
        pltpu.make_async_copy(tabs, tabs_out, out_s.at[2]),
        pltpu.make_async_copy(p1, p1_out, out_s.at[3]),
    ]
    for out in outs:
        out.start()
    tops.step(1)

    def copy(row, slot, by):
        return pltpu.make_async_remote_copy(
            kv.at[row, 2], kv.at[row, slot], s_s.at[row, slot], s_g.at[row, slot],
            device_id=nar_device(r, n, w, by), device_id_type=MESH,
        )

    lane = lax.broadcasted_iota(jnp.int32, (256, 128), 1)
    weight = p1[:, :, 0:384].reshape(2048, 384)
    for row in range(2):
        def tile(i, carry):
            rows = pl.ds(pl.multiple_of(i * 256, 256), 256)
            cosine, sine = tabs[row, rows, 0:128], tabs[row, rows, 128:256]
            left = buf[row, pl.ds(i * 2, 2)].reshape(256, 2048)
            pre = jnp.dot(left, weight, preferred_element_type=f32)
            q_out[row, rows, 0:128] = turn(pre[:, 0:128], cosine, sine).astype(bf16)
            q_out[row, rows, 128:256] = turn(pre[:, 128:256], cosine, sine).astype(bf16)
            both = pre[:, 256:384]
            kv[row, 2, rows, :] = jnp.where(lane < 64, turn(both, cosine, sine), both).astype(bf16)
            return carry

        lax.fori_loop(0, 2, tile, 0)

        @pl.when(n <= 2)
        def _():
            copy(row, 1, 1).start()

        @pl.when(n <= 1)
        def _():
            copy(row, 0, 2).start()

        for slot, least in ((1, 1), (0, 2)):
            @pl.when(n < least)
            def _():
                kv[row, slot] = jnp.zeros((512, 128), bf16)

    tops.step(2)
    for row in range(2):
        for slot, least, by in ((1, 1, 1), (0, 2, 2)):
            @pl.when(n >= least)
            def _():
                copy(row, slot, by).wait_recv()

    outs.append(pltpu.make_async_copy(kv, kv_out, out_s.at[4]))
    outs[3].start()
    tops.step(3)
    tops.rest()
    outs.append(pltpu.make_async_copy(tbuf, tops_out, out_s.at[5]))
    outs[4].start()
    for row in range(2):
        @pl.when(n <= 2)
        def _():
            copy(row, 1, 1).wait_send()

        @pl.when(n <= 1)
        def _():
            copy(row, 0, 2).wait_send()

    gather.sent()
    tops.sent()
    tab_copy.wait_send()
    down.finish()
    for out in outs:
        out.wait()


def enter(hidden, gain, tab, grad_top, p1_own, down_own):
    shard, width = hidden.shape
    return comm_call(
        enter_kernel, "enter", 1,
        (
            jax.ShapeDtypeStruct((2, 512, 256), bf16),
            jax.ShapeDtypeStruct((2, 4, shard, width), bf16),
            jax.ShapeDtypeStruct((2,) + tab.shape, f32),
            jax.ShapeDtypeStruct((4,) + p1_own.shape, bf16),
            jax.ShapeDtypeStruct((4, 256, 1024), bf16),
            jax.ShapeDtypeStruct((2, 3, 512, 128), bf16),
            jax.ShapeDtypeStruct((2, 4, 64, width), bf16),
        ),
        [vmem()] * 4 + [hbm()] * 2, [vmem()] + [hbm()] * 6,
        gather_scratch(shard, width)
        + gather_scratch(64, width)
        + [
            pltpu.VMEM((2,) + tab.shape, f32),
            pltpu.VMEM((4,) + p1_own.shape, bf16),
            pltpu.VMEM((2, 3, 512, 128), bf16),
            pltpu.SemaphoreType.DMA(()),
            pltpu.SemaphoreType.DMA(()),
            pltpu.SemaphoreType.DMA((6,)),
        ]
        + square_sems() * 2
        + [pltpu.SemaphoreType.DMA((2, 3))] * 2,
        (hidden, gain, tab, grad_top, p1_own, down_own), flops=10**10, sent=10**8,
    )


KEYS = 256
QUERIES = 128


def stack_low(x):
    lane = lax.broadcasted_iota(jnp.int32, (QUERIES, 128), 1)
    zero = jnp.zeros((QUERIES, 128), x.dtype)
    parts = []
    for pair in range(2):
        block = x[:, pair * 128 : pair * 128 + 128]
        parts.append(jnp.where(lane < 64, block, zero))
        parts.append(jnp.where(lane < 64, pltpu.roll(block, 64, 1), zero))
    return jnp.concatenate(parts, axis=0)


def stack_high(x):
    lane = lax.broadcasted_iota(jnp.int32, (QUERIES, 128), 1)
    zero = jnp.zeros((QUERIES, 128), x.dtype)
    parts = []
    for pair in range(2):
        block = x[:, pair * 128 : pair * 128 + 128]
        parts.append(jnp.where(lane >= 64, pltpu.roll(block, 64, 1), zero))
        parts.append(jnp.where(lane >= 64, block, zero))
    return jnp.concatenate(parts, axis=0)


def unstack(x, low):
    lane = lax.broadcasted_iota(jnp.int32, (QUERIES, 128), 1)
    out = []
    for pair in range(2):
        even = x[2 * pair * QUERIES : (2 * pair + 1) * QUERIES]
        odd = x[(2 * pair + 1) * QUERIES : (2 * pair + 2) * QUERIES]
        if low:
            out.append(jnp.where(lane < 64, even, pltpu.roll(odd, 64, 1)))
        else:
            out.append(jnp.where(lane < 64, pltpu.roll(even, 64, 1), odd))
    return jnp.concatenate(out, axis=1)


def allowed_tile(starts, tile, first_query):
    key = lax.broadcasted_iota(jnp.int32, (QUERIES, KEYS), 1) + tile * KEYS
    query = lax.broadcasted_iota(jnp.int32, (QUERIES, KEYS), 0) + first_query
    start = jnp.concatenate([starts] * (KEYS // 128), axis=1)
    ok = (key <= query) & (key.astype(f32) >= start)
    return jnp.concatenate([ok] * 4, axis=0)


def attend_block(q, kv, starts, first_query):
    query = stack_low(q.astype(f32)).astype(bf16)

    def body(step, carry):
        tile = (first_query - 1024) // KEYS + step
        top, total, acc = carry
        both = kv[pl.ds(pl.multiple_of(tile * KEYS, KEYS), KEYS), :]
        scores = contract_last(query, both) * 0.125
        ok = allowed_tile(starts, tile, first_query)
        scores = jnp.where(ok, scores, masked_score)
        new_top = jnp.maximum(top, jnp.max(scores, axis=1, keepdims=True))
        shrink = jnp.exp(top - new_top)
        part = jnp.exp(scores - new_top)
        total = total * shrink + jnp.sum(part, axis=1, keepdims=True)
        acc = acc * shrink + jnp.dot(part.astype(bf16), both, preferred_element_type=f32)
        return new_top, total, acc

    top, total, acc = lax.fori_loop(
        0, 5, body,
        (
            jnp.full((4 * QUERIES, 1), masked_score, f32),
            jnp.zeros((4 * QUERIES, 1), f32),
            jnp.zeros((4 * QUERIES, 128), f32),
        ),
        unroll=True,
    )
    logsum = jnp.broadcast_to(top + jnp.log(total), (4 * QUERIES, 128))
    return unstack(acc / total, False).astype(bf16), logsum


def out_block(p1, nn, half):
    return p1[nn, half * 256 : half * 256 + 256, 384:640]


def middle_kernel(
    q, kv, tabs, p1, hidden, gain, gate_own, up_own, down_own,
    att, lse, mid_out, ffn_out, gate_out, up_out, down_out,
    theirs, mine, from_pt, from_up, from_dn, s0, s1, s2, s3, s4, s5, fbuf, h0, h1, h2, h3, out_s,
    gate_s, gate_g, up_s, up_g, down_s, down_g,
):
    me = spot()
    r, n, w = me
    greet(line_partners(r, n, w, 4) + square_partners(r, n, w))
    here = pl.ds(pl.multiple_of(r * 1024, 1024), 1024)
    gate = Square(gate_own.at[:, here], gate_out, (gate_s, gate_g), me)
    up = Square(up_own.at[:, here], up_out, (up_s, up_g), me)
    gate.start()
    up.start()
    down = Square(down_own.at[256:512], down_out, (down_s, down_g), me)
    down.start()
    scatter = Scatter(
        mine, theirs, (from_pt, from_up, from_dn), (s0, s1, s2, s3, s4, s5), me, 4
    )
    ffn = Gather(fbuf, (h0, h1, h2, h3), me, 4)
    def shard(i, carry):
        s = scatter.order(i)
        rows = pl.ds(pl.multiple_of(s * 128, 128), 128)
        for row in range(2):
            att[row, rows, :], lse[row, s] = attend_block(
                q[row, rows, :], kv.at[row], tabs[row, rows, 256:384], 1024 + s * 128
            )

        @pl.when((i >= 1) & ((w == 0) | (w == 3)))
        def _():
            scatter.step(scatter.order(i - 1))

        left = jnp.concatenate([att[1 - r, rows, :], att[r, rows, :]], axis=0)
        for nn in range(4):
            for half in range(2):
                part = jnp.dot(left, out_block(p1, nn, half), preferred_element_type=f32).astype(bf16)
                columns = slice(nn * 512 + half * 256, nn * 512 + half * 256 + 256)
                theirs[s, :, columns] = part[0:128]
                mine[s, :, columns] = part[128:256]
        scatter.pair(s).start()
        return carry

    lax.fori_loop(0, 4, shard, 0)
    scatter.advance((3,), (0, 1, 2, 3))
    scatter.total(mid_out)

    def body(rows):
        middle = mid_out[rows, :] + hidden[rows, :].astype(f32)
        mid_out[rows, :] = middle
        fbuf[r, w, rows, :] = norm_rows(middle, gain[...]).astype(bf16)

    each_rows(hidden.shape[0], 16, body)
    ffn.own()
    gate.turn()
    up.turn()
    ffn.step(1)
    down.turn()
    ffn.step(2)
    ffn.step(3)
    ffn.rest()
    out_f = pltpu.make_async_copy(fbuf, ffn_out, out_s)
    out_f.start()
    scatter.sent()
    ffn.sent()
    gate.finish()
    up.finish()
    down.finish()
    out_f.wait()


def middle_stage(q, kv, tabs, p1, hidden, gain, *weights):
    shard, width = hidden.shape
    rows = jax.ShapeDtypeStruct((2, 4, shard, width), bf16)
    return comm_call(
        middle_kernel, "middle", 3,
        (
            jax.ShapeDtypeStruct((2, 512, 256), bf16),
            jax.ShapeDtypeStruct((2, 4, 4 * QUERIES, 128), f32),
            jax.ShapeDtypeStruct((shard, width), f32),
            rows,
        )
        + (jax.ShapeDtypeStruct((4, 512, 1024), bf16),) * 2
        + (jax.ShapeDtypeStruct((4, 256, 1024), bf16),),
        [vmem()] * 6 + [hbm()] * 3, [vmem()] * 3 + [hbm()] * 4,
        [pltpu.VMEM((4, shard, width), bf16)] * 2
        + scatter_bufs(shard, width) + scatter_sems()
        + gather_scratch(shard, width)
        + [pltpu.SemaphoreType.DMA(())]
        + square_sems() * 3,
        (q, kv, tabs, p1, hidden, gain, *weights), flops=10**10, sent=2 * 10**8,
    )


class Spread:
    def __init__(self, outs, sems, me):
        self.a_send, self.a_keep, self.b_send, self.b_keep = outs
        self.r, self.n, self.w = me
        self.give_s, self.give_g, self.keep_s = sems

    def copies(self, wide, row, place, give):
        for k in range(4):
            block = wide.at[self.n ^ k]
            for part in range(2):
                source = block.at[pl.ds(part * 128, 128)]
                if part == 0:
                    target = (self.a_send if k & 1 else self.a_keep).at[k >> 1]
                else:
                    target = (self.b_send if k >= 2 else self.b_keep).at[k & 1]
                target = place(target)
                at = k * 2 + part
                if give:
                    yield pltpu.make_async_remote_copy(
                        source, target, self.give_s.at[row, at], self.give_g.at[row, at],
                        device_id=(1 - self.r, self.n, self.w), device_id_type=MESH,
                    )
                else:
                    yield pltpu.make_async_copy(source, target, self.keep_s.at[row, at])

    def start(self, *args):
        for copy in self.copies(*args):
            copy.start()

    def wait_send(self, *args):
        for copy in self.copies(*args):
            copy.wait_send()

    def wait_recv(self, *args):
        for copy in self.copies(*args):
            copy.wait_recv()

    def wait(self, *args):
        for copy in self.copies(*args):
            copy.wait()


def spread_sems(count):
    return [pltpu.SemaphoreType.DMA((count, 8))] * 3


def ffn_kernel(
    x, tops_in, grad_top, gate_own, gate_in, up_own, up_in, down_own, down_a, down_b, gain,
    part_out, sum_out, gain_out, o0, o1, o2, o3, ra_out, rb_out,
    theirs, mine, from_pt, from_up, from_dn, s0, s1, s2, s3, s4, s5,
    act, dgu, wide, out_s, give_s, give_g, keep_s, p2, in_s, n_s, n_g,
    tops4, h0, h1, h2, h3, tops_s,
):
    me = spot()
    r, n, w = me
    here = pl.ds(pl.multiple_of(r * 1024, 1024), 1024)
    loads = [
        fetch(gate_own.at[:, here], gate_in, p2.at[0], in_s.at[0], n),
        fetch(up_own.at[:, here], up_in, p2.at[1], in_s.at[1], n),
        fetch(down_own.at[0:256], down_a, p2.at[2, :, 0:256], in_s.at[2], n)
        + fetch(down_own.at[256:512], down_b, p2.at[2, :, 256:512], in_s.at[3], n),
        [pltpu.make_async_copy(tops_in, tops4.at[:, :, 0:64], tops_s)],
    ]
    for group in loads:
        for load in group:
            load.start()

    def loaded(k):
        for load in loads[k]:
            load.wait()

    greet(line_partners(r, n, w, 4) + square_partners(r, n, w))
    scatter = Scatter(
        mine, theirs, (from_pt, from_up, from_dn), (s0, s1, s2, s3, s4, s5), me, 4
    )
    late = pl.ds(64, 64)
    gather = Gather(tops4, (h0, h1, h2, h3), me, 4, late)

    def keep(rows):
        tops4[r, w, pl.ds(64 + rows.start, 16), :] = grad_top[pl.ds(64 + rows.start, 16), :]

    each_rows(64, 16, keep)
    gather.own()
    gain_out[...] = jnp.zeros_like(gain_out)
    loaded(0)
    loaded(1)

    def hidden_tile(i, carry):
        ft, row = i // 2, i % 2
        rows = pl.ds(pl.multiple_of(row * 512, 512), 512)
        columns = pl.ds(pl.multiple_of(ft * 256, 256), 256)
        left = x[rows, :]
        gate = jnp.dot(left, p2[0, :, :, columns].reshape(2048, 256), preferred_element_type=f32)
        up = jnp.dot(left, p2[1, :, :, columns].reshape(2048, 256), preferred_element_type=f32)
        sig = 1.0 / (1.0 + jnp.exp(-gate))
        silu = gate * sig
        act[rows, columns] = (silu * up).astype(bf16)
        dgu[rows, columns] = (up * (sig * (1.0 + gate * (1.0 - sig)))).astype(bf16)
        later = pl.ds(pl.multiple_of(1024 + ft * 256, 256), 256)
        dgu[rows, later] = silu.astype(bf16)
        return carry

    lax.fori_loop(0, 4, hidden_tile, 0)
    gather.step(1)
    lax.fori_loop(4, 8, hidden_tile, 0)
    gather.step(2)
    loaded(2)

    def down_tile(dt, carry):
        nn, half = dt // 2, dt % 2
        columns = pl.ds(pl.multiple_of(dt * 256, 256), 256)
        inner = pl.ds(pl.multiple_of(half * 256, 256), 256)
        other = pl.ds(pl.multiple_of(512 + half * 256, 256), 256)
        right = jnp.concatenate([p2[2, nn, :, inner], p2[2, nn, :, other]], axis=0)
        for row, stage in ((0, theirs), (1, mine)):
            part = jnp.dot(act[row * 512 : row * 512 + 512, :], right, preferred_element_type=f32)
            stage[:, :, columns] = part.astype(bf16).reshape(4, 128, 256)
        return carry

    lax.fori_loop(0, 8, down_tile, 0)
    puts = [
        pltpu.make_async_copy(theirs, part_out.at[0], out_s.at[0]),
        pltpu.make_async_copy(mine, part_out.at[1], out_s.at[1]),
    ]
    for put in puts:
        put.start()
    gather.step(3)
    gather.rest()
    loaded(3)

    def top_rows(row):
        return tops4[row].reshape(512, 2048)

    def back_tile(ft, carry):
        columns = pl.ds(pl.multiple_of(ft * 256, 256), 256)
        f_rows = pl.ds(pl.multiple_of((ft % 2) * 256, 256), 256)
        f_cols = pl.ds(pl.multiple_of((ft // 2) * 512, 512), 512)
        later = pl.ds(pl.multiple_of(1024 + ft * 256, 256), 256)
        right = jnp.concatenate([p2[2, nn, f_rows, f_cols] for nn in range(4)], axis=1)
        for row in range(2):
            rows = slice(row * 512, row * 512 + 512)
            dact = contract_last(top_rows(row), right)
            dgu[rows, columns] = (dact * dgu[rows, columns].astype(f32)).astype(bf16)
            dgu[rows, later] = (dact * dgu[rows, later].astype(f32)).astype(bf16)
        return carry

    lax.fori_loop(0, 4, back_tile, 0)
    for put in puts:
        put.wait()

    spread = Spread((o0, o1, o2, o3), (give_s, give_g, keep_s), me)
    columns_here = pl.ds(pl.multiple_of(r * 1024, 1024), 1024)
    slots = {2: 0, 0: 1, 1: 0}

    def moved(which, half):
        def place(target):
            return target.at[which, :, columns_here]

        return wide.at[slots[which], half], which, place, half == 0

    def weights(which, between=None):
        for half in range(2):
            d_first = (jnp.where(half == 0, 1 - r, r)) * 1024

            def weight_tile(i, carry):
                d_cols = pl.ds(pl.multiple_of(d_first + i * 256, 256), 256)
                if which < 2:
                    left = x[:, d_cols]
                    right = dgu[:, which * 1024 : which * 1024 + 1024]
                else:
                    left = tops4[:, :, :, d_cols].reshape(1024, 256)
                    right = act[...]
                wide[slots[which], half, i] = contract_first(left, right).astype(bf16)
                return carry

            lax.fori_loop(0, 4, weight_tile, 0)
            spread.start(*moved(which, half))
            if half == 0 and between is not None:
                between()

    def hop(which, at):
        return (
            push(o0.at[:, which], ra_out.at[at], n_s.at[0, at], n_g.at[0, at], over_x(r, n, w)),
            push(o2.at[:, which], rb_out.at[at], n_s.at[1, at], n_g.at[1, at], over_y(r, n, w)),
        )

    hops = hop(2, 0) + (
        push(o0.at[1, 0], ra_out.at[1, 1], n_s.at[0, 1], n_g.at[0, 1], over_x(r, n, w)),
        push(o2.at[1, 0], rb_out.at[1, 1], n_s.at[1, 1], n_g.at[1, 1], over_y(r, n, w)),
    )
    for i in range(4):
        s = scatter.order(i)
        rows_t = pl.ds(pl.multiple_of((1 - r) * 512 + s * 128, 128), 128)
        rows_m = pl.ds(pl.multiple_of(r * 512 + s * 128, 128), 128)

        def model_tile(dt, carry):
            nn, half = dt // 2, dt % 2
            columns = pl.ds(pl.multiple_of(dt * 256, 256), 256)
            inner = pl.ds(pl.multiple_of(half * 256, 256), 256)
            left = jnp.concatenate([dgu[rows_t, :], dgu[rows_m, :]], axis=0)
            right = jnp.concatenate([p2[0, nn, inner, :], p2[1, nn, inner, :]], axis=1)
            part = contract_last(left, right)
            seen = jnp.concatenate([x[rows_t, columns], x[rows_m, columns]], axis=0)
            terms = part * seen.astype(f32)
            gain_out[:, columns] += jnp.sum(terms.reshape(32, 8, 256), axis=0)
            part = part.astype(bf16)
            theirs[s, :, columns] = part[0:128]
            mine[s, :, columns] = part[128:256]
            return carry

        lax.fori_loop(0, 8, model_tile, 0)
        scatter.pair(s).start()
        if i == 0:
            weights(2, lambda: scatter.advance((0,), ()))
        elif i < 3:
            which = (2, 0)[i - 1]
            spread.wait_recv(*moved(which, 0))
            spread.wait(*moved(which, 1))
            hops[2 * i - 2].start()
            hops[2 * i - 1].start()
        if i == 1:
            weights(0, lambda: scatter.advance((1,), ()))
            scatter.advance((), (0,))
        elif i > 1:
            scatter.advance((i,), (1,) if i == 3 else ())

    def scale(rows):
        gain_out[rows, :] = gain_out[rows, :] / gain[...]

    each_rows(8, 8, scale)
    spread.wait_send(*moved(2, 0))
    weights(1)
    scatter.advance((), (2, 3))
    scatter.total(sum_out)
    scatter.sent()
    gather.sent()
    spread.wait_send(*moved(0, 0))
    spread.wait_recv(*moved(1, 0))
    spread.wait_send(*moved(1, 0))
    spread.wait(*moved(1, 1))
    for hop in hops:
        hop.wait()


def spread_shapes(*dims):
    return (jax.ShapeDtypeStruct((2,) + dims, bf16),) * 4


def ffn_stage(*args):
    shard, width = 128, 2048
    return comm_call(
        ffn_kernel, "ffn", 4,
        (
            jax.ShapeDtypeStruct((2, 4, shard, width), bf16),
            jax.ShapeDtypeStruct((shard, width), f32),
            jax.ShapeDtypeStruct((8, width), f32),
        )
        + spread_shapes(3, 128, width)
        + (jax.ShapeDtypeStruct((2, 2, 128, width), bf16),) * 2,
        [vmem(), hbm(), vmem()] + [hbm()] * 7 + [vmem()], [hbm(), vmem(), vmem()] + [hbm()] * 6,
        [pltpu.VMEM((4, shard, width), bf16)] * 2
        + scatter_bufs(shard, width) + scatter_sems()
        + [
            pltpu.VMEM((1024, 1024), bf16),
            pltpu.VMEM((1024, 2048), bf16),
            pltpu.VMEM((2, 2, 4, 256, 1024), bf16),
            pltpu.SemaphoreType.DMA((2,)),
        ]
        + spread_sems(3)
        + [pltpu.VMEM((3, 4, 512, 1024), bf16), pltpu.SemaphoreType.DMA((4, 4))]
        + [pltpu.SemaphoreType.DMA((2, 2))] * 2
        + gather_scratch(shard, width)
        + [pltpu.SemaphoreType.DMA(())],
        args, flops=4 * 10**10, sent=10**8,
    )


def norm_back(values, gain, grad):
    root = lax.rsqrt(jnp.mean(values * values, axis=-1, keepdims=True) + norm_eps)
    weighted = grad * gain
    inner = jnp.mean(weighted * values, axis=-1, keepdims=True)
    return root * weighted - values * (root * root * root) * inner


def back_kernel(
    total, mid, grad_top, gain_f, p1, att, q, kv, lse, x, tabs, gain,
    parts, a_send, b_send, a_keep, b_keep, a_came, b_came,
    gmid_out, part_out, gain_out, hid_out, o0, o1, o2, o3, oa_out, ob_out,
    q0, q1, q2, q3, ua_out, ub_out, ga_out, gb_out, la_out, lb_out,
    buf, g0, g1, g2, g3, grad, wide, give_s, give_g, keep_s,
    send, recv, both, wide_q, wide_kv, s_s, s_g, qgive_s, qgive_g, qkeep_s,
    mine, from_pt, from_up, from_dn, s0, s1, s2, s3, s4, s5,
    kept, came, acc, in_s, n_s, n_g, m_s, dkv,
):
    me = spot()
    r, n, w = me
    x_side, y_side = over_x(r, n, w), over_y(r, n, w)
    loads = [pltpu.make_async_copy(parts.at[r], mine, m_s)]
    for j, (keep, first) in enumerate(((a_keep, a_came), (b_keep, b_came))):
        loads += [
            pltpu.make_async_copy(keep.at[1], kept.at[j], in_s.at[j, 0]),
            pltpu.make_async_copy(first.at[1, 1], came.at[j, 0], in_s.at[j, 1]),
            pltpu.make_async_copy(first.at[0, 1], came.at[j, 2], in_s.at[j, 2]),
        ]
    for load in loads:
        load.start()
    greet(
        line_partners(r, n, w, 4)
        + [
            (n >= 1, nar_device(r, n, w, -1)),
            (n >= 2, nar_device(r, n, w, -2)),
            (n <= 2, nar_device(r, n, w, 1)),
            (n <= 1, nar_device(r, n, w, 2)),
        ]
    )
    scatter = Scatter(
        mine, parts.at[1 - r], (from_pt, from_up, from_dn), (s0, s1, s2, s3, s4, s5), me, 4
    )
    gather = Gather(buf, (g0, g1, g2, g3), me, 4)

    def hop(k, source, target, device):
        return push(source, target, n_s.at[k], n_g.at[k], device)

    up_hops = [
        hop(0, a_send.at[:, 1], ua_out, x_side),
        hop(1, b_send.at[:, 1], ub_out, y_side),
    ]
    last_hops = [
        [
            hop(2 + which, kept.at[0, which], la_out.at[which], y_side),
            hop(5 + which, kept.at[1, which], lb_out.at[which], x_side),
        ]
        for which in range(3)
    ]
    gate_hops = [hop(10, a_send.at[0, 0], ga_out, x_side), hop(11, b_send.at[0, 0], gb_out, y_side)]
    o_hops = [hop(8, o0, oa_out, x_side), hop(9, o2, ob_out, y_side)]
    for one in up_hops:
        one.start()

    def body(rows):
        got = norm_back(mid[rows, :], gain_f[...], total[rows, :]) + grad_top[rows, :].astype(f32)
        gmid_out[rows, :] = got
        buf[r, w, rows, :] = got.astype(bf16)

    each_rows(mid.shape[0], 16, body)
    gather.own()
    for load in loads:
        load.wait()

    def join(which):
        for j in range(2):
            def add(rows):
                one = kept[j, which, rows, :].astype(f32) + came[j, which, rows, :].astype(f32)
                kept[j, which, rows, :] = one.astype(bf16)

            each_rows(128, 16, add)
            last_hops[which][j].start()

    join(2)
    join(0)
    for one in gate_hops:
        one.start()
    for i in range(4):
        scatter.pair(scatter.order(i)).start()
    for k in (1, 2, 3):
        gather.step(k)
    gather.rest()
    scatter.advance((0, 1, 2, 3), ())
    for row in range(2):
        for pair in range(2):
            left = jnp.concatenate([buf[row, 2 * pair], buf[row, 2 * pair + 1]], axis=0)
            right = jnp.concatenate(
                [out_block(p1, nn, half) for nn in range(4) for half in range(2)], axis=1
            )
            grad[row, pair * 256 : pair * 256 + 256, :] = contract_last(left, right).astype(bf16)

    def copy(row, slot, by):
        return pltpu.make_async_remote_copy(
            send.at[row, slot], recv.at[row, slot], s_s.at[row, slot], s_g.at[row, slot],
            device_id=nar_device(r, n, w, by), device_id_type=MESH,
        )

    def attention(i, carry):
        row, block = i // 4, i % 4
        first_query = 1024 + block * QUERIES
        here = pl.ds(pl.multiple_of(block * QUERIES, QUERIES), QUERIES)

        @pl.when(block == 0)
        def _():
            dkv[row] = jnp.zeros((1536, 128), f32)

        query = stack_low(q[row, here, :].astype(f32)).astype(bf16)
        grads = stack_high(grad[row, here, :].astype(f32))
        inner = jnp.sum(grads * stack_high(att[row, here, :].astype(f32)), axis=1, keepdims=True)
        grads = grads.astype(bf16)
        logsum = jnp.concatenate([lse[row, block]] * (KEYS // 128), axis=1)
        starts = tabs[row, here, 256:384]

        def key_tile(step, dq):
            tile = block // 2 + step
            rows = pl.ds(pl.multiple_of(tile * KEYS, KEYS), KEYS)
            pair = kv[row, rows, :]
            ok = allowed_tile(starts, tile, first_query)
            scores = contract_last(query, pair) * 0.125
            prob = jnp.where(ok, jnp.exp(scores - logsum), 0.0)
            grad_prob = contract_last(grads, pair)
            grad_scores = (prob * (grad_prob - inner)).astype(bf16)
            dkv[row, rows, :] += contract_first(grad_scores, query) * 0.125 + contract_first(
                prob.astype(bf16), grads
            )
            return dq + jnp.dot(grad_scores, pair, preferred_element_type=f32)

        dq = lax.fori_loop(0, 5, key_tile, jnp.zeros((4 * QUERIES, 128), f32), unroll=True)
        flat = unstack(dq, True) * 0.125
        cosine, sine = tabs[row, here, 0:128], -tabs[row, here, 128:256]
        there = pl.ds(pl.multiple_of(i * QUERIES, QUERIES), QUERIES)
        both[there, 0:128] = turn(flat[:, 0:128], cosine, sine).astype(bf16)
        both[there, 128:256] = turn(flat[:, 128:256], cosine, sine).astype(bf16)

        @pl.when(block == 3)
        def _():
            for slot, by in ((1, -1), (0, -2)):
                @pl.when(n >= -by)
                def _():
                    send[row, slot] = dkv[row, slot * 512 : slot * 512 + 512, :].astype(bf16)
                    copy(row, slot, by).start()

        @pl.when(i == 3)
        def _():
            scatter.advance((), (0,))

        return carry

    lax.fori_loop(0, 8, attention, 0)
    scatter.advance((), (1,))

    fresh = []
    for j, first in enumerate((ua_out, ub_out)):
        up_hops[j].wait_recv()
        fresh.append(pltpu.make_async_copy(first.at[1], came.at[j, 1], in_s.at[j, 3]))
        fresh[j].start()
    for load in fresh:
        load.wait()
    join(1)

    spread_o = Spread((o0, o1, o2, o3), (give_s, give_g, keep_s), me)
    spread = Spread((q0, q1, q2, q3), (qgive_s, qgive_g, qkeep_s), me)

    def moved_o(half):
        def place(target):
            return target.at[:, pl.ds(pl.multiple_of(r * 256, 256), 256)]

        return wide.at[half], 0, place, half == 0

    for half in range(2):
        d_first = (jnp.where(half == 0, 1 - r, r)) * 1024

        def weight_tile(i, carry):
            columns = pl.ds(pl.multiple_of(d_first + i * 256, 256), 256)
            left = buf[:, :, :, columns].reshape(1024, 256)
            wide[half, i] = contract_first(left, att[...].reshape(1024, 256)).astype(bf16)
            return carry

        lax.fori_loop(0, 4, weight_tile, 0)
        spread_o.start(*moved_o(half))

    def moved_q(half):
        def place(target):
            return target.at[:, pl.ds(pl.multiple_of(r * 256, 256), 256)]

        return wide_q.at[half], 0, place, half == 0

    def moved_kv(half):
        def place(target):
            return target.at[:, pl.ds(pl.multiple_of(512 + r * 128, 128), 128)]

        return wide_kv.at[half], 1, place, half == 0

    def weight(half, columns, wide):
        d_first = (jnp.where(half == 0, 1 - r, r)) * 1024

        def tile(i, carry):
            d_cols = pl.ds(pl.multiple_of(d_first + i * 256, 256), 256)
            wide[half, i] = contract_first(x[:, d_cols], both[:, columns]).astype(bf16)
            return carry

        lax.fori_loop(0, 4, tile, 0)

    for half in range(2):
        weight(half, slice(0, 256), wide_q)
        spread.start(*moved_q(half))
    lane = lax.broadcasted_iota(jnp.int32, (128, 128), 1)
    for row in range(2):
        for slot, by in ((1, -1), (0, -2)):
            @pl.when(n <= 3 + by)
            def _():
                copy(row, slot, by).wait_recv()

        def tile(i, carry):
            rows = pl.ds(pl.multiple_of(i * 128, 128), 128)
            total = dkv[row, pl.ds(pl.multiple_of(1024 + i * 128, 128), 128), :]
            zero = jnp.zeros_like(total)
            total = total + jnp.where(n <= 2, recv[row, 1, rows, :].astype(f32), zero)
            total = total + jnp.where(n <= 1, recv[row, 0, rows, :].astype(f32), zero)
            turned = turn(total, tabs[row, rows, 0:128], -tabs[row, rows, 128:256])
            both[pl.ds(pl.multiple_of(row * 512 + i * 128, 128), 128), 256:384] = jnp.where(
                lane < 64, turned, total
            ).astype(bf16)
            return carry

        lax.fori_loop(0, 4, tile, 0)
    for half in range(2):
        weight(half, slice(256, 384), wide_kv)
        spread.start(*moved_kv(half))
    scatter.advance((), (2,))
    spread_o.wait_recv(*moved_o(0))
    spread_o.wait(*moved_o(1))
    for one in o_hops:
        one.start()
    gain_out[...] = jnp.zeros_like(gain_out)

    def model_tile(dt, carry):
        nn, half = dt // 2, dt % 2
        columns = pl.ds(pl.multiple_of(dt * 256, 256), 256)
        inner = pl.ds(pl.multiple_of(half * 256, 256), 256)
        right = p1[nn, inner, 0:384]
        for row in range(2):
            for block in range(2):
                first = row * 512 + block * 256
                part = contract_last(both[first : first + 256, :], right)
                terms = part * x[first : first + 256, columns].astype(f32)
                gain_out[:, columns] += jnp.sum(terms.reshape(32, 8, 256), axis=0)
                part_out[row, 2 * block, :, columns] = part[0:128].astype(bf16)
                part_out[row, 2 * block + 1, :, columns] = part[128:256].astype(bf16)
        return carry

    lax.fori_loop(0, 8, model_tile, 0)
    gain_out[...] = gain_out[...] / gain[...]
    scatter.advance((), (3,))
    scatter.total(acc)

    def last(rows):
        hid_out[rows, :] = (acc[rows, :] + mid[rows, :]).astype(bf16)

    each_rows(128, 16, last)
    scatter.sent()
    for row in range(2):
        for slot, by in ((1, -1), (0, -2)):
            @pl.when(n >= -by)
            def _():
                copy(row, slot, by).wait_send()

    for half in range(2):
        spread.wait(*moved_q(half))
        spread.wait(*moved_kv(half))
    spread_o.wait_send(*moved_o(0))
    gather.sent()
    for one in up_hops:
        one.wait_send()
    for one in last_hops[0] + last_hops[1] + last_hops[2] + gate_hops + o_hops:
        one.wait()


def back(*args):
    shard, width = 128, 2048
    return comm_call(
        back_kernel, "back", 5,
        (
            jax.ShapeDtypeStruct((shard, width), f32),
            jax.ShapeDtypeStruct((2, 4, shard, width), bf16),
            jax.ShapeDtypeStruct((8, width), f32),
            jax.ShapeDtypeStruct((shard, width), bf16),
        )
        + spread_shapes(128, 512)
        + (jax.ShapeDtypeStruct((2, 128, 512), bf16),) * 2
        + spread_shapes(128, 768)
        + (jax.ShapeDtypeStruct((2, 128, width), bf16),) * 2
        + (jax.ShapeDtypeStruct((128, width), bf16),) * 2
        + (jax.ShapeDtypeStruct((3, 128, width), bf16),) * 2,
        [vmem()] * 12 + [hbm()] * 7, [vmem()] * 4 + [hbm()] * 16,
        gather_scratch(shard, width)
        + [pltpu.VMEM((2, 512, 256), bf16), pltpu.VMEM((2, 4, 256, 256), bf16)]
        + spread_sems(1)
        + [
            pltpu.VMEM((2, 2, 512, 128), bf16),
            pltpu.VMEM((2, 2, 512, 128), bf16),
            pltpu.VMEM((1024, 384), bf16),
            pltpu.VMEM((2, 4, 256, 256), bf16),
            pltpu.VMEM((2, 4, 256, 128), bf16),
            pltpu.SemaphoreType.DMA((2, 2)),
            pltpu.SemaphoreType.DMA((2, 2)),
        ]
        + spread_sems(2)
        + [pltpu.VMEM((4, shard, width), bf16)]
        + scatter_bufs(shard, width) + scatter_sems()
        + [
            pltpu.VMEM((2, 3, shard, width), bf16),
            pltpu.VMEM((2, 3, shard, width), bf16),
            pltpu.VMEM((shard, width), f32),
            pltpu.SemaphoreType.DMA((2, 4)),
            pltpu.SemaphoreType.DMA((12,)),
            pltpu.SemaphoreType.DMA((12,)),
            pltpu.SemaphoreType.DMA(()),
            pltpu.VMEM((2, 1536, 128), f32),
        ],
        args, flops=10**10, sent=10**8,
    )


def leave_kernel(
    parts, hidden, gain, gmid, gains, qa_send, qa_keep, qb_send, qb_keep, oa_keep, ob_keep, oa_in, ob_in,
    grad_out, ga_out, query_out, key_out, value_out, output_out,
    mine, from_pt, from_up, from_dn, s0, s1, s2, s3, s4, s5,
    acc, over_wid, summed, over_rest, w_s, w_g, t_s, t_g,
    first_q, next_q, then_q, next_o, then_o, kv, n_s, n_g, k0, k1, k2, k3, m_s,
):
    me = spot()
    r, n, w = me
    own_parts = pltpu.make_async_copy(parts.at[r], mine, m_s)
    own_parts.start()
    partners = [(w != j, (r, n, jnp.int32(j))) for j in range(4)]
    partners += [
        ((r != a) | (n != b), (jnp.int32(a), jnp.int32(b), w)) for a in range(2) for b in range(4)
    ]
    greet(partners)
    kv_gather = Gather(kv, (k0, k1, k2, k3), me, 4, pair=False)
    x_side, y_side = over_x(r, n, w), over_y(r, n, w)
    q_hops = [
        push(qa_send, first_q.at[0], n_s.at[0], n_g.at[0], x_side),
        push(qb_send, first_q.at[1], n_s.at[1], n_g.at[1], y_side),
    ]
    q_later = [
        push(next_q.at[0], then_q.at[0], n_s.at[2], n_g.at[2], y_side),
        push(next_q.at[1], then_q.at[1], n_s.at[3], n_g.at[3], x_side),
    ]
    o_hops = [
        push(next_o.at[0], then_o.at[0], n_s.at[4], n_g.at[4], y_side),
        push(next_o.at[1], then_o.at[1], n_s.at[5], n_g.at[5], x_side),
    ]
    for hop in q_hops:
        hop.start()
    scatter = Scatter(
        mine, parts.at[1 - r], (from_pt, from_up, from_dn), (s0, s1, s2, s3, s4, s5), me, 4
    )
    for i in range(4):
        scatter.pair(scatter.order(i)).start()

    def wid_copy(j, slot):
        return pltpu.make_async_remote_copy(
            gains, over_wid.at[slot], w_s.at[j], w_g.at[slot],
            device_id=(r, n, jnp.int32(j)), device_id_type=MESH,
        )

    def rest_copy(a, b, slot):
        return pltpu.make_async_remote_copy(
            summed, over_rest.at[slot], t_s.at[a * 4 + b], t_g.at[slot],
            device_id=(jnp.int32(a), jnp.int32(b), w), device_id_type=MESH,
        )

    for j in range(4):
        @pl.when(w != j)
        def _():
            wid_copy(j, w).start()

    own_parts.wait()
    scatter.advance((0, 1, 2), ())
    for j, (keep, came) in enumerate(((oa_keep, oa_in), (ob_keep, ob_in))):
        next_o[j] = (keep[1].astype(f32) + came[1].astype(f32)).astype(bf16)
        o_hops[j].start()
    summed[...] = gains[...]
    for j in range(4):
        @pl.when(w != j)
        def _():
            wid_copy(j, j).wait_recv()
            summed[...] += over_wid[j]

    for a in range(2):
        for b in range(4):
            @pl.when((r != a) | (n != b))
            def _():
                rest_copy(a, b, r * 4 + n).start()

    for j, keep in enumerate((qa_keep, qb_keep)):
        q_hops[j].wait_recv()
        next_q[j] = (keep[1].astype(f32) + first_q[j, 1].astype(f32)).astype(bf16)
        q_later[j].start()
    scatter.advance((), (0,))
    for j, keep in enumerate((qa_keep, qb_keep)):
        q_later[j].wait_recv()
        total = keep[0].astype(f32) + first_q[j, 0].astype(f32) + then_q[j].astype(f32)
        query_out[j * 128 : j * 128 + 128, :] = total[:, 0:512]
        kv[0, w, j * 128 : j * 128 + 128, :] = total[:, 512:768].astype(bf16)
    kv_gather.own()
    scatter.advance((3,), (1, 2))
    kv_gather.advance((), (1,))
    scatter.advance((), (3,))
    kv_gather.advance((), (2,))
    for j, (keep, came) in enumerate(((oa_keep, oa_in), (ob_keep, ob_in))):
        o_hops[j].wait_recv()
        output_out[:, j * 128 : j * 128 + 128] = (
            keep[0].astype(f32) + came[0].astype(f32) + then_o[j].astype(f32)
        ).T
    mine_block = r * 4 + n
    ga_out[0:1] = summed[pl.ds(mine_block, 1), :]
    ga_out[1:2] = summed[pl.ds(mine_block + 8, 1), :]
    for a in range(2):
        for b in range(4):
            @pl.when((r != a) | (n != b))
            def _():
                slot = a * 4 + b
                rest_copy(a, b, slot).wait_recv()
                ga_out[0:1] += over_rest[slot, pl.ds(mine_block, 1), :]
                ga_out[1:2] += over_rest[slot, pl.ds(mine_block + 8, 1), :]

    scatter.total(acc)

    def last(rows):
        grad = norm_back(hidden[rows, :].astype(f32), gain[...], acc[rows, :])
        grad_out[rows, :] = (grad + gmid[rows, :]).astype(bf16)

    each_rows(hidden.shape[0], 16, last)
    kv_gather.advance((1, 2, 3), (3,))
    lane = lax.broadcasted_iota(jnp.int32, (256, 128), 1)
    for j in range(4):
        even, odd = kv[0, j, :, 0:128].astype(f32), kv[0, j, :, 128:256].astype(f32)
        here = slice(j * 128, j * 128 + 128)
        key_out[:, here] = jnp.where(lane < 64, even, pltpu.roll(odd, 64, 1))
        value_out[:, here] = jnp.where(lane < 64, pltpu.roll(even, 64, 1), odd)
    scatter.sent()
    kv_gather.sent()
    for hop in q_hops + q_later + o_hops:
        hop.wait_send()
    for j in range(4):
        @pl.when(w != j)
        def _():
            wid_copy(j, w).wait_send()

    for a in range(2):
        for b in range(4):
            @pl.when((r != a) | (n != b))
            def _():
                rest_copy(a, b, r * 4 + n).wait_send()


def leave(*args):
    shard, width = 128, 2048
    grad = jax.ShapeDtypeStruct((256, 512), f32)
    return comm_call(
        leave_kernel, "leave", 7,
        (jax.ShapeDtypeStruct((shard, width), bf16), jax.ShapeDtypeStruct((8, 256), f32))
        + (grad,) * 3
        + (jax.ShapeDtypeStruct((512, 256), f32),),
        [hbm()] + [vmem()] * 12, [vmem()] * 6,
        [pltpu.VMEM((4, shard, width), bf16)]
        + scatter_bufs(shard, width) + scatter_sems()
        + [
            pltpu.VMEM((shard, width), f32),
            pltpu.VMEM((4, 16, 256), f32),
            pltpu.VMEM((16, 256), f32),
            pltpu.VMEM((8, 16, 256), f32),
            pltpu.SemaphoreType.DMA((4,)),
            pltpu.SemaphoreType.DMA((4,)),
            pltpu.SemaphoreType.DMA((8,)),
            pltpu.SemaphoreType.DMA((8,)),
            pltpu.VMEM((2, 2, 128, 768), bf16),
            pltpu.VMEM((2, 128, 768), bf16),
            pltpu.VMEM((2, 128, 768), bf16),
            pltpu.VMEM((2, 128, 512), bf16),
            pltpu.VMEM((2, 128, 512), bf16),
            pltpu.VMEM((1, 4, 256, 256), bf16),
            pltpu.SemaphoreType.DMA((6,)),
            pltpu.SemaphoreType.DMA((6,)),
        ]
        + gather_sems()
        + [pltpu.SemaphoreType.DMA(())],
        args, flops=10**10, sent=10**8,
    )


def local_fast(
    hidden_in, doc_lengths, w_query, w_key, w_value, w_output, w_gate, w_up, w_down,
    gain_attn, gain_ffn, grad_out,
):
    r, n, w = spot()
    hidden, grad_top = hidden_in[0], grad_out[0]
    gain_a, gain_f = gain_attn[None], gain_ffn[None]
    def half(weight, axis):
        size = weight.shape[axis] // 2
        return lax.dynamic_slice_in_dim(weight, r * size, size, axis)

    head = (w * 2 + r) * HD
    kv_pack = jnp.concatenate(
        [lax.dynamic_slice_in_dim(w_key, head, HD, 1), lax.dynamic_slice_in_dim(w_value, head, HD, 1)],
        axis=1,
    )
    out_half = half(w_output, 0)
    p1_shard = jnp.concatenate(
        [half(w_query, 1), kv_pack, jnp.concatenate([out_half[:, :256], out_half[:, 256:]], axis=0)],
        axis=1,
    )
    down_half = half(w_down, 0)
    down_own = jnp.concatenate([down_half[:512], down_half[512:]], axis=1)

    token_ids = n * 512 + jnp.arange(512, dtype=jnp.int32)
    doc_start, places = doc_layout(doc_lengths[0], token_ids)
    angles = places.astype(f32)[:, None] * inverse_freq()[None, :]
    cosine, sine = jnp.cos(angles), jnp.sin(angles)
    start_here = (doc_start - (n - 2) * 512).astype(f32)
    tab = jnp.concatenate(
        [cosine] * 4 + [-sine, sine] * 2 + [jnp.broadcast_to(start_here[:, None], (512, 128))],
        axis=1,
    )

    q, rows, tabs, p1, down_a, kv, tops = enter(
        hidden, gain_a, tab, grad_top, p1_shard, down_own
    )
    rows2 = rows.reshape(1024, 2048)
    kv_flat = kv.reshape(2, 1536, 128)
    att, lse, mid, ffn_rows, gate_all, up_all, down_b = middle_stage(
        q, kv_flat, tabs, p1, hidden, gain_f, w_gate, w_up, down_own
    )
    parts, total, gain_f_part, a_send, a_keep, b_send, b_keep, ra_dg, rb_dg = ffn_stage(
        ffn_rows.reshape(1024, 2048), tops, grad_top,
        w_gate, gate_all, w_up, up_all, down_own, down_a, down_b, gain_f,
    )
    (
        gmid, dparts, gain_a_part, hidden_out, _, oa_keep, _, ob_keep, oa_came, ob_came,
        qa_send, qa_keep, qb_send, qb_keep, ra_u, rb_u, ra_g, rb_g, a_last, b_last,
    ) = back(
        total, mid, grad_top, gain_f, p1, att, q, kv_flat, lse, rows2, tabs, gain_a,
        parts, a_send, b_send, a_keep, b_keep, ra_dg, rb_dg,
    )
    gains = jnp.concatenate(
        [gain_f_part.sum(axis=0).reshape(8, 256), gain_a_part.sum(axis=0).reshape(8, 256)], axis=0
    )
    grad_in, gain_sums, grad_query, grad_key, grad_value, output_sum = leave(
        dparts, hidden, gain_a, gmid, gains,
        qa_send, qa_keep, qb_send, qb_keep, oa_keep, ob_keep, oa_came, ob_came,
    )

    def joined(which):
        def half_rows(keep, came, last):
            return keep[0, which].astype(f32) + came.astype(f32) + last.astype(f32)

        a_came, b_came = (
            (ra_g, rb_g), (ra_u[0], rb_u[0]), (ra_dg[0, 0], rb_dg[0, 0])
        )[which]
        return jnp.concatenate(
            [half_rows(a_keep, a_came, a_last[which]), half_rows(b_keep, b_came, b_last[which])], axis=0
        )

    return (
        hidden_out[None],
        grad_in[None],
        grad_query,
        grad_key,
        grad_value,
        output_sum,
        joined(0),
        joined(1),
        joined(2).T,
        gain_sums[1],
        gain_sums[0],
    )


def solution(mesh):
    in_specs = (
        P("row", ("nar", "wid"), None),
        P("row", None),
        P("nar", "wid"),
        P("nar", None),
        P("nar", None),
        P("wid", "nar"),
        P("nar", "wid"),
        P("nar", "wid"),
        P("wid", "nar"),
        P(),
        P(),
        P("row", ("nar", "wid"), None),
    )
    out_specs = (
        P("row", ("nar", "wid"), None),
        P("row", ("nar", "wid"), None),
        P(("row", "nar"), "wid"),
        P(("row", "nar"), None),
        P(("row", "nar"), None),
        P("wid", ("row", "nar")),
        P(("row", "nar"), "wid"),
        P(("row", "nar"), "wid"),
        P("wid", ("row", "nar")),
        P(("row", "nar")),
        P(("row", "nar")),
    )
    sizes = dict(mesh.shape)
    fits = sizes == {"row": 2, "nar": 4, "wid": 4}

    def body(*args):
        small = args[0].shape == (1, 128, 2048)
        return (local_fast if fits and small else local)(*args)

    return jax.shard_map(body, mesh=mesh, in_specs=in_specs, out_specs=out_specs, check_vma=False)
```

```python
import math

import jax
import jax.numpy as jnp
from jax import lax
from jax.experimental import pallas as pl
from jax.experimental.pallas import tpu as pltpu
from jax.sharding import PartitionSpec as P

H = 32
KV = 8
HD = 64


norm_eps = 1e-05
masked_score = -1e30


def inverse_freq():
    listed = []
    for pair_index in range(HD // 2):
        base_freq = 500000.0 ** (-2.0 * pair_index / HD)
        wavelength = 2.0 * math.pi / base_freq
        smoothing = (8192.0 / wavelength - 1.0) / 3.0
        blended = (1.0 - smoothing) * base_freq / 32.0 + smoothing * base_freq
        if wavelength < 2048.0:
            listed.append(base_freq)
        elif wavelength > 8192.0:
            listed.append(base_freq / 32.0)
        else:
            listed.append(blended)
    return jnp.asarray(listed, dtype=jnp.float32)


def rotate(values, cosine_table, sine_table):
    half_dim = HD // 2
    first_half = values[..., :half_dim]
    second_half = values[..., half_dim:]
    return jnp.concatenate(
        [
            first_half * cosine_table - second_half * sine_table,
            second_half * cosine_table + first_half * sine_table,
        ],
        axis=-1,
    )


def rotate_back(grads_in, cosine_table, sine_table):
    half_dim = HD // 2
    first_half = grads_in[..., :half_dim]
    second_half = grads_in[..., half_dim:]
    return jnp.concatenate(
        [
            first_half * cosine_table + second_half * sine_table,
            second_half * cosine_table - first_half * sine_table,
        ],
        axis=-1,
    )


def doc_layout(lengths_row, token_ids):
    ends_at = jnp.cumsum(lengths_row, dtype=jnp.int32)
    starts_at = ends_at - lengths_row
    inside = (token_ids[:, None] >= starts_at[None, :]) & (token_ids[:, None] < ends_at[None, :])
    doc_start = jnp.sum(jnp.where(inside, starts_at[None, :], 0), axis=1, dtype=jnp.int32)
    return (doc_start, token_ids - doc_start)


def norm_forward(values, gain_vector):
    root_inv = lax.rsqrt(jnp.mean(values * values, axis=-1, keepdims=True) + norm_eps)
    return (root_inv, (values * root_inv * gain_vector).astype(jnp.bfloat16))


def norm_backward(values, root_inv, gain_vector, grad_normed):
    weighted = grad_normed * gain_vector
    inner_sum = jnp.mean(weighted * values, axis=-1, keepdims=True)
    grad_values = root_inv * weighted - values * (root_inv * root_inv * root_inv) * inner_sum
    gain_term = jnp.sum(grad_normed * values * root_inv, axis=0)
    return (grad_values, gain_term)


def contract_last(left_side, right_side):
    return lax.dot_general(
        left_side, right_side, (((1,), (1,)), ((), ())), preferred_element_type=jnp.float32
    )


def contract_first(left_side, right_side):
    return lax.dot_general(
        left_side, right_side, (((0,), (0,)), ((), ())), preferred_element_type=jnp.float32
    )


def local(
    hidden_in,
    doc_lengths,
    w_query,
    w_key,
    w_value,
    w_output,
    w_gate,
    w_up,
    w_down,
    gain_attn,
    gain_ffn,
    grad_out,
):
    wid_count = lax.axis_size("wid")
    nar_count = lax.axis_size("nar")
    wid_index = lax.axis_index("wid")
    nar_index = lax.axis_index("nar")
    local_tokens = hidden_in.shape[1]
    block_tokens = local_tokens * wid_count
    seq_length = block_tokens * nar_count
    query_heads = w_query.shape[1] // HD
    group_size = H // KV
    kv_local = max(query_heads // group_size, 1)
    heads_per_kv = query_heads // kv_local
    kv_first = wid_index * query_heads // group_size
    query_block = min(512, block_tokens)
    block_count = block_tokens // query_block
    item_count = block_count * query_heads
    attn_scale = HD ** (-0.5)
    query_full, key_full, value_full, output_full, gate_full, up_full, down_full = (
        lax.all_gather(w_query, "nar", axis=0, tiled=True),
        lax.all_gather(w_key, "nar", axis=0, tiled=True),
        lax.all_gather(w_value, "nar", axis=0, tiled=True),
        lax.all_gather(w_output, "nar", axis=1, tiled=True),
        lax.all_gather(w_gate, "nar", axis=0, tiled=True),
        lax.all_gather(w_up, "nar", axis=0, tiled=True),
        lax.all_gather(w_down, "nar", axis=1, tiled=True),
    )
    key_local = lax.dynamic_slice_in_dim(key_full, kv_first * HD, kv_local * HD, 1)
    value_local = lax.dynamic_slice_in_dim(value_full, kv_first * HD, kv_local * HD, 1)
    token_ids = nar_index * block_tokens + jnp.arange(block_tokens, dtype=jnp.int32)
    doc_start, places = doc_layout(doc_lengths[0], token_ids)
    angles = places.astype(jnp.float32)[:, None] * inverse_freq()[None, :]
    cosine_table = jnp.cos(angles)[:, None, :]
    sine_table = jnp.sin(angles)[:, None, :]
    key_ids = jnp.arange(seq_length, dtype=jnp.int32)
    residual = hidden_in[0].astype(jnp.float32)
    root_attn, normed_attn = norm_forward(residual, gain_attn)
    normed_rows = lax.all_gather(normed_attn, "wid", axis=0, tiled=True)
    query_pre = jnp.dot(normed_rows, query_full, preferred_element_type=jnp.float32)
    key_pre = jnp.dot(normed_rows, key_local, preferred_element_type=jnp.float32)
    value_rows = jnp.dot(normed_rows, value_local, preferred_element_type=jnp.float32).astype(
        jnp.bfloat16
    )
    query_rot = (
        rotate(query_pre.reshape(block_tokens, query_heads, HD), cosine_table, sine_table)
        .astype(jnp.bfloat16)
        .reshape(block_tokens, query_heads * HD)
    )
    key_rot = (
        rotate(key_pre.reshape(block_tokens, kv_local, HD), cosine_table, sine_table)
        .astype(jnp.bfloat16)
        .reshape(block_tokens, kv_local * HD)
    )
    key_seq, value_seq = (
        lax.all_gather(key_rot, "nar", axis=0, tiled=True),
        lax.all_gather(value_rows, "nar", axis=0, tiled=True),
    )

    def item_inputs(item_index):
        block_index = item_index // query_heads
        head_index = item_index % query_heads
        kv_index = head_index // heads_per_kv
        row_first = block_index * query_block
        query_part = lax.dynamic_slice(query_rot, (row_first, head_index * HD), (query_block, HD))
        key_head = lax.dynamic_slice_in_dim(key_seq, kv_index * HD, HD, 1)
        value_head = lax.dynamic_slice_in_dim(value_seq, kv_index * HD, HD, 1)
        query_ids = lax.dynamic_slice_in_dim(token_ids, row_first, query_block, 0)
        query_starts = lax.dynamic_slice_in_dim(doc_start, row_first, query_block, 0)
        allowed = (key_ids[None, :] <= query_ids[:, None]) & (
            key_ids[None, :] >= query_starts[:, None]
        )
        scores = contract_last(query_part, key_head) * attn_scale
        return (
            row_first,
            head_index,
            kv_index,
            query_part,
            key_head,
            value_head,
            jnp.where(allowed, scores, masked_score),
        )

    def attend(item_index):
        row_first, head_index, kv_index, query_part, key_head, value_head, scores = item_inputs(
            item_index
        )
        row_max = jnp.max(scores, axis=1, keepdims=True)
        exp_scores = jnp.exp(scores - row_max)
        row_total = jnp.sum(exp_scores, axis=1, keepdims=True)
        probability = (exp_scores / row_total).astype(jnp.bfloat16)
        attended = jnp.dot(probability, value_head, preferred_element_type=jnp.float32)
        return (attended, (row_max + jnp.log(row_total))[:, 0])

    attended_items, logsum_items = lax.map(attend, jnp.arange(item_count, dtype=jnp.int32))
    attended_rows = (
        attended_items.reshape(block_count, query_heads, query_block, HD)
        .transpose(0, 2, 1, 3)
        .reshape(block_tokens, query_heads * HD)
        .astype(jnp.bfloat16)
    )
    rows_here = attended_rows
    branch_attn = lax.psum_scatter(
        jnp.dot(rows_here, output_full, preferred_element_type=jnp.float32),
        "wid",
        scatter_dimension=0,
        tiled=True,
    )
    middle = residual + branch_attn
    root_ffn, normed_ffn = norm_forward(middle, gain_ffn)
    ffn_rows = lax.all_gather(normed_ffn, "wid", axis=0, tiled=True)
    gate_proj = jnp.dot(ffn_rows, gate_full, preferred_element_type=jnp.float32)
    up_proj = jnp.dot(ffn_rows, up_full, preferred_element_type=jnp.float32)
    gate_sigmoid = jax.nn.sigmoid(gate_proj)
    gate_silu = gate_proj * gate_sigmoid
    activated = (gate_silu * up_proj).astype(jnp.bfloat16)
    rows_here = activated
    branch_ffn = lax.psum_scatter(
        jnp.dot(rows_here, down_full, preferred_element_type=jnp.float32).astype(jnp.bfloat16),
        "wid",
        scatter_dimension=0,
        tiled=True,
    ).astype(jnp.float32)
    hidden_out = (middle + branch_ffn).astype(jnp.bfloat16)[None]
    grad_top = grad_out[0]
    grad_rows = lax.all_gather(grad_top, "wid", axis=0, tiled=True)
    grad_activated = contract_last(grad_rows, down_full)
    down_weight_grad = contract_first(activated, grad_rows)
    silu_slope = gate_sigmoid * (1.0 + gate_proj * (1.0 - gate_sigmoid))
    grad_gate_b = (grad_activated * up_proj * silu_slope).astype(jnp.bfloat16)
    grad_up_b = (grad_activated * gate_silu).astype(jnp.bfloat16)
    gate_weight_grad = contract_first(ffn_rows, grad_gate_b)
    up_weight_grad = contract_first(ffn_rows, grad_up_b)
    grad_normed_ffn = lax.psum_scatter(
        contract_last(grad_gate_b, gate_full) + contract_last(grad_up_b, up_full),
        "wid",
        scatter_dimension=0,
        tiled=True,
    )
    grad_middle, gain_ffn_term = norm_backward(middle, root_ffn, gain_ffn, grad_normed_ffn)
    grad_middle = grad_middle + grad_top.astype(jnp.float32)
    grad_branch = grad_middle.astype(jnp.bfloat16)
    branch_rows = lax.all_gather(grad_branch, "wid", axis=0, tiled=True)
    grad_attended = contract_last(branch_rows, output_full).astype(jnp.bfloat16)
    output_weight_grad = contract_first(attended_rows, branch_rows)

    def attend_back(carried, item_index):
        key_grad, value_grad = carried
        row_first, head_index, kv_index, query_part, key_head, value_head, scores = item_inputs(
            item_index
        )
        logsum = lax.dynamic_index_in_dim(logsum_items, item_index, 0, keepdims=False)
        probability = jnp.exp(scores - logsum[:, None])
        grad_part = lax.dynamic_slice(
            grad_attended, (row_first, head_index * HD), (query_block, HD)
        )
        grad_prob = contract_last(grad_part, value_head)
        inner_sum = jnp.sum(probability * grad_prob, axis=1, keepdims=True)
        grad_scores = (probability * (grad_prob - inner_sum)).astype(jnp.bfloat16)
        query_grad = jnp.dot(grad_scores, key_head, preferred_element_type=jnp.float32) * attn_scale
        key_part = contract_first(grad_scores, query_part) * attn_scale
        value_part = contract_first(probability.astype(jnp.bfloat16), grad_part)
        key_old = lax.dynamic_slice_in_dim(key_grad, kv_index * HD, HD, 1)
        key_grad = lax.dynamic_update_slice_in_dim(key_grad, key_old + key_part, kv_index * HD, 1)
        value_old = lax.dynamic_slice_in_dim(value_grad, kv_index * HD, HD, 1)
        value_grad = lax.dynamic_update_slice_in_dim(
            value_grad, value_old + value_part, kv_index * HD, 1
        )
        return ((key_grad, value_grad), query_grad)

    zero_grads = jnp.zeros((seq_length, kv_local * HD), jnp.float32)
    (key_grad_seq, value_grad_seq), query_grad_items = lax.scan(
        attend_back, (zero_grads, zero_grads), jnp.arange(item_count, dtype=jnp.int32)
    )
    key_grad_block, value_grad_block = (
        lax.psum_scatter(
            key_grad_seq.astype(jnp.bfloat16), "nar", scatter_dimension=0, tiled=True
        ).astype(jnp.float32),
        lax.psum_scatter(
            value_grad_seq.astype(jnp.bfloat16), "nar", scatter_dimension=0, tiled=True
        ).astype(jnp.float32),
    )
    query_grad_rows = (
        query_grad_items.reshape(block_count, query_heads, query_block, HD)
        .transpose(0, 2, 1, 3)
        .reshape(block_tokens, query_heads, HD)
    )
    query_grad_b = (
        rotate_back(query_grad_rows, cosine_table, sine_table)
        .astype(jnp.bfloat16)
        .reshape(block_tokens, query_heads * HD)
    )
    key_grad_b = (
        rotate_back(key_grad_block.reshape(block_tokens, kv_local, HD), cosine_table, sine_table)
        .astype(jnp.bfloat16)
        .reshape(block_tokens, kv_local * HD)
    )
    value_grad_b = value_grad_block.astype(jnp.bfloat16)
    query_weight_grad = contract_first(normed_rows, query_grad_b)
    key_weight_grad = contract_first(normed_rows, key_grad_b)
    value_weight_grad = contract_first(normed_rows, value_grad_b)
    grad_normed_attn = lax.psum_scatter(
        (
            contract_last(query_grad_b, query_full)
            + contract_last(key_grad_b, key_local)
            + contract_last(value_grad_b, value_local)
        ).astype(jnp.bfloat16),
        "wid",
        scatter_dimension=0,
        tiled=True,
    ).astype(jnp.float32)
    grad_residual, gain_attn_term = norm_backward(residual, root_attn, gain_attn, grad_normed_attn)
    grad_in = (grad_residual + grad_middle).astype(jnp.bfloat16)[None]
    summed = (
        lax.psum_scatter(
            query_weight_grad.astype(jnp.bfloat16), ("row", "nar"), scatter_dimension=0, tiled=True
        ).astype(jnp.float32),
        lax.psum_scatter(
            key_weight_grad.astype(jnp.bfloat16), ("row", "nar"), scatter_dimension=0, tiled=True
        ).astype(jnp.float32),
        lax.psum_scatter(
            value_weight_grad.astype(jnp.bfloat16), ("row", "nar"), scatter_dimension=0, tiled=True
        ).astype(jnp.float32),
        lax.psum_scatter(
            output_weight_grad.astype(jnp.bfloat16), ("row", "nar"), scatter_dimension=1, tiled=True
        ).astype(jnp.float32),
        lax.psum_scatter(
            gate_weight_grad.astype(jnp.bfloat16), ("row", "nar"), scatter_dimension=0, tiled=True
        ).astype(jnp.float32),
        lax.psum_scatter(
            up_weight_grad.astype(jnp.bfloat16), ("row", "nar"), scatter_dimension=0, tiled=True
        ).astype(jnp.float32),
        lax.psum_scatter(
            down_weight_grad.astype(jnp.bfloat16), ("row", "nar"), scatter_dimension=1, tiled=True
        ).astype(jnp.float32),
        lax.psum_scatter(
            gain_attn_term.astype(jnp.bfloat16), ("row", "nar"), scatter_dimension=0, tiled=True
        ).astype(jnp.float32),
        lax.psum_scatter(
            gain_ffn_term.astype(jnp.bfloat16), ("row", "nar"), scatter_dimension=0, tiled=True
        ).astype(jnp.float32),
    )
    (
        grad_query,
        key_sum,
        value_sum,
        grad_output,
        grad_gate,
        grad_up,
        grad_down,
        gain_attn_sum,
        gain_ffn_sum,
    ) = summed
    key_all, value_all, gain_attn_all, gain_ffn_all = (
        lax.all_gather(key_sum.astype(jnp.bfloat16), "wid", axis=1, tiled=True).astype(
            key_sum.dtype
        ),
        lax.all_gather(value_sum.astype(jnp.bfloat16), "wid", axis=1, tiled=True).astype(
            value_sum.dtype
        ),
        lax.all_gather(gain_attn_sum.astype(jnp.bfloat16), "wid", axis=0, tiled=True).astype(
            gain_attn_sum.dtype
        ),
        lax.all_gather(gain_ffn_sum.astype(jnp.bfloat16), "wid", axis=0, tiled=True).astype(
            gain_ffn_sum.dtype
        ),
    )
    shard_rows = key_sum.shape[0]
    repeats = wid_count * kv_local // KV
    grad_key = key_all.reshape(shard_rows, KV, repeats, HD).sum(axis=2).reshape(shard_rows, KV * HD)
    grad_value = (
        value_all.reshape(shard_rows, KV, repeats, HD).sum(axis=2).reshape(shard_rows, KV * HD)
    )
    grad_gain_attn = gain_attn_all.reshape(wid_count, shard_rows).sum(axis=0)
    grad_gain_ffn = gain_ffn_all.reshape(wid_count, shard_rows).sum(axis=0)
    return (
        hidden_out,
        grad_in,
        grad_query,
        grad_key,
        grad_value,
        grad_output,
        grad_gate,
        grad_up,
        grad_down,
        grad_gain_attn,
        grad_gain_ffn,
    )


MESH = pl.DeviceIdType.MESH
bf16 = jnp.bfloat16
f32 = jnp.float32
VMEM_LIMIT = 60 * 2**20


def spot():
    return lax.axis_index("row"), lax.axis_index("nar"), lax.axis_index("wid")


def greet(partners):
    barrier = pltpu.get_barrier_semaphore()
    total = 0
    for there, device in partners:
        @pl.when(there)
        def _():
            pl.semaphore_signal(barrier, inc=1, device_id=device, device_id_type=MESH)

        total = total + there.astype(jnp.int32)
    pl.semaphore_wait(barrier, total)


def line_partners(r, n, w, wid_count):
    return [
        (w < wid_count - 1, (r, n, jnp.minimum(w + 1, wid_count - 1))),
        (w > 0, (r, n, jnp.maximum(w - 1, 0))),
        (w >= 0, (1 - r, n, w)),
    ]


def each_rows(count, step, body):
    def run(i, carry):
        body(pl.ds(pl.multiple_of(i * step, step), step))
        return carry

    lax.fori_loop(0, count // step, run, 0)


def square_partners(r, n, w):
    return [(n >= 0, over_x(r, n, w)), (n >= 0, over_y(r, n, w))]


def over_x(r, n, w):
    return (r, n + 1 - 2 * (n % 2), w)


def over_y(r, n, w):
    return (r, (n + 2) % 4, w)


def push(source, target, s_s, s_g, device):
    return pltpu.make_async_remote_copy(
        source, target, s_s, s_g, device_id=device, device_id_type=MESH
    )


class Square:
    def __init__(self, shard, full, sems, me):
        self.shard, self.full = shard, full
        self.sent, self.got = sems
        r, n, w = me
        self.n, self.x, self.y = n, n + 1 - 2 * (n % 2), (n + 2) % 4
        self.by_x, self.by_y = over_x(*me), over_y(*me)
        size = shard.shape[0] // 2
        self.upper, self.lower = pl.ds(0, size), pl.ds(size, size)

    def first(self, k, place):
        return push(
            self.shard, self.full.at[place], self.sent.at[k], self.got.at[k],
            (self.by_x, self.by_y)[k],
        )

    def second(self, k, place):
        part = self.full.at[place, (self.upper, self.lower)[k]]
        return push(
            part, part, self.sent.at[2 + k], self.got.at[2 + k], (self.by_y, self.by_x)[k]
        )

    def start(self):
        self.first(0, self.n).start()
        self.first(1, self.n).start()

    def turn(self):
        self.first(0, self.x).wait_recv()
        self.second(0, self.x).start()
        self.first(1, self.y).wait_recv()
        self.second(1, self.y).start()

    def finish(self):
        for k in range(2):
            self.second(k, 3 - self.n).wait_recv()
            self.first(k, self.n).wait_send()
            self.second(k, (self.x, self.y)[k]).wait_send()


def square_sems():
    return [pltpu.SemaphoreType.DMA((4,))] * 2


def fetch(own, full, target, sems, n):
    copies = [pltpu.make_async_copy(own, target.at[n], sems.at[0])]
    for k, place in enumerate((n + 1 - 2 * (n % 2), (n + 2) % 4, 3 - n)):
        copies.append(pltpu.make_async_copy(full.at[place], target.at[place], sems.at[1 + k]))
    return copies


class Gather:
    def __init__(self, buf, sems, me, wid_count, rows=slice(None), pair=True):
        self.rows, self.both = rows, pair
        self.buf, (self.up_s, self.dn_s, self.pt_s, self.got) = buf, sems
        self.r, self.n, self.w = me
        self.last = wid_count - 1
        self.up = (self.r, self.n, jnp.minimum(self.w + 1, self.last))
        self.dn = (self.r, self.n, jnp.maximum(self.w - 1, 0))
        self.pt = (1 - self.r, self.n, self.w)

    def copy(self, j, sem, device, row=None):
        row = (self.r if self.both else 0) if row is None else row
        return pltpu.make_async_remote_copy(
            self.buf.at[row, j, self.rows],
            self.buf.at[row, j, self.rows],
            sem.at[j],
            self.got.at[row, j],
            device_id=device,
            device_id_type=MESH,
        )

    def pass_on(self, j, go_up, go_dn):
        if go_up:
            @pl.when(self.w < self.last)
            def _():
                self.copy(j, self.up_s, self.up).start()

        if go_dn:
            @pl.when(self.w > 0)
            def _():
                self.copy(j, self.dn_s, self.dn).start()

        if self.both:
            self.copy(j, self.pt_s, self.pt).start()

    def own(self):
        self.pass_on(self.w, True, True)

    def arrive(self, row, j):
        self.copy(j, self.pt_s, self.pt, row).wait_recv()

    def step(self, k):
        below, above = self.w - k, self.w + k

        @pl.when(below >= 0)
        def _():
            self.arrive(None, below)
            self.pass_on(below, True, False)

        @pl.when(above <= self.last)
        def _():
            self.arrive(None, above)
            self.pass_on(above, False, True)

    def advance(self, edge_steps, inner_steps):
        at_end = (self.w == 0) | (self.w == self.last)
        for ends, steps in ((True, edge_steps), (False, inner_steps)):
            if steps:
                @pl.when(at_end if ends else jnp.logical_not(at_end))
                def _():
                    for k in steps:
                        self.step(k)

    def rest(self):
        for j in range(self.last + 1):
            self.arrive(1 - self.r, j)

    def sent(self):
        for j in range(self.last + 1):
            @pl.when((j <= self.w) & (self.w < self.last))
            def _():
                self.copy(j, self.up_s, self.up).wait_send()

            @pl.when((j >= self.w) & (self.w > 0))
            def _():
                self.copy(j, self.dn_s, self.dn).wait_send()

            if self.both:
                self.copy(j, self.pt_s, self.pt).wait_send()


def gather_scratch(shard, width):
    return [pltpu.VMEM((2, 4, shard, width), bf16)] + gather_sems()


def gather_sems():
    return [pltpu.SemaphoreType.DMA((4,))] * 3 + [pltpu.SemaphoreType.DMA((2, 4))]


class Scatter:
    def __init__(self, mine, theirs, bufs, sems, me, wid_count, first=0, count=None):
        self.mine, self.theirs = mine, theirs
        self.from_pt, self.from_up, self.from_dn = bufs
        self.pt_s, self.pt_g, self.up_s, self.up_g, self.dn_s, self.dn_g = sems
        self.r, self.n, self.w = me
        self.first, self.count = first, mine.shape[1] if count is None else count
        self.rows = pl.ds(first, self.count)
        self.last = wid_count - 1
        self.up = (self.r, self.n, jnp.minimum(self.w + 1, self.last))
        self.dn = (self.r, self.n, jnp.maximum(self.w - 1, 0))
        self.pt = (1 - self.r, self.n, self.w)

    def order(self, i):
        low = jnp.where(i == 0, 3, jnp.where(i == 1, 0, jnp.where(i == 2, 2, 1)))
        return jnp.where(self.w < 2, low, 3 - low)

    def send(self, source, target, sent, got, s, device):
        return pltpu.make_async_remote_copy(
            source.at[s, self.rows], target.at[s, self.rows], sent.at[s], got.at[s],
            device_id=device, device_id_type=MESH,
        )

    def pair(self, s):
        return self.send(self.theirs, self.from_pt, self.pt_s, self.pt_g, s, self.pt)

    def climb(self, s):
        return self.send(self.mine, self.from_dn, self.up_s, self.up_g, s, self.up)

    def fall(self, s):
        return self.send(self.mine, self.from_up, self.dn_s, self.dn_g, s, self.dn)

    def each(self, body):
        def run(i, carry):
            body(pl.ds(pl.multiple_of(self.first + i * 16, 16), 16))
            return carry

        lax.fori_loop(0, self.count // 16, run, 0)

    def add(self, s, others):
        def body(rows):
            total = self.mine[s, rows, :].astype(f32)
            for other in others:
                total = total + other[s, rows, :].astype(f32)
            self.mine[s, rows, :] = total.astype(bf16)

        self.each(body)

    def step(self, s):
        self.pair(s).wait_recv()

        @pl.when((s > self.w) & (self.w > 0))
        def _():
            self.climb(s).wait_recv()
            self.add(s, (self.from_pt, self.from_dn))

        @pl.when((s < self.w) & (self.w < self.last))
        def _():
            self.fall(s).wait_recv()
            self.add(s, (self.from_pt, self.from_up))

        @pl.when(((s > self.w) & (self.w == 0)) | ((s < self.w) & (self.w == self.last)))
        def _():
            self.add(s, (self.from_pt,))

        @pl.when(s > self.w)
        def _():
            self.climb(s).start()

        @pl.when(s < self.w)
        def _():
            self.fall(s).start()

    def advance(self, edge_steps, inner_steps):
        for ends, steps in ((True, edge_steps), (False, inner_steps)):
            at_end = (self.w == 0) | (self.w == self.last)

            def body(i, carry):
                self.step(self.order(i))
                return carry

            if steps:
                @pl.when(at_end if ends else jnp.logical_not(at_end))
                def _():
                    lax.fori_loop(steps[0], steps[-1] + 1, body, 0)

    def total(self, out):
        w = self.w

        def first(rows):
            out[rows, :] = self.mine[w, rows, :].astype(f32) + self.from_pt[w, rows, :].astype(f32)

        self.each(first)

        @pl.when(w > 0)
        def _():
            self.climb(w).wait_recv()

            def more(rows):
                out[rows, :] += self.from_dn[w, rows, :].astype(f32)

            self.each(more)

        @pl.when(w < self.last)
        def _():
            self.fall(w).wait_recv()

            def more(rows):
                out[rows, :] += self.from_up[w, rows, :].astype(f32)

            self.each(more)

    def sent(self):
        for s in range(self.last + 1):
            self.pair(s).wait_send()

            @pl.when(s > self.w)
            def _():
                self.climb(s).wait_send()

            @pl.when(s < self.w)
            def _():
                self.fall(s).wait_send()


def scatter_bufs(shard, width):
    return [pltpu.VMEM((4, shard, width), bf16)] * 3


def scatter_sems():
    return [pltpu.SemaphoreType.DMA((4,))] * 6


def vmem():
    return pl.BlockSpec(memory_space=pltpu.VMEM)


def hbm():
    return pl.BlockSpec(memory_space=pl.ANY)


def comm_call(kernel, name, cid, out_shape, in_specs, out_specs, scratch, args, flops=0, sent=0):
    return pl.pallas_call(
        kernel,
        out_shape=out_shape,
        in_specs=in_specs,
        out_specs=out_specs,
        scratch_shapes=scratch,
        compiler_params=pltpu.CompilerParams(
            collective_id=cid, has_side_effects=True, vmem_limit_bytes=VMEM_LIMIT
        ),
        cost_estimate=pl.CostEstimate(flops=flops, bytes_accessed=sent, transcendentals=0),
        name=name,
    )(*args)


def norm_rows(x, gain):
    root = lax.rsqrt(jnp.mean(x * x, axis=-1, keepdims=True) + norm_eps)
    return x * root * gain


def turn(x, cosine, sine):
    lane = lax.broadcasted_iota(jnp.int32, x.shape, 1)
    swapped = jnp.where(lane % 64 < 32, pltpu.roll(x, 96, 1), pltpu.roll(x, 32, 1))
    return x * cosine + swapped * sine


def nar_device(r, n, w, by):
    return (r, jnp.clip(n + by, 0, 3), w)


def enter_kernel(
    hidden, gain, tab, grad_top, p1_own, down_own,
    q_out, rows_out, tabs_out, p1_out, down_out, kv_out, tops_out,
    buf, up_s, dn_s, pt_s, got, tbuf, h0, h1, h2, h3, tabs, p1, kv,
    tab_s, tab_g, out_s, p1_s, p1_g, down_s, down_g, s_s, s_g,
):
    me = spot()
    r, n, w = me
    bring = pltpu.make_async_copy(p1_own, p1.at[n], out_s.at[0])
    bring.start()
    greet(
        line_partners(r, n, w, 4)
        + [
            (n >= 1, nar_device(r, n, w, -1)),
            (n >= 2, nar_device(r, n, w, -2)),
            (n <= 2, nar_device(r, n, w, 1)),
            (n <= 1, nar_device(r, n, w, 2)),
        ]
    )
    p1_square = Square(p1_own, p1, (p1_s, p1_g), me)
    down = Square(down_own.at[0:256], down_out, (down_s, down_g), me)
    p1_square.start()
    down.start()
    gather = Gather(buf, (up_s, dn_s, pt_s, got), me, 4)
    tops = Gather(tbuf, (h0, h1, h2, h3), me, 4)
    tab_copy = pltpu.make_async_remote_copy(
        tab, tabs.at[r], tab_s, tab_g, device_id=(1 - r, n, w), device_id_type=MESH
    )

    def body(rows):
        buf[r, w, rows, :] = norm_rows(hidden[rows, :].astype(f32), gain[...]).astype(bf16)

    each_rows(hidden.shape[0], 16, body)
    gather.own()
    tab_copy.start()

    def keep(rows):
        tabs[r, rows, :] = tab[rows, :]

    each_rows(tab.shape[0], 16, keep)

    def keep_top(rows):
        tbuf[r, w, rows, :] = grad_top[rows, :]

    each_rows(64, 16, keep_top)
    gather.step(1)
    p1_square.turn()
    gather.step(2)
    tops.own()
    down.turn()
    gather.step(3)
    gather.rest()
    tab_copy.wait_recv()
    p1_square.finish()
    bring.wait()
    outs = [
        pltpu.make_async_copy(buf, rows_out, out_s.at[1]),
        pltpu.make_async_copy(tabs, tabs_out, out_s.at[2]),
        pltpu.make_async_copy(p1, p1_out, out_s.at[3]),
    ]
    for out in outs:
        out.start()
    tops.step(1)

    def copy(row, slot, by):
        return pltpu.make_async_remote_copy(
            kv.at[row, 2], kv.at[row, slot], s_s.at[row, slot], s_g.at[row, slot],
            device_id=nar_device(r, n, w, by), device_id_type=MESH,
        )

    lane = lax.broadcasted_iota(jnp.int32, (256, 128), 1)
    weight = p1[:, :, 0:384].reshape(2048, 384)
    for row in range(2):
        def tile(i, carry):
            rows = pl.ds(pl.multiple_of(i * 256, 256), 256)
            cosine, sine = tabs[row, rows, 0:128], tabs[row, rows, 128:256]
            left = buf[row, pl.ds(i * 2, 2)].reshape(256, 2048)
            pre = jnp.dot(left, weight, preferred_element_type=f32)
            q_out[row, rows, 0:128] = turn(pre[:, 0:128], cosine, sine).astype(bf16)
            q_out[row, rows, 128:256] = turn(pre[:, 128:256], cosine, sine).astype(bf16)
            both = pre[:, 256:384]
            kv[row, 2, rows, :] = jnp.where(lane < 64, turn(both, cosine, sine), both).astype(bf16)
            return carry

        lax.fori_loop(0, 2, tile, 0)

        @pl.when(n <= 2)
        def _():
            copy(row, 1, 1).start()

        @pl.when(n <= 1)
        def _():
            copy(row, 0, 2).start()

        for slot, least in ((1, 1), (0, 2)):
            @pl.when(n < least)
            def _():
                kv[row, slot] = jnp.zeros((512, 128), bf16)

    tops.step(2)
    for row in range(2):
        for slot, least, by in ((1, 1, 1), (0, 2, 2)):
            @pl.when(n >= least)
            def _():
                copy(row, slot, by).wait_recv()

    outs.append(pltpu.make_async_copy(kv, kv_out, out_s.at[4]))
    outs[3].start()
    tops.step(3)
    tops.rest()
    outs.append(pltpu.make_async_copy(tbuf, tops_out, out_s.at[5]))
    outs[4].start()
    for row in range(2):
        @pl.when(n <= 2)
        def _():
            copy(row, 1, 1).wait_send()

        @pl.when(n <= 1)
        def _():
            copy(row, 0, 2).wait_send()

    gather.sent()
    tops.sent()
    tab_copy.wait_send()
    down.finish()
    for out in outs:
        out.wait()


def enter(hidden, gain, tab, grad_top, p1_own, down_own):
    shard, width = hidden.shape
    return comm_call(
        enter_kernel, "enter", 1,
        (
            jax.ShapeDtypeStruct((2, 512, 256), bf16),
            jax.ShapeDtypeStruct((2, 4, shard, width), bf16),
            jax.ShapeDtypeStruct((2,) + tab.shape, f32),
            jax.ShapeDtypeStruct((4,) + p1_own.shape, bf16),
            jax.ShapeDtypeStruct((4, 256, 1024), bf16),
            jax.ShapeDtypeStruct((2, 3, 512, 128), bf16),
            jax.ShapeDtypeStruct((2, 4, 64, width), bf16),
        ),
        [vmem()] * 4 + [hbm()] * 2, [vmem()] + [hbm()] * 6,
        gather_scratch(shard, width)
        + gather_scratch(64, width)
        + [
            pltpu.VMEM((2,) + tab.shape, f32),
            pltpu.VMEM((4,) + p1_own.shape, bf16),
            pltpu.VMEM((2, 3, 512, 128), bf16),
            pltpu.SemaphoreType.DMA(()),
            pltpu.SemaphoreType.DMA(()),
            pltpu.SemaphoreType.DMA((6,)),
        ]
        + square_sems() * 2
        + [pltpu.SemaphoreType.DMA((2, 3))] * 2,
        (hidden, gain, tab, grad_top, p1_own, down_own), flops=10**10, sent=10**8,
    )


KEYS = 256
QUERIES = 128


def stack_low(x):
    lane = lax.broadcasted_iota(jnp.int32, (QUERIES, 128), 1)
    zero = jnp.zeros((QUERIES, 128), x.dtype)
    parts = []
    for pair in range(2):
        block = x[:, pair * 128 : pair * 128 + 128]
        parts.append(jnp.where(lane < 64, block, zero))
        parts.append(jnp.where(lane < 64, pltpu.roll(block, 64, 1), zero))
    return jnp.concatenate(parts, axis=0)


def stack_high(x):
    lane = lax.broadcasted_iota(jnp.int32, (QUERIES, 128), 1)
    zero = jnp.zeros((QUERIES, 128), x.dtype)
    parts = []
    for pair in range(2):
        block = x[:, pair * 128 : pair * 128 + 128]
        parts.append(jnp.where(lane >= 64, pltpu.roll(block, 64, 1), zero))
        parts.append(jnp.where(lane >= 64, block, zero))
    return jnp.concatenate(parts, axis=0)


def unstack(x, low):
    lane = lax.broadcasted_iota(jnp.int32, (QUERIES, 128), 1)
    out = []
    for pair in range(2):
        even = x[2 * pair * QUERIES : (2 * pair + 1) * QUERIES]
        odd = x[(2 * pair + 1) * QUERIES : (2 * pair + 2) * QUERIES]
        if low:
            out.append(jnp.where(lane < 64, even, pltpu.roll(odd, 64, 1)))
        else:
            out.append(jnp.where(lane < 64, pltpu.roll(even, 64, 1), odd))
    return jnp.concatenate(out, axis=1)


def allowed_tile(starts, tile, first_query):
    key = lax.broadcasted_iota(jnp.int32, (QUERIES, KEYS), 1) + tile * KEYS
    query = lax.broadcasted_iota(jnp.int32, (QUERIES, KEYS), 0) + first_query
    start = jnp.concatenate([starts] * (KEYS // 128), axis=1)
    ok = (key <= query) & (key.astype(f32) >= start)
    return jnp.concatenate([ok] * 4, axis=0)


def attend_block(q, kv, starts, first_query):
    query = stack_low(q.astype(f32)).astype(bf16)

    def body(step, carry):
        tile = (first_query - 1024) // KEYS + step
        top, total, acc = carry
        both = kv[pl.ds(pl.multiple_of(tile * KEYS, KEYS), KEYS), :]
        scores = contract_last(query, both) * 0.125
        ok = allowed_tile(starts, tile, first_query)
        scores = jnp.where(ok, scores, masked_score)
        new_top = jnp.maximum(top, jnp.max(scores, axis=1, keepdims=True))
        shrink = jnp.exp(top - new_top)
        part = jnp.exp(scores - new_top)
        total = total * shrink + jnp.sum(part, axis=1, keepdims=True)
        acc = acc * shrink + jnp.dot(part.astype(bf16), both, preferred_element_type=f32)
        return new_top, total, acc

    top, total, acc = lax.fori_loop(
        0, 5, body,
        (
            jnp.full((4 * QUERIES, 1), masked_score, f32),
            jnp.zeros((4 * QUERIES, 1), f32),
            jnp.zeros((4 * QUERIES, 128), f32),
        ),
        unroll=True,
    )
    logsum = jnp.broadcast_to(top + jnp.log(total), (4 * QUERIES, 128))
    return unstack(acc / total, False).astype(bf16), logsum


def out_block(p1, nn, half):
    return p1[nn, half * 256 : half * 256 + 256, 384:640]


def middle_kernel(
    q, kv, tabs, p1, hidden, gain, gate_own, up_own, down_own,
    att, lse, mid_out, ffn_out, gate_out, up_out, down_out,
    theirs, mine, from_pt, from_up, from_dn, s0, s1, s2, s3, s4, s5, fbuf, h0, h1, h2, h3, out_s,
    gate_s, gate_g, up_s, up_g, down_s, down_g,
):
    me = spot()
    r, n, w = me
    greet(line_partners(r, n, w, 4) + square_partners(r, n, w))
    here = pl.ds(pl.multiple_of(r * 1024, 1024), 1024)
    gate = Square(gate_own.at[:, here], gate_out, (gate_s, gate_g), me)
    up = Square(up_own.at[:, here], up_out, (up_s, up_g), me)
    gate.start()
    up.start()
    down = Square(down_own.at[256:512], down_out, (down_s, down_g), me)
    down.start()
    scatter = Scatter(
        mine, theirs, (from_pt, from_up, from_dn), (s0, s1, s2, s3, s4, s5), me, 4
    )
    ffn = Gather(fbuf, (h0, h1, h2, h3), me, 4)
    def shard(i, carry):
        s = scatter.order(i)
        rows = pl.ds(pl.multiple_of(s * 128, 128), 128)
        for row in range(2):
            att[row, rows, :], lse[row, s] = attend_block(
                q[row, rows, :], kv.at[row], tabs[row, rows, 256:384], 1024 + s * 128
            )

        @pl.when((i >= 1) & ((w == 0) | (w == 3)))
        def _():
            scatter.step(scatter.order(i - 1))

        left = jnp.concatenate([att[1 - r, rows, :], att[r, rows, :]], axis=0)
        for nn in range(4):
            for half in range(2):
                part = jnp.dot(left, out_block(p1, nn, half), preferred_element_type=f32).astype(bf16)
                columns = slice(nn * 512 + half * 256, nn * 512 + half * 256 + 256)
                theirs[s, :, columns] = part[0:128]
                mine[s, :, columns] = part[128:256]
        scatter.pair(s).start()
        return carry

    lax.fori_loop(0, 4, shard, 0)
    scatter.advance((3,), (0, 1, 2, 3))
    scatter.total(mid_out)

    def body(rows):
        middle = mid_out[rows, :] + hidden[rows, :].astype(f32)
        mid_out[rows, :] = middle
        fbuf[r, w, rows, :] = norm_rows(middle, gain[...]).astype(bf16)

    each_rows(hidden.shape[0], 16, body)
    ffn.own()
    gate.turn()
    up.turn()
    ffn.step(1)
    down.turn()
    ffn.step(2)
    ffn.step(3)
    ffn.rest()
    out_f = pltpu.make_async_copy(fbuf, ffn_out, out_s)
    out_f.start()
    scatter.sent()
    ffn.sent()
    gate.finish()
    up.finish()
    down.finish()
    out_f.wait()


def middle_stage(q, kv, tabs, p1, hidden, gain, *weights):
    shard, width = hidden.shape
    rows = jax.ShapeDtypeStruct((2, 4, shard, width), bf16)
    return comm_call(
        middle_kernel, "middle", 3,
        (
            jax.ShapeDtypeStruct((2, 512, 256), bf16),
            jax.ShapeDtypeStruct((2, 4, 4 * QUERIES, 128), f32),
            jax.ShapeDtypeStruct((shard, width), f32),
            rows,
        )
        + (jax.ShapeDtypeStruct((4, 512, 1024), bf16),) * 2
        + (jax.ShapeDtypeStruct((4, 256, 1024), bf16),),
        [vmem()] * 6 + [hbm()] * 3, [vmem()] * 3 + [hbm()] * 4,
        [pltpu.VMEM((4, shard, width), bf16)] * 2
        + scatter_bufs(shard, width) + scatter_sems()
        + gather_scratch(shard, width)
        + [pltpu.SemaphoreType.DMA(())]
        + square_sems() * 3,
        (q, kv, tabs, p1, hidden, gain, *weights), flops=10**10, sent=2 * 10**8,
    )


class Spread:
    def __init__(self, outs, sems, me):
        self.a_send, self.a_keep, self.b_send, self.b_keep = outs
        self.r, self.n, self.w = me
        self.give_s, self.give_g, self.keep_s = sems

    def copies(self, wide, row, place, give):
        for k in range(4):
            block = wide.at[self.n ^ k]
            for part in range(2):
                source = block.at[pl.ds(part * 128, 128)]
                if part == 0:
                    target = (self.a_send if k & 1 else self.a_keep).at[k >> 1]
                else:
                    target = (self.b_send if k >= 2 else self.b_keep).at[k & 1]
                target = place(target)
                at = k * 2 + part
                if give:
                    yield pltpu.make_async_remote_copy(
                        source, target, self.give_s.at[row, at], self.give_g.at[row, at],
                        device_id=(1 - self.r, self.n, self.w), device_id_type=MESH,
                    )
                else:
                    yield pltpu.make_async_copy(source, target, self.keep_s.at[row, at])

    def start(self, *args):
        for copy in self.copies(*args):
            copy.start()

    def wait_send(self, *args):
        for copy in self.copies(*args):
            copy.wait_send()

    def wait_recv(self, *args):
        for copy in self.copies(*args):
            copy.wait_recv()

    def wait(self, *args):
        for copy in self.copies(*args):
            copy.wait()


def spread_sems(count):
    return [pltpu.SemaphoreType.DMA((count, 8))] * 3


def ffn_kernel(
    x, tops_in, grad_top, gate_own, gate_in, up_own, up_in, down_own, down_a, down_b, gain,
    part_out, sum_out, gain_out, o0, o1, o2, o3, ra_out, rb_out,
    theirs, mine, from_pt, from_up, from_dn, s0, s1, s2, s3, s4, s5,
    act, dgu, wide, out_s, give_s, give_g, keep_s, p2, in_s, n_s, n_g,
    tops4, h0, h1, h2, h3, tops_s,
):
    me = spot()
    r, n, w = me
    here = pl.ds(pl.multiple_of(r * 1024, 1024), 1024)
    loads = [
        fetch(gate_own.at[:, here], gate_in, p2.at[0], in_s.at[0], n),
        fetch(up_own.at[:, here], up_in, p2.at[1], in_s.at[1], n),
        fetch(down_own.at[0:256], down_a, p2.at[2, :, 0:256], in_s.at[2], n)
        + fetch(down_own.at[256:512], down_b, p2.at[2, :, 256:512], in_s.at[3], n),
        [pltpu.make_async_copy(tops_in, tops4.at[:, :, 0:64], tops_s)],
    ]
    for group in loads:
        for load in group:
            load.start()

    def loaded(k):
        for load in loads[k]:
            load.wait()

    greet(line_partners(r, n, w, 4) + square_partners(r, n, w))
    scatter = Scatter(
        mine, theirs, (from_pt, from_up, from_dn), (s0, s1, s2, s3, s4, s5), me, 4
    )
    late = pl.ds(64, 64)
    gather = Gather(tops4, (h0, h1, h2, h3), me, 4, late)

    def keep(rows):
        tops4[r, w, pl.ds(64 + rows.start, 16), :] = grad_top[pl.ds(64 + rows.start, 16), :]

    each_rows(64, 16, keep)
    gather.own()
    gain_out[...] = jnp.zeros_like(gain_out)
    loaded(0)
    loaded(1)

    def hidden_tile(i, carry):
        ft, row = i // 2, i % 2
        rows = pl.ds(pl.multiple_of(row * 512, 512), 512)
        columns = pl.ds(pl.multiple_of(ft * 256, 256), 256)
        left = x[rows, :]
        gate = jnp.dot(left, p2[0, :, :, columns].reshape(2048, 256), preferred_element_type=f32)
        up = jnp.dot(left, p2[1, :, :, columns].reshape(2048, 256), preferred_element_type=f32)
        sig = 1.0 / (1.0 + jnp.exp(-gate))
        silu = gate * sig
        act[rows, columns] = (silu * up).astype(bf16)
        dgu[rows, columns] = (up * (sig * (1.0 + gate * (1.0 - sig)))).astype(bf16)
        later = pl.ds(pl.multiple_of(1024 + ft * 256, 256), 256)
        dgu[rows, later] = silu.astype(bf16)
        return carry

    lax.fori_loop(0, 4, hidden_tile, 0)
    gather.step(1)
    lax.fori_loop(4, 8, hidden_tile, 0)
    gather.step(2)
    loaded(2)

    def down_tile(dt, carry):
        nn, half = dt // 2, dt % 2
        columns = pl.ds(pl.multiple_of(dt * 256, 256), 256)
        inner = pl.ds(pl.multiple_of(half * 256, 256), 256)
        other = pl.ds(pl.multiple_of(512 + half * 256, 256), 256)
        right = jnp.concatenate([p2[2, nn, :, inner], p2[2, nn, :, other]], axis=0)
        for row, stage in ((0, theirs), (1, mine)):
            part = jnp.dot(act[row * 512 : row * 512 + 512, :], right, preferred_element_type=f32)
            stage[:, :, columns] = part.astype(bf16).reshape(4, 128, 256)
        return carry

    lax.fori_loop(0, 8, down_tile, 0)
    puts = [
        pltpu.make_async_copy(theirs, part_out.at[0], out_s.at[0]),
        pltpu.make_async_copy(mine, part_out.at[1], out_s.at[1]),
    ]
    for put in puts:
        put.start()
    gather.step(3)
    gather.rest()
    loaded(3)

    def top_rows(row):
        return tops4[row].reshape(512, 2048)

    def back_tile(ft, carry):
        columns = pl.ds(pl.multiple_of(ft * 256, 256), 256)
        f_rows = pl.ds(pl.multiple_of((ft % 2) * 256, 256), 256)
        f_cols = pl.ds(pl.multiple_of((ft // 2) * 512, 512), 512)
        later = pl.ds(pl.multiple_of(1024 + ft * 256, 256), 256)
        right = jnp.concatenate([p2[2, nn, f_rows, f_cols] for nn in range(4)], axis=1)
        for row in range(2):
            rows = slice(row * 512, row * 512 + 512)
            dact = contract_last(top_rows(row), right)
            dgu[rows, columns] = (dact * dgu[rows, columns].astype(f32)).astype(bf16)
            dgu[rows, later] = (dact * dgu[rows, later].astype(f32)).astype(bf16)
        return carry

    lax.fori_loop(0, 4, back_tile, 0)
    for put in puts:
        put.wait()

    spread = Spread((o0, o1, o2, o3), (give_s, give_g, keep_s), me)
    columns_here = pl.ds(pl.multiple_of(r * 1024, 1024), 1024)
    slots = {2: 0, 0: 1, 1: 0}

    def moved(which, half):
        def place(target):
            return target.at[which, :, columns_here]

        return wide.at[slots[which], half], which, place, half == 0

    def weights(which, between=None):
        for half in range(2):
            d_first = (jnp.where(half == 0, 1 - r, r)) * 1024

            def weight_tile(i, carry):
                d_cols = pl.ds(pl.multiple_of(d_first + i * 256, 256), 256)
                if which < 2:
                    left = x[:, d_cols]
                    right = dgu[:, which * 1024 : which * 1024 + 1024]
                else:
                    left = tops4[:, :, :, d_cols].reshape(1024, 256)
                    right = act[...]
                wide[slots[which], half, i] = contract_first(left, right).astype(bf16)
                return carry

            lax.fori_loop(0, 4, weight_tile, 0)
            spread.start(*moved(which, half))
            if half == 0 and between is not None:
                between()

    def hop(which, at):
        return (
            push(o0.at[:, which], ra_out.at[at], n_s.at[0, at], n_g.at[0, at], over_x(r, n, w)),
            push(o2.at[:, which], rb_out.at[at], n_s.at[1, at], n_g.at[1, at], over_y(r, n, w)),
        )

    hops = hop(2, 0) + (
        push(o0.at[1, 0], ra_out.at[1, 1], n_s.at[0, 1], n_g.at[0, 1], over_x(r, n, w)),
        push(o2.at[1, 0], rb_out.at[1, 1], n_s.at[1, 1], n_g.at[1, 1], over_y(r, n, w)),
    )
    for i in range(4):
        s = scatter.order(i)
        rows_t = pl.ds(pl.multiple_of((1 - r) * 512 + s * 128, 128), 128)
        rows_m = pl.ds(pl.multiple_of(r * 512 + s * 128, 128), 128)

        def model_tile(dt, carry):
            nn, half = dt // 2, dt % 2
            columns = pl.ds(pl.multiple_of(dt * 256, 256), 256)
            inner = pl.ds(pl.multiple_of(half * 256, 256), 256)
            left = jnp.concatenate([dgu[rows_t, :], dgu[rows_m, :]], axis=0)
            right = jnp.concatenate([p2[0, nn, inner, :], p2[1, nn, inner, :]], axis=1)
            part = contract_last(left, right)
            seen = jnp.concatenate([x[rows_t, columns], x[rows_m, columns]], axis=0)
            terms = part * seen.astype(f32)
            gain_out[:, columns] += jnp.sum(terms.reshape(32, 8, 256), axis=0)
            part = part.astype(bf16)
            theirs[s, :, columns] = part[0:128]
            mine[s, :, columns] = part[128:256]
            return carry

        lax.fori_loop(0, 8, model_tile, 0)
        scatter.pair(s).start()
        if i == 0:
            weights(2, lambda: scatter.advance((0,), ()))
        elif i < 3:
            which = (2, 0)[i - 1]
            spread.wait_recv(*moved(which, 0))
            spread.wait(*moved(which, 1))
            hops[2 * i - 2].start()
            hops[2 * i - 1].start()
        if i == 1:
            weights(0, lambda: scatter.advance((1,), ()))
            scatter.advance((), (0,))
        elif i > 1:
            scatter.advance((i,), (1,) if i == 3 else ())

    def scale(rows):
        gain_out[rows, :] = gain_out[rows, :] / gain[...]

    each_rows(8, 8, scale)
    spread.wait_send(*moved(2, 0))
    weights(1)
    scatter.advance((), (2, 3))
    scatter.total(sum_out)
    scatter.sent()
    gather.sent()
    spread.wait_send(*moved(0, 0))
    spread.wait_recv(*moved(1, 0))
    spread.wait_send(*moved(1, 0))
    spread.wait(*moved(1, 1))
    for hop in hops:
        hop.wait()


def spread_shapes(*dims):
    return (jax.ShapeDtypeStruct((2,) + dims, bf16),) * 4


def ffn_stage(*args):
    shard, width = 128, 2048
    return comm_call(
        ffn_kernel, "ffn", 4,
        (
            jax.ShapeDtypeStruct((2, 4, shard, width), bf16),
            jax.ShapeDtypeStruct((shard, width), f32),
            jax.ShapeDtypeStruct((8, width), f32),
        )
        + spread_shapes(3, 128, width)
        + (jax.ShapeDtypeStruct((2, 2, 128, width), bf16),) * 2,
        [vmem(), hbm(), vmem()] + [hbm()] * 7 + [vmem()], [hbm(), vmem(), vmem()] + [hbm()] * 6,
        [pltpu.VMEM((4, shard, width), bf16)] * 2
        + scatter_bufs(shard, width) + scatter_sems()
        + [
            pltpu.VMEM((1024, 1024), bf16),
            pltpu.VMEM((1024, 2048), bf16),
            pltpu.VMEM((2, 2, 4, 256, 1024), bf16),
            pltpu.SemaphoreType.DMA((2,)),
        ]
        + spread_sems(3)
        + [pltpu.VMEM((3, 4, 512, 1024), bf16), pltpu.SemaphoreType.DMA((4, 4))]
        + [pltpu.SemaphoreType.DMA((2, 2))] * 2
        + gather_scratch(shard, width)
        + [pltpu.SemaphoreType.DMA(())],
        args, flops=4 * 10**10, sent=10**8,
    )


def norm_back(values, gain, grad):
    root = lax.rsqrt(jnp.mean(values * values, axis=-1, keepdims=True) + norm_eps)
    weighted = grad * gain
    inner = jnp.mean(weighted * values, axis=-1, keepdims=True)
    return root * weighted - values * (root * root * root) * inner


def back_kernel(
    total, mid, grad_top, gain_f, p1, att, q, kv, lse, x, tabs, gain,
    parts, a_send, b_send, a_keep, b_keep, a_came, b_came,
    gmid_out, part_out, gain_out, hid_out, o0, o1, o2, o3, oa_out, ob_out,
    q0, q1, q2, q3, ua_out, ub_out, ga_out, gb_out, la_out, lb_out,
    buf, g0, g1, g2, g3, grad, wide, give_s, give_g, keep_s,
    send, recv, both, wide_q, wide_kv, s_s, s_g, qgive_s, qgive_g, qkeep_s,
    mine, from_pt, from_up, from_dn, s0, s1, s2, s3, s4, s5,
    kept, came, acc, in_s, n_s, n_g, m_s, dkv,
):
    me = spot()
    r, n, w = me
    x_side, y_side = over_x(r, n, w), over_y(r, n, w)
    loads = [pltpu.make_async_copy(parts.at[r], mine, m_s)]
    for j, (keep, first) in enumerate(((a_keep, a_came), (b_keep, b_came))):
        loads += [
            pltpu.make_async_copy(keep.at[1], kept.at[j], in_s.at[j, 0]),
            pltpu.make_async_copy(first.at[1, 1], came.at[j, 0], in_s.at[j, 1]),
            pltpu.make_async_copy(first.at[0, 1], came.at[j, 2], in_s.at[j, 2]),
        ]
    for load in loads:
        load.start()
    greet(
        line_partners(r, n, w, 4)
        + [
            (n >= 1, nar_device(r, n, w, -1)),
            (n >= 2, nar_device(r, n, w, -2)),
            (n <= 2, nar_device(r, n, w, 1)),
            (n <= 1, nar_device(r, n, w, 2)),
        ]
    )
    scatter = Scatter(
        mine, parts.at[1 - r], (from_pt, from_up, from_dn), (s0, s1, s2, s3, s4, s5), me, 4
    )
    gather = Gather(buf, (g0, g1, g2, g3), me, 4)

    def hop(k, source, target, device):
        return push(source, target, n_s.at[k], n_g.at[k], device)

    up_hops = [
        hop(0, a_send.at[:, 1], ua_out, x_side),
        hop(1, b_send.at[:, 1], ub_out, y_side),
    ]
    last_hops = [
        [
            hop(2 + which, kept.at[0, which], la_out.at[which], y_side),
            hop(5 + which, kept.at[1, which], lb_out.at[which], x_side),
        ]
        for which in range(3)
    ]
    gate_hops = [hop(10, a_send.at[0, 0], ga_out, x_side), hop(11, b_send.at[0, 0], gb_out, y_side)]
    o_hops = [hop(8, o0, oa_out, x_side), hop(9, o2, ob_out, y_side)]
    for one in up_hops:
        one.start()

    def body(rows):
        got = norm_back(mid[rows, :], gain_f[...], total[rows, :]) + grad_top[rows, :].astype(f32)
        gmid_out[rows, :] = got
        buf[r, w, rows, :] = got.astype(bf16)

    each_rows(mid.shape[0], 16, body)
    gather.own()
    for load in loads:
        load.wait()

    def join(which):
        for j in range(2):
            def add(rows):
                one = kept[j, which, rows, :].astype(f32) + came[j, which, rows, :].astype(f32)
                kept[j, which, rows, :] = one.astype(bf16)

            each_rows(128, 16, add)
            last_hops[which][j].start()

    join(2)
    join(0)
    for one in gate_hops:
        one.start()
    for i in range(4):
        scatter.pair(scatter.order(i)).start()
    for k in (1, 2, 3):
        gather.step(k)
    gather.rest()
    scatter.advance((0, 1, 2, 3), ())
    for row in range(2):
        for pair in range(2):
            left = jnp.concatenate([buf[row, 2 * pair], buf[row, 2 * pair + 1]], axis=0)
            right = jnp.concatenate(
                [out_block(p1, nn, half) for nn in range(4) for half in range(2)], axis=1
            )
            grad[row, pair * 256 : pair * 256 + 256, :] = contract_last(left, right).astype(bf16)

    def copy(row, slot, by):
        return pltpu.make_async_remote_copy(
            send.at[row, slot], recv.at[row, slot], s_s.at[row, slot], s_g.at[row, slot],
            device_id=nar_device(r, n, w, by), device_id_type=MESH,
        )

    def attention(i, carry):
        row, block = i // 4, i % 4
        first_query = 1024 + block * QUERIES
        here = pl.ds(pl.multiple_of(block * QUERIES, QUERIES), QUERIES)

        @pl.when(block == 0)
        def _():
            dkv[row] = jnp.zeros((1536, 128), f32)

        query = stack_low(q[row, here, :].astype(f32)).astype(bf16)
        grads = stack_high(grad[row, here, :].astype(f32))
        inner = jnp.sum(grads * stack_high(att[row, here, :].astype(f32)), axis=1, keepdims=True)
        grads = grads.astype(bf16)
        logsum = jnp.concatenate([lse[row, block]] * (KEYS // 128), axis=1)
        starts = tabs[row, here, 256:384]

        def key_tile(step, dq):
            tile = block // 2 + step
            rows = pl.ds(pl.multiple_of(tile * KEYS, KEYS), KEYS)
            pair = kv[row, rows, :]
            ok = allowed_tile(starts, tile, first_query)
            scores = contract_last(query, pair) * 0.125
            prob = jnp.where(ok, jnp.exp(scores - logsum), 0.0)
            grad_prob = contract_last(grads, pair)
            grad_scores = (prob * (grad_prob - inner)).astype(bf16)
            dkv[row, rows, :] += contract_first(grad_scores, query) * 0.125 + contract_first(
                prob.astype(bf16), grads
            )
            return dq + jnp.dot(grad_scores, pair, preferred_element_type=f32)

        dq = lax.fori_loop(0, 5, key_tile, jnp.zeros((4 * QUERIES, 128), f32), unroll=True)
        flat = unstack(dq, True) * 0.125
        cosine, sine = tabs[row, here, 0:128], -tabs[row, here, 128:256]
        there = pl.ds(pl.multiple_of(i * QUERIES, QUERIES), QUERIES)
        both[there, 0:128] = turn(flat[:, 0:128], cosine, sine).astype(bf16)
        both[there, 128:256] = turn(flat[:, 128:256], cosine, sine).astype(bf16)

        @pl.when(block == 3)
        def _():
            for slot, by in ((1, -1), (0, -2)):
                @pl.when(n >= -by)
                def _():
                    send[row, slot] = dkv[row, slot * 512 : slot * 512 + 512, :].astype(bf16)
                    copy(row, slot, by).start()

        @pl.when(i == 3)
        def _():
            scatter.advance((), (0,))

        return carry

    lax.fori_loop(0, 8, attention, 0)
    scatter.advance((), (1,))

    fresh = []
    for j, first in enumerate((ua_out, ub_out)):
        up_hops[j].wait_recv()
        fresh.append(pltpu.make_async_copy(first.at[1], came.at[j, 1], in_s.at[j, 3]))
        fresh[j].start()
    for load in fresh:
        load.wait()
    join(1)

    spread_o = Spread((o0, o1, o2, o3), (give_s, give_g, keep_s), me)
    spread = Spread((q0, q1, q2, q3), (qgive_s, qgive_g, qkeep_s), me)

    def moved_o(half):
        def place(target):
            return target.at[:, pl.ds(pl.multiple_of(r * 256, 256), 256)]

        return wide.at[half], 0, place, half == 0

    for half in range(2):
        d_first = (jnp.where(half == 0, 1 - r, r)) * 1024

        def weight_tile(i, carry):
            columns = pl.ds(pl.multiple_of(d_first + i * 256, 256), 256)
            left = buf[:, :, :, columns].reshape(1024, 256)
            wide[half, i] = contract_first(left, att[...].reshape(1024, 256)).astype(bf16)
            return carry

        lax.fori_loop(0, 4, weight_tile, 0)
        spread_o.start(*moved_o(half))

    def moved_q(half):
        def place(target):
            return target.at[:, pl.ds(pl.multiple_of(r * 256, 256), 256)]

        return wide_q.at[half], 0, place, half == 0

    def moved_kv(half):
        def place(target):
            return target.at[:, pl.ds(pl.multiple_of(512 + r * 128, 128), 128)]

        return wide_kv.at[half], 1, place, half == 0

    def weight(half, columns, wide):
        d_first = (jnp.where(half == 0, 1 - r, r)) * 1024

        def tile(i, carry):
            d_cols = pl.ds(pl.multiple_of(d_first + i * 256, 256), 256)
            wide[half, i] = contract_first(x[:, d_cols], both[:, columns]).astype(bf16)
            return carry

        lax.fori_loop(0, 4, tile, 0)

    for half in range(2):
        weight(half, slice(0, 256), wide_q)
        spread.start(*moved_q(half))
    lane = lax.broadcasted_iota(jnp.int32, (128, 128), 1)
    for row in range(2):
        for slot, by in ((1, -1), (0, -2)):
            @pl.when(n <= 3 + by)
            def _():
                copy(row, slot, by).wait_recv()

        def tile(i, carry):
            rows = pl.ds(pl.multiple_of(i * 128, 128), 128)
            total = dkv[row, pl.ds(pl.multiple_of(1024 + i * 128, 128), 128), :]
            zero = jnp.zeros_like(total)
            total = total + jnp.where(n <= 2, recv[row, 1, rows, :].astype(f32), zero)
            total = total + jnp.where(n <= 1, recv[row, 0, rows, :].astype(f32), zero)
            turned = turn(total, tabs[row, rows, 0:128], -tabs[row, rows, 128:256])
            both[pl.ds(pl.multiple_of(row * 512 + i * 128, 128), 128), 256:384] = jnp.where(
                lane < 64, turned, total
            ).astype(bf16)
            return carry

        lax.fori_loop(0, 4, tile, 0)
    for half in range(2):
        weight(half, slice(256, 384), wide_kv)
        spread.start(*moved_kv(half))
    scatter.advance((), (2,))
    spread_o.wait_recv(*moved_o(0))
    spread_o.wait(*moved_o(1))
    for one in o_hops:
        one.start()
    gain_out[...] = jnp.zeros_like(gain_out)

    def model_tile(dt, carry):
        nn, half = dt // 2, dt % 2
        columns = pl.ds(pl.multiple_of(dt * 256, 256), 256)
        inner = pl.ds(pl.multiple_of(half * 256, 256), 256)
        right = p1[nn, inner, 0:384]
        for row in range(2):
            for block in range(2):
                first = row * 512 + block * 256
                part = contract_last(both[first : first + 256, :], right)
                terms = part * x[first : first + 256, columns].astype(f32)
                gain_out[:, columns] += jnp.sum(terms.reshape(32, 8, 256), axis=0)
                part_out[row, 2 * block, :, columns] = part[0:128].astype(bf16)
                part_out[row, 2 * block + 1, :, columns] = part[128:256].astype(bf16)
        return carry

    lax.fori_loop(0, 8, model_tile, 0)
    gain_out[...] = gain_out[...] / gain[...]
    scatter.advance((), (3,))
    scatter.total(acc)

    def last(rows):
        hid_out[rows, :] = (acc[rows, :] + mid[rows, :]).astype(bf16)

    each_rows(128, 16, last)
    scatter.sent()
    for row in range(2):
        for slot, by in ((1, -1), (0, -2)):
            @pl.when(n >= -by)
            def _():
                copy(row, slot, by).wait_send()

    for half in range(2):
        spread.wait(*moved_q(half))
        spread.wait(*moved_kv(half))
    spread_o.wait_send(*moved_o(0))
    gather.sent()
    for one in up_hops:
        one.wait_send()
    for one in last_hops[0] + last_hops[1] + last_hops[2] + gate_hops + o_hops:
        one.wait()


def back(*args):
    shard, width = 128, 2048
    return comm_call(
        back_kernel, "back", 5,
        (
            jax.ShapeDtypeStruct((shard, width), f32),
            jax.ShapeDtypeStruct((2, 4, shard, width), bf16),
            jax.ShapeDtypeStruct((8, width), f32),
            jax.ShapeDtypeStruct((shard, width), bf16),
        )
        + spread_shapes(128, 512)
        + (jax.ShapeDtypeStruct((2, 128, 512), bf16),) * 2
        + spread_shapes(128, 768)
        + (jax.ShapeDtypeStruct((2, 128, width), bf16),) * 2
        + (jax.ShapeDtypeStruct((128, width), bf16),) * 2
        + (jax.ShapeDtypeStruct((3, 128, width), bf16),) * 2,
        [vmem()] * 12 + [hbm()] * 7, [vmem()] * 4 + [hbm()] * 16,
        gather_scratch(shard, width)
        + [pltpu.VMEM((2, 512, 256), bf16), pltpu.VMEM((2, 4, 256, 256), bf16)]
        + spread_sems(1)
        + [
            pltpu.VMEM((2, 2, 512, 128), bf16),
            pltpu.VMEM((2, 2, 512, 128), bf16),
            pltpu.VMEM((1024, 384), bf16),
            pltpu.VMEM((2, 4, 256, 256), bf16),
            pltpu.VMEM((2, 4, 256, 128), bf16),
            pltpu.SemaphoreType.DMA((2, 2)),
            pltpu.SemaphoreType.DMA((2, 2)),
        ]
        + spread_sems(2)
        + [pltpu.VMEM((4, shard, width), bf16)]
        + scatter_bufs(shard, width) + scatter_sems()
        + [
            pltpu.VMEM((2, 3, shard, width), bf16),
            pltpu.VMEM((2, 3, shard, width), bf16),
            pltpu.VMEM((shard, width), f32),
            pltpu.SemaphoreType.DMA((2, 4)),
            pltpu.SemaphoreType.DMA((12,)),
            pltpu.SemaphoreType.DMA((12,)),
            pltpu.SemaphoreType.DMA(()),
            pltpu.VMEM((2, 1536, 128), f32),
        ],
        args, flops=10**10, sent=10**8,
    )


def leave_kernel(
    parts, hidden, gain, gmid, gains, qa_send, qa_keep, qb_send, qb_keep, oa_keep, ob_keep, oa_in, ob_in,
    a_keep, b_keep, a_gate, b_gate, a_up, b_up, a_down, b_down, a_last, b_last,
    grad_out, ga_out, query_out, key_out, value_out, output_out, gate_out, up_out, down_out,
    mine, from_pt, from_up, from_dn, s0, s1, s2, s3, s4, s5,
    acc, over_wid, summed, over_rest, w_s, w_g, t_s, t_g,
    first_q, next_q, then_q, next_o, then_o, kv, n_s, n_g, k0, k1, k2, k3, m_s,
    terms, joined, t_in, t_out,
):
    me = spot()
    r, n, w = me
    own_parts = pltpu.make_async_copy(parts.at[r], mine, m_s)
    own_parts.start()
    loads, puts = [], []
    for j, (keep, gate, up, down, last_hop) in enumerate(
        ((a_keep, a_gate, a_up, a_down, a_last), (b_keep, b_gate, b_up, b_down, b_last))
    ):
        for which, first in enumerate((gate, up.at[0], down.at[0, 0])):
            at = 2 * which + j
            for k, source in enumerate((keep.at[0, which], first, last_hop.at[which])):
                loads.append(pltpu.make_async_copy(source, terms.at[k, at], t_in.at[k, at]))
            place = (gate_out, up_out, down_out)[which].at[j * 128 : j * 128 + 128]
            puts.append(pltpu.make_async_copy(joined.at[at], place, t_out.at[at]))
    partners = [(w != j, (r, n, jnp.int32(j))) for j in range(4)]
    partners += [
        ((r != a) | (n != b), (jnp.int32(a), jnp.int32(b), w)) for a in range(2) for b in range(4)
    ]
    greet(partners)
    kv_gather = Gather(kv, (k0, k1, k2, k3), me, 4, pair=False)
    x_side, y_side = over_x(r, n, w), over_y(r, n, w)
    q_hops = [
        push(qa_send, first_q.at[0], n_s.at[0], n_g.at[0], x_side),
        push(qb_send, first_q.at[1], n_s.at[1], n_g.at[1], y_side),
    ]
    q_later = [
        push(next_q.at[0], then_q.at[0], n_s.at[2], n_g.at[2], y_side),
        push(next_q.at[1], then_q.at[1], n_s.at[3], n_g.at[3], x_side),
    ]
    o_hops = [
        push(next_o.at[0], then_o.at[0], n_s.at[4], n_g.at[4], y_side),
        push(next_o.at[1], then_o.at[1], n_s.at[5], n_g.at[5], x_side),
    ]
    for hop in q_hops:
        hop.start()
    for load in loads:
        load.start()
    scatter = Scatter(
        mine, parts.at[1 - r], (from_pt, from_up, from_dn), (s0, s1, s2, s3, s4, s5), me, 4
    )
    for i in range(4):
        scatter.pair(scatter.order(i)).start()

    def wid_copy(j, slot):
        return pltpu.make_async_remote_copy(
            gains, over_wid.at[slot], w_s.at[j], w_g.at[slot],
            device_id=(r, n, jnp.int32(j)), device_id_type=MESH,
        )

    def rest_copy(a, b, slot):
        return pltpu.make_async_remote_copy(
            summed, over_rest.at[slot], t_s.at[a * 4 + b], t_g.at[slot],
            device_id=(jnp.int32(a), jnp.int32(b), w), device_id_type=MESH,
        )

    for j in range(4):
        @pl.when(w != j)
        def _():
            wid_copy(j, w).start()

    own_parts.wait()
    scatter.advance((0, 1, 2), ())
    for j, (keep, came) in enumerate(((oa_keep, oa_in), (ob_keep, ob_in))):
        next_o[j] = (keep[1].astype(f32) + came[1].astype(f32)).astype(bf16)
        o_hops[j].start()
    summed[...] = gains[...]
    for j in range(4):
        @pl.when(w != j)
        def _():
            wid_copy(j, j).wait_recv()
            summed[...] += over_wid[j]

    for a in range(2):
        for b in range(4):
            @pl.when((r != a) | (n != b))
            def _():
                rest_copy(a, b, r * 4 + n).start()

    for j, keep in enumerate((qa_keep, qb_keep)):
        q_hops[j].wait_recv()
        next_q[j] = (keep[1].astype(f32) + first_q[j, 1].astype(f32)).astype(bf16)
        q_later[j].start()
    scatter.advance((), (0,))
    for j, keep in enumerate((qa_keep, qb_keep)):
        q_later[j].wait_recv()
        total = keep[0].astype(f32) + first_q[j, 0].astype(f32) + then_q[j].astype(f32)
        query_out[j * 128 : j * 128 + 128, :] = total[:, 0:512]
        kv[0, w, j * 128 : j * 128 + 128, :] = total[:, 512:768].astype(bf16)
    kv_gather.own()
    scatter.advance((3,), (1, 2))
    kv_gather.advance((), (1,))
    for load in loads:
        load.wait()

    def add_terms(at, carry):
        def body(rows):
            joined[at, rows, :] = (
                terms[0, at, rows, :].astype(f32) + terms[1, at, rows, :].astype(f32)
            ) + terms[2, at, rows, :].astype(f32)

        each_rows(128, 16, body)
        return carry

    lax.fori_loop(0, 6, add_terms, 0)
    for put in puts:
        put.start()
    scatter.advance((), (3,))
    kv_gather.advance((), (2,))
    for j, (keep, came) in enumerate(((oa_keep, oa_in), (ob_keep, ob_in))):
        o_hops[j].wait_recv()
        output_out[:, j * 128 : j * 128 + 128] = (
            keep[0].astype(f32) + came[0].astype(f32) + then_o[j].astype(f32)
        ).T
    mine_block = r * 4 + n
    ga_out[0:1] = summed[pl.ds(mine_block, 1), :]
    ga_out[1:2] = summed[pl.ds(mine_block + 8, 1), :]
    for a in range(2):
        for b in range(4):
            @pl.when((r != a) | (n != b))
            def _():
                slot = a * 4 + b
                rest_copy(a, b, slot).wait_recv()
                ga_out[0:1] += over_rest[slot, pl.ds(mine_block, 1), :]
                ga_out[1:2] += over_rest[slot, pl.ds(mine_block + 8, 1), :]

    scatter.total(acc)

    def last(rows):
        grad = norm_back(hidden[rows, :].astype(f32), gain[...], acc[rows, :])
        grad_out[rows, :] = (grad + gmid[rows, :]).astype(bf16)

    each_rows(hidden.shape[0], 16, last)
    kv_gather.advance((1, 2, 3), (3,))
    lane = lax.broadcasted_iota(jnp.int32, (256, 128), 1)
    for j in range(4):
        even, odd = kv[0, j, :, 0:128].astype(f32), kv[0, j, :, 128:256].astype(f32)
        here = slice(j * 128, j * 128 + 128)
        key_out[:, here] = jnp.where(lane < 64, even, pltpu.roll(odd, 64, 1))
        value_out[:, here] = jnp.where(lane < 64, pltpu.roll(even, 64, 1), odd)
    scatter.sent()
    kv_gather.sent()
    for put in puts:
        put.wait()
    for hop in q_hops + q_later + o_hops:
        hop.wait_send()
    for j in range(4):
        @pl.when(w != j)
        def _():
            wid_copy(j, w).wait_send()

    for a in range(2):
        for b in range(4):
            @pl.when((r != a) | (n != b))
            def _():
                rest_copy(a, b, r * 4 + n).wait_send()


def leave(*args):
    shard, width = 128, 2048
    grad = jax.ShapeDtypeStruct((256, 512), f32)
    return comm_call(
        leave_kernel, "leave", 7,
        (jax.ShapeDtypeStruct((shard, width), bf16), jax.ShapeDtypeStruct((8, 256), f32))
        + (grad,) * 3
        + (jax.ShapeDtypeStruct((512, 256), f32),)
        + (jax.ShapeDtypeStruct((256, 2048), f32),) * 3,
        [hbm()] + [vmem()] * 12 + [hbm()] * 10, [vmem()] * 6 + [hbm()] * 3,
        [pltpu.VMEM((4, shard, width), bf16)]
        + scatter_bufs(shard, width) + scatter_sems()
        + [
            pltpu.VMEM((shard, width), f32),
            pltpu.VMEM((4, 16, 256), f32),
            pltpu.VMEM((16, 256), f32),
            pltpu.VMEM((8, 16, 256), f32),
            pltpu.SemaphoreType.DMA((4,)),
            pltpu.SemaphoreType.DMA((4,)),
            pltpu.SemaphoreType.DMA((8,)),
            pltpu.SemaphoreType.DMA((8,)),
            pltpu.VMEM((2, 2, 128, 768), bf16),
            pltpu.VMEM((2, 128, 768), bf16),
            pltpu.VMEM((2, 128, 768), bf16),
            pltpu.VMEM((2, 128, 512), bf16),
            pltpu.VMEM((2, 128, 512), bf16),
            pltpu.VMEM((1, 4, 256, 256), bf16),
            pltpu.SemaphoreType.DMA((6,)),
            pltpu.SemaphoreType.DMA((6,)),
        ]
        + gather_sems()
        + [
            pltpu.SemaphoreType.DMA(()),
            pltpu.VMEM((3, 6, shard, width), bf16),
            pltpu.VMEM((6, shard, width), f32),
            pltpu.SemaphoreType.DMA((3, 6)),
            pltpu.SemaphoreType.DMA((6,)),
        ],
        args, flops=10**10, sent=10**8,
    )


def local_fast(
    hidden_in, doc_lengths, w_query, w_key, w_value, w_output, w_gate, w_up, w_down,
    gain_attn, gain_ffn, grad_out,
):
    r, n, w = spot()
    hidden, grad_top = hidden_in[0], grad_out[0]
    gain_a, gain_f = gain_attn[None], gain_ffn[None]
    def half(weight, axis):
        size = weight.shape[axis] // 2
        return lax.dynamic_slice_in_dim(weight, r * size, size, axis)

    head = (w * 2 + r) * HD
    kv_pack = jnp.concatenate(
        [lax.dynamic_slice_in_dim(w_key, head, HD, 1), lax.dynamic_slice_in_dim(w_value, head, HD, 1)],
        axis=1,
    )
    out_half = half(w_output, 0)
    p1_shard = jnp.concatenate(
        [half(w_query, 1), kv_pack, jnp.concatenate([out_half[:, :256], out_half[:, 256:]], axis=0)],
        axis=1,
    )
    down_half = half(w_down, 0)
    down_own = jnp.concatenate([down_half[:512], down_half[512:]], axis=1)

    token_ids = n * 512 + jnp.arange(512, dtype=jnp.int32)
    doc_start, places = doc_layout(doc_lengths[0], token_ids)
    angles = places.astype(f32)[:, None] * inverse_freq()[None, :]
    cosine, sine = jnp.cos(angles), jnp.sin(angles)
    start_here = (doc_start - (n - 2) * 512).astype(f32)
    tab = jnp.concatenate(
        [cosine] * 4 + [-sine, sine] * 2 + [jnp.broadcast_to(start_here[:, None], (512, 128))],
        axis=1,
    )

    q, rows, tabs, p1, down_a, kv, tops = enter(
        hidden, gain_a, tab, grad_top, p1_shard, down_own
    )
    rows2 = rows.reshape(1024, 2048)
    kv_flat = kv.reshape(2, 1536, 128)
    att, lse, mid, ffn_rows, gate_all, up_all, down_b = middle_stage(
        q, kv_flat, tabs, p1, hidden, gain_f, w_gate, w_up, down_own
    )
    parts, total, gain_f_part, a_send, a_keep, b_send, b_keep, ra_dg, rb_dg = ffn_stage(
        ffn_rows.reshape(1024, 2048), tops, grad_top,
        w_gate, gate_all, w_up, up_all, down_own, down_a, down_b, gain_f,
    )
    (
        gmid, dparts, gain_a_part, hidden_out, _, oa_keep, _, ob_keep, oa_came, ob_came,
        qa_send, qa_keep, qb_send, qb_keep, ra_u, rb_u, ra_g, rb_g, a_last, b_last,
    ) = back(
        total, mid, grad_top, gain_f, p1, att, q, kv_flat, lse, rows2, tabs, gain_a,
        parts, a_send, b_send, a_keep, b_keep, ra_dg, rb_dg,
    )
    gains = jnp.concatenate(
        [gain_f_part.sum(axis=0).reshape(8, 256), gain_a_part.sum(axis=0).reshape(8, 256)], axis=0
    )
    (
        grad_in, gain_sums, grad_query, grad_key, grad_value, output_sum,
        grad_gate, grad_up, down_sum,
    ) = leave(
        dparts, hidden, gain_a, gmid, gains,
        qa_send, qa_keep, qb_send, qb_keep, oa_keep, ob_keep, oa_came, ob_came,
        a_keep, b_keep, ra_g, rb_g, ra_u, rb_u, ra_dg, rb_dg, a_last, b_last,
    )

    return (
        hidden_out[None],
        grad_in[None],
        grad_query,
        grad_key,
        grad_value,
        output_sum,
        grad_gate,
        grad_up,
        down_sum.T,
        gain_sums[1],
        gain_sums[0],
    )


def solution(mesh):
    in_specs = (
        P("row", ("nar", "wid"), None),
        P("row", None),
        P("nar", "wid"),
        P("nar", None),
        P("nar", None),
        P("wid", "nar"),
        P("nar", "wid"),
        P("nar", "wid"),
        P("wid", "nar"),
        P(),
        P(),
        P("row", ("nar", "wid"), None),
    )
    out_specs = (
        P("row", ("nar", "wid"), None),
        P("row", ("nar", "wid"), None),
        P(("row", "nar"), "wid"),
        P(("row", "nar"), None),
        P(("row", "nar"), None),
        P("wid", ("row", "nar")),
        P(("row", "nar"), "wid"),
        P(("row", "nar"), "wid"),
        P("wid", ("row", "nar")),
        P(("row", "nar")),
        P(("row", "nar")),
    )
    sizes = dict(mesh.shape)
    fits = sizes == {"row": 2, "nar": 4, "wid": 4}

    def body(*args):
        small = args[0].shape == (1, 128, 2048)
        return (local_fast if fits and small else local)(*args)

    return jax.shard_map(body, mesh=mesh, in_specs=in_specs, out_specs=out_specs, check_vma=False)
```
